32 devices in a mesh: dp: 8 (over y, x, core), shard: 4 (over z).
Axes of the slice: x: 2, y: 2, z: 4, core: 2. Of those that a mesh axis runs over, the one named last changes fastest.
Arguments:
- tokens: bfloat16 [8192, 1536], P(('dp', 'shard')), may hold values from -6 to 6
- cotangent: bfloat16 [8192, 1536], P(('dp', 'shard')), may hold values from -6 to 6
- seq_start: int32 [8192], P(('dp', 'shard')), may hold values from 0 to 192, as said below
- live_mask: int32 [8192], P(('dp', 'shard')), may hold values from 0 to 1, as said below
- input_proj: bfloat16 [2, 1536, 2048], P(None, None, 'shard'), may hold values from -0.15625 to 0.15625
- gate_blocks: bfloat16 [2, 16, 128, 128], P(None, 'shard'), may hold values from -0.5 to 0.5
- output_proj: bfloat16 [2048, 1536], P('shard'), may hold values from -0.375 to 0.375
- ffn_gate_up: bfloat16 [2, 1536, 4608], P(None, None, 'shard'), may hold values from -0.15625 to 0.15625
- ffn_down: bfloat16 [4608, 1536], P('shard'), may hold values from -0.1875 to 0.1875
- conv_taps: bfloat16 [5, 2048], P(None, 'shard'), may hold values from -3 to 3
- gate_bias: bfloat16 [2, 2048], P(None, 'shard'), may hold values from -3 to 3
- decay_param: bfloat16 [2048], P('shard'), may hold values from 3 to 8
- norm_gains: bfloat16 [2, 1536], P(None, 'shard'), may hold values from 0.5 to 1.5
- master_shard: float32 [4, 7803648], P('shard', 'dp'), may hold values from -0.75 to 0.75
- first_moment: float32 [4, 7803648], P('shard', 'dp'), may hold values from -6 to 6
- second_moment: float32 [4, 7803648], P('shard', 'dp'), may hold values from 0.1 to 10
Outputs:
- block_out: bfloat16 [8192, 1536], P(('dp', 'shard'))
- tokens_grad: bfloat16 [8192, 1536], P(('dp', 'shard'))
- weight_grads: float32 [4, 7803648], P('shard', 'dp')
- new_master: float32 [4, 7803648], P('shard', 'dp')
- new_first: float32 [4, 7803648], P('shard', 'dp')
- new_second: float32 [4, 7803648], P('shard', 'dp')
- new_weights: bfloat16 [4, 7803648], P(None, 'dp')
- bias_grad: float32 [2, 2048], P(None, 'shard')
The draws below stay inside these ranges and needn't reach their ends.
Inputs may be any that keep to these rules, and one draw needn't show every extreme that they name: Within each device's block of 256 slots the live slots form a prefix of 2, 3 or 4 times 256 // 4 slots, and some device has all its slots live; every sequence begins at a multiple of 64, and every live sequence has 64 slots or more; seq_start is constant over a sequence and equals its first slot; the block holds one to four live sequences, and its padding forms one more sequence. `live_mask`: 1 exactly on the live prefix of each device's block.
All inputs are finite; a program needn't handle non-finite values.
Results may differ from the reference program's by a relative error of at most 0.017.
Values may be sent and summed in bfloat16 or wider, within the bound.
A program may use at most 384 MiB of HBM per device.

```python
import math
import jax
import jax.numpy as jnp
from jax import lax

D = 1536
R = 2048
F = 4608
BLK = 128
CONV = 4
SLOTS = 256
HEADS = 16
TOKENS = 8192
SHARD_LEN = 7803648
N_SHARD = 4
DEVICES = 32


def layout_ints(key):
    base_key = jax.random.fold_in(key, 11)
    key_fill, key_full, key_cut = jax.random.split(base_key, 3)
    buffers = TOKENS // SLOTS
    quarter = SLOTS // 4
    fill_count = jax.random.randint(key_fill, (buffers,), 2, 5) * quarter
    chosen = jax.random.randint(key_full, (), 0, buffers)
    is_chosen = jnp.arange(buffers) == chosen
    fill_count = jnp.where(is_chosen, SLOTS, fill_count).astype(jnp.int32)
    cut_points = jax.random.randint(key_cut, (buffers, 3), 1, 4) * quarter
    last_cut = is_chosen[:, None] & (jnp.arange(3) == 2)[None, :]
    cut_points = jnp.where(last_cut, 3 * quarter, cut_points)
    cut_points = jnp.where(cut_points <= fill_count[:, None] - quarter, cut_points, 0).astype(jnp.int32)
    bounds = jnp.concatenate([jnp.zeros((buffers, 1), jnp.int32), cut_points, fill_count[:, None]], axis=1)
    position = jnp.arange(SLOTS, dtype=jnp.int32)
    starts = jnp.max(jnp.where(bounds[:, None, :] <= position[None, :, None], bounds[:, None, :], 0), axis=-1)
    live_flags = (position[None, :] < fill_count[:, None]).astype(jnp.int32)
    return (starts.reshape(-1).astype(jnp.int32), live_flags.reshape(-1))


def draw_seq_start(key, part):
    return layout_ints(key)[0]


def draw_live_mask(key, part):
    return layout_ints(key)[1]


def block_scale(rng, extent, pieces, smallest, largest):
    def one(axis_at, shards_of):
        heights = jax.random.uniform(jax.random.fold_in(jax.random.fold_in(rng, 6), axis_at), (shards_of,), jnp.float32, smallest / len(pieces), largest / len(pieces))
        return jnp.repeat(jnp.exp(heights), extent[axis_at] // shards_of).reshape((-1,) + (1,) * (len(extent) - axis_at - 1))

    loudness = one(*pieces[0])
    for cut in pieces[1:]:
        loudness = loudness * one(*cut)
    return loudness


def bell_draw(key, dims, scale, bound, cuts=(), kind=jnp.bfloat16):
    level = block_scale(key, dims, cuts, -0.22, 0.18) if cuts else 1.0
    entries = jax.random.normal(key, dims, jnp.float32) * scale * level
    return jnp.minimum(jnp.maximum(entries, -bound), bound).astype(kind)


def setup_inputs(seed: int = 0) -> dict:
    keys = jax.random.split(jax.random.key(seed), 17)
    tokens = bell_draw(keys[0], (TOKENS, D), 1.0, 6.0, ((0, 32),))
    cotangent = bell_draw(keys[1], (TOKENS, D), 1.0, 6.0, ((0, 32),))
    seq_start = draw_seq_start(jax.random.fold_in(keys[16], 71), 0)
    live_mask = draw_live_mask(jax.random.fold_in(keys[16], 71), 0)
    input_proj = bell_draw(keys[4], (2, D, R), D ** -0.5, 0.15625, ((2, 4),))
    gate_blocks = bell_draw(keys[5], (2, HEADS, BLK, BLK), BLK ** -0.5, 0.5, ((1, 4),))
    output_proj = bell_draw(keys[6], (R, D), (R // 8) ** -0.5, 0.375, ((0, 4),))
    ffn_gate_up = bell_draw(keys[7], (2, D, F), D ** -0.5, 0.15625, ((2, 4),))
    ffn_down = bell_draw(keys[8], (F, D), (F // 4) ** -0.5, 0.1875, ((0, 4),))
    conv_taps = bell_draw(keys[9], (CONV + 1, R), CONV ** -0.5, 3.0, ((1, 4),))
    gate_bias = bell_draw(keys[10], (2, R), 0.5, 3.0, ((1, 4),))
    decay_param = jnp.clip(3.0 + 5.0 * jax.random.uniform(keys[11], (R,), jnp.float32) ** block_scale(keys[11], (R,), ((0, 4),), -0.2, 0.2), 3.0, 8.0).astype(jnp.bfloat16)
    norm_gains = jnp.clip(1.0 + 0.1 * jax.random.normal(keys[12], (2, D), jnp.float32), 0.5, 1.5).astype(jnp.bfloat16)
    master_shard = bell_draw(keys[13], (N_SHARD, SHARD_LEN), 0.05, 0.75, ((0, 4), (1, 8)), jnp.float32)
    first_moment = bell_draw(keys[14], (N_SHARD, SHARD_LEN), 1.0, 6.0, ((0, 4), (1, 8)), jnp.float32)
    second_moment = jnp.clip(jnp.exp(math.log(10.0) - 4.6051702 * jax.random.uniform(keys[15], (N_SHARD, SHARD_LEN), jnp.float32) ** block_scale(keys[15], (N_SHARD, SHARD_LEN), ((0, 4), (1, 8)), -0.2, 0.2)), 0.1, 10.0)
    return {"tokens": tokens, "cotangent": cotangent, "seq_start": seq_start, "live_mask": live_mask, "input_proj": input_proj, "gate_blocks": gate_blocks, "output_proj": output_proj, "ffn_gate_up": ffn_gate_up, "ffn_down": ffn_down, "conv_taps": conv_taps, "gate_bias": gate_bias, "decay_param": decay_param, "norm_gains": norm_gains, "master_shard": master_shard, "first_moment": first_moment, "second_moment": second_moment}


@jax.custom_vjp
def low(v):
    return lax.optimization_barrier(v.astype(jnp.bfloat16)).astype(jnp.float32)

@jax.custom_vjp
def low_back(v):
    return v

def low_keep(v):
    return (low(v), None)

def low_pass(kept, grad):
    return (grad,)

def back_keep(v):
    return (v, None)

def back_low(kept, grad):
    return (low(grad),)
low.defvjp(low_keep, low_pass)
low_back.defvjp(back_keep, back_low)
norm_eps = 1e-06
gate_scale = 8.0
beta_one = 0.9
beta_two = 0.95
learn_rate = 0.01
weight_decay = 0.1
adam_eps = 1e-08
corr_one = 1.0 - beta_one ** 10.0
corr_two = 1.0 - beta_two ** 10.0
shard_dims = (2, 1, 0, 2, 0, 1, 1, 0, 1)
highest = lax.Precision.HIGHEST

def rms_scale(values, gain):
    return values * lax.rsqrt(lax.optimization_barrier(jnp.mean(values * values, axis=-1, keepdims=True)) + norm_eps) * gain

def conv_mix(signal, taps, position):
    result = taps[-1] + taps[0] * signal
    for shift_by in range(1, taps.shape[0] - 1):
        moved = jnp.pad(signal, ((shift_by, 0), (0, 0)))[:-shift_by]
        result = result + taps[shift_by] * jnp.where((position >= shift_by)[:, None], moved, 0.0)
    return result

def combine_steps(earlier, later):
    decay_first, value_first = earlier
    decay_second, value_second = later
    return (decay_first * decay_second, decay_second * value_first + value_second)

def recurrence(logits, signal, branch, bias_term, decay_term, position):
    row_count = signal.shape[0]
    recur_gate = jax.nn.sigmoid(logits[0].reshape(row_count, -1) + bias_term[0])
    input_gate = jax.nn.sigmoid(logits[1].reshape(row_count, -1) + bias_term[1])
    log_decay = -gate_scale * recur_gate * jax.nn.softplus(-decay_term)
    decay_rate = jnp.where((position > 0)[:, None], jnp.exp(log_decay), 0.0)
    drive_term = jnp.sqrt(-jnp.expm1(2.0 * log_decay)) * input_gate * signal
    states = lax.associative_scan(combine_steps, (decay_rate, drive_term), axis=0)[1]
    return states * jax.nn.gelu(branch)

def gated_gelu(ffn_pre):
    return jax.nn.gelu(ffn_pre[0]) * ffn_pre[1]

def split_flat(gradient, split_dim, piece_count):
    return jnp.stack(jnp.split(gradient, piece_count, axis=split_dim), 0).reshape(piece_count, -1)

def forward_block(stream, params, position, mask_rows):
    input_proj, gate_blocks, output_proj, ffn_gate_up, ffn_down, conv_taps, gate_bias, decay_param, norm_gains = params
    mix_in = low(rms_scale(stream, norm_gains[0]))
    projected = low_back(jnp.einsum('sd,kdr->ksr', mix_in, input_proj, precision=highest, preferred_element_type=jnp.float32))
    conv_out = conv_mix(projected[0], conv_taps, position)
    conv_low = low(conv_out)
    row_count = conv_out.shape[0]
    blocked = conv_low.reshape(row_count, gate_blocks.shape[1], gate_blocks.shape[2])
    gate_logits = low_back(jnp.einsum('shb,khbc->kshc', blocked, gate_blocks, precision=highest, preferred_element_type=jnp.float32))
    mixed_low = low(recurrence(gate_logits, conv_out, projected[1], gate_bias, decay_param, position))
    residual = stream + low_back(jnp.dot(mixed_low, output_proj, precision=highest, preferred_element_type=jnp.float32))
    ffn_in_low = low(rms_scale(residual, norm_gains[1]))
    ffn_pre = low_back(jnp.einsum('sd,kdf->ksf', ffn_in_low, ffn_gate_up, precision=highest, preferred_element_type=jnp.float32))
    ffn_low = low(gated_gelu(ffn_pre))
    ffn_result = low_back(jnp.dot(ffn_low, ffn_down, precision=highest, preferred_element_type=jnp.float32))
    return mask_rows * (residual + ffn_result)

def reference(tokens, cotangent, seq_start, live_mask, input_proj, gate_blocks, output_proj, ffn_gate_up, ffn_down, conv_taps, gate_bias, decay_param, norm_gains, master_shard, first_moment, second_moment):
    params = tuple((weight.astype(jnp.float32) for weight in (input_proj, gate_blocks, output_proj, ffn_gate_up, ffn_down, conv_taps, gate_bias, decay_param, norm_gains)))
    streams = tokens.astype(jnp.float32).reshape(DEVICES, SLOTS, D)
    cotangents = cotangent.astype(jnp.float32).reshape(DEVICES, SLOTS, D)
    starts = seq_start.reshape(DEVICES, SLOTS)
    lives = live_mask.reshape(DEVICES, SLOTS)

    def one_block(carry, item):
        stream, block_cot, start_row, live_row = item
        position = jnp.arange(SLOTS, dtype=jnp.int32) - start_row.astype(jnp.int32)
        mask_rows = live_row.astype(jnp.float32)[:, None]

        def run(stream_in, *weights):
            return forward_block(stream_in, weights, position, mask_rows)
        result, pull = jax.vjp(run, stream, *params)
        grads = pull(block_cot)
        totals = tuple((total + grad for total, grad in zip(carry, grads[1:])))
        return (totals, (result.astype(jnp.bfloat16), grads[0].astype(jnp.bfloat16)))
    zeros = tuple((jnp.zeros(weight.shape, jnp.float32) for weight in params))
    totals, (outputs, input_grads) = lax.scan(one_block, zeros, (streams, cotangents, starts, lives))
    weight_grads = jnp.concatenate([split_flat(grad, dim, N_SHARD) for grad, dim in zip(totals, shard_dims)], axis=1)
    new_first = beta_one * first_moment + (1.0 - beta_one) * weight_grads
    new_second = beta_two * second_moment + (1.0 - beta_two) * weight_grads * weight_grads
    new_master = master_shard - learn_rate * (new_first / corr_one / (jnp.sqrt(new_second / corr_two) + adam_eps) + weight_decay * master_shard)
    new_weights = new_master.astype(jnp.bfloat16)
    return (outputs.reshape(TOKENS, D), input_grads.reshape(TOKENS, D), weight_grads, new_master, new_first, new_second, new_weights, totals[6])
```

```python
import functools
import jax
import jax.numpy as jnp
from jax import lax
from jax.experimental import pallas as pl
from jax.experimental.pallas import tpu as pltpu
from jax.sharding import PartitionSpec as P

norm_eps = 1e-06
gate_scale = 8.0
beta_one = 0.9
beta_two = 0.95
learn_rate = 0.01
weight_decay = 0.1
adam_eps = 1e-08
corr_one = 1.0 - beta_one**10.0
corr_two = 1.0 - beta_two**10.0
low_type = jnp.bfloat16
wide = jnp.float32
axes = ("dp", "shard")
gelu_scale = 0.7978845608028654
gelu_cube = 0.044715


def device_pairs(target):
    found = []
    for chip in range(4):
        for core in range(2):
            for z in range(4):
                to = target(chip, core, z)
                if to is not None:
                    source = (chip * 2 + core) * 4 + z
                    found.append((source, (to[0] * 2 + to[1]) * 4 + to[2]))
    return found


def line_pairs(moves):
    moves = dict(moves)

    def target(chip, core, z):
        end = z if core == 0 else 3 - z
        if end not in moves:
            return None
        to = moves[end]
        return (chip, core, to if core == 0 else 3 - to)

    return device_pairs(target)


def step_pairs(step):
    return device_pairs(
        lambda chip, core, z: (chip, core, z + step) if 0 <= z + step < 4 else None
    )


def plane_pairs(flip, owners_only=False):
    return device_pairs(
        lambda chip, core, z: None if owners_only and core != z // 2 else (chip ^ flip, core, z)
    )


core_pairs = device_pairs(lambda chip, core, z: (chip, 1 - core, z))
owner_core_pairs = device_pairs(
    lambda chip, core, z: (chip, 1 - core, z) if core == z // 2 else None
)


def move(value, pairs):
    return lax.ppermute(value, axes, pairs)


def plane_gather(value, dim=0, owners_only=False):
    half = value.shape[dim] // 2
    across_x = move(value, plane_pairs(1, owners_only))
    across_y = move(value, plane_pairs(2, owners_only))
    first = lax.slice_in_dim(across_x, 0, half, axis=dim)
    second = lax.slice_in_dim(across_y, half, 2 * half, axis=dim)
    first = move(first, plane_pairs(2, owners_only))
    second = move(second, plane_pairs(1, owners_only))
    return (value, across_x, across_y, jnp.concatenate([first, second], axis=dim))


def plane_reduce(parts):
    slots = parts.shape[0] // 4
    half = slots // 2
    mine, for_x, for_y, for_d = (
        parts[number * slots : (number + 1) * slots] for number in range(4)
    )
    top = slice(0, half)
    low = slice(half, slots)
    from_x = move(jnp.concatenate([for_x[top], for_d[top]]), plane_pairs(1))
    from_y = move(jnp.concatenate([for_y[low], for_d[low]]), plane_pairs(2))
    send_y = (for_y[top].astype(wide) + from_x[half:].astype(wide)).astype(low_type)
    send_x = (for_x[low].astype(wide) + from_y[half:].astype(wide)).astype(low_type)
    last_top = move(send_y, plane_pairs(2))
    last_low = move(send_x, plane_pairs(1))
    return jnp.concatenate(
        [
            mine[top].astype(wide) + from_x[:half].astype(wide) + last_top.astype(wide),
            mine[low].astype(wide) + from_y[:half].astype(wide) + last_low.astype(wide),
        ]
    )


def pick(end, choices):
    result = choices[3]
    for number in (2, 1, 0):
        result = jnp.where(end == number, choices[number], result)
    return result


def line_spread(own, end):
    ahead = move(own, line_pairs({0: 1, 1: 2}))
    back = move(own, line_pairs({1: 0}))
    ahead_two = move(ahead, line_pairs({1: 2, 2: 3}))
    ahead_three = move(ahead_two, line_pairs({2: 3}))
    return (
        pick(end, [own, ahead, ahead_two, ahead_three]),
        pick(end, [back, own, ahead, ahead_two]),
    )


def add_low(left, right):
    return (left.astype(wide) + right.astype(wide)).astype(low_type)


def line_sum(outer, inner, end):
    first = add_low(outer, move(outer, line_pairs({3: 2})))
    inner_one = add_low(inner, move(inner, line_pairs({3: 2, 0: 1})))
    second = add_low(outer, move(first, line_pairs({2: 1})))
    inner_two = add_low(inner_one, move(inner_one, line_pairs({2: 1})))
    third = add_low(outer, move(second, line_pairs({1: 0})))
    return jnp.where(end == 0, third, inner_two)


def dot_rows(left, right):
    return lax.dot_general(left, right, (((1,), (1,)), ((), ())), preferred_element_type=wide)


def dot_plain(left, right):
    return lax.dot_general(left, right, (((1,), (0,)), ((), ())), preferred_element_type=wide)


def dot_slots(left, right):
    return lax.dot_general(left, right, (((0,), (0,)), ((), ())), preferred_element_type=wide)


def gelu_parts(value):
    square = value * value
    bent = jnp.tanh(gelu_scale * value * (1.0 + gelu_cube * square))
    half = 0.5 * (1.0 + bent)
    slope = half + 0.5 * value * (1.0 - bent * bent) * gelu_scale * (
        1.0 + 3.0 * gelu_cube * square
    )
    return (value * half, slope)


def shift_down(value, step):
    if step % 8 == 0:
        return jnp.concatenate([value[-step:], value[:-step]], axis=0)
    return pltpu.roll(value, step, 0)


def shift_up(value, step):
    if step % 8 == 0:
        return jnp.concatenate([value[step:], value[:step]], axis=0)
    return pltpu.roll(value, value.shape[0] - step, 0)


def scan_slots(decay, value, shift):
    step = 1
    while step < value.shape[0]:
        value = value + decay * shift(value, step)
        if 2 * step < value.shape[0]:
            decay = decay * shift(decay, step)
        step *= 2
    return value


def one_minus_exp(value):
    series = jnp.ones_like(value)
    for number in range(11, 1, -1):
        series = 1.0 - value * (1.0 / number) * series
    return jnp.where(value < 0.8, value * series, 1.0 - jnp.exp(-value))


def soft_plus(value):
    return jnp.maximum(value, 0.0) + jnp.log1p(jnp.exp(-jnp.abs(value)))


def mixer_parts(first, position, small, gates):
    conv_out = small[4:5] + small[0:1] * first
    shifted = []
    for step in range(1, 4):
        moved = jnp.where(position >= step, shift_down(first, step), 0.0)
        shifted.append(moved)
        conv_out = conv_out + small[step : step + 1] * moved
    conv_low = conv_out.astype(low_type)
    logits = dot_plain(conv_low, gates)
    width = first.shape[1]
    recur_gate = jax.nn.sigmoid(logits[:, :width] + small[5:6])
    input_gate = jax.nn.sigmoid(logits[:, width:] + small[6:7])
    rate = gate_scale * soft_plus(-small[7:8])
    log_decay = -rate * recur_gate
    decay = jnp.where(position > 0, jnp.exp(log_decay), 0.0)
    gone = one_minus_exp(-2.0 * log_decay)
    root = jnp.sqrt(gone)
    return conv_out, shifted, conv_low, recur_gate, input_gate, rate, decay, gone, root


def weight_views(w_ref, width):
    model = w_ref.shape[2] - width
    proj = w_ref[0, 0 : 2 * width, 0:model]
    out = w_ref[0, 2 * width : 3 * width, 0:model]
    gates = jnp.concatenate(
        [w_ref[0, 0:width, model:], w_ref[0, width : 2 * width, model:]], axis=1
    )
    small = w_ref[0, 2 * width : 2 * width + 16, model:].astype(wide)
    return proj, out, gates, small


def mixer_forward_kernel(width, x_ref, pos_ref, w_ref, out_ref, p_ref, state_ref, low_ref, acc_ref):
    head = pl.program_id(0)
    block = pl.program_id(1)
    slots = x_ref.shape[0]
    proj, out, gates, small = weight_views(w_ref, width)
    position = pos_ref[...]
    projected = dot_rows(x_ref[...], proj)
    p_ref[0] = projected
    conv_out, _, _, _, input_gate, _, decay, _, root = mixer_parts(
        projected[:, :width], position, small, gates
    )
    states = scan_slots(decay, root * input_gate * conv_out, shift_down)
    state_ref[0] = states
    mixed_low = (states * gelu_parts(projected[:, width:])[0]).astype(low_type)
    low_ref[0] = mixed_low
    part = dot_plain(mixed_low, out)
    rows = pl.ds(pl.multiple_of(block * slots, slots), slots)

    @pl.when(head == 0)
    def _():
        acc_ref[rows, :] = part

    @pl.when(head > 0)
    def _():
        acc_ref[rows, :] += part

    @pl.when(head == pl.num_programs(0) - 1)
    def _():
        out_ref[rows, :] = acc_ref[rows, :].astype(low_type)


def mix_forward(mix_in, position, weights, slots, width):
    rows, model = mix_in.shape
    heads = weights.shape[0]
    blocks = rows // slots
    return pl.pallas_call(
        functools.partial(mixer_forward_kernel, width),
        grid=(heads, blocks),
        in_specs=[
            pl.BlockSpec((slots, model), lambda h, b: (b, 0)),
            pl.BlockSpec((slots, 1), lambda h, b: (b, 0)),
            pl.BlockSpec((1,) + weights.shape[1:], lambda h, b: (h, 0, 0)),
        ],
        out_specs=[
            pl.BlockSpec((rows, model), lambda h, b: (0, 0)),
            pl.BlockSpec((1, slots, 2 * width), lambda h, b: (h, b, 0)),
            pl.BlockSpec((1, slots, width), lambda h, b: (h, b, 0)),
            pl.BlockSpec((1, slots, width), lambda h, b: (h, b, 0)),
        ],
        out_shape=[
            jax.ShapeDtypeStruct((rows, model), low_type),
            jax.ShapeDtypeStruct((heads, rows, 2 * width), wide),
            jax.ShapeDtypeStruct((heads, rows, width), wide),
            jax.ShapeDtypeStruct((heads, rows, width), low_type),
        ],
        scratch_shapes=[pltpu.VMEM((rows, model), wide)],
        compiler_params=pltpu.CompilerParams(vmem_limit_bytes=48 * 1024 * 1024),
        cost_estimate=pl.CostEstimate(
            flops=2 * rows * model * heads * width * 3,
            bytes_accessed=heads * rows * width * 14 + weights.size * 2 + rows * model * 4,
            transcendentals=heads * rows * width * 6,
        ),
        name="mixer_forward",
    )(mix_in, position, weights)


def mixer_backward_kernel(
    width,
    x_ref,
    res_ref,
    pos_ref,
    w_ref,
    p_ref,
    state_ref,
    low_ref,
    grad_ref,
    gin_ref,
    acc_w,
    acc_in,
):
    head = pl.program_id(0)
    block = pl.program_id(1)
    slots, model = x_ref.shape
    proj, out, gates, small = weight_views(w_ref, width)
    position = pos_ref[...]
    first = p_ref[0, :, 0:width]
    res_low = res_ref[...]
    states = state_ref[0]
    conv_out, shifted, conv_low, recur_gate, input_gate, rate, decay, gone, root = mixer_parts(
        first, position, small, gates
    )
    grad_mixed = dot_rows(res_low, out)
    active, slope = gelu_parts(p_ref[0, :, width:])
    grad_second = grad_mixed * states * slope
    adjoint = scan_slots(shift_up(decay, 1), grad_mixed * active, shift_up)
    grad_decay = adjoint * shift_down(states, 1)
    grad_root = adjoint * input_gate * conv_out
    grad_input_gate = adjoint * root * conv_out
    grad_conv = adjoint * root * input_gate
    grad_log = grad_decay * decay - grad_root * (1.0 - gone) / root
    grad_recur = -rate * grad_log
    grad_logit_a = grad_recur * recur_gate * (1.0 - recur_gate)
    grad_logit_b = grad_input_gate * input_gate * (1.0 - input_gate)
    grad_param = jnp.sum(grad_log * recur_gate, axis=0, keepdims=True) * (
        gate_scale * jax.nn.sigmoid(-small[7:8])
    )
    logits_low = jnp.concatenate([grad_logit_a, grad_logit_b], axis=1).astype(low_type)
    grad_conv = grad_conv + dot_rows(logits_low, gates)
    grad_gates = dot_slots(conv_low, logits_low)
    sums = [jnp.sum(grad_conv * first, axis=0, keepdims=True)]
    grad_first = small[0:1] * grad_conv
    for step in range(1, 4):
        sums.append(jnp.sum(grad_conv * shifted[step - 1], axis=0, keepdims=True))
        kept = jnp.where(position >= step, grad_conv, 0.0)
        grad_first = grad_first + small[step : step + 1] * shift_up(kept, step)
    sums.append(jnp.sum(grad_conv, axis=0, keepdims=True))
    sums.append(jnp.sum(grad_logit_a, axis=0, keepdims=True))
    sums.append(jnp.sum(grad_logit_b, axis=0, keepdims=True))
    sums.append(grad_param)
    grad_small = jnp.concatenate(sums, axis=0)
    proj_low = jnp.concatenate([grad_first, grad_second], axis=1).astype(low_type)
    part = dot_plain(proj_low, proj)
    rows = pl.ds(pl.multiple_of(block * slots, slots), slots)

    @pl.when(block == 0)
    def _():
        acc_w[...] = jnp.zeros_like(acc_w)

    acc_w[0 : 2 * width, 0:model] += dot_slots(proj_low, x_ref[...])
    acc_w[2 * width : 3 * width, 0:model] += dot_slots(low_ref[0], res_low)
    acc_w[0:width, model:] += grad_gates[:, :width]
    acc_w[width : 2 * width, model:] += grad_gates[:, width:]
    acc_w[2 * width : 2 * width + 8, model:] += grad_small

    @pl.when(head == 0)
    def _():
        acc_in[rows, :] = part

    @pl.when(head > 0)
    def _():
        acc_in[rows, :] += part

    @pl.when(block == pl.num_programs(1) - 1)
    def _():
        grad_ref[0] = acc_w[...].astype(low_type)

    @pl.when(head == pl.num_programs(0) - 1)
    def _():
        gin_ref[rows, :] = acc_in[rows, :].astype(low_type)


def mix_backward(mix_in, res_low, position, weights, saved, slots, width):
    rows, model = mix_in.shape
    heads = weights.shape[0]
    blocks = rows // slots
    return pl.pallas_call(
        functools.partial(mixer_backward_kernel, width),
        grid=(heads, blocks),
        in_specs=[
            pl.BlockSpec((slots, model), lambda h, b: (b, 0)),
            pl.BlockSpec((slots, model), lambda h, b: (b, 0)),
            pl.BlockSpec((slots, 1), lambda h, b: (b, 0)),
            pl.BlockSpec((1,) + weights.shape[1:], lambda h, b: (h, 0, 0)),
            pl.BlockSpec((1, slots, 2 * width), lambda h, b: (h, b, 0)),
            pl.BlockSpec((1, slots, width), lambda h, b: (h, b, 0)),
            pl.BlockSpec((1, slots, width), lambda h, b: (h, b, 0)),
        ],
        out_specs=[
            pl.BlockSpec((1,) + weights.shape[1:], lambda h, b: (h, 0, 0)),
            pl.BlockSpec((rows, model), lambda h, b: (0, 0)),
        ],
        out_shape=[
            jax.ShapeDtypeStruct(weights.shape, low_type),
            jax.ShapeDtypeStruct((rows, model), low_type),
        ],
        scratch_shapes=[
            pltpu.VMEM(weights.shape[1:], wide),
            pltpu.VMEM((rows, model), wide),
        ],
        compiler_params=pltpu.CompilerParams(vmem_limit_bytes=48 * 1024 * 1024),
        cost_estimate=pl.CostEstimate(
            flops=2 * rows * model * heads * width * 6,
            bytes_accessed=heads * rows * width * 14 + weights.size * 4 + rows * model * 6,
            transcendentals=heads * rows * width * 6,
        ),
        name="mixer_backward",
    )(mix_in, res_low, position, weights, *saved)


def ffn_kernel(
    x_ref, go_ref, w_ref, grad_ref, out_ref, gin_ref, acc_w, acc_out, acc_in
):
    tile = pl.program_id(0)
    block = pl.program_id(1)
    slots = x_ref.shape[0]
    x = x_ref[...]
    grad_out = go_ref[...]
    pre_gate = dot_rows(x, w_ref[0])
    pre_up = dot_rows(x, w_ref[1])
    active, slope = gelu_parts(pre_gate)
    ffn_low = (active * pre_up).astype(low_type)
    grad_act = dot_rows(grad_out, w_ref[2])
    gate_low = (grad_act * pre_up * slope).astype(low_type)
    up_low = (grad_act * active).astype(low_type)
    part_out = dot_plain(ffn_low, w_ref[2])
    part_in = dot_plain(gate_low, w_ref[0]) + dot_plain(up_low, w_ref[1])
    rows = pl.ds(pl.multiple_of(block * slots, slots), slots)

    @pl.when(block == 0)
    def _():
        acc_w[...] = jnp.zeros_like(acc_w)

    acc_w[0] += dot_slots(gate_low, x)
    acc_w[1] += dot_slots(up_low, x)
    acc_w[2] += dot_slots(ffn_low, grad_out)

    @pl.when(tile == 0)
    def _():
        acc_out[rows, :] = part_out
        acc_in[rows, :] = part_in

    @pl.when(tile > 0)
    def _():
        acc_out[rows, :] += part_out
        acc_in[rows, :] += part_in

    @pl.when(block == pl.num_programs(1) - 1)
    def _():
        grad_ref[...] = acc_w[...].astype(low_type)

    @pl.when(tile == pl.num_programs(0) - 1)
    def _():
        out_ref[rows, :] = acc_out[rows, :].astype(low_type)
        gin_ref[rows, :] = acc_in[rows, :].astype(low_type)


def ffn_both(x, grad_out, weights, slots, tile):
    rows, model = x.shape
    hidden = weights.shape[1]
    return pl.pallas_call(
        ffn_kernel,
        grid=(hidden // tile, rows // slots),
        in_specs=[
            pl.BlockSpec((slots, model), lambda j, b: (b, 0)),
            pl.BlockSpec((slots, model), lambda j, b: (b, 0)),
            pl.BlockSpec((3, tile, model), lambda j, b: (0, j, 0)),
        ],
        out_specs=[
            pl.BlockSpec((3, tile, model), lambda j, b: (0, j, 0)),
            pl.BlockSpec((rows, model), lambda j, b: (0, 0)),
            pl.BlockSpec((rows, model), lambda j, b: (0, 0)),
        ],
        out_shape=[
            jax.ShapeDtypeStruct(weights.shape, low_type),
            jax.ShapeDtypeStruct((rows, model), low_type),
            jax.ShapeDtypeStruct((rows, model), low_type),
        ],
        scratch_shapes=[
            pltpu.VMEM((3, tile, model), wide),
            pltpu.VMEM((rows, model), wide),
            pltpu.VMEM((rows, model), wide),
        ],
        compiler_params=pltpu.CompilerParams(vmem_limit_bytes=58 * 1024 * 1024),
        cost_estimate=pl.CostEstimate(
            flops=2 * rows * model * hidden * 9,
            bytes_accessed=weights.size * 4 + rows * model * 16,
            transcendentals=rows * hidden,
        ),
        name="ffn_both",
    )(x, grad_out, weights)


def piece_rows(start, length, low, high):
    return max(low - start, 0), min(high - start, length)


def build_piece(member, piece_length, sizes, mix, ffn):
    model, width, ffn_width, slice_rec, slice_ffn = sizes
    chip = member // 2
    mix = [mix[number ^ chip] for number in range(4)]
    ffn = [ffn[number ^ chip] for number in range(4)]
    low = member * piece_length
    high = low + piece_length
    parts = []
    start = 0

    def add(length, row, rows_of):
        nonlocal start
        first, last = piece_rows(start, length, low, high)
        if first < last:
            row_low, row_high = first // row, -(-last // row)
            block = rows_of(row_low, row_high)
            flat = block.reshape(-1)
            parts.append(flat[first - row_low * row : last - row_low * row])
        start += length

    def columns(source, kinds, row_low, row_high):
        found = []
        for kind in range(kinds):
            a, b = max(row_low - kind * model, 0), min(row_high - kind * model, model)
            if a < b:
                found.append(
                    jnp.concatenate([source(q, kind)[:, a:b] for q in range(4)], axis=0).T
                )
        return jnp.concatenate(found, axis=0)

    def quarter_rows(source, count, row_low, row_high):
        found = []
        for q in range(4):
            a, b = max(row_low - q * count, 0), min(row_high - q * count, count)
            if a < b:
                found.append(source(q)[a:b])
        return jnp.concatenate(found, axis=0)

    def gate_rows(row_low, row_high):
        found = []
        for number in range(8):
            kind, q = number // 4, number % 4
            a, b = max(row_low - number * width, 0), min(row_high - number * width, width)
            if a < b:
                found.append(mix[q][kind * width + a : kind * width + b, model:])
        return jnp.concatenate(found, axis=0)

    def small_rows(offset):
        return lambda a, b: jnp.concatenate(
            [mix[q][2 * width + offset + a : 2 * width + offset + b, model:] for q in range(4)],
            axis=1,
        )

    add(
        2 * model * slice_rec,
        slice_rec,
        lambda a, b: columns(lambda q, k: mix[q][k * width : (k + 1) * width, :model], 2, a, b),
    )
    add(2 * 4 * width * width, width, gate_rows)
    add(
        slice_rec * model,
        model,
        lambda a, b: quarter_rows(lambda q: mix[q][2 * width : 3 * width, :model], width, a, b),
    )
    add(2 * model * slice_ffn, slice_ffn, lambda a, b: columns(lambda q, k: ffn[q][k], 2, a, b))
    add(
        slice_ffn * model,
        model,
        lambda a, b: quarter_rows(lambda q: ffn[q][2], ffn_width, a, b),
    )
    add(5 * slice_rec, slice_rec, small_rows(0))
    add(2 * slice_rec, slice_rec, small_rows(5))
    add(slice_rec, slice_rec, small_rows(7))
    gains = 2 * (model // 4)
    add(gains, gains, lambda a, b: jnp.zeros((gains,), low_type))
    bias = jnp.concatenate(
        [mix[q][2 * width + 5 : 2 * width + 7, model:] for q in range(4)], axis=1
    )
    return jnp.concatenate(parts).astype(wide), bias.astype(wide)


def group_body(
    tokens,
    cotangent,
    seq_start,
    live_mask,
    input_proj,
    gate_blocks,
    output_proj,
    ffn_gate_up,
    ffn_down,
    conv_taps,
    gate_bias,
    decay_param,
    norm_gains,
    master_shard,
    first_moment,
    second_moment,
):
    slots, model = tokens.shape
    slice_rec = input_proj.shape[2]
    slice_ffn = ffn_down.shape[0]
    width = slice_rec // 4
    ffn_width = slice_ffn // 4
    piece_length = master_shard.shape[1]
    member = lax.axis_index("dp")
    chip = member // 2
    core = member % 2
    z = lax.axis_index("shard")
    end = jnp.where(core == 0, z, 3 - z)

    mask_rows = live_mask.astype(wide)[:, None]
    stream = tokens.astype(wide)
    grad_stream = cotangent.astype(wide) * mask_rows

    def quarter(value, dim, count):
        return lax.dynamic_slice_in_dim(value, chip * count, count, axis=dim)

    own_proj = quarter(input_proj, 2, width).transpose(0, 2, 1).reshape(2 * width, model)
    own_out = quarter(output_proj, 0, width)
    own_gates = quarter(gate_blocks, 1, 1).reshape(2 * width, width)
    own_small = jnp.concatenate(
        [
            quarter(conv_taps, 1, width),
            quarter(gate_bias, 1, width),
            quarter(decay_param[None], 1, width),
            jnp.zeros((width - 8, width), low_type),
        ]
    )
    own_mix = jnp.concatenate(
        [
            jnp.concatenate([own_proj, own_out]),
            jnp.concatenate([own_gates, own_small]),
        ],
        axis=1,
    )
    own_ffn = jnp.concatenate(
        [
            quarter(ffn_gate_up, 2, ffn_width).transpose(0, 2, 1),
            quarter(ffn_down, 0, ffn_width)[None],
        ]
    )

    gains = lax.all_gather(norm_gains, "shard", axis=1, tiled=True).astype(wide)

    start_row = jnp.zeros((16, model), low_type).at[0, :slots].set(seq_start.astype(low_type))
    gathered = plane_gather(jnp.concatenate([tokens, start_row]))
    starts = jnp.stack([block[slots, :slots] for block in gathered]).astype(jnp.int32)
    position = (jnp.arange(slots, dtype=jnp.int32)[None] - starts).reshape(-1, 1)
    all_tokens = jnp.concatenate([block[:slots] for block in gathered])
    mix_in = rms_scale(all_tokens.astype(wide), gains[0]).astype(low_type)

    mix_a, mix_b = line_spread(own_mix, end)
    mix_pair = jnp.stack([mix_a, mix_b])
    mix_weights = jnp.concatenate([mix_pair, move(mix_pair, core_pairs)])

    ffn_a, ffn_b = line_spread(own_ffn, end)
    ffn_pair = jnp.concatenate([ffn_a, ffn_b], axis=1)
    ffn_weights = jnp.concatenate([ffn_pair, move(ffn_pair, core_pairs)], axis=1)

    all_grad_out = jnp.concatenate(plane_gather(grad_stream.astype(low_type)))

    mix_part, *saved = mix_forward(mix_in, position, mix_weights, slots, width)
    residual = stream + plane_reduce(mix_part)
    normed_two, second_pull = jax.vjp(rms_scale, residual, gains[1])
    ffn_in = jnp.concatenate(plane_gather(normed_two.astype(low_type)))

    grad_ffn, ffn_part, ffn_in_part = ffn_both(
        ffn_in, all_grad_out, ffn_weights, slots, ffn_width * 4 // 3
    )
    grad_norm_two, grad_gain_two = second_pull(plane_reduce(ffn_in_part))
    grad_residual = grad_stream + grad_norm_two
    res_low = jnp.concatenate(plane_gather(grad_residual.astype(low_type)))
    block_out = (mask_rows * (residual + plane_reduce(ffn_part))).astype(low_type)

    grad_mix, mix_in_part = mix_backward(
        mix_in, res_low, position, mix_weights, saved, slots, width
    )
    _, norm_pull = jax.vjp(rms_scale, stream, gains[0])
    grad_norm_one, grad_gain_one = norm_pull(plane_reduce(mix_in_part))
    tokens_grad = (grad_residual + grad_norm_one).astype(low_type)

    both = 2 * ffn_width
    pair_ffn = add_low(grad_ffn[:, :both], move(grad_ffn[:, both:], core_pairs))
    sum_ffn = line_sum(pair_ffn[:, :ffn_width], pair_ffn[:, ffn_width:], end)
    pair_mix = add_low(grad_mix[:2], move(grad_mix[2:], core_pairs))
    sum_mix = line_sum(pair_mix[0], pair_mix[1], end)
    owner = core == z // 2

    def share(total, dim):
        four = jnp.stack(plane_gather(total, dim, owners_only=True))
        return jnp.where(owner, four, move(four, owner_core_pairs))

    four_ffn = share(sum_ffn, 1)
    four_mix = share(sum_mix, 0)
    sizes = (model, width, ffn_width, slice_rec, slice_ffn)
    piece, bias_total = lax.switch(
        member,
        [
            functools.partial(build_piece, number, piece_length, sizes)
            for number in range(8)
        ],
        four_mix,
        four_ffn,
    )
    gain_total = lax.psum(jnp.stack([grad_gain_one, grad_gain_two]), axes)
    gain_slice = lax.dynamic_slice_in_dim(gain_total, z * (model // 4), model // 4, axis=1)
    gain_flat = gain_slice.reshape(-1)
    tail = jnp.where(member == 7, gain_flat, piece[-gain_flat.shape[0] :])
    piece = jnp.concatenate([piece[: -gain_flat.shape[0]], tail]).reshape(1, -1)

    new_first = beta_one * first_moment + (1.0 - beta_one) * piece
    new_second = beta_two * second_moment + (1.0 - beta_two) * piece * piece
    new_master = master_shard - learn_rate * (
        new_first / corr_one / (jnp.sqrt(new_second / corr_two) + adam_eps)
        + weight_decay * master_shard
    )
    own = new_master.astype(low_type).reshape(-1)
    right = [own]
    left = [own]
    for _ in range(3):
        right.append(move(right[-1], step_pairs(1)))
        left.append(move(left[-1], step_pairs(-1)))
    new_weights = jnp.stack(
        [
            pick(z, [right[at - target] if at >= target else left[target - at] for at in range(4)])
            for target in range(4)
        ]
    )
    return (
        block_out,
        tokens_grad,
        piece,
        new_master,
        new_first,
        new_second,
        new_weights,
        bias_total,
    )


def rms_scale(values, gain):
    return values * lax.rsqrt(jnp.mean(values * values, axis=-1, keepdims=True) + norm_eps) * gain


def conv_mix(signal, taps, position):
    result = taps[-1] + taps[0] * signal
    for shift_by in range(1, taps.shape[0] - 1):
        moved = jnp.pad(signal, ((shift_by, 0), (0, 0)))[:-shift_by]
        result = result + taps[shift_by] * jnp.where((position >= shift_by)[:, None], moved, 0.0)
    return result


def combine_steps(earlier, later):
    decay_first, value_first = earlier
    decay_second, value_second = later
    return (decay_first * decay_second, decay_second * value_first + value_second)


def recurrence(logits, signal, branch, bias_term, decay_term, position):
    row_count = signal.shape[0]
    recur_gate = jax.nn.sigmoid(logits[0].reshape(row_count, -1) + bias_term[0])
    input_gate = jax.nn.sigmoid(logits[1].reshape(row_count, -1) + bias_term[1])
    log_decay = -gate_scale * recur_gate * jax.nn.softplus(-decay_term)
    decay_rate = jnp.where((position > 0)[:, None], jnp.exp(log_decay), 0.0)
    drive_term = jnp.sqrt(-jnp.expm1(2.0 * log_decay)) * input_gate * signal
    states = lax.associative_scan(combine_steps, (decay_rate, drive_term), axis=0)[1]
    return states * jax.nn.gelu(branch)


def gated_gelu(ffn_pre):
    return jax.nn.gelu(ffn_pre[0]) * ffn_pre[1]


def mixer_forward(
    mix_in, input_proj, gate_blocks, output_proj, conv_taps, gate_bias, decay_param, position
):
    projected = jnp.einsum("sd,kdr->ksr", mix_in, input_proj, preferred_element_type=jnp.float32)
    conv_out, conv_pull = jax.vjp(
        lambda signal, taps: conv_mix(signal, taps, position), projected[0], conv_taps
    )
    row_count = conv_out.shape[0]
    conv_low = conv_out.astype(jnp.bfloat16).reshape(
        row_count, gate_blocks.shape[1], gate_blocks.shape[2]
    )
    gate_logits = jnp.einsum(
        "shb,khbc->kshc", conv_low, gate_blocks, preferred_element_type=jnp.float32
    )
    mixed, mix_pull = jax.vjp(
        lambda logits, signal, branch, bias_term, decay_term: recurrence(
            logits, signal, branch, bias_term, decay_term, position
        ),
        gate_logits,
        conv_out,
        projected[1],
        gate_bias,
        decay_param,
    )
    mixed_low = mixed.astype(jnp.bfloat16)
    partial_out = jnp.dot(mixed_low, output_proj, preferred_element_type=jnp.float32)
    return (partial_out, (conv_pull, conv_low, mix_pull, mixed_low))


def mixer_backward(grad_out_low, mix_in, saved, input_proj, gate_blocks, output_proj):
    conv_pull, conv_low, mix_pull, mixed_low = saved
    grad_output_proj = jnp.einsum(
        "sr,sd->rd", mixed_low, grad_out_low, preferred_element_type=jnp.float32
    )
    grad_mixed = jnp.einsum(
        "sd,rd->sr", grad_out_low, output_proj, preferred_element_type=jnp.float32
    )
    grad_logits, grad_conv_direct, grad_branch, grad_bias, grad_decay = mix_pull(grad_mixed)
    logits_low = grad_logits.astype(jnp.bfloat16)
    grad_blocks = jnp.einsum(
        "shb,kshc->khbc", conv_low, logits_low, preferred_element_type=jnp.float32
    )
    grad_conv_gates = jnp.einsum(
        "kshc,khbc->shb", logits_low, gate_blocks, preferred_element_type=jnp.float32
    )
    grad_signal, grad_taps = conv_pull(
        grad_conv_direct + grad_conv_gates.reshape(grad_conv_direct.shape)
    )
    proj_low = jnp.stack([grad_signal, grad_branch]).astype(jnp.bfloat16)
    grad_input_proj = jnp.einsum(
        "sd,ksr->kdr", mix_in, proj_low, preferred_element_type=jnp.float32
    )
    grad_mix_in = jnp.einsum(
        "ksr,kdr->sd", proj_low, input_proj, preferred_element_type=jnp.float32
    )
    return (
        grad_mix_in,
        (grad_input_proj, grad_blocks, grad_output_proj, grad_taps, grad_bias, grad_decay),
    )


def ffn_forward(ffn_in_low, ffn_gate_up, ffn_down):
    ffn_pre = jnp.einsum("sd,kdf->ksf", ffn_in_low, ffn_gate_up, preferred_element_type=jnp.float32)
    ffn_act, ffn_pull = jax.vjp(gated_gelu, ffn_pre)
    ffn_low = ffn_act.astype(jnp.bfloat16)
    partial_ffn = jnp.dot(ffn_low, ffn_down, preferred_element_type=jnp.float32)
    return (partial_ffn, (ffn_pull, ffn_low))


def ffn_backward(grad_low, ffn_in_low, saved, ffn_gate_up, ffn_down):
    ffn_pull, ffn_low = saved
    grad_down = jnp.einsum("sf,sd->fd", ffn_low, grad_low, preferred_element_type=jnp.float32)
    grad_act = jnp.einsum("sd,fd->sf", grad_low, ffn_down, preferred_element_type=jnp.float32)
    grad_pre = ffn_pull(grad_act)[0]
    pre_low = grad_pre.astype(jnp.bfloat16)
    grad_gate_up = jnp.einsum(
        "sd,ksf->kdf", ffn_in_low, pre_low, preferred_element_type=jnp.float32
    )
    grad_ffn_in = jnp.einsum(
        "ksf,kdf->sd", pre_low, ffn_gate_up, preferred_element_type=jnp.float32
    )
    return (grad_ffn_in, grad_gate_up, grad_down)


def body(
    tokens,
    cotangent,
    seq_start,
    live_mask,
    input_proj,
    gate_blocks,
    output_proj,
    ffn_gate_up,
    ffn_down,
    conv_taps,
    gate_bias,
    decay_param,
    norm_gains,
    master_shard,
    first_moment,
    second_moment,
):
    slot_count = tokens.shape[0]
    position = jnp.arange(slot_count, dtype=jnp.int32) - seq_start
    mask_rows = live_mask.astype(jnp.float32)[:, None]
    stream = tokens.astype(jnp.float32)
    grad_stream = cotangent.astype(jnp.float32) * mask_rows
    shards = (
        input_proj,
        gate_blocks,
        output_proj,
        ffn_gate_up,
        ffn_down,
        conv_taps,
        gate_bias,
        decay_param,
        norm_gains,
    )
    (
        full_in,
        full_blocks,
        full_out,
        full_up,
        full_down,
        full_taps,
        full_bias,
        full_decay,
        full_gains,
    ) = (
        lax.all_gather(shards[0], "shard", axis=2, tiled=True),
        lax.all_gather(shards[1], "shard", axis=1, tiled=True),
        lax.all_gather(shards[2], "shard", axis=0, tiled=True),
        lax.all_gather(shards[3], "shard", axis=2, tiled=True),
        lax.all_gather(shards[4], "shard", axis=0, tiled=True),
        lax.all_gather(shards[5], "shard", axis=1, tiled=True),
        lax.all_gather(shards[6], "shard", axis=1, tiled=True),
        lax.all_gather(shards[7], "shard", axis=0, tiled=True),
        lax.all_gather(shards[8], "shard", axis=1, tiled=True),
    )
    gains = full_gains.astype(jnp.float32)
    normed, norm_pull = jax.vjp(rms_scale, stream, gains[0])
    mix_in = normed.astype(jnp.bfloat16)
    mix_out, mix_saved = mixer_forward(
        mix_in,
        full_in,
        full_blocks,
        full_out,
        full_taps.astype(jnp.float32),
        full_bias.astype(jnp.float32),
        full_decay.astype(jnp.float32),
        position,
    )
    residual = stream + mix_out
    normed_two, second_pull = jax.vjp(rms_scale, residual, gains[1])
    ffn_in_low = normed_two.astype(jnp.bfloat16)
    ffn_result, ffn_saved = ffn_forward(ffn_in_low, full_up, full_down)
    block_out = (mask_rows * (residual + ffn_result)).astype(jnp.bfloat16)
    grad_ffn_in, grad_up, grad_down = ffn_backward(
        grad_stream.astype(jnp.bfloat16), ffn_in_low, ffn_saved, full_up, full_down
    )
    grad_norm_two, grad_gain_two = second_pull(grad_ffn_in)
    grad_residual = grad_stream + grad_norm_two
    grad_mix_in, mix_grads = mixer_backward(
        grad_residual.astype(jnp.bfloat16), mix_in, mix_saved, full_in, full_blocks, full_out
    )
    grad_norm_one, grad_gain_one = norm_pull(grad_mix_in)
    tokens_grad = (grad_residual + grad_norm_one).astype(jnp.bfloat16)
    grads = (
        mix_grads[0],
        mix_grads[1],
        mix_grads[2],
        grad_up,
        grad_down,
        mix_grads[3],
        mix_grads[4],
        mix_grads[5],
        jnp.stack([grad_gain_one, grad_gain_two]),
    )
    summed = (
        lax.psum_scatter(
            grads[0].astype(jnp.bfloat16), "shard", scatter_dimension=2, tiled=True
        ).astype(jnp.float32),
        lax.psum_scatter(
            grads[1].astype(jnp.bfloat16), "shard", scatter_dimension=1, tiled=True
        ).astype(jnp.float32),
        lax.psum_scatter(
            grads[2].astype(jnp.bfloat16), "shard", scatter_dimension=0, tiled=True
        ).astype(jnp.float32),
        lax.psum_scatter(
            grads[3].astype(jnp.bfloat16), "shard", scatter_dimension=2, tiled=True
        ).astype(jnp.float32),
        lax.psum_scatter(
            grads[4].astype(jnp.bfloat16), "shard", scatter_dimension=0, tiled=True
        ).astype(jnp.float32),
        lax.psum_scatter(
            grads[5].astype(jnp.bfloat16), "shard", scatter_dimension=1, tiled=True
        ).astype(jnp.float32),
        lax.psum_scatter(
            grads[6].astype(jnp.bfloat16), "shard", scatter_dimension=1, tiled=True
        ).astype(jnp.float32),
        lax.psum_scatter(
            grads[7].astype(jnp.bfloat16), "shard", scatter_dimension=0, tiled=True
        ).astype(jnp.float32),
        lax.psum_scatter(
            grads[8].astype(jnp.bfloat16), "shard", scatter_dimension=1, tiled=True
        ).astype(jnp.float32),
    )
    flat = jnp.concatenate([member.reshape(1, -1) for member in summed], axis=1)
    piece = lax.psum_scatter(flat, "dp", scatter_dimension=1, tiled=True)
    bias_total = lax.psum(summed[6], "dp")
    new_first = beta_one * first_moment + (1.0 - beta_one) * piece
    new_second = beta_two * second_moment + (1.0 - beta_two) * piece * piece
    new_master = master_shard - learn_rate * (
        new_first / corr_one / (jnp.sqrt(new_second / corr_two) + adam_eps)
        + weight_decay * master_shard
    )
    new_weights = lax.all_gather(new_master.astype(jnp.bfloat16), "shard", axis=0, tiled=True)
    return (
        block_out,
        tokens_grad,
        piece,
        new_master,
        new_first,
        new_second,
        new_weights,
        bias_total,
    )


def solution(mesh):
    fits = mesh.shape["dp"] == 8 and mesh.shape["shard"] == 4
    placed = (
        P(("dp", "shard"), None),
        P(("dp", "shard"), None),
        P(("dp", "shard")),
        P(("dp", "shard")),
        P(None, None, "shard"),
        P(None, "shard", None, None),
        P("shard", None),
        P(None, None, "shard"),
        P("shard", None),
        P(None, "shard"),
        P(None, "shard"),
        P("shard"),
        P(None, "shard"),
        P("shard", "dp"),
        P("shard", "dp"),
        P("shard", "dp"),
    )
    return jax.shard_map(
        group_body if fits else body,
        mesh=mesh,
        in_specs=placed,
        out_specs=(
            P(("dp", "shard"), None),
            P(("dp", "shard"), None),
            P("shard", "dp"),
            P("shard", "dp"),
            P("shard", "dp"),
            P("shard", "dp"),
            P(None, "dp"),
            P(None, "shard"),
        ),
        check_vma=False,
    )
```

```python
import functools
import jax
import jax.numpy as jnp
from jax import lax
from jax.experimental import pallas as pl
from jax.experimental.pallas import tpu as pltpu
from jax.sharding import PartitionSpec as P

norm_eps = 1e-06
gate_scale = 8.0
beta_one = 0.9
beta_two = 0.95
learn_rate = 0.01
weight_decay = 0.1
adam_eps = 1e-08
corr_one = 1.0 - beta_one**10.0
corr_two = 1.0 - beta_two**10.0
low_type = jnp.bfloat16
wide = jnp.float32
axes = ("dp", "shard")
gelu_scale = 0.7978845608028654
gelu_cube = 0.044715


def device_pairs(target):
    found = []
    for chip in range(4):
        for core in range(2):
            for z in range(4):
                to = target(chip, core, z)
                if to is not None:
                    source = (chip * 2 + core) * 4 + z
                    found.append((source, (to[0] * 2 + to[1]) * 4 + to[2]))
    return found


def line_pairs(moves):
    moves = dict(moves)

    def target(chip, core, z):
        end = z if core == 0 else 3 - z
        if end not in moves:
            return None
        to = moves[end]
        return (chip, core, to if core == 0 else 3 - to)

    return device_pairs(target)


def step_pairs(step):
    return device_pairs(
        lambda chip, core, z: (chip, core, z + step) if 0 <= z + step < 4 else None
    )


def plane_pairs(flip, owners_only=False):
    return device_pairs(
        lambda chip, core, z: None if owners_only and core != z // 2 else (chip ^ flip, core, z)
    )


core_pairs = device_pairs(lambda chip, core, z: (chip, 1 - core, z))
owner_core_pairs = device_pairs(
    lambda chip, core, z: (chip, 1 - core, z) if core == z // 2 else None
)


def move(value, pairs):
    return lax.ppermute(value, axes, pairs)


def plane_gather(value, dim=0, owners_only=False):
    half = value.shape[dim] // 2
    across_x = move(value, plane_pairs(1, owners_only))
    across_y = move(value, plane_pairs(2, owners_only))
    first = lax.slice_in_dim(across_x, 0, half, axis=dim)
    second = lax.slice_in_dim(across_y, half, 2 * half, axis=dim)
    first = move(first, plane_pairs(2, owners_only))
    second = move(second, plane_pairs(1, owners_only))
    return (value, across_x, across_y, jnp.concatenate([first, second], axis=dim))


def plane_reduce(parts):
    slots = parts.shape[0] // 4
    half = slots // 2
    mine, for_x, for_y, for_d = (
        parts[number * slots : (number + 1) * slots] for number in range(4)
    )
    top = slice(0, half)
    low = slice(half, slots)
    from_x = move(jnp.concatenate([for_x[top], for_d[top]]), plane_pairs(1))
    from_y = move(jnp.concatenate([for_y[low], for_d[low]]), plane_pairs(2))
    send_y = (for_y[top].astype(wide) + from_x[half:].astype(wide)).astype(low_type)
    send_x = (for_x[low].astype(wide) + from_y[half:].astype(wide)).astype(low_type)
    last_top = move(send_y, plane_pairs(2))
    last_low = move(send_x, plane_pairs(1))
    return jnp.concatenate(
        [
            mine[top].astype(wide) + from_x[:half].astype(wide) + last_top.astype(wide),
            mine[low].astype(wide) + from_y[:half].astype(wide) + last_low.astype(wide),
        ]
    )


def pick(end, choices):
    result = choices[3]
    for number in (2, 1, 0):
        result = jnp.where(end == number, choices[number], result)
    return result


def line_spread(own, end):
    ahead = move(own, line_pairs({0: 1, 1: 2}))
    back = move(own, line_pairs({1: 0}))
    ahead_two = move(ahead, line_pairs({1: 2, 2: 3}))
    ahead_three = move(ahead_two, line_pairs({2: 3}))
    return (
        pick(end, [own, ahead, ahead_two, ahead_three]),
        pick(end, [back, own, ahead, ahead_two]),
    )


def add_low(left, right):
    return (left.astype(wide) + right.astype(wide)).astype(low_type)


def line_sum(outer, inner, end):
    first = add_low(outer, move(outer, line_pairs({3: 2})))
    inner_one = add_low(inner, move(inner, line_pairs({3: 2, 0: 1})))
    second = add_low(outer, move(first, line_pairs({2: 1})))
    inner_two = add_low(inner_one, move(inner_one, line_pairs({2: 1})))
    third = add_low(outer, move(second, line_pairs({1: 0})))
    return jnp.where(end == 0, third, inner_two)


def turn_pairs(turn):
    return device_pairs(lambda chip, core, z: (chip, core, (z + turn) % 4))


def all_slices(own, z):
    found = [own] + [move(own, turn_pairs(turn)) for turn in (1, 2, 3)]
    return jnp.concatenate(
        [
            sum(jnp.where((z - at) % 4 == turn, found[turn], 0) for turn in range(4))
            for at in range(4)
        ],
        axis=-1,
    )


def shard_slices(value, z):
    size = value.shape[-1] // 4

    def part(turn):
        return lax.dynamic_slice_in_dim(value, ((z + turn) % 4) * size, size, axis=1)

    return part(0) + sum(move(part(turn), turn_pairs(turn)) for turn in (1, 2, 3))


def dot_rows(left, right):
    return lax.dot_general(left, right, (((1,), (1,)), ((), ())), preferred_element_type=wide)


def dot_plain(left, right):
    return lax.dot_general(left, right, (((1,), (0,)), ((), ())), preferred_element_type=wide)


def dot_slots(left, right):
    return lax.dot_general(left, right, (((0,), (0,)), ((), ())), preferred_element_type=wide)


def gelu_parts(value):
    square = value * value
    bent = jnp.tanh(gelu_scale * value * (1.0 + gelu_cube * square))
    half = 0.5 * (1.0 + bent)
    slope = half + 0.5 * value * (1.0 - bent * bent) * gelu_scale * (
        1.0 + 3.0 * gelu_cube * square
    )
    return (value * half, slope)


def shift_down(value, step):
    if step % 8 == 0:
        return jnp.concatenate([value[-step:], value[:-step]], axis=0)
    return pltpu.roll(value, step, 0)


def shift_up(value, step):
    if step % 8 == 0:
        return jnp.concatenate([value[step:], value[:step]], axis=0)
    return pltpu.roll(value, value.shape[0] - step, 0)


def scan_slots(decay, value, shift):
    step = 1
    while step < value.shape[0]:
        value = value + decay * shift(value, step)
        if 2 * step < value.shape[0]:
            decay = decay * shift(decay, step)
        step *= 2
    return value


def one_minus_exp(value):
    series = jnp.ones_like(value)
    for number in range(11, 1, -1):
        series = 1.0 - value * (1.0 / number) * series
    return jnp.where(value < 0.8, value * series, 1.0 - jnp.exp(-value))


def soft_plus(value):
    return jnp.maximum(value, 0.0) + jnp.log1p(jnp.exp(-jnp.abs(value)))


def mixer_parts(first, position, small, gates):
    conv_out = small[4:5] + small[0:1] * first
    shifted = []
    for step in range(1, 4):
        moved = jnp.where(position >= step, shift_down(first, step), 0.0)
        shifted.append(moved)
        conv_out = conv_out + small[step : step + 1] * moved
    conv_low = conv_out.astype(low_type)
    logits = dot_plain(conv_low, gates)
    width = first.shape[1]
    recur_gate = jax.nn.sigmoid(logits[:, :width] + small[5:6])
    input_gate = jax.nn.sigmoid(logits[:, width:] + small[6:7])
    rate = gate_scale * soft_plus(-small[7:8])
    log_decay = -rate * recur_gate
    decay = jnp.where(position > 0, jnp.exp(log_decay), 0.0)
    gone = one_minus_exp(-2.0 * log_decay)
    root = jnp.sqrt(gone)
    return conv_out, shifted, conv_low, recur_gate, input_gate, rate, decay, gone, root


def weight_views(w_ref, width):
    model = w_ref.shape[2] - width
    proj = w_ref[0, 0 : 2 * width, 0:model]
    out = w_ref[0, 2 * width : 3 * width, 0:model]
    gates = jnp.concatenate(
        [w_ref[0, 0:width, model:], w_ref[0, width : 2 * width, model:]], axis=1
    )
    small = w_ref[0, 2 * width : 2 * width + 16, model:].astype(wide)
    return proj, out, gates, small


def mixer_forward_kernel(width, x_ref, pos_ref, w_ref, out_ref, p_ref, state_ref, low_ref, acc_ref):
    head = pl.program_id(0)
    block = pl.program_id(1)
    slots = x_ref.shape[0]
    proj, out, gates, small = weight_views(w_ref, width)
    position = pos_ref[...]
    projected = dot_rows(x_ref[...], proj)
    p_ref[0] = projected
    conv_out, _, _, _, input_gate, _, decay, _, root = mixer_parts(
        projected[:, :width], position, small, gates
    )
    states = scan_slots(decay, root * input_gate * conv_out, shift_down)
    state_ref[0] = states
    mixed_low = (states * gelu_parts(projected[:, width:])[0]).astype(low_type)
    low_ref[0] = mixed_low
    part = dot_plain(mixed_low, out)
    rows = pl.ds(pl.multiple_of(block * slots, slots), slots)

    @pl.when(head == 0)
    def _():
        acc_ref[rows, :] = part

    @pl.when(head > 0)
    def _():
        acc_ref[rows, :] += part

    @pl.when(head == pl.num_programs(0) - 1)
    def _():
        out_ref[rows, :] = acc_ref[rows, :].astype(low_type)


def mix_forward(mix_in, position, weights, slots, width):
    rows, model = mix_in.shape
    heads = weights.shape[0]
    blocks = rows // slots
    return pl.pallas_call(
        functools.partial(mixer_forward_kernel, width),
        grid=(heads, blocks),
        in_specs=[
            pl.BlockSpec((slots, model), lambda h, b: (b, 0)),
            pl.BlockSpec((slots, 1), lambda h, b: (b, 0)),
            pl.BlockSpec((1,) + weights.shape[1:], lambda h, b: (h, 0, 0)),
        ],
        out_specs=[
            pl.BlockSpec((rows, model), lambda h, b: (0, 0)),
            pl.BlockSpec((1, slots, 2 * width), lambda h, b: (h, b, 0)),
            pl.BlockSpec((1, slots, width), lambda h, b: (h, b, 0)),
            pl.BlockSpec((1, slots, width), lambda h, b: (h, b, 0)),
        ],
        out_shape=[
            jax.ShapeDtypeStruct((rows, model), low_type),
            jax.ShapeDtypeStruct((heads, rows, 2 * width), wide),
            jax.ShapeDtypeStruct((heads, rows, width), wide),
            jax.ShapeDtypeStruct((heads, rows, width), low_type),
        ],
        scratch_shapes=[pltpu.VMEM((rows, model), wide)],
        compiler_params=pltpu.CompilerParams(vmem_limit_bytes=48 * 1024 * 1024),
        cost_estimate=pl.CostEstimate(
            flops=2 * rows * model * heads * width * 3,
            bytes_accessed=heads * rows * width * 14 + weights.size * 2 + rows * model * 4,
            transcendentals=heads * rows * width * 6,
        ),
        name="mixer_forward",
    )(mix_in, position, weights)


def mixer_backward_kernel(
    width,
    x_ref,
    res_ref,
    pos_ref,
    w_ref,
    p_ref,
    state_ref,
    low_ref,
    grad_ref,
    gin_ref,
    acc_w,
    acc_in,
):
    head = pl.program_id(0)
    block = pl.program_id(1)
    slots, model = x_ref.shape
    proj, out, gates, small = weight_views(w_ref, width)
    position = pos_ref[...]
    first = p_ref[0, :, 0:width]
    res_low = res_ref[...]
    states = state_ref[0]
    conv_out, shifted, conv_low, recur_gate, input_gate, rate, decay, gone, root = mixer_parts(
        first, position, small, gates
    )
    grad_mixed = dot_rows(res_low, out)
    active, slope = gelu_parts(p_ref[0, :, width:])
    grad_second = grad_mixed * states * slope
    adjoint = scan_slots(shift_up(decay, 1), grad_mixed * active, shift_up)
    grad_decay = adjoint * shift_down(states, 1)
    grad_root = adjoint * input_gate * conv_out
    grad_input_gate = adjoint * root * conv_out
    grad_conv = adjoint * root * input_gate
    grad_log = grad_decay * decay - grad_root * (1.0 - gone) / root
    grad_recur = -rate * grad_log
    grad_logit_a = grad_recur * recur_gate * (1.0 - recur_gate)
    grad_logit_b = grad_input_gate * input_gate * (1.0 - input_gate)
    grad_param = jnp.sum(grad_log * recur_gate, axis=0, keepdims=True) * (
        gate_scale * jax.nn.sigmoid(-small[7:8])
    )
    logits_low = jnp.concatenate([grad_logit_a, grad_logit_b], axis=1).astype(low_type)
    grad_conv = grad_conv + dot_rows(logits_low, gates)
    grad_gates = dot_slots(conv_low, logits_low)
    sums = [jnp.sum(grad_conv * first, axis=0, keepdims=True)]
    grad_first = small[0:1] * grad_conv
    for step in range(1, 4):
        sums.append(jnp.sum(grad_conv * shifted[step - 1], axis=0, keepdims=True))
        kept = jnp.where(position >= step, grad_conv, 0.0)
        grad_first = grad_first + small[step : step + 1] * shift_up(kept, step)
    sums.append(jnp.sum(grad_conv, axis=0, keepdims=True))
    sums.append(jnp.sum(grad_logit_a, axis=0, keepdims=True))
    sums.append(jnp.sum(grad_logit_b, axis=0, keepdims=True))
    sums.append(grad_param)
    grad_small = jnp.concatenate(sums, axis=0)
    proj_low = jnp.concatenate([grad_first, grad_second], axis=1).astype(low_type)
    part = dot_plain(proj_low, proj)
    rows = pl.ds(pl.multiple_of(block * slots, slots), slots)

    @pl.when(block == 0)
    def _():
        acc_w[...] = jnp.zeros_like(acc_w)

    acc_w[0 : 2 * width, 0:model] += dot_slots(proj_low, x_ref[...])
    acc_w[2 * width : 3 * width, 0:model] += dot_slots(low_ref[0], res_low)
    acc_w[0:width, model:] += grad_gates[:, :width]
    acc_w[width : 2 * width, model:] += grad_gates[:, width:]
    acc_w[2 * width : 2 * width + 8, model:] += grad_small

    @pl.when(head == 0)
    def _():
        acc_in[rows, :] = part

    @pl.when(head > 0)
    def _():
        acc_in[rows, :] += part

    @pl.when(block == pl.num_programs(1) - 1)
    def _():
        grad_ref[0] = acc_w[...].astype(low_type)

    @pl.when(head == pl.num_programs(0) - 1)
    def _():
        gin_ref[rows, :] = acc_in[rows, :].astype(low_type)


def mix_backward(mix_in, res_low, position, weights, saved, slots, width):
    rows, model = mix_in.shape
    heads = weights.shape[0]
    blocks = rows // slots
    return pl.pallas_call(
        functools.partial(mixer_backward_kernel, width),
        grid=(heads, blocks),
        in_specs=[
            pl.BlockSpec((slots, model), lambda h, b: (b, 0)),
            pl.BlockSpec((slots, model), lambda h, b: (b, 0)),
            pl.BlockSpec((slots, 1), lambda h, b: (b, 0)),
            pl.BlockSpec((1,) + weights.shape[1:], lambda h, b: (h, 0, 0)),
            pl.BlockSpec((1, slots, 2 * width), lambda h, b: (h, b, 0)),
            pl.BlockSpec((1, slots, width), lambda h, b: (h, b, 0)),
            pl.BlockSpec((1, slots, width), lambda h, b: (h, b, 0)),
        ],
        out_specs=[
            pl.BlockSpec((1,) + weights.shape[1:], lambda h, b: (h, 0, 0)),
            pl.BlockSpec((rows, model), lambda h, b: (0, 0)),
        ],
        out_shape=[
            jax.ShapeDtypeStruct(weights.shape, low_type),
            jax.ShapeDtypeStruct((rows, model), low_type),
        ],
        scratch_shapes=[
            pltpu.VMEM(weights.shape[1:], wide),
            pltpu.VMEM((rows, model), wide),
        ],
        compiler_params=pltpu.CompilerParams(vmem_limit_bytes=48 * 1024 * 1024),
        cost_estimate=pl.CostEstimate(
            flops=2 * rows * model * heads * width * 6,
            bytes_accessed=heads * rows * width * 14 + weights.size * 4 + rows * model * 6,
            transcendentals=heads * rows * width * 6,
        ),
        name="mixer_backward",
    )(mix_in, res_low, position, weights, *saved)


def ffn_kernel(
    x_ref, go_ref, w_ref, grad_ref, out_ref, gin_ref, acc_w, acc_out, acc_in
):
    tile = pl.program_id(0)
    block = pl.program_id(1)
    slots = x_ref.shape[0]
    x = x_ref[...]
    grad_out = go_ref[...]
    pre_gate = dot_rows(x, w_ref[0])
    pre_up = dot_rows(x, w_ref[1])
    active, slope = gelu_parts(pre_gate)
    ffn_low = (active * pre_up).astype(low_type)
    grad_act = dot_rows(grad_out, w_ref[2])
    gate_low = (grad_act * pre_up * slope).astype(low_type)
    up_low = (grad_act * active).astype(low_type)
    part_out = dot_plain(ffn_low, w_ref[2])
    part_in = dot_plain(gate_low, w_ref[0]) + dot_plain(up_low, w_ref[1])
    rows = pl.ds(pl.multiple_of(block * slots, slots), slots)

    @pl.when(block == 0)
    def _():
        acc_w[...] = jnp.zeros_like(acc_w)

    acc_w[0] += dot_slots(gate_low, x)
    acc_w[1] += dot_slots(up_low, x)
    acc_w[2] += dot_slots(ffn_low, grad_out)

    @pl.when(tile == 0)
    def _():
        acc_out[rows, :] = part_out
        acc_in[rows, :] = part_in

    @pl.when(tile > 0)
    def _():
        acc_out[rows, :] += part_out
        acc_in[rows, :] += part_in

    @pl.when(block == pl.num_programs(1) - 1)
    def _():
        grad_ref[...] = acc_w[...].astype(low_type)

    @pl.when(tile == pl.num_programs(0) - 1)
    def _():
        out_ref[rows, :] = acc_out[rows, :].astype(low_type)
        gin_ref[rows, :] = acc_in[rows, :].astype(low_type)


def ffn_both(x, grad_out, weights, slots, tile):
    rows, model = x.shape
    hidden = weights.shape[1]
    return pl.pallas_call(
        ffn_kernel,
        grid=(hidden // tile, rows // slots),
        in_specs=[
            pl.BlockSpec((slots, model), lambda j, b: (b, 0)),
            pl.BlockSpec((slots, model), lambda j, b: (b, 0)),
            pl.BlockSpec((3, tile, model), lambda j, b: (0, j, 0)),
        ],
        out_specs=[
            pl.BlockSpec((3, tile, model), lambda j, b: (0, j, 0)),
            pl.BlockSpec((rows, model), lambda j, b: (0, 0)),
            pl.BlockSpec((rows, model), lambda j, b: (0, 0)),
        ],
        out_shape=[
            jax.ShapeDtypeStruct(weights.shape, low_type),
            jax.ShapeDtypeStruct((rows, model), low_type),
            jax.ShapeDtypeStruct((rows, model), low_type),
        ],
        scratch_shapes=[
            pltpu.VMEM((3, tile, model), wide),
            pltpu.VMEM((rows, model), wide),
            pltpu.VMEM((rows, model), wide),
        ],
        compiler_params=pltpu.CompilerParams(vmem_limit_bytes=58 * 1024 * 1024),
        cost_estimate=pl.CostEstimate(
            flops=2 * rows * model * hidden * 9,
            bytes_accessed=weights.size * 4 + rows * model * 16,
            transcendentals=rows * hidden,
        ),
        name="ffn_both",
    )(x, grad_out, weights)


def tail_kernel(
    sizes,
    mix_ref,
    ffn_ref,
    gain_ref,
    master_ref,
    first_ref,
    second_ref,
    piece_ref,
    new_master_ref,
    new_first_ref,
    new_second_ref,
    weights_ref,
    bias_ref,
    grad,
    held,
    spread,
    send_sem,
    recv_sem,
):
    model, width, ffn_width, piece_length, chunks, lines, margin = sizes
    member = lax.axis_index("dp")
    z = lax.axis_index("shard")
    chip = member // 2
    step = pl.program_id(0)
    lead = 128
    start_row = (member * piece_length) // lead
    offset = (member * piece_length) % lead
    used_rows = piece_length // lead + 2
    tiles_in = 4 * width // lead
    tiles_ffn = 4 * ffn_width // lead
    tiles_model = model // lead

    def relative(q):
        return ((q // 2 + chip // 2) % 2) * 2 + (q % 2 + chip % 2) % 2

    def copy_to(origin, chunk, side, to):
        return pltpu.make_async_remote_copy(
            src_ref=held.at[origin, chunk],
            dst_ref=held.at[origin, chunk],
            send_sem=send_sem.at[side, origin, chunk],
            recv_sem=recv_sem.at[origin, chunk],
            device_id=(member, to),
            device_id_type=pl.DeviceIdType.MESH,
        )

    @pl.when(step == 0)
    def _():
        barrier = pltpu.get_barrier_semaphore()

        @pl.when(z > 0)
        def _():
            pl.semaphore_signal(
                barrier, inc=1, device_id=(member, z - 1), device_id_type=pl.DeviceIdType.MESH
            )

        @pl.when(z < 3)
        def _():
            pl.semaphore_signal(
                barrier, inc=1, device_id=(member, z + 1), device_id_type=pl.DeviceIdType.MESH
            )

        @pl.when((z == 0) | (z == 3))
        def _():
            pl.semaphore_wait(barrier, 1)

        @pl.when((z > 0) & (z < 3))
        def _():
            pl.semaphore_wait(barrier, 2)

        def clear(number, carry):
            grad[pl.ds(pl.multiple_of(number * 256, 256), 256), :] = jnp.zeros((256, lead), wide)
            return carry

        lax.fori_loop(0, grad.shape[0] // 256, clear, 0)

        def place(row, count, body):
            @pl.when((row < start_row + used_rows) & (row + count > start_row))
            def _():
                body(row - start_row + margin)

        base = 0

        def in_unit(number, carry):
            kind = number // tiles_model
            at = number % tiles_model

            def body(to):
                for q in range(4):
                    tile = mix_ref[
                        relative(q),
                        pl.ds(pl.multiple_of(kind * width, width), width),
                        pl.ds(pl.multiple_of(at * lead, lead), lead),
                    ].astype(wide)
                    grad[pl.ds(to + q, lead, stride=tiles_in), :] = tile.T

            place((kind * model + at * lead) * tiles_in, lead * tiles_in, body)
            return carry

        lax.fori_loop(0, 2 * tiles_model, in_unit, 0)
        base = 2 * model * tiles_in

        def gate_body(number, carry):
            kind = number // 4
            q = number % 4

            def body(to):
                grad[pl.ds(to, width), :] = mix_ref[
                    relative(q), pl.ds(pl.multiple_of(kind * width, width), width), model:
                ].astype(wide)

            place(2 * model * tiles_in + number * width, width, body)
            return carry

        lax.fori_loop(0, 8, gate_body, 0)
        base = base + 8 * width
        out_base = base

        def out_unit(q, carry):
            def body(to):
                for at in range(tiles_model):
                    grad[pl.ds(to + at, width, stride=tiles_model), :] = mix_ref[
                        relative(q), 2 * width : 3 * width, at * lead : (at + 1) * lead
                    ].astype(wide)

            place(out_base + q * width * tiles_model, width * tiles_model, body)
            return carry

        lax.fori_loop(0, 4, out_unit, 0)
        base = base + 4 * width * tiles_model
        up_base = base

        def up_unit(number, carry):
            kind = number // tiles_model
            at = number % tiles_model
            columns = pl.ds(pl.multiple_of(at * lead, lead), lead)

            def body(to):
                for tile in range(tiles_ffn):
                    found = []
                    row = tile * lead
                    while row < (tile + 1) * lead:
                        q = row // ffn_width
                        last = min((q + 1) * ffn_width, (tile + 1) * lead)
                        found.append(
                            ffn_ref[
                                relative(q),
                                kind,
                                row - q * ffn_width : last - q * ffn_width,
                                columns,
                            ].astype(wide)
                        )
                        row = last
                    block = found[0] if len(found) == 1 else jnp.concatenate(found, axis=0)
                    grad[pl.ds(to + tile, lead, stride=tiles_ffn), :] = block.T

            place(up_base + (kind * model + at * lead) * tiles_ffn, lead * tiles_ffn, body)
            return carry

        lax.fori_loop(0, 2 * tiles_model, up_unit, 0)
        base = base + 2 * model * tiles_ffn
        down_base = base
        third = ffn_width // 3

        def down_unit(number, carry):
            q = number // 3
            part = number % 3

            def body(to):
                for at in range(tiles_model):
                    grad[pl.ds(to + at, third, stride=tiles_model), :] = ffn_ref[
                        relative(q),
                        2,
                        pl.ds(pl.multiple_of(part * third, 16), third),
                        at * lead : (at + 1) * lead,
                    ].astype(wide)

            place(down_base + number * third * tiles_model, third * tiles_model, body)
            return carry

        lax.fori_loop(0, 12, down_unit, 0)
        small_base = base + 4 * ffn_width * tiles_model
        smalls = [
            mix_ref[relative(q), 2 * width : 2 * width + 16, model:].astype(wide)
            for q in range(4)
        ]

        def small_body(to):
            for q in range(4):
                grad[pl.ds(to + q, 8, stride=tiles_in), :] = smalls[q][:8]
            grad[pl.ds(to + 8 * tiles_in, 6), :] = gain_ref[0:6, :]

        place(small_base, 8 * tiles_in + 6, small_body)
        bias_ref[...] = jnp.concatenate([small[5:7] for small in smalls], axis=1)

    @pl.when(step < chunks)
    def _():
        row = margin + step * lines
        shift = (lead - offset) % lead
        here = pltpu.roll(grad[pl.ds(row, lines), :], shift, 1)
        after = pltpu.roll(grad[pl.ds(row + 1, lines), :], shift, 1)
        lane = lax.broadcasted_iota(jnp.int32, (lines, lead), 1)
        piece = jnp.where(lane < lead - offset, here, after).reshape(1, lines * lead)
        piece_ref[...] = piece
        new_first = beta_one * first_ref[...] + (1.0 - beta_one) * piece
        new_second = beta_two * second_ref[...] + (1.0 - beta_two) * piece * piece
        master = master_ref[...]
        new_master = master - learn_rate * (
            new_first / corr_one / (jnp.sqrt(new_second / corr_two) + adam_eps)
            + weight_decay * master
        )
        new_first_ref[...] = new_first
        new_second_ref[...] = new_second
        new_master_ref[...] = new_master
        held[z, step] = new_master.reshape(lines, lead).astype(low_type)

        @pl.when(z < 3)
        def _():
            copy_to(z, step, 0, z + 1).start()

        @pl.when(z > 0)
        def _():
            copy_to(z, step, 1, z - 1).start()

    def pass_on(origin, chunk, right):
        copy_to(origin, chunk, 0, z).wait_recv()
        if right:

            @pl.when(z < 3)
            def _():
                copy_to(origin, chunk, 0, z + 1).start()
        else:

            @pl.when(z > 0)
            def _():
                copy_to(origin, chunk, 1, z - 1).start()

    @pl.when((step >= chunks) & (step < 2 * chunks))
    def _():
        chunk = step - chunks

        @pl.when(z > 0)
        def _():
            pass_on(z - 1, chunk, True)

        @pl.when(z < 3)
        def _():
            pass_on(z + 1, chunk, False)

    @pl.when(step >= 2 * chunks)
    def _():
        chunk = step - 2 * chunks

        @pl.when(z >= 2)
        def _():
            pass_on(z - 2, chunk, True)

        @pl.when(z <= 1)
        def _():
            pass_on(z + 2, chunk, False)

        @pl.when(z == 3)
        def _():
            copy_to(0, chunk, 0, z).wait_recv()

        @pl.when(z == 0)
        def _():
            copy_to(3, chunk, 0, z).wait_recv()

        for origin in range(4):
            spread[origin * lines : (origin + 1) * lines, :] = held[origin, chunk].astype(wide)

        def line(number, carry):
            weights_ref[:, pl.ds(pl.multiple_of(number * lead, lead), lead)] = spread[
                pl.ds(number, 4, stride=lines), :
            ].astype(low_type)
            return carry

        lax.fori_loop(0, lines, line, 0, unroll=8)

    @pl.when(step == 3 * chunks - 1)
    def _():
        for origin in range(4):

            def finish(chunk, carry):
                @pl.when((origin <= z) & (z < 3))
                def _():
                    copy_to(origin, chunk, 0, z).wait_send()

                @pl.when((origin >= z) & (z > 0))
                def _():
                    copy_to(origin, chunk, 1, z).wait_send()

                return carry

            lax.fori_loop(0, chunks, finish, 0)


def tail(mix, ffn, gains, master, first, second, sizes):
    model, width, ffn_width = sizes
    piece_length = master.shape[1]
    chunks = 8
    lines = -(-piece_length // (chunks * 128 * 16)) * 16
    block = lines * 128
    margin = 1536
    rows = -(-(2 * margin + chunks * lines + 8) // 256) * 256
    packed = jax.ShapeDtypeStruct(master.shape, wide)
    whole = lambda shape: pl.BlockSpec(shape, lambda s: (0,) * len(shape))
    chunk_spec = pl.BlockSpec((1, block), lambda s: (0, jnp.minimum(s, chunks - 1)))
    once = lambda shape: pl.BlockSpec(
        shape, lambda s: (0,) * len(shape), pipeline_mode=pl.Buffered(1)
    )
    return pl.pallas_call(
        functools.partial(
            tail_kernel, (model, width, ffn_width, piece_length, chunks, lines, margin)
        ),
        grid=(3 * chunks,),
        in_specs=[once(mix.shape), once(ffn.shape), once(gains.shape)] + [chunk_spec] * 3,
        out_specs=[chunk_spec] * 4
        + [
            pl.BlockSpec((4, block), lambda s: (0, jnp.maximum(s - 2 * chunks, 0))),
            whole((2, 4 * width)),
        ],
        out_shape=[packed] * 4
        + [
            jax.ShapeDtypeStruct((4, piece_length), low_type),
            jax.ShapeDtypeStruct((2, 4 * width), wide),
        ],
        scratch_shapes=[
            pltpu.VMEM((rows, 128), wide),
            pltpu.VMEM((4, chunks, lines, 128), low_type),
            pltpu.VMEM((4 * lines, 128), wide),
            pltpu.SemaphoreType.DMA((2, 4, chunks)),
            pltpu.SemaphoreType.DMA((4, chunks)),
        ],
        compiler_params=pltpu.CompilerParams(
            collective_id=1, has_side_effects=True, vmem_limit_bytes=58 * 1024 * 1024
        ),
        cost_estimate=pl.CostEstimate(
            flops=20 * piece_length,
            bytes_accessed=40 * piece_length,
            transcendentals=piece_length,
        ),
        name="tail",
    )(mix, ffn, gains, master, first, second)


def group_body(
    tokens,
    cotangent,
    seq_start,
    live_mask,
    input_proj,
    gate_blocks,
    output_proj,
    ffn_gate_up,
    ffn_down,
    conv_taps,
    gate_bias,
    decay_param,
    norm_gains,
    master_shard,
    first_moment,
    second_moment,
):
    slots, model = tokens.shape
    slice_rec = input_proj.shape[2]
    slice_ffn = ffn_down.shape[0]
    width = slice_rec // 4
    ffn_width = slice_ffn // 4
    piece_length = master_shard.shape[1]
    member = lax.axis_index("dp")
    chip = member // 2
    core = member % 2
    z = lax.axis_index("shard")
    end = jnp.where(core == 0, z, 3 - z)

    mask_rows = live_mask.astype(wide)[:, None]
    stream = tokens.astype(wide)
    grad_stream = cotangent.astype(wide) * mask_rows

    def quarter(value, dim, count):
        return lax.dynamic_slice_in_dim(value, chip * count, count, axis=dim)

    own_proj = quarter(input_proj, 2, width).transpose(0, 2, 1).reshape(2 * width, model)
    own_out = quarter(output_proj, 0, width)
    own_gates = quarter(gate_blocks, 1, 1).reshape(2 * width, width)
    own_small = jnp.concatenate(
        [
            quarter(conv_taps, 1, width),
            quarter(gate_bias, 1, width),
            quarter(decay_param[None], 1, width),
            jnp.zeros((width - 8, width), low_type),
        ]
    )
    own_mix = jnp.concatenate(
        [
            jnp.concatenate([own_proj, own_out]),
            jnp.concatenate([own_gates, own_small]),
        ],
        axis=1,
    )
    own_ffn = jnp.concatenate(
        [
            quarter(ffn_gate_up, 2, ffn_width).transpose(0, 2, 1),
            quarter(ffn_down, 0, ffn_width)[None],
        ]
    )

    gains = all_slices(norm_gains, z).astype(wide)

    start_row = jnp.zeros((16, model), low_type).at[0, :slots].set(seq_start.astype(low_type))
    gathered = plane_gather(jnp.concatenate([tokens, start_row]))
    starts = jnp.stack([block[slots, :slots] for block in gathered]).astype(jnp.int32)
    position = (jnp.arange(slots, dtype=jnp.int32)[None] - starts).reshape(-1, 1)
    all_tokens = jnp.concatenate([block[:slots] for block in gathered])
    mix_in = rms_scale(all_tokens.astype(wide), gains[0]).astype(low_type)

    mix_a, mix_b = line_spread(own_mix, end)
    mix_pair = jnp.stack([mix_a, mix_b])
    mix_weights = jnp.concatenate([mix_pair, move(mix_pair, core_pairs)])

    ffn_a, ffn_b = line_spread(own_ffn, end)
    ffn_pair = jnp.concatenate([ffn_a, ffn_b], axis=1)
    ffn_weights = jnp.concatenate([ffn_pair, move(ffn_pair, core_pairs)], axis=1)

    all_grad_out = jnp.concatenate(plane_gather(grad_stream.astype(low_type)))

    mix_part, *saved = mix_forward(mix_in, position, mix_weights, slots, width)
    residual = stream + plane_reduce(mix_part)
    normed_two, second_pull = jax.vjp(rms_scale, residual, gains[1])
    ffn_in = jnp.concatenate(plane_gather(normed_two.astype(low_type)))

    grad_ffn, ffn_part, ffn_in_part = ffn_both(
        ffn_in, all_grad_out, ffn_weights, slots, ffn_width * 4 // 3
    )
    grad_norm_two, grad_gain_two = second_pull(plane_reduce(ffn_in_part))
    grad_residual = grad_stream + grad_norm_two
    res_low = jnp.concatenate(plane_gather(grad_residual.astype(low_type)))
    block_out = (mask_rows * (residual + plane_reduce(ffn_part))).astype(low_type)

    grad_mix, mix_in_part = mix_backward(
        mix_in, res_low, position, mix_weights, saved, slots, width
    )
    _, norm_pull = jax.vjp(rms_scale, stream, gains[0])
    grad_norm_one, grad_gain_one = norm_pull(plane_reduce(mix_in_part))
    tokens_grad = (grad_residual + grad_norm_one).astype(low_type)

    both = 2 * ffn_width
    pair_ffn = add_low(grad_ffn[:, :both], move(grad_ffn[:, both:], core_pairs))
    sum_ffn = line_sum(pair_ffn[:, :ffn_width], pair_ffn[:, ffn_width:], end)
    pair_mix = add_low(grad_mix[:2], move(grad_mix[2:], core_pairs))
    sum_mix = line_sum(pair_mix[0], pair_mix[1], end)
    owner = core == z // 2

    def share(total, dim):
        four = jnp.stack(plane_gather(total, dim, owners_only=True))
        return jnp.where(owner, four, move(four, owner_core_pairs))

    four_ffn = share(sum_ffn, 1)
    four_mix = share(sum_mix, 0)
    gain_sum = jnp.stack([grad_gain_one, grad_gain_two])
    gain_sum = gain_sum + move(gain_sum, core_pairs)
    gain_sum = gain_sum + move(gain_sum, plane_pairs(1))
    gain_sum = gain_sum + move(gain_sum, plane_pairs(2))
    gain_slice = shard_slices(gain_sum, z)
    piece, new_master, new_first, new_second, new_weights, bias_total = tail(
        four_mix,
        four_ffn,
        jnp.concatenate([gain_slice.reshape(-1, 128), jnp.zeros((2, 128), wide)]),
        master_shard,
        first_moment,
        second_moment,
        (model, width, ffn_width),
    )
    return (
        block_out,
        tokens_grad,
        piece,
        new_master,
        new_first,
        new_second,
        new_weights,
        bias_total,
    )


def rms_scale(values, gain):
    return values * lax.rsqrt(jnp.mean(values * values, axis=-1, keepdims=True) + norm_eps) * gain


def conv_mix(signal, taps, position):
    result = taps[-1] + taps[0] * signal
    for shift_by in range(1, taps.shape[0] - 1):
        moved = jnp.pad(signal, ((shift_by, 0), (0, 0)))[:-shift_by]
        result = result + taps[shift_by] * jnp.where((position >= shift_by)[:, None], moved, 0.0)
    return result


def combine_steps(earlier, later):
    decay_first, value_first = earlier
    decay_second, value_second = later
    return (decay_first * decay_second, decay_second * value_first + value_second)


def recurrence(logits, signal, branch, bias_term, decay_term, position):
    row_count = signal.shape[0]
    recur_gate = jax.nn.sigmoid(logits[0].reshape(row_count, -1) + bias_term[0])
    input_gate = jax.nn.sigmoid(logits[1].reshape(row_count, -1) + bias_term[1])
    log_decay = -gate_scale * recur_gate * jax.nn.softplus(-decay_term)
    decay_rate = jnp.where((position > 0)[:, None], jnp.exp(log_decay), 0.0)
    drive_term = jnp.sqrt(-jnp.expm1(2.0 * log_decay)) * input_gate * signal
    states = lax.associative_scan(combine_steps, (decay_rate, drive_term), axis=0)[1]
    return states * jax.nn.gelu(branch)


def gated_gelu(ffn_pre):
    return jax.nn.gelu(ffn_pre[0]) * ffn_pre[1]


def mixer_forward(
    mix_in, input_proj, gate_blocks, output_proj, conv_taps, gate_bias, decay_param, position
):
    projected = jnp.einsum("sd,kdr->ksr", mix_in, input_proj, preferred_element_type=jnp.float32)
    conv_out, conv_pull = jax.vjp(
        lambda signal, taps: conv_mix(signal, taps, position), projected[0], conv_taps
    )
    row_count = conv_out.shape[0]
    conv_low = conv_out.astype(jnp.bfloat16).reshape(
        row_count, gate_blocks.shape[1], gate_blocks.shape[2]
    )
    gate_logits = jnp.einsum(
        "shb,khbc->kshc", conv_low, gate_blocks, preferred_element_type=jnp.float32
    )
    mixed, mix_pull = jax.vjp(
        lambda logits, signal, branch, bias_term, decay_term: recurrence(
            logits, signal, branch, bias_term, decay_term, position
        ),
        gate_logits,
        conv_out,
        projected[1],
        gate_bias,
        decay_param,
    )
    mixed_low = mixed.astype(jnp.bfloat16)
    partial_out = jnp.dot(mixed_low, output_proj, preferred_element_type=jnp.float32)
    return (partial_out, (conv_pull, conv_low, mix_pull, mixed_low))


def mixer_backward(grad_out_low, mix_in, saved, input_proj, gate_blocks, output_proj):
    conv_pull, conv_low, mix_pull, mixed_low = saved
    grad_output_proj = jnp.einsum(
        "sr,sd->rd", mixed_low, grad_out_low, preferred_element_type=jnp.float32
    )
    grad_mixed = jnp.einsum(
        "sd,rd->sr", grad_out_low, output_proj, preferred_element_type=jnp.float32
    )
    grad_logits, grad_conv_direct, grad_branch, grad_bias, grad_decay = mix_pull(grad_mixed)
    logits_low = grad_logits.astype(jnp.bfloat16)
    grad_blocks = jnp.einsum(
        "shb,kshc->khbc", conv_low, logits_low, preferred_element_type=jnp.float32
    )
    grad_conv_gates = jnp.einsum(
        "kshc,khbc->shb", logits_low, gate_blocks, preferred_element_type=jnp.float32
    )
    grad_signal, grad_taps = conv_pull(
        grad_conv_direct + grad_conv_gates.reshape(grad_conv_direct.shape)
    )
    proj_low = jnp.stack([grad_signal, grad_branch]).astype(jnp.bfloat16)
    grad_input_proj = jnp.einsum(
        "sd,ksr->kdr", mix_in, proj_low, preferred_element_type=jnp.float32
    )
    grad_mix_in = jnp.einsum(
        "ksr,kdr->sd", proj_low, input_proj, preferred_element_type=jnp.float32
    )
    return (
        grad_mix_in,
        (grad_input_proj, grad_blocks, grad_output_proj, grad_taps, grad_bias, grad_decay),
    )


def ffn_forward(ffn_in_low, ffn_gate_up, ffn_down):
    ffn_pre = jnp.einsum("sd,kdf->ksf", ffn_in_low, ffn_gate_up, preferred_element_type=jnp.float32)
    ffn_act, ffn_pull = jax.vjp(gated_gelu, ffn_pre)
    ffn_low = ffn_act.astype(jnp.bfloat16)
    partial_ffn = jnp.dot(ffn_low, ffn_down, preferred_element_type=jnp.float32)
    return (partial_ffn, (ffn_pull, ffn_low))


def ffn_backward(grad_low, ffn_in_low, saved, ffn_gate_up, ffn_down):
    ffn_pull, ffn_low = saved
    grad_down = jnp.einsum("sf,sd->fd", ffn_low, grad_low, preferred_element_type=jnp.float32)
    grad_act = jnp.einsum("sd,fd->sf", grad_low, ffn_down, preferred_element_type=jnp.float32)
    grad_pre = ffn_pull(grad_act)[0]
    pre_low = grad_pre.astype(jnp.bfloat16)
    grad_gate_up = jnp.einsum(
        "sd,ksf->kdf", ffn_in_low, pre_low, preferred_element_type=jnp.float32
    )
    grad_ffn_in = jnp.einsum(
        "ksf,kdf->sd", pre_low, ffn_gate_up, preferred_element_type=jnp.float32
    )
    return (grad_ffn_in, grad_gate_up, grad_down)


def body(
    tokens,
    cotangent,
    seq_start,
    live_mask,
    input_proj,
    gate_blocks,
    output_proj,
    ffn_gate_up,
    ffn_down,
    conv_taps,
    gate_bias,
    decay_param,
    norm_gains,
    master_shard,
    first_moment,
    second_moment,
):
    slot_count = tokens.shape[0]
    position = jnp.arange(slot_count, dtype=jnp.int32) - seq_start
    mask_rows = live_mask.astype(jnp.float32)[:, None]
    stream = tokens.astype(jnp.float32)
    grad_stream = cotangent.astype(jnp.float32) * mask_rows
    shards = (
        input_proj,
        gate_blocks,
        output_proj,
        ffn_gate_up,
        ffn_down,
        conv_taps,
        gate_bias,
        decay_param,
        norm_gains,
    )
    (
        full_in,
        full_blocks,
        full_out,
        full_up,
        full_down,
        full_taps,
        full_bias,
        full_decay,
        full_gains,
    ) = (
        lax.all_gather(shards[0], "shard", axis=2, tiled=True),
        lax.all_gather(shards[1], "shard", axis=1, tiled=True),
        lax.all_gather(shards[2], "shard", axis=0, tiled=True),
        lax.all_gather(shards[3], "shard", axis=2, tiled=True),
        lax.all_gather(shards[4], "shard", axis=0, tiled=True),
        lax.all_gather(shards[5], "shard", axis=1, tiled=True),
        lax.all_gather(shards[6], "shard", axis=1, tiled=True),
        lax.all_gather(shards[7], "shard", axis=0, tiled=True),
        lax.all_gather(shards[8], "shard", axis=1, tiled=True),
    )
    gains = full_gains.astype(jnp.float32)
    normed, norm_pull = jax.vjp(rms_scale, stream, gains[0])
    mix_in = normed.astype(jnp.bfloat16)
    mix_out, mix_saved = mixer_forward(
        mix_in,
        full_in,
        full_blocks,
        full_out,
        full_taps.astype(jnp.float32),
        full_bias.astype(jnp.float32),
        full_decay.astype(jnp.float32),
        position,
    )
    residual = stream + mix_out
    normed_two, second_pull = jax.vjp(rms_scale, residual, gains[1])
    ffn_in_low = normed_two.astype(jnp.bfloat16)
    ffn_result, ffn_saved = ffn_forward(ffn_in_low, full_up, full_down)
    block_out = (mask_rows * (residual + ffn_result)).astype(jnp.bfloat16)
    grad_ffn_in, grad_up, grad_down = ffn_backward(
        grad_stream.astype(jnp.bfloat16), ffn_in_low, ffn_saved, full_up, full_down
    )
    grad_norm_two, grad_gain_two = second_pull(grad_ffn_in)
    grad_residual = grad_stream + grad_norm_two
    grad_mix_in, mix_grads = mixer_backward(
        grad_residual.astype(jnp.bfloat16), mix_in, mix_saved, full_in, full_blocks, full_out
    )
    grad_norm_one, grad_gain_one = norm_pull(grad_mix_in)
    tokens_grad = (grad_residual + grad_norm_one).astype(jnp.bfloat16)
    grads = (
        mix_grads[0],
        mix_grads[1],
        mix_grads[2],
        grad_up,
        grad_down,
        mix_grads[3],
        mix_grads[4],
        mix_grads[5],
        jnp.stack([grad_gain_one, grad_gain_two]),
    )
    summed = (
        lax.psum_scatter(
            grads[0].astype(jnp.bfloat16), "shard", scatter_dimension=2, tiled=True
        ).astype(jnp.float32),
        lax.psum_scatter(
            grads[1].astype(jnp.bfloat16), "shard", scatter_dimension=1, tiled=True
        ).astype(jnp.float32),
        lax.psum_scatter(
            grads[2].astype(jnp.bfloat16), "shard", scatter_dimension=0, tiled=True
        ).astype(jnp.float32),
        lax.psum_scatter(
            grads[3].astype(jnp.bfloat16), "shard", scatter_dimension=2, tiled=True
        ).astype(jnp.float32),
        lax.psum_scatter(
            grads[4].astype(jnp.bfloat16), "shard", scatter_dimension=0, tiled=True
        ).astype(jnp.float32),
        lax.psum_scatter(
            grads[5].astype(jnp.bfloat16), "shard", scatter_dimension=1, tiled=True
        ).astype(jnp.float32),
        lax.psum_scatter(
            grads[6].astype(jnp.bfloat16), "shard", scatter_dimension=1, tiled=True
        ).astype(jnp.float32),
        lax.psum_scatter(
            grads[7].astype(jnp.bfloat16), "shard", scatter_dimension=0, tiled=True
        ).astype(jnp.float32),
        lax.psum_scatter(
            grads[8].astype(jnp.bfloat16), "shard", scatter_dimension=1, tiled=True
        ).astype(jnp.float32),
    )
    flat = jnp.concatenate([member.reshape(1, -1) for member in summed], axis=1)
    piece = lax.psum_scatter(flat, "dp", scatter_dimension=1, tiled=True)
    bias_total = lax.psum(summed[6], "dp")
    new_first = beta_one * first_moment + (1.0 - beta_one) * piece
    new_second = beta_two * second_moment + (1.0 - beta_two) * piece * piece
    new_master = master_shard - learn_rate * (
        new_first / corr_one / (jnp.sqrt(new_second / corr_two) + adam_eps)
        + weight_decay * master_shard
    )
    new_weights = lax.all_gather(new_master.astype(jnp.bfloat16), "shard", axis=0, tiled=True)
    return (
        block_out,
        tokens_grad,
        piece,
        new_master,
        new_first,
        new_second,
        new_weights,
        bias_total,
    )


def solution(mesh):
    fits = mesh.shape["dp"] == 8 and mesh.shape["shard"] == 4
    placed = (
        P(("dp", "shard"), None),
        P(("dp", "shard"), None),
        P(("dp", "shard")),
        P(("dp", "shard")),
        P(None, None, "shard"),
        P(None, "shard", None, None),
        P("shard", None),
        P(None, None, "shard"),
        P("shard", None),
        P(None, "shard"),
        P(None, "shard"),
        P("shard"),
        P(None, "shard"),
        P("shard", "dp"),
        P("shard", "dp"),
        P("shard", "dp"),
    )
    return jax.shard_map(
        group_body if fits else body,
        mesh=mesh,
        in_specs=placed,
        out_specs=(
            P(("dp", "shard"), None),
            P(("dp", "shard"), None),
            P("shard", "dp"),
            P("shard", "dp"),
            P("shard", "dp"),
            P("shard", "dp"),
            P(None, "dp"),
            P(None, "shard"),
        ),
        check_vma=False,
    )
```

```python
import functools
import jax
import jax.numpy as jnp
from jax import lax
from jax.experimental import pallas as pl
from jax.experimental.pallas import tpu as pltpu
from jax.sharding import PartitionSpec as P

norm_eps = 1e-06
gate_scale = 8.0
beta_one = 0.9
beta_two = 0.95
learn_rate = 0.01
weight_decay = 0.1
adam_eps = 1e-08
corr_one = 1.0 - beta_one**10.0
corr_two = 1.0 - beta_two**10.0
low_type = jnp.bfloat16
wide = jnp.float32
axes = ("dp", "shard")
gelu_scale = 0.7978845608028654
gelu_cube = 0.044715


def device_pairs(target):
    found = []
    for chip in range(4):
        for core in range(2):
            for z in range(4):
                to = target(chip, core, z)
                if to is not None:
                    source = (chip * 2 + core) * 4 + z
                    found.append((source, (to[0] * 2 + to[1]) * 4 + to[2]))
    return found


def line_pairs(moves):
    moves = dict(moves)

    def target(chip, core, z):
        end = z if core == 0 else 3 - z
        if end not in moves:
            return None
        to = moves[end]
        return (chip, core, to if core == 0 else 3 - to)

    return device_pairs(target)


def step_pairs(step):
    return device_pairs(
        lambda chip, core, z: (chip, core, z + step) if 0 <= z + step < 4 else None
    )


def plane_pairs(flip, owners_only=False):
    return device_pairs(
        lambda chip, core, z: None if owners_only and core != z // 2 else (chip ^ flip, core, z)
    )


core_pairs = device_pairs(lambda chip, core, z: (chip, 1 - core, z))
owner_core_pairs = device_pairs(
    lambda chip, core, z: (chip, 1 - core, z) if core == z // 2 else None
)


def move(value, pairs):
    return lax.ppermute(value, axes, pairs)


def plane_gather(value, dim=0, owners_only=False):
    half = value.shape[dim] // 2
    across_x = move(value, plane_pairs(1, owners_only))
    across_y = move(value, plane_pairs(2, owners_only))
    first = lax.slice_in_dim(across_x, 0, half, axis=dim)
    second = lax.slice_in_dim(across_y, half, 2 * half, axis=dim)
    first = move(first, plane_pairs(2, owners_only))
    second = move(second, plane_pairs(1, owners_only))
    return (value, across_x, across_y, jnp.concatenate([first, second], axis=dim))


def plane_reduce(parts):
    slots = parts.shape[0] // 4
    half = slots // 2
    mine, for_x, for_y, for_d = (
        parts[number * slots : (number + 1) * slots] for number in range(4)
    )
    top = slice(0, half)
    low = slice(half, slots)
    from_x = move(jnp.concatenate([for_x[top], for_d[top]]), plane_pairs(1))
    from_y = move(jnp.concatenate([for_y[low], for_d[low]]), plane_pairs(2))
    send_y = (for_y[top].astype(wide) + from_x[half:].astype(wide)).astype(low_type)
    send_x = (for_x[low].astype(wide) + from_y[half:].astype(wide)).astype(low_type)
    last_top = move(send_y, plane_pairs(2))
    last_low = move(send_x, plane_pairs(1))
    return jnp.concatenate(
        [
            mine[top].astype(wide) + from_x[:half].astype(wide) + last_top.astype(wide),
            mine[low].astype(wide) + from_y[:half].astype(wide) + last_low.astype(wide),
        ]
    )


def pick(end, choices):
    result = choices[3]
    for number in (2, 1, 0):
        result = jnp.where(end == number, choices[number], result)
    return result


def line_spread(own, end):
    ahead = move(own, line_pairs({0: 1, 1: 2}))
    back = move(own, line_pairs({1: 0}))
    ahead_two = move(ahead, line_pairs({1: 2, 2: 3}))
    ahead_three = move(ahead_two, line_pairs({2: 3}))
    return (
        pick(end, [own, ahead, ahead_two, ahead_three]),
        pick(end, [back, own, ahead, ahead_two]),
    )


def add_low(left, right):
    return (left.astype(wide) + right.astype(wide)).astype(low_type)


def line_sum(outer, inner, end):
    first = add_low(outer, move(outer, line_pairs({3: 2})))
    inner_one = add_low(inner, move(inner, line_pairs({3: 2, 0: 1})))
    second = add_low(outer, move(first, line_pairs({2: 1})))
    inner_two = add_low(inner_one, move(inner_one, line_pairs({2: 1})))
    third = add_low(outer, move(second, line_pairs({1: 0})))
    return jnp.where(end == 0, third, inner_two)


def turn_pairs(turn):
    return device_pairs(lambda chip, core, z: (chip, core, (z + turn) % 4))


def all_slices(own, z):
    found = [own] + [move(own, turn_pairs(turn)) for turn in (1, 2, 3)]
    return jnp.concatenate(
        [
            sum(jnp.where((z - at) % 4 == turn, found[turn], 0) for turn in range(4))
            for at in range(4)
        ],
        axis=-1,
    )


def shard_slices(value, z):
    size = value.shape[-1] // 4

    def part(turn):
        return lax.dynamic_slice_in_dim(value, ((z + turn) % 4) * size, size, axis=1)

    return part(0) + sum(move(part(turn), turn_pairs(turn)) for turn in (1, 2, 3))


def dot_rows(left, right):
    return lax.dot_general(left, right, (((1,), (1,)), ((), ())), preferred_element_type=wide)


def dot_plain(left, right):
    return lax.dot_general(left, right, (((1,), (0,)), ((), ())), preferred_element_type=wide)


def dot_slots(left, right):
    return lax.dot_general(left, right, (((0,), (0,)), ((), ())), preferred_element_type=wide)


def gelu_parts(value):
    square = value * value
    bent = jnp.tanh(gelu_scale * value * (1.0 + gelu_cube * square))
    half = 0.5 * (1.0 + bent)
    slope = half + 0.5 * value * (1.0 - bent * bent) * gelu_scale * (
        1.0 + 3.0 * gelu_cube * square
    )
    return (value * half, slope)


def shift_down(value, step):
    if step % 8 == 0:
        return jnp.concatenate([value[-step:], value[:-step]], axis=0)
    return pltpu.roll(value, step, 0)


def shift_up(value, step):
    if step % 8 == 0:
        return jnp.concatenate([value[step:], value[:step]], axis=0)
    return pltpu.roll(value, value.shape[0] - step, 0)


def scan_slots(decay, value, shift):
    step = 1
    while step < value.shape[0]:
        value = value + decay * shift(value, step)
        if 2 * step < value.shape[0]:
            decay = decay * shift(decay, step)
        step *= 2
    return value


def one_minus_exp(value):
    series = jnp.ones_like(value)
    for number in range(11, 1, -1):
        series = 1.0 - value * (1.0 / number) * series
    return jnp.where(value < 0.8, value * series, 1.0 - jnp.exp(-value))


def soft_plus(value):
    return jnp.maximum(value, 0.0) + jnp.log1p(jnp.exp(-jnp.abs(value)))


def mixer_parts(first, position, small, gates):
    conv_out = small[4:5] + small[0:1] * first
    shifted = []
    for step in range(1, 4):
        moved = jnp.where(position >= step, shift_down(first, step), 0.0)
        shifted.append(moved)
        conv_out = conv_out + small[step : step + 1] * moved
    conv_low = conv_out.astype(low_type)
    logits = dot_plain(conv_low, gates)
    width = first.shape[1]
    recur_gate = jax.nn.sigmoid(logits[:, :width] + small[5:6])
    input_gate = jax.nn.sigmoid(logits[:, width:] + small[6:7])
    rate = gate_scale * soft_plus(-small[7:8])
    log_decay = -rate * recur_gate
    decay = jnp.where(position > 0, jnp.exp(log_decay), 0.0)
    gone = one_minus_exp(-2.0 * log_decay)
    root = jnp.sqrt(gone)
    return conv_out, shifted, conv_low, recur_gate, input_gate, rate, decay, gone, root


def weight_views(w_ref, width):
    model = w_ref.shape[2] - width
    proj = w_ref[0, 0 : 2 * width, 0:model]
    out = w_ref[0, 2 * width : 3 * width, 0:model]
    gates = jnp.concatenate(
        [w_ref[0, 0:width, model:], w_ref[0, width : 2 * width, model:]], axis=1
    )
    small = w_ref[0, 2 * width : 2 * width + 16, model:].astype(wide)
    return proj, out, gates, small


def mixer_forward_kernel(width, x_ref, pos_ref, w_ref, out_ref, p_ref, state_ref, low_ref, acc_ref):
    head = pl.program_id(0)
    block = pl.program_id(1)
    slots = x_ref.shape[0]
    proj, out, gates, small = weight_views(w_ref, width)
    position = pos_ref[...]
    projected = dot_rows(x_ref[...], proj)
    p_ref[0] = projected
    conv_out, _, _, _, input_gate, _, decay, _, root = mixer_parts(
        projected[:, :width], position, small, gates
    )
    states = scan_slots(decay, root * input_gate * conv_out, shift_down)
    state_ref[0] = states
    mixed_low = (states * gelu_parts(projected[:, width:])[0]).astype(low_type)
    low_ref[0] = mixed_low
    part = dot_plain(mixed_low, out)
    rows = pl.ds(pl.multiple_of(block * slots, slots), slots)

    @pl.when(head == 0)
    def _():
        acc_ref[rows, :] = part

    @pl.when(head > 0)
    def _():
        acc_ref[rows, :] += part

    @pl.when(head == pl.num_programs(0) - 1)
    def _():
        out_ref[rows, :] = acc_ref[rows, :].astype(low_type)


def mix_forward(mix_in, position, weights, slots, width):
    rows, model = mix_in.shape
    heads = weights.shape[0]
    blocks = rows // slots
    return pl.pallas_call(
        functools.partial(mixer_forward_kernel, width),
        grid=(heads, blocks),
        in_specs=[
            pl.BlockSpec((slots, model), lambda h, b: (b, 0)),
            pl.BlockSpec((slots, 1), lambda h, b: (b, 0)),
            pl.BlockSpec((1,) + weights.shape[1:], lambda h, b: (h, 0, 0)),
        ],
        out_specs=[
            pl.BlockSpec((rows, model), lambda h, b: (0, 0)),
            pl.BlockSpec((1, slots, 2 * width), lambda h, b: (h, b, 0)),
            pl.BlockSpec((1, slots, width), lambda h, b: (h, b, 0)),
            pl.BlockSpec((1, slots, width), lambda h, b: (h, b, 0)),
        ],
        out_shape=[
            jax.ShapeDtypeStruct((rows, model), low_type),
            jax.ShapeDtypeStruct((heads, rows, 2 * width), wide),
            jax.ShapeDtypeStruct((heads, rows, width), wide),
            jax.ShapeDtypeStruct((heads, rows, width), low_type),
        ],
        scratch_shapes=[pltpu.VMEM((rows, model), wide)],
        compiler_params=pltpu.CompilerParams(vmem_limit_bytes=48 * 1024 * 1024),
        cost_estimate=pl.CostEstimate(
            flops=2 * rows * model * heads * width * 3,
            bytes_accessed=heads * rows * width * 14 + weights.size * 2 + rows * model * 4,
            transcendentals=heads * rows * width * 6,
        ),
        name="mixer_forward",
    )(mix_in, position, weights)


def mixer_backward_kernel(
    width,
    x_ref,
    res_ref,
    pos_ref,
    w_ref,
    p_ref,
    state_ref,
    low_ref,
    grad_ref,
    gin_ref,
    acc_w,
    acc_in,
):
    head = pl.program_id(0)
    block = pl.program_id(1)
    slots, model = x_ref.shape
    proj, out, gates, small = weight_views(w_ref, width)
    position = pos_ref[...]
    first = p_ref[0, :, 0:width]
    res_low = res_ref[...]
    states = state_ref[0]
    conv_out, shifted, conv_low, recur_gate, input_gate, rate, decay, gone, root = mixer_parts(
        first, position, small, gates
    )
    grad_mixed = dot_rows(res_low, out)
    active, slope = gelu_parts(p_ref[0, :, width:])
    grad_second = grad_mixed * states * slope
    adjoint = scan_slots(shift_up(decay, 1), grad_mixed * active, shift_up)
    grad_decay = adjoint * shift_down(states, 1)
    grad_root = adjoint * input_gate * conv_out
    grad_input_gate = adjoint * root * conv_out
    grad_conv = adjoint * root * input_gate
    grad_log = grad_decay * decay - grad_root * (1.0 - gone) / root
    grad_recur = -rate * grad_log
    grad_logit_a = grad_recur * recur_gate * (1.0 - recur_gate)
    grad_logit_b = grad_input_gate * input_gate * (1.0 - input_gate)
    grad_param = jnp.sum(grad_log * recur_gate, axis=0, keepdims=True) * (
        gate_scale * jax.nn.sigmoid(-small[7:8])
    )
    logits_low = jnp.concatenate([grad_logit_a, grad_logit_b], axis=1).astype(low_type)
    grad_conv = grad_conv + dot_rows(logits_low, gates)
    grad_gates = dot_slots(conv_low, logits_low)
    sums = [jnp.sum(grad_conv * first, axis=0, keepdims=True)]
    grad_first = small[0:1] * grad_conv
    for step in range(1, 4):
        sums.append(jnp.sum(grad_conv * shifted[step - 1], axis=0, keepdims=True))
        kept = jnp.where(position >= step, grad_conv, 0.0)
        grad_first = grad_first + small[step : step + 1] * shift_up(kept, step)
    sums.append(jnp.sum(grad_conv, axis=0, keepdims=True))
    sums.append(jnp.sum(grad_logit_a, axis=0, keepdims=True))
    sums.append(jnp.sum(grad_logit_b, axis=0, keepdims=True))
    sums.append(grad_param)
    grad_small = jnp.concatenate(sums, axis=0)
    proj_low = jnp.concatenate([grad_first, grad_second], axis=1).astype(low_type)
    part = dot_plain(proj_low, proj)
    rows = pl.ds(pl.multiple_of(block * slots, slots), slots)

    @pl.when(block == 0)
    def _():
        acc_w[...] = jnp.zeros_like(acc_w)

    acc_w[0 : 2 * width, 0:model] += dot_slots(proj_low, x_ref[...])
    acc_w[2 * width : 3 * width, 0:model] += dot_slots(low_ref[0], res_low)
    acc_w[0:width, model:] += grad_gates[:, :width]
    acc_w[width : 2 * width, model:] += grad_gates[:, width:]
    acc_w[2 * width : 2 * width + 8, model:] += grad_small

    @pl.when(head == 0)
    def _():
        acc_in[rows, :] = part

    @pl.when(head > 0)
    def _():
        acc_in[rows, :] += part

    @pl.when(block == pl.num_programs(1) - 1)
    def _():
        grad_ref[0] = acc_w[...].astype(low_type)

    @pl.when(head == pl.num_programs(0) - 1)
    def _():
        gin_ref[rows, :] = acc_in[rows, :].astype(low_type)


def mix_backward(mix_in, res_low, position, weights, saved, slots, width):
    rows, model = mix_in.shape
    heads = weights.shape[0]
    blocks = rows // slots
    return pl.pallas_call(
        functools.partial(mixer_backward_kernel, width),
        grid=(heads, blocks),
        in_specs=[
            pl.BlockSpec((slots, model), lambda h, b: (b, 0)),
            pl.BlockSpec((slots, model), lambda h, b: (b, 0)),
            pl.BlockSpec((slots, 1), lambda h, b: (b, 0)),
            pl.BlockSpec((1,) + weights.shape[1:], lambda h, b: (h, 0, 0)),
            pl.BlockSpec((1, slots, 2 * width), lambda h, b: (h, b, 0)),
            pl.BlockSpec((1, slots, width), lambda h, b: (h, b, 0)),
            pl.BlockSpec((1, slots, width), lambda h, b: (h, b, 0)),
        ],
        out_specs=[
            pl.BlockSpec((1,) + weights.shape[1:], lambda h, b: (h, 0, 0)),
            pl.BlockSpec((rows, model), lambda h, b: (0, 0)),
        ],
        out_shape=[
            jax.ShapeDtypeStruct(weights.shape, low_type),
            jax.ShapeDtypeStruct((rows, model), low_type),
        ],
        scratch_shapes=[
            pltpu.VMEM(weights.shape[1:], wide),
            pltpu.VMEM((rows, model), wide),
        ],
        compiler_params=pltpu.CompilerParams(vmem_limit_bytes=48 * 1024 * 1024),
        cost_estimate=pl.CostEstimate(
            flops=2 * rows * model * heads * width * 6,
            bytes_accessed=heads * rows * width * 14 + weights.size * 4 + rows * model * 6,
            transcendentals=heads * rows * width * 6,
        ),
        name="mixer_backward",
    )(mix_in, res_low, position, weights, *saved)


def ffn_kernel(
    x_ref, go_ref, w_ref, grad_ref, out_ref, gin_ref, acc_w, acc_out, acc_in
):
    tile = pl.program_id(0)
    block = pl.program_id(1)
    slots = x_ref.shape[0]
    x = x_ref[...]
    grad_out = go_ref[...]
    pre_gate = dot_rows(x, w_ref[0])
    pre_up = dot_rows(x, w_ref[1])
    active, slope = gelu_parts(pre_gate)
    ffn_low = (active * pre_up).astype(low_type)
    grad_act = dot_rows(grad_out, w_ref[2])
    gate_low = (grad_act * pre_up * slope).astype(low_type)
    up_low = (grad_act * active).astype(low_type)
    part_out = dot_plain(ffn_low, w_ref[2])
    part_in = dot_plain(gate_low, w_ref[0]) + dot_plain(up_low, w_ref[1])
    rows = pl.ds(pl.multiple_of(block * slots, slots), slots)

    @pl.when(block == 0)
    def _():
        acc_w[...] = jnp.zeros_like(acc_w)

    acc_w[0] += dot_slots(gate_low, x)
    acc_w[1] += dot_slots(up_low, x)
    acc_w[2] += dot_slots(ffn_low, grad_out)

    @pl.when(tile == 0)
    def _():
        acc_out[rows, :] = part_out
        acc_in[rows, :] = part_in

    @pl.when(tile > 0)
    def _():
        acc_out[rows, :] += part_out
        acc_in[rows, :] += part_in

    @pl.when(block == pl.num_programs(1) - 1)
    def _():
        grad_ref[...] = acc_w[...].astype(low_type)

    @pl.when(tile == pl.num_programs(0) - 1)
    def _():
        out_ref[rows, :] = acc_out[rows, :].astype(low_type)
        gin_ref[rows, :] = acc_in[rows, :].astype(low_type)


def ffn_both(x, grad_out, weights, slots, tile):
    rows, model = x.shape
    hidden = weights.shape[1]
    return pl.pallas_call(
        ffn_kernel,
        grid=(hidden // tile, rows // slots),
        in_specs=[
            pl.BlockSpec((slots, model), lambda j, b: (b, 0)),
            pl.BlockSpec((slots, model), lambda j, b: (b, 0)),
            pl.BlockSpec((3, tile, model), lambda j, b: (0, j, 0)),
        ],
        out_specs=[
            pl.BlockSpec((3, tile, model), lambda j, b: (0, j, 0)),
            pl.BlockSpec((rows, model), lambda j, b: (0, 0)),
            pl.BlockSpec((rows, model), lambda j, b: (0, 0)),
        ],
        out_shape=[
            jax.ShapeDtypeStruct(weights.shape, low_type),
            jax.ShapeDtypeStruct((rows, model), low_type),
            jax.ShapeDtypeStruct((rows, model), low_type),
        ],
        scratch_shapes=[
            pltpu.VMEM((3, tile, model), wide),
            pltpu.VMEM((rows, model), wide),
            pltpu.VMEM((rows, model), wide),
        ],
        compiler_params=pltpu.CompilerParams(vmem_limit_bytes=58 * 1024 * 1024),
        cost_estimate=pl.CostEstimate(
            flops=2 * rows * model * hidden * 9,
            bytes_accessed=weights.size * 4 + rows * model * 16,
            transcendentals=rows * hidden,
        ),
        name="ffn_both",
    )(x, grad_out, weights)


def peer_x(chip):
    return chip + 1 - 2 * (chip % 2)


def peer_y(chip):
    return chip + 2 - 4 * (chip // 2)


def line_place(end, core):
    return end + core * (3 - 2 * end)


def remote(source, target, send, recv, member, z):
    return pltpu.make_async_remote_copy(
        src_ref=source,
        dst_ref=target,
        send_sem=send,
        recv_sem=recv,
        device_id=(member, z),
        device_id_type=pl.DeviceIdType.MESH,
    )


def enter(member, z):
    barrier = pltpu.get_barrier_semaphore()
    for other in range(8):

        @pl.when(member != other)
        def _():
            pl.semaphore_signal(
                barrier, inc=1, device_id=(other, z), device_id_type=pl.DeviceIdType.MESH
            )

    for other in range(4):

        @pl.when(z != other)
        def _():
            pl.semaphore_signal(
                barrier, inc=1, device_id=(member, other), device_id_type=pl.DeviceIdType.MESH
            )

    pl.semaphore_wait(barrier, 10)


class Scatter:
    def __init__(self, sizes, member, z, send_sem, recv_sem):
        self.model, self.width, self.ffn_width, self.piece_length = sizes
        self.member, self.z = member, z
        self.chip, self.core = member // 2, member % 2
        self.owner = self.core == z // 2
        self.send_sem, self.recv_sem = send_sem, recv_sem
        self.across = self.model // 128
        rec, ffn, model = 4 * self.width, 4 * self.ffn_width, self.model
        self.gate_base = 2 * model * rec
        self.out_base = self.gate_base + 8 * self.width * self.width
        self.up_base = self.out_base + rec * model
        self.down_base = self.up_base + 2 * model * ffn
        self.rec, self.ffn = rec, ffn
        self.first_in = 0
        self.first_gate = 2 * self.across
        self.first_out = self.first_gate + 2
        self.first_small = self.first_out + 4
        self.first_up = self.first_small + 1
        self.first_down = self.first_up + 2 * self.across
        self.count = self.first_down + 6

    def in_unit(self, number, q):
        kind, at = number // self.across, number % self.across
        low = (kind * self.model + at * 128) * self.rec
        where = (
            pl.ds(pl.multiple_of(kind * self.width, self.width), self.width),
            pl.ds(pl.multiple_of(at * 128, 128), 128),
        )
        return self.first_in + number, where, low, low + 128 * self.rec

    def gate_unit(self, kind, q):
        low = self.gate_base + (kind * 4 + q) * self.width * self.width
        where = (
            pl.ds(pl.multiple_of(kind * self.width, self.width), self.width),
            pl.ds(self.model, self.width),
        )
        return self.first_gate + kind, where, low, low + self.width * self.width

    def out_unit(self, number, q):
        rows = self.width // 4
        low = self.out_base + (q * self.width + number * rows) * self.model
        where = (
            pl.ds(pl.multiple_of(2 * self.width + number * rows, rows), rows),
            pl.ds(0, self.model),
        )
        return self.first_out + number, where, low, low + rows * self.model

    def up_unit(self, number, q):
        kind, at = number // self.across, number % self.across
        low = self.up_base + (kind * self.model + at * 128) * self.ffn
        where = (kind, pl.ds(0, self.ffn_width), pl.ds(pl.multiple_of(at * 128, 128), 128))
        return self.first_up + number, where, low, low + 128 * self.ffn

    def down_unit(self, number, q):
        rows = self.ffn_width // 6
        low = self.down_base + (q * self.ffn_width + number * rows) * self.model
        where = (2, pl.ds(pl.multiple_of(number * rows, 16), rows), pl.ds(0, self.model))
        return self.first_down + number, where, low, low + rows * self.model

    def small_where(self):
        return (pl.ds(2 * self.width, 16), pl.ds(self.model, self.width))

    def copies(self, unit, source, target, q, act):
        number, where, low, high = unit
        first = low // self.piece_length
        last = (high - 1) // self.piece_length
        for which, to in ((0, first), (1, last)):
            wanted = True if which == 0 else last != first

            @pl.when((to != self.member) & wanted)
            def _():
                act(
                    remote(
                        source.at[where],
                        target.at[(q,) + where],
                        self.send_sem.at[which, number],
                        self.recv_sem.at[q, number],
                        to,
                        self.z,
                    ),
                    True,
                )

            @pl.when((to == self.member) & wanted)
            def _():
                act(
                    pltpu.make_async_copy(
                        source.at[where], target.at[(q,) + where], self.recv_sem.at[q, number]
                    ),
                    False,
                )

    def each(self, unit_of, low, high, source, target, act):
        def body(number, carry):
            self.copies(unit_of(number, self.chip), source, target, self.chip, act)
            return carry

        lax.fori_loop(low, high, body, 0)

    def smalls(self, source, target, act):
        where = self.small_where()
        for to in range(8):

            @pl.when(self.member != to)
            def _():
                act(
                    remote(
                        source.at[where],
                        target.at[(self.chip,) + where],
                        self.send_sem.at[2, to],
                        self.recv_sem.at[self.chip, self.first_small],
                        to,
                        self.z,
                    ),
                    True,
                )

        act(
            pltpu.make_async_copy(
                source.at[where],
                target.at[(self.chip,) + where],
                self.recv_sem.at[self.chip, self.first_small],
            ),
            False,
        )

    def arrivals(self, unit_of, count, source, target):
        low = self.member * self.piece_length

        def body(number, carry):
            for q in range(4):
                index, where, first, last = unit_of(number, q)
                mine = (first < low + self.piece_length) & (last > low)
                here = (self.chip == q) & self.owner

                @pl.when(mine & here)
                def _():
                    pltpu.make_async_copy(
                        source.at[where], target.at[(q,) + where], self.recv_sem.at[q, index]
                    ).wait()

                @pl.when(mine & jnp.logical_not(here))
                def _():
                    remote(
                        source.at[where],
                        target.at[(q,) + where],
                        self.send_sem.at[0, index],
                        self.recv_sem.at[q, index],
                        self.member,
                        self.z,
                    ).wait_recv()

            return carry

        lax.fori_loop(0, count, body, 0)

    def small_arrivals(self, source, target):
        where = self.small_where()
        for q in range(4):
            here = (self.chip == q) & self.owner

            @pl.when(here)
            def _():
                pltpu.make_async_copy(
                    source.at[where],
                    target.at[(q,) + where],
                    self.recv_sem.at[q, self.first_small],
                ).wait()

            @pl.when(jnp.logical_not(here))
            def _():
                remote(
                    source.at[where],
                    target.at[(q,) + where],
                    self.send_sem.at[2, 0],
                    self.recv_sem.at[q, self.first_small],
                    self.member,
                    self.z,
                ).wait_recv()


def begin(copy, is_remote):
    copy.start()


def finish_send(copy, is_remote):
    if is_remote:
        copy.wait_send()


def sums_kernel(
    sizes,
    mix_ref,
    part_ref,
    ffn_ref,
    tokens_ref,
    res_ref,
    gain_ref,
    mix_out,
    ffn_out,
    tokens_out,
    gain_out,
    paired,
    arrived,
    total,
    from_x,
    from_y,
    passing,
    last,
    gain_part,
    gain_plane,
    gain_line,
    gain_seen,
    core_send,
    core_recv,
    line_send,
    line_recv,
    plane_send,
    plane_recv,
    gain_send,
    gain_recv,
    unit_send,
    unit_recv,
):
    model, width, ffn_width, piece_length = sizes
    member = lax.axis_index("dp")
    z = lax.axis_index("shard")
    chip, core = member // 2, member % 2
    end = z + core * (3 - 2 * z)
    slots = tokens_ref.shape[0]
    half = slots // 2
    to_x = peer_x(chip) * 2 + core
    to_y = peer_y(chip) * 2 + core
    other = chip * 2 + 1 - core
    scatter = Scatter(sizes, member, z, unit_send, unit_recv)
    enter(member, z)

    def rows(number):
        return pl.ds(number * width, width)

    def core_copy(slot, number):
        return remote(
            mix_ref.at[2 + slot, rows(number)],
            paired.at[slot, rows(number)],
            core_send.at[slot, number],
            core_recv.at[slot, number],
            other,
            z,
        )

    for slot in range(2):
        for number in range(3):
            core_copy(slot, number).start()

    def plane_copy(number):
        source, target, to = (
            (part_ref.at[pl.ds(slots, half)], from_x.at[0], to_x),
            (part_ref.at[pl.ds(3 * slots, half)], from_x.at[1], to_x),
            (part_ref.at[pl.ds(2 * slots + half, half)], from_y.at[0], to_y),
            (part_ref.at[pl.ds(3 * slots + half, half)], from_y.at[1], to_y),
            (passing.at[0], last.at[0], to_y),
            (passing.at[1], last.at[1], to_x),
        )[number]
        return remote(source, target, plane_send.at[number], plane_recv.at[number], to, z)

    for number in (1, 3, 0, 2):
        plane_copy(number).start()

    @pl.when(scatter.owner)
    def _():
        scatter.each(scatter.up_unit, 0, 2 * scatter.across, ffn_ref, ffn_out, begin)
        scatter.each(scatter.down_unit, 0, 6, ffn_ref, ffn_out, begin)

    def line_copy(kind, number, source, to_end):
        return remote(
            source,
            arrived.at[kind, rows(number)],
            line_send.at[kind, number],
            line_recv.at[kind, number],
            member,
            line_place(to_end, core),
        )

    for slot in range(2):
        for number in range(3):
            core_copy(slot, number).wait_recv()
            both = mix_ref[slot, rows(number)].astype(wide) + paired[slot, rows(number)].astype(wide)
            paired[slot, rows(number)] = both.astype(low_type)

            @pl.when(end == 3)
            def _():
                line_copy(slot, number, paired.at[slot, rows(number)], 2).start()

            if slot == 1:

                @pl.when(end == 0)
                def _():
                    line_copy(2, number, paired.at[slot, rows(number)], 1).start()

    plane_copy(1).wait_recv()
    passing[0] = (
        part_ref[2 * slots : 2 * slots + half].astype(wide) + from_x[1].astype(wide)
    ).astype(low_type)
    plane_copy(4).start()
    plane_copy(3).wait_recv()
    passing[1] = (
        part_ref[slots + half : 2 * slots].astype(wide) + from_y[1].astype(wide)
    ).astype(low_type)
    plane_copy(5).start()

    def summed(slot, kinds, number):
        result = paired[slot, rows(number)].astype(wide)
        for kind in kinds:
            result = result + arrived[kind, rows(number)].astype(wide)
        return result.astype(low_type)

    def on_arrival(kind, number):
        line_copy(kind, number, paired.at[0, rows(number)], 0).wait_recv()

    def share(number):
        if number < 2:
            across = scatter.across
            scatter.each(
                scatter.in_unit, number * across, (number + 1) * across, total, mix_out, begin
            )
            scatter.each(scatter.gate_unit, number, number + 1, total, mix_out, begin)
        else:
            scatter.each(scatter.out_unit, 0, 4, total, mix_out, begin)
            scatter.smalls(total, mix_out, begin)

    for number in range(3):

        @pl.when((end == 2) | (end == 1))
        def _():
            on_arrival(0, number)
            paired[0, rows(number)] = summed(0, (0,), number)

        @pl.when(end == 2)
        def _():
            line_copy(0, number, paired.at[0, rows(number)], 1).start()

        @pl.when(end == 1)
        def _():
            line_copy(0, number, paired.at[0, rows(number)], 0).start()

    for number in range(3):

        @pl.when(end == 2)
        def _():
            on_arrival(1, number)
            paired[1, rows(number)] = summed(1, (1,), number)
            line_copy(1, number, paired.at[1, rows(number)], 1).start()

        @pl.when(end == 1)
        def _():
            on_arrival(1, number)
            on_arrival(2, number)
            total[rows(number)] = summed(1, (1, 2), number)

        @pl.when(end == 0)
        def _():
            on_arrival(0, number)
            total[rows(number)] = summed(0, (0,), number)

        @pl.when(scatter.owner)
        def _():
            share(number)

    plane_copy(0).wait_recv()
    plane_copy(2).wait_recv()
    plane_copy(4).wait_recv()
    plane_copy(5).wait_recv()
    gain = gain_ref[0:1]
    gain_sum = jnp.zeros((1, model), wide)
    for number, direct in ((0, from_x), (1, from_y)):
        at = slice(number * half, (number + 1) * half)
        grad = part_ref[at].astype(wide) + direct[0].astype(wide) + last[number].astype(wide)
        value = tokens_ref[at].astype(wide)
        scale = lax.rsqrt(jnp.mean(value * value, axis=1, keepdims=True) + norm_eps)
        scaled = grad * gain
        gain_sum = gain_sum + jnp.sum(grad * value * scale, axis=0, keepdims=True)
        inner = jnp.mean(scaled * value, axis=1, keepdims=True)
        back = scale * scaled - value * (scale * scale * scale * inner)
        tokens_out[at] = (res_ref[at] + back).astype(low_type)
    gain_part[...] = jnp.concatenate([gain_sum, gain_ref[1:2], jnp.zeros((6, model), wide)], axis=0)

    def gain_copy():
        return remote(
            gain_part, gain_plane.at[member], gain_send.at[0], gain_recv.at[member], 7, z
        )

    @pl.when(member != 7)
    def _():
        gain_copy().start()
        gain_copy().wait_send()
        gain_out[...] = jnp.zeros_like(gain_out)

    @pl.when(member == 7)
    def _():
        result = gain_part[...]
        for source in range(7):
            remote(
                gain_part,
                gain_plane.at[source],
                gain_send.at[0],
                gain_recv.at[source],
                7,
                z,
            ).wait_recv()
            result = result + gain_plane[source]
        quarter = model // 4
        for place in range(4):
            gain_line[place] = result[:, place * quarter : (place + 1) * quarter]

        def line_gain(place, slot):
            return remote(
                gain_line.at[place],
                gain_seen.at[slot],
                gain_send.at[1 + place],
                gain_recv.at[8 + slot],
                7,
                place,
            )

        for place in range(4):

            @pl.when(place != z)
            def _():
                line_gain(place, z).start()

        gain_out[...] = gain_line[z]
        for place in range(4):

            @pl.when(place != z)
            def _():
                line_gain(place, place).wait_recv()
                gain_out[...] += gain_seen[place]
                line_gain(place, z).wait_send()

    across = scatter.across
    scatter.arrivals(scatter.up_unit, 2 * across, ffn_ref, ffn_out)
    scatter.arrivals(scatter.down_unit, 6, ffn_ref, ffn_out)
    scatter.arrivals(scatter.in_unit, 2 * across, total, mix_out)
    scatter.arrivals(scatter.gate_unit, 2, total, mix_out)
    scatter.arrivals(scatter.out_unit, 4, total, mix_out)
    scatter.small_arrivals(total, mix_out)

    @pl.when(scatter.owner)
    def _():
        scatter.each(scatter.up_unit, 0, 2 * across, ffn_ref, ffn_out, finish_send)
        scatter.each(scatter.down_unit, 0, 6, ffn_ref, ffn_out, finish_send)
        scatter.each(scatter.in_unit, 0, 2 * across, total, mix_out, finish_send)
        scatter.each(scatter.gate_unit, 0, 2, total, mix_out, finish_send)
        scatter.each(scatter.out_unit, 0, 4, total, mix_out, finish_send)
        scatter.smalls(total, mix_out, finish_send)

    for number in range(6):
        plane_copy(number).wait_send()
    for slot in range(2):
        for number in range(3):
            core_copy(slot, number).wait_send()
    for number in range(3):

        @pl.when(end > 0)
        def _():
            line_copy(0, number, paired.at[0, rows(number)], 0).wait_send()

        @pl.when(end > 1)
        def _():
            line_copy(1, number, paired.at[1, rows(number)], 0).wait_send()

        @pl.when(end == 0)
        def _():
            line_copy(2, number, paired.at[1, rows(number)], 1).wait_send()


def sums(mix, part, ffn, tokens, residual_grad, gains, piece_length, width):
    model = tokens.shape[1]
    ffn_width = ffn.shape[1]
    sizes = (model, width, ffn_width, piece_length)
    half = tokens.shape[0] // 2
    block = mix.shape[1:]
    count = Scatter(sizes, 0, 0, None, None).count
    dma = pltpu.SemaphoreType.DMA
    vmem = pl.BlockSpec(memory_space=pltpu.VMEM)
    anywhere = pl.BlockSpec(memory_space=pl.ANY)
    return pl.pallas_call(
        functools.partial(sums_kernel, sizes),
        in_specs=[vmem, vmem, anywhere, vmem, vmem, vmem],
        out_specs=[anywhere, anywhere, vmem, vmem],
        out_shape=[
            jax.ShapeDtypeStruct(mix.shape, low_type),
            jax.ShapeDtypeStruct((4,) + ffn.shape, low_type),
            jax.ShapeDtypeStruct(tokens.shape, low_type),
            jax.ShapeDtypeStruct((8, model // 4), wide),
        ],
        scratch_shapes=[
            pltpu.VMEM((2,) + block, low_type),
            pltpu.VMEM((3,) + block, low_type),
            pltpu.VMEM(block, low_type),
            pltpu.VMEM((2, half, model), low_type),
            pltpu.VMEM((2, half, model), low_type),
            pltpu.VMEM((2, half, model), low_type),
            pltpu.VMEM((2, half, model), low_type),
            pltpu.VMEM((8, model), wide),
            pltpu.VMEM((8, 8, model), wide),
            pltpu.VMEM((4, 8, model // 4), wide),
            pltpu.VMEM((4, 8, model // 4), wide),
            dma((2, 3)),
            dma((2, 3)),
            dma((3, 3)),
            dma((3, 3)),
            dma((6,)),
            dma((6,)),
            dma((5,)),
            dma((12,)),
            dma((3, count)),
            dma((4, count)),
        ],
        compiler_params=pltpu.CompilerParams(
            collective_id=2, has_side_effects=True, vmem_limit_bytes=40 * 1024 * 1024
        ),
        cost_estimate=pl.CostEstimate(
            flops=mix.size * 4, bytes_accessed=mix.size * 8, transcendentals=0
        ),
        name="sums",
    )(mix, part, ffn, tokens, residual_grad, gains)


def tail_kernel(
    sizes,
    mix_ref,
    ffn_ref,
    gain_ref,
    master_ref,
    first_ref,
    second_ref,
    piece_ref,
    new_master_ref,
    new_first_ref,
    new_second_ref,
    weights_ref,
    bias_ref,
    grad,
    held,
    spread,
    send_sem,
    recv_sem,
):
    model, width, ffn_width, piece_length, chunks, lines, margin = sizes
    member = lax.axis_index("dp")
    z = lax.axis_index("shard")
    step = pl.program_id(0)
    lead = 128
    start_row = (member * piece_length) // lead
    offset = (member * piece_length) % lead
    tiles_in = 4 * width // lead
    tiles_ffn = 4 * ffn_width // lead
    tiles_model = model // lead

    def copy_to(origin, chunk, side, to):
        return pltpu.make_async_remote_copy(
            src_ref=held.at[origin, chunk],
            dst_ref=held.at[origin, chunk],
            send_sem=send_sem.at[side, origin, chunk],
            recv_sem=recv_sem.at[origin, chunk],
            device_id=(member, to),
            device_id_type=pl.DeviceIdType.MESH,
        )

    @pl.when(step == 0)
    def _():
        barrier = pltpu.get_barrier_semaphore()

        @pl.when(z > 0)
        def _():
            pl.semaphore_signal(
                barrier, inc=1, device_id=(member, z - 1), device_id_type=pl.DeviceIdType.MESH
            )

        @pl.when(z < 3)
        def _():
            pl.semaphore_signal(
                barrier, inc=1, device_id=(member, z + 1), device_id_type=pl.DeviceIdType.MESH
            )

        @pl.when((z == 0) | (z == 3))
        def _():
            pl.semaphore_wait(barrier, 1)

        @pl.when((z > 0) & (z < 3))
        def _():
            pl.semaphore_wait(barrier, 2)

        def clear(number, carry):
            grad[pl.ds(pl.multiple_of(number * 256, 256), 256), :] = jnp.zeros((256, lead), wide)
            return carry

        lax.fori_loop(0, grad.shape[0] // 256, clear, 0)

        def place(row, count, body):
            low = member * piece_length

            @pl.when((row * lead < low + piece_length) & ((row + count) * lead > low))
            def _():
                body(row - start_row + margin)

        base = 0

        def in_unit(number, carry):
            kind = number // tiles_model
            at = number % tiles_model

            def body(to):
                for q in range(4):
                    tile = mix_ref[
                        q,
                        pl.ds(pl.multiple_of(kind * width, width), width),
                        pl.ds(pl.multiple_of(at * lead, lead), lead),
                    ].astype(wide)
                    grad[pl.ds(to + q, lead, stride=tiles_in), :] = tile.T

            place((kind * model + at * lead) * tiles_in, lead * tiles_in, body)
            return carry

        lax.fori_loop(0, 2 * tiles_model, in_unit, 0)
        base = 2 * model * tiles_in

        def gate_body(number, carry):
            kind = number // 4
            q = number % 4

            def body(to):
                grad[pl.ds(to, width), :] = mix_ref[
                    q, pl.ds(pl.multiple_of(kind * width, width), width), model:
                ].astype(wide)

            place(2 * model * tiles_in + number * width, width, body)
            return carry

        lax.fori_loop(0, 8, gate_body, 0)
        base = base + 8 * width
        out_base = base

        quarter = width // 4

        def out_unit(number, carry):
            q = number // 4
            part = number % 4

            def body(to):
                for at in range(tiles_model):
                    grad[pl.ds(to + at, quarter, stride=tiles_model), :] = mix_ref[
                        q,
                        pl.ds(pl.multiple_of(2 * width + part * quarter, quarter), quarter),
                        at * lead : (at + 1) * lead,
                    ].astype(wide)

            place(out_base + number * quarter * tiles_model, quarter * tiles_model, body)
            return carry

        lax.fori_loop(0, 16, out_unit, 0)
        base = base + 4 * width * tiles_model
        up_base = base

        def up_unit(number, carry):
            kind = number // tiles_model
            at = number % tiles_model
            columns = pl.ds(pl.multiple_of(at * lead, lead), lead)

            def body(to):
                for tile in range(tiles_ffn):
                    found = []
                    row = tile * lead
                    while row < (tile + 1) * lead:
                        q = row // ffn_width
                        last = min((q + 1) * ffn_width, (tile + 1) * lead)
                        found.append(
                            ffn_ref[
                                q,
                                kind,
                                row - q * ffn_width : last - q * ffn_width,
                                columns,
                            ].astype(wide)
                        )
                        row = last
                    block = found[0] if len(found) == 1 else jnp.concatenate(found, axis=0)
                    grad[pl.ds(to + tile, lead, stride=tiles_ffn), :] = block.T

            place(up_base + (kind * model + at * lead) * tiles_ffn, lead * tiles_ffn, body)
            return carry

        lax.fori_loop(0, 2 * tiles_model, up_unit, 0)
        base = base + 2 * model * tiles_ffn
        down_base = base
        sixth = ffn_width // 6

        def down_unit(number, carry):
            q = number // 6
            part = number % 6

            def body(to):
                for at in range(tiles_model):
                    grad[pl.ds(to + at, sixth, stride=tiles_model), :] = ffn_ref[
                        q,
                        2,
                        pl.ds(pl.multiple_of(part * sixth, 16), sixth),
                        at * lead : (at + 1) * lead,
                    ].astype(wide)

            place(down_base + number * sixth * tiles_model, sixth * tiles_model, body)
            return carry

        lax.fori_loop(0, 24, down_unit, 0)
        small_base = base + 4 * ffn_width * tiles_model
        smalls = [
            mix_ref[q, 2 * width : 2 * width + 16, model:].astype(wide)
            for q in range(4)
        ]

        def small_body(to):
            for q in range(4):
                grad[pl.ds(to + q, 8, stride=tiles_in), :] = smalls[q][:8]
            for number in range(6):
                kind, at = number // 3, number % 3
                grad[pl.ds(to + 8 * tiles_in + number, 1), :] = gain_ref[
                    kind : kind + 1, at * lead : (at + 1) * lead
                ]

        place(small_base, 8 * tiles_in + 6, small_body)
        bias_ref[...] = jnp.concatenate([small[5:7] for small in smalls], axis=1)

    @pl.when(step < chunks)
    def _():
        row = margin + step * lines
        shift = (lead - offset) % lead
        here = pltpu.roll(grad[pl.ds(row, lines), :], shift, 1)
        after = pltpu.roll(grad[pl.ds(row + 1, lines), :], shift, 1)
        lane = lax.broadcasted_iota(jnp.int32, (lines, lead), 1)
        piece = jnp.where(lane < lead - offset, here, after).reshape(1, lines * lead)
        piece_ref[...] = piece
        new_first = beta_one * first_ref[...] + (1.0 - beta_one) * piece
        new_second = beta_two * second_ref[...] + (1.0 - beta_two) * piece * piece
        master = master_ref[...]
        new_master = master - learn_rate * (
            new_first / corr_one / (jnp.sqrt(new_second / corr_two) + adam_eps)
            + weight_decay * master
        )
        new_first_ref[...] = new_first
        new_second_ref[...] = new_second
        new_master_ref[...] = new_master
        held[z, step] = new_master.reshape(lines, lead).astype(low_type)

        @pl.when(z < 3)
        def _():
            copy_to(z, step, 0, z + 1).start()

        @pl.when(z > 0)
        def _():
            copy_to(z, step, 1, z - 1).start()

    def pass_on(origin, chunk, right):
        copy_to(origin, chunk, 0, z).wait_recv()
        if right:

            @pl.when(z < 3)
            def _():
                copy_to(origin, chunk, 0, z + 1).start()
        else:

            @pl.when(z > 0)
            def _():
                copy_to(origin, chunk, 1, z - 1).start()

    @pl.when((step >= chunks) & (step < 2 * chunks))
    def _():
        chunk = step - chunks

        @pl.when(z > 0)
        def _():
            pass_on(z - 1, chunk, True)

        @pl.when(z < 3)
        def _():
            pass_on(z + 1, chunk, False)

    @pl.when(step >= 2 * chunks)
    def _():
        chunk = step - 2 * chunks

        @pl.when(z >= 2)
        def _():
            pass_on(z - 2, chunk, True)

        @pl.when(z <= 1)
        def _():
            pass_on(z + 2, chunk, False)

        @pl.when(z == 3)
        def _():
            copy_to(0, chunk, 0, z).wait_recv()

        @pl.when(z == 0)
        def _():
            copy_to(3, chunk, 0, z).wait_recv()

        for origin in range(4):
            spread[origin * lines : (origin + 1) * lines, :] = held[origin, chunk].astype(wide)

        def line(number, carry):
            weights_ref[:, pl.ds(pl.multiple_of(number * lead, lead), lead)] = spread[
                pl.ds(number, 4, stride=lines), :
            ].astype(low_type)
            return carry

        lax.fori_loop(0, lines, line, 0, unroll=8)

    @pl.when(step == 3 * chunks - 1)
    def _():
        for origin in range(4):

            def finish(chunk, carry):
                @pl.when((origin <= z) & (z < 3))
                def _():
                    copy_to(origin, chunk, 0, z).wait_send()

                @pl.when((origin >= z) & (z > 0))
                def _():
                    copy_to(origin, chunk, 1, z).wait_send()

                return carry

            lax.fori_loop(0, chunks, finish, 0)


def tail(mix, ffn, gains, master, first, second, sizes):
    model, width, ffn_width = sizes
    piece_length = master.shape[1]
    chunks = 8
    lines = -(-piece_length // (chunks * 128 * 16)) * 16
    block = lines * 128
    margin = 1536
    rows = -(-(2 * margin + chunks * lines + 8) // 256) * 256
    packed = jax.ShapeDtypeStruct(master.shape, wide)
    whole = lambda shape: pl.BlockSpec(shape, lambda s: (0,) * len(shape))
    chunk_spec = pl.BlockSpec((1, block), lambda s: (0, jnp.minimum(s, chunks - 1)))
    once = lambda shape: pl.BlockSpec(
        shape, lambda s: (0,) * len(shape), pipeline_mode=pl.Buffered(1)
    )
    return pl.pallas_call(
        functools.partial(
            tail_kernel, (model, width, ffn_width, piece_length, chunks, lines, margin)
        ),
        grid=(3 * chunks,),
        in_specs=[once(mix.shape), once(ffn.shape), once(gains.shape)] + [chunk_spec] * 3,
        out_specs=[chunk_spec] * 4
        + [
            pl.BlockSpec((4, block), lambda s: (0, jnp.maximum(s - 2 * chunks, 0))),
            whole((2, 4 * width)),
        ],
        out_shape=[packed] * 4
        + [
            jax.ShapeDtypeStruct((4, piece_length), low_type),
            jax.ShapeDtypeStruct((2, 4 * width), wide),
        ],
        scratch_shapes=[
            pltpu.VMEM((rows, 128), wide),
            pltpu.VMEM((4, chunks, lines, 128), low_type),
            pltpu.VMEM((4 * lines, 128), wide),
            pltpu.SemaphoreType.DMA((2, 4, chunks)),
            pltpu.SemaphoreType.DMA((4, chunks)),
        ],
        compiler_params=pltpu.CompilerParams(
            collective_id=1, has_side_effects=True, vmem_limit_bytes=58 * 1024 * 1024
        ),
        cost_estimate=pl.CostEstimate(
            flops=20 * piece_length,
            bytes_accessed=40 * piece_length,
            transcendentals=piece_length,
        ),
        name="tail",
    )(mix, ffn, gains, master, first, second)


def group_body(
    tokens,
    cotangent,
    seq_start,
    live_mask,
    input_proj,
    gate_blocks,
    output_proj,
    ffn_gate_up,
    ffn_down,
    conv_taps,
    gate_bias,
    decay_param,
    norm_gains,
    master_shard,
    first_moment,
    second_moment,
):
    slots, model = tokens.shape
    slice_rec = input_proj.shape[2]
    slice_ffn = ffn_down.shape[0]
    width = slice_rec // 4
    ffn_width = slice_ffn // 4
    piece_length = master_shard.shape[1]
    member = lax.axis_index("dp")
    chip = member // 2
    core = member % 2
    z = lax.axis_index("shard")
    end = jnp.where(core == 0, z, 3 - z)

    mask_rows = live_mask.astype(wide)[:, None]
    stream = tokens.astype(wide)
    grad_stream = cotangent.astype(wide) * mask_rows

    def quarter(value, dim, count):
        return lax.dynamic_slice_in_dim(value, chip * count, count, axis=dim)

    own_proj = quarter(input_proj, 2, width).transpose(0, 2, 1).reshape(2 * width, model)
    own_out = quarter(output_proj, 0, width)
    own_gates = quarter(gate_blocks, 1, 1).reshape(2 * width, width)
    own_small = jnp.concatenate(
        [
            quarter(conv_taps, 1, width),
            quarter(gate_bias, 1, width),
            quarter(decay_param[None], 1, width),
            jnp.zeros((width - 8, width), low_type),
        ]
    )
    own_mix = jnp.concatenate(
        [
            jnp.concatenate([own_proj, own_out]),
            jnp.concatenate([own_gates, own_small]),
        ],
        axis=1,
    )
    own_ffn = jnp.concatenate(
        [
            quarter(ffn_gate_up, 2, ffn_width).transpose(0, 2, 1),
            quarter(ffn_down, 0, ffn_width)[None],
        ]
    )

    gains = all_slices(norm_gains, z).astype(wide)

    start_row = jnp.zeros((16, model), low_type).at[0, :slots].set(seq_start.astype(low_type))
    gathered = plane_gather(jnp.concatenate([tokens, start_row]))
    starts = jnp.stack([block[slots, :slots] for block in gathered]).astype(jnp.int32)
    position = (jnp.arange(slots, dtype=jnp.int32)[None] - starts).reshape(-1, 1)
    all_tokens = jnp.concatenate([block[:slots] for block in gathered])
    mix_in = rms_scale(all_tokens.astype(wide), gains[0]).astype(low_type)

    mix_a, mix_b = line_spread(own_mix, end)
    mix_pair = jnp.stack([mix_a, mix_b])
    mix_weights = jnp.concatenate([mix_pair, move(mix_pair, core_pairs)])

    ffn_a, ffn_b = line_spread(own_ffn, end)
    ffn_pair = jnp.concatenate([ffn_a, ffn_b], axis=1)
    ffn_weights = jnp.concatenate([ffn_pair, move(ffn_pair, core_pairs)], axis=1)

    all_grad_out = jnp.concatenate(plane_gather(grad_stream.astype(low_type)))

    mix_part, *saved = mix_forward(mix_in, position, mix_weights, slots, width)
    residual = stream + plane_reduce(mix_part)
    normed_two, second_pull = jax.vjp(rms_scale, residual, gains[1])
    ffn_in = jnp.concatenate(plane_gather(normed_two.astype(low_type)))

    grad_ffn, ffn_part, ffn_in_part = ffn_both(
        ffn_in, all_grad_out, ffn_weights, slots, ffn_width * 4 // 3
    )
    grad_norm_two, grad_gain_two = second_pull(plane_reduce(ffn_in_part))
    grad_residual = grad_stream + grad_norm_two
    res_low = jnp.concatenate(plane_gather(grad_residual.astype(low_type)))
    block_out = (mask_rows * (residual + plane_reduce(ffn_part))).astype(low_type)

    grad_mix, mix_in_part = mix_backward(
        mix_in, res_low, position, mix_weights, saved, slots, width
    )
    both = 2 * ffn_width
    pair_ffn = add_low(grad_ffn[:, :both], move(grad_ffn[:, both:], core_pairs))
    sum_ffn = line_sum(pair_ffn[:, :ffn_width], pair_ffn[:, ffn_width:], end)
    four_mix, four_ffn, tokens_grad, gain_total = sums(
        grad_mix,
        mix_in_part,
        sum_ffn,
        tokens,
        grad_residual,
        jnp.concatenate([gains[0:1], grad_gain_two[None], jnp.zeros((6, model), wide)]),
        piece_length,
        width,
    )
    piece, new_master, new_first, new_second, new_weights, bias_total = tail(
        four_mix,
        four_ffn,
        gain_total,
        master_shard,
        first_moment,
        second_moment,
        (model, width, ffn_width),
    )
    return (
        block_out,
        tokens_grad,
        piece,
        new_master,
        new_first,
        new_second,
        new_weights,
        bias_total,
    )


def rms_scale(values, gain):
    return values * lax.rsqrt(jnp.mean(values * values, axis=-1, keepdims=True) + norm_eps) * gain


def conv_mix(signal, taps, position):
    result = taps[-1] + taps[0] * signal
    for shift_by in range(1, taps.shape[0] - 1):
        moved = jnp.pad(signal, ((shift_by, 0), (0, 0)))[:-shift_by]
        result = result + taps[shift_by] * jnp.where((position >= shift_by)[:, None], moved, 0.0)
    return result


def combine_steps(earlier, later):
    decay_first, value_first = earlier
    decay_second, value_second = later
    return (decay_first * decay_second, decay_second * value_first + value_second)


def recurrence(logits, signal, branch, bias_term, decay_term, position):
    row_count = signal.shape[0]
    recur_gate = jax.nn.sigmoid(logits[0].reshape(row_count, -1) + bias_term[0])
    input_gate = jax.nn.sigmoid(logits[1].reshape(row_count, -1) + bias_term[1])
    log_decay = -gate_scale * recur_gate * jax.nn.softplus(-decay_term)
    decay_rate = jnp.where((position > 0)[:, None], jnp.exp(log_decay), 0.0)
    drive_term = jnp.sqrt(-jnp.expm1(2.0 * log_decay)) * input_gate * signal
    states = lax.associative_scan(combine_steps, (decay_rate, drive_term), axis=0)[1]
    return states * jax.nn.gelu(branch)


def gated_gelu(ffn_pre):
    return jax.nn.gelu(ffn_pre[0]) * ffn_pre[1]


def mixer_forward(
    mix_in, input_proj, gate_blocks, output_proj, conv_taps, gate_bias, decay_param, position
):
    projected = jnp.einsum("sd,kdr->ksr", mix_in, input_proj, preferred_element_type=jnp.float32)
    conv_out, conv_pull = jax.vjp(
        lambda signal, taps: conv_mix(signal, taps, position), projected[0], conv_taps
    )
    row_count = conv_out.shape[0]
    conv_low = conv_out.astype(jnp.bfloat16).reshape(
        row_count, gate_blocks.shape[1], gate_blocks.shape[2]
    )
    gate_logits = jnp.einsum(
        "shb,khbc->kshc", conv_low, gate_blocks, preferred_element_type=jnp.float32
    )
    mixed, mix_pull = jax.vjp(
        lambda logits, signal, branch, bias_term, decay_term: recurrence(
            logits, signal, branch, bias_term, decay_term, position
        ),
        gate_logits,
        conv_out,
        projected[1],
        gate_bias,
        decay_param,
    )
    mixed_low = mixed.astype(jnp.bfloat16)
    partial_out = jnp.dot(mixed_low, output_proj, preferred_element_type=jnp.float32)
    return (partial_out, (conv_pull, conv_low, mix_pull, mixed_low))


def mixer_backward(grad_out_low, mix_in, saved, input_proj, gate_blocks, output_proj):
    conv_pull, conv_low, mix_pull, mixed_low = saved
    grad_output_proj = jnp.einsum(
        "sr,sd->rd", mixed_low, grad_out_low, preferred_element_type=jnp.float32
    )
    grad_mixed = jnp.einsum(
        "sd,rd->sr", grad_out_low, output_proj, preferred_element_type=jnp.float32
    )
    grad_logits, grad_conv_direct, grad_branch, grad_bias, grad_decay = mix_pull(grad_mixed)
    logits_low = grad_logits.astype(jnp.bfloat16)
    grad_blocks = jnp.einsum(
        "shb,kshc->khbc", conv_low, logits_low, preferred_element_type=jnp.float32
    )
    grad_conv_gates = jnp.einsum(
        "kshc,khbc->shb", logits_low, gate_blocks, preferred_element_type=jnp.float32
    )
    grad_signal, grad_taps = conv_pull(
        grad_conv_direct + grad_conv_gates.reshape(grad_conv_direct.shape)
    )
    proj_low = jnp.stack([grad_signal, grad_branch]).astype(jnp.bfloat16)
    grad_input_proj = jnp.einsum(
        "sd,ksr->kdr", mix_in, proj_low, preferred_element_type=jnp.float32
    )
    grad_mix_in = jnp.einsum(
        "ksr,kdr->sd", proj_low, input_proj, preferred_element_type=jnp.float32
    )
    return (
        grad_mix_in,
        (grad_input_proj, grad_blocks, grad_output_proj, grad_taps, grad_bias, grad_decay),
    )


def ffn_forward(ffn_in_low, ffn_gate_up, ffn_down):
    ffn_pre = jnp.einsum("sd,kdf->ksf", ffn_in_low, ffn_gate_up, preferred_element_type=jnp.float32)
    ffn_act, ffn_pull = jax.vjp(gated_gelu, ffn_pre)
    ffn_low = ffn_act.astype(jnp.bfloat16)
    partial_ffn = jnp.dot(ffn_low, ffn_down, preferred_element_type=jnp.float32)
    return (partial_ffn, (ffn_pull, ffn_low))


def ffn_backward(grad_low, ffn_in_low, saved, ffn_gate_up, ffn_down):
    ffn_pull, ffn_low = saved
    grad_down = jnp.einsum("sf,sd->fd", ffn_low, grad_low, preferred_element_type=jnp.float32)
    grad_act = jnp.einsum("sd,fd->sf", grad_low, ffn_down, preferred_element_type=jnp.float32)
    grad_pre = ffn_pull(grad_act)[0]
    pre_low = grad_pre.astype(jnp.bfloat16)
    grad_gate_up = jnp.einsum(
        "sd,ksf->kdf", ffn_in_low, pre_low, preferred_element_type=jnp.float32
    )
    grad_ffn_in = jnp.einsum(
        "ksf,kdf->sd", pre_low, ffn_gate_up, preferred_element_type=jnp.float32
    )
    return (grad_ffn_in, grad_gate_up, grad_down)


def body(
    tokens,
    cotangent,
    seq_start,
    live_mask,
    input_proj,
    gate_blocks,
    output_proj,
    ffn_gate_up,
    ffn_down,
    conv_taps,
    gate_bias,
    decay_param,
    norm_gains,
    master_shard,
    first_moment,
    second_moment,
):
    slot_count = tokens.shape[0]
    position = jnp.arange(slot_count, dtype=jnp.int32) - seq_start
    mask_rows = live_mask.astype(jnp.float32)[:, None]
    stream = tokens.astype(jnp.float32)
    grad_stream = cotangent.astype(jnp.float32) * mask_rows
    shards = (
        input_proj,
        gate_blocks,
        output_proj,
        ffn_gate_up,
        ffn_down,
        conv_taps,
        gate_bias,
        decay_param,
        norm_gains,
    )
    (
        full_in,
        full_blocks,
        full_out,
        full_up,
        full_down,
        full_taps,
        full_bias,
        full_decay,
        full_gains,
    ) = (
        lax.all_gather(shards[0], "shard", axis=2, tiled=True),
        lax.all_gather(shards[1], "shard", axis=1, tiled=True),
        lax.all_gather(shards[2], "shard", axis=0, tiled=True),
        lax.all_gather(shards[3], "shard", axis=2, tiled=True),
        lax.all_gather(shards[4], "shard", axis=0, tiled=True),
        lax.all_gather(shards[5], "shard", axis=1, tiled=True),
        lax.all_gather(shards[6], "shard", axis=1, tiled=True),
        lax.all_gather(shards[7], "shard", axis=0, tiled=True),
        lax.all_gather(shards[8], "shard", axis=1, tiled=True),
    )
    gains = full_gains.astype(jnp.float32)
    normed, norm_pull = jax.vjp(rms_scale, stream, gains[0])
    mix_in = normed.astype(jnp.bfloat16)
    mix_out, mix_saved = mixer_forward(
        mix_in,
        full_in,
        full_blocks,
        full_out,
        full_taps.astype(jnp.float32),
        full_bias.astype(jnp.float32),
        full_decay.astype(jnp.float32),
        position,
    )
    residual = stream + mix_out
    normed_two, second_pull = jax.vjp(rms_scale, residual, gains[1])
    ffn_in_low = normed_two.astype(jnp.bfloat16)
    ffn_result, ffn_saved = ffn_forward(ffn_in_low, full_up, full_down)
    block_out = (mask_rows * (residual + ffn_result)).astype(jnp.bfloat16)
    grad_ffn_in, grad_up, grad_down = ffn_backward(
        grad_stream.astype(jnp.bfloat16), ffn_in_low, ffn_saved, full_up, full_down
    )
    grad_norm_two, grad_gain_two = second_pull(grad_ffn_in)
    grad_residual = grad_stream + grad_norm_two
    grad_mix_in, mix_grads = mixer_backward(
        grad_residual.astype(jnp.bfloat16), mix_in, mix_saved, full_in, full_blocks, full_out
    )
    grad_norm_one, grad_gain_one = norm_pull(grad_mix_in)
    tokens_grad = (grad_residual + grad_norm_one).astype(jnp.bfloat16)
    grads = (
        mix_grads[0],
        mix_grads[1],
        mix_grads[2],
        grad_up,
        grad_down,
        mix_grads[3],
        mix_grads[4],
        mix_grads[5],
        jnp.stack([grad_gain_one, grad_gain_two]),
    )
    summed = (
        lax.psum_scatter(
            grads[0].astype(jnp.bfloat16), "shard", scatter_dimension=2, tiled=True
        ).astype(jnp.float32),
        lax.psum_scatter(
            grads[1].astype(jnp.bfloat16), "shard", scatter_dimension=1, tiled=True
        ).astype(jnp.float32),
        lax.psum_scatter(
            grads[2].astype(jnp.bfloat16), "shard", scatter_dimension=0, tiled=True
        ).astype(jnp.float32),
        lax.psum_scatter(
            grads[3].astype(jnp.bfloat16), "shard", scatter_dimension=2, tiled=True
        ).astype(jnp.float32),
        lax.psum_scatter(
            grads[4].astype(jnp.bfloat16), "shard", scatter_dimension=0, tiled=True
        ).astype(jnp.float32),
        lax.psum_scatter(
            grads[5].astype(jnp.bfloat16), "shard", scatter_dimension=1, tiled=True
        ).astype(jnp.float32),
        lax.psum_scatter(
            grads[6].astype(jnp.bfloat16), "shard", scatter_dimension=1, tiled=True
        ).astype(jnp.float32),
        lax.psum_scatter(
            grads[7].astype(jnp.bfloat16), "shard", scatter_dimension=0, tiled=True
        ).astype(jnp.float32),
        lax.psum_scatter(
            grads[8].astype(jnp.bfloat16), "shard", scatter_dimension=1, tiled=True
        ).astype(jnp.float32),
    )
    flat = jnp.concatenate([member.reshape(1, -1) for member in summed], axis=1)
    piece = lax.psum_scatter(flat, "dp", scatter_dimension=1, tiled=True)
    bias_total = lax.psum(summed[6], "dp")
    new_first = beta_one * first_moment + (1.0 - beta_one) * piece
    new_second = beta_two * second_moment + (1.0 - beta_two) * piece * piece
    new_master = master_shard - learn_rate * (
        new_first / corr_one / (jnp.sqrt(new_second / corr_two) + adam_eps)
        + weight_decay * master_shard
    )
    new_weights = lax.all_gather(new_master.astype(jnp.bfloat16), "shard", axis=0, tiled=True)
    return (
        block_out,
        tokens_grad,
        piece,
        new_master,
        new_first,
        new_second,
        new_weights,
        bias_total,
    )


def solution(mesh):
    fits = mesh.shape["dp"] == 8 and mesh.shape["shard"] == 4
    placed = (
        P(("dp", "shard"), None),
        P(("dp", "shard"), None),
        P(("dp", "shard")),
        P(("dp", "shard")),
        P(None, None, "shard"),
        P(None, "shard", None, None),
        P("shard", None),
        P(None, None, "shard"),
        P("shard", None),
        P(None, "shard"),
        P(None, "shard"),
        P("shard"),
        P(None, "shard"),
        P("shard", "dp"),
        P("shard", "dp"),
        P("shard", "dp"),
    )
    return jax.shard_map(
        group_body if fits else body,
        mesh=mesh,
        in_specs=placed,
        out_specs=(
            P(("dp", "shard"), None),
            P(("dp", "shard"), None),
            P("shard", "dp"),
            P("shard", "dp"),
            P("shard", "dp"),
            P("shard", "dp"),
            P(None, "dp"),
            P(None, "shard"),
        ),
        check_vma=False,
    )
```

```python
import functools
import jax
import jax.numpy as jnp
from jax import lax
from jax.experimental import pallas as pl
from jax.experimental.pallas import tpu as pltpu
from jax.sharding import PartitionSpec as P

norm_eps = 1e-06
gate_scale = 8.0
beta_one = 0.9
beta_two = 0.95
learn_rate = 0.01
weight_decay = 0.1
adam_eps = 1e-08
corr_one = 1.0 - beta_one**10.0
corr_two = 1.0 - beta_two**10.0
low_type = jnp.bfloat16
wide = jnp.float32
axes = ("dp", "shard")
gelu_scale = 0.7978845608028654
gelu_cube = 0.044715


def device_pairs(target):
    found = []
    for chip in range(4):
        for core in range(2):
            for z in range(4):
                to = target(chip, core, z)
                if to is not None:
                    source = (chip * 2 + core) * 4 + z
                    found.append((source, (to[0] * 2 + to[1]) * 4 + to[2]))
    return found


def line_pairs(moves):
    moves = dict(moves)

    def target(chip, core, z):
        end = z if core == 0 else 3 - z
        if end not in moves:
            return None
        to = moves[end]
        return (chip, core, to if core == 0 else 3 - to)

    return device_pairs(target)


def step_pairs(step):
    return device_pairs(
        lambda chip, core, z: (chip, core, z + step) if 0 <= z + step < 4 else None
    )


def plane_pairs(flip, owners_only=False):
    return device_pairs(
        lambda chip, core, z: None if owners_only and core != z // 2 else (chip ^ flip, core, z)
    )


core_pairs = device_pairs(lambda chip, core, z: (chip, 1 - core, z))
owner_core_pairs = device_pairs(
    lambda chip, core, z: (chip, 1 - core, z) if core == z // 2 else None
)


def move(value, pairs):
    return lax.ppermute(value, axes, pairs)


def plane_gather(value, dim=0, owners_only=False):
    half = value.shape[dim] // 2
    across_x = move(value, plane_pairs(1, owners_only))
    across_y = move(value, plane_pairs(2, owners_only))
    first = lax.slice_in_dim(across_x, 0, half, axis=dim)
    second = lax.slice_in_dim(across_y, half, 2 * half, axis=dim)
    first = move(first, plane_pairs(2, owners_only))
    second = move(second, plane_pairs(1, owners_only))
    return (value, across_x, across_y, jnp.concatenate([first, second], axis=dim))


def plane_reduce(parts):
    slots = parts.shape[0] // 4
    half = slots // 2
    mine, for_x, for_y, for_d = (
        parts[number * slots : (number + 1) * slots] for number in range(4)
    )
    top = slice(0, half)
    low = slice(half, slots)
    from_x = move(jnp.concatenate([for_x[top], for_d[top]]), plane_pairs(1))
    from_y = move(jnp.concatenate([for_y[low], for_d[low]]), plane_pairs(2))
    send_y = (for_y[top].astype(wide) + from_x[half:].astype(wide)).astype(low_type)
    send_x = (for_x[low].astype(wide) + from_y[half:].astype(wide)).astype(low_type)
    last_top = move(send_y, plane_pairs(2))
    last_low = move(send_x, plane_pairs(1))
    return jnp.concatenate(
        [
            mine[top].astype(wide) + from_x[:half].astype(wide) + last_top.astype(wide),
            mine[low].astype(wide) + from_y[:half].astype(wide) + last_low.astype(wide),
        ]
    )


def pick(end, choices):
    result = choices[3]
    for number in (2, 1, 0):
        result = jnp.where(end == number, choices[number], result)
    return result


def line_spread(own, end):
    ahead = move(own, line_pairs({0: 1, 1: 2}))
    back = move(own, line_pairs({1: 0}))
    ahead_two = move(ahead, line_pairs({1: 2, 2: 3}))
    ahead_three = move(ahead_two, line_pairs({2: 3}))
    return (
        pick(end, [own, ahead, ahead_two, ahead_three]),
        pick(end, [back, own, ahead, ahead_two]),
    )


def add_low(left, right):
    return (left.astype(wide) + right.astype(wide)).astype(low_type)


def line_sum(outer, inner, end):
    first = add_low(outer, move(outer, line_pairs({3: 2})))
    inner_one = add_low(inner, move(inner, line_pairs({3: 2, 0: 1})))
    second = add_low(outer, move(first, line_pairs({2: 1})))
    inner_two = add_low(inner_one, move(inner_one, line_pairs({2: 1})))
    third = add_low(outer, move(second, line_pairs({1: 0})))
    return jnp.where(end == 0, third, inner_two)


def turn_pairs(turn):
    return device_pairs(lambda chip, core, z: (chip, core, (z + turn) % 4))


def all_slices(own, z):
    found = [own] + [move(own, turn_pairs(turn)) for turn in (1, 2, 3)]
    return jnp.concatenate(
        [
            sum(jnp.where((z - at) % 4 == turn, found[turn], 0) for turn in range(4))
            for at in range(4)
        ],
        axis=-1,
    )


def shard_slices(value, z):
    size = value.shape[-1] // 4

    def part(turn):
        return lax.dynamic_slice_in_dim(value, ((z + turn) % 4) * size, size, axis=1)

    return part(0) + sum(move(part(turn), turn_pairs(turn)) for turn in (1, 2, 3))


def dot_rows(left, right):
    return lax.dot_general(left, right, (((1,), (1,)), ((), ())), preferred_element_type=wide)


def dot_plain(left, right):
    return lax.dot_general(left, right, (((1,), (0,)), ((), ())), preferred_element_type=wide)


def dot_slots(left, right):
    return lax.dot_general(left, right, (((0,), (0,)), ((), ())), preferred_element_type=wide)


def gelu_parts(value):
    square = value * value
    bent = jnp.tanh(gelu_scale * value * (1.0 + gelu_cube * square))
    half = 0.5 * (1.0 + bent)
    slope = half + 0.5 * value * (1.0 - bent * bent) * gelu_scale * (
        1.0 + 3.0 * gelu_cube * square
    )
    return (value * half, slope)


def shift_down(value, step):
    if step % 8 == 0:
        return jnp.concatenate([value[-step:], value[:-step]], axis=0)
    return pltpu.roll(value, step, 0)


def shift_up(value, step):
    if step % 8 == 0:
        return jnp.concatenate([value[step:], value[:step]], axis=0)
    return pltpu.roll(value, value.shape[0] - step, 0)


def scan_slots(decay, value, shift):
    step = 1
    while step < value.shape[0]:
        value = value + decay * shift(value, step)
        if 2 * step < value.shape[0]:
            decay = decay * shift(decay, step)
        step *= 2
    return value


def one_minus_exp(value):
    series = jnp.ones_like(value)
    for number in range(11, 1, -1):
        series = 1.0 - value * (1.0 / number) * series
    return jnp.where(value < 0.8, value * series, 1.0 - jnp.exp(-value))


def soft_plus(value):
    return jnp.maximum(value, 0.0) + jnp.log1p(jnp.exp(-jnp.abs(value)))


def mixer_parts(first, position, small, gates):
    conv_out = small[4:5] + small[0:1] * first
    shifted = []
    for step in range(1, 4):
        moved = jnp.where(position >= step, shift_down(first, step), 0.0)
        shifted.append(moved)
        conv_out = conv_out + small[step : step + 1] * moved
    conv_low = conv_out.astype(low_type)
    logits = dot_plain(conv_low, gates)
    width = first.shape[1]
    recur_gate = jax.nn.sigmoid(logits[:, :width] + small[5:6])
    input_gate = jax.nn.sigmoid(logits[:, width:] + small[6:7])
    rate = gate_scale * soft_plus(-small[7:8])
    log_decay = -rate * recur_gate
    decay = jnp.where(position > 0, jnp.exp(log_decay), 0.0)
    gone = one_minus_exp(-2.0 * log_decay)
    root = jnp.sqrt(gone)
    return conv_out, shifted, conv_low, recur_gate, input_gate, rate, decay, gone, root


def weight_views(w_ref, width):
    model = w_ref.shape[2] - width
    proj = w_ref[0, 0 : 2 * width, 0:model]
    out = w_ref[0, 2 * width : 3 * width, 0:model]
    gates = jnp.concatenate(
        [w_ref[0, 0:width, model:], w_ref[0, width : 2 * width, model:]], axis=1
    )
    small = w_ref[0, 2 * width : 2 * width + 16, model:].astype(wide)
    return proj, out, gates, small


def slot_position(starts):
    slot = lax.broadcasted_iota(jnp.int32, (starts.shape[0], 1), 0)
    return slot - starts[:, 0:1].astype(wide).astype(jnp.int32)


def mixer_step(x, position, views, width):
    proj, out, gates, small = views
    projected = dot_rows(x, proj)
    conv_out, _, _, _, input_gate, _, decay, _, root = mixer_parts(
        projected[:, :width], position, small, gates
    )
    states = scan_slots(decay, root * input_gate * conv_out, shift_down)
    mixed_low = (states * gelu_parts(projected[:, width:])[0]).astype(low_type)
    return projected, states, mixed_low, dot_plain(mixed_low, out)


def mixer_backward_kernel(
    width,
    x_ref,
    res_ref,
    pos_ref,
    w_ref,
    p_ref,
    state_ref,
    low_ref,
    grad_ref,
    gin_ref,
    acc_w,
    acc_in,
):
    head = pl.program_id(0)
    block = pl.program_id(1)
    slots, model = x_ref.shape
    proj, out, gates, small = weight_views(w_ref, width)
    position = slot_position(pos_ref[...])
    first = p_ref[0, :, 0:width]
    res_low = res_ref[...]
    states = state_ref[0]
    conv_out, shifted, conv_low, recur_gate, input_gate, rate, decay, gone, root = mixer_parts(
        first, position, small, gates
    )
    grad_mixed = dot_rows(res_low, out)
    active, slope = gelu_parts(p_ref[0, :, width:])
    grad_second = grad_mixed * states * slope
    adjoint = scan_slots(shift_up(decay, 1), grad_mixed * active, shift_up)
    grad_decay = adjoint * shift_down(states, 1)
    grad_root = adjoint * input_gate * conv_out
    grad_input_gate = adjoint * root * conv_out
    grad_conv = adjoint * root * input_gate
    grad_log = grad_decay * decay - grad_root * (1.0 - gone) / root
    grad_recur = -rate * grad_log
    grad_logit_a = grad_recur * recur_gate * (1.0 - recur_gate)
    grad_logit_b = grad_input_gate * input_gate * (1.0 - input_gate)
    grad_param = jnp.sum(grad_log * recur_gate, axis=0, keepdims=True) * (
        gate_scale * jax.nn.sigmoid(-small[7:8])
    )
    logits_low = jnp.concatenate([grad_logit_a, grad_logit_b], axis=1).astype(low_type)
    grad_conv = grad_conv + dot_rows(logits_low, gates)
    grad_gates = dot_slots(conv_low, logits_low)
    sums = [jnp.sum(grad_conv * first, axis=0, keepdims=True)]
    grad_first = small[0:1] * grad_conv
    for step in range(1, 4):
        sums.append(jnp.sum(grad_conv * shifted[step - 1], axis=0, keepdims=True))
        kept = jnp.where(position >= step, grad_conv, 0.0)
        grad_first = grad_first + small[step : step + 1] * shift_up(kept, step)
    sums.append(jnp.sum(grad_conv, axis=0, keepdims=True))
    sums.append(jnp.sum(grad_logit_a, axis=0, keepdims=True))
    sums.append(jnp.sum(grad_logit_b, axis=0, keepdims=True))
    sums.append(grad_param)
    grad_small = jnp.concatenate(sums, axis=0)
    proj_low = jnp.concatenate([grad_first, grad_second], axis=1).astype(low_type)
    part = dot_plain(proj_low, proj)
    rows = pl.ds(pl.multiple_of(block * slots, slots), slots)

    @pl.when(block == 0)
    def _():
        acc_w[...] = jnp.zeros_like(acc_w)

    acc_w[0 : 2 * width, 0:model] += dot_slots(proj_low, x_ref[...])
    acc_w[2 * width : 3 * width, 0:model] += dot_slots(low_ref[0], res_low)
    acc_w[0:width, model:] += grad_gates[:, :width]
    acc_w[width : 2 * width, model:] += grad_gates[:, width:]
    acc_w[2 * width : 2 * width + 8, model:] += grad_small

    @pl.when(head == 0)
    def _():
        acc_in[rows, :] = part

    @pl.when(head > 0)
    def _():
        acc_in[rows, :] += part

    @pl.when(block == pl.num_programs(1) - 1)
    def _():
        grad_ref[0] = acc_w[...].astype(low_type)

    @pl.when(head == pl.num_programs(0) - 1)
    def _():
        gin_ref[rows, :] = acc_in[rows, :].astype(low_type)


def mix_backward(mix_in, res_low, position, weights, saved, slots, width):
    rows, model = mix_in.shape
    heads = weights.shape[0]
    blocks = rows // slots
    return pl.pallas_call(
        functools.partial(mixer_backward_kernel, width),
        grid=(heads, blocks),
        in_specs=[
            pl.BlockSpec((slots, model), lambda h, b: (b, 0)),
            pl.BlockSpec((slots, model), lambda h, b: (b, 0)),
            pl.BlockSpec((slots, width), lambda h, b: (b, 0)),
            pl.BlockSpec((1,) + weights.shape[1:], lambda h, b: (h, 0, 0)),
            pl.BlockSpec((1, slots, 2 * width), lambda h, b: (h, b, 0)),
            pl.BlockSpec((1, slots, width), lambda h, b: (h, b, 0)),
            pl.BlockSpec((1, slots, width), lambda h, b: (h, b, 0)),
        ],
        out_specs=[
            pl.BlockSpec((1,) + weights.shape[1:], lambda h, b: (h, 0, 0)),
            pl.BlockSpec((rows, model), lambda h, b: (0, 0)),
        ],
        out_shape=[
            jax.ShapeDtypeStruct(weights.shape, low_type),
            jax.ShapeDtypeStruct((rows, model), low_type),
        ],
        scratch_shapes=[
            pltpu.VMEM(weights.shape[1:], wide),
            pltpu.VMEM((rows, model), wide),
        ],
        compiler_params=pltpu.CompilerParams(vmem_limit_bytes=48 * 1024 * 1024),
        cost_estimate=pl.CostEstimate(
            flops=2 * rows * model * heads * width * 6,
            bytes_accessed=heads * rows * width * 14 + weights.size * 4 + rows * model * 6,
            transcendentals=heads * rows * width * 6,
        ),
        name="mixer_backward",
    )(mix_in, res_low, position, weights, *saved)


def ffn_kernel(
    x_ref, go_ref, w_ref, grad_ref, out_ref, gin_ref, acc_w, acc_out, acc_in
):
    tile = pl.program_id(0)
    block = pl.program_id(1)
    slots = x_ref.shape[0]
    x = x_ref[...]
    grad_out = go_ref[...]
    pre_gate = dot_rows(x, w_ref[0])
    pre_up = dot_rows(x, w_ref[1])
    active, slope = gelu_parts(pre_gate)
    ffn_low = (active * pre_up).astype(low_type)
    grad_act = dot_rows(grad_out, w_ref[2])
    gate_low = (grad_act * pre_up * slope).astype(low_type)
    up_low = (grad_act * active).astype(low_type)
    part_out = dot_plain(ffn_low, w_ref[2])
    part_in = dot_plain(gate_low, w_ref[0]) + dot_plain(up_low, w_ref[1])
    rows = pl.ds(pl.multiple_of(block * slots, slots), slots)

    @pl.when(block == 0)
    def _():
        acc_w[...] = jnp.zeros_like(acc_w)

    acc_w[0] += dot_slots(gate_low, x)
    acc_w[1] += dot_slots(up_low, x)
    acc_w[2] += dot_slots(ffn_low, grad_out)

    @pl.when(tile == 0)
    def _():
        acc_out[rows, :] = part_out
        acc_in[rows, :] = part_in

    @pl.when(tile > 0)
    def _():
        acc_out[rows, :] += part_out
        acc_in[rows, :] += part_in

    @pl.when(block == pl.num_programs(1) - 1)
    def _():
        grad_ref[...] = acc_w[...].astype(low_type)

    @pl.when(tile == pl.num_programs(0) - 1)
    def _():
        out_ref[rows, :] = acc_out[rows, :].astype(low_type)
        gin_ref[rows, :] = acc_in[rows, :].astype(low_type)


def ffn_both(x, grad_out, weights, slots, tile):
    rows, model = x.shape
    hidden = weights.shape[1]
    return pl.pallas_call(
        ffn_kernel,
        grid=(hidden // tile, rows // slots),
        in_specs=[
            pl.BlockSpec((slots, model), lambda j, b: (b, 0)),
            pl.BlockSpec((slots, model), lambda j, b: (b, 0)),
            pl.BlockSpec((3, tile, model), lambda j, b: (0, j, 0)),
        ],
        out_specs=[
            pl.BlockSpec((3, tile, model), lambda j, b: (0, j, 0)),
            pl.BlockSpec((rows, model), lambda j, b: (0, 0)),
            pl.BlockSpec((rows, model), lambda j, b: (0, 0)),
        ],
        out_shape=[
            jax.ShapeDtypeStruct(weights.shape, low_type),
            jax.ShapeDtypeStruct((rows, model), low_type),
            jax.ShapeDtypeStruct((rows, model), low_type),
        ],
        scratch_shapes=[
            pltpu.VMEM((3, tile, model), wide),
            pltpu.VMEM((rows, model), wide),
            pltpu.VMEM((rows, model), wide),
        ],
        compiler_params=pltpu.CompilerParams(vmem_limit_bytes=58 * 1024 * 1024),
        cost_estimate=pl.CostEstimate(
            flops=2 * rows * model * hidden * 9,
            bytes_accessed=weights.size * 4 + rows * model * 16,
            transcendentals=rows * hidden,
        ),
        name="ffn_both",
    )(x, grad_out, weights)


def peer_x(chip):
    return chip + 1 - 2 * (chip % 2)


def peer_y(chip):
    return chip + 2 - 4 * (chip // 2)


def line_place(end, core):
    return end + core * (3 - 2 * end)


def remote(source, target, send, recv, member, z):
    return pltpu.make_async_remote_copy(
        src_ref=source,
        dst_ref=target,
        send_sem=send,
        recv_sem=recv,
        device_id=(member, z),
        device_id_type=pl.DeviceIdType.MESH,
    )


def enter(member, z):
    barrier = pltpu.get_barrier_semaphore()
    for other in range(8):

        @pl.when(member != other)
        def _():
            pl.semaphore_signal(
                barrier, inc=1, device_id=(other, z), device_id_type=pl.DeviceIdType.MESH
            )

    for other in range(4):

        @pl.when(z != other)
        def _():
            pl.semaphore_signal(
                barrier, inc=1, device_id=(member, other), device_id_type=pl.DeviceIdType.MESH
            )

    pl.semaphore_wait(barrier, 10)


class Gather:
    def __init__(self, own, target, send, recv, member, z):
        self.own, self.target = own, target
        self.send, self.recv = send, recv
        chip, core = member // 2, member % 2
        self.to_x = peer_x(chip) * 2 + core
        self.to_y = peer_y(chip) * 2 + core
        self.z = z
        self.half = own.shape[0] // 2

    def copy(self, number):
        low, high = pl.ds(0, self.half), pl.ds(self.half, self.half)
        source, target, to = (
            (self.own, self.target.at[1], self.to_x),
            (self.own, self.target.at[2], self.to_y),
            (self.target.at[1, low], self.target.at[3, low], self.to_y),
            (self.target.at[2, high], self.target.at[3, high], self.to_x),
        )[number]
        return remote(source, target, self.send.at[number], self.recv.at[number], to, self.z)

    def begin(self):
        self.copy(0).start()
        self.copy(1).start()

    def relay(self):
        self.copy(0).wait_recv()
        self.copy(2).start()
        self.copy(1).wait_recv()
        self.copy(3).start()

    def arrive(self):
        self.copy(2).wait_recv()
        self.copy(3).wait_recv()

    def finish(self):
        for number in range(4):
            self.copy(number).wait_send()


class Reduce:
    def __init__(self, part, from_x, from_y, passing, last, send, recv, member, z):
        self.part, self.from_x, self.from_y = part, from_x, from_y
        self.passing, self.last = passing, last
        self.send, self.recv = send, recv
        chip, core = member // 2, member % 2
        self.to_x = peer_x(chip) * 2 + core
        self.to_y = peer_y(chip) * 2 + core
        self.z = z
        self.slots = part.shape[0] // 4
        self.half = self.slots // 2

    def copy(self, number):
        slots, half = self.slots, self.half
        source, target, to = (
            (self.part.at[pl.ds(slots, half)], self.from_x.at[0], self.to_x),
            (self.part.at[pl.ds(3 * slots, half)], self.from_x.at[1], self.to_x),
            (self.part.at[pl.ds(2 * slots + half, half)], self.from_y.at[0], self.to_y),
            (self.part.at[pl.ds(3 * slots + half, half)], self.from_y.at[1], self.to_y),
            (self.passing.at[0], self.last.at[0], self.to_y),
            (self.passing.at[1], self.last.at[1], self.to_x),
        )[number]
        return remote(source, target, self.send.at[number], self.recv.at[number], to, self.z)

    def begin(self):
        for number in (1, 3, 0, 2):
            self.copy(number).start()

    def relay(self):
        slots, half = self.slots, self.half
        self.copy(1).wait_recv()
        self.passing[0] = (
            self.part[2 * slots : 2 * slots + half].astype(wide) + self.from_x[1].astype(wide)
        ).astype(low_type)
        self.copy(4).start()
        self.copy(3).wait_recv()
        self.passing[1] = (
            self.part[slots + half : 2 * slots].astype(wide) + self.from_y[1].astype(wide)
        ).astype(low_type)
        self.copy(5).start()

    def arrive(self):
        for number in (0, 2, 4, 5):
            self.copy(number).wait_recv()

    def result(self, number):
        direct = self.from_x if number == 0 else self.from_y
        return (
            self.part[number * self.half : (number + 1) * self.half].astype(wide)
            + direct[0].astype(wide)
            + self.last[number].astype(wide)
        )

    def finish(self):
        for number in range(6):
            self.copy(number).wait_send()

    @staticmethod
    def scratch(slots, model):
        return [pltpu.VMEM((2, slots // 2, model), low_type)] * 4


def norm_rows(value, gain):
    scale = lax.rsqrt(jnp.mean(value * value, axis=1, keepdims=True) + norm_eps)
    return value * scale * gain


def front_kernel(
    sizes,
    tokens_ref,
    cot_ref,
    gain_ref,
    small_ref,
    in_ref,
    gate_ref,
    out_ref,
    up_ref,
    down_ref,
    mix_in,
    weights,
    ffn_weights,
    saved_p,
    saved_state,
    saved_low,
    starts_out,
    residual_out,
    ffn_in,
    cot_out,
    gains_out,
    tokens_all,
    raw_in,
    raw_up,
    turned,
    gain_seen,
    acc,
    part,
    from_x,
    from_y,
    passing,
    last,
    load_sem,
    gain_send,
    gain_recv,
    m_send,
    m_recv,
    m_core_send,
    m_core_recv,
    f_send,
    f_recv,
    f_core_send,
    f_core_recv,
    g_send,
    g_recv,
    r_send,
    r_recv,
):
    model, width, ffn_width = sizes
    member = lax.axis_index("dp")
    z = lax.axis_index("shard")
    chip, core = member // 2, member % 2
    end = z + core * (3 - 2 * z)
    other = chip * 2 + 1 - core
    slots = cot_ref.shape[0]
    half_ffn = ffn_width // 2
    owner = core == z // 2

    window = 128 * ((chip * ffn_width) // 128)
    skew = chip * ffn_width - window
    quarter = pl.ds(pl.multiple_of(chip * width, width), width)
    wide_window = pl.ds(pl.multiple_of(window, 128), raw_up.shape[2])

    def loads():
        found = []
        for kind in range(2):
            found.append((in_ref.at[kind, :, quarter], raw_in.at[kind]))
            found.append(
                (
                    gate_ref.at[kind, chip],
                    weights.at[end, pl.ds(kind * width, width), pl.ds(model, width)],
                )
            )
        found.append((out_ref.at[quarter], weights.at[end, pl.ds(2 * width, width), pl.ds(0, model)]))
        found.append(
            (
                small_ref.at[:, quarter],
                weights.at[end, pl.ds(2 * width, 16), pl.ds(model, width)],
            )
        )
        for kind in range(2):
            found.append((up_ref.at[kind, :, wide_window], raw_up.at[kind]))
        found.append(
            (
                down_ref.at[pl.ds(pl.multiple_of(chip * ffn_width, 32), ffn_width)],
                ffn_weights.at[2, pl.ds(pl.multiple_of(end * ffn_width, 32), ffn_width)],
            )
        )
        return [
            pltpu.make_async_copy(source, target, load_sem.at[number])
            for number, (source, target) in enumerate(found)
        ]

    def turned_copy(kind):
        return pltpu.make_async_copy(
            turned.at[kind, pl.ds(pl.multiple_of(skew, 32), ffn_width)],
            ffn_weights.at[kind, pl.ds(pl.multiple_of(end * ffn_width, 32), ffn_width)],
            load_sem.at[9 + kind],
        )

    @pl.when(owner)
    def _():
        for copy in loads():
            copy.start()

    enter(member, z)

    gather_tokens = Gather(tokens_ref, tokens_all, g_send.at[0], g_recv.at[0], member, z)
    gather_cot = Gather(cot_ref, cot_out, g_send.at[1], g_recv.at[1], member, z)
    gather_ffn = Gather(ffn_in.at[0], ffn_in, g_send.at[2], g_recv.at[2], member, z)
    reduce = Reduce(part, from_x, from_y, passing, last, r_send, r_recv, member, z)
    own_cot = pltpu.make_async_copy(cot_ref, cot_out.at[0], load_sem.at[11])

    gather_tokens.begin()
    own_cot.start()

    def gain_copy(to, slot):
        return remote(
            gain_ref, gain_seen.at[slot], gain_send.at[to], gain_recv.at[slot], member, to
        )

    for to in range(4):

        @pl.when(to != z)
        def _():
            gain_copy(to, z).start()

    gain_seen[z] = gain_ref[...]

    def m_rows(number):
        return pl.ds(number * width, width)

    def m_copy(slot, number, way, to_end):
        place = weights.at[slot, m_rows(number)]
        return remote(
            place,
            place,
            m_send.at[way, slot, number],
            m_recv.at[slot, number],
            member,
            line_place(to_end, core),
        )

    def m_core(slot, number):
        return remote(
            weights.at[slot, m_rows(number)],
            weights.at[2 + slot, m_rows(number)],
            m_core_send.at[slot, number],
            m_core_recv.at[slot, number],
            other,
            z,
        )

    def f_place(slot, number):
        row = slot * ffn_width + (number % 2) * half_ffn
        return ffn_weights.at[number // 2, pl.ds(row, half_ffn)]

    def f_copy(slot, number, way, to_end):
        place = f_place(slot, number)
        return remote(
            place,
            place,
            f_send.at[way, slot, number],
            f_recv.at[slot, number],
            member,
            line_place(to_end, core),
        )

    def f_core(slot, number):
        return remote(
            f_place(slot, number),
            f_place(2 + slot, number),
            f_core_send.at[slot, number],
            f_core_recv.at[slot, number],
            other,
            z,
        )

    def pass_on(copy, core_copy, slot, number):
        if slot == 0:

            @pl.when(end < 3)
            def _():
                copy(slot, number, 0, end + 1).start()
        else:

            @pl.when((end == 1) | (end == 2))
            def _():
                copy(slot, number, 0, end + 1).start()

            @pl.when(end == 1)
            def _():
                copy(slot, number, 1, 0).start()

        core_copy(slot, number).start()

    @pl.when(owner)
    def _():
        for copy in loads()[:6]:
            copy.wait()
        for kind in range(2):
            for at in range(model // 128):
                weights[end, kind * width : (kind + 1) * width, at * 128 : (at + 1) * 128] = (
                    raw_in[kind, at * 128 : (at + 1) * 128, :].astype(wide).T.astype(low_type)
                )
        for row in range(2 * width + 16, 3 * width, 16):
            weights[end, row : row + 16, model:] = jnp.zeros((16, width), low_type)

    for slot in range(2):

        @pl.when(end == slot)
        def _():
            for number in range(3):
                pass_on(m_copy, m_core, slot, number)

    @pl.when(owner)
    def _():
        for copy in loads()[6:]:
            copy.wait()
        for kind in range(2):

            def turn(at, carry):
                columns = pl.ds(pl.multiple_of(at * 128, 128), 128)
                for tile in range(raw_up.shape[2] // 128):
                    turned[kind, tile * 128 : (tile + 1) * 128, columns] = (
                        raw_up[kind, columns, tile * 128 : (tile + 1) * 128]
                        .astype(wide)
                        .T.astype(low_type)
                    )
                return carry

            lax.fori_loop(0, model // 128, turn, 0)
            turned_copy(kind).start()

    gather_tokens.relay()

    for number in range(3):
        for slot in range(2):

            @pl.when(end != slot)
            def _():
                m_copy(slot, number, 0, 0).wait_recv()
                pass_on(m_copy, m_core, slot, number)

    @pl.when(owner)
    def _():
        turned_copy(0).wait()
        turned_copy(1).wait()

    for slot in range(2):

        @pl.when(end == slot)
        def _():
            for number in range(6):
                pass_on(f_copy, f_core, slot, number)

    def f_step(step):
        slot, number = 1 - step % 2, step // 2

        @pl.when((end != slot) & (end < 3))
        def _():
            f_copy(slot, number, 0, 0).wait_recv()
            pass_on(f_copy, f_core, slot, number)

    for to in range(4):

        @pl.when(to != z)
        def _():
            gain_copy(to, to).wait_recv()

    gains = jnp.concatenate([gain_seen[at].astype(wide) for at in range(4)], axis=1)
    gains_out[...] = gains[0:8]
    gather_tokens.arrive()

    def norm_block(block):
        if block == 0:
            source, starts = tokens_ref[:, :model], tokens_ref[:, model:]
        else:
            source, starts = tokens_all[block, :, :model], tokens_all[block, :, model:]
        at = slice(block * slots, (block + 1) * slots)
        mix_in[at, :] = norm_rows(source.astype(wide), gains_out[0:1]).astype(low_type)
        starts_out[at, :] = starts

    for block in range(4):
        norm_block(block)
    gather_cot.begin()
    for step in range(3):
        f_step(step)

    for head in range(4):
        if head >= 2:
            for number in range(3):
                m_core(head - 2, number).wait_recv()
        views = weight_views(weights.at[pl.ds(head, 1)], width)

        def step_block(block, carry):
            rows = pl.ds(pl.multiple_of(block * slots, slots), slots)
            position = slot_position(starts_out[rows, :])
            projected, states, mixed_low, product = mixer_step(
                mix_in[rows, :], position, views, width
            )
            saved_p[head, rows, :] = projected
            saved_state[head, rows, :] = states
            saved_low[head, rows, :] = mixed_low
            if head == 0:
                acc[rows, :] = product
            elif head < 3:
                acc[rows, :] += product
            else:
                part[rows, :] = (acc[rows, :] + product).astype(low_type)
            return carry

        lax.fori_loop(0, 4, step_block, 0)
        f_step(2 * head + 3)
        if head < 3:
            f_step(2 * head + 4)
        if head == 0:
            gather_cot.relay()
        if head == 3:
            reduce.begin()

    f_step(10)
    f_step(11)
    reduce.relay()
    reduce.arrive()
    half = slots // 2
    for number in range(2):
        at = slice(number * half, (number + 1) * half)
        residual = tokens_ref[at, :model].astype(wide) + reduce.result(number)
        residual_out[at, :] = residual
        ffn_in[0, at, :] = norm_rows(residual, gains_out[1:2]).astype(low_type)
    gather_ffn.begin()
    gather_ffn.relay()

    @pl.when(end == 3)
    def _():
        for number in range(6):
            for slot in (1, 0):
                f_copy(slot, number, 0, 0).wait_recv()
                f_core(slot, number).start()

    gather_ffn.arrive()
    gather_cot.arrive()
    own_cot.wait()
    for slot in range(2):
        for number in range(6):
            f_core(slot, number).wait_recv()

    for gather in (gather_tokens, gather_cot, gather_ffn, reduce):
        gather.finish()
    for to in range(4):

        @pl.when(to != z)
        def _():
            gain_copy(to, z).wait_send()

    for copy, core_copy, count in ((m_copy, m_core, 3), (f_copy, f_core, 6)):
        for number in range(count):
            for slot in range(2):
                core_copy(slot, number).wait_send()

            @pl.when(end < 3)
            def _():
                copy(0, number, 0, 0).wait_send()

            @pl.when((end == 1) | (end == 2))
            def _():
                copy(1, number, 0, 0).wait_send()

            @pl.when(end == 1)
            def _():
                copy(1, number, 1, 0).wait_send()


def front(tokens, cot, gains, small, in_proj, gates, out_proj, gate_up, down, sizes):
    model, width, ffn_width = sizes
    slots = cot.shape[0]
    rows = 4 * slots
    dma = pltpu.SemaphoreType.DMA
    vmem = pl.BlockSpec(memory_space=pltpu.VMEM)
    anywhere = pl.BlockSpec(memory_space=pl.ANY)
    window = -(-ffn_width // 128) * 128
    return pl.pallas_call(
        functools.partial(front_kernel, sizes),
        in_specs=[vmem] * 3 + [anywhere] * 6,
        out_specs=[vmem, vmem, anywhere, vmem, vmem, vmem, vmem, vmem, vmem, anywhere, vmem],
        out_shape=[
            jax.ShapeDtypeStruct((rows, model), low_type),
            jax.ShapeDtypeStruct((4, 3 * width, model + width), low_type),
            jax.ShapeDtypeStruct((3, 4 * ffn_width, model), low_type),
            jax.ShapeDtypeStruct((4, rows, 2 * width), wide),
            jax.ShapeDtypeStruct((4, rows, width), wide),
            jax.ShapeDtypeStruct((4, rows, width), low_type),
            jax.ShapeDtypeStruct((rows, width), low_type),
            jax.ShapeDtypeStruct((slots, model), wide),
            jax.ShapeDtypeStruct((4, slots, model), low_type),
            jax.ShapeDtypeStruct((4, slots, model), low_type),
            jax.ShapeDtypeStruct((8, model), wide),
        ],
        scratch_shapes=[
            pltpu.VMEM((4, slots, model + width), low_type),
            pltpu.VMEM((2, model, width), low_type),
            pltpu.VMEM((2, model, window), low_type),
            pltpu.VMEM((2, window, model), low_type),
            pltpu.VMEM((4, 16, model // 4), low_type),
            pltpu.VMEM((rows, model), wide),
            pltpu.VMEM((rows, model), low_type),
        ]
        + Reduce.scratch(slots, model)
        + [
            dma((12,)),
            dma((4,)),
            dma((4,)),
            dma((2, 2, 3)),
            dma((2, 3)),
            dma((2, 3)),
            dma((2, 3)),
            dma((2, 2, 6)),
            dma((2, 6)),
            dma((2, 6)),
            dma((2, 6)),
            dma((3, 4)),
            dma((3, 4)),
            dma((6,)),
            dma((6,)),
        ],
        compiler_params=pltpu.CompilerParams(
            collective_id=3, has_side_effects=True, vmem_limit_bytes=60 * 1024 * 1024
        ),
        cost_estimate=pl.CostEstimate(
            flops=2 * rows * model * 4 * width * 3,
            bytes_accessed=6 * ffn_width * 4 * model,
            transcendentals=rows * 4 * width * 6,
        ),
        name="front",
    )(tokens, cot, gains, small, in_proj, gates, out_proj, gate_up, down)


class Scatter:
    def __init__(self, sizes, member, z, send_sem, recv_sem):
        self.model, self.width, self.ffn_width, self.piece_length = sizes
        self.member, self.z = member, z
        self.chip, self.core = member // 2, member % 2
        self.owner = self.core == z // 2
        self.send_sem, self.recv_sem = send_sem, recv_sem
        self.across = self.model // 128
        rec, ffn, model = 4 * self.width, 4 * self.ffn_width, self.model
        self.gate_base = 2 * model * rec
        self.out_base = self.gate_base + 8 * self.width * self.width
        self.up_base = self.out_base + rec * model
        self.down_base = self.up_base + 2 * model * ffn
        self.rec, self.ffn = rec, ffn
        self.first_in = 0
        self.first_gate = 2 * self.across
        self.first_out = self.first_gate + 2
        self.first_small = self.first_out + 4
        self.first_up = self.first_small + 1
        self.first_down = self.first_up + 2 * self.across
        self.count = self.first_down + 6

    def in_unit(self, number, q):
        kind, at = number // self.across, number % self.across
        low = (kind * self.model + at * 128) * self.rec
        where = (
            pl.ds(pl.multiple_of(kind * self.width, self.width), self.width),
            pl.ds(pl.multiple_of(at * 128, 128), 128),
        )
        return self.first_in + number, where, low, low + 128 * self.rec

    def gate_unit(self, kind, q):
        low = self.gate_base + (kind * 4 + q) * self.width * self.width
        where = (
            pl.ds(pl.multiple_of(kind * self.width, self.width), self.width),
            pl.ds(self.model, self.width),
        )
        return self.first_gate + kind, where, low, low + self.width * self.width

    def out_unit(self, number, q):
        rows = self.width // 4
        low = self.out_base + (q * self.width + number * rows) * self.model
        where = (
            pl.ds(pl.multiple_of(2 * self.width + number * rows, rows), rows),
            pl.ds(0, self.model),
        )
        return self.first_out + number, where, low, low + rows * self.model

    def up_unit(self, number, q):
        kind, at = number // self.across, number % self.across
        low = self.up_base + (kind * self.model + at * 128) * self.ffn
        where = (kind, pl.ds(0, self.ffn_width), pl.ds(pl.multiple_of(at * 128, 128), 128))
        return self.first_up + number, where, low, low + 128 * self.ffn

    def down_unit(self, number, q):
        rows = self.ffn_width // 6
        low = self.down_base + (q * self.ffn_width + number * rows) * self.model
        where = (2, pl.ds(pl.multiple_of(number * rows, 16), rows), pl.ds(0, self.model))
        return self.first_down + number, where, low, low + rows * self.model

    def small_where(self):
        return (pl.ds(2 * self.width, 16), pl.ds(self.model, self.width))

    def copies(self, unit, source, target, q, act):
        number, where, low, high = unit
        first = low // self.piece_length
        last = (high - 1) // self.piece_length
        for which, to in ((0, first), (1, last)):
            wanted = True if which == 0 else last != first

            @pl.when((to != self.member) & wanted)
            def _():
                act(
                    remote(
                        source.at[where],
                        target.at[(q,) + where],
                        self.send_sem.at[which, number],
                        self.recv_sem.at[q, number],
                        to,
                        self.z,
                    ),
                    True,
                )

            @pl.when((to == self.member) & wanted)
            def _():
                act(
                    pltpu.make_async_copy(
                        source.at[where], target.at[(q,) + where], self.recv_sem.at[q, number]
                    ),
                    False,
                )

    def each(self, unit_of, low, high, source, target, act):
        def body(number, carry):
            self.copies(unit_of(number, self.chip), source, target, self.chip, act)
            return carry

        lax.fori_loop(low, high, body, 0)

    def smalls(self, source, target, act):
        where = self.small_where()
        for to in range(8):

            @pl.when(self.member != to)
            def _():
                act(
                    remote(
                        source.at[where],
                        target.at[(self.chip,) + where],
                        self.send_sem.at[2, to],
                        self.recv_sem.at[self.chip, self.first_small],
                        to,
                        self.z,
                    ),
                    True,
                )

        act(
            pltpu.make_async_copy(
                source.at[where],
                target.at[(self.chip,) + where],
                self.recv_sem.at[self.chip, self.first_small],
            ),
            False,
        )

    def arrivals(self, unit_of, count, source, target):
        low = self.member * self.piece_length

        def body(number, carry):
            for q in range(4):
                index, where, first, last = unit_of(number, q)
                mine = (first < low + self.piece_length) & (last > low)
                here = (self.chip == q) & self.owner

                @pl.when(mine & here)
                def _():
                    pltpu.make_async_copy(
                        source.at[where], target.at[(q,) + where], self.recv_sem.at[q, index]
                    ).wait()

                @pl.when(mine & jnp.logical_not(here))
                def _():
                    remote(
                        source.at[where],
                        target.at[(q,) + where],
                        self.send_sem.at[0, index],
                        self.recv_sem.at[q, index],
                        self.member,
                        self.z,
                    ).wait_recv()

            return carry

        lax.fori_loop(0, count, body, 0)

    def small_arrivals(self, source, target):
        where = self.small_where()
        for q in range(4):
            here = (self.chip == q) & self.owner

            @pl.when(here)
            def _():
                pltpu.make_async_copy(
                    source.at[where],
                    target.at[(q,) + where],
                    self.recv_sem.at[q, self.first_small],
                ).wait()

            @pl.when(jnp.logical_not(here))
            def _():
                remote(
                    source.at[where],
                    target.at[(q,) + where],
                    self.send_sem.at[2, 0],
                    self.recv_sem.at[q, self.first_small],
                    self.member,
                    self.z,
                ).wait_recv()


def begin(copy, is_remote):
    copy.start()


def finish_send(copy, is_remote):
    if is_remote:
        copy.wait_send()


def sums_kernel(
    sizes,
    mix_ref,
    part_ref,
    ffn_ref,
    tokens_ref,
    res_ref,
    gain_ref,
    mix_out,
    ffn_out,
    tokens_out,
    gain_out,
    paired,
    arrived,
    total,
    from_x,
    from_y,
    passing,
    last,
    gain_part,
    gain_plane,
    gain_line,
    gain_seen,
    core_send,
    core_recv,
    line_send,
    line_recv,
    plane_send,
    plane_recv,
    gain_send,
    gain_recv,
    unit_send,
    unit_recv,
):
    model, width, ffn_width, piece_length = sizes
    member = lax.axis_index("dp")
    z = lax.axis_index("shard")
    chip, core = member // 2, member % 2
    end = z + core * (3 - 2 * z)
    slots = tokens_ref.shape[0]
    half = slots // 2
    to_x = peer_x(chip) * 2 + core
    to_y = peer_y(chip) * 2 + core
    other = chip * 2 + 1 - core
    scatter = Scatter(sizes, member, z, unit_send, unit_recv)
    enter(member, z)

    def rows(number):
        return pl.ds(number * width, width)

    def core_copy(slot, number):
        return remote(
            mix_ref.at[2 + slot, rows(number)],
            paired.at[slot, rows(number)],
            core_send.at[slot, number],
            core_recv.at[slot, number],
            other,
            z,
        )

    for slot in range(2):
        for number in range(3):
            core_copy(slot, number).start()

    def plane_copy(number):
        source, target, to = (
            (part_ref.at[pl.ds(slots, half)], from_x.at[0], to_x),
            (part_ref.at[pl.ds(3 * slots, half)], from_x.at[1], to_x),
            (part_ref.at[pl.ds(2 * slots + half, half)], from_y.at[0], to_y),
            (part_ref.at[pl.ds(3 * slots + half, half)], from_y.at[1], to_y),
            (passing.at[0], last.at[0], to_y),
            (passing.at[1], last.at[1], to_x),
        )[number]
        return remote(source, target, plane_send.at[number], plane_recv.at[number], to, z)

    for number in (1, 3, 0, 2):
        plane_copy(number).start()

    @pl.when(scatter.owner)
    def _():
        scatter.each(scatter.up_unit, 0, 2 * scatter.across, ffn_ref, ffn_out, begin)
        scatter.each(scatter.down_unit, 0, 6, ffn_ref, ffn_out, begin)

    def line_copy(kind, number, source, to_end):
        return remote(
            source,
            arrived.at[kind, rows(number)],
            line_send.at[kind, number],
            line_recv.at[kind, number],
            member,
            line_place(to_end, core),
        )

    for slot in range(2):
        for number in range(3):
            core_copy(slot, number).wait_recv()
            both = mix_ref[slot, rows(number)].astype(wide) + paired[slot, rows(number)].astype(wide)
            paired[slot, rows(number)] = both.astype(low_type)

            @pl.when(end == 3)
            def _():
                line_copy(slot, number, paired.at[slot, rows(number)], 2).start()

            if slot == 1:

                @pl.when(end == 0)
                def _():
                    line_copy(2, number, paired.at[slot, rows(number)], 1).start()

    plane_copy(1).wait_recv()
    passing[0] = (
        part_ref[2 * slots : 2 * slots + half].astype(wide) + from_x[1].astype(wide)
    ).astype(low_type)
    plane_copy(4).start()
    plane_copy(3).wait_recv()
    passing[1] = (
        part_ref[slots + half : 2 * slots].astype(wide) + from_y[1].astype(wide)
    ).astype(low_type)
    plane_copy(5).start()

    def summed(slot, kinds, number):
        result = paired[slot, rows(number)].astype(wide)
        for kind in kinds:
            result = result + arrived[kind, rows(number)].astype(wide)
        return result.astype(low_type)

    def on_arrival(kind, number):
        line_copy(kind, number, paired.at[0, rows(number)], 0).wait_recv()

    def share(number):
        if number < 2:
            across = scatter.across
            scatter.each(
                scatter.in_unit, number * across, (number + 1) * across, total, mix_out, begin
            )
            scatter.each(scatter.gate_unit, number, number + 1, total, mix_out, begin)
        else:
            scatter.each(scatter.out_unit, 0, 4, total, mix_out, begin)
            scatter.smalls(total, mix_out, begin)

    for number in range(3):

        @pl.when((end == 2) | (end == 1))
        def _():
            on_arrival(0, number)
            paired[0, rows(number)] = summed(0, (0,), number)

        @pl.when(end == 2)
        def _():
            line_copy(0, number, paired.at[0, rows(number)], 1).start()

        @pl.when(end == 1)
        def _():
            line_copy(0, number, paired.at[0, rows(number)], 0).start()

    for number in range(3):

        @pl.when(end == 2)
        def _():
            on_arrival(1, number)
            paired[1, rows(number)] = summed(1, (1,), number)
            line_copy(1, number, paired.at[1, rows(number)], 1).start()

        @pl.when(end == 1)
        def _():
            on_arrival(1, number)
            on_arrival(2, number)
            total[rows(number)] = summed(1, (1, 2), number)

        @pl.when(end == 0)
        def _():
            on_arrival(0, number)
            total[rows(number)] = summed(0, (0,), number)

        @pl.when(scatter.owner)
        def _():
            share(number)

    plane_copy(0).wait_recv()
    plane_copy(2).wait_recv()
    plane_copy(4).wait_recv()
    plane_copy(5).wait_recv()
    gain = gain_ref[0:1]
    gain_sum = jnp.zeros((1, model), wide)
    for number, direct in ((0, from_x), (1, from_y)):
        at = slice(number * half, (number + 1) * half)
        grad = part_ref[at].astype(wide) + direct[0].astype(wide) + last[number].astype(wide)
        value = tokens_ref[at].astype(wide)
        scale = lax.rsqrt(jnp.mean(value * value, axis=1, keepdims=True) + norm_eps)
        scaled = grad * gain
        gain_sum = gain_sum + jnp.sum(grad * value * scale, axis=0, keepdims=True)
        inner = jnp.mean(scaled * value, axis=1, keepdims=True)
        back = scale * scaled - value * (scale * scale * scale * inner)
        tokens_out[at] = (res_ref[at] + back).astype(low_type)
    gain_part[...] = jnp.concatenate([gain_sum, gain_ref[1:2], jnp.zeros((6, model), wide)], axis=0)

    def gain_copy():
        return remote(
            gain_part, gain_plane.at[member], gain_send.at[0], gain_recv.at[member], 7, z
        )

    @pl.when(member != 7)
    def _():
        gain_copy().start()
        gain_copy().wait_send()
        gain_out[...] = jnp.zeros_like(gain_out)

    @pl.when(member == 7)
    def _():
        result = gain_part[...]
        for source in range(7):
            remote(
                gain_part,
                gain_plane.at[source],
                gain_send.at[0],
                gain_recv.at[source],
                7,
                z,
            ).wait_recv()
            result = result + gain_plane[source]
        quarter = model // 4
        for place in range(4):
            gain_line[place] = result[:, place * quarter : (place + 1) * quarter]

        def line_gain(place, slot):
            return remote(
                gain_line.at[place],
                gain_seen.at[slot],
                gain_send.at[1 + place],
                gain_recv.at[8 + slot],
                7,
                place,
            )

        for place in range(4):

            @pl.when(place != z)
            def _():
                line_gain(place, z).start()

        gain_out[...] = gain_line[z]
        for place in range(4):

            @pl.when(place != z)
            def _():
                line_gain(place, place).wait_recv()
                gain_out[...] += gain_seen[place]
                line_gain(place, z).wait_send()

    across = scatter.across
    scatter.arrivals(scatter.up_unit, 2 * across, ffn_ref, ffn_out)
    scatter.arrivals(scatter.down_unit, 6, ffn_ref, ffn_out)
    scatter.arrivals(scatter.in_unit, 2 * across, total, mix_out)
    scatter.arrivals(scatter.gate_unit, 2, total, mix_out)
    scatter.arrivals(scatter.out_unit, 4, total, mix_out)
    scatter.small_arrivals(total, mix_out)

    @pl.when(scatter.owner)
    def _():
        scatter.each(scatter.up_unit, 0, 2 * across, ffn_ref, ffn_out, finish_send)
        scatter.each(scatter.down_unit, 0, 6, ffn_ref, ffn_out, finish_send)
        scatter.each(scatter.in_unit, 0, 2 * across, total, mix_out, finish_send)
        scatter.each(scatter.gate_unit, 0, 2, total, mix_out, finish_send)
        scatter.each(scatter.out_unit, 0, 4, total, mix_out, finish_send)
        scatter.smalls(total, mix_out, finish_send)

    for number in range(6):
        plane_copy(number).wait_send()
    for slot in range(2):
        for number in range(3):
            core_copy(slot, number).wait_send()
    for number in range(3):

        @pl.when(end > 0)
        def _():
            line_copy(0, number, paired.at[0, rows(number)], 0).wait_send()

        @pl.when(end > 1)
        def _():
            line_copy(1, number, paired.at[1, rows(number)], 0).wait_send()

        @pl.when(end == 0)
        def _():
            line_copy(2, number, paired.at[1, rows(number)], 1).wait_send()


def sums(mix, part, ffn, tokens, residual_grad, gains, piece_length, width):
    model = tokens.shape[1]
    ffn_width = ffn.shape[1]
    sizes = (model, width, ffn_width, piece_length)
    half = tokens.shape[0] // 2
    block = mix.shape[1:]
    count = Scatter(sizes, 0, 0, None, None).count
    dma = pltpu.SemaphoreType.DMA
    vmem = pl.BlockSpec(memory_space=pltpu.VMEM)
    anywhere = pl.BlockSpec(memory_space=pl.ANY)
    return pl.pallas_call(
        functools.partial(sums_kernel, sizes),
        in_specs=[vmem, vmem, anywhere, vmem, vmem, vmem],
        out_specs=[anywhere, anywhere, vmem, vmem],
        out_shape=[
            jax.ShapeDtypeStruct(mix.shape, low_type),
            jax.ShapeDtypeStruct((4,) + ffn.shape, low_type),
            jax.ShapeDtypeStruct(tokens.shape, low_type),
            jax.ShapeDtypeStruct((8, model // 4), wide),
        ],
        scratch_shapes=[
            pltpu.VMEM((2,) + block, low_type),
            pltpu.VMEM((3,) + block, low_type),
            pltpu.VMEM(block, low_type),
            pltpu.VMEM((2, half, model), low_type),
            pltpu.VMEM((2, half, model), low_type),
            pltpu.VMEM((2, half, model), low_type),
            pltpu.VMEM((2, half, model), low_type),
            pltpu.VMEM((8, model), wide),
            pltpu.VMEM((8, 8, model), wide),
            pltpu.VMEM((4, 8, model // 4), wide),
            pltpu.VMEM((4, 8, model // 4), wide),
            dma((2, 3)),
            dma((2, 3)),
            dma((3, 3)),
            dma((3, 3)),
            dma((6,)),
            dma((6,)),
            dma((5,)),
            dma((12,)),
            dma((3, count)),
            dma((4, count)),
        ],
        compiler_params=pltpu.CompilerParams(
            collective_id=2, has_side_effects=True, vmem_limit_bytes=40 * 1024 * 1024
        ),
        cost_estimate=pl.CostEstimate(
            flops=mix.size * 4, bytes_accessed=mix.size * 8, transcendentals=0
        ),
        name="sums",
    )(mix, part, ffn, tokens, residual_grad, gains)


def tail_kernel(
    sizes,
    mix_ref,
    ffn_ref,
    gain_ref,
    master_ref,
    first_ref,
    second_ref,
    piece_ref,
    new_master_ref,
    new_first_ref,
    new_second_ref,
    weights_ref,
    bias_ref,
    grad,
    held,
    spread,
    send_sem,
    recv_sem,
):
    model, width, ffn_width, piece_length, chunks, lines, margin = sizes
    member = lax.axis_index("dp")
    z = lax.axis_index("shard")
    step = pl.program_id(0)
    lead = 128
    start_row = (member * piece_length) // lead
    offset = (member * piece_length) % lead
    tiles_in = 4 * width // lead
    tiles_ffn = 4 * ffn_width // lead
    tiles_model = model // lead

    def copy_to(origin, chunk, side, to):
        return pltpu.make_async_remote_copy(
            src_ref=held.at[origin, chunk],
            dst_ref=held.at[origin, chunk],
            send_sem=send_sem.at[side, origin, chunk],
            recv_sem=recv_sem.at[origin, chunk],
            device_id=(member, to),
            device_id_type=pl.DeviceIdType.MESH,
        )

    @pl.when(step == 0)
    def _():
        barrier = pltpu.get_barrier_semaphore()

        @pl.when(z > 0)
        def _():
            pl.semaphore_signal(
                barrier, inc=1, device_id=(member, z - 1), device_id_type=pl.DeviceIdType.MESH
            )

        @pl.when(z < 3)
        def _():
            pl.semaphore_signal(
                barrier, inc=1, device_id=(member, z + 1), device_id_type=pl.DeviceIdType.MESH
            )

        @pl.when((z == 0) | (z == 3))
        def _():
            pl.semaphore_wait(barrier, 1)

        @pl.when((z > 0) & (z < 3))
        def _():
            pl.semaphore_wait(barrier, 2)

        def clear(number, carry):
            grad[pl.ds(pl.multiple_of(number * 256, 256), 256), :] = jnp.zeros((256, lead), wide)
            return carry

        lax.fori_loop(0, grad.shape[0] // 256, clear, 0)

        def place(row, count, body):
            low = member * piece_length

            @pl.when((row * lead < low + piece_length) & ((row + count) * lead > low))
            def _():
                body(row - start_row + margin)

        base = 0

        def in_unit(number, carry):
            kind = number // tiles_model
            at = number % tiles_model

            def body(to):
                for q in range(4):
                    tile = mix_ref[
                        q,
                        pl.ds(pl.multiple_of(kind * width, width), width),
                        pl.ds(pl.multiple_of(at * lead, lead), lead),
                    ].astype(wide)
                    grad[pl.ds(to + q, lead, stride=tiles_in), :] = tile.T

            place((kind * model + at * lead) * tiles_in, lead * tiles_in, body)
            return carry

        lax.fori_loop(0, 2 * tiles_model, in_unit, 0)
        base = 2 * model * tiles_in

        def gate_body(number, carry):
            kind = number // 4
            q = number % 4

            def body(to):
                grad[pl.ds(to, width), :] = mix_ref[
                    q, pl.ds(pl.multiple_of(kind * width, width), width), model:
                ].astype(wide)

            place(2 * model * tiles_in + number * width, width, body)
            return carry

        lax.fori_loop(0, 8, gate_body, 0)
        base = base + 8 * width
        out_base = base

        quarter = width // 4

        def out_unit(number, carry):
            q = number // 4
            part = number % 4

            def body(to):
                for at in range(tiles_model):
                    grad[pl.ds(to + at, quarter, stride=tiles_model), :] = mix_ref[
                        q,
                        pl.ds(pl.multiple_of(2 * width + part * quarter, quarter), quarter),
                        at * lead : (at + 1) * lead,
                    ].astype(wide)

            place(out_base + number * quarter * tiles_model, quarter * tiles_model, body)
            return carry

        lax.fori_loop(0, 16, out_unit, 0)
        base = base + 4 * width * tiles_model
        up_base = base

        def up_unit(number, carry):
            kind = number // tiles_model
            at = number % tiles_model
            columns = pl.ds(pl.multiple_of(at * lead, lead), lead)

            def body(to):
                for tile in range(tiles_ffn):
                    found = []
                    row = tile * lead
                    while row < (tile + 1) * lead:
                        q = row // ffn_width
                        last = min((q + 1) * ffn_width, (tile + 1) * lead)
                        found.append(
                            ffn_ref[
                                q,
                                kind,
                                row - q * ffn_width : last - q * ffn_width,
                                columns,
                            ].astype(wide)
                        )
                        row = last
                    block = found[0] if len(found) == 1 else jnp.concatenate(found, axis=0)
                    grad[pl.ds(to + tile, lead, stride=tiles_ffn), :] = block.T

            place(up_base + (kind * model + at * lead) * tiles_ffn, lead * tiles_ffn, body)
            return carry

        lax.fori_loop(0, 2 * tiles_model, up_unit, 0)
        base = base + 2 * model * tiles_ffn
        down_base = base
        sixth = ffn_width // 6

        def down_unit(number, carry):
            q = number // 6
            part = number % 6

            def body(to):
                for at in range(tiles_model):
                    grad[pl.ds(to + at, sixth, stride=tiles_model), :] = ffn_ref[
                        q,
                        2,
                        pl.ds(pl.multiple_of(part * sixth, 16), sixth),
                        at * lead : (at + 1) * lead,
                    ].astype(wide)

            place(down_base + number * sixth * tiles_model, sixth * tiles_model, body)
            return carry

        lax.fori_loop(0, 24, down_unit, 0)
        small_base = base + 4 * ffn_width * tiles_model
        smalls = [
            mix_ref[q, 2 * width : 2 * width + 16, model:].astype(wide)
            for q in range(4)
        ]

        def small_body(to):
            for q in range(4):
                grad[pl.ds(to + q, 8, stride=tiles_in), :] = smalls[q][:8]
            for number in range(6):
                kind, at = number // 3, number % 3
                grad[pl.ds(to + 8 * tiles_in + number, 1), :] = gain_ref[
                    kind : kind + 1, at * lead : (at + 1) * lead
                ]

        place(small_base, 8 * tiles_in + 6, small_body)
        bias_ref[...] = jnp.concatenate([small[5:7] for small in smalls], axis=1)

    @pl.when(step < chunks)
    def _():
        row = margin + step * lines
        shift = (lead - offset) % lead
        here = pltpu.roll(grad[pl.ds(row, lines), :], shift, 1)
        after = pltpu.roll(grad[pl.ds(row + 1, lines), :], shift, 1)
        lane = lax.broadcasted_iota(jnp.int32, (lines, lead), 1)
        piece = jnp.where(lane < lead - offset, here, after).reshape(1, lines * lead)
        piece_ref[...] = piece
        new_first = beta_one * first_ref[...] + (1.0 - beta_one) * piece
        new_second = beta_two * second_ref[...] + (1.0 - beta_two) * piece * piece
        master = master_ref[...]
        new_master = master - learn_rate * (
            new_first / corr_one / (jnp.sqrt(new_second / corr_two) + adam_eps)
            + weight_decay * master
        )
        new_first_ref[...] = new_first
        new_second_ref[...] = new_second
        new_master_ref[...] = new_master
        held[z, step] = new_master.reshape(lines, lead).astype(low_type)

        @pl.when(z < 3)
        def _():
            copy_to(z, step, 0, z + 1).start()

        @pl.when(z > 0)
        def _():
            copy_to(z, step, 1, z - 1).start()

    def pass_on(origin, chunk, right):
        copy_to(origin, chunk, 0, z).wait_recv()
        if right:

            @pl.when(z < 3)
            def _():
                copy_to(origin, chunk, 0, z + 1).start()
        else:

            @pl.when(z > 0)
            def _():
                copy_to(origin, chunk, 1, z - 1).start()

    @pl.when((step >= chunks) & (step < 2 * chunks))
    def _():
        chunk = step - chunks

        @pl.when(z > 0)
        def _():
            pass_on(z - 1, chunk, True)

        @pl.when(z < 3)
        def _():
            pass_on(z + 1, chunk, False)

    @pl.when(step >= 2 * chunks)
    def _():
        chunk = step - 2 * chunks

        @pl.when(z >= 2)
        def _():
            pass_on(z - 2, chunk, True)

        @pl.when(z <= 1)
        def _():
            pass_on(z + 2, chunk, False)

        @pl.when(z == 3)
        def _():
            copy_to(0, chunk, 0, z).wait_recv()

        @pl.when(z == 0)
        def _():
            copy_to(3, chunk, 0, z).wait_recv()

        for origin in range(4):
            spread[origin * lines : (origin + 1) * lines, :] = held[origin, chunk].astype(wide)

        def line(number, carry):
            weights_ref[:, pl.ds(pl.multiple_of(number * lead, lead), lead)] = spread[
                pl.ds(number, 4, stride=lines), :
            ].astype(low_type)
            return carry

        lax.fori_loop(0, lines, line, 0, unroll=8)

    @pl.when(step == 3 * chunks - 1)
    def _():
        for origin in range(4):

            def finish(chunk, carry):
                @pl.when((origin <= z) & (z < 3))
                def _():
                    copy_to(origin, chunk, 0, z).wait_send()

                @pl.when((origin >= z) & (z > 0))
                def _():
                    copy_to(origin, chunk, 1, z).wait_send()

                return carry

            lax.fori_loop(0, chunks, finish, 0)


def tail(mix, ffn, gains, master, first, second, sizes):
    model, width, ffn_width = sizes
    piece_length = master.shape[1]
    chunks = 8
    lines = -(-piece_length // (chunks * 128 * 16)) * 16
    block = lines * 128
    margin = 1536
    rows = -(-(2 * margin + chunks * lines + 8) // 256) * 256
    packed = jax.ShapeDtypeStruct(master.shape, wide)
    whole = lambda shape: pl.BlockSpec(shape, lambda s: (0,) * len(shape))
    chunk_spec = pl.BlockSpec((1, block), lambda s: (0, jnp.minimum(s, chunks - 1)))
    once = lambda shape: pl.BlockSpec(
        shape, lambda s: (0,) * len(shape), pipeline_mode=pl.Buffered(1)
    )
    return pl.pallas_call(
        functools.partial(
            tail_kernel, (model, width, ffn_width, piece_length, chunks, lines, margin)
        ),
        grid=(3 * chunks,),
        in_specs=[once(mix.shape), once(ffn.shape), once(gains.shape)] + [chunk_spec] * 3,
        out_specs=[chunk_spec] * 4
        + [
            pl.BlockSpec((4, block), lambda s: (0, jnp.maximum(s - 2 * chunks, 0))),
            whole((2, 4 * width)),
        ],
        out_shape=[packed] * 4
        + [
            jax.ShapeDtypeStruct((4, piece_length), low_type),
            jax.ShapeDtypeStruct((2, 4 * width), wide),
        ],
        scratch_shapes=[
            pltpu.VMEM((rows, 128), wide),
            pltpu.VMEM((4, chunks, lines, 128), low_type),
            pltpu.VMEM((4 * lines, 128), wide),
            pltpu.SemaphoreType.DMA((2, 4, chunks)),
            pltpu.SemaphoreType.DMA((4, chunks)),
        ],
        compiler_params=pltpu.CompilerParams(
            collective_id=1, has_side_effects=True, vmem_limit_bytes=58 * 1024 * 1024
        ),
        cost_estimate=pl.CostEstimate(
            flops=20 * piece_length,
            bytes_accessed=40 * piece_length,
            transcendentals=piece_length,
        ),
        name="tail",
    )(mix, ffn, gains, master, first, second)


def group_body(
    tokens,
    cotangent,
    seq_start,
    live_mask,
    input_proj,
    gate_blocks,
    output_proj,
    ffn_gate_up,
    ffn_down,
    conv_taps,
    gate_bias,
    decay_param,
    norm_gains,
    master_shard,
    first_moment,
    second_moment,
):
    slots, model = tokens.shape
    slice_rec = input_proj.shape[2]
    slice_ffn = ffn_down.shape[0]
    width = slice_rec // 4
    ffn_width = slice_ffn // 4
    piece_length = master_shard.shape[1]
    member = lax.axis_index("dp")
    chip = member // 2
    core = member % 2
    z = lax.axis_index("shard")
    end = jnp.where(core == 0, z, 3 - z)

    mask_rows = live_mask.astype(wide)[:, None]
    stream = tokens.astype(wide)
    grad_stream = cotangent.astype(wide) * mask_rows

    starts = jnp.broadcast_to(seq_start.astype(low_type)[:, None], (slots, width))
    (
        mix_in,
        mix_weights,
        ffn_weights,
        saved_p,
        saved_state,
        saved_low,
        all_starts,
        residual,
        ffn_in,
        all_grad_out,
        gains,
    ) = front(
        jnp.concatenate([tokens, starts], axis=1),
        grad_stream.astype(low_type),
        jnp.concatenate([norm_gains, jnp.zeros((14, norm_gains.shape[1]), low_type)]),
        jnp.concatenate(
            [conv_taps, gate_bias, decay_param[None], jnp.zeros((8, slice_rec), low_type)]
        ),
        input_proj,
        gate_blocks,
        output_proj,
        ffn_gate_up,
        ffn_down,
        (model, width, ffn_width),
    )
    saved = (saved_p, saved_state, saved_low)
    ffn_in = ffn_in.reshape(4 * slots, model)
    all_grad_out = all_grad_out.reshape(4 * slots, model)
    _, second_pull = jax.vjp(rms_scale, residual, gains[1])

    grad_ffn, ffn_part, ffn_in_part = ffn_both(
        ffn_in, all_grad_out, ffn_weights, slots, ffn_width * 4 // 3
    )
    grad_norm_two, grad_gain_two = second_pull(plane_reduce(ffn_in_part))
    grad_residual = grad_stream + grad_norm_two
    res_low = jnp.concatenate(plane_gather(grad_residual.astype(low_type)))
    block_out = (mask_rows * (residual + plane_reduce(ffn_part))).astype(low_type)

    grad_mix, mix_in_part = mix_backward(
        mix_in, res_low, all_starts, mix_weights, saved, slots, width
    )
    both = 2 * ffn_width
    pair_ffn = add_low(grad_ffn[:, :both], move(grad_ffn[:, both:], core_pairs))
    sum_ffn = line_sum(pair_ffn[:, :ffn_width], pair_ffn[:, ffn_width:], end)
    four_mix, four_ffn, tokens_grad, gain_total = sums(
        grad_mix,
        mix_in_part,
        sum_ffn,
        tokens,
        grad_residual,
        jnp.concatenate([gains[0:1], grad_gain_two[None], jnp.zeros((6, model), wide)]),
        piece_length,
        width,
    )
    piece, new_master, new_first, new_second, new_weights, bias_total = tail(
        four_mix,
        four_ffn,
        gain_total,
        master_shard,
        first_moment,
        second_moment,
        (model, width, ffn_width),
    )
    return (
        block_out,
        tokens_grad,
        piece,
        new_master,
        new_first,
        new_second,
        new_weights,
        bias_total,
    )


def rms_scale(values, gain):
    return values * lax.rsqrt(jnp.mean(values * values, axis=-1, keepdims=True) + norm_eps) * gain


def conv_mix(signal, taps, position):
    result = taps[-1] + taps[0] * signal
    for shift_by in range(1, taps.shape[0] - 1):
        moved = jnp.pad(signal, ((shift_by, 0), (0, 0)))[:-shift_by]
        result = result + taps[shift_by] * jnp.where((position >= shift_by)[:, None], moved, 0.0)
    return result


def combine_steps(earlier, later):
    decay_first, value_first = earlier
    decay_second, value_second = later
    return (decay_first * decay_second, decay_second * value_first + value_second)


def recurrence(logits, signal, branch, bias_term, decay_term, position):
    row_count = signal.shape[0]
    recur_gate = jax.nn.sigmoid(logits[0].reshape(row_count, -1) + bias_term[0])
    input_gate = jax.nn.sigmoid(logits[1].reshape(row_count, -1) + bias_term[1])
    log_decay = -gate_scale * recur_gate * jax.nn.softplus(-decay_term)
    decay_rate = jnp.where((position > 0)[:, None], jnp.exp(log_decay), 0.0)
    drive_term = jnp.sqrt(-jnp.expm1(2.0 * log_decay)) * input_gate * signal
    states = lax.associative_scan(combine_steps, (decay_rate, drive_term), axis=0)[1]
    return states * jax.nn.gelu(branch)


def gated_gelu(ffn_pre):
    return jax.nn.gelu(ffn_pre[0]) * ffn_pre[1]


def mixer_forward(
    mix_in, input_proj, gate_blocks, output_proj, conv_taps, gate_bias, decay_param, position
):
    projected = jnp.einsum("sd,kdr->ksr", mix_in, input_proj, preferred_element_type=jnp.float32)
    conv_out, conv_pull = jax.vjp(
        lambda signal, taps: conv_mix(signal, taps, position), projected[0], conv_taps
    )
    row_count = conv_out.shape[0]
    conv_low = conv_out.astype(jnp.bfloat16).reshape(
        row_count, gate_blocks.shape[1], gate_blocks.shape[2]
    )
    gate_logits = jnp.einsum(
        "shb,khbc->kshc", conv_low, gate_blocks, preferred_element_type=jnp.float32
    )
    mixed, mix_pull = jax.vjp(
        lambda logits, signal, branch, bias_term, decay_term: recurrence(
            logits, signal, branch, bias_term, decay_term, position
        ),
        gate_logits,
        conv_out,
        projected[1],
        gate_bias,
        decay_param,
    )
    mixed_low = mixed.astype(jnp.bfloat16)
    partial_out = jnp.dot(mixed_low, output_proj, preferred_element_type=jnp.float32)
    return (partial_out, (conv_pull, conv_low, mix_pull, mixed_low))


def mixer_backward(grad_out_low, mix_in, saved, input_proj, gate_blocks, output_proj):
    conv_pull, conv_low, mix_pull, mixed_low = saved
    grad_output_proj = jnp.einsum(
        "sr,sd->rd", mixed_low, grad_out_low, preferred_element_type=jnp.float32
    )
    grad_mixed = jnp.einsum(
        "sd,rd->sr", grad_out_low, output_proj, preferred_element_type=jnp.float32
    )
    grad_logits, grad_conv_direct, grad_branch, grad_bias, grad_decay = mix_pull(grad_mixed)
    logits_low = grad_logits.astype(jnp.bfloat16)
    grad_blocks = jnp.einsum(
        "shb,kshc->khbc", conv_low, logits_low, preferred_element_type=jnp.float32
    )
    grad_conv_gates = jnp.einsum(
        "kshc,khbc->shb", logits_low, gate_blocks, preferred_element_type=jnp.float32
    )
    grad_signal, grad_taps = conv_pull(
        grad_conv_direct + grad_conv_gates.reshape(grad_conv_direct.shape)
    )
    proj_low = jnp.stack([grad_signal, grad_branch]).astype(jnp.bfloat16)
    grad_input_proj = jnp.einsum(
        "sd,ksr->kdr", mix_in, proj_low, preferred_element_type=jnp.float32
    )
    grad_mix_in = jnp.einsum(
        "ksr,kdr->sd", proj_low, input_proj, preferred_element_type=jnp.float32
    )
    return (
        grad_mix_in,
        (grad_input_proj, grad_blocks, grad_output_proj, grad_taps, grad_bias, grad_decay),
    )


def ffn_forward(ffn_in_low, ffn_gate_up, ffn_down):
    ffn_pre = jnp.einsum("sd,kdf->ksf", ffn_in_low, ffn_gate_up, preferred_element_type=jnp.float32)
    ffn_act, ffn_pull = jax.vjp(gated_gelu, ffn_pre)
    ffn_low = ffn_act.astype(jnp.bfloat16)
    partial_ffn = jnp.dot(ffn_low, ffn_down, preferred_element_type=jnp.float32)
    return (partial_ffn, (ffn_pull, ffn_low))


def ffn_backward(grad_low, ffn_in_low, saved, ffn_gate_up, ffn_down):
    ffn_pull, ffn_low = saved
    grad_down = jnp.einsum("sf,sd->fd", ffn_low, grad_low, preferred_element_type=jnp.float32)
    grad_act = jnp.einsum("sd,fd->sf", grad_low, ffn_down, preferred_element_type=jnp.float32)
    grad_pre = ffn_pull(grad_act)[0]
    pre_low = grad_pre.astype(jnp.bfloat16)
    grad_gate_up = jnp.einsum(
        "sd,ksf->kdf", ffn_in_low, pre_low, preferred_element_type=jnp.float32
    )
    grad_ffn_in = jnp.einsum(
        "ksf,kdf->sd", pre_low, ffn_gate_up, preferred_element_type=jnp.float32
    )
    return (grad_ffn_in, grad_gate_up, grad_down)


def body(
    tokens,
    cotangent,
    seq_start,
    live_mask,
    input_proj,
    gate_blocks,
    output_proj,
    ffn_gate_up,
    ffn_down,
    conv_taps,
    gate_bias,
    decay_param,
    norm_gains,
    master_shard,
    first_moment,
    second_moment,
):
    slot_count = tokens.shape[0]
    position = jnp.arange(slot_count, dtype=jnp.int32) - seq_start
    mask_rows = live_mask.astype(jnp.float32)[:, None]
    stream = tokens.astype(jnp.float32)
    grad_stream = cotangent.astype(jnp.float32) * mask_rows
    shards = (
        input_proj,
        gate_blocks,
        output_proj,
        ffn_gate_up,
        ffn_down,
        conv_taps,
        gate_bias,
        decay_param,
        norm_gains,
    )
    (
        full_in,
        full_blocks,
        full_out,
        full_up,
        full_down,
        full_taps,
        full_bias,
        full_decay,
        full_gains,
    ) = (
        lax.all_gather(shards[0], "shard", axis=2, tiled=True),
        lax.all_gather(shards[1], "shard", axis=1, tiled=True),
        lax.all_gather(shards[2], "shard", axis=0, tiled=True),
        lax.all_gather(shards[3], "shard", axis=2, tiled=True),
        lax.all_gather(shards[4], "shard", axis=0, tiled=True),
        lax.all_gather(shards[5], "shard", axis=1, tiled=True),
        lax.all_gather(shards[6], "shard", axis=1, tiled=True),
        lax.all_gather(shards[7], "shard", axis=0, tiled=True),
        lax.all_gather(shards[8], "shard", axis=1, tiled=True),
    )
    gains = full_gains.astype(jnp.float32)
    normed, norm_pull = jax.vjp(rms_scale, stream, gains[0])
    mix_in = normed.astype(jnp.bfloat16)
    mix_out, mix_saved = mixer_forward(
        mix_in,
        full_in,
        full_blocks,
        full_out,
        full_taps.astype(jnp.float32),
        full_bias.astype(jnp.float32),
        full_decay.astype(jnp.float32),
        position,
    )
    residual = stream + mix_out
    normed_two, second_pull = jax.vjp(rms_scale, residual, gains[1])
    ffn_in_low = normed_two.astype(jnp.bfloat16)
    ffn_result, ffn_saved = ffn_forward(ffn_in_low, full_up, full_down)
    block_out = (mask_rows * (residual + ffn_result)).astype(jnp.bfloat16)
    grad_ffn_in, grad_up, grad_down = ffn_backward(
        grad_stream.astype(jnp.bfloat16), ffn_in_low, ffn_saved, full_up, full_down
    )
    grad_norm_two, grad_gain_two = second_pull(grad_ffn_in)
    grad_residual = grad_stream + grad_norm_two
    grad_mix_in, mix_grads = mixer_backward(
        grad_residual.astype(jnp.bfloat16), mix_in, mix_saved, full_in, full_blocks, full_out
    )
    grad_norm_one, grad_gain_one = norm_pull(grad_mix_in)
    tokens_grad = (grad_residual + grad_norm_one).astype(jnp.bfloat16)
    grads = (
        mix_grads[0],
        mix_grads[1],
        mix_grads[2],
        grad_up,
        grad_down,
        mix_grads[3],
        mix_grads[4],
        mix_grads[5],
        jnp.stack([grad_gain_one, grad_gain_two]),
    )
    summed = (
        lax.psum_scatter(
            grads[0].astype(jnp.bfloat16), "shard", scatter_dimension=2, tiled=True
        ).astype(jnp.float32),
        lax.psum_scatter(
            grads[1].astype(jnp.bfloat16), "shard", scatter_dimension=1, tiled=True
        ).astype(jnp.float32),
        lax.psum_scatter(
            grads[2].astype(jnp.bfloat16), "shard", scatter_dimension=0, tiled=True
        ).astype(jnp.float32),
        lax.psum_scatter(
            grads[3].astype(jnp.bfloat16), "shard", scatter_dimension=2, tiled=True
        ).astype(jnp.float32),
        lax.psum_scatter(
            grads[4].astype(jnp.bfloat16), "shard", scatter_dimension=0, tiled=True
        ).astype(jnp.float32),
        lax.psum_scatter(
            grads[5].astype(jnp.bfloat16), "shard", scatter_dimension=1, tiled=True
        ).astype(jnp.float32),
        lax.psum_scatter(
            grads[6].astype(jnp.bfloat16), "shard", scatter_dimension=1, tiled=True
        ).astype(jnp.float32),
        lax.psum_scatter(
            grads[7].astype(jnp.bfloat16), "shard", scatter_dimension=0, tiled=True
        ).astype(jnp.float32),
        lax.psum_scatter(
            grads[8].astype(jnp.bfloat16), "shard", scatter_dimension=1, tiled=True
        ).astype(jnp.float32),
    )
    flat = jnp.concatenate([member.reshape(1, -1) for member in summed], axis=1)
    piece = lax.psum_scatter(flat, "dp", scatter_dimension=1, tiled=True)
    bias_total = lax.psum(summed[6], "dp")
    new_first = beta_one * first_moment + (1.0 - beta_one) * piece
    new_second = beta_two * second_moment + (1.0 - beta_two) * piece * piece
    new_master = master_shard - learn_rate * (
        new_first / corr_one / (jnp.sqrt(new_second / corr_two) + adam_eps)
        + weight_decay * master_shard
    )
    new_weights = lax.all_gather(new_master.astype(jnp.bfloat16), "shard", axis=0, tiled=True)
    return (
        block_out,
        tokens_grad,
        piece,
        new_master,
        new_first,
        new_second,
        new_weights,
        bias_total,
    )


def solution(mesh):
    fits = mesh.shape["dp"] == 8 and mesh.shape["shard"] == 4
    placed = (
        P(("dp", "shard"), None),
        P(("dp", "shard"), None),
        P(("dp", "shard")),
        P(("dp", "shard")),
        P(None, None, "shard"),
        P(None, "shard", None, None),
        P("shard", None),
        P(None, None, "shard"),
        P("shard", None),
        P(None, "shard"),
        P(None, "shard"),
        P("shard"),
        P(None, "shard"),
        P("shard", "dp"),
        P("shard", "dp"),
        P("shard", "dp"),
    )
    return jax.shard_map(
        group_body if fits else body,
        mesh=mesh,
        in_specs=placed,
        out_specs=(
            P(("dp", "shard"), None),
            P(("dp", "shard"), None),
            P("shard", "dp"),
            P("shard", "dp"),
            P("shard", "dp"),
            P("shard", "dp"),
            P(None, "dp"),
            P(None, "shard"),
        ),
        check_vma=False,
    )
```

```python
import functools
import jax
import jax.numpy as jnp
from jax import lax
from jax.experimental import pallas as pl
from jax.experimental.pallas import tpu as pltpu
from jax.sharding import PartitionSpec as P

norm_eps = 1e-06
gate_scale = 8.0
beta_one = 0.9
beta_two = 0.95
learn_rate = 0.01
weight_decay = 0.1
adam_eps = 1e-08
corr_one = 1.0 - beta_one**10.0
corr_two = 1.0 - beta_two**10.0
low_type = jnp.bfloat16
wide = jnp.float32
axes = ("dp", "shard")
gelu_scale = 0.7978845608028654
gelu_cube = 0.044715


def device_pairs(target):
    found = []
    for chip in range(4):
        for core in range(2):
            for z in range(4):
                to = target(chip, core, z)
                if to is not None:
                    source = (chip * 2 + core) * 4 + z
                    found.append((source, (to[0] * 2 + to[1]) * 4 + to[2]))
    return found


def line_pairs(moves):
    moves = dict(moves)

    def target(chip, core, z):
        end = z if core == 0 else 3 - z
        if end not in moves:
            return None
        to = moves[end]
        return (chip, core, to if core == 0 else 3 - to)

    return device_pairs(target)


def step_pairs(step):
    return device_pairs(
        lambda chip, core, z: (chip, core, z + step) if 0 <= z + step < 4 else None
    )


def plane_pairs(flip, owners_only=False):
    return device_pairs(
        lambda chip, core, z: None if owners_only and core != z // 2 else (chip ^ flip, core, z)
    )


core_pairs = device_pairs(lambda chip, core, z: (chip, 1 - core, z))
owner_core_pairs = device_pairs(
    lambda chip, core, z: (chip, 1 - core, z) if core == z // 2 else None
)


def move(value, pairs):
    return lax.ppermute(value, axes, pairs)


def plane_gather(value, dim=0, owners_only=False):
    half = value.shape[dim] // 2
    across_x = move(value, plane_pairs(1, owners_only))
    across_y = move(value, plane_pairs(2, owners_only))
    first = lax.slice_in_dim(across_x, 0, half, axis=dim)
    second = lax.slice_in_dim(across_y, half, 2 * half, axis=dim)
    first = move(first, plane_pairs(2, owners_only))
    second = move(second, plane_pairs(1, owners_only))
    return (value, across_x, across_y, jnp.concatenate([first, second], axis=dim))


def plane_reduce(parts):
    slots = parts.shape[0] // 4
    half = slots // 2
    mine, for_x, for_y, for_d = (
        parts[number * slots : (number + 1) * slots] for number in range(4)
    )
    top = slice(0, half)
    low = slice(half, slots)
    from_x = move(jnp.concatenate([for_x[top], for_d[top]]), plane_pairs(1))
    from_y = move(jnp.concatenate([for_y[low], for_d[low]]), plane_pairs(2))
    send_y = (for_y[top].astype(wide) + from_x[half:].astype(wide)).astype(low_type)
    send_x = (for_x[low].astype(wide) + from_y[half:].astype(wide)).astype(low_type)
    last_top = move(send_y, plane_pairs(2))
    last_low = move(send_x, plane_pairs(1))
    return jnp.concatenate(
        [
            mine[top].astype(wide) + from_x[:half].astype(wide) + last_top.astype(wide),
            mine[low].astype(wide) + from_y[:half].astype(wide) + last_low.astype(wide),
        ]
    )


def pick(end, choices):
    result = choices[3]
    for number in (2, 1, 0):
        result = jnp.where(end == number, choices[number], result)
    return result


def line_spread(own, end):
    ahead = move(own, line_pairs({0: 1, 1: 2}))
    back = move(own, line_pairs({1: 0}))
    ahead_two = move(ahead, line_pairs({1: 2, 2: 3}))
    ahead_three = move(ahead_two, line_pairs({2: 3}))
    return (
        pick(end, [own, ahead, ahead_two, ahead_three]),
        pick(end, [back, own, ahead, ahead_two]),
    )


def add_low(left, right):
    return (left.astype(wide) + right.astype(wide)).astype(low_type)


def line_sum(outer, inner, end):
    first = add_low(outer, move(outer, line_pairs({3: 2})))
    inner_one = add_low(inner, move(inner, line_pairs({3: 2, 0: 1})))
    second = add_low(outer, move(first, line_pairs({2: 1})))
    inner_two = add_low(inner_one, move(inner_one, line_pairs({2: 1})))
    third = add_low(outer, move(second, line_pairs({1: 0})))
    return jnp.where(end == 0, third, inner_two)


def turn_pairs(turn):
    return device_pairs(lambda chip, core, z: (chip, core, (z + turn) % 4))


def all_slices(own, z):
    found = [own] + [move(own, turn_pairs(turn)) for turn in (1, 2, 3)]
    return jnp.concatenate(
        [
            sum(jnp.where((z - at) % 4 == turn, found[turn], 0) for turn in range(4))
            for at in range(4)
        ],
        axis=-1,
    )


def shard_slices(value, z):
    size = value.shape[-1] // 4

    def part(turn):
        return lax.dynamic_slice_in_dim(value, ((z + turn) % 4) * size, size, axis=1)

    return part(0) + sum(move(part(turn), turn_pairs(turn)) for turn in (1, 2, 3))


def dot_rows(left, right):
    return lax.dot_general(left, right, (((1,), (1,)), ((), ())), preferred_element_type=wide)


def dot_plain(left, right):
    return lax.dot_general(left, right, (((1,), (0,)), ((), ())), preferred_element_type=wide)


def dot_slots(left, right):
    return lax.dot_general(left, right, (((0,), (0,)), ((), ())), preferred_element_type=wide)


def gelu_parts(value):
    square = value * value
    bent = jnp.tanh(gelu_scale * value * (1.0 + gelu_cube * square))
    half = 0.5 * (1.0 + bent)
    slope = half + 0.5 * value * (1.0 - bent * bent) * gelu_scale * (
        1.0 + 3.0 * gelu_cube * square
    )
    return (value * half, slope)


def shift_down(value, step):
    if step % 8 == 0:
        return jnp.concatenate([value[-step:], value[:-step]], axis=0)
    return pltpu.roll(value, step, 0)


def shift_up(value, step):
    if step % 8 == 0:
        return jnp.concatenate([value[step:], value[:step]], axis=0)
    return pltpu.roll(value, value.shape[0] - step, 0)


def scan_slots(decay, value, shift):
    step = 1
    while step < value.shape[0]:
        value = value + decay * shift(value, step)
        if 2 * step < value.shape[0]:
            decay = decay * shift(decay, step)
        step *= 2
    return value


def one_minus_exp(value):
    series = jnp.ones_like(value)
    for number in range(11, 1, -1):
        series = 1.0 - value * (1.0 / number) * series
    return jnp.where(value < 0.8, value * series, 1.0 - jnp.exp(-value))


def soft_plus(value):
    return jnp.maximum(value, 0.0) + jnp.log1p(jnp.exp(-jnp.abs(value)))


def mixer_parts(first, position, small, gates):
    conv_out = small[4:5] + small[0:1] * first
    shifted = []
    for step in range(1, 4):
        moved = jnp.where(position >= step, shift_down(first, step), 0.0)
        shifted.append(moved)
        conv_out = conv_out + small[step : step + 1] * moved
    conv_low = conv_out.astype(low_type)
    logits = dot_plain(conv_low, gates)
    width = first.shape[1]
    recur_gate = jax.nn.sigmoid(logits[:, :width] + small[5:6])
    input_gate = jax.nn.sigmoid(logits[:, width:] + small[6:7])
    rate = gate_scale * soft_plus(-small[7:8])
    log_decay = -rate * recur_gate
    decay = jnp.where(position > 0, jnp.exp(log_decay), 0.0)
    gone = one_minus_exp(-2.0 * log_decay)
    root = jnp.sqrt(gone)
    return conv_out, shifted, conv_low, recur_gate, input_gate, rate, decay, gone, root


def weight_views(w_ref, width):
    model = w_ref.shape[2] - width
    proj = w_ref[0, 0 : 2 * width, 0:model]
    out = w_ref[0, 2 * width : 3 * width, 0:model]
    gates = jnp.concatenate(
        [w_ref[0, 0:width, model:], w_ref[0, width : 2 * width, model:]], axis=1
    )
    small = w_ref[0, 2 * width : 2 * width + 16, model:].astype(wide)
    return proj, out, gates, small


def slot_position(starts):
    slot = lax.broadcasted_iota(jnp.int32, (starts.shape[0], 1), 0)
    return slot - starts[:, 0:1].astype(wide).astype(jnp.int32)


def mixer_step(x, position, views, width):
    proj, out, gates, small = views
    projected = dot_rows(x, proj)
    conv_out, _, _, _, input_gate, _, decay, _, root = mixer_parts(
        projected[:, :width], position, small, gates
    )
    states = scan_slots(decay, root * input_gate * conv_out, shift_down)
    mixed_low = (states * gelu_parts(projected[:, width:])[0]).astype(low_type)
    return projected, states, mixed_low, dot_plain(mixed_low, out)


def mixer_backward_kernel(
    width,
    x_ref,
    res_ref,
    pos_ref,
    w_ref,
    p_ref,
    state_ref,
    low_ref,
    grad_ref,
    gin_ref,
    acc_w,
    acc_in,
):
    head = pl.program_id(0)
    block = pl.program_id(1)
    slots, model = x_ref.shape
    proj, out, gates, small = weight_views(w_ref, width)
    position = slot_position(pos_ref[...])
    first = p_ref[0, :, 0:width]
    res_low = res_ref[...]
    states = state_ref[0]
    conv_out, shifted, conv_low, recur_gate, input_gate, rate, decay, gone, root = mixer_parts(
        first, position, small, gates
    )
    grad_mixed = dot_rows(res_low, out)
    active, slope = gelu_parts(p_ref[0, :, width:])
    grad_second = grad_mixed * states * slope
    adjoint = scan_slots(shift_up(decay, 1), grad_mixed * active, shift_up)
    grad_decay = adjoint * shift_down(states, 1)
    grad_root = adjoint * input_gate * conv_out
    grad_input_gate = adjoint * root * conv_out
    grad_conv = adjoint * root * input_gate
    grad_log = grad_decay * decay - grad_root * (1.0 - gone) / root
    grad_recur = -rate * grad_log
    grad_logit_a = grad_recur * recur_gate * (1.0 - recur_gate)
    grad_logit_b = grad_input_gate * input_gate * (1.0 - input_gate)
    grad_param = jnp.sum(grad_log * recur_gate, axis=0, keepdims=True) * (
        gate_scale * jax.nn.sigmoid(-small[7:8])
    )
    logits_low = jnp.concatenate([grad_logit_a, grad_logit_b], axis=1).astype(low_type)
    grad_conv = grad_conv + dot_rows(logits_low, gates)
    grad_gates = dot_slots(conv_low, logits_low)
    sums = [jnp.sum(grad_conv * first, axis=0, keepdims=True)]
    grad_first = small[0:1] * grad_conv
    for step in range(1, 4):
        sums.append(jnp.sum(grad_conv * shifted[step - 1], axis=0, keepdims=True))
        kept = jnp.where(position >= step, grad_conv, 0.0)
        grad_first = grad_first + small[step : step + 1] * shift_up(kept, step)
    sums.append(jnp.sum(grad_conv, axis=0, keepdims=True))
    sums.append(jnp.sum(grad_logit_a, axis=0, keepdims=True))
    sums.append(jnp.sum(grad_logit_b, axis=0, keepdims=True))
    sums.append(grad_param)
    grad_small = jnp.concatenate(sums, axis=0)
    proj_low = jnp.concatenate([grad_first, grad_second], axis=1).astype(low_type)
    part = dot_plain(proj_low, proj)
    rows = pl.ds(pl.multiple_of(block * slots, slots), slots)

    @pl.when(block == 0)
    def _():
        acc_w[...] = jnp.zeros_like(acc_w)

    acc_w[0 : 2 * width, 0:model] += dot_slots(proj_low, x_ref[...])
    acc_w[2 * width : 3 * width, 0:model] += dot_slots(low_ref[0], res_low)
    acc_w[0:width, model:] += grad_gates[:, :width]
    acc_w[width : 2 * width, model:] += grad_gates[:, width:]
    acc_w[2 * width : 2 * width + 8, model:] += grad_small

    @pl.when(head == 0)
    def _():
        acc_in[rows, :] = part

    @pl.when(head > 0)
    def _():
        acc_in[rows, :] += part

    @pl.when(block == pl.num_programs(1) - 1)
    def _():
        grad_ref[0] = acc_w[...].astype(low_type)

    @pl.when(head == pl.num_programs(0) - 1)
    def _():
        gin_ref[rows, :] = acc_in[rows, :].astype(low_type)


def mix_backward(mix_in, res_low, position, weights, saved, slots, width):
    rows, model = mix_in.shape
    heads = weights.shape[0]
    blocks = rows // slots
    return pl.pallas_call(
        functools.partial(mixer_backward_kernel, width),
        grid=(heads, blocks),
        in_specs=[
            pl.BlockSpec((slots, model), lambda h, b: (b, 0)),
            pl.BlockSpec((slots, model), lambda h, b: (b, 0)),
            pl.BlockSpec((slots, width), lambda h, b: (b, 0)),
            pl.BlockSpec((1,) + weights.shape[1:], lambda h, b: (h, 0, 0)),
            pl.BlockSpec((1, slots, 2 * width), lambda h, b: (h, b, 0)),
            pl.BlockSpec((1, slots, width), lambda h, b: (h, b, 0)),
            pl.BlockSpec((1, slots, width), lambda h, b: (h, b, 0)),
        ],
        out_specs=[
            pl.BlockSpec((1,) + weights.shape[1:], lambda h, b: (h, 0, 0)),
            pl.BlockSpec((rows, model), lambda h, b: (0, 0)),
        ],
        out_shape=[
            jax.ShapeDtypeStruct(weights.shape, low_type),
            jax.ShapeDtypeStruct((rows, model), low_type),
        ],
        scratch_shapes=[
            pltpu.VMEM(weights.shape[1:], wide),
            pltpu.VMEM((rows, model), wide),
        ],
        compiler_params=pltpu.CompilerParams(vmem_limit_bytes=48 * 1024 * 1024),
        cost_estimate=pl.CostEstimate(
            flops=2 * rows * model * heads * width * 6,
            bytes_accessed=heads * rows * width * 14 + weights.size * 4 + rows * model * 6,
            transcendentals=heads * rows * width * 6,
        ),
        name="mixer_backward",
    )(mix_in, res_low, position, weights, *saved)


def peer_x(chip):
    return chip + 1 - 2 * (chip % 2)


def peer_y(chip):
    return chip + 2 - 4 * (chip // 2)


def line_place(end, core):
    return end + core * (3 - 2 * end)


def remote(source, target, send, recv, member, z):
    return pltpu.make_async_remote_copy(
        src_ref=source,
        dst_ref=target,
        send_sem=send,
        recv_sem=recv,
        device_id=(member, z),
        device_id_type=pl.DeviceIdType.MESH,
    )


def enter(member, z):
    barrier = pltpu.get_barrier_semaphore()
    for other in range(8):

        @pl.when(member != other)
        def _():
            pl.semaphore_signal(
                barrier, inc=1, device_id=(other, z), device_id_type=pl.DeviceIdType.MESH
            )

    for other in range(4):

        @pl.when(z != other)
        def _():
            pl.semaphore_signal(
                barrier, inc=1, device_id=(member, other), device_id_type=pl.DeviceIdType.MESH
            )

    pl.semaphore_wait(barrier, 10)


class Gather:
    def __init__(self, own, target, send, recv, member, z):
        self.own, self.target = own, target
        self.send, self.recv = send, recv
        chip, core = member // 2, member % 2
        self.to_x = peer_x(chip) * 2 + core
        self.to_y = peer_y(chip) * 2 + core
        self.z = z
        self.half = own.shape[0] // 2

    def copy(self, number):
        low, high = pl.ds(0, self.half), pl.ds(self.half, self.half)
        source, target, to = (
            (self.own, self.target.at[1], self.to_x),
            (self.own, self.target.at[2], self.to_y),
            (self.target.at[1, low], self.target.at[3, low], self.to_y),
            (self.target.at[2, high], self.target.at[3, high], self.to_x),
        )[number]
        return remote(source, target, self.send.at[number], self.recv.at[number], to, self.z)

    def begin(self):
        self.copy(0).start()
        self.copy(1).start()

    def relay(self):
        self.copy(0).wait_recv()
        self.copy(2).start()
        self.copy(1).wait_recv()
        self.copy(3).start()

    def arrive(self):
        self.copy(2).wait_recv()
        self.copy(3).wait_recv()

    def finish(self):
        for number in range(4):
            self.copy(number).wait_send()


class Reduce:
    def __init__(self, part, from_x, from_y, passing, last, send, recv, member, z):
        self.part, self.from_x, self.from_y = part, from_x, from_y
        self.passing, self.last = passing, last
        self.send, self.recv = send, recv
        chip, core = member // 2, member % 2
        self.to_x = peer_x(chip) * 2 + core
        self.to_y = peer_y(chip) * 2 + core
        self.z = z
        self.slots = part.shape[0] // 4
        self.half = self.slots // 2

    def copy(self, number):
        slots, half = self.slots, self.half
        source, target, to = (
            (self.part.at[pl.ds(slots, half)], self.from_x.at[0], self.to_x),
            (self.part.at[pl.ds(3 * slots, half)], self.from_x.at[1], self.to_x),
            (self.part.at[pl.ds(2 * slots + half, half)], self.from_y.at[0], self.to_y),
            (self.part.at[pl.ds(3 * slots + half, half)], self.from_y.at[1], self.to_y),
            (self.passing.at[0], self.last.at[0], self.to_y),
            (self.passing.at[1], self.last.at[1], self.to_x),
        )[number]
        return remote(source, target, self.send.at[number], self.recv.at[number], to, self.z)

    def begin(self):
        for number in (1, 3, 0, 2):
            self.copy(number).start()

    def relay(self):
        slots, half = self.slots, self.half
        self.copy(1).wait_recv()
        self.passing[0] = (
            self.part[2 * slots : 2 * slots + half].astype(wide) + self.from_x[1].astype(wide)
        ).astype(low_type)
        self.copy(4).start()
        self.copy(3).wait_recv()
        self.passing[1] = (
            self.part[slots + half : 2 * slots].astype(wide) + self.from_y[1].astype(wide)
        ).astype(low_type)
        self.copy(5).start()

    def arrive(self):
        for number in (0, 2, 4, 5):
            self.copy(number).wait_recv()

    def result(self, number):
        direct = self.from_x if number == 0 else self.from_y
        return (
            self.part[number * self.half : (number + 1) * self.half].astype(wide)
            + direct[0].astype(wide)
            + self.last[number].astype(wide)
        )

    def finish(self):
        for number in range(6):
            self.copy(number).wait_send()

    @staticmethod
    def scratch(slots, model):
        return [pltpu.VMEM((2, slots // 2, model), low_type)] * 4


def norm_rows(value, gain):
    scale = lax.rsqrt(jnp.mean(value * value, axis=1, keepdims=True) + norm_eps)
    return value * scale * gain


def front_kernel(
    sizes,
    tokens_ref,
    cot_ref,
    gain_ref,
    small_ref,
    in_ref,
    gate_ref,
    out_ref,
    up_ref,
    down_ref,
    mix_in,
    weights,
    ffn_weights,
    saved_p,
    saved_state,
    saved_low,
    starts_out,
    residual_out,
    ffn_in,
    cot_out,
    gains_out,
    tokens_all,
    raw_in,
    raw_up,
    turned,
    gain_seen,
    acc,
    part,
    from_x,
    from_y,
    passing,
    last,
    load_sem,
    gain_send,
    gain_recv,
    m_send,
    m_recv,
    m_core_send,
    m_core_recv,
    f_send,
    f_recv,
    f_core_send,
    f_core_recv,
    g_send,
    g_recv,
    r_send,
    r_recv,
):
    model, width, ffn_width = sizes
    member = lax.axis_index("dp")
    z = lax.axis_index("shard")
    chip, core = member // 2, member % 2
    end = z + core * (3 - 2 * z)
    other = chip * 2 + 1 - core
    slots = cot_ref.shape[0]
    half_ffn = ffn_width // 2
    owner = core == z // 2

    window = 128 * ((chip * ffn_width) // 128)
    skew = chip * ffn_width - window
    quarter = pl.ds(pl.multiple_of(chip * width, width), width)
    wide_window = pl.ds(pl.multiple_of(window, 128), raw_up.shape[2])

    def loads():
        found = []
        for kind in range(2):
            found.append((in_ref.at[kind, :, quarter], raw_in.at[kind]))
            found.append(
                (
                    gate_ref.at[kind, chip],
                    weights.at[end, pl.ds(kind * width, width), pl.ds(model, width)],
                )
            )
        found.append((out_ref.at[quarter], weights.at[end, pl.ds(2 * width, width), pl.ds(0, model)]))
        found.append(
            (
                small_ref.at[:, quarter],
                weights.at[end, pl.ds(2 * width, 16), pl.ds(model, width)],
            )
        )
        for kind in range(2):
            found.append((up_ref.at[kind, :, wide_window], raw_up.at[kind]))
        found.append(
            (
                down_ref.at[pl.ds(pl.multiple_of(chip * ffn_width, 32), ffn_width)],
                ffn_weights.at[2, pl.ds(pl.multiple_of(end * ffn_width, 32), ffn_width)],
            )
        )
        return [
            pltpu.make_async_copy(source, target, load_sem.at[number])
            for number, (source, target) in enumerate(found)
        ]

    def turned_copy(kind):
        return pltpu.make_async_copy(
            turned.at[kind, pl.ds(pl.multiple_of(skew, 32), ffn_width)],
            ffn_weights.at[kind, pl.ds(pl.multiple_of(end * ffn_width, 32), ffn_width)],
            load_sem.at[9 + kind],
        )

    @pl.when(owner)
    def _():
        for copy in loads():
            copy.start()

    enter(member, z)

    gather_tokens = Gather(tokens_ref, tokens_all, g_send.at[0], g_recv.at[0], member, z)
    gather_cot = Gather(cot_ref, cot_out, g_send.at[1], g_recv.at[1], member, z)
    gather_ffn = Gather(ffn_in.at[0], ffn_in, g_send.at[2], g_recv.at[2], member, z)
    reduce = Reduce(part, from_x, from_y, passing, last, r_send, r_recv, member, z)
    own_cot = pltpu.make_async_copy(cot_ref, cot_out.at[0], load_sem.at[11])

    gather_tokens.begin()
    own_cot.start()

    def gain_copy(to, slot):
        return remote(
            gain_ref, gain_seen.at[slot], gain_send.at[to], gain_recv.at[slot], member, to
        )

    for to in range(4):

        @pl.when(to != z)
        def _():
            gain_copy(to, z).start()

    gain_seen[z] = gain_ref[...]

    def m_rows(number):
        return pl.ds(number * width, width)

    def m_copy(slot, number, way, to_end):
        place = weights.at[slot, m_rows(number)]
        return remote(
            place,
            place,
            m_send.at[way, slot, number],
            m_recv.at[slot, number],
            member,
            line_place(to_end, core),
        )

    def m_core(slot, number):
        return remote(
            weights.at[slot, m_rows(number)],
            weights.at[2 + slot, m_rows(number)],
            m_core_send.at[slot, number],
            m_core_recv.at[slot, number],
            other,
            z,
        )

    def f_place(slot, number):
        row = slot * ffn_width + (number % 2) * half_ffn
        return ffn_weights.at[number // 2, pl.ds(row, half_ffn)]

    def f_copy(slot, number, way, to_end):
        place = f_place(slot, number)
        return remote(
            place,
            place,
            f_send.at[way, slot, number],
            f_recv.at[slot, number],
            member,
            line_place(to_end, core),
        )

    def f_core(slot, number):
        return remote(
            f_place(slot, number),
            f_place(2 + slot, number),
            f_core_send.at[slot, number],
            f_core_recv.at[slot, number],
            other,
            z,
        )

    def pass_on(copy, core_copy, slot, number):
        if slot == 0:

            @pl.when(end < 3)
            def _():
                copy(slot, number, 0, end + 1).start()
        else:

            @pl.when((end == 1) | (end == 2))
            def _():
                copy(slot, number, 0, end + 1).start()

            @pl.when(end == 1)
            def _():
                copy(slot, number, 1, 0).start()

        core_copy(slot, number).start()

    @pl.when(owner)
    def _():
        for copy in loads()[:6]:
            copy.wait()
        for kind in range(2):
            for at in range(model // 128):
                weights[end, kind * width : (kind + 1) * width, at * 128 : (at + 1) * 128] = (
                    raw_in[kind, at * 128 : (at + 1) * 128, :].astype(wide).T.astype(low_type)
                )
        for row in range(2 * width + 16, 3 * width, 16):
            weights[end, row : row + 16, model:] = jnp.zeros((16, width), low_type)

    for slot in range(2):

        @pl.when(end == slot)
        def _():
            for number in range(3):
                pass_on(m_copy, m_core, slot, number)

    @pl.when(owner)
    def _():
        for copy in loads()[6:]:
            copy.wait()
        for kind in range(2):

            def turn(at, carry):
                columns = pl.ds(pl.multiple_of(at * 128, 128), 128)
                for tile in range(raw_up.shape[2] // 128):
                    turned[kind, tile * 128 : (tile + 1) * 128, columns] = (
                        raw_up[kind, columns, tile * 128 : (tile + 1) * 128]
                        .astype(wide)
                        .T.astype(low_type)
                    )
                return carry

            lax.fori_loop(0, model // 128, turn, 0)
            turned_copy(kind).start()

    gather_tokens.relay()

    for number in range(3):
        for slot in range(2):

            @pl.when(end != slot)
            def _():
                m_copy(slot, number, 0, 0).wait_recv()
                pass_on(m_copy, m_core, slot, number)

    @pl.when(owner)
    def _():
        turned_copy(0).wait()
        turned_copy(1).wait()

    for slot in range(2):

        @pl.when(end == slot)
        def _():
            for number in range(6):
                pass_on(f_copy, f_core, slot, number)

    def f_step(step):
        slot, number = 1 - step % 2, step // 2

        @pl.when((end != slot) & (end < 3))
        def _():
            f_copy(slot, number, 0, 0).wait_recv()
            pass_on(f_copy, f_core, slot, number)

    for to in range(4):

        @pl.when(to != z)
        def _():
            gain_copy(to, to).wait_recv()

    gains = jnp.concatenate([gain_seen[at].astype(wide) for at in range(4)], axis=1)
    gains_out[...] = gains[0:8]
    gather_tokens.arrive()

    def norm_block(block):
        if block == 0:
            source, starts = tokens_ref[:, :model], tokens_ref[:, model:]
        else:
            source, starts = tokens_all[block, :, :model], tokens_all[block, :, model:]
        at = slice(block * slots, (block + 1) * slots)
        mix_in[at, :] = norm_rows(source.astype(wide), gains_out[0:1]).astype(low_type)
        starts_out[at, :] = starts

    for block in range(4):
        norm_block(block)
    gather_cot.begin()
    for step in range(3):
        f_step(step)

    for head in range(4):
        if head >= 2:
            for number in range(3):
                m_core(head - 2, number).wait_recv()
        views = weight_views(weights.at[pl.ds(head, 1)], width)

        def step_block(block, carry):
            rows = pl.ds(pl.multiple_of(block * slots, slots), slots)
            position = slot_position(starts_out[rows, :])
            projected, states, mixed_low, product = mixer_step(
                mix_in[rows, :], position, views, width
            )
            saved_p[head, rows, :] = projected
            saved_state[head, rows, :] = states
            saved_low[head, rows, :] = mixed_low
            if head == 0:
                acc[rows, :] = product
            elif head < 3:
                acc[rows, :] += product
            else:
                part[rows, :] = (acc[rows, :] + product).astype(low_type)
            return carry

        lax.fori_loop(0, 4, step_block, 0)
        f_step(2 * head + 3)
        if head < 3:
            f_step(2 * head + 4)
        if head == 0:
            gather_cot.relay()
        if head == 3:
            reduce.begin()

    f_step(10)
    f_step(11)
    reduce.relay()
    reduce.arrive()
    half = slots // 2
    for number in range(2):
        at = slice(number * half, (number + 1) * half)
        residual = tokens_ref[at, :model].astype(wide) + reduce.result(number)
        residual_out[at, :] = residual
        ffn_in[0, at, :] = norm_rows(residual, gains_out[1:2]).astype(low_type)
    gather_ffn.begin()
    gather_ffn.relay()

    @pl.when(end == 3)
    def _():
        for number in range(6):
            for slot in (1, 0):
                f_copy(slot, number, 0, 0).wait_recv()
                f_core(slot, number).start()

    gather_ffn.arrive()
    gather_cot.arrive()
    own_cot.wait()
    for slot in range(2):
        for number in range(6):
            f_core(slot, number).wait_recv()

    for gather in (gather_tokens, gather_cot, gather_ffn, reduce):
        gather.finish()
    for to in range(4):

        @pl.when(to != z)
        def _():
            gain_copy(to, z).wait_send()

    for copy, core_copy, count in ((m_copy, m_core, 3), (f_copy, f_core, 6)):
        for number in range(count):
            for slot in range(2):
                core_copy(slot, number).wait_send()

            @pl.when(end < 3)
            def _():
                copy(0, number, 0, 0).wait_send()

            @pl.when((end == 1) | (end == 2))
            def _():
                copy(1, number, 0, 0).wait_send()

            @pl.when(end == 1)
            def _():
                copy(1, number, 1, 0).wait_send()


def front(tokens, cot, gains, small, in_proj, gates, out_proj, gate_up, down, sizes):
    model, width, ffn_width = sizes
    slots = cot.shape[0]
    rows = 4 * slots
    dma = pltpu.SemaphoreType.DMA
    vmem = pl.BlockSpec(memory_space=pltpu.VMEM)
    anywhere = pl.BlockSpec(memory_space=pl.ANY)
    window = -(-ffn_width // 128) * 128
    return pl.pallas_call(
        functools.partial(front_kernel, sizes),
        in_specs=[vmem] * 3 + [anywhere] * 6,
        out_specs=[vmem, vmem, anywhere, vmem, vmem, vmem, vmem, vmem, vmem, anywhere, vmem],
        out_shape=[
            jax.ShapeDtypeStruct((rows, model), low_type),
            jax.ShapeDtypeStruct((4, 3 * width, model + width), low_type),
            jax.ShapeDtypeStruct((3, 4 * ffn_width, model), low_type),
            jax.ShapeDtypeStruct((4, rows, 2 * width), wide),
            jax.ShapeDtypeStruct((4, rows, width), wide),
            jax.ShapeDtypeStruct((4, rows, width), low_type),
            jax.ShapeDtypeStruct((rows, width), low_type),
            jax.ShapeDtypeStruct((slots, model), wide),
            jax.ShapeDtypeStruct((4, slots, model), low_type),
            jax.ShapeDtypeStruct((4, slots, model), low_type),
            jax.ShapeDtypeStruct((8, model), wide),
        ],
        scratch_shapes=[
            pltpu.VMEM((4, slots, model + width), low_type),
            pltpu.VMEM((2, model, width), low_type),
            pltpu.VMEM((2, model, window), low_type),
            pltpu.VMEM((2, window, model), low_type),
            pltpu.VMEM((4, 16, model // 4), low_type),
            pltpu.VMEM((rows, model), wide),
            pltpu.VMEM((rows, model), low_type),
        ]
        + Reduce.scratch(slots, model)
        + [
            dma((12,)),
            dma((4,)),
            dma((4,)),
            dma((2, 2, 3)),
            dma((2, 3)),
            dma((2, 3)),
            dma((2, 3)),
            dma((2, 2, 6)),
            dma((2, 6)),
            dma((2, 6)),
            dma((2, 6)),
            dma((3, 4)),
            dma((3, 4)),
            dma((6,)),
            dma((6,)),
        ],
        compiler_params=pltpu.CompilerParams(
            collective_id=3, has_side_effects=True, vmem_limit_bytes=60 * 1024 * 1024
        ),
        cost_estimate=pl.CostEstimate(
            flops=2 * rows * model * 4 * width * 3,
            bytes_accessed=6 * ffn_width * 4 * model,
            transcendentals=rows * 4 * width * 6,
        ),
        name="front",
    )(tokens, cot, gains, small, in_proj, gates, out_proj, gate_up, down)


def middle_kernel(
    sizes,
    x_ref,
    go_ref,
    weights_ref,
    residual_ref,
    gain_ref,
    mask_ref,
    total,
    res_low,
    res_out,
    gain_out,
    block_out,
    held,
    lows,
    paired,
    arrived,
    part_in,
    part_out,
    in_x,
    in_y,
    in_pass,
    in_last,
    load_sem,
    core_send,
    core_recv,
    line_send,
    line_recv,
    i_send,
    i_recv,
    o_send,
    o_recv,
    g_send,
    g_recv,
):
    model, ffn_width = sizes
    member = lax.axis_index("dp")
    z = lax.axis_index("shard")
    chip, core = member // 2, member % 2
    end = z + core * (3 - 2 * z)
    other = chip * 2 + 1 - core
    slots = residual_ref.shape[0]
    half = slots // 2
    hidden = 4 * ffn_width
    half_ffn = ffn_width // 2

    loads = [
        pltpu.make_async_copy(weights_ref.at[kind], held.at[kind], load_sem.at[kind])
        for kind in range(3)
    ]
    for load in loads:
        load.start()
    enter(member, z)
    for load in loads:
        load.wait()

    cuts = []
    low = 0
    while low < hidden:
        cuts.append((low, min(low + 512, hidden)))
        low += 512

    def block_step(block, carry):
        rows = pl.ds(pl.multiple_of(block * slots, slots), slots)
        x = x_ref[rows, :]
        grad_out = go_ref[rows, :]
        sum_out = jnp.zeros((slots, model), wide)
        sum_in = jnp.zeros((slots, model), wide)
        for low, high in cuts:
            pre_gate = dot_rows(x, held[0, low:high])
            pre_up = dot_rows(x, held[1, low:high])
            active, slope = gelu_parts(pre_gate)
            ffn_low = (active * pre_up).astype(low_type)
            grad_act = dot_rows(grad_out, held[2, low:high])
            gate_low = (grad_act * pre_up * slope).astype(low_type)
            up_low = (grad_act * active).astype(low_type)
            sum_out = sum_out + dot_plain(ffn_low, held[2, low:high])
            sum_in = (
                sum_in + dot_plain(gate_low, held[0, low:high]) + dot_plain(up_low, held[1, low:high])
            )
            lows[0, rows, low:high] = gate_low
            lows[1, rows, low:high] = up_low
            lows[2, rows, low:high] = ffn_low
        part_in[rows, :] = sum_in.astype(low_type)
        part_out[rows, :] = sum_out.astype(low_type)
        return carry

    lax.fori_loop(0, 4, block_step, 0)

    reduce_in = Reduce(part_in, in_x, in_y, in_pass, in_last, i_send, i_recv, member, z)
    reduce_out = Reduce(
        part_out,
        in_x.at[pl.ds(2, 2)],
        in_y.at[pl.ds(2, 2)],
        in_pass.at[pl.ds(2, 2)],
        in_last.at[pl.ds(2, 2)],
        o_send,
        o_recv,
        member,
        z,
    )
    gather = Gather(res_low.at[0], res_low, g_send, g_recv, member, z)
    reduce_in.begin()

    split = (2 * ffn_width // 128) * 128
    middle = model // 2

    def weight_grads(kind, low, high):
        factor = go_ref if kind == 2 else x_ref
        for at in range(2):
            columns = slice(at * middle, (at + 1) * middle)
            held[kind, low:high, columns] = dot_slots(
                lows[kind, :, low:high], factor[:, columns]
            ).astype(low_type)

    def core_copy(slot, kind):
        return remote(
            held.at[kind, pl.ds((2 + slot) * ffn_width, ffn_width)],
            paired.at[slot, kind],
            core_send.at[slot, kind],
            core_recv.at[slot, kind],
            other,
            z,
        )

    for kind in range(3):
        weight_grads(kind, split, hidden)
        core_copy(0, kind).start()
        core_copy(1, kind).start()

    def chunk(number):
        return number // 2, pl.ds((number % 2) * half_ffn, half_ffn)

    def line_copy(kind, number, to_end):
        at, rows = chunk(number)
        return remote(
            paired.at[min(kind, 1), at, rows],
            arrived.at[kind, at, rows],
            line_send.at[kind, number],
            line_recv.at[kind, number],
            member,
            line_place(to_end, core),
        )

    def pair_up(slot, number):
        at, rows = chunk(number)
        own = held[at, pl.ds(slot * ffn_width + (number % 2) * half_ffn, half_ffn)]
        paired[slot, at, rows] = add_low(own, paired[slot, at, rows])

    for kind in range(3):
        weight_grads(kind, 0, split)
        for slot in range(2):
            core_copy(slot, kind).wait_recv()
            for number in (2 * kind, 2 * kind + 1):
                pair_up(slot, number)

                @pl.when(end == 3)
                def _():
                    line_copy(slot, number, 2).start()

                if slot == 1:

                    @pl.when(end == 0)
                    def _():
                        line_copy(2, number, 1).start()

        if kind == 0:
            reduce_in.relay()

    def summed(slot, kinds, number):
        at, rows = chunk(number)
        result = paired[slot, at, rows].astype(wide)
        for kind in kinds:
            result = result + arrived[kind, at, rows].astype(wide)
        return result.astype(low_type)

    def line_step(number):
        at, rows = chunk(number)

        @pl.when((end == 2) | (end == 1))
        def _():
            line_copy(0, number, 0).wait_recv()
            paired[0, at, rows] = summed(0, (0,), number)

        @pl.when(end == 2)
        def _():
            line_copy(0, number, 1).start()
            line_copy(1, number, 0).wait_recv()
            paired[1, at, rows] = summed(1, (1,), number)
            line_copy(1, number, 1).start()

        @pl.when(end == 1)
        def _():
            line_copy(0, number, 0).start()

    def out_copy(slot, number):
        at, rows = chunk(number)
        return pltpu.make_async_copy(
            paired.at[slot, at, rows], total.at[at, rows], load_sem.at[number]
        )

    def last_step(number):
        at, rows = chunk(number)

        @pl.when(end == 1)
        def _():
            line_copy(1, number, 0).wait_recv()
            line_copy(2, number, 0).wait_recv()
            paired[1, at, rows] = summed(1, (1, 2), number)
            out_copy(1, number).start()

        @pl.when(end == 0)
        def _():
            line_copy(0, number, 0).wait_recv()
            paired[0, at, rows] = summed(0, (0,), number)
            out_copy(0, number).start()

    line_step(0)

    reduce_in.arrive()
    gain = gain_ref[1:2]
    gain_sum = jnp.zeros((1, model), wide)
    for number in range(2):
        at = slice(number * half, (number + 1) * half)
        grad = reduce_in.result(number)
        value = residual_ref[at]
        scale = lax.rsqrt(jnp.mean(value * value, axis=1, keepdims=True) + norm_eps)
        scaled = grad * gain
        gain_sum = gain_sum + jnp.sum(grad * value * scale, axis=0, keepdims=True)
        inner = jnp.mean(scaled * value, axis=1, keepdims=True)
        back = scale * scaled - value * (scale * scale * scale * inner)
        result = go_ref[at].astype(wide) + back
        res_out[at] = result
        res_low[0, at] = result.astype(low_type)
    gain_out[...] = jnp.concatenate([gain_ref[0:1], gain_sum, jnp.zeros((6, model), wide)], axis=0)
    gather.begin()
    line_step(1)
    line_step(2)
    gather.relay()
    line_step(3)
    gather.arrive()
    reduce_out.begin()
    line_step(4)
    line_step(5)
    reduce_out.relay()
    for number in range(6):
        last_step(number)
    reduce_out.arrive()
    live = mask_ref[:, 0:1].astype(wide)
    for number in range(2):
        at = slice(number * half, (number + 1) * half)
        block_out[at] = (live[at] * (residual_ref[at] + reduce_out.result(number))).astype(low_type)

    for sent in (reduce_in, reduce_out, gather):
        sent.finish()
    for slot in range(2):
        for kind in range(3):
            core_copy(slot, kind).wait_send()
    for number in range(6):

        @pl.when(end > 0)
        def _():
            line_copy(0, number, 0).wait_send()

        @pl.when(end > 1)
        def _():
            line_copy(1, number, 0).wait_send()

        @pl.when(end == 0)
        def _():
            line_copy(2, number, 1).wait_send()

        @pl.when(end < 2)
        def _():
            out_copy(0, number).wait()


def middle(x, grad_out, weights, residual, gains, mask):
    rows, model = x.shape
    hidden = weights.shape[1]
    ffn_width = hidden // 4
    slots = rows // 4
    dma = pltpu.SemaphoreType.DMA
    vmem = pl.BlockSpec(memory_space=pltpu.VMEM)
    anywhere = pl.BlockSpec(memory_space=pl.ANY)
    quarter = (3, ffn_width, model)
    return pl.pallas_call(
        functools.partial(middle_kernel, (model, ffn_width)),
        in_specs=[vmem, vmem, anywhere, vmem, vmem, vmem],
        out_specs=[anywhere] + [vmem] * 4,
        out_shape=[
            jax.ShapeDtypeStruct(quarter, low_type),
            jax.ShapeDtypeStruct((4, slots, model), low_type),
            jax.ShapeDtypeStruct((slots, model), wide),
            jax.ShapeDtypeStruct((8, model), wide),
            jax.ShapeDtypeStruct((slots, model), low_type),
        ],
        scratch_shapes=[
            pltpu.VMEM(weights.shape, low_type),
            pltpu.VMEM((3, rows, hidden), low_type),
            pltpu.VMEM((2,) + quarter, low_type),
            pltpu.VMEM((3,) + quarter, low_type),
            pltpu.VMEM((rows, model), low_type),
            pltpu.VMEM((rows, model), low_type),
        ]
        + [pltpu.VMEM((4, slots // 2, model), low_type)] * 4
        + [
            dma((6,)),
            dma((2, 3)),
            dma((2, 3)),
            dma((3, 6)),
            dma((3, 6)),
            dma((6,)),
            dma((6,)),
            dma((6,)),
            dma((6,)),
            dma((4,)),
            dma((4,)),
        ],
        compiler_params=pltpu.CompilerParams(
            collective_id=4, has_side_effects=True, vmem_limit_bytes=63 * 1024 * 1024
        ),
        cost_estimate=pl.CostEstimate(
            flops=2 * rows * model * hidden * 9,
            bytes_accessed=weights.size * 4 + rows * model * 16,
            transcendentals=rows * hidden,
        ),
        name="middle",
    )(x, grad_out, weights, residual, gains, mask)


class Scatter:
    def __init__(self, sizes, member, z, send_sem, recv_sem):
        self.model, self.width, self.ffn_width, self.piece_length = sizes
        self.member, self.z = member, z
        self.chip, self.core = member // 2, member % 2
        self.owner = self.core == z // 2
        self.send_sem, self.recv_sem = send_sem, recv_sem
        self.across = self.model // 128
        rec, ffn, model = 4 * self.width, 4 * self.ffn_width, self.model
        self.gate_base = 2 * model * rec
        self.out_base = self.gate_base + 8 * self.width * self.width
        self.up_base = self.out_base + rec * model
        self.down_base = self.up_base + 2 * model * ffn
        self.rec, self.ffn = rec, ffn
        self.first_in = 0
        self.first_gate = 2 * self.across
        self.first_out = self.first_gate + 2
        self.first_small = self.first_out + 4
        self.first_up = self.first_small + 1
        self.first_down = self.first_up + 2 * self.across
        self.count = self.first_down + 6

    def in_unit(self, number, q):
        kind, at = number // self.across, number % self.across
        low = (kind * self.model + at * 128) * self.rec
        where = (
            pl.ds(pl.multiple_of(kind * self.width, self.width), self.width),
            pl.ds(pl.multiple_of(at * 128, 128), 128),
        )
        return self.first_in + number, where, low, low + 128 * self.rec

    def gate_unit(self, kind, q):
        low = self.gate_base + (kind * 4 + q) * self.width * self.width
        where = (
            pl.ds(pl.multiple_of(kind * self.width, self.width), self.width),
            pl.ds(self.model, self.width),
        )
        return self.first_gate + kind, where, low, low + self.width * self.width

    def out_unit(self, number, q):
        rows = self.width // 4
        low = self.out_base + (q * self.width + number * rows) * self.model
        where = (
            pl.ds(pl.multiple_of(2 * self.width + number * rows, rows), rows),
            pl.ds(0, self.model),
        )
        return self.first_out + number, where, low, low + rows * self.model

    def up_unit(self, number, q):
        kind, at = number // self.across, number % self.across
        low = self.up_base + (kind * self.model + at * 128) * self.ffn
        where = (kind, pl.ds(0, self.ffn_width), pl.ds(pl.multiple_of(at * 128, 128), 128))
        return self.first_up + number, where, low, low + 128 * self.ffn

    def down_unit(self, number, q):
        rows = self.ffn_width // 6
        low = self.down_base + (q * self.ffn_width + number * rows) * self.model
        where = (2, pl.ds(pl.multiple_of(number * rows, 16), rows), pl.ds(0, self.model))
        return self.first_down + number, where, low, low + rows * self.model

    def small_where(self):
        return (pl.ds(2 * self.width, 16), pl.ds(self.model, self.width))

    def copies(self, unit, source, target, q, act):
        number, where, low, high = unit
        first = low // self.piece_length
        last = (high - 1) // self.piece_length
        for which, to in ((0, first), (1, last)):
            wanted = True if which == 0 else last != first

            @pl.when((to != self.member) & wanted)
            def _():
                act(
                    remote(
                        source.at[where],
                        target.at[(q,) + where],
                        self.send_sem.at[which, number],
                        self.recv_sem.at[q, number],
                        to,
                        self.z,
                    ),
                    True,
                )

            @pl.when((to == self.member) & wanted)
            def _():
                act(
                    pltpu.make_async_copy(
                        source.at[where], target.at[(q,) + where], self.recv_sem.at[q, number]
                    ),
                    False,
                )

    def each(self, unit_of, low, high, source, target, act):
        def body(number, carry):
            self.copies(unit_of(number, self.chip), source, target, self.chip, act)
            return carry

        lax.fori_loop(low, high, body, 0)

    def smalls(self, source, target, act):
        where = self.small_where()
        for to in range(8):

            @pl.when(self.member != to)
            def _():
                act(
                    remote(
                        source.at[where],
                        target.at[(self.chip,) + where],
                        self.send_sem.at[2, to],
                        self.recv_sem.at[self.chip, self.first_small],
                        to,
                        self.z,
                    ),
                    True,
                )

        act(
            pltpu.make_async_copy(
                source.at[where],
                target.at[(self.chip,) + where],
                self.recv_sem.at[self.chip, self.first_small],
            ),
            False,
        )

    def arrivals(self, unit_of, count, source, target):
        low = self.member * self.piece_length

        def body(number, carry):
            for q in range(4):
                index, where, first, last = unit_of(number, q)
                mine = (first < low + self.piece_length) & (last > low)
                here = (self.chip == q) & self.owner

                @pl.when(mine & here)
                def _():
                    pltpu.make_async_copy(
                        source.at[where], target.at[(q,) + where], self.recv_sem.at[q, index]
                    ).wait()

                @pl.when(mine & jnp.logical_not(here))
                def _():
                    remote(
                        source.at[where],
                        target.at[(q,) + where],
                        self.send_sem.at[0, index],
                        self.recv_sem.at[q, index],
                        self.member,
                        self.z,
                    ).wait_recv()

            return carry

        lax.fori_loop(0, count, body, 0)

    def small_arrivals(self, source, target):
        where = self.small_where()
        for q in range(4):
            here = (self.chip == q) & self.owner

            @pl.when(here)
            def _():
                pltpu.make_async_copy(
                    source.at[where],
                    target.at[(q,) + where],
                    self.recv_sem.at[q, self.first_small],
                ).wait()

            @pl.when(jnp.logical_not(here))
            def _():
                remote(
                    source.at[where],
                    target.at[(q,) + where],
                    self.send_sem.at[2, 0],
                    self.recv_sem.at[q, self.first_small],
                    self.member,
                    self.z,
                ).wait_recv()


def begin(copy, is_remote):
    copy.start()


def finish_send(copy, is_remote):
    if is_remote:
        copy.wait_send()


def sums_kernel(
    sizes,
    mix_ref,
    part_ref,
    ffn_ref,
    tokens_ref,
    res_ref,
    gain_ref,
    mix_out,
    ffn_out,
    tokens_out,
    gain_out,
    paired,
    arrived,
    total,
    from_x,
    from_y,
    passing,
    last,
    gain_part,
    gain_plane,
    gain_line,
    gain_seen,
    core_send,
    core_recv,
    line_send,
    line_recv,
    plane_send,
    plane_recv,
    gain_send,
    gain_recv,
    unit_send,
    unit_recv,
):
    model, width, ffn_width, piece_length = sizes
    member = lax.axis_index("dp")
    z = lax.axis_index("shard")
    chip, core = member // 2, member % 2
    end = z + core * (3 - 2 * z)
    slots = tokens_ref.shape[0]
    half = slots // 2
    to_x = peer_x(chip) * 2 + core
    to_y = peer_y(chip) * 2 + core
    other = chip * 2 + 1 - core
    scatter = Scatter(sizes, member, z, unit_send, unit_recv)
    enter(member, z)

    def rows(number):
        return pl.ds(number * width, width)

    def core_copy(slot, number):
        return remote(
            mix_ref.at[2 + slot, rows(number)],
            paired.at[slot, rows(number)],
            core_send.at[slot, number],
            core_recv.at[slot, number],
            other,
            z,
        )

    for slot in range(2):
        for number in range(3):
            core_copy(slot, number).start()

    def plane_copy(number):
        source, target, to = (
            (part_ref.at[pl.ds(slots, half)], from_x.at[0], to_x),
            (part_ref.at[pl.ds(3 * slots, half)], from_x.at[1], to_x),
            (part_ref.at[pl.ds(2 * slots + half, half)], from_y.at[0], to_y),
            (part_ref.at[pl.ds(3 * slots + half, half)], from_y.at[1], to_y),
            (passing.at[0], last.at[0], to_y),
            (passing.at[1], last.at[1], to_x),
        )[number]
        return remote(source, target, plane_send.at[number], plane_recv.at[number], to, z)

    for number in (1, 3, 0, 2):
        plane_copy(number).start()

    @pl.when(scatter.owner)
    def _():
        scatter.each(scatter.up_unit, 0, 2 * scatter.across, ffn_ref, ffn_out, begin)
        scatter.each(scatter.down_unit, 0, 6, ffn_ref, ffn_out, begin)

    def line_copy(kind, number, source, to_end):
        return remote(
            source,
            arrived.at[kind, rows(number)],
            line_send.at[kind, number],
            line_recv.at[kind, number],
            member,
            line_place(to_end, core),
        )

    for slot in range(2):
        for number in range(3):
            core_copy(slot, number).wait_recv()
            both = mix_ref[slot, rows(number)].astype(wide) + paired[slot, rows(number)].astype(wide)
            paired[slot, rows(number)] = both.astype(low_type)

            @pl.when(end == 3)
            def _():
                line_copy(slot, number, paired.at[slot, rows(number)], 2).start()

            if slot == 1:

                @pl.when(end == 0)
                def _():
                    line_copy(2, number, paired.at[slot, rows(number)], 1).start()

    plane_copy(1).wait_recv()
    passing[0] = (
        part_ref[2 * slots : 2 * slots + half].astype(wide) + from_x[1].astype(wide)
    ).astype(low_type)
    plane_copy(4).start()
    plane_copy(3).wait_recv()
    passing[1] = (
        part_ref[slots + half : 2 * slots].astype(wide) + from_y[1].astype(wide)
    ).astype(low_type)
    plane_copy(5).start()

    def summed(slot, kinds, number):
        result = paired[slot, rows(number)].astype(wide)
        for kind in kinds:
            result = result + arrived[kind, rows(number)].astype(wide)
        return result.astype(low_type)

    def on_arrival(kind, number):
        line_copy(kind, number, paired.at[0, rows(number)], 0).wait_recv()

    def share(number):
        if number < 2:
            across = scatter.across
            scatter.each(
                scatter.in_unit, number * across, (number + 1) * across, total, mix_out, begin
            )
            scatter.each(scatter.gate_unit, number, number + 1, total, mix_out, begin)
        else:
            scatter.each(scatter.out_unit, 0, 4, total, mix_out, begin)
            scatter.smalls(total, mix_out, begin)

    for number in range(3):

        @pl.when((end == 2) | (end == 1))
        def _():
            on_arrival(0, number)
            paired[0, rows(number)] = summed(0, (0,), number)

        @pl.when(end == 2)
        def _():
            line_copy(0, number, paired.at[0, rows(number)], 1).start()

        @pl.when(end == 1)
        def _():
            line_copy(0, number, paired.at[0, rows(number)], 0).start()

    for number in range(3):

        @pl.when(end == 2)
        def _():
            on_arrival(1, number)
            paired[1, rows(number)] = summed(1, (1,), number)
            line_copy(1, number, paired.at[1, rows(number)], 1).start()

        @pl.when(end == 1)
        def _():
            on_arrival(1, number)
            on_arrival(2, number)
            total[rows(number)] = summed(1, (1, 2), number)

        @pl.when(end == 0)
        def _():
            on_arrival(0, number)
            total[rows(number)] = summed(0, (0,), number)

        @pl.when(scatter.owner)
        def _():
            share(number)

    plane_copy(0).wait_recv()
    plane_copy(2).wait_recv()
    plane_copy(4).wait_recv()
    plane_copy(5).wait_recv()
    gain = gain_ref[0:1]
    gain_sum = jnp.zeros((1, model), wide)
    for number, direct in ((0, from_x), (1, from_y)):
        at = slice(number * half, (number + 1) * half)
        grad = part_ref[at].astype(wide) + direct[0].astype(wide) + last[number].astype(wide)
        value = tokens_ref[at].astype(wide)
        scale = lax.rsqrt(jnp.mean(value * value, axis=1, keepdims=True) + norm_eps)
        scaled = grad * gain
        gain_sum = gain_sum + jnp.sum(grad * value * scale, axis=0, keepdims=True)
        inner = jnp.mean(scaled * value, axis=1, keepdims=True)
        back = scale * scaled - value * (scale * scale * scale * inner)
        tokens_out[at] = (res_ref[at] + back).astype(low_type)
    gain_part[...] = jnp.concatenate([gain_sum, gain_ref[1:2], jnp.zeros((6, model), wide)], axis=0)

    def gain_copy():
        return remote(
            gain_part, gain_plane.at[member], gain_send.at[0], gain_recv.at[member], 7, z
        )

    @pl.when(member != 7)
    def _():
        gain_copy().start()
        gain_copy().wait_send()
        gain_out[...] = jnp.zeros_like(gain_out)

    @pl.when(member == 7)
    def _():
        result = gain_part[...]
        for source in range(7):
            remote(
                gain_part,
                gain_plane.at[source],
                gain_send.at[0],
                gain_recv.at[source],
                7,
                z,
            ).wait_recv()
            result = result + gain_plane[source]
        quarter = model // 4
        for place in range(4):
            gain_line[place] = result[:, place * quarter : (place + 1) * quarter]

        def line_gain(place, slot):
            return remote(
                gain_line.at[place],
                gain_seen.at[slot],
                gain_send.at[1 + place],
                gain_recv.at[8 + slot],
                7,
                place,
            )

        for place in range(4):

            @pl.when(place != z)
            def _():
                line_gain(place, z).start()

        gain_out[...] = gain_line[z]
        for place in range(4):

            @pl.when(place != z)
            def _():
                line_gain(place, place).wait_recv()
                gain_out[...] += gain_seen[place]
                line_gain(place, z).wait_send()

    across = scatter.across
    scatter.arrivals(scatter.up_unit, 2 * across, ffn_ref, ffn_out)
    scatter.arrivals(scatter.down_unit, 6, ffn_ref, ffn_out)
    scatter.arrivals(scatter.in_unit, 2 * across, total, mix_out)
    scatter.arrivals(scatter.gate_unit, 2, total, mix_out)
    scatter.arrivals(scatter.out_unit, 4, total, mix_out)
    scatter.small_arrivals(total, mix_out)

    @pl.when(scatter.owner)
    def _():
        scatter.each(scatter.up_unit, 0, 2 * across, ffn_ref, ffn_out, finish_send)
        scatter.each(scatter.down_unit, 0, 6, ffn_ref, ffn_out, finish_send)
        scatter.each(scatter.in_unit, 0, 2 * across, total, mix_out, finish_send)
        scatter.each(scatter.gate_unit, 0, 2, total, mix_out, finish_send)
        scatter.each(scatter.out_unit, 0, 4, total, mix_out, finish_send)
        scatter.smalls(total, mix_out, finish_send)

    for number in range(6):
        plane_copy(number).wait_send()
    for slot in range(2):
        for number in range(3):
            core_copy(slot, number).wait_send()
    for number in range(3):

        @pl.when(end > 0)
        def _():
            line_copy(0, number, paired.at[0, rows(number)], 0).wait_send()

        @pl.when(end > 1)
        def _():
            line_copy(1, number, paired.at[1, rows(number)], 0).wait_send()

        @pl.when(end == 0)
        def _():
            line_copy(2, number, paired.at[1, rows(number)], 1).wait_send()


def sums(mix, part, ffn, tokens, residual_grad, gains, piece_length, width):
    model = tokens.shape[1]
    ffn_width = ffn.shape[1]
    sizes = (model, width, ffn_width, piece_length)
    half = tokens.shape[0] // 2
    block = mix.shape[1:]
    count = Scatter(sizes, 0, 0, None, None).count
    dma = pltpu.SemaphoreType.DMA
    vmem = pl.BlockSpec(memory_space=pltpu.VMEM)
    anywhere = pl.BlockSpec(memory_space=pl.ANY)
    return pl.pallas_call(
        functools.partial(sums_kernel, sizes),
        in_specs=[vmem, vmem, anywhere, vmem, vmem, vmem],
        out_specs=[anywhere, anywhere, vmem, vmem],
        out_shape=[
            jax.ShapeDtypeStruct(mix.shape, low_type),
            jax.ShapeDtypeStruct((4,) + ffn.shape, low_type),
            jax.ShapeDtypeStruct(tokens.shape, low_type),
            jax.ShapeDtypeStruct((8, model // 4), wide),
        ],
        scratch_shapes=[
            pltpu.VMEM((2,) + block, low_type),
            pltpu.VMEM((3,) + block, low_type),
            pltpu.VMEM(block, low_type),
            pltpu.VMEM((2, half, model), low_type),
            pltpu.VMEM((2, half, model), low_type),
            pltpu.VMEM((2, half, model), low_type),
            pltpu.VMEM((2, half, model), low_type),
            pltpu.VMEM((8, model), wide),
            pltpu.VMEM((8, 8, model), wide),
            pltpu.VMEM((4, 8, model // 4), wide),
            pltpu.VMEM((4, 8, model // 4), wide),
            dma((2, 3)),
            dma((2, 3)),
            dma((3, 3)),
            dma((3, 3)),
            dma((6,)),
            dma((6,)),
            dma((5,)),
            dma((12,)),
            dma((3, count)),
            dma((4, count)),
        ],
        compiler_params=pltpu.CompilerParams(
            collective_id=2, has_side_effects=True, vmem_limit_bytes=40 * 1024 * 1024
        ),
        cost_estimate=pl.CostEstimate(
            flops=mix.size * 4, bytes_accessed=mix.size * 8, transcendentals=0
        ),
        name="sums",
    )(mix, part, ffn, tokens, residual_grad, gains)


def tail_kernel(
    sizes,
    mix_ref,
    ffn_ref,
    gain_ref,
    master_ref,
    first_ref,
    second_ref,
    piece_ref,
    new_master_ref,
    new_first_ref,
    new_second_ref,
    weights_ref,
    bias_ref,
    grad,
    held,
    spread,
    send_sem,
    recv_sem,
):
    model, width, ffn_width, piece_length, chunks, lines, margin = sizes
    member = lax.axis_index("dp")
    z = lax.axis_index("shard")
    step = pl.program_id(0)
    lead = 128
    start_row = (member * piece_length) // lead
    offset = (member * piece_length) % lead
    tiles_in = 4 * width // lead
    tiles_ffn = 4 * ffn_width // lead
    tiles_model = model // lead

    def copy_to(origin, chunk, side, to):
        return pltpu.make_async_remote_copy(
            src_ref=held.at[origin, chunk],
            dst_ref=held.at[origin, chunk],
            send_sem=send_sem.at[side, origin, chunk],
            recv_sem=recv_sem.at[origin, chunk],
            device_id=(member, to),
            device_id_type=pl.DeviceIdType.MESH,
        )

    @pl.when(step == 0)
    def _():
        barrier = pltpu.get_barrier_semaphore()

        @pl.when(z > 0)
        def _():
            pl.semaphore_signal(
                barrier, inc=1, device_id=(member, z - 1), device_id_type=pl.DeviceIdType.MESH
            )

        @pl.when(z < 3)
        def _():
            pl.semaphore_signal(
                barrier, inc=1, device_id=(member, z + 1), device_id_type=pl.DeviceIdType.MESH
            )

        @pl.when((z == 0) | (z == 3))
        def _():
            pl.semaphore_wait(barrier, 1)

        @pl.when((z > 0) & (z < 3))
        def _():
            pl.semaphore_wait(barrier, 2)

        def clear(number, carry):
            grad[pl.ds(pl.multiple_of(number * 256, 256), 256), :] = jnp.zeros((256, lead), wide)
            return carry

        lax.fori_loop(0, grad.shape[0] // 256, clear, 0)

        def place(row, count, body):
            low = member * piece_length

            @pl.when((row * lead < low + piece_length) & ((row + count) * lead > low))
            def _():
                body(row - start_row + margin)

        base = 0

        def in_unit(number, carry):
            kind = number // tiles_model
            at = number % tiles_model

            def body(to):
                for q in range(4):
                    tile = mix_ref[
                        q,
                        pl.ds(pl.multiple_of(kind * width, width), width),
                        pl.ds(pl.multiple_of(at * lead, lead), lead),
                    ].astype(wide)
                    grad[pl.ds(to + q, lead, stride=tiles_in), :] = tile.T

            place((kind * model + at * lead) * tiles_in, lead * tiles_in, body)
            return carry

        lax.fori_loop(0, 2 * tiles_model, in_unit, 0)
        base = 2 * model * tiles_in

        def gate_body(number, carry):
            kind = number // 4
            q = number % 4

            def body(to):
                grad[pl.ds(to, width), :] = mix_ref[
                    q, pl.ds(pl.multiple_of(kind * width, width), width), model:
                ].astype(wide)

            place(2 * model * tiles_in + number * width, width, body)
            return carry

        lax.fori_loop(0, 8, gate_body, 0)
        base = base + 8 * width
        out_base = base

        quarter = width // 4

        def out_unit(number, carry):
            q = number // 4
            part = number % 4

            def body(to):
                for at in range(tiles_model):
                    grad[pl.ds(to + at, quarter, stride=tiles_model), :] = mix_ref[
                        q,
                        pl.ds(pl.multiple_of(2 * width + part * quarter, quarter), quarter),
                        at * lead : (at + 1) * lead,
                    ].astype(wide)

            place(out_base + number * quarter * tiles_model, quarter * tiles_model, body)
            return carry

        lax.fori_loop(0, 16, out_unit, 0)
        base = base + 4 * width * tiles_model
        up_base = base

        def up_unit(number, carry):
            kind = number // tiles_model
            at = number % tiles_model
            columns = pl.ds(pl.multiple_of(at * lead, lead), lead)

            def body(to):
                for tile in range(tiles_ffn):
                    found = []
                    row = tile * lead
                    while row < (tile + 1) * lead:
                        q = row // ffn_width
                        last = min((q + 1) * ffn_width, (tile + 1) * lead)
                        found.append(
                            ffn_ref[
                                q,
                                kind,
                                row - q * ffn_width : last - q * ffn_width,
                                columns,
                            ].astype(wide)
                        )
                        row = last
                    block = found[0] if len(found) == 1 else jnp.concatenate(found, axis=0)
                    grad[pl.ds(to + tile, lead, stride=tiles_ffn), :] = block.T

            place(up_base + (kind * model + at * lead) * tiles_ffn, lead * tiles_ffn, body)
            return carry

        lax.fori_loop(0, 2 * tiles_model, up_unit, 0)
        base = base + 2 * model * tiles_ffn
        down_base = base
        sixth = ffn_width // 6

        def down_unit(number, carry):
            q = number // 6
            part = number % 6

            def body(to):
                for at in range(tiles_model):
                    grad[pl.ds(to + at, sixth, stride=tiles_model), :] = ffn_ref[
                        q,
                        2,
                        pl.ds(pl.multiple_of(part * sixth, 16), sixth),
                        at * lead : (at + 1) * lead,
                    ].astype(wide)

            place(down_base + number * sixth * tiles_model, sixth * tiles_model, body)
            return carry

        lax.fori_loop(0, 24, down_unit, 0)
        small_base = base + 4 * ffn_width * tiles_model
        smalls = [
            mix_ref[q, 2 * width : 2 * width + 16, model:].astype(wide)
            for q in range(4)
        ]

        def small_body(to):
            for q in range(4):
                grad[pl.ds(to + q, 8, stride=tiles_in), :] = smalls[q][:8]
            for number in range(6):
                kind, at = number // 3, number % 3
                grad[pl.ds(to + 8 * tiles_in + number, 1), :] = gain_ref[
                    kind : kind + 1, at * lead : (at + 1) * lead
                ]

        place(small_base, 8 * tiles_in + 6, small_body)
        bias_ref[...] = jnp.concatenate([small[5:7] for small in smalls], axis=1)

    @pl.when(step < chunks)
    def _():
        row = margin + step * lines
        shift = (lead - offset) % lead
        here = pltpu.roll(grad[pl.ds(row, lines), :], shift, 1)
        after = pltpu.roll(grad[pl.ds(row + 1, lines), :], shift, 1)
        lane = lax.broadcasted_iota(jnp.int32, (lines, lead), 1)
        piece = jnp.where(lane < lead - offset, here, after).reshape(1, lines * lead)
        piece_ref[...] = piece
        new_first = beta_one * first_ref[...] + (1.0 - beta_one) * piece
        new_second = beta_two * second_ref[...] + (1.0 - beta_two) * piece * piece
        master = master_ref[...]
        new_master = master - learn_rate * (
            new_first / corr_one / (jnp.sqrt(new_second / corr_two) + adam_eps)
            + weight_decay * master
        )
        new_first_ref[...] = new_first
        new_second_ref[...] = new_second
        new_master_ref[...] = new_master
        held[z, step] = new_master.reshape(lines, lead).astype(low_type)

        @pl.when(z < 3)
        def _():
            copy_to(z, step, 0, z + 1).start()

        @pl.when(z > 0)
        def _():
            copy_to(z, step, 1, z - 1).start()

    def pass_on(origin, chunk, right):
        copy_to(origin, chunk, 0, z).wait_recv()
        if right:

            @pl.when(z < 3)
            def _():
                copy_to(origin, chunk, 0, z + 1).start()
        else:

            @pl.when(z > 0)
            def _():
                copy_to(origin, chunk, 1, z - 1).start()

    @pl.when((step >= chunks) & (step < 2 * chunks))
    def _():
        chunk = step - chunks

        @pl.when(z > 0)
        def _():
            pass_on(z - 1, chunk, True)

        @pl.when(z < 3)
        def _():
            pass_on(z + 1, chunk, False)

    @pl.when(step >= 2 * chunks)
    def _():
        chunk = step - 2 * chunks

        @pl.when(z >= 2)
        def _():
            pass_on(z - 2, chunk, True)

        @pl.when(z <= 1)
        def _():
            pass_on(z + 2, chunk, False)

        @pl.when(z == 3)
        def _():
            copy_to(0, chunk, 0, z).wait_recv()

        @pl.when(z == 0)
        def _():
            copy_to(3, chunk, 0, z).wait_recv()

        for origin in range(4):
            spread[origin * lines : (origin + 1) * lines, :] = held[origin, chunk].astype(wide)

        def line(number, carry):
            weights_ref[:, pl.ds(pl.multiple_of(number * lead, lead), lead)] = spread[
                pl.ds(number, 4, stride=lines), :
            ].astype(low_type)
            return carry

        lax.fori_loop(0, lines, line, 0, unroll=8)

    @pl.when(step == 3 * chunks - 1)
    def _():
        for origin in range(4):

            def finish(chunk, carry):
                @pl.when((origin <= z) & (z < 3))
                def _():
                    copy_to(origin, chunk, 0, z).wait_send()

                @pl.when((origin >= z) & (z > 0))
                def _():
                    copy_to(origin, chunk, 1, z).wait_send()

                return carry

            lax.fori_loop(0, chunks, finish, 0)


def tail(mix, ffn, gains, master, first, second, sizes):
    model, width, ffn_width = sizes
    piece_length = master.shape[1]
    chunks = 8
    lines = -(-piece_length // (chunks * 128 * 16)) * 16
    block = lines * 128
    margin = 1536
    rows = -(-(2 * margin + chunks * lines + 8) // 256) * 256
    packed = jax.ShapeDtypeStruct(master.shape, wide)
    whole = lambda shape: pl.BlockSpec(shape, lambda s: (0,) * len(shape))
    chunk_spec = pl.BlockSpec((1, block), lambda s: (0, jnp.minimum(s, chunks - 1)))
    once = lambda shape: pl.BlockSpec(
        shape, lambda s: (0,) * len(shape), pipeline_mode=pl.Buffered(1)
    )
    return pl.pallas_call(
        functools.partial(
            tail_kernel, (model, width, ffn_width, piece_length, chunks, lines, margin)
        ),
        grid=(3 * chunks,),
        in_specs=[once(mix.shape), once(ffn.shape), once(gains.shape)] + [chunk_spec] * 3,
        out_specs=[chunk_spec] * 4
        + [
            pl.BlockSpec((4, block), lambda s: (0, jnp.maximum(s - 2 * chunks, 0))),
            whole((2, 4 * width)),
        ],
        out_shape=[packed] * 4
        + [
            jax.ShapeDtypeStruct((4, piece_length), low_type),
            jax.ShapeDtypeStruct((2, 4 * width), wide),
        ],
        scratch_shapes=[
            pltpu.VMEM((rows, 128), wide),
            pltpu.VMEM((4, chunks, lines, 128), low_type),
            pltpu.VMEM((4 * lines, 128), wide),
            pltpu.SemaphoreType.DMA((2, 4, chunks)),
            pltpu.SemaphoreType.DMA((4, chunks)),
        ],
        compiler_params=pltpu.CompilerParams(
            collective_id=1, has_side_effects=True, vmem_limit_bytes=58 * 1024 * 1024
        ),
        cost_estimate=pl.CostEstimate(
            flops=20 * piece_length,
            bytes_accessed=40 * piece_length,
            transcendentals=piece_length,
        ),
        name="tail",
    )(mix, ffn, gains, master, first, second)


def group_body(
    tokens,
    cotangent,
    seq_start,
    live_mask,
    input_proj,
    gate_blocks,
    output_proj,
    ffn_gate_up,
    ffn_down,
    conv_taps,
    gate_bias,
    decay_param,
    norm_gains,
    master_shard,
    first_moment,
    second_moment,
):
    slots, model = tokens.shape
    slice_rec = input_proj.shape[2]
    slice_ffn = ffn_down.shape[0]
    width = slice_rec // 4
    ffn_width = slice_ffn // 4
    piece_length = master_shard.shape[1]
    member = lax.axis_index("dp")
    chip = member // 2
    core = member % 2
    z = lax.axis_index("shard")
    end = jnp.where(core == 0, z, 3 - z)

    mask_rows = live_mask.astype(wide)[:, None]
    stream = tokens.astype(wide)
    grad_stream = cotangent.astype(wide) * mask_rows

    starts = jnp.broadcast_to(seq_start.astype(low_type)[:, None], (slots, width))
    (
        mix_in,
        mix_weights,
        ffn_weights,
        saved_p,
        saved_state,
        saved_low,
        all_starts,
        residual,
        ffn_in,
        all_grad_out,
        gains,
    ) = front(
        jnp.concatenate([tokens, starts], axis=1),
        grad_stream.astype(low_type),
        jnp.concatenate([norm_gains, jnp.zeros((14, norm_gains.shape[1]), low_type)]),
        jnp.concatenate(
            [conv_taps, gate_bias, decay_param[None], jnp.zeros((8, slice_rec), low_type)]
        ),
        input_proj,
        gate_blocks,
        output_proj,
        ffn_gate_up,
        ffn_down,
        (model, width, ffn_width),
    )
    saved = (saved_p, saved_state, saved_low)
    ffn_in = ffn_in.reshape(4 * slots, model)
    all_grad_out = all_grad_out.reshape(4 * slots, model)
    sum_ffn, res_low, grad_residual, gain_sums, block_out = middle(
        ffn_in,
        all_grad_out,
        ffn_weights,
        residual,
        gains,
        jnp.broadcast_to(mask_rows.astype(low_type), (slots, width)),
    )
    res_low = res_low.reshape(4 * slots, model)
    grad_mix, mix_in_part = mix_backward(
        mix_in, res_low, all_starts, mix_weights, saved, slots, width
    )
    four_mix, four_ffn, tokens_grad, gain_total = sums(
        grad_mix,
        mix_in_part,
        sum_ffn,
        tokens,
        grad_residual,
        gain_sums,
        piece_length,
        width,
    )
    piece, new_master, new_first, new_second, new_weights, bias_total = tail(
        four_mix,
        four_ffn,
        gain_total,
        master_shard,
        first_moment,
        second_moment,
        (model, width, ffn_width),
    )
    return (
        block_out,
        tokens_grad,
        piece,
        new_master,
        new_first,
        new_second,
        new_weights,
        bias_total,
    )


def rms_scale(values, gain):
    return values * lax.rsqrt(jnp.mean(values * values, axis=-1, keepdims=True) + norm_eps) * gain


def conv_mix(signal, taps, position):
    result = taps[-1] + taps[0] * signal
    for shift_by in range(1, taps.shape[0] - 1):
        moved = jnp.pad(signal, ((shift_by, 0), (0, 0)))[:-shift_by]
        result = result + taps[shift_by] * jnp.where((position >= shift_by)[:, None], moved, 0.0)
    return result


def combine_steps(earlier, later):
    decay_first, value_first = earlier
    decay_second, value_second = later
    return (decay_first * decay_second, decay_second * value_first + value_second)


def recurrence(logits, signal, branch, bias_term, decay_term, position):
    row_count = signal.shape[0]
    recur_gate = jax.nn.sigmoid(logits[0].reshape(row_count, -1) + bias_term[0])
    input_gate = jax.nn.sigmoid(logits[1].reshape(row_count, -1) + bias_term[1])
    log_decay = -gate_scale * recur_gate * jax.nn.softplus(-decay_term)
    decay_rate = jnp.where((position > 0)[:, None], jnp.exp(log_decay), 0.0)
    drive_term = jnp.sqrt(-jnp.expm1(2.0 * log_decay)) * input_gate * signal
    states = lax.associative_scan(combine_steps, (decay_rate, drive_term), axis=0)[1]
    return states * jax.nn.gelu(branch)


def gated_gelu(ffn_pre):
    return jax.nn.gelu(ffn_pre[0]) * ffn_pre[1]


def mixer_forward(
    mix_in, input_proj, gate_blocks, output_proj, conv_taps, gate_bias, decay_param, position
):
    projected = jnp.einsum("sd,kdr->ksr", mix_in, input_proj, preferred_element_type=jnp.float32)
    conv_out, conv_pull = jax.vjp(
        lambda signal, taps: conv_mix(signal, taps, position), projected[0], conv_taps
    )
    row_count = conv_out.shape[0]
    conv_low = conv_out.astype(jnp.bfloat16).reshape(
        row_count, gate_blocks.shape[1], gate_blocks.shape[2]
    )
    gate_logits = jnp.einsum(
        "shb,khbc->kshc", conv_low, gate_blocks, preferred_element_type=jnp.float32
    )
    mixed, mix_pull = jax.vjp(
        lambda logits, signal, branch, bias_term, decay_term: recurrence(
            logits, signal, branch, bias_term, decay_term, position
        ),
        gate_logits,
        conv_out,
        projected[1],
        gate_bias,
        decay_param,
    )
    mixed_low = mixed.astype(jnp.bfloat16)
    partial_out = jnp.dot(mixed_low, output_proj, preferred_element_type=jnp.float32)
    return (partial_out, (conv_pull, conv_low, mix_pull, mixed_low))


def mixer_backward(grad_out_low, mix_in, saved, input_proj, gate_blocks, output_proj):
    conv_pull, conv_low, mix_pull, mixed_low = saved
    grad_output_proj = jnp.einsum(
        "sr,sd->rd", mixed_low, grad_out_low, preferred_element_type=jnp.float32
    )
    grad_mixed = jnp.einsum(
        "sd,rd->sr", grad_out_low, output_proj, preferred_element_type=jnp.float32
    )
    grad_logits, grad_conv_direct, grad_branch, grad_bias, grad_decay = mix_pull(grad_mixed)
    logits_low = grad_logits.astype(jnp.bfloat16)
    grad_blocks = jnp.einsum(
        "shb,kshc->khbc", conv_low, logits_low, preferred_element_type=jnp.float32
    )
    grad_conv_gates = jnp.einsum(
        "kshc,khbc->shb", logits_low, gate_blocks, preferred_element_type=jnp.float32
    )
    grad_signal, grad_taps = conv_pull(
        grad_conv_direct + grad_conv_gates.reshape(grad_conv_direct.shape)
    )
    proj_low = jnp.stack([grad_signal, grad_branch]).astype(jnp.bfloat16)
    grad_input_proj = jnp.einsum(
        "sd,ksr->kdr", mix_in, proj_low, preferred_element_type=jnp.float32
    )
    grad_mix_in = jnp.einsum(
        "ksr,kdr->sd", proj_low, input_proj, preferred_element_type=jnp.float32
    )
    return (
        grad_mix_in,
        (grad_input_proj, grad_blocks, grad_output_proj, grad_taps, grad_bias, grad_decay),
    )


def ffn_forward(ffn_in_low, ffn_gate_up, ffn_down):
    ffn_pre = jnp.einsum("sd,kdf->ksf", ffn_in_low, ffn_gate_up, preferred_element_type=jnp.float32)
    ffn_act, ffn_pull = jax.vjp(gated_gelu, ffn_pre)
    ffn_low = ffn_act.astype(jnp.bfloat16)
    partial_ffn = jnp.dot(ffn_low, ffn_down, preferred_element_type=jnp.float32)
    return (partial_ffn, (ffn_pull, ffn_low))


def ffn_backward(grad_low, ffn_in_low, saved, ffn_gate_up, ffn_down):
    ffn_pull, ffn_low = saved
    grad_down = jnp.einsum("sf,sd->fd", ffn_low, grad_low, preferred_element_type=jnp.float32)
    grad_act = jnp.einsum("sd,fd->sf", grad_low, ffn_down, preferred_element_type=jnp.float32)
    grad_pre = ffn_pull(grad_act)[0]
    pre_low = grad_pre.astype(jnp.bfloat16)
    grad_gate_up = jnp.einsum(
        "sd,ksf->kdf", ffn_in_low, pre_low, preferred_element_type=jnp.float32
    )
    grad_ffn_in = jnp.einsum(
        "ksf,kdf->sd", pre_low, ffn_gate_up, preferred_element_type=jnp.float32
    )
    return (grad_ffn_in, grad_gate_up, grad_down)


def body(
    tokens,
    cotangent,
    seq_start,
    live_mask,
    input_proj,
    gate_blocks,
    output_proj,
    ffn_gate_up,
    ffn_down,
    conv_taps,
    gate_bias,
    decay_param,
    norm_gains,
    master_shard,
    first_moment,
    second_moment,
):
    slot_count = tokens.shape[0]
    position = jnp.arange(slot_count, dtype=jnp.int32) - seq_start
    mask_rows = live_mask.astype(jnp.float32)[:, None]
    stream = tokens.astype(jnp.float32)
    grad_stream = cotangent.astype(jnp.float32) * mask_rows
    shards = (
        input_proj,
        gate_blocks,
        output_proj,
        ffn_gate_up,
        ffn_down,
        conv_taps,
        gate_bias,
        decay_param,
        norm_gains,
    )
    (
        full_in,
        full_blocks,
        full_out,
        full_up,
        full_down,
        full_taps,
        full_bias,
        full_decay,
        full_gains,
    ) = (
        lax.all_gather(shards[0], "shard", axis=2, tiled=True),
        lax.all_gather(shards[1], "shard", axis=1, tiled=True),
        lax.all_gather(shards[2], "shard", axis=0, tiled=True),
        lax.all_gather(shards[3], "shard", axis=2, tiled=True),
        lax.all_gather(shards[4], "shard", axis=0, tiled=True),
        lax.all_gather(shards[5], "shard", axis=1, tiled=True),
        lax.all_gather(shards[6], "shard", axis=1, tiled=True),
        lax.all_gather(shards[7], "shard", axis=0, tiled=True),
        lax.all_gather(shards[8], "shard", axis=1, tiled=True),
    )
    gains = full_gains.astype(jnp.float32)
    normed, norm_pull = jax.vjp(rms_scale, stream, gains[0])
    mix_in = normed.astype(jnp.bfloat16)
    mix_out, mix_saved = mixer_forward(
        mix_in,
        full_in,
        full_blocks,
        full_out,
        full_taps.astype(jnp.float32),
        full_bias.astype(jnp.float32),
        full_decay.astype(jnp.float32),
        position,
    )
    residual = stream + mix_out
    normed_two, second_pull = jax.vjp(rms_scale, residual, gains[1])
    ffn_in_low = normed_two.astype(jnp.bfloat16)
    ffn_result, ffn_saved = ffn_forward(ffn_in_low, full_up, full_down)
    block_out = (mask_rows * (residual + ffn_result)).astype(jnp.bfloat16)
    grad_ffn_in, grad_up, grad_down = ffn_backward(
        grad_stream.astype(jnp.bfloat16), ffn_in_low, ffn_saved, full_up, full_down
    )
    grad_norm_two, grad_gain_two = second_pull(grad_ffn_in)
    grad_residual = grad_stream + grad_norm_two
    grad_mix_in, mix_grads = mixer_backward(
        grad_residual.astype(jnp.bfloat16), mix_in, mix_saved, full_in, full_blocks, full_out
    )
    grad_norm_one, grad_gain_one = norm_pull(grad_mix_in)
    tokens_grad = (grad_residual + grad_norm_one).astype(jnp.bfloat16)
    grads = (
        mix_grads[0],
        mix_grads[1],
        mix_grads[2],
        grad_up,
        grad_down,
        mix_grads[3],
        mix_grads[4],
        mix_grads[5],
        jnp.stack([grad_gain_one, grad_gain_two]),
    )
    summed = (
        lax.psum_scatter(
            grads[0].astype(jnp.bfloat16), "shard", scatter_dimension=2, tiled=True
        ).astype(jnp.float32),
        lax.psum_scatter(
            grads[1].astype(jnp.bfloat16), "shard", scatter_dimension=1, tiled=True
        ).astype(jnp.float32),
        lax.psum_scatter(
            grads[2].astype(jnp.bfloat16), "shard", scatter_dimension=0, tiled=True
        ).astype(jnp.float32),
        lax.psum_scatter(
            grads[3].astype(jnp.bfloat16), "shard", scatter_dimension=2, tiled=True
        ).astype(jnp.float32),
        lax.psum_scatter(
            grads[4].astype(jnp.bfloat16), "shard", scatter_dimension=0, tiled=True
        ).astype(jnp.float32),
        lax.psum_scatter(
            grads[5].astype(jnp.bfloat16), "shard", scatter_dimension=1, tiled=True
        ).astype(jnp.float32),
        lax.psum_scatter(
            grads[6].astype(jnp.bfloat16), "shard", scatter_dimension=1, tiled=True
        ).astype(jnp.float32),
        lax.psum_scatter(
            grads[7].astype(jnp.bfloat16), "shard", scatter_dimension=0, tiled=True
        ).astype(jnp.float32),
        lax.psum_scatter(
            grads[8].astype(jnp.bfloat16), "shard", scatter_dimension=1, tiled=True
        ).astype(jnp.float32),
    )
    flat = jnp.concatenate([member.reshape(1, -1) for member in summed], axis=1)
    piece = lax.psum_scatter(flat, "dp", scatter_dimension=1, tiled=True)
    bias_total = lax.psum(summed[6], "dp")
    new_first = beta_one * first_moment + (1.0 - beta_one) * piece
    new_second = beta_two * second_moment + (1.0 - beta_two) * piece * piece
    new_master = master_shard - learn_rate * (
        new_first / corr_one / (jnp.sqrt(new_second / corr_two) + adam_eps)
        + weight_decay * master_shard
    )
    new_weights = lax.all_gather(new_master.astype(jnp.bfloat16), "shard", axis=0, tiled=True)
    return (
        block_out,
        tokens_grad,
        piece,
        new_master,
        new_first,
        new_second,
        new_weights,
        bias_total,
    )


def solution(mesh):
    fits = mesh.shape["dp"] == 8 and mesh.shape["shard"] == 4
    placed = (
        P(("dp", "shard"), None),
        P(("dp", "shard"), None),
        P(("dp", "shard")),
        P(("dp", "shard")),
        P(None, None, "shard"),
        P(None, "shard", None, None),
        P("shard", None),
        P(None, None, "shard"),
        P("shard", None),
        P(None, "shard"),
        P(None, "shard"),
        P("shard"),
        P(None, "shard"),
        P("shard", "dp"),
        P("shard", "dp"),
        P("shard", "dp"),
    )
    return jax.shard_map(
        group_body if fits else body,
        mesh=mesh,
        in_specs=placed,
        out_specs=(
            P(("dp", "shard"), None),
            P(("dp", "shard"), None),
            P("shard", "dp"),
            P("shard", "dp"),
            P("shard", "dp"),
            P("shard", "dp"),
            P(None, "dp"),
            P(None, "shard"),
        ),
        check_vma=False,
    )
```

```python
import functools
import jax
import jax.numpy as jnp
from jax import lax
from jax.experimental import pallas as pl
from jax.experimental.pallas import tpu as pltpu
from jax.sharding import PartitionSpec as P

norm_eps = 1e-06
gate_scale = 8.0
beta_one = 0.9
beta_two = 0.95
learn_rate = 0.01
weight_decay = 0.1
adam_eps = 1e-08
corr_one = 1.0 - beta_one**10.0
corr_two = 1.0 - beta_two**10.0
low_type = jnp.bfloat16
wide = jnp.float32
axes = ("dp", "shard")
gelu_scale = 0.7978845608028654
gelu_cube = 0.044715


def device_pairs(target):
    found = []
    for chip in range(4):
        for core in range(2):
            for z in range(4):
                to = target(chip, core, z)
                if to is not None:
                    source = (chip * 2 + core) * 4 + z
                    found.append((source, (to[0] * 2 + to[1]) * 4 + to[2]))
    return found


def line_pairs(moves):
    moves = dict(moves)

    def target(chip, core, z):
        end = z if core == 0 else 3 - z
        if end not in moves:
            return None
        to = moves[end]
        return (chip, core, to if core == 0 else 3 - to)

    return device_pairs(target)


def step_pairs(step):
    return device_pairs(
        lambda chip, core, z: (chip, core, z + step) if 0 <= z + step < 4 else None
    )


def plane_pairs(flip, owners_only=False):
    return device_pairs(
        lambda chip, core, z: None if owners_only and core != z // 2 else (chip ^ flip, core, z)
    )


core_pairs = device_pairs(lambda chip, core, z: (chip, 1 - core, z))
owner_core_pairs = device_pairs(
    lambda chip, core, z: (chip, 1 - core, z) if core == z // 2 else None
)


def move(value, pairs):
    return lax.ppermute(value, axes, pairs)


def plane_gather(value, dim=0, owners_only=False):
    half = value.shape[dim] // 2
    across_x = move(value, plane_pairs(1, owners_only))
    across_y = move(value, plane_pairs(2, owners_only))
    first = lax.slice_in_dim(across_x, 0, half, axis=dim)
    second = lax.slice_in_dim(across_y, half, 2 * half, axis=dim)
    first = move(first, plane_pairs(2, owners_only))
    second = move(second, plane_pairs(1, owners_only))
    return (value, across_x, across_y, jnp.concatenate([first, second], axis=dim))


def plane_reduce(parts):
    slots = parts.shape[0] // 4
    half = slots // 2
    mine, for_x, for_y, for_d = (
        parts[number * slots : (number + 1) * slots] for number in range(4)
    )
    top = slice(0, half)
    low = slice(half, slots)
    from_x = move(jnp.concatenate([for_x[top], for_d[top]]), plane_pairs(1))
    from_y = move(jnp.concatenate([for_y[low], for_d[low]]), plane_pairs(2))
    send_y = (for_y[top].astype(wide) + from_x[half:].astype(wide)).astype(low_type)
    send_x = (for_x[low].astype(wide) + from_y[half:].astype(wide)).astype(low_type)
    last_top = move(send_y, plane_pairs(2))
    last_low = move(send_x, plane_pairs(1))
    return jnp.concatenate(
        [
            mine[top].astype(wide) + from_x[:half].astype(wide) + last_top.astype(wide),
            mine[low].astype(wide) + from_y[:half].astype(wide) + last_low.astype(wide),
        ]
    )


def pick(end, choices):
    result = choices[3]
    for number in (2, 1, 0):
        result = jnp.where(end == number, choices[number], result)
    return result


def line_spread(own, end):
    ahead = move(own, line_pairs({0: 1, 1: 2}))
    back = move(own, line_pairs({1: 0}))
    ahead_two = move(ahead, line_pairs({1: 2, 2: 3}))
    ahead_three = move(ahead_two, line_pairs({2: 3}))
    return (
        pick(end, [own, ahead, ahead_two, ahead_three]),
        pick(end, [back, own, ahead, ahead_two]),
    )


def add_low(left, right):
    return (left.astype(wide) + right.astype(wide)).astype(low_type)


def line_sum(outer, inner, end):
    first = add_low(outer, move(outer, line_pairs({3: 2})))
    inner_one = add_low(inner, move(inner, line_pairs({3: 2, 0: 1})))
    second = add_low(outer, move(first, line_pairs({2: 1})))
    inner_two = add_low(inner_one, move(inner_one, line_pairs({2: 1})))
    third = add_low(outer, move(second, line_pairs({1: 0})))
    return jnp.where(end == 0, third, inner_two)


def turn_pairs(turn):
    return device_pairs(lambda chip, core, z: (chip, core, (z + turn) % 4))


def all_slices(own, z):
    found = [own] + [move(own, turn_pairs(turn)) for turn in (1, 2, 3)]
    return jnp.concatenate(
        [
            sum(jnp.where((z - at) % 4 == turn, found[turn], 0) for turn in range(4))
            for at in range(4)
        ],
        axis=-1,
    )


def shard_slices(value, z):
    size = value.shape[-1] // 4

    def part(turn):
        return lax.dynamic_slice_in_dim(value, ((z + turn) % 4) * size, size, axis=1)

    return part(0) + sum(move(part(turn), turn_pairs(turn)) for turn in (1, 2, 3))


def dot_rows(left, right):
    return lax.dot_general(left, right, (((1,), (1,)), ((), ())), preferred_element_type=wide)


def dot_plain(left, right):
    return lax.dot_general(left, right, (((1,), (0,)), ((), ())), preferred_element_type=wide)


def dot_slots(left, right):
    return lax.dot_general(left, right, (((0,), (0,)), ((), ())), preferred_element_type=wide)


def gelu_parts(value):
    square = value * value
    bent = jnp.tanh(gelu_scale * value * (1.0 + gelu_cube * square))
    half = 0.5 * (1.0 + bent)
    slope = half + 0.5 * value * (1.0 - bent * bent) * gelu_scale * (
        1.0 + 3.0 * gelu_cube * square
    )
    return (value * half, slope)


def shift_down(value, step):
    if step % 8 == 0:
        return jnp.concatenate([value[-step:], value[:-step]], axis=0)
    return pltpu.roll(value, step, 0)


def shift_up(value, step):
    if step % 8 == 0:
        return jnp.concatenate([value[step:], value[:step]], axis=0)
    return pltpu.roll(value, value.shape[0] - step, 0)


def scan_slots(decay, value, shift):
    step = 1
    while step < value.shape[0]:
        value = value + decay * shift(value, step)
        if 2 * step < value.shape[0]:
            decay = decay * shift(decay, step)
        step *= 2
    return value


def one_minus_exp(value):
    series = jnp.ones_like(value)
    for number in range(11, 1, -1):
        series = 1.0 - value * (1.0 / number) * series
    return jnp.where(value < 0.8, value * series, 1.0 - jnp.exp(-value))


def soft_plus(value):
    return jnp.maximum(value, 0.0) + jnp.log1p(jnp.exp(-jnp.abs(value)))


def mixer_parts(first, position, small, gates):
    conv_out = small[4:5] + small[0:1] * first
    shifted = []
    for step in range(1, 4):
        moved = jnp.where(position >= step, shift_down(first, step), 0.0)
        shifted.append(moved)
        conv_out = conv_out + small[step : step + 1] * moved
    conv_low = conv_out.astype(low_type)
    logits = dot_plain(conv_low, gates)
    width = first.shape[1]
    recur_gate = jax.nn.sigmoid(logits[:, :width] + small[5:6])
    input_gate = jax.nn.sigmoid(logits[:, width:] + small[6:7])
    rate = gate_scale * soft_plus(-small[7:8])
    log_decay = -rate * recur_gate
    decay = jnp.where(position > 0, jnp.exp(log_decay), 0.0)
    gone = one_minus_exp(-2.0 * log_decay)
    root = jnp.sqrt(gone)
    return conv_out, shifted, conv_low, recur_gate, input_gate, rate, decay, gone, root


def weight_views(w_ref, width):
    model = w_ref.shape[2] - width
    proj = w_ref[0, 0 : 2 * width, 0:model]
    out = w_ref[0, 2 * width : 3 * width, 0:model]
    gates = jnp.concatenate(
        [w_ref[0, 0:width, model:], w_ref[0, width : 2 * width, model:]], axis=1
    )
    small = w_ref[0, 2 * width : 2 * width + 16, model:].astype(wide)
    return proj, out, gates, small


def slot_position(starts):
    slot = lax.broadcasted_iota(jnp.int32, (starts.shape[0], 1), 0)
    return slot - starts[:, 0:1].astype(wide).astype(jnp.int32)


def mixer_step(x, position, views, width):
    proj, out, gates, small = views
    projected = dot_rows(x, proj)
    conv_out, _, _, _, input_gate, _, decay, _, root = mixer_parts(
        projected[:, :width], position, small, gates
    )
    states = scan_slots(decay, root * input_gate * conv_out, shift_down)
    mixed_low = (states * gelu_parts(projected[:, width:])[0]).astype(low_type)
    return projected, states, mixed_low, dot_plain(mixed_low, out)


def mixer_backward_kernel(
    width,
    x_ref,
    res_ref,
    pos_ref,
    w_ref,
    p_ref,
    state_ref,
    low_ref,
    grad_ref,
    gin_ref,
    acc_w,
    acc_in,
):
    head = pl.program_id(0)
    block = pl.program_id(1)
    slots, model = x_ref.shape
    proj, out, gates, small = weight_views(w_ref, width)
    position = slot_position(pos_ref[...])
    first = p_ref[0, :, 0:width]
    res_low = res_ref[...]
    states = state_ref[0]
    conv_out, shifted, conv_low, recur_gate, input_gate, rate, decay, gone, root = mixer_parts(
        first, position, small, gates
    )
    grad_mixed = dot_rows(res_low, out)
    active, slope = gelu_parts(p_ref[0, :, width:])
    grad_second = grad_mixed * states * slope
    adjoint = scan_slots(shift_up(decay, 1), grad_mixed * active, shift_up)
    grad_decay = adjoint * shift_down(states, 1)
    grad_root = adjoint * input_gate * conv_out
    grad_input_gate = adjoint * root * conv_out
    grad_conv = adjoint * root * input_gate
    grad_log = grad_decay * decay - grad_root * (1.0 - gone) / root
    grad_recur = -rate * grad_log
    grad_logit_a = grad_recur * recur_gate * (1.0 - recur_gate)
    grad_logit_b = grad_input_gate * input_gate * (1.0 - input_gate)
    grad_param = jnp.sum(grad_log * recur_gate, axis=0, keepdims=True) * (
        gate_scale * jax.nn.sigmoid(-small[7:8])
    )
    logits_low = jnp.concatenate([grad_logit_a, grad_logit_b], axis=1).astype(low_type)
    grad_conv = grad_conv + dot_rows(logits_low, gates)
    grad_gates = dot_slots(conv_low, logits_low)
    sums = [jnp.sum(grad_conv * first, axis=0, keepdims=True)]
    grad_first = small[0:1] * grad_conv
    for step in range(1, 4):
        sums.append(jnp.sum(grad_conv * shifted[step - 1], axis=0, keepdims=True))
        kept = jnp.where(position >= step, grad_conv, 0.0)
        grad_first = grad_first + small[step : step + 1] * shift_up(kept, step)
    sums.append(jnp.sum(grad_conv, axis=0, keepdims=True))
    sums.append(jnp.sum(grad_logit_a, axis=0, keepdims=True))
    sums.append(jnp.sum(grad_logit_b, axis=0, keepdims=True))
    sums.append(grad_param)
    grad_small = jnp.concatenate(sums, axis=0)
    proj_low = jnp.concatenate([grad_first, grad_second], axis=1).astype(low_type)
    part = dot_plain(proj_low, proj)
    rows = pl.ds(pl.multiple_of(block * slots, slots), slots)

    @pl.when(block == 0)
    def _():
        acc_w[...] = jnp.zeros_like(acc_w)

    acc_w[0 : 2 * width, 0:model] += dot_slots(proj_low, x_ref[...])
    acc_w[2 * width : 3 * width, 0:model] += dot_slots(low_ref[0], res_low)
    acc_w[0:width, model:] += grad_gates[:, :width]
    acc_w[width : 2 * width, model:] += grad_gates[:, width:]
    acc_w[2 * width : 2 * width + 8, model:] += grad_small

    @pl.when(head == 0)
    def _():
        acc_in[rows, :] = part

    @pl.when(head > 0)
    def _():
        acc_in[rows, :] += part

    @pl.when(block == pl.num_programs(1) - 1)
    def _():
        grad_ref[0] = acc_w[...].astype(low_type)

    @pl.when(head == pl.num_programs(0) - 1)
    def _():
        gin_ref[rows, :] = acc_in[rows, :].astype(low_type)


def mix_backward(mix_in, res_low, position, weights, saved, slots, width):
    rows, model = mix_in.shape
    heads = weights.shape[0]
    blocks = rows // slots
    return pl.pallas_call(
        functools.partial(mixer_backward_kernel, width),
        grid=(heads, blocks),
        in_specs=[
            pl.BlockSpec((slots, model), lambda h, b: (b, 0)),
            pl.BlockSpec((slots, model), lambda h, b: (b, 0)),
            pl.BlockSpec((slots, width), lambda h, b: (b, 0)),
            pl.BlockSpec((1,) + weights.shape[1:], lambda h, b: (h, 0, 0)),
            pl.BlockSpec((1, slots, 2 * width), lambda h, b: (h, b, 0)),
            pl.BlockSpec((1, slots, width), lambda h, b: (h, b, 0)),
            pl.BlockSpec((1, slots, width), lambda h, b: (h, b, 0)),
        ],
        out_specs=[
            pl.BlockSpec((1,) + weights.shape[1:], lambda h, b: (h, 0, 0)),
            pl.BlockSpec((rows, model), lambda h, b: (0, 0)),
        ],
        out_shape=[
            jax.ShapeDtypeStruct(weights.shape, low_type),
            jax.ShapeDtypeStruct((rows, model), low_type),
        ],
        scratch_shapes=[
            pltpu.VMEM(weights.shape[1:], wide),
            pltpu.VMEM((rows, model), wide),
        ],
        compiler_params=pltpu.CompilerParams(vmem_limit_bytes=48 * 1024 * 1024),
        cost_estimate=pl.CostEstimate(
            flops=2 * rows * model * heads * width * 6,
            bytes_accessed=heads * rows * width * 14 + weights.size * 4 + rows * model * 6,
            transcendentals=heads * rows * width * 6,
        ),
        name="mixer_backward",
    )(mix_in, res_low, position, weights, *saved)


def peer_x(chip):
    return chip + 1 - 2 * (chip % 2)


def peer_y(chip):
    return chip + 2 - 4 * (chip // 2)


def line_place(end, core):
    return end + core * (3 - 2 * end)


def remote(source, target, send, recv, member, z):
    return pltpu.make_async_remote_copy(
        src_ref=source,
        dst_ref=target,
        send_sem=send,
        recv_sem=recv,
        device_id=(member, z),
        device_id_type=pl.DeviceIdType.MESH,
    )


def enter(member, z):
    barrier = pltpu.get_barrier_semaphore()
    for other in range(8):

        @pl.when(member != other)
        def _():
            pl.semaphore_signal(
                barrier, inc=1, device_id=(other, z), device_id_type=pl.DeviceIdType.MESH
            )

    for other in range(4):

        @pl.when(z != other)
        def _():
            pl.semaphore_signal(
                barrier, inc=1, device_id=(member, other), device_id_type=pl.DeviceIdType.MESH
            )

    pl.semaphore_wait(barrier, 10)


class Gather:
    def __init__(self, own, target, send, recv, member, z):
        self.own, self.target = own, target
        self.send, self.recv = send, recv
        chip, core = member // 2, member % 2
        self.to_x = peer_x(chip) * 2 + core
        self.to_y = peer_y(chip) * 2 + core
        self.z = z
        self.half = own.shape[0] // 2

    def copy(self, number):
        low, high = pl.ds(0, self.half), pl.ds(self.half, self.half)
        source, target, to = (
            (self.own, self.target.at[1], self.to_x),
            (self.own, self.target.at[2], self.to_y),
            (self.target.at[1, low], self.target.at[3, low], self.to_y),
            (self.target.at[2, high], self.target.at[3, high], self.to_x),
        )[number]
        return remote(source, target, self.send.at[number], self.recv.at[number], to, self.z)

    def begin(self):
        self.copy(0).start()
        self.copy(1).start()

    def relay(self):
        self.copy(0).wait_recv()
        self.copy(2).start()
        self.copy(1).wait_recv()
        self.copy(3).start()

    def arrive(self):
        self.copy(2).wait_recv()
        self.copy(3).wait_recv()

    def finish(self):
        for number in range(4):
            self.copy(number).wait_send()


class Reduce:
    def __init__(self, part, from_x, from_y, passing, last, send, recv, member, z):
        self.part, self.from_x, self.from_y = part, from_x, from_y
        self.passing, self.last = passing, last
        self.send, self.recv = send, recv
        chip, core = member // 2, member % 2
        self.to_x = peer_x(chip) * 2 + core
        self.to_y = peer_y(chip) * 2 + core
        self.z = z
        self.slots = part.shape[0] // 4
        self.half = self.slots // 2

    def copy(self, number):
        slots, half = self.slots, self.half
        source, target, to = (
            (self.part.at[pl.ds(slots, half)], self.from_x.at[0], self.to_x),
            (self.part.at[pl.ds(3 * slots, half)], self.from_x.at[1], self.to_x),
            (self.part.at[pl.ds(2 * slots + half, half)], self.from_y.at[0], self.to_y),
            (self.part.at[pl.ds(3 * slots + half, half)], self.from_y.at[1], self.to_y),
            (self.passing.at[0], self.last.at[0], self.to_y),
            (self.passing.at[1], self.last.at[1], self.to_x),
        )[number]
        return remote(source, target, self.send.at[number], self.recv.at[number], to, self.z)

    def begin(self):
        for number in (1, 3, 0, 2):
            self.copy(number).start()

    def relay(self):
        slots, half = self.slots, self.half
        self.copy(1).wait_recv()
        self.passing[0] = (
            self.part[2 * slots : 2 * slots + half].astype(wide) + self.from_x[1].astype(wide)
        ).astype(low_type)
        self.copy(4).start()
        self.copy(3).wait_recv()
        self.passing[1] = (
            self.part[slots + half : 2 * slots].astype(wide) + self.from_y[1].astype(wide)
        ).astype(low_type)
        self.copy(5).start()

    def arrive(self):
        for number in (0, 2, 4, 5):
            self.copy(number).wait_recv()

    def result(self, number):
        direct = self.from_x if number == 0 else self.from_y
        return (
            self.part[number * self.half : (number + 1) * self.half].astype(wide)
            + direct[0].astype(wide)
            + self.last[number].astype(wide)
        )

    def finish(self):
        for number in range(6):
            self.copy(number).wait_send()

    @staticmethod
    def scratch(slots, model):
        return [pltpu.VMEM((2, slots // 2, model), low_type)] * 4


def norm_rows(value, gain):
    scale = lax.rsqrt(jnp.mean(value * value, axis=1, keepdims=True) + norm_eps)
    return value * scale * gain


def front_kernel(
    sizes,
    tokens_ref,
    cot_ref,
    gain_ref,
    small_ref,
    in_ref,
    gate_ref,
    out_ref,
    up_ref,
    down_ref,
    mix_in,
    weights,
    ffn_weights,
    saved_p,
    saved_state,
    saved_low,
    starts_out,
    residual_out,
    ffn_in,
    cot_out,
    gains_out,
    tokens_all,
    raw_in,
    raw_up,
    raw_down,
    turned,
    gain_seen,
    acc,
    part,
    from_x,
    from_y,
    passing,
    last,
    load_sem,
    gain_send,
    gain_recv,
    m_send,
    m_recv,
    m_core_send,
    m_core_recv,
    f_send,
    f_recv,
    f_core_send,
    f_core_recv,
    g_send,
    g_recv,
    r_send,
    r_recv,
):
    model, width, ffn_width = sizes
    member = lax.axis_index("dp")
    z = lax.axis_index("shard")
    chip, core = member // 2, member % 2
    end = z + core * (3 - 2 * z)
    other = chip * 2 + 1 - core
    slots = cot_ref.shape[0]
    half_ffn = ffn_width // 2
    owner = core == z // 2

    window = 128 * ((chip * ffn_width) // 128)
    skew = chip * ffn_width - window
    quarter = pl.ds(pl.multiple_of(chip * width, width), width)
    wide_window = pl.ds(pl.multiple_of(window, 128), raw_up.shape[2])

    def loads():
        found = [
            (out_ref.at[quarter], weights.at[end, pl.ds(2 * width, width), pl.ds(0, model)]),
            (
                small_ref.at[:, quarter],
                weights.at[end, pl.ds(2 * width, 16), pl.ds(model, width)],
            ),
        ]
        for kind in range(2):
            found.append((in_ref.at[kind, :, quarter], raw_in.at[kind]))
            found.append(
                (
                    gate_ref.at[kind, chip],
                    weights.at[end, pl.ds(kind * width, width), pl.ds(model, width)],
                )
            )
        found.append(
            (down_ref.at[pl.ds(pl.multiple_of(chip * ffn_width, 32), ffn_width)], raw_down)
        )
        for kind in range(2):
            found.append((up_ref.at[kind, :, wide_window], raw_up.at[kind]))
        return [
            pltpu.make_async_copy(source, target, load_sem.at[number])
            for number, (source, target) in enumerate(found)
        ]

    def turned_copy(kind):
        return pltpu.make_async_copy(
            raw_down
            if kind == 2
            else turned.at[kind, pl.ds(pl.multiple_of(skew, 32), ffn_width)],
            ffn_weights.at[kind, pl.ds(pl.multiple_of(2 * end * ffn_width, 32), ffn_width)],
            load_sem.at[9 + kind],
        )

    @pl.when(owner)
    def _():
        for copy in loads():
            copy.start()

    enter(member, z)

    gather_tokens = Gather(tokens_ref, tokens_all, g_send.at[0], g_recv.at[0], member, z)
    gather_cot = Gather(cot_ref, cot_out, g_send.at[1], g_recv.at[1], member, z)
    gather_ffn = Gather(ffn_in.at[0], ffn_in, g_send.at[2], g_recv.at[2], member, z)
    reduce = Reduce(part, from_x, from_y, passing, last, r_send, r_recv, member, z)
    own_cot = pltpu.make_async_copy(cot_ref, cot_out.at[0], load_sem.at[12])

    gather_tokens.begin()
    own_cot.start()

    def gain_copy(to, slot):
        return remote(
            gain_ref, gain_seen.at[slot], gain_send.at[to], gain_recv.at[slot], member, to
        )

    for to in range(4):

        @pl.when(to != z)
        def _():
            gain_copy(to, z).start()

    gain_seen[z] = gain_ref[...]

    def m_rows(number):
        return pl.ds(number * width, width)

    def m_copy(slot, number, way, to_end):
        place = weights.at[slot, m_rows(number)]
        return remote(
            place,
            place,
            m_send.at[way, slot, number],
            m_recv.at[slot, number],
            member,
            line_place(to_end, core),
        )

    def m_core(slot, number):
        return remote(
            weights.at[slot, m_rows(number)],
            weights.at[2 + slot, m_rows(number)],
            m_core_send.at[slot, number],
            m_core_recv.at[slot, number],
            other,
            z,
        )

    def f_place(slot, number):
        row = ((slot % 2) * 2 + slot // 2) * ffn_width + (number % 2) * half_ffn
        return ffn_weights.at[number // 2, pl.ds(row, half_ffn)]

    def f_copy(slot, number, way, to_end):
        place = f_place(slot, number)
        return remote(
            place,
            place,
            f_send.at[way, slot, number],
            f_recv.at[slot, number],
            member,
            line_place(to_end, core),
        )

    def f_core(slot, number):
        return remote(
            f_place(slot, number),
            f_place(2 + slot, number),
            f_core_send.at[slot, number],
            f_core_recv.at[slot, number],
            other,
            z,
        )

    def pass_on(copy, core_copy, slot, number):
        if slot == 0:

            @pl.when(end < 3)
            def _():
                copy(slot, number, 0, end + 1).start()
        else:

            @pl.when((end == 1) | (end == 2))
            def _():
                copy(slot, number, 0, end + 1).start()

        core_copy(slot, number).start()

    def pass_back(copy, numbers):
        @pl.when(end == 1)
        def _():
            for number in numbers:
                copy(1, number, 1, 0).start()

    def start_own(copy, core_copy, numbers):
        for slot in range(2):

            @pl.when(end == slot)
            def _():
                for number in numbers:
                    pass_on(copy, core_copy, slot, number)

    def turn_in(kind):
        @pl.when(owner)
        def _():
            for copy in loads()[2 + 2 * kind : 4 + 2 * kind]:
                copy.wait()

            def turn(at, carry):
                columns = pl.ds(pl.multiple_of(at * 256, 256), 256)
                weights[end, kind * width : (kind + 1) * width, columns] = raw_in[
                    kind, columns, :
                ].T
                return carry

            lax.fori_loop(0, model // 256, turn, 0)

        start_own(m_copy, m_core, (kind,))
        pass_back(m_copy, (kind,))

    def turn_up(kind):
        @pl.when(owner)
        def _():
            loads()[7 + kind].wait()

            def turn(at, carry):
                columns = pl.ds(pl.multiple_of(at * 256, 256), 256)
                turned[kind, :, columns] = raw_up[kind, columns, :].T
                return carry

            lax.fori_loop(0, model // 256, turn, 0)
            turned_copy(kind).start()

    @pl.when(owner)
    def _():
        for copy in loads()[:2]:
            copy.wait()
        for row in range(2 * width + 16, 3 * width, 16):
            weights[end, row : row + 16, model:] = jnp.zeros((16, width), low_type)

    start_own(m_copy, m_core, (2,))
    pass_back(m_copy, (2,))
    turn_in(0)
    turn_in(1)

    @pl.when(owner)
    def _():
        loads()[6].wait()
        turned_copy(2).start()

    turn_up(0)
    turn_up(1)
    gather_tokens.relay()
    m_order = (2, 0, 1)

    @pl.when(end < 3)
    def _():
        for number in m_order:
            for slot in (1, 0):

                @pl.when(end != slot)
                def _():
                    m_copy(slot, number, 0, 0).wait_recv()
                    pass_on(m_copy, m_core, slot, number)

    @pl.when(owner)
    def _():
        for kind in range(3):
            turned_copy(kind).wait()

    f_order = (4, 5, 0, 1, 2, 3)
    start_own(f_copy, f_core, f_order)

    def f_pass(slot, numbers):
        for number in numbers:
            f_copy(slot, number, 0, 0).wait_recv()
            pass_on(f_copy, f_core, slot, number)

    def f_step(step):
        @pl.when(end == 1)
        def _():
            f_pass(0, ((), (4, 5), (0, 1), (2, 3), (), ())[step])

        @pl.when(end == 2)
        def _():
            f_pass(1, ((4,), (5, 0), (1, 2), (3,), (), ())[step])
            f_pass(0, ((), (), (), (4,), (5, 0), (1, 2, 3))[step])

        if step == 0:
            pass_back(f_copy, f_order)

        @pl.when(end == 0)
        def _():
            f_pass(1, ((), (), (), (), (), f_order)[step])

    for to in range(4):

        @pl.when(to != z)
        def _():
            gain_copy(to, to).wait_recv()

    gains = jnp.concatenate([gain_seen[at].astype(wide) for at in range(4)], axis=1)
    gains_out[...] = gains[0:8]
    gather_tokens.arrive()

    def norm_block(block):
        if block == 0:
            source, starts = tokens_ref[:, :model], tokens_ref[:, model:]
        else:
            source, starts = tokens_all[block, :, :model], tokens_all[block, :, model:]
        at = slice(block * slots, (block + 1) * slots)
        mix_in[at, :] = norm_rows(source.astype(wide), gains_out[0:1]).astype(low_type)
        starts_out[at, :] = starts

    for block in range(4):
        norm_block(block)
    gather_cot.begin()
    f_step(0)

    late = end >= 2
    for turn in range(4):
        head = (turn + 2 * late) % 4
        if turn == 2:

            @pl.when(end == 3)
            def _():
                for number in m_order:
                    for slot in (1, 0):
                        m_copy(slot, number, 0, 0).wait_recv()
                        m_core(slot, number).start()

        @pl.when(head >= 2)
        def _():
            for number in m_order:
                m_core(head - 2, number).wait_recv()

        views = weight_views(weights.at[pl.ds(head, 1)], width)

        def step_block(block, carry):
            rows = pl.ds(pl.multiple_of(block * slots, slots), slots)
            position = slot_position(starts_out[rows, :])
            projected, states, mixed_low, product = mixer_step(
                mix_in[rows, :], position, views, width
            )
            saved_p[head, rows, :] = projected
            saved_state[head, rows, :] = states
            saved_low[head, rows, :] = mixed_low
            if turn == 0:
                acc[rows, :] = product
            elif turn < 3:
                acc[rows, :] += product
            else:
                part[rows, :] = (acc[rows, :] + product).astype(low_type)
            return carry

        lax.fori_loop(0, 4, step_block, 0)
        if turn == 3:
            reduce.begin()
        f_step(turn + 1)
        if turn == 0:
            gather_cot.relay()

    reduce.relay()
    f_step(5)
    reduce.arrive()
    half = slots // 2
    for number in range(2):
        at = slice(number * half, (number + 1) * half)
        residual = tokens_ref[at, :model].astype(wide) + reduce.result(number)
        residual_out[at, :] = residual
        ffn_in[0, at, :] = norm_rows(residual, gains_out[1:2]).astype(low_type)
    gather_ffn.begin()
    gather_ffn.relay()

    @pl.when(end == 3)
    def _():
        for slot in (1, 0):
            for number in f_order:
                f_copy(slot, number, 0, 0).wait_recv()
                f_core(slot, number).start()

    gather_ffn.arrive()
    gather_cot.arrive()
    own_cot.wait()
    for slot in range(2):
        for number in range(6):
            f_core(slot, number).wait_recv()

    for gather in (gather_tokens, gather_cot, gather_ffn, reduce):
        gather.finish()
    for to in range(4):

        @pl.when(to != z)
        def _():
            gain_copy(to, z).wait_send()

    for copy, core_copy, count in ((m_copy, m_core, 3), (f_copy, f_core, 6)):
        for number in range(count):
            for slot in range(2):
                core_copy(slot, number).wait_send()

            @pl.when(end < 3)
            def _():
                copy(0, number, 0, 0).wait_send()

            @pl.when((end == 1) | (end == 2))
            def _():
                copy(1, number, 0, 0).wait_send()

            @pl.when(end == 1)
            def _():
                copy(1, number, 1, 0).wait_send()


def front(tokens, cot, gains, small, in_proj, gates, out_proj, gate_up, down, sizes):
    model, width, ffn_width = sizes
    slots = cot.shape[0]
    rows = 4 * slots
    dma = pltpu.SemaphoreType.DMA
    vmem = pl.BlockSpec(memory_space=pltpu.VMEM)
    anywhere = pl.BlockSpec(memory_space=pl.ANY)
    window = -(-ffn_width // 128) * 128
    return pl.pallas_call(
        functools.partial(front_kernel, sizes),
        in_specs=[vmem] * 3 + [anywhere] * 6,
        out_specs=[vmem, vmem, anywhere, vmem, vmem, vmem, vmem, vmem, vmem, anywhere, vmem],
        out_shape=[
            jax.ShapeDtypeStruct((rows, model), low_type),
            jax.ShapeDtypeStruct((4, 3 * width, model + width), low_type),
            jax.ShapeDtypeStruct((3, 4 * ffn_width, model), low_type),
            jax.ShapeDtypeStruct((4, rows, 2 * width), wide),
            jax.ShapeDtypeStruct((4, rows, width), wide),
            jax.ShapeDtypeStruct((4, rows, width), low_type),
            jax.ShapeDtypeStruct((rows, width), low_type),
            jax.ShapeDtypeStruct((slots, model), wide),
            jax.ShapeDtypeStruct((4, slots, model), low_type),
            jax.ShapeDtypeStruct((4, slots, model), low_type),
            jax.ShapeDtypeStruct((8, model), wide),
        ],
        scratch_shapes=[
            pltpu.VMEM((4, slots, model + width), low_type),
            pltpu.VMEM((2, model, width), low_type),
            pltpu.VMEM((2, model, window), low_type),
            pltpu.VMEM((ffn_width, model), low_type),
            pltpu.VMEM((2, window, model), low_type),
            pltpu.VMEM((4, 16, model // 4), low_type),
            pltpu.VMEM((rows, model), wide),
            pltpu.VMEM((rows, model), low_type),
        ]
        + Reduce.scratch(slots, model)
        + [
            dma((13,)),
            dma((4,)),
            dma((4,)),
            dma((2, 2, 3)),
            dma((2, 3)),
            dma((2, 3)),
            dma((2, 3)),
            dma((2, 2, 6)),
            dma((2, 6)),
            dma((2, 6)),
            dma((2, 6)),
            dma((3, 4)),
            dma((3, 4)),
            dma((6,)),
            dma((6,)),
        ],
        compiler_params=pltpu.CompilerParams(
            collective_id=3, has_side_effects=True, vmem_limit_bytes=60 * 1024 * 1024
        ),
        cost_estimate=pl.CostEstimate(
            flops=2 * rows * model * 4 * width * 3,
            bytes_accessed=6 * ffn_width * 4 * model,
            transcendentals=rows * 4 * width * 6,
        ),
        name="front",
    )(tokens, cot, gains, small, in_proj, gates, out_proj, gate_up, down)


def middle_kernel(
    sizes,
    x_ref,
    go_ref,
    weights_ref,
    residual_ref,
    gain_ref,
    mask_ref,
    total,
    res_low,
    res_out,
    gain_out,
    block_out,
    held,
    lows,
    paired,
    arrived,
    part_in,
    part_out,
    in_x,
    in_y,
    in_pass,
    in_last,
    load_sem,
    core_send,
    core_recv,
    line_send,
    line_recv,
    i_send,
    i_recv,
    o_send,
    o_recv,
    g_send,
    g_recv,
):
    model, ffn_width = sizes
    member = lax.axis_index("dp")
    z = lax.axis_index("shard")
    chip, core = member // 2, member % 2
    end = z + core * (3 - 2 * z)
    other = chip * 2 + 1 - core
    slots = residual_ref.shape[0]
    half = slots // 2
    hidden = 4 * ffn_width
    half_ffn = ffn_width // 2

    loads = [
        pltpu.make_async_copy(weights_ref.at[kind], held.at[kind], load_sem.at[kind])
        for kind in range(3)
    ]
    for load in loads:
        load.start()
    enter(member, z)
    for load in loads:
        load.wait()

    split = -(-2 * ffn_width // 128) * 128

    def block_step(low, high, block, carry):
        rows = pl.ds(pl.multiple_of(block * slots, slots), slots)
        x = x_ref[rows, :]
        grad_out = go_ref[rows, :]
        pre_gate = dot_rows(x, held[0, low:high])
        pre_up = dot_rows(x, held[1, low:high])
        active, slope = gelu_parts(pre_gate)
        ffn_low = (active * pre_up).astype(low_type)
        grad_act = dot_rows(grad_out, held[2, low:high])
        gate_low = (grad_act * pre_up * slope).astype(low_type)
        up_low = (grad_act * active).astype(low_type)
        sum_out = dot_plain(ffn_low, held[2, low:high])
        sum_in = dot_plain(gate_low, held[0, low:high]) + dot_plain(up_low, held[1, low:high])
        lows[0, rows, low:high] = gate_low
        lows[1, rows, low:high] = up_low
        lows[2, rows, low:high] = ffn_low
        if low > 0:
            sum_in = sum_in + part_in[rows, :].astype(wide)
            sum_out = sum_out + part_out[rows, :].astype(wide)
        part_in[rows, :] = sum_in.astype(low_type)
        part_out[rows, :] = sum_out.astype(low_type)
        return carry

    reduce_in = Reduce(part_in, in_x, in_y, in_pass, in_last, i_send, i_recv, member, z)
    reduce_out = Reduce(
        part_out,
        in_x.at[pl.ds(2, 2)],
        in_y.at[pl.ds(2, 2)],
        in_pass.at[pl.ds(2, 2)],
        in_last.at[pl.ds(2, 2)],
        o_send,
        o_recv,
        member,
        z,
    )
    gather = Gather(res_low.at[0], res_low, g_send, g_recv, member, z)
    middle = model // 2

    def weight_grads(kind, low, high):
        factor = go_ref if kind == 2 else x_ref
        for at in range(2):
            columns = slice(at * middle, (at + 1) * middle)
            held[kind, low:high, columns] = dot_slots(
                lows[kind, :, low:high], factor[:, columns]
            ).astype(low_type)

    def core_copy(slot, kind):
        return remote(
            held.at[kind, pl.ds((2 * slot + 1) * ffn_width, ffn_width)],
            paired.at[slot, kind],
            core_send.at[slot, kind],
            core_recv.at[slot, kind],
            other,
            z,
        )

    def chunk(number):
        return number // 2, pl.ds((number % 2) * half_ffn, half_ffn)

    def line_copy(kind, number, to_end):
        at, rows = chunk(number)
        return remote(
            paired.at[min(kind, 1), at, rows],
            arrived.at[kind, at, rows],
            line_send.at[kind, number],
            line_recv.at[kind, number],
            member,
            line_place(to_end, core),
        )

    def pair_up(slot, kind):
        core_copy(slot, kind).wait_recv()
        for number in (2 * kind, 2 * kind + 1):
            at, rows = chunk(number)
            own = held[at, pl.ds(2 * slot * ffn_width + (number % 2) * half_ffn, half_ffn)]
            paired[slot, at, rows] = add_low(own, paired[slot, at, rows])

            @pl.when(end == 3)
            def _():
                line_copy(slot, number, 2).start()

            if slot == 1:

                @pl.when(end == 0)
                def _():
                    line_copy(2, number, 1).start()

    def part_grads(slot, low, high):
        for kind in range(3):
            weight_grads(kind, low, high)
            core_copy(slot, kind).start()
            if kind > 0:
                pair_up(slot, kind - 1)
        pair_up(slot, 2)

    def summed(slot, kinds, number):
        at, rows = chunk(number)
        result = paired[slot, at, rows].astype(wide)
        for kind in kinds:
            result = result + arrived[kind, at, rows].astype(wide)
        return result.astype(low_type)

    def outer_step(number):
        at, rows = chunk(number)

        @pl.when((end == 2) | (end == 1))
        def _():
            line_copy(0, number, 0).wait_recv()
            paired[0, at, rows] = summed(0, (0,), number)
            line_copy(0, number, end - 1).start()

    def inner_step(number):
        at, rows = chunk(number)

        @pl.when(end == 2)
        def _():
            line_copy(1, number, 0).wait_recv()
            paired[1, at, rows] = summed(1, (1,), number)
            line_copy(1, number, 1).start()

    def out_copy(slot, number):
        at, rows = chunk(number)
        return pltpu.make_async_copy(
            paired.at[slot, at, rows], total.at[at, rows], load_sem.at[number]
        )

    def last_step(number):
        at, rows = chunk(number)

        @pl.when(end == 1)
        def _():
            line_copy(1, number, 0).wait_recv()
            line_copy(2, number, 0).wait_recv()
            paired[1, at, rows] = summed(1, (1, 2), number)
            out_copy(1, number).start()

        @pl.when(end == 0)
        def _():
            line_copy(0, number, 0).wait_recv()
            paired[0, at, rows] = summed(0, (0,), number)
            out_copy(0, number).start()

    lax.fori_loop(0, 4, functools.partial(block_step, 0, split), 0)
    part_grads(0, 0, split)
    lax.fori_loop(0, 4, functools.partial(block_step, split, hidden), 0)
    reduce_in.begin()
    part_grads(1, split, hidden)
    for number in range(3):
        outer_step(number)
    reduce_in.relay()
    for number in range(3, 6):
        outer_step(number)

    reduce_in.arrive()
    gain = gain_ref[1:2]
    gain_sum = jnp.zeros((1, model), wide)
    for number in range(2):
        at = slice(number * half, (number + 1) * half)
        grad = reduce_in.result(number)
        value = residual_ref[at]
        scale = lax.rsqrt(jnp.mean(value * value, axis=1, keepdims=True) + norm_eps)
        scaled = grad * gain
        gain_sum = gain_sum + jnp.sum(grad * value * scale, axis=0, keepdims=True)
        inner = jnp.mean(scaled * value, axis=1, keepdims=True)
        back = scale * scaled - value * (scale * scale * scale * inner)
        result = go_ref[at].astype(wide) + back
        res_out[at] = result
        res_low[0, at] = result.astype(low_type)
    gain_out[...] = jnp.concatenate([gain_ref[0:1], gain_sum, jnp.zeros((6, model), wide)], axis=0)
    gather.begin()
    inner_step(0)
    gather.relay()
    inner_step(1)
    inner_step(2)
    gather.arrive()
    reduce_out.begin()
    inner_step(3)
    inner_step(4)
    reduce_out.relay()
    inner_step(5)
    for number in range(6):
        last_step(number)
    reduce_out.arrive()
    live = mask_ref[:, 0:1].astype(wide)
    for number in range(2):
        at = slice(number * half, (number + 1) * half)
        block_out[at] = (live[at] * (residual_ref[at] + reduce_out.result(number))).astype(low_type)

    for sent in (reduce_in, reduce_out, gather):
        sent.finish()
    for slot in range(2):
        for kind in range(3):
            core_copy(slot, kind).wait_send()
    for number in range(6):

        @pl.when(end > 0)
        def _():
            line_copy(0, number, 0).wait_send()

        @pl.when(end > 1)
        def _():
            line_copy(1, number, 0).wait_send()

        @pl.when(end == 0)
        def _():
            line_copy(2, number, 1).wait_send()

        @pl.when(end < 2)
        def _():
            out_copy(0, number).wait()


def middle(x, grad_out, weights, residual, gains, mask):
    rows, model = x.shape
    hidden = weights.shape[1]
    ffn_width = hidden // 4
    slots = rows // 4
    dma = pltpu.SemaphoreType.DMA
    vmem = pl.BlockSpec(memory_space=pltpu.VMEM)
    anywhere = pl.BlockSpec(memory_space=pl.ANY)
    quarter = (3, ffn_width, model)
    return pl.pallas_call(
        functools.partial(middle_kernel, (model, ffn_width)),
        in_specs=[vmem, vmem, anywhere, vmem, vmem, vmem],
        out_specs=[anywhere] + [vmem] * 4,
        out_shape=[
            jax.ShapeDtypeStruct(quarter, low_type),
            jax.ShapeDtypeStruct((4, slots, model), low_type),
            jax.ShapeDtypeStruct((slots, model), wide),
            jax.ShapeDtypeStruct((8, model), wide),
            jax.ShapeDtypeStruct((slots, model), low_type),
        ],
        scratch_shapes=[
            pltpu.VMEM(weights.shape, low_type),
            pltpu.VMEM((3, rows, hidden), low_type),
            pltpu.VMEM((2,) + quarter, low_type),
            pltpu.VMEM((3,) + quarter, low_type),
            pltpu.VMEM((rows, model), low_type),
            pltpu.VMEM((rows, model), low_type),
        ]
        + [pltpu.VMEM((4, slots // 2, model), low_type)] * 4
        + [
            dma((6,)),
            dma((2, 3)),
            dma((2, 3)),
            dma((3, 6)),
            dma((3, 6)),
            dma((6,)),
            dma((6,)),
            dma((6,)),
            dma((6,)),
            dma((4,)),
            dma((4,)),
        ],
        compiler_params=pltpu.CompilerParams(
            collective_id=4, has_side_effects=True, vmem_limit_bytes=63 * 1024 * 1024
        ),
        cost_estimate=pl.CostEstimate(
            flops=2 * rows * model * hidden * 9,
            bytes_accessed=weights.size * 4 + rows * model * 16,
            transcendentals=rows * hidden,
        ),
        name="middle",
    )(x, grad_out, weights, residual, gains, mask)


class Scatter:
    def __init__(self, sizes, member, z, send_sem, recv_sem):
        self.model, self.width, self.ffn_width, self.piece_length = sizes
        self.member, self.z = member, z
        self.chip, self.core = member // 2, member % 2
        self.owner = self.core == z // 2
        self.send_sem, self.recv_sem = send_sem, recv_sem
        self.across = self.model // 128
        rec, ffn, model = 4 * self.width, 4 * self.ffn_width, self.model
        self.gate_base = 2 * model * rec
        self.out_base = self.gate_base + 8 * self.width * self.width
        self.up_base = self.out_base + rec * model
        self.down_base = self.up_base + 2 * model * ffn
        self.rec, self.ffn = rec, ffn
        self.first_in = 0
        self.first_gate = 2 * self.across
        self.first_out = self.first_gate + 2
        self.first_small = self.first_out + 4
        self.first_up = self.first_small + 1
        self.first_down = self.first_up + 2 * self.across
        self.count = self.first_down + 6

    def in_unit(self, number, q):
        kind, at = number // self.across, number % self.across
        low = (kind * self.model + at * 128) * self.rec
        where = (
            pl.ds(pl.multiple_of(kind * self.width, self.width), self.width),
            pl.ds(pl.multiple_of(at * 128, 128), 128),
        )
        return self.first_in + number, where, low, low + 128 * self.rec

    def gate_unit(self, kind, q):
        low = self.gate_base + (kind * 4 + q) * self.width * self.width
        where = (
            pl.ds(pl.multiple_of(kind * self.width, self.width), self.width),
            pl.ds(self.model, self.width),
        )
        return self.first_gate + kind, where, low, low + self.width * self.width

    def out_unit(self, number, q):
        rows = self.width // 4
        low = self.out_base + (q * self.width + number * rows) * self.model
        where = (
            pl.ds(pl.multiple_of(2 * self.width + number * rows, rows), rows),
            pl.ds(0, self.model),
        )
        return self.first_out + number, where, low, low + rows * self.model

    def up_unit(self, number, q):
        kind, at = number // self.across, number % self.across
        low = self.up_base + (kind * self.model + at * 128) * self.ffn
        where = (kind, pl.ds(0, self.ffn_width), pl.ds(pl.multiple_of(at * 128, 128), 128))
        return self.first_up + number, where, low, low + 128 * self.ffn

    def down_unit(self, number, q):
        rows = self.ffn_width // 6
        low = self.down_base + (q * self.ffn_width + number * rows) * self.model
        where = (2, pl.ds(pl.multiple_of(number * rows, 16), rows), pl.ds(0, self.model))
        return self.first_down + number, where, low, low + rows * self.model

    def small_where(self):
        return (pl.ds(2 * self.width, 16), pl.ds(self.model, self.width))

    def copies(self, unit, source, target, q, act):
        number, where, low, high = unit
        first = low // self.piece_length
        last = (high - 1) // self.piece_length
        for which, to in ((0, first), (1, last)):
            wanted = True if which == 0 else last != first

            @pl.when((to != self.member) & wanted)
            def _():
                act(
                    remote(
                        source.at[where],
                        target.at[(q,) + where],
                        self.send_sem.at[which, number],
                        self.recv_sem.at[q, number],
                        to,
                        self.z,
                    ),
                    True,
                )

            @pl.when((to == self.member) & wanted)
            def _():
                act(
                    pltpu.make_async_copy(
                        source.at[where], target.at[(q,) + where], self.recv_sem.at[q, number]
                    ),
                    False,
                )

    def each(self, unit_of, low, high, source, target, act):
        def body(number, carry):
            self.copies(unit_of(number, self.chip), source, target, self.chip, act)
            return carry

        lax.fori_loop(low, high, body, 0)

    def smalls(self, source, target, act):
        where = self.small_where()
        for to in range(8):

            @pl.when(self.member != to)
            def _():
                act(
                    remote(
                        source.at[where],
                        target.at[(self.chip,) + where],
                        self.send_sem.at[2, to],
                        self.recv_sem.at[self.chip, self.first_small],
                        to,
                        self.z,
                    ),
                    True,
                )

        act(
            pltpu.make_async_copy(
                source.at[where],
                target.at[(self.chip,) + where],
                self.recv_sem.at[self.chip, self.first_small],
            ),
            False,
        )

    def arrivals(self, unit_of, count, source, target):
        low = self.member * self.piece_length

        def body(number, carry):
            for q in range(4):
                index, where, first, last = unit_of(number, q)
                mine = (first < low + self.piece_length) & (last > low)
                here = (self.chip == q) & self.owner

                @pl.when(mine & here)
                def _():
                    pltpu.make_async_copy(
                        source.at[where], target.at[(q,) + where], self.recv_sem.at[q, index]
                    ).wait()

                @pl.when(mine & jnp.logical_not(here))
                def _():
                    remote(
                        source.at[where],
                        target.at[(q,) + where],
                        self.send_sem.at[0, index],
                        self.recv_sem.at[q, index],
                        self.member,
                        self.z,
                    ).wait_recv()

            return carry

        lax.fori_loop(0, count, body, 0)

    def small_arrivals(self, source, target):
        where = self.small_where()
        for q in range(4):
            here = (self.chip == q) & self.owner

            @pl.when(here)
            def _():
                pltpu.make_async_copy(
                    source.at[where],
                    target.at[(q,) + where],
                    self.recv_sem.at[q, self.first_small],
                ).wait()

            @pl.when(jnp.logical_not(here))
            def _():
                remote(
                    source.at[where],
                    target.at[(q,) + where],
                    self.send_sem.at[2, 0],
                    self.recv_sem.at[q, self.first_small],
                    self.member,
                    self.z,
                ).wait_recv()


def begin(copy, is_remote):
    copy.start()


def finish_send(copy, is_remote):
    if is_remote:
        copy.wait_send()


def sums_kernel(
    sizes,
    mix_ref,
    part_ref,
    ffn_ref,
    tokens_ref,
    res_ref,
    gain_ref,
    mix_out,
    ffn_out,
    tokens_out,
    gain_out,
    paired,
    arrived,
    total,
    from_x,
    from_y,
    passing,
    last,
    gain_part,
    gain_plane,
    gain_line,
    gain_seen,
    core_send,
    core_recv,
    line_send,
    line_recv,
    plane_send,
    plane_recv,
    gain_send,
    gain_recv,
    unit_send,
    unit_recv,
):
    model, width, ffn_width, piece_length = sizes
    member = lax.axis_index("dp")
    z = lax.axis_index("shard")
    chip, core = member // 2, member % 2
    end = z + core * (3 - 2 * z)
    slots = tokens_ref.shape[0]
    half = slots // 2
    to_x = peer_x(chip) * 2 + core
    to_y = peer_y(chip) * 2 + core
    other = chip * 2 + 1 - core
    scatter = Scatter(sizes, member, z, unit_send, unit_recv)
    enter(member, z)

    def rows(number):
        return pl.ds(number * width, width)

    def core_copy(slot, number):
        return remote(
            mix_ref.at[2 + slot, rows(number)],
            paired.at[slot, rows(number)],
            core_send.at[slot, number],
            core_recv.at[slot, number],
            other,
            z,
        )

    for slot in range(2):
        for number in range(3):
            core_copy(slot, number).start()

    def plane_copy(number):
        source, target, to = (
            (part_ref.at[pl.ds(slots, half)], from_x.at[0], to_x),
            (part_ref.at[pl.ds(3 * slots, half)], from_x.at[1], to_x),
            (part_ref.at[pl.ds(2 * slots + half, half)], from_y.at[0], to_y),
            (part_ref.at[pl.ds(3 * slots + half, half)], from_y.at[1], to_y),
            (passing.at[0], last.at[0], to_y),
            (passing.at[1], last.at[1], to_x),
        )[number]
        return remote(source, target, plane_send.at[number], plane_recv.at[number], to, z)

    for number in (1, 3, 0, 2):
        plane_copy(number).start()

    @pl.when(scatter.owner)
    def _():
        scatter.each(scatter.up_unit, 0, 2 * scatter.across, ffn_ref, ffn_out, begin)
        scatter.each(scatter.down_unit, 0, 6, ffn_ref, ffn_out, begin)

    def line_copy(kind, number, source, to_end):
        return remote(
            source,
            arrived.at[kind, rows(number)],
            line_send.at[kind, number],
            line_recv.at[kind, number],
            member,
            line_place(to_end, core),
        )

    for slot in range(2):
        for number in range(3):
            core_copy(slot, number).wait_recv()
            both = mix_ref[slot, rows(number)].astype(wide) + paired[slot, rows(number)].astype(wide)
            paired[slot, rows(number)] = both.astype(low_type)

            @pl.when(end == 3)
            def _():
                line_copy(slot, number, paired.at[slot, rows(number)], 2).start()

            if slot == 1:

                @pl.when(end == 0)
                def _():
                    line_copy(2, number, paired.at[slot, rows(number)], 1).start()

    plane_copy(1).wait_recv()
    passing[0] = (
        part_ref[2 * slots : 2 * slots + half].astype(wide) + from_x[1].astype(wide)
    ).astype(low_type)
    plane_copy(4).start()
    plane_copy(3).wait_recv()
    passing[1] = (
        part_ref[slots + half : 2 * slots].astype(wide) + from_y[1].astype(wide)
    ).astype(low_type)
    plane_copy(5).start()

    def summed(slot, kinds, number):
        result = paired[slot, rows(number)].astype(wide)
        for kind in kinds:
            result = result + arrived[kind, rows(number)].astype(wide)
        return result.astype(low_type)

    def on_arrival(kind, number):
        line_copy(kind, number, paired.at[0, rows(number)], 0).wait_recv()

    def share(number):
        if number < 2:
            across = scatter.across
            scatter.each(
                scatter.in_unit, number * across, (number + 1) * across, total, mix_out, begin
            )
            scatter.each(scatter.gate_unit, number, number + 1, total, mix_out, begin)
        else:
            scatter.each(scatter.out_unit, 0, 4, total, mix_out, begin)
            scatter.smalls(total, mix_out, begin)

    for number in range(3):

        @pl.when((end == 2) | (end == 1))
        def _():
            on_arrival(0, number)
            paired[0, rows(number)] = summed(0, (0,), number)

        @pl.when(end == 2)
        def _():
            line_copy(0, number, paired.at[0, rows(number)], 1).start()

        @pl.when(end == 1)
        def _():
            line_copy(0, number, paired.at[0, rows(number)], 0).start()

    for number in range(3):

        @pl.when(end == 2)
        def _():
            on_arrival(1, number)
            paired[1, rows(number)] = summed(1, (1,), number)
            line_copy(1, number, paired.at[1, rows(number)], 1).start()

        @pl.when(end == 1)
        def _():
            on_arrival(1, number)
            on_arrival(2, number)
            total[rows(number)] = summed(1, (1, 2), number)

        @pl.when(end == 0)
        def _():
            on_arrival(0, number)
            total[rows(number)] = summed(0, (0,), number)

        @pl.when(scatter.owner)
        def _():
            share(number)

    plane_copy(0).wait_recv()
    plane_copy(2).wait_recv()
    plane_copy(4).wait_recv()
    plane_copy(5).wait_recv()
    gain = gain_ref[0:1]
    gain_sum = jnp.zeros((1, model), wide)
    for number, direct in ((0, from_x), (1, from_y)):
        at = slice(number * half, (number + 1) * half)
        grad = part_ref[at].astype(wide) + direct[0].astype(wide) + last[number].astype(wide)
        value = tokens_ref[at].astype(wide)
        scale = lax.rsqrt(jnp.mean(value * value, axis=1, keepdims=True) + norm_eps)
        scaled = grad * gain
        gain_sum = gain_sum + jnp.sum(grad * value * scale, axis=0, keepdims=True)
        inner = jnp.mean(scaled * value, axis=1, keepdims=True)
        back = scale * scaled - value * (scale * scale * scale * inner)
        tokens_out[at] = (res_ref[at] + back).astype(low_type)
    gain_part[...] = jnp.concatenate([gain_sum, gain_ref[1:2], jnp.zeros((6, model), wide)], axis=0)

    def gain_copy():
        return remote(
            gain_part, gain_plane.at[member], gain_send.at[0], gain_recv.at[member], 7, z
        )

    @pl.when(member != 7)
    def _():
        gain_copy().start()
        gain_copy().wait_send()
        gain_out[...] = jnp.zeros_like(gain_out)

    @pl.when(member == 7)
    def _():
        result = gain_part[...]
        for source in range(7):
            remote(
                gain_part,
                gain_plane.at[source],
                gain_send.at[0],
                gain_recv.at[source],
                7,
                z,
            ).wait_recv()
            result = result + gain_plane[source]
        quarter = model // 4
        for place in range(4):
            gain_line[place] = result[:, place * quarter : (place + 1) * quarter]

        def line_gain(place, slot):
            return remote(
                gain_line.at[place],
                gain_seen.at[slot],
                gain_send.at[1 + place],
                gain_recv.at[8 + slot],
                7,
                place,
            )

        for place in range(4):

            @pl.when(place != z)
            def _():
                line_gain(place, z).start()

        gain_out[...] = gain_line[z]
        for place in range(4):

            @pl.when(place != z)
            def _():
                line_gain(place, place).wait_recv()
                gain_out[...] += gain_seen[place]
                line_gain(place, z).wait_send()

    across = scatter.across
    scatter.arrivals(scatter.up_unit, 2 * across, ffn_ref, ffn_out)
    scatter.arrivals(scatter.down_unit, 6, ffn_ref, ffn_out)
    scatter.arrivals(scatter.in_unit, 2 * across, total, mix_out)
    scatter.arrivals(scatter.gate_unit, 2, total, mix_out)
    scatter.arrivals(scatter.out_unit, 4, total, mix_out)
    scatter.small_arrivals(total, mix_out)

    @pl.when(scatter.owner)
    def _():
        scatter.each(scatter.up_unit, 0, 2 * across, ffn_ref, ffn_out, finish_send)
        scatter.each(scatter.down_unit, 0, 6, ffn_ref, ffn_out, finish_send)
        scatter.each(scatter.in_unit, 0, 2 * across, total, mix_out, finish_send)
        scatter.each(scatter.gate_unit, 0, 2, total, mix_out, finish_send)
        scatter.each(scatter.out_unit, 0, 4, total, mix_out, finish_send)
        scatter.smalls(total, mix_out, finish_send)

    for number in range(6):
        plane_copy(number).wait_send()
    for slot in range(2):
        for number in range(3):
            core_copy(slot, number).wait_send()
    for number in range(3):

        @pl.when(end > 0)
        def _():
            line_copy(0, number, paired.at[0, rows(number)], 0).wait_send()

        @pl.when(end > 1)
        def _():
            line_copy(1, number, paired.at[1, rows(number)], 0).wait_send()

        @pl.when(end == 0)
        def _():
            line_copy(2, number, paired.at[1, rows(number)], 1).wait_send()


def sums(mix, part, ffn, tokens, residual_grad, gains, piece_length, width):
    model = tokens.shape[1]
    ffn_width = ffn.shape[1]
    sizes = (model, width, ffn_width, piece_length)
    half = tokens.shape[0] // 2
    block = mix.shape[1:]
    count = Scatter(sizes, 0, 0, None, None).count
    dma = pltpu.SemaphoreType.DMA
    vmem = pl.BlockSpec(memory_space=pltpu.VMEM)
    anywhere = pl.BlockSpec(memory_space=pl.ANY)
    return pl.pallas_call(
        functools.partial(sums_kernel, sizes),
        in_specs=[vmem, vmem, anywhere, vmem, vmem, vmem],
        out_specs=[anywhere, anywhere, vmem, vmem],
        out_shape=[
            jax.ShapeDtypeStruct(mix.shape, low_type),
            jax.ShapeDtypeStruct((4,) + ffn.shape, low_type),
            jax.ShapeDtypeStruct(tokens.shape, low_type),
            jax.ShapeDtypeStruct((8, model // 4), wide),
        ],
        scratch_shapes=[
            pltpu.VMEM((2,) + block, low_type),
            pltpu.VMEM((3,) + block, low_type),
            pltpu.VMEM(block, low_type),
            pltpu.VMEM((2, half, model), low_type),
            pltpu.VMEM((2, half, model), low_type),
            pltpu.VMEM((2, half, model), low_type),
            pltpu.VMEM((2, half, model), low_type),
            pltpu.VMEM((8, model), wide),
            pltpu.VMEM((8, 8, model), wide),
            pltpu.VMEM((4, 8, model // 4), wide),
            pltpu.VMEM((4, 8, model // 4), wide),
            dma((2, 3)),
            dma((2, 3)),
            dma((3, 3)),
            dma((3, 3)),
            dma((6,)),
            dma((6,)),
            dma((5,)),
            dma((12,)),
            dma((3, count)),
            dma((4, count)),
        ],
        compiler_params=pltpu.CompilerParams(
            collective_id=2, has_side_effects=True, vmem_limit_bytes=40 * 1024 * 1024
        ),
        cost_estimate=pl.CostEstimate(
            flops=mix.size * 4, bytes_accessed=mix.size * 8, transcendentals=0
        ),
        name="sums",
    )(mix, part, ffn, tokens, residual_grad, gains)


def tail_kernel(
    sizes,
    mix_ref,
    ffn_ref,
    gain_ref,
    master_ref,
    first_ref,
    second_ref,
    piece_ref,
    new_master_ref,
    new_first_ref,
    new_second_ref,
    weights_ref,
    bias_ref,
    grad,
    held,
    spread,
    send_sem,
    recv_sem,
):
    model, width, ffn_width, piece_length, chunks, lines, margin = sizes
    member = lax.axis_index("dp")
    z = lax.axis_index("shard")
    step = pl.program_id(0)
    lead = 128
    start_row = (member * piece_length) // lead
    offset = (member * piece_length) % lead
    tiles_in = 4 * width // lead
    tiles_ffn = 4 * ffn_width // lead
    tiles_model = model // lead

    def copy_to(origin, chunk, side, to):
        return pltpu.make_async_remote_copy(
            src_ref=held.at[origin, chunk],
            dst_ref=held.at[origin, chunk],
            send_sem=send_sem.at[side, origin, chunk],
            recv_sem=recv_sem.at[origin, chunk],
            device_id=(member, to),
            device_id_type=pl.DeviceIdType.MESH,
        )

    @pl.when(step == 0)
    def _():
        barrier = pltpu.get_barrier_semaphore()

        @pl.when(z > 0)
        def _():
            pl.semaphore_signal(
                barrier, inc=1, device_id=(member, z - 1), device_id_type=pl.DeviceIdType.MESH
            )

        @pl.when(z < 3)
        def _():
            pl.semaphore_signal(
                barrier, inc=1, device_id=(member, z + 1), device_id_type=pl.DeviceIdType.MESH
            )

        @pl.when((z == 0) | (z == 3))
        def _():
            pl.semaphore_wait(barrier, 1)

        @pl.when((z > 0) & (z < 3))
        def _():
            pl.semaphore_wait(barrier, 2)

        def clear(number, carry):
            grad[pl.ds(pl.multiple_of(number * 256, 256), 256), :] = jnp.zeros((256, lead), wide)
            return carry

        lax.fori_loop(0, grad.shape[0] // 256, clear, 0)

        def place(row, count, body):
            low = member * piece_length

            @pl.when((row * lead < low + piece_length) & ((row + count) * lead > low))
            def _():
                body(row - start_row + margin)

        base = 0

        def in_unit(number, carry):
            kind = number // tiles_model
            at = number % tiles_model

            def body(to):
                for q in range(4):
                    tile = mix_ref[
                        q,
                        pl.ds(pl.multiple_of(kind * width, width), width),
                        pl.ds(pl.multiple_of(at * lead, lead), lead),
                    ].astype(wide)
                    grad[pl.ds(to + q, lead, stride=tiles_in), :] = tile.T

            place((kind * model + at * lead) * tiles_in, lead * tiles_in, body)
            return carry

        lax.fori_loop(0, 2 * tiles_model, in_unit, 0)
        base = 2 * model * tiles_in

        def gate_body(number, carry):
            kind = number // 4
            q = number % 4

            def body(to):
                grad[pl.ds(to, width), :] = mix_ref[
                    q, pl.ds(pl.multiple_of(kind * width, width), width), model:
                ].astype(wide)

            place(2 * model * tiles_in + number * width, width, body)
            return carry

        lax.fori_loop(0, 8, gate_body, 0)
        base = base + 8 * width
        out_base = base

        quarter = width // 4

        def out_unit(number, carry):
            q = number // 4
            part = number % 4

            def body(to):
                for at in range(tiles_model):
                    grad[pl.ds(to + at, quarter, stride=tiles_model), :] = mix_ref[
                        q,
                        pl.ds(pl.multiple_of(2 * width + part * quarter, quarter), quarter),
                        at * lead : (at + 1) * lead,
                    ].astype(wide)

            place(out_base + number * quarter * tiles_model, quarter * tiles_model, body)
            return carry

        lax.fori_loop(0, 16, out_unit, 0)
        base = base + 4 * width * tiles_model
        up_base = base

        def up_unit(number, carry):
            kind = number // tiles_model
            at = number % tiles_model
            columns = pl.ds(pl.multiple_of(at * lead, lead), lead)

            def body(to):
                for tile in range(tiles_ffn):
                    found = []
                    row = tile * lead
                    while row < (tile + 1) * lead:
                        q = row // ffn_width
                        last = min((q + 1) * ffn_width, (tile + 1) * lead)
                        found.append(
                            ffn_ref[
                                q,
                                kind,
                                row - q * ffn_width : last - q * ffn_width,
                                columns,
                            ].astype(wide)
                        )
                        row = last
                    block = found[0] if len(found) == 1 else jnp.concatenate(found, axis=0)
                    grad[pl.ds(to + tile, lead, stride=tiles_ffn), :] = block.T

            place(up_base + (kind * model + at * lead) * tiles_ffn, lead * tiles_ffn, body)
            return carry

        lax.fori_loop(0, 2 * tiles_model, up_unit, 0)
        base = base + 2 * model * tiles_ffn
        down_base = base
        sixth = ffn_width // 6

        def down_unit(number, carry):
            q = number // 6
            part = number % 6

            def body(to):
                for at in range(tiles_model):
                    grad[pl.ds(to + at, sixth, stride=tiles_model), :] = ffn_ref[
                        q,
                        2,
                        pl.ds(pl.multiple_of(part * sixth, 16), sixth),
                        at * lead : (at + 1) * lead,
                    ].astype(wide)

            place(down_base + number * sixth * tiles_model, sixth * tiles_model, body)
            return carry

        lax.fori_loop(0, 24, down_unit, 0)
        small_base = base + 4 * ffn_width * tiles_model
        smalls = [
            mix_ref[q, 2 * width : 2 * width + 16, model:].astype(wide)
            for q in range(4)
        ]

        def small_body(to):
            for q in range(4):
                grad[pl.ds(to + q, 8, stride=tiles_in), :] = smalls[q][:8]
            for number in range(6):
                kind, at = number // 3, number % 3
                grad[pl.ds(to + 8 * tiles_in + number, 1), :] = gain_ref[
                    kind : kind + 1, at * lead : (at + 1) * lead
                ]

        place(small_base, 8 * tiles_in + 6, small_body)
        bias_ref[...] = jnp.concatenate([small[5:7] for small in smalls], axis=1)

    @pl.when(step < chunks)
    def _():
        row = margin + step * lines
        shift = (lead - offset) % lead
        here = pltpu.roll(grad[pl.ds(row, lines), :], shift, 1)
        after = pltpu.roll(grad[pl.ds(row + 1, lines), :], shift, 1)
        lane = lax.broadcasted_iota(jnp.int32, (lines, lead), 1)
        piece = jnp.where(lane < lead - offset, here, after).reshape(1, lines * lead)
        piece_ref[...] = piece
        new_first = beta_one * first_ref[...] + (1.0 - beta_one) * piece
        new_second = beta_two * second_ref[...] + (1.0 - beta_two) * piece * piece
        master = master_ref[...]
        new_master = master - learn_rate * (
            new_first / corr_one / (jnp.sqrt(new_second / corr_two) + adam_eps)
            + weight_decay * master
        )
        new_first_ref[...] = new_first
        new_second_ref[...] = new_second
        new_master_ref[...] = new_master
        held[z, step] = new_master.reshape(lines, lead).astype(low_type)

        @pl.when(z < 3)
        def _():
            copy_to(z, step, 0, z + 1).start()

        @pl.when(z > 0)
        def _():
            copy_to(z, step, 1, z - 1).start()

    def pass_on(origin, chunk, right):
        copy_to(origin, chunk, 0, z).wait_recv()
        if right:

            @pl.when(z < 3)
            def _():
                copy_to(origin, chunk, 0, z + 1).start()
        else:

            @pl.when(z > 0)
            def _():
                copy_to(origin, chunk, 1, z - 1).start()

    @pl.when((step >= chunks) & (step < 2 * chunks))
    def _():
        chunk = step - chunks

        @pl.when(z > 0)
        def _():
            pass_on(z - 1, chunk, True)

        @pl.when(z < 3)
        def _():
            pass_on(z + 1, chunk, False)

    @pl.when(step >= 2 * chunks)
    def _():
        chunk = step - 2 * chunks

        @pl.when(z >= 2)
        def _():
            pass_on(z - 2, chunk, True)

        @pl.when(z <= 1)
        def _():
            pass_on(z + 2, chunk, False)

        @pl.when(z == 3)
        def _():
            copy_to(0, chunk, 0, z).wait_recv()

        @pl.when(z == 0)
        def _():
            copy_to(3, chunk, 0, z).wait_recv()

        for origin in range(4):
            spread[origin * lines : (origin + 1) * lines, :] = held[origin, chunk].astype(wide)

        def line(number, carry):
            weights_ref[:, pl.ds(pl.multiple_of(number * lead, lead), lead)] = spread[
                pl.ds(number, 4, stride=lines), :
            ].astype(low_type)
            return carry

        lax.fori_loop(0, lines, line, 0, unroll=8)

    @pl.when(step == 3 * chunks - 1)
    def _():
        for origin in range(4):

            def finish(chunk, carry):
                @pl.when((origin <= z) & (z < 3))
                def _():
                    copy_to(origin, chunk, 0, z).wait_send()

                @pl.when((origin >= z) & (z > 0))
                def _():
                    copy_to(origin, chunk, 1, z).wait_send()

                return carry

            lax.fori_loop(0, chunks, finish, 0)


def tail(mix, ffn, gains, master, first, second, sizes):
    model, width, ffn_width = sizes
    piece_length = master.shape[1]
    chunks = 8
    lines = -(-piece_length // (chunks * 128 * 16)) * 16
    block = lines * 128
    margin = 1536
    rows = -(-(2 * margin + chunks * lines + 8) // 256) * 256
    packed = jax.ShapeDtypeStruct(master.shape, wide)
    whole = lambda shape: pl.BlockSpec(shape, lambda s: (0,) * len(shape))
    chunk_spec = pl.BlockSpec((1, block), lambda s: (0, jnp.minimum(s, chunks - 1)))
    once = lambda shape: pl.BlockSpec(
        shape, lambda s: (0,) * len(shape), pipeline_mode=pl.Buffered(1)
    )
    return pl.pallas_call(
        functools.partial(
            tail_kernel, (model, width, ffn_width, piece_length, chunks, lines, margin)
        ),
        grid=(3 * chunks,),
        in_specs=[once(mix.shape), once(ffn.shape), once(gains.shape)] + [chunk_spec] * 3,
        out_specs=[chunk_spec] * 4
        + [
            pl.BlockSpec((4, block), lambda s: (0, jnp.maximum(s - 2 * chunks, 0))),
            whole((2, 4 * width)),
        ],
        out_shape=[packed] * 4
        + [
            jax.ShapeDtypeStruct((4, piece_length), low_type),
            jax.ShapeDtypeStruct((2, 4 * width), wide),
        ],
        scratch_shapes=[
            pltpu.VMEM((rows, 128), wide),
            pltpu.VMEM((4, chunks, lines, 128), low_type),
            pltpu.VMEM((4 * lines, 128), wide),
            pltpu.SemaphoreType.DMA((2, 4, chunks)),
            pltpu.SemaphoreType.DMA((4, chunks)),
        ],
        compiler_params=pltpu.CompilerParams(
            collective_id=1, has_side_effects=True, vmem_limit_bytes=58 * 1024 * 1024
        ),
        cost_estimate=pl.CostEstimate(
            flops=20 * piece_length,
            bytes_accessed=40 * piece_length,
            transcendentals=piece_length,
        ),
        name="tail",
    )(mix, ffn, gains, master, first, second)


def group_body(
    tokens,
    cotangent,
    seq_start,
    live_mask,
    input_proj,
    gate_blocks,
    output_proj,
    ffn_gate_up,
    ffn_down,
    conv_taps,
    gate_bias,
    decay_param,
    norm_gains,
    master_shard,
    first_moment,
    second_moment,
):
    slots, model = tokens.shape
    slice_rec = input_proj.shape[2]
    slice_ffn = ffn_down.shape[0]
    width = slice_rec // 4
    ffn_width = slice_ffn // 4
    piece_length = master_shard.shape[1]
    member = lax.axis_index("dp")
    chip = member // 2
    core = member % 2
    z = lax.axis_index("shard")
    end = jnp.where(core == 0, z, 3 - z)

    mask_rows = live_mask.astype(wide)[:, None]
    stream = tokens.astype(wide)
    grad_stream = cotangent.astype(wide) * mask_rows

    starts = jnp.broadcast_to(seq_start.astype(low_type)[:, None], (slots, width))
    (
        mix_in,
        mix_weights,
        ffn_weights,
        saved_p,
        saved_state,
        saved_low,
        all_starts,
        residual,
        ffn_in,
        all_grad_out,
        gains,
    ) = front(
        jnp.concatenate([tokens, starts], axis=1),
        grad_stream.astype(low_type),
        jnp.concatenate([norm_gains, jnp.zeros((14, norm_gains.shape[1]), low_type)]),
        jnp.concatenate(
            [conv_taps, gate_bias, decay_param[None], jnp.zeros((8, slice_rec), low_type)]
        ),
        input_proj,
        gate_blocks,
        output_proj,
        ffn_gate_up,
        ffn_down,
        (model, width, ffn_width),
    )
    saved = (saved_p, saved_state, saved_low)
    ffn_in = ffn_in.reshape(4 * slots, model)
    all_grad_out = all_grad_out.reshape(4 * slots, model)
    sum_ffn, res_low, grad_residual, gain_sums, block_out = middle(
        ffn_in,
        all_grad_out,
        ffn_weights,
        residual,
        gains,
        jnp.broadcast_to(mask_rows.astype(low_type), (slots, width)),
    )
    res_low = res_low.reshape(4 * slots, model)
    grad_mix, mix_in_part = mix_backward(
        mix_in, res_low, all_starts, mix_weights, saved, slots, width
    )
    four_mix, four_ffn, tokens_grad, gain_total = sums(
        grad_mix,
        mix_in_part,
        sum_ffn,
        tokens,
        grad_residual,
        gain_sums,
        piece_length,
        width,
    )
    piece, new_master, new_first, new_second, new_weights, bias_total = tail(
        four_mix,
        four_ffn,
        gain_total,
        master_shard,
        first_moment,
        second_moment,
        (model, width, ffn_width),
    )
    return (
        block_out,
        tokens_grad,
        piece,
        new_master,
        new_first,
        new_second,
        new_weights,
        bias_total,
    )


def rms_scale(values, gain):
    return values * lax.rsqrt(jnp.mean(values * values, axis=-1, keepdims=True) + norm_eps) * gain


def conv_mix(signal, taps, position):
    result = taps[-1] + taps[0] * signal
    for shift_by in range(1, taps.shape[0] - 1):
        moved = jnp.pad(signal, ((shift_by, 0), (0, 0)))[:-shift_by]
        result = result + taps[shift_by] * jnp.where((position >= shift_by)[:, None], moved, 0.0)
    return result


def combine_steps(earlier, later):
    decay_first, value_first = earlier
    decay_second, value_second = later
    return (decay_first * decay_second, decay_second * value_first + value_second)


def recurrence(logits, signal, branch, bias_term, decay_term, position):
    row_count = signal.shape[0]
    recur_gate = jax.nn.sigmoid(logits[0].reshape(row_count, -1) + bias_term[0])
    input_gate = jax.nn.sigmoid(logits[1].reshape(row_count, -1) + bias_term[1])
    log_decay = -gate_scale * recur_gate * jax.nn.softplus(-decay_term)
    decay_rate = jnp.where((position > 0)[:, None], jnp.exp(log_decay), 0.0)
    drive_term = jnp.sqrt(-jnp.expm1(2.0 * log_decay)) * input_gate * signal
    states = lax.associative_scan(combine_steps, (decay_rate, drive_term), axis=0)[1]
    return states * jax.nn.gelu(branch)


def gated_gelu(ffn_pre):
    return jax.nn.gelu(ffn_pre[0]) * ffn_pre[1]


def mixer_forward(
    mix_in, input_proj, gate_blocks, output_proj, conv_taps, gate_bias, decay_param, position
):
    projected = jnp.einsum("sd,kdr->ksr", mix_in, input_proj, preferred_element_type=jnp.float32)
    conv_out, conv_pull = jax.vjp(
        lambda signal, taps: conv_mix(signal, taps, position), projected[0], conv_taps
    )
    row_count = conv_out.shape[0]
    conv_low = conv_out.astype(jnp.bfloat16).reshape(
        row_count, gate_blocks.shape[1], gate_blocks.shape[2]
    )
    gate_logits = jnp.einsum(
        "shb,khbc->kshc", conv_low, gate_blocks, preferred_element_type=jnp.float32
    )
    mixed, mix_pull = jax.vjp(
        lambda logits, signal, branch, bias_term, decay_term: recurrence(
            logits, signal, branch, bias_term, decay_term, position
        ),
        gate_logits,
        conv_out,
        projected[1],
        gate_bias,
        decay_param,
    )
    mixed_low = mixed.astype(jnp.bfloat16)
    partial_out = jnp.dot(mixed_low, output_proj, preferred_element_type=jnp.float32)
    return (partial_out, (conv_pull, conv_low, mix_pull, mixed_low))


def mixer_backward(grad_out_low, mix_in, saved, input_proj, gate_blocks, output_proj):
    conv_pull, conv_low, mix_pull, mixed_low = saved
    grad_output_proj = jnp.einsum(
        "sr,sd->rd", mixed_low, grad_out_low, preferred_element_type=jnp.float32
    )
    grad_mixed = jnp.einsum(
        "sd,rd->sr", grad_out_low, output_proj, preferred_element_type=jnp.float32
    )
    grad_logits, grad_conv_direct, grad_branch, grad_bias, grad_decay = mix_pull(grad_mixed)
    logits_low = grad_logits.astype(jnp.bfloat16)
    grad_blocks = jnp.einsum(
        "shb,kshc->khbc", conv_low, logits_low, preferred_element_type=jnp.float32
    )
    grad_conv_gates = jnp.einsum(
        "kshc,khbc->shb", logits_low, gate_blocks, preferred_element_type=jnp.float32
    )
    grad_signal, grad_taps = conv_pull(
        grad_conv_direct + grad_conv_gates.reshape(grad_conv_direct.shape)
    )
    proj_low = jnp.stack([grad_signal, grad_branch]).astype(jnp.bfloat16)
    grad_input_proj = jnp.einsum(
        "sd,ksr->kdr", mix_in, proj_low, preferred_element_type=jnp.float32
    )
    grad_mix_in = jnp.einsum(
        "ksr,kdr->sd", proj_low, input_proj, preferred_element_type=jnp.float32
    )
    return (
        grad_mix_in,
        (grad_input_proj, grad_blocks, grad_output_proj, grad_taps, grad_bias, grad_decay),
    )


def ffn_forward(ffn_in_low, ffn_gate_up, ffn_down):
    ffn_pre = jnp.einsum("sd,kdf->ksf", ffn_in_low, ffn_gate_up, preferred_element_type=jnp.float32)
    ffn_act, ffn_pull = jax.vjp(gated_gelu, ffn_pre)
    ffn_low = ffn_act.astype(jnp.bfloat16)
    partial_ffn = jnp.dot(ffn_low, ffn_down, preferred_element_type=jnp.float32)
    return (partial_ffn, (ffn_pull, ffn_low))


def ffn_backward(grad_low, ffn_in_low, saved, ffn_gate_up, ffn_down):
    ffn_pull, ffn_low = saved
    grad_down = jnp.einsum("sf,sd->fd", ffn_low, grad_low, preferred_element_type=jnp.float32)
    grad_act = jnp.einsum("sd,fd->sf", grad_low, ffn_down, preferred_element_type=jnp.float32)
    grad_pre = ffn_pull(grad_act)[0]
    pre_low = grad_pre.astype(jnp.bfloat16)
    grad_gate_up = jnp.einsum(
        "sd,ksf->kdf", ffn_in_low, pre_low, preferred_element_type=jnp.float32
    )
    grad_ffn_in = jnp.einsum(
        "ksf,kdf->sd", pre_low, ffn_gate_up, preferred_element_type=jnp.float32
    )
    return (grad_ffn_in, grad_gate_up, grad_down)


def body(
    tokens,
    cotangent,
    seq_start,
    live_mask,
    input_proj,
    gate_blocks,
    output_proj,
    ffn_gate_up,
    ffn_down,
    conv_taps,
    gate_bias,
    decay_param,
    norm_gains,
    master_shard,
    first_moment,
    second_moment,
):
    slot_count = tokens.shape[0]
    position = jnp.arange(slot_count, dtype=jnp.int32) - seq_start
    mask_rows = live_mask.astype(jnp.float32)[:, None]
    stream = tokens.astype(jnp.float32)
    grad_stream = cotangent.astype(jnp.float32) * mask_rows
    shards = (
        input_proj,
        gate_blocks,
        output_proj,
        ffn_gate_up,
        ffn_down,
        conv_taps,
        gate_bias,
        decay_param,
        norm_gains,
    )
    (
        full_in,
        full_blocks,
        full_out,
        full_up,
        full_down,
        full_taps,
        full_bias,
        full_decay,
        full_gains,
    ) = (
        lax.all_gather(shards[0], "shard", axis=2, tiled=True),
        lax.all_gather(shards[1], "shard", axis=1, tiled=True),
        lax.all_gather(shards[2], "shard", axis=0, tiled=True),
        lax.all_gather(shards[3], "shard", axis=2, tiled=True),
        lax.all_gather(shards[4], "shard", axis=0, tiled=True),
        lax.all_gather(shards[5], "shard", axis=1, tiled=True),
        lax.all_gather(shards[6], "shard", axis=1, tiled=True),
        lax.all_gather(shards[7], "shard", axis=0, tiled=True),
        lax.all_gather(shards[8], "shard", axis=1, tiled=True),
    )
    gains = full_gains.astype(jnp.float32)
    normed, norm_pull = jax.vjp(rms_scale, stream, gains[0])
    mix_in = normed.astype(jnp.bfloat16)
    mix_out, mix_saved = mixer_forward(
        mix_in,
        full_in,
        full_blocks,
        full_out,
        full_taps.astype(jnp.float32),
        full_bias.astype(jnp.float32),
        full_decay.astype(jnp.float32),
        position,
    )
    residual = stream + mix_out
    normed_two, second_pull = jax.vjp(rms_scale, residual, gains[1])
    ffn_in_low = normed_two.astype(jnp.bfloat16)
    ffn_result, ffn_saved = ffn_forward(ffn_in_low, full_up, full_down)
    block_out = (mask_rows * (residual + ffn_result)).astype(jnp.bfloat16)
    grad_ffn_in, grad_up, grad_down = ffn_backward(
        grad_stream.astype(jnp.bfloat16), ffn_in_low, ffn_saved, full_up, full_down
    )
    grad_norm_two, grad_gain_two = second_pull(grad_ffn_in)
    grad_residual = grad_stream + grad_norm_two
    grad_mix_in, mix_grads = mixer_backward(
        grad_residual.astype(jnp.bfloat16), mix_in, mix_saved, full_in, full_blocks, full_out
    )
    grad_norm_one, grad_gain_one = norm_pull(grad_mix_in)
    tokens_grad = (grad_residual + grad_norm_one).astype(jnp.bfloat16)
    grads = (
        mix_grads[0],
        mix_grads[1],
        mix_grads[2],
        grad_up,
        grad_down,
        mix_grads[3],
        mix_grads[4],
        mix_grads[5],
        jnp.stack([grad_gain_one, grad_gain_two]),
    )
    summed = (
        lax.psum_scatter(
            grads[0].astype(jnp.bfloat16), "shard", scatter_dimension=2, tiled=True
        ).astype(jnp.float32),
        lax.psum_scatter(
            grads[1].astype(jnp.bfloat16), "shard", scatter_dimension=1, tiled=True
        ).astype(jnp.float32),
        lax.psum_scatter(
            grads[2].astype(jnp.bfloat16), "shard", scatter_dimension=0, tiled=True
        ).astype(jnp.float32),
        lax.psum_scatter(
            grads[3].astype(jnp.bfloat16), "shard", scatter_dimension=2, tiled=True
        ).astype(jnp.float32),
        lax.psum_scatter(
            grads[4].astype(jnp.bfloat16), "shard", scatter_dimension=0, tiled=True
        ).astype(jnp.float32),
        lax.psum_scatter(
            grads[5].astype(jnp.bfloat16), "shard", scatter_dimension=1, tiled=True
        ).astype(jnp.float32),
        lax.psum_scatter(
            grads[6].astype(jnp.bfloat16), "shard", scatter_dimension=1, tiled=True
        ).astype(jnp.float32),
        lax.psum_scatter(
            grads[7].astype(jnp.bfloat16), "shard", scatter_dimension=0, tiled=True
        ).astype(jnp.float32),
        lax.psum_scatter(
            grads[8].astype(jnp.bfloat16), "shard", scatter_dimension=1, tiled=True
        ).astype(jnp.float32),
    )
    flat = jnp.concatenate([member.reshape(1, -1) for member in summed], axis=1)
    piece = lax.psum_scatter(flat, "dp", scatter_dimension=1, tiled=True)
    bias_total = lax.psum(summed[6], "dp")
    new_first = beta_one * first_moment + (1.0 - beta_one) * piece
    new_second = beta_two * second_moment + (1.0 - beta_two) * piece * piece
    new_master = master_shard - learn_rate * (
        new_first / corr_one / (jnp.sqrt(new_second / corr_two) + adam_eps)
        + weight_decay * master_shard
    )
    new_weights = lax.all_gather(new_master.astype(jnp.bfloat16), "shard", axis=0, tiled=True)
    return (
        block_out,
        tokens_grad,
        piece,
        new_master,
        new_first,
        new_second,
        new_weights,
        bias_total,
    )


def solution(mesh):
    fits = mesh.shape["dp"] == 8 and mesh.shape["shard"] == 4
    placed = (
        P(("dp", "shard"), None),
        P(("dp", "shard"), None),
        P(("dp", "shard")),
        P(("dp", "shard")),
        P(None, None, "shard"),
        P(None, "shard", None, None),
        P("shard", None),
        P(None, None, "shard"),
        P("shard", None),
        P(None, "shard"),
        P(None, "shard"),
        P("shard"),
        P(None, "shard"),
        P("shard", "dp"),
        P("shard", "dp"),
        P("shard", "dp"),
    )
    return jax.shard_map(
        group_body if fits else body,
        mesh=mesh,
        in_specs=placed,
        out_specs=(
            P(("dp", "shard"), None),
            P(("dp", "shard"), None),
            P("shard", "dp"),
            P("shard", "dp"),
            P("shard", "dp"),
            P("shard", "dp"),
            P(None, "dp"),
            P(None, "shard"),
        ),
        check_vma=False,
    )
```

```python
import functools
import jax
import jax.numpy as jnp
from jax import lax
from jax.experimental import pallas as pl
from jax.experimental.pallas import tpu as pltpu
from jax.sharding import PartitionSpec as P

norm_eps = 1e-06
gate_scale = 8.0
beta_one = 0.9
beta_two = 0.95
learn_rate = 0.01
weight_decay = 0.1
adam_eps = 1e-08
corr_one = 1.0 - beta_one**10.0
corr_two = 1.0 - beta_two**10.0
low_type = jnp.bfloat16
wide = jnp.float32
gelu_scale = 0.7978845608028654
gelu_cube = 0.044715


def add_low(left, right):
    return (left.astype(wide) + right.astype(wide)).astype(low_type)


def dot_rows(left, right):
    return lax.dot_general(left, right, (((1,), (1,)), ((), ())), preferred_element_type=wide)


def dot_plain(left, right):
    return lax.dot_general(left, right, (((1,), (0,)), ((), ())), preferred_element_type=wide)


def dot_slots(left, right):
    return lax.dot_general(left, right, (((0,), (0,)), ((), ())), preferred_element_type=wide)


def gelu_parts(value):
    square = value * value
    bent = jnp.tanh(gelu_scale * value * (1.0 + gelu_cube * square))
    half = 0.5 * (1.0 + bent)
    slope = half + 0.5 * value * (1.0 - bent * bent) * gelu_scale * (
        1.0 + 3.0 * gelu_cube * square
    )
    return (value * half, slope)


def shift_down(value, step):
    if step % 8 == 0:
        return jnp.concatenate([value[-step:], value[:-step]], axis=0)
    return pltpu.roll(value, step, 0)


def shift_up(value, step):
    if step % 8 == 0:
        return jnp.concatenate([value[step:], value[:step]], axis=0)
    return pltpu.roll(value, value.shape[0] - step, 0)


def scan_slots(decay, value, shift):
    step = 1
    while step < value.shape[0]:
        value = value + decay * shift(value, step)
        if 2 * step < value.shape[0]:
            decay = decay * shift(decay, step)
        step *= 2
    return value


def one_minus_exp(value):
    series = jnp.ones_like(value)
    for number in range(11, 1, -1):
        series = 1.0 - value * (1.0 / number) * series
    return jnp.where(value < 0.8, value * series, 1.0 - jnp.exp(-value))


def soft_plus(value):
    return jnp.maximum(value, 0.0) + jnp.log1p(jnp.exp(-jnp.abs(value)))


def mixer_parts(first, position, small, gates):
    conv_out = small[4:5] + small[0:1] * first
    shifted = []
    for step in range(1, 4):
        moved = jnp.where(position >= step, shift_down(first, step), 0.0)
        shifted.append(moved)
        conv_out = conv_out + small[step : step + 1] * moved
    conv_low = conv_out.astype(low_type)
    logits = dot_plain(conv_low, gates)
    width = first.shape[1]
    recur_gate = jax.nn.sigmoid(logits[:, :width] + small[5:6])
    input_gate = jax.nn.sigmoid(logits[:, width:] + small[6:7])
    rate = gate_scale * soft_plus(-small[7:8])
    log_decay = -rate * recur_gate
    decay = jnp.where(position > 0, jnp.exp(log_decay), 0.0)
    gone = one_minus_exp(-2.0 * log_decay)
    root = jnp.sqrt(gone)
    return conv_out, shifted, conv_low, recur_gate, input_gate, rate, decay, gone, root


def weight_views(w_ref, width):
    model = w_ref.shape[2] - width
    proj = w_ref[0, 0 : 2 * width, 0:model]
    out = w_ref[0, 2 * width : 3 * width, 0:model]
    gates = jnp.concatenate(
        [w_ref[0, 0:width, model:], w_ref[0, width : 2 * width, model:]], axis=1
    )
    small = w_ref[0, 2 * width : 2 * width + 16, model:].astype(wide)
    return proj, out, gates, small


def slot_position(starts):
    slot = lax.broadcasted_iota(jnp.int32, (starts.shape[0], 1), 0)
    return slot - starts[:, 0:1].astype(wide).astype(jnp.int32)


def mixer_step(x, position, views, width):
    proj, out, gates, small = views
    projected = dot_rows(x, proj)
    conv_out, _, _, _, input_gate, _, decay, _, root = mixer_parts(
        projected[:, :width], position, small, gates
    )
    states = scan_slots(decay, root * input_gate * conv_out, shift_down)
    mixed_low = (states * gelu_parts(projected[:, width:])[0]).astype(low_type)
    return projected, states, mixed_low, dot_plain(mixed_low, out)


def mixer_back_step(position, views, projected, states, res_low, width):
    _, out, gates, small = views
    first = projected[:, :width]
    conv_out, shifted, conv_low, recur_gate, input_gate, rate, decay, gone, root = mixer_parts(
        first, position, small, gates
    )
    grad_mixed = dot_rows(res_low, out)
    active, slope = gelu_parts(projected[:, width:])
    grad_second = grad_mixed * states * slope
    adjoint = scan_slots(shift_up(decay, 1), grad_mixed * active, shift_up)
    grad_decay = adjoint * shift_down(states, 1)
    gated = adjoint * conv_out
    grad_root = gated * input_gate
    grad_input_gate = gated * root
    grad_conv = adjoint * root * input_gate
    grad_log = grad_decay * decay - grad_root * (1.0 - gone) / root
    grad_recur = -rate * grad_log
    grad_logit_a = grad_recur * recur_gate * (1.0 - recur_gate)
    grad_logit_b = grad_input_gate * input_gate * (1.0 - input_gate)
    grad_param = jnp.sum(grad_log * recur_gate, axis=0, keepdims=True) * (
        gate_scale * jax.nn.sigmoid(-small[7:8])
    )
    logits_low = jnp.concatenate([grad_logit_a, grad_logit_b], axis=1).astype(low_type)
    grad_conv = grad_conv + dot_rows(logits_low, gates)
    grad_gates = dot_slots(conv_low, logits_low)
    sums = [jnp.sum(grad_conv * first, axis=0, keepdims=True)]
    grad_first = small[0:1] * grad_conv
    for step in range(1, 4):
        sums.append(jnp.sum(grad_conv * shifted[step - 1], axis=0, keepdims=True))
        kept = jnp.where(position >= step, grad_conv, 0.0)
        grad_first = grad_first + small[step : step + 1] * shift_up(kept, step)
    sums.append(jnp.sum(grad_conv, axis=0, keepdims=True))
    sums.append(jnp.sum(grad_logit_a, axis=0, keepdims=True))
    sums.append(jnp.sum(grad_logit_b, axis=0, keepdims=True))
    sums.append(grad_param)
    proj_low = jnp.concatenate([grad_first, grad_second], axis=1).astype(low_type)
    return proj_low, grad_gates, jnp.concatenate(sums, axis=0)


def peer_x(chip):
    return chip + 1 - 2 * (chip % 2)


def peer_y(chip):
    return chip + 2 - 4 * (chip // 2)


def line_place(end, core):
    return end + core * (3 - 2 * end)


def remote(source, target, send, recv, member, z):
    return pltpu.make_async_remote_copy(
        src_ref=source,
        dst_ref=target,
        send_sem=send,
        recv_sem=recv,
        device_id=(member, z),
        device_id_type=pl.DeviceIdType.MESH,
    )


def enter(member, z):
    barrier = pltpu.get_barrier_semaphore()
    for other in range(8):

        @pl.when(member != other)
        def _():
            pl.semaphore_signal(
                barrier, inc=1, device_id=(other, z), device_id_type=pl.DeviceIdType.MESH
            )

    for other in range(4):

        @pl.when(z != other)
        def _():
            pl.semaphore_signal(
                barrier, inc=1, device_id=(member, other), device_id_type=pl.DeviceIdType.MESH
            )

    pl.semaphore_wait(barrier, 10)


class Gather:
    def __init__(self, own, target, send, recv, member, z):
        self.own, self.target = own, target
        self.send, self.recv = send, recv
        chip, core = member // 2, member % 2
        self.to_x = peer_x(chip) * 2 + core
        self.to_y = peer_y(chip) * 2 + core
        self.z = z
        self.half = own.shape[0] // 2

    def copy(self, number):
        low, high = pl.ds(0, self.half), pl.ds(self.half, self.half)
        source, target, to = (
            (self.own, self.target.at[1], self.to_x),
            (self.own, self.target.at[2], self.to_y),
            (self.target.at[1, low], self.target.at[3, low], self.to_y),
            (self.target.at[2, high], self.target.at[3, high], self.to_x),
        )[number]
        return remote(source, target, self.send.at[number], self.recv.at[number], to, self.z)

    def begin(self):
        self.copy(0).start()
        self.copy(1).start()

    def relay(self):
        self.copy(0).wait_recv()
        self.copy(2).start()
        self.copy(1).wait_recv()
        self.copy(3).start()

    def arrive(self):
        self.copy(2).wait_recv()
        self.copy(3).wait_recv()

    def finish(self):
        for number in range(4):
            self.copy(number).wait_send()


class Reduce:
    def __init__(self, part, from_x, from_y, passing, last, send, recv, member, z):
        self.part, self.from_x, self.from_y = part, from_x, from_y
        self.passing, self.last = passing, last
        self.send, self.recv = send, recv
        chip, core = member // 2, member % 2
        self.to_x = peer_x(chip) * 2 + core
        self.to_y = peer_y(chip) * 2 + core
        self.z = z
        self.slots = part.shape[0] // 4
        self.half = self.slots // 2

    def copy(self, number):
        slots, half = self.slots, self.half
        source, target, to = (
            (self.part.at[pl.ds(slots, half)], self.from_x.at[0], self.to_x),
            (self.part.at[pl.ds(3 * slots, half)], self.from_x.at[1], self.to_x),
            (self.part.at[pl.ds(2 * slots + half, half)], self.from_y.at[0], self.to_y),
            (self.part.at[pl.ds(3 * slots + half, half)], self.from_y.at[1], self.to_y),
            (self.passing.at[0], self.last.at[0], self.to_y),
            (self.passing.at[1], self.last.at[1], self.to_x),
        )[number]
        return remote(source, target, self.send.at[number], self.recv.at[number], to, self.z)

    def begin(self):
        for number in (1, 3, 0, 2):
            self.copy(number).start()

    def relay(self):
        slots, half = self.slots, self.half
        self.copy(1).wait_recv()
        self.passing[0] = (
            self.part[2 * slots : 2 * slots + half].astype(wide) + self.from_x[1].astype(wide)
        ).astype(low_type)
        self.copy(4).start()
        self.copy(3).wait_recv()
        self.passing[1] = (
            self.part[slots + half : 2 * slots].astype(wide) + self.from_y[1].astype(wide)
        ).astype(low_type)
        self.copy(5).start()

    def arrive(self):
        for number in (0, 2, 4, 5):
            self.copy(number).wait_recv()

    def result(self, number):
        direct = self.from_x if number == 0 else self.from_y
        return (
            self.part[number * self.half : (number + 1) * self.half].astype(wide)
            + direct[0].astype(wide)
            + self.last[number].astype(wide)
        )

    def finish(self):
        for number in range(6):
            self.copy(number).wait_send()

    @staticmethod
    def scratch(slots, model):
        return [pltpu.VMEM((2, slots // 2, model), low_type)] * 4


def norm_rows(value, gain):
    scale = lax.rsqrt(jnp.mean(value * value, axis=1, keepdims=True) + norm_eps)
    return value * scale * gain


def front_kernel(
    sizes,
    tokens_ref,
    cot_ref,
    gain_ref,
    small_ref,
    in_ref,
    gate_ref,
    out_ref,
    up_ref,
    down_ref,
    mix_in,
    weights,
    ffn_weights,
    saved_p,
    saved_state,
    saved_low,
    starts_out,
    residual_out,
    ffn_in,
    cot_out,
    gains_out,
    tokens_all,
    raw_in,
    raw_up,
    raw_down,
    turned,
    gain_seen,
    acc,
    part,
    from_x,
    from_y,
    passing,
    last,
    load_sem,
    gain_send,
    gain_recv,
    m_send,
    m_recv,
    m_core_send,
    m_core_recv,
    f_send,
    f_recv,
    f_core_send,
    f_core_recv,
    g_send,
    g_recv,
    r_send,
    r_recv,
):
    model, width, ffn_width = sizes
    member = lax.axis_index("dp")
    z = lax.axis_index("shard")
    chip, core = member // 2, member % 2
    end = z + core * (3 - 2 * z)
    other = chip * 2 + 1 - core
    slots = cot_ref.shape[0]
    half_ffn = ffn_width // 2
    owner = core == z // 2

    window = 128 * ((chip * ffn_width) // 128)
    skew = chip * ffn_width - window
    quarter = pl.ds(pl.multiple_of(chip * width, width), width)
    wide_window = pl.ds(pl.multiple_of(window, 128), raw_up.shape[2])

    def loads():
        found = [
            (out_ref.at[quarter], weights.at[end, pl.ds(2 * width, width), pl.ds(0, model)]),
            (
                small_ref.at[:, quarter],
                weights.at[end, pl.ds(2 * width, 16), pl.ds(model, width)],
            ),
        ]
        for kind in range(2):
            found.append((in_ref.at[kind, :, quarter], raw_in.at[kind]))
            found.append(
                (
                    gate_ref.at[kind, chip],
                    weights.at[end, pl.ds(kind * width, width), pl.ds(model, width)],
                )
            )
        found.append(
            (down_ref.at[pl.ds(pl.multiple_of(chip * ffn_width, 32), ffn_width)], raw_down)
        )
        for kind in range(2):
            found.append((up_ref.at[kind, :, wide_window], raw_up.at[kind]))
        return [
            pltpu.make_async_copy(source, target, load_sem.at[number])
            for number, (source, target) in enumerate(found)
        ]

    def turned_copy(kind):
        return pltpu.make_async_copy(
            raw_down
            if kind == 2
            else turned.at[kind, pl.ds(pl.multiple_of(skew, 32), ffn_width)],
            ffn_weights.at[kind, pl.ds(pl.multiple_of(2 * end * ffn_width, 32), ffn_width)],
            load_sem.at[9 + kind],
        )

    @pl.when(owner)
    def _():
        for copy in loads():
            copy.start()

    enter(member, z)

    gather_tokens = Gather(tokens_ref, tokens_all, g_send.at[0], g_recv.at[0], member, z)
    gather_cot = Gather(cot_ref, cot_out, g_send.at[1], g_recv.at[1], member, z)
    gather_ffn = Gather(ffn_in.at[0], ffn_in, g_send.at[2], g_recv.at[2], member, z)
    reduce = Reduce(part, from_x, from_y, passing, last, r_send, r_recv, member, z)
    own_cot = pltpu.make_async_copy(cot_ref, cot_out.at[0], load_sem.at[12])

    gather_tokens.begin()
    own_cot.start()

    def gain_copy(to, slot):
        return remote(
            gain_ref, gain_seen.at[slot], gain_send.at[to], gain_recv.at[slot], member, to
        )

    for to in range(4):

        @pl.when(to != z)
        def _():
            gain_copy(to, z).start()

    gain_seen[z] = gain_ref[...]

    def m_rows(number):
        return pl.ds(number * width, width)

    def m_copy(slot, number, way, to_end):
        place = weights.at[slot, m_rows(number)]
        return remote(
            place,
            place,
            m_send.at[way, slot, number],
            m_recv.at[slot, number],
            member,
            line_place(to_end, core),
        )

    def m_core(slot, number):
        return remote(
            weights.at[slot, m_rows(number)],
            weights.at[2 + slot, m_rows(number)],
            m_core_send.at[slot, number],
            m_core_recv.at[slot, number],
            other,
            z,
        )

    def f_place(slot, number):
        row = ((slot % 2) * 2 + slot // 2) * ffn_width + (number % 2) * half_ffn
        return ffn_weights.at[number // 2, pl.ds(row, half_ffn)]

    def f_copy(slot, number, way, to_end):
        place = f_place(slot, number)
        return remote(
            place,
            place,
            f_send.at[way, slot, number],
            f_recv.at[slot, number],
            member,
            line_place(to_end, core),
        )

    def f_core(slot, number):
        return remote(
            f_place(slot, number),
            f_place(2 + slot, number),
            f_core_send.at[slot, number],
            f_core_recv.at[slot, number],
            other,
            z,
        )

    def pass_on(copy, core_copy, slot, number):
        if slot == 0:

            @pl.when(end < 3)
            def _():
                copy(slot, number, 0, end + 1).start()
        else:

            @pl.when((end == 1) | (end == 2))
            def _():
                copy(slot, number, 0, end + 1).start()

        core_copy(slot, number).start()

    def pass_back(copy, numbers):
        @pl.when(end == 1)
        def _():
            for number in numbers:
                copy(1, number, 1, 0).start()

    def start_own(copy, core_copy, numbers):
        for slot in range(2):

            @pl.when(end == slot)
            def _():
                for number in numbers:
                    pass_on(copy, core_copy, slot, number)

    def turn_in(kind):
        @pl.when(owner)
        def _():
            for copy in loads()[2 + 2 * kind : 4 + 2 * kind]:
                copy.wait()

            def turn(at, carry):
                columns = pl.ds(pl.multiple_of(at * 256, 256), 256)
                weights[end, kind * width : (kind + 1) * width, columns] = raw_in[
                    kind, columns, :
                ].T
                return carry

            lax.fori_loop(0, model // 256, turn, 0)

        start_own(m_copy, m_core, (kind,))
        pass_back(m_copy, (kind,))

    def turn_up(kind):
        @pl.when(owner)
        def _():
            loads()[7 + kind].wait()

            def turn(at, carry):
                columns = pl.ds(pl.multiple_of(at * 256, 256), 256)
                turned[kind, :, columns] = raw_up[kind, columns, :].T
                return carry

            lax.fori_loop(0, model // 256, turn, 0)
            turned_copy(kind).start()

    @pl.when(owner)
    def _():
        for copy in loads()[:2]:
            copy.wait()
        for row in range(2 * width + 16, 3 * width, 16):
            weights[end, row : row + 16, model:] = jnp.zeros((16, width), low_type)

    start_own(m_copy, m_core, (2,))
    pass_back(m_copy, (2,))
    turn_in(0)
    turn_in(1)

    @pl.when(owner)
    def _():
        loads()[6].wait()
        turned_copy(2).start()

    turn_up(0)
    turn_up(1)
    gather_tokens.relay()
    m_order = (2, 0, 1)

    @pl.when(end < 3)
    def _():
        for number in m_order:
            for slot in (1, 0):

                @pl.when(end != slot)
                def _():
                    m_copy(slot, number, 0, 0).wait_recv()
                    pass_on(m_copy, m_core, slot, number)

    @pl.when(owner)
    def _():
        for kind in range(3):
            turned_copy(kind).wait()

    f_order = (4, 5, 0, 1, 2, 3)
    start_own(f_copy, f_core, f_order)

    def f_pass(slot, numbers):
        for number in numbers:
            f_copy(slot, number, 0, 0).wait_recv()
            pass_on(f_copy, f_core, slot, number)

    def f_step(step):
        @pl.when(end == 1)
        def _():
            f_pass(0, ((), (4, 5), (0, 1), (2, 3), (), ())[step])

        @pl.when(end == 2)
        def _():
            f_pass(1, ((4,), (5, 0), (1, 2), (3,), (), ())[step])
            f_pass(0, ((), (), (), (4,), (5, 0), (1, 2, 3))[step])

        if step == 0:
            pass_back(f_copy, f_order)

        @pl.when(end == 0)
        def _():
            f_pass(1, ((), (), (), (), (), f_order)[step])

    for to in range(4):

        @pl.when(to != z)
        def _():
            gain_copy(to, to).wait_recv()

    gains = jnp.concatenate([gain_seen[at].astype(wide) for at in range(4)], axis=1)
    gains_out[...] = gains[0:8]
    gather_tokens.arrive()

    def norm_block(block):
        if block == 0:
            source, starts = tokens_ref[:, :model], tokens_ref[:, model:]
        else:
            source, starts = tokens_all[block, :, :model], tokens_all[block, :, model:]
        at = slice(block * slots, (block + 1) * slots)
        mix_in[at, :] = norm_rows(source.astype(wide), gains_out[0:1]).astype(low_type)
        starts_out[at, :] = starts

    for block in range(4):
        norm_block(block)
    gather_cot.begin()
    f_step(0)

    late = end >= 2
    for turn in range(4):
        head = (turn + 2 * late) % 4
        if turn == 2:

            @pl.when(end == 3)
            def _():
                for number in m_order:
                    for slot in (1, 0):
                        m_copy(slot, number, 0, 0).wait_recv()
                        m_core(slot, number).start()

        @pl.when(head >= 2)
        def _():
            for number in m_order:
                m_core(head - 2, number).wait_recv()

        views = weight_views(weights.at[pl.ds(head, 1)], width)

        def step_block(block, carry):
            rows = pl.ds(pl.multiple_of(block * slots, slots), slots)
            position = slot_position(starts_out[rows, :])
            projected, states, mixed_low, product = mixer_step(
                mix_in[rows, :], position, views, width
            )
            saved_p[head, rows, :] = projected
            saved_state[head, rows, :] = states
            saved_low[head, rows, :] = mixed_low
            if turn == 0:
                acc[rows, :] = product
            elif turn < 3:
                acc[rows, :] += product
            else:
                part[rows, :] = (acc[rows, :] + product).astype(low_type)
            return carry

        lax.fori_loop(0, 4, step_block, 0)
        if turn == 3:
            reduce.begin()
        f_step(turn + 1)
        if turn == 0:
            gather_cot.relay()

    reduce.relay()
    f_step(5)
    reduce.arrive()
    half = slots // 2
    for number in range(2):
        at = slice(number * half, (number + 1) * half)
        residual = tokens_ref[at, :model].astype(wide) + reduce.result(number)
        residual_out[at, :] = residual
        ffn_in[0, at, :] = norm_rows(residual, gains_out[1:2]).astype(low_type)
    gather_ffn.begin()
    gather_ffn.relay()

    @pl.when(end == 3)
    def _():
        for slot in (1, 0):
            for number in f_order:
                f_copy(slot, number, 0, 0).wait_recv()
                f_core(slot, number).start()

    gather_ffn.arrive()
    gather_cot.arrive()
    own_cot.wait()
    for slot in range(2):
        for number in range(6):
            f_core(slot, number).wait_recv()

    for gather in (gather_tokens, gather_cot, gather_ffn, reduce):
        gather.finish()
    for to in range(4):

        @pl.when(to != z)
        def _():
            gain_copy(to, z).wait_send()

    for copy, core_copy, count in ((m_copy, m_core, 3), (f_copy, f_core, 6)):
        for number in range(count):
            for slot in range(2):
                core_copy(slot, number).wait_send()

            @pl.when(end < 3)
            def _():
                copy(0, number, 0, 0).wait_send()

            @pl.when((end == 1) | (end == 2))
            def _():
                copy(1, number, 0, 0).wait_send()

            @pl.when(end == 1)
            def _():
                copy(1, number, 1, 0).wait_send()


def front(tokens, cot, gains, small, in_proj, gates, out_proj, gate_up, down, sizes):
    model, width, ffn_width = sizes
    slots = cot.shape[0]
    rows = 4 * slots
    dma = pltpu.SemaphoreType.DMA
    vmem = pl.BlockSpec(memory_space=pltpu.VMEM)
    anywhere = pl.BlockSpec(memory_space=pl.ANY)
    window = -(-ffn_width // 128) * 128
    return pl.pallas_call(
        functools.partial(front_kernel, sizes),
        in_specs=[vmem] * 3 + [anywhere] * 6,
        out_specs=[vmem, vmem, anywhere, vmem, vmem, vmem, vmem, vmem, vmem, anywhere, vmem],
        out_shape=[
            jax.ShapeDtypeStruct((rows, model), low_type),
            jax.ShapeDtypeStruct((4, 3 * width, model + width), low_type),
            jax.ShapeDtypeStruct((3, 4 * ffn_width, model), low_type),
            jax.ShapeDtypeStruct((4, rows, 2 * width), wide),
            jax.ShapeDtypeStruct((4, rows, width), wide),
            jax.ShapeDtypeStruct((4, rows, width), low_type),
            jax.ShapeDtypeStruct((rows, width), low_type),
            jax.ShapeDtypeStruct((slots, model), wide),
            jax.ShapeDtypeStruct((4, slots, model), low_type),
            jax.ShapeDtypeStruct((4, slots, model), low_type),
            jax.ShapeDtypeStruct((8, model), wide),
        ],
        scratch_shapes=[
            pltpu.VMEM((4, slots, model + width), low_type),
            pltpu.VMEM((2, model, width), low_type),
            pltpu.VMEM((2, model, window), low_type),
            pltpu.VMEM((ffn_width, model), low_type),
            pltpu.VMEM((2, window, model), low_type),
            pltpu.VMEM((4, 16, model // 4), low_type),
            pltpu.VMEM((rows, model), wide),
            pltpu.VMEM((rows, model), low_type),
        ]
        + Reduce.scratch(slots, model)
        + [
            dma((13,)),
            dma((4,)),
            dma((4,)),
            dma((2, 2, 3)),
            dma((2, 3)),
            dma((2, 3)),
            dma((2, 3)),
            dma((2, 2, 6)),
            dma((2, 6)),
            dma((2, 6)),
            dma((2, 6)),
            dma((3, 4)),
            dma((3, 4)),
            dma((6,)),
            dma((6,)),
        ],
        compiler_params=pltpu.CompilerParams(
            collective_id=3, has_side_effects=True, vmem_limit_bytes=60 * 1024 * 1024
        ),
        cost_estimate=pl.CostEstimate(
            flops=2 * rows * model * 4 * width * 3,
            bytes_accessed=6 * ffn_width * 4 * model,
            transcendentals=rows * 4 * width * 6,
        ),
        name="front",
    )(tokens, cot, gains, small, in_proj, gates, out_proj, gate_up, down)


def middle_kernel(
    sizes,
    x_ref,
    go_ref,
    weights_ref,
    residual_ref,
    gain_ref,
    mask_ref,
    total,
    res_low,
    res_out,
    gain_out,
    block_out,
    held,
    lows,
    paired,
    arrived,
    part_in,
    part_out,
    in_x,
    in_y,
    in_pass,
    in_last,
    load_sem,
    core_send,
    core_recv,
    line_send,
    line_recv,
    i_send,
    i_recv,
    o_send,
    o_recv,
    g_send,
    g_recv,
):
    model, ffn_width = sizes
    member = lax.axis_index("dp")
    z = lax.axis_index("shard")
    chip, core = member // 2, member % 2
    end = z + core * (3 - 2 * z)
    other = chip * 2 + 1 - core
    slots = residual_ref.shape[0]
    half = slots // 2
    hidden = 4 * ffn_width
    half_ffn = ffn_width // 2

    loads = [
        pltpu.make_async_copy(weights_ref.at[kind], held.at[kind], load_sem.at[kind])
        for kind in range(3)
    ]
    for load in loads:
        load.start()
    enter(member, z)
    for load in loads:
        load.wait()

    split = -(-2 * ffn_width // 128) * 128

    def block_step(low, high, block, carry):
        rows = pl.ds(pl.multiple_of(block * slots, slots), slots)
        x = x_ref[rows, :]
        grad_out = go_ref[rows, :]
        pre_gate = dot_rows(x, held[0, low:high])
        pre_up = dot_rows(x, held[1, low:high])
        active, slope = gelu_parts(pre_gate)
        ffn_low = (active * pre_up).astype(low_type)
        grad_act = dot_rows(grad_out, held[2, low:high])
        gate_low = (grad_act * pre_up * slope).astype(low_type)
        up_low = (grad_act * active).astype(low_type)
        sum_out = dot_plain(ffn_low, held[2, low:high])
        sum_in = dot_plain(gate_low, held[0, low:high]) + dot_plain(up_low, held[1, low:high])
        lows[0, rows, low:high] = gate_low
        lows[1, rows, low:high] = up_low
        lows[2, rows, low:high] = ffn_low
        if low > 0:
            sum_in = sum_in + part_in[rows, :].astype(wide)
            sum_out = sum_out + part_out[rows, :].astype(wide)
        part_in[rows, :] = sum_in.astype(low_type)
        part_out[rows, :] = sum_out.astype(low_type)
        return carry

    reduce_in = Reduce(part_in, in_x, in_y, in_pass, in_last, i_send, i_recv, member, z)
    reduce_out = Reduce(
        part_out,
        in_x.at[pl.ds(2, 2)],
        in_y.at[pl.ds(2, 2)],
        in_pass.at[pl.ds(2, 2)],
        in_last.at[pl.ds(2, 2)],
        o_send,
        o_recv,
        member,
        z,
    )
    gather = Gather(res_low.at[0], res_low, g_send, g_recv, member, z)
    middle = model // 2

    def weight_grads(kind, low, high):
        factor = go_ref if kind == 2 else x_ref
        for at in range(2):
            columns = slice(at * middle, (at + 1) * middle)
            held[kind, low:high, columns] = dot_slots(
                lows[kind, :, low:high], factor[:, columns]
            ).astype(low_type)

    def core_copy(slot, kind):
        return remote(
            held.at[kind, pl.ds((2 * slot + 1) * ffn_width, ffn_width)],
            paired.at[slot, kind],
            core_send.at[slot, kind],
            core_recv.at[slot, kind],
            other,
            z,
        )

    def chunk(number):
        return number // 2, pl.ds((number % 2) * half_ffn, half_ffn)

    def line_copy(kind, number, to_end):
        at, rows = chunk(number)
        return remote(
            paired.at[min(kind, 1), at, rows],
            arrived.at[kind, at, rows],
            line_send.at[kind, number],
            line_recv.at[kind, number],
            member,
            line_place(to_end, core),
        )

    def pair_up(slot, kind):
        core_copy(slot, kind).wait_recv()
        for number in (2 * kind, 2 * kind + 1):
            at, rows = chunk(number)
            own = held[at, pl.ds(2 * slot * ffn_width + (number % 2) * half_ffn, half_ffn)]
            paired[slot, at, rows] = add_low(own, paired[slot, at, rows])

            @pl.when(end == 3)
            def _():
                line_copy(slot, number, 2).start()

            if slot == 1:

                @pl.when(end == 0)
                def _():
                    line_copy(2, number, 1).start()

    def part_grads(slot, low, high):
        for kind in range(3):
            weight_grads(kind, low, high)
            core_copy(slot, kind).start()
            if kind > 0:
                pair_up(slot, kind - 1)
        pair_up(slot, 2)

    def summed(slot, kinds, number):
        at, rows = chunk(number)
        result = paired[slot, at, rows].astype(wide)
        for kind in kinds:
            result = result + arrived[kind, at, rows].astype(wide)
        return result.astype(low_type)

    def outer_step(number):
        at, rows = chunk(number)

        @pl.when((end == 2) | (end == 1))
        def _():
            line_copy(0, number, 0).wait_recv()
            paired[0, at, rows] = summed(0, (0,), number)
            line_copy(0, number, end - 1).start()

    def inner_step(number):
        at, rows = chunk(number)

        @pl.when(end == 2)
        def _():
            line_copy(1, number, 0).wait_recv()
            paired[1, at, rows] = summed(1, (1,), number)
            line_copy(1, number, 1).start()

    def out_copy(slot, number):
        at, rows = chunk(number)
        return pltpu.make_async_copy(
            paired.at[slot, at, rows], total.at[at, rows], load_sem.at[number]
        )

    def last_step(number):
        at, rows = chunk(number)

        @pl.when(end == 1)
        def _():
            line_copy(1, number, 0).wait_recv()
            line_copy(2, number, 0).wait_recv()
            paired[1, at, rows] = summed(1, (1, 2), number)
            out_copy(1, number).start()

        @pl.when(end == 0)
        def _():
            line_copy(0, number, 0).wait_recv()
            paired[0, at, rows] = summed(0, (0,), number)
            out_copy(0, number).start()

    lax.fori_loop(0, 4, functools.partial(block_step, 0, split), 0)
    part_grads(0, 0, split)
    lax.fori_loop(0, 4, functools.partial(block_step, split, hidden), 0)
    reduce_in.begin()
    part_grads(1, split, hidden)
    for number in range(3):
        outer_step(number)
    reduce_in.relay()
    for number in range(3, 6):
        outer_step(number)

    reduce_in.arrive()
    gain = gain_ref[1:2]
    gain_sum = jnp.zeros((1, model), wide)
    for number in range(2):
        at = slice(number * half, (number + 1) * half)
        grad = reduce_in.result(number)
        value = residual_ref[at]
        scale = lax.rsqrt(jnp.mean(value * value, axis=1, keepdims=True) + norm_eps)
        scaled = grad * gain
        gain_sum = gain_sum + jnp.sum(grad * value * scale, axis=0, keepdims=True)
        inner = jnp.mean(scaled * value, axis=1, keepdims=True)
        back = scale * scaled - value * (scale * scale * scale * inner)
        result = go_ref[at].astype(wide) + back
        res_out[at] = result
        res_low[0, at] = result.astype(low_type)
    gain_out[...] = jnp.concatenate([gain_ref[0:1], gain_sum, jnp.zeros((6, model), wide)], axis=0)
    gather.begin()
    inner_step(0)
    gather.relay()
    inner_step(1)
    inner_step(2)
    gather.arrive()
    reduce_out.begin()
    inner_step(3)
    inner_step(4)
    reduce_out.relay()
    inner_step(5)
    for number in range(6):
        last_step(number)
    reduce_out.arrive()
    live = mask_ref[:, 0:1].astype(wide)
    for number in range(2):
        at = slice(number * half, (number + 1) * half)
        block_out[at] = (live[at] * (residual_ref[at] + reduce_out.result(number))).astype(low_type)

    for sent in (reduce_in, reduce_out, gather):
        sent.finish()
    for slot in range(2):
        for kind in range(3):
            core_copy(slot, kind).wait_send()
    for number in range(6):

        @pl.when(end > 0)
        def _():
            line_copy(0, number, 0).wait_send()

        @pl.when(end > 1)
        def _():
            line_copy(1, number, 0).wait_send()

        @pl.when(end == 0)
        def _():
            line_copy(2, number, 1).wait_send()

        @pl.when(end < 2)
        def _():
            out_copy(0, number).wait()


def middle(x, grad_out, weights, residual, gains, mask):
    rows, model = x.shape
    hidden = weights.shape[1]
    ffn_width = hidden // 4
    slots = rows // 4
    dma = pltpu.SemaphoreType.DMA
    vmem = pl.BlockSpec(memory_space=pltpu.VMEM)
    anywhere = pl.BlockSpec(memory_space=pl.ANY)
    quarter = (3, ffn_width, model)
    return pl.pallas_call(
        functools.partial(middle_kernel, (model, ffn_width)),
        in_specs=[vmem, vmem, anywhere, vmem, vmem, vmem],
        out_specs=[anywhere] + [vmem] * 4,
        out_shape=[
            jax.ShapeDtypeStruct(quarter, low_type),
            jax.ShapeDtypeStruct((4, slots, model), low_type),
            jax.ShapeDtypeStruct((slots, model), wide),
            jax.ShapeDtypeStruct((8, model), wide),
            jax.ShapeDtypeStruct((slots, model), low_type),
        ],
        scratch_shapes=[
            pltpu.VMEM(weights.shape, low_type),
            pltpu.VMEM((3, rows, hidden), low_type),
            pltpu.VMEM((2,) + quarter, low_type),
            pltpu.VMEM((3,) + quarter, low_type),
            pltpu.VMEM((rows, model), low_type),
            pltpu.VMEM((rows, model), low_type),
        ]
        + [pltpu.VMEM((4, slots // 2, model), low_type)] * 4
        + [
            dma((6,)),
            dma((2, 3)),
            dma((2, 3)),
            dma((3, 6)),
            dma((3, 6)),
            dma((6,)),
            dma((6,)),
            dma((6,)),
            dma((6,)),
            dma((4,)),
            dma((4,)),
        ],
        compiler_params=pltpu.CompilerParams(
            collective_id=4, has_side_effects=True, vmem_limit_bytes=63 * 1024 * 1024
        ),
        cost_estimate=pl.CostEstimate(
            flops=2 * rows * model * hidden * 9,
            bytes_accessed=weights.size * 4 + rows * model * 16,
            transcendentals=rows * hidden,
        ),
        name="middle",
    )(x, grad_out, weights, residual, gains, mask)


class Scatter:
    def __init__(self, sizes, member, z, send_sem, recv_sem):
        self.model, self.width, self.ffn_width, self.piece_length = sizes
        self.member, self.z = member, z
        self.chip, self.core = member // 2, member % 2
        self.owner = self.core == z // 2
        self.send_sem, self.recv_sem = send_sem, recv_sem
        self.across = self.model // 128
        rec, ffn, model = 4 * self.width, 4 * self.ffn_width, self.model
        self.gate_base = 2 * model * rec
        self.out_base = self.gate_base + 8 * self.width * self.width
        self.up_base = self.out_base + rec * model
        self.down_base = self.up_base + 2 * model * ffn
        self.rec, self.ffn = rec, ffn
        self.first_in = 0
        self.first_gate = 2 * self.across
        self.first_out = self.first_gate + 2
        self.first_small = self.first_out + 4
        self.first_up = self.first_small + 1
        self.first_down = self.first_up + 2 * self.across
        self.count = self.first_down + 6

    def in_unit(self, number, q):
        kind, at = number // self.across, number % self.across
        low = (kind * self.model + at * 128) * self.rec
        where = (
            pl.ds(pl.multiple_of(kind * self.width, self.width), self.width),
            pl.ds(pl.multiple_of(at * 128, 128), 128),
        )
        return self.first_in + number, where, low, low + 128 * self.rec

    def gate_unit(self, kind, q):
        low = self.gate_base + (kind * 4 + q) * self.width * self.width
        where = (
            pl.ds(pl.multiple_of(kind * self.width, self.width), self.width),
            pl.ds(self.model, self.width),
        )
        return self.first_gate + kind, where, low, low + self.width * self.width

    def out_unit(self, number, q):
        rows = self.width // 4
        low = self.out_base + (q * self.width + number * rows) * self.model
        where = (
            pl.ds(pl.multiple_of(2 * self.width + number * rows, rows), rows),
            pl.ds(0, self.model),
        )
        return self.first_out + number, where, low, low + rows * self.model

    def up_unit(self, number, q):
        kind, at = number // self.across, number % self.across
        low = self.up_base + (kind * self.model + at * 128) * self.ffn
        where = (kind, pl.ds(0, self.ffn_width), pl.ds(pl.multiple_of(at * 128, 128), 128))
        return self.first_up + number, where, low, low + 128 * self.ffn

    def down_unit(self, number, q):
        rows = self.ffn_width // 6
        low = self.down_base + (q * self.ffn_width + number * rows) * self.model
        where = (2, pl.ds(pl.multiple_of(number * rows, 16), rows), pl.ds(0, self.model))
        return self.first_down + number, where, low, low + rows * self.model

    def small_where(self):
        return (pl.ds(2 * self.width, 16), pl.ds(self.model, self.width))

    def copies(self, unit, source, target, q, act):
        number, where, low, high = unit
        first = low // self.piece_length
        last = (high - 1) // self.piece_length
        for which, to in ((0, first), (1, last)):
            wanted = True if which == 0 else last != first

            @pl.when((to != self.member) & wanted)
            def _():
                act(
                    remote(
                        source.at[where],
                        target.at[(q,) + where],
                        self.send_sem.at[which, number],
                        self.recv_sem.at[q, number],
                        to,
                        self.z,
                    ),
                    True,
                )

            @pl.when((to == self.member) & wanted)
            def _():
                act(
                    pltpu.make_async_copy(
                        source.at[where], target.at[(q,) + where], self.recv_sem.at[q, number]
                    ),
                    False,
                )

    def each(self, unit_of, low, high, source, target, act):
        def body(number, carry):
            self.copies(unit_of(number, self.chip), source, target, self.chip, act)
            return carry

        lax.fori_loop(low, high, body, 0)

    def smalls(self, source, target, act):
        where = self.small_where()
        for to in range(8):

            @pl.when(self.member != to)
            def _():
                act(
                    remote(
                        source.at[where],
                        target.at[(self.chip,) + where],
                        self.send_sem.at[2, to],
                        self.recv_sem.at[self.chip, self.first_small],
                        to,
                        self.z,
                    ),
                    True,
                )

        act(
            pltpu.make_async_copy(
                source.at[where],
                target.at[(self.chip,) + where],
                self.recv_sem.at[self.chip, self.first_small],
            ),
            False,
        )

    def arrivals(self, unit_of, count, source, target):
        low = self.member * self.piece_length

        def body(number, carry):
            for q in range(4):
                index, where, first, last = unit_of(number, q)
                mine = (first < low + self.piece_length) & (last > low)
                here = (self.chip == q) & self.owner

                @pl.when(mine & here)
                def _():
                    pltpu.make_async_copy(
                        source.at[where], target.at[(q,) + where], self.recv_sem.at[q, index]
                    ).wait()

                @pl.when(mine & jnp.logical_not(here))
                def _():
                    remote(
                        source.at[where],
                        target.at[(q,) + where],
                        self.send_sem.at[0, index],
                        self.recv_sem.at[q, index],
                        self.member,
                        self.z,
                    ).wait_recv()

            return carry

        lax.fori_loop(0, count, body, 0)

    def small_arrivals(self, source, target):
        where = self.small_where()
        for q in range(4):
            here = (self.chip == q) & self.owner

            @pl.when(here)
            def _():
                pltpu.make_async_copy(
                    source.at[where],
                    target.at[(q,) + where],
                    self.recv_sem.at[q, self.first_small],
                ).wait()

            @pl.when(jnp.logical_not(here))
            def _():
                remote(
                    source.at[where],
                    target.at[(q,) + where],
                    self.send_sem.at[2, 0],
                    self.recv_sem.at[q, self.first_small],
                    self.member,
                    self.z,
                ).wait_recv()


def begin(copy, is_remote):
    copy.start()


def finish_send(copy, is_remote):
    if is_remote:
        copy.wait_send()


def back_kernel(
    sizes,
    x_hbm,
    res_hbm,
    starts_ref,
    w_hbm,
    p_hbm,
    state_hbm,
    low_hbm,
    ffn_ref,
    tokens_ref,
    res_ref,
    gain_ref,
    mix_out,
    ffn_out,
    tokens_out,
    gain_out,
    x_ref,
    low_res,
    w_ref,
    p_ref,
    state_ref,
    low_ref,
    proj_grads,
    gate_acc,
    small_acc,
    grads,
    part_ref,
    paired,
    arrived,
    total,
    from_x,
    from_y,
    passing,
    last,
    gain_part,
    gain_plane,
    gain_line,
    gain_seen,
    load_sem,
    core_send,
    core_recv,
    line_send,
    line_recv,
    plane_send,
    plane_recv,
    gain_send,
    gain_recv,
    unit_send,
    unit_recv,
):
    model, width, ffn_width, piece_length = sizes
    member = lax.axis_index("dp")
    z = lax.axis_index("shard")
    chip, core = member // 2, member % 2
    end = z + core * (3 - 2 * z)
    slots = tokens_ref.shape[0]
    half = slots // 2
    other = chip * 2 + 1 - core
    scatter = Scatter(sizes, member, z, unit_send, unit_recv)

    order = (2, 0, 3, 1)
    common = [
        pltpu.make_async_copy(x_hbm, x_ref, load_sem.at[4, 0]),
        pltpu.make_async_copy(res_hbm, low_res, load_sem.at[4, 1]),
    ]

    def head_loads(head):
        return [
            pltpu.make_async_copy(source.at[head], target.at[head], load_sem.at[head, number])
            for number, (source, target) in enumerate(
                ((w_hbm, w_ref), (p_hbm, p_ref), (state_hbm, state_ref), (low_hbm, low_ref))
            )
        ]

    for copy in head_loads(order[0]) + common:
        copy.start()
    for head in order[1:]:
        for copy in head_loads(head):
            copy.start()
    enter(member, z)

    @pl.when(scatter.owner)
    def _():
        scatter.each(scatter.up_unit, 0, 2 * scatter.across, ffn_ref, ffn_out, begin)
        scatter.each(scatter.down_unit, 0, 6, ffn_ref, ffn_out, begin)

    def rows(number):
        return pl.ds(number * width, width)

    def core_copy(slot, number):
        return remote(
            grads.at[2 + slot, rows(number)],
            paired.at[slot, rows(number)],
            core_send.at[slot, number],
            core_recv.at[slot, number],
            other,
            z,
        )

    reduce = Reduce(
        part_ref, from_x, from_y, passing, last, plane_send, plane_recv, member, z
    )

    def line_copy(kind, number, source, to_end):
        return remote(
            source,
            arrived.at[kind, rows(number)],
            line_send.at[kind, number],
            line_recv.at[kind, number],
            member,
            line_place(to_end, core),
        )

    def pair_up(slot):
        for number in range(3):
            core_copy(slot, number).wait_recv()
            both = grads[slot, rows(number)].astype(wide) + paired[slot, rows(number)].astype(wide)
            paired[slot, rows(number)] = both.astype(low_type)

            @pl.when(end == 3)
            def _():
                line_copy(slot, number, paired.at[slot, rows(number)], 2).start()

            if slot == 1:

                @pl.when(end == 0)
                def _():
                    line_copy(2, number, paired.at[slot, rows(number)], 1).start()

    def summed(slot, kinds, number):
        result = paired[slot, rows(number)].astype(wide)
        for kind in kinds:
            result = result + arrived[kind, rows(number)].astype(wide)
        return result.astype(low_type)

    def on_arrival(kind, number):
        line_copy(kind, number, paired.at[0, rows(number)], 0).wait_recv()

    def outer_step(place, number):
        @pl.when(end == place)
        def _():
            on_arrival(0, number)
            paired[0, rows(number)] = summed(0, (0,), number)
            line_copy(0, number, paired.at[0, rows(number)], place - 1).start()

    def share(number):
        if number < 2:
            across = scatter.across
            scatter.each(
                scatter.in_unit, number * across, (number + 1) * across, total, mix_out, begin
            )
            scatter.each(scatter.gate_unit, number, number + 1, total, mix_out, begin)
        else:
            scatter.each(scatter.out_unit, 0, 4, total, mix_out, begin)
            scatter.smalls(total, mix_out, begin)

    for copy in common:
        copy.wait()
    for turn, head in enumerate(order):
        for copy in head_loads(head):
            copy.wait()
        views = weight_views(w_ref.at[pl.ds(head, 1)], width)
        gate_acc[...] = jnp.zeros_like(gate_acc)
        small_acc[...] = jnp.zeros_like(small_acc)

        def step_block(block, carry):
            at = pl.ds(pl.multiple_of(block * slots, slots), slots)
            proj_low, grad_gates, grad_small = mixer_back_step(
                slot_position(starts_ref[at, :]),
                views,
                p_ref[head, at, :],
                state_ref[head, at, :],
                low_res[at, :],
                width,
            )
            proj_grads[at, head * 2 * width : (head + 1) * 2 * width] = proj_low
            gate_acc[...] += grad_gates
            small_acc[...] += grad_small
            return carry

        lax.fori_loop(0, 4, step_block, 0)
        grads[head, 0 : 2 * width, 0:model] = dot_slots(
            proj_grads[:, head * 2 * width : (head + 1) * 2 * width], x_ref[...]
        ).astype(low_type)
        grads[head, 2 * width : 3 * width, 0:model] = dot_slots(
            low_ref[head], low_res[...]
        ).astype(low_type)
        grads[head, 0:width, model:] = gate_acc[:, :width].astype(low_type)
        grads[head, width : 2 * width, model:] = gate_acc[:, width:].astype(low_type)
        grads[head, 2 * width : 3 * width, model:] = jnp.concatenate(
            [small_acc[...], jnp.zeros((width - 8, width), wide)], axis=0
        ).astype(low_type)
        if head >= 2:
            for number in range(3):
                core_copy(head - 2, number).start()
        if turn == 1:
            pair_up(0)
        elif turn == 2:
            outer_step(2, 0)
            outer_step(2, 1)
        elif turn == 3:
            outer_step(2, 2)
            outer_step(1, 0)
            outer_step(1, 1)

    def in_block(block, carry):
        at = pl.ds(pl.multiple_of(block * slots, slots), slots)
        result = jnp.zeros((slots, model), wide)
        for head in range(4):
            result = result + dot_plain(
                proj_grads[at, head * 2 * width : (head + 1) * 2 * width],
                w_ref[head, 0 : 2 * width, 0:model],
            )
        part_ref[at, :] = result.astype(low_type)
        return carry

    pair_up(1)
    lax.fori_loop(0, 4, in_block, 0)
    reduce.begin()
    outer_step(1, 2)
    reduce.relay()

    for number in range(3):

        @pl.when(end == 2)
        def _():
            on_arrival(1, number)
            paired[1, rows(number)] = summed(1, (1,), number)
            line_copy(1, number, paired.at[1, rows(number)], 1).start()

        @pl.when(end == 1)
        def _():
            on_arrival(1, number)
            on_arrival(2, number)
            total[rows(number)] = summed(1, (1, 2), number)

        @pl.when(end == 0)
        def _():
            on_arrival(0, number)
            total[rows(number)] = summed(0, (0,), number)

        @pl.when(scatter.owner)
        def _():
            share(number)

    reduce.arrive()
    gain = gain_ref[0:1]
    gain_sum = jnp.zeros((1, model), wide)
    for number in range(2):
        at = slice(number * half, (number + 1) * half)
        grad = reduce.result(number)
        value = tokens_ref[at].astype(wide)
        scale = lax.rsqrt(jnp.mean(value * value, axis=1, keepdims=True) + norm_eps)
        scaled = grad * gain
        gain_sum = gain_sum + jnp.sum(grad * value * scale, axis=0, keepdims=True)
        inner = jnp.mean(scaled * value, axis=1, keepdims=True)
        back = scale * scaled - value * (scale * scale * scale * inner)
        tokens_out[at] = (res_ref[at] + back).astype(low_type)
    gain_part[...] = jnp.concatenate([gain_sum, gain_ref[1:2], jnp.zeros((6, model), wide)], axis=0)

    def gain_copy():
        return remote(
            gain_part, gain_plane.at[member], gain_send.at[0], gain_recv.at[member], 7, z
        )

    @pl.when(member != 7)
    def _():
        gain_copy().start()
        gain_copy().wait_send()
        gain_out[...] = jnp.zeros_like(gain_out)

    @pl.when(member == 7)
    def _():
        result = gain_part[...]
        for source in range(7):
            remote(
                gain_part,
                gain_plane.at[source],
                gain_send.at[0],
                gain_recv.at[source],
                7,
                z,
            ).wait_recv()
            result = result + gain_plane[source]
        quarter = model // 4
        for place in range(4):
            gain_line[place] = result[:, place * quarter : (place + 1) * quarter]

        def line_gain(place, slot):
            return remote(
                gain_line.at[place],
                gain_seen.at[slot],
                gain_send.at[1 + place],
                gain_recv.at[8 + slot],
                7,
                place,
            )

        for place in range(4):

            @pl.when(place != z)
            def _():
                line_gain(place, z).start()

        gain_out[...] = gain_line[z]
        for place in range(4):

            @pl.when(place != z)
            def _():
                line_gain(place, place).wait_recv()
                gain_out[...] += gain_seen[place]
                line_gain(place, z).wait_send()

    across = scatter.across
    scatter.arrivals(scatter.up_unit, 2 * across, ffn_ref, ffn_out)
    scatter.arrivals(scatter.down_unit, 6, ffn_ref, ffn_out)
    scatter.arrivals(scatter.in_unit, 2 * across, total, mix_out)
    scatter.arrivals(scatter.gate_unit, 2, total, mix_out)
    scatter.arrivals(scatter.out_unit, 4, total, mix_out)
    scatter.small_arrivals(total, mix_out)

    @pl.when(scatter.owner)
    def _():
        scatter.each(scatter.up_unit, 0, 2 * across, ffn_ref, ffn_out, finish_send)
        scatter.each(scatter.down_unit, 0, 6, ffn_ref, ffn_out, finish_send)
        scatter.each(scatter.in_unit, 0, 2 * across, total, mix_out, finish_send)
        scatter.each(scatter.gate_unit, 0, 2, total, mix_out, finish_send)
        scatter.each(scatter.out_unit, 0, 4, total, mix_out, finish_send)
        scatter.smalls(total, mix_out, finish_send)

    reduce.finish()
    for slot in range(2):
        for number in range(3):
            core_copy(slot, number).wait_send()
    for number in range(3):

        @pl.when(end > 0)
        def _():
            line_copy(0, number, paired.at[0, rows(number)], 0).wait_send()

        @pl.when(end > 1)
        def _():
            line_copy(1, number, paired.at[1, rows(number)], 0).wait_send()

        @pl.when(end == 0)
        def _():
            line_copy(2, number, paired.at[1, rows(number)], 1).wait_send()


def back(x, res, starts, weights, saved, ffn, tokens, residual_grad, gains, piece_length, width):
    model = tokens.shape[1]
    ffn_width = ffn.shape[1]
    sizes = (model, width, ffn_width, piece_length)
    slots = tokens.shape[0]
    block = weights.shape[1:]
    count = Scatter(sizes, 0, 0, None, None).count
    dma = pltpu.SemaphoreType.DMA
    vmem = pl.BlockSpec(memory_space=pltpu.VMEM)
    anywhere = pl.BlockSpec(memory_space=pl.ANY)
    held = lambda value: pltpu.VMEM(value.shape, value.dtype)
    return pl.pallas_call(
        functools.partial(back_kernel, sizes),
        in_specs=[anywhere, anywhere, vmem] + [anywhere] * 5 + [vmem] * 3,
        out_specs=[anywhere, anywhere, vmem, vmem],
        out_shape=[
            jax.ShapeDtypeStruct(weights.shape, low_type),
            jax.ShapeDtypeStruct((4,) + ffn.shape, low_type),
            jax.ShapeDtypeStruct(tokens.shape, low_type),
            jax.ShapeDtypeStruct((8, model // 4), wide),
        ],
        scratch_shapes=[held(x), held(res), held(weights)]
        + [held(value) for value in saved]
        + [
            pltpu.VMEM((4 * slots, 8 * width), low_type),
            pltpu.VMEM((width, 2 * width), wide),
            pltpu.VMEM((8, width), wide),
            pltpu.VMEM(weights.shape, low_type),
            pltpu.VMEM((4 * slots, model), low_type),
            pltpu.VMEM((2,) + block, low_type),
            pltpu.VMEM((3,) + block, low_type),
            pltpu.VMEM(block, low_type),
        ]
        + Reduce.scratch(slots, model)
        + [
            pltpu.VMEM((8, model), wide),
            pltpu.VMEM((8, 8, model), wide),
            pltpu.VMEM((4, 8, model // 4), wide),
            pltpu.VMEM((4, 8, model // 4), wide),
            dma((5, 4)),
            dma((2, 3)),
            dma((2, 3)),
            dma((3, 3)),
            dma((3, 3)),
            dma((6,)),
            dma((6,)),
            dma((5,)),
            dma((12,)),
            dma((3, count)),
            dma((4, count)),
        ],
        compiler_params=pltpu.CompilerParams(
            collective_id=2, has_side_effects=True, vmem_limit_bytes=60 * 1024 * 1024
        ),
        cost_estimate=pl.CostEstimate(
            flops=weights.size * 4 * slots * 4, bytes_accessed=weights.size * 8, transcendentals=0
        ),
        name="back",
    )(x, res, starts, weights, *saved, ffn, tokens, residual_grad, gains)


def adam_kernel(
    sizes,
    mix_ref,
    ffn_ref,
    gain_ref,
    master_ref,
    first_ref,
    second_ref,
    piece_ref,
    new_master_ref,
    new_first_ref,
    new_second_ref,
    rows_ref,
    bias_ref,
    grad,
):
    model, width, ffn_width, piece_length, lines, margin = sizes
    member = lax.axis_index("dp")
    step = pl.program_id(0)
    lead = 128
    start_row = (member * piece_length) // lead
    offset = (member * piece_length) % lead
    tiles_in = 4 * width // lead
    tiles_ffn = 4 * ffn_width // lead
    tiles_model = model // lead

    @pl.when(step == 0)
    def _():
        def clear(number, carry):
            grad[pl.ds(pl.multiple_of(number * 256, 256), 256), :] = jnp.zeros((256, lead), wide)
            return carry

        lax.fori_loop(0, grad.shape[0] // 256, clear, 0)

        def place(row, count, body):
            low = member * piece_length

            @pl.when((row * lead < low + piece_length) & ((row + count) * lead > low))
            def _():
                body(row - start_row + margin)

        base = 0

        def in_unit(number, carry):
            kind = number // tiles_model
            at = number % tiles_model

            def body(to):
                for q in range(4):
                    tile = mix_ref[
                        q,
                        pl.ds(pl.multiple_of(kind * width, width), width),
                        pl.ds(pl.multiple_of(at * lead, lead), lead),
                    ].astype(wide)
                    grad[pl.ds(to + q, lead, stride=tiles_in), :] = tile.T

            place((kind * model + at * lead) * tiles_in, lead * tiles_in, body)
            return carry

        lax.fori_loop(0, 2 * tiles_model, in_unit, 0)
        base = 2 * model * tiles_in

        def gate_body(number, carry):
            kind = number // 4
            q = number % 4

            def body(to):
                grad[pl.ds(to, width), :] = mix_ref[
                    q, pl.ds(pl.multiple_of(kind * width, width), width), model:
                ].astype(wide)

            place(2 * model * tiles_in + number * width, width, body)
            return carry

        lax.fori_loop(0, 8, gate_body, 0)
        base = base + 8 * width
        out_base = base

        quarter = width // 4

        def out_unit(number, carry):
            q = number // 4
            part = number % 4

            def body(to):
                for at in range(tiles_model):
                    grad[pl.ds(to + at, quarter, stride=tiles_model), :] = mix_ref[
                        q,
                        pl.ds(pl.multiple_of(2 * width + part * quarter, quarter), quarter),
                        at * lead : (at + 1) * lead,
                    ].astype(wide)

            place(out_base + number * quarter * tiles_model, quarter * tiles_model, body)
            return carry

        lax.fori_loop(0, 16, out_unit, 0)
        base = base + 4 * width * tiles_model
        up_base = base

        def up_unit(number, carry):
            kind = number // tiles_model
            at = number % tiles_model
            columns = pl.ds(pl.multiple_of(at * lead, lead), lead)

            def body(to):
                for tile in range(tiles_ffn):
                    found = []
                    row = tile * lead
                    while row < (tile + 1) * lead:
                        q = row // ffn_width
                        last = min((q + 1) * ffn_width, (tile + 1) * lead)
                        found.append(
                            ffn_ref[
                                q,
                                kind,
                                row - q * ffn_width : last - q * ffn_width,
                                columns,
                            ].astype(wide)
                        )
                        row = last
                    block = found[0] if len(found) == 1 else jnp.concatenate(found, axis=0)
                    grad[pl.ds(to + tile, lead, stride=tiles_ffn), :] = block.T

            place(up_base + (kind * model + at * lead) * tiles_ffn, lead * tiles_ffn, body)
            return carry

        lax.fori_loop(0, 2 * tiles_model, up_unit, 0)
        base = base + 2 * model * tiles_ffn
        down_base = base
        sixth = ffn_width // 6

        def down_unit(number, carry):
            q = number // 6
            part = number % 6

            def body(to):
                for at in range(tiles_model):
                    grad[pl.ds(to + at, sixth, stride=tiles_model), :] = ffn_ref[
                        q,
                        2,
                        pl.ds(pl.multiple_of(part * sixth, 16), sixth),
                        at * lead : (at + 1) * lead,
                    ].astype(wide)

            place(down_base + number * sixth * tiles_model, sixth * tiles_model, body)
            return carry

        lax.fori_loop(0, 24, down_unit, 0)
        small_base = base + 4 * ffn_width * tiles_model
        smalls = [
            mix_ref[q, 2 * width : 2 * width + 16, model:].astype(wide)
            for q in range(4)
        ]

        def small_body(to):
            for q in range(4):
                grad[pl.ds(to + q, 8, stride=tiles_in), :] = smalls[q][:8]
            for number in range(6):
                kind, at = number // 3, number % 3
                grad[pl.ds(to + 8 * tiles_in + number, 1), :] = gain_ref[
                    kind : kind + 1, at * lead : (at + 1) * lead
                ]

        place(small_base, 8 * tiles_in + 6, small_body)
        bias_ref[...] = jnp.concatenate([small[5:7] for small in smalls], axis=1)

    row = margin + step * lines
    shift = (lead - offset) % lead
    here = pltpu.roll(grad[pl.ds(row, lines), :], shift, 1)
    after = pltpu.roll(grad[pl.ds(row + 1, lines), :], shift, 1)
    lane = lax.broadcasted_iota(jnp.int32, (lines, lead), 1)
    piece = jnp.where(lane < lead - offset, here, after).reshape(1, lines * lead)
    piece_ref[...] = piece
    new_first = beta_one * first_ref[...] + (1.0 - beta_one) * piece
    new_second = beta_two * second_ref[...] + (1.0 - beta_two) * piece * piece
    master = master_ref[...]
    new_master = master - learn_rate * (
        new_first / corr_one / (jnp.sqrt(new_second / corr_two) + adam_eps)
        + weight_decay * master
    )
    new_first_ref[...] = new_first
    new_second_ref[...] = new_second
    new_master_ref[...] = new_master
    rows_ref[0] = new_master.reshape(lines, lead).astype(low_type)


def adam(mix, ffn, gains, master, first, second, sizes, chunks):
    model, width, ffn_width = sizes
    piece_length = master.shape[1]
    lines = -(-piece_length // (chunks * 128 * 16)) * 16
    block = lines * 128
    margin = 1536
    rows = -(-(2 * margin + chunks * lines + 8) // 256) * 256
    packed = jax.ShapeDtypeStruct(master.shape, wide)
    chunk_spec = pl.BlockSpec((1, block), lambda s: (0, s))
    once = lambda shape: pl.BlockSpec(
        shape, lambda s: (0,) * len(shape), pipeline_mode=pl.Buffered(1)
    )
    return pl.pallas_call(
        functools.partial(
            adam_kernel, (model, width, ffn_width, piece_length, lines, margin)
        ),
        grid=(chunks,),
        in_specs=[once(mix.shape), once(ffn.shape), once(gains.shape)] + [chunk_spec] * 3,
        out_specs=[chunk_spec] * 4
        + [
            pl.BlockSpec((1, lines, 128), lambda s: (s, 0, 0)),
            pl.BlockSpec((2, 4 * width), lambda s: (0, 0)),
        ],
        out_shape=[packed] * 4
        + [
            jax.ShapeDtypeStruct((chunks, lines, 128), low_type),
            jax.ShapeDtypeStruct((2, 4 * width), wide),
        ],
        scratch_shapes=[pltpu.VMEM((rows, 128), wide)],
        compiler_params=pltpu.CompilerParams(vmem_limit_bytes=48 * 1024 * 1024),
        cost_estimate=pl.CostEstimate(
            flops=20 * piece_length,
            bytes_accessed=40 * piece_length,
            transcendentals=piece_length,
        ),
        name="adam",
    )(mix, ffn, gains, master, first, second)


def spread_kernel(own_ref, weights_ref, held, spread, load_sem, send_sem, recv_sem):
    chunks, lines, lead = own_ref.shape
    member = lax.axis_index("dp")
    z = lax.axis_index("shard")
    step = pl.program_id(0)

    def copy_to(origin, chunk, side, to):
        return remote(
            held.at[origin, chunk],
            held.at[origin, chunk],
            send_sem.at[side, origin, chunk],
            recv_sem.at[origin, chunk],
            member,
            to,
        )

    def own_load(chunk):
        return pltpu.make_async_copy(own_ref.at[chunk], held.at[z, chunk], load_sem.at[chunk])

    def pass_on(origin, chunk, right):
        copy_to(origin, chunk, 0, z).wait_recv()
        if right:

            @pl.when(z < 3)
            def _():
                copy_to(origin, chunk, 0, z + 1).start()
        else:

            @pl.when(z > 0)
            def _():
                copy_to(origin, chunk, 1, z - 1).start()

    @pl.when(step == 0)
    def _():
        for chunk in range(chunks):
            own_load(chunk).start()
        barrier = pltpu.get_barrier_semaphore()

        @pl.when(z > 0)
        def _():
            pl.semaphore_signal(
                barrier, inc=1, device_id=(member, z - 1), device_id_type=pl.DeviceIdType.MESH
            )

        @pl.when(z < 3)
        def _():
            pl.semaphore_signal(
                barrier, inc=1, device_id=(member, z + 1), device_id_type=pl.DeviceIdType.MESH
            )

        @pl.when((z == 0) | (z == 3))
        def _():
            pl.semaphore_wait(barrier, 1)

        @pl.when((z > 0) & (z < 3))
        def _():
            pl.semaphore_wait(barrier, 2)

        def send_own(chunk, carry):
            own_load(chunk).wait()

            @pl.when(z < 3)
            def _():
                copy_to(z, chunk, 0, z + 1).start()

            @pl.when(z > 0)
            def _():
                copy_to(z, chunk, 1, z - 1).start()

            return carry

        lax.fori_loop(0, chunks, send_own, 0)

        def near(chunk, carry):
            @pl.when(z > 0)
            def _():
                pass_on(z - 1, chunk, True)

            @pl.when(z < 3)
            def _():
                pass_on(z + 1, chunk, False)

            return carry

        lax.fori_loop(0, chunks, near, 0)

    @pl.when(z >= 2)
    def _():
        pass_on(z - 2, step, True)

    @pl.when(z <= 1)
    def _():
        pass_on(z + 2, step, False)

    @pl.when(z == 3)
    def _():
        copy_to(0, step, 0, z).wait_recv()

    @pl.when(z == 0)
    def _():
        copy_to(3, step, 0, z).wait_recv()

    for origin in range(4):
        spread[origin * lines : (origin + 1) * lines, :] = held[origin, step].astype(wide)

    def line(number, carry):
        weights_ref[:, pl.ds(pl.multiple_of(number * lead, lead), lead)] = spread[
            pl.ds(number, 4, stride=lines), :
        ].astype(low_type)
        return carry

    lax.fori_loop(0, lines, line, 0, unroll=8)

    @pl.when(step == chunks - 1)
    def _():
        for origin in range(4):

            def finish(chunk, carry):
                @pl.when((origin <= z) & (z < 3))
                def _():
                    copy_to(origin, chunk, 0, z).wait_send()

                @pl.when((origin >= z) & (z > 0))
                def _():
                    copy_to(origin, chunk, 1, z).wait_send()

                return carry

            lax.fori_loop(0, chunks, finish, 0)


def spread_weights(own, piece_length):
    chunks, lines, lead = own.shape
    return pl.pallas_call(
        spread_kernel,
        grid=(chunks,),
        in_specs=[pl.BlockSpec(memory_space=pl.ANY)],
        out_specs=pl.BlockSpec((4, lines * lead), lambda s: (0, s)),
        out_shape=jax.ShapeDtypeStruct((4, piece_length), low_type),
        scratch_shapes=[
            pltpu.VMEM((4, chunks, lines, lead), low_type),
            pltpu.VMEM((4 * lines, lead), wide),
            pltpu.SemaphoreType.DMA((chunks,)),
            pltpu.SemaphoreType.DMA((2, 4, chunks)),
            pltpu.SemaphoreType.DMA((4, chunks)),
        ],
        compiler_params=pltpu.CompilerParams(
            collective_id=1, has_side_effects=True, vmem_limit_bytes=32 * 1024 * 1024
        ),
        cost_estimate=pl.CostEstimate(
            flops=4 * piece_length, bytes_accessed=16 * piece_length, transcendentals=0
        ),
        name="spread",
    )(own)


def group_body(
    tokens,
    cotangent,
    seq_start,
    live_mask,
    input_proj,
    gate_blocks,
    output_proj,
    ffn_gate_up,
    ffn_down,
    conv_taps,
    gate_bias,
    decay_param,
    norm_gains,
    master_shard,
    first_moment,
    second_moment,
):
    slots, model = tokens.shape
    slice_rec = input_proj.shape[2]
    slice_ffn = ffn_down.shape[0]
    width = slice_rec // 4
    ffn_width = slice_ffn // 4
    piece_length = master_shard.shape[1]
    mask_rows = live_mask.astype(wide)[:, None]
    grad_stream = cotangent.astype(wide) * mask_rows

    starts = jnp.broadcast_to(seq_start.astype(low_type)[:, None], (slots, width))
    (
        mix_in,
        mix_weights,
        ffn_weights,
        saved_p,
        saved_state,
        saved_low,
        all_starts,
        residual,
        ffn_in,
        all_grad_out,
        gains,
    ) = front(
        jnp.concatenate([tokens, starts], axis=1),
        grad_stream.astype(low_type),
        jnp.concatenate([norm_gains, jnp.zeros((14, norm_gains.shape[1]), low_type)]),
        jnp.concatenate(
            [conv_taps, gate_bias, decay_param[None], jnp.zeros((8, slice_rec), low_type)]
        ),
        input_proj,
        gate_blocks,
        output_proj,
        ffn_gate_up,
        ffn_down,
        (model, width, ffn_width),
    )
    ffn_in = ffn_in.reshape(4 * slots, model)
    all_grad_out = all_grad_out.reshape(4 * slots, model)
    sum_ffn, res_low, grad_residual, gain_sums, block_out = middle(
        ffn_in,
        all_grad_out,
        ffn_weights,
        residual,
        gains,
        jnp.broadcast_to(mask_rows.astype(low_type), (slots, width)),
    )
    four_mix, four_ffn, tokens_grad, gain_total = back(
        mix_in,
        res_low.reshape(4 * slots, model),
        all_starts,
        mix_weights,
        (saved_p, saved_state, saved_low),
        sum_ffn,
        tokens,
        grad_residual,
        gain_sums,
        piece_length,
        width,
    )
    piece, new_master, new_first, new_second, rows, bias_total = adam(
        four_mix,
        four_ffn,
        gain_total,
        master_shard,
        first_moment,
        second_moment,
        (model, width, ffn_width),
        8,
    )
    new_weights = spread_weights(rows, piece_length)
    return (
        block_out,
        tokens_grad,
        piece,
        new_master,
        new_first,
        new_second,
        new_weights,
        bias_total,
    )


def rms_scale(values, gain):
    return values * lax.rsqrt(jnp.mean(values * values, axis=-1, keepdims=True) + norm_eps) * gain


def conv_mix(signal, taps, position):
    result = taps[-1] + taps[0] * signal
    for shift_by in range(1, taps.shape[0] - 1):
        moved = jnp.pad(signal, ((shift_by, 0), (0, 0)))[:-shift_by]
        result = result + taps[shift_by] * jnp.where((position >= shift_by)[:, None], moved, 0.0)
    return result


def combine_steps(earlier, later):
    decay_first, value_first = earlier
    decay_second, value_second = later
    return (decay_first * decay_second, decay_second * value_first + value_second)


def recurrence(logits, signal, branch, bias_term, decay_term, position):
    row_count = signal.shape[0]
    recur_gate = jax.nn.sigmoid(logits[0].reshape(row_count, -1) + bias_term[0])
    input_gate = jax.nn.sigmoid(logits[1].reshape(row_count, -1) + bias_term[1])
    log_decay = -gate_scale * recur_gate * jax.nn.softplus(-decay_term)
    decay_rate = jnp.where((position > 0)[:, None], jnp.exp(log_decay), 0.0)
    drive_term = jnp.sqrt(-jnp.expm1(2.0 * log_decay)) * input_gate * signal
    states = lax.associative_scan(combine_steps, (decay_rate, drive_term), axis=0)[1]
    return states * jax.nn.gelu(branch)


def gated_gelu(ffn_pre):
    return jax.nn.gelu(ffn_pre[0]) * ffn_pre[1]


def mixer_forward(
    mix_in, input_proj, gate_blocks, output_proj, conv_taps, gate_bias, decay_param, position
):
    projected = jnp.einsum("sd,kdr->ksr", mix_in, input_proj, preferred_element_type=jnp.float32)
    conv_out, conv_pull = jax.vjp(
        lambda signal, taps: conv_mix(signal, taps, position), projected[0], conv_taps
    )
    row_count = conv_out.shape[0]
    conv_low = conv_out.astype(jnp.bfloat16).reshape(
        row_count, gate_blocks.shape[1], gate_blocks.shape[2]
    )
    gate_logits = jnp.einsum(
        "shb,khbc->kshc", conv_low, gate_blocks, preferred_element_type=jnp.float32
    )
    mixed, mix_pull = jax.vjp(
        lambda logits, signal, branch, bias_term, decay_term: recurrence(
            logits, signal, branch, bias_term, decay_term, position
        ),
        gate_logits,
        conv_out,
        projected[1],
        gate_bias,
        decay_param,
    )
    mixed_low = mixed.astype(jnp.bfloat16)
    partial_out = jnp.dot(mixed_low, output_proj, preferred_element_type=jnp.float32)
    return (partial_out, (conv_pull, conv_low, mix_pull, mixed_low))


def mixer_backward(grad_out_low, mix_in, saved, input_proj, gate_blocks, output_proj):
    conv_pull, conv_low, mix_pull, mixed_low = saved
    grad_output_proj = jnp.einsum(
        "sr,sd->rd", mixed_low, grad_out_low, preferred_element_type=jnp.float32
    )
    grad_mixed = jnp.einsum(
        "sd,rd->sr", grad_out_low, output_proj, preferred_element_type=jnp.float32
    )
    grad_logits, grad_conv_direct, grad_branch, grad_bias, grad_decay = mix_pull(grad_mixed)
    logits_low = grad_logits.astype(jnp.bfloat16)
    grad_blocks = jnp.einsum(
        "shb,kshc->khbc", conv_low, logits_low, preferred_element_type=jnp.float32
    )
    grad_conv_gates = jnp.einsum(
        "kshc,khbc->shb", logits_low, gate_blocks, preferred_element_type=jnp.float32
    )
    grad_signal, grad_taps = conv_pull(
        grad_conv_direct + grad_conv_gates.reshape(grad_conv_direct.shape)
    )
    proj_low = jnp.stack([grad_signal, grad_branch]).astype(jnp.bfloat16)
    grad_input_proj = jnp.einsum(
        "sd,ksr->kdr", mix_in, proj_low, preferred_element_type=jnp.float32
    )
    grad_mix_in = jnp.einsum(
        "ksr,kdr->sd", proj_low, input_proj, preferred_element_type=jnp.float32
    )
    return (
        grad_mix_in,
        (grad_input_proj, grad_blocks, grad_output_proj, grad_taps, grad_bias, grad_decay),
    )


def ffn_forward(ffn_in_low, ffn_gate_up, ffn_down):
    ffn_pre = jnp.einsum("sd,kdf->ksf", ffn_in_low, ffn_gate_up, preferred_element_type=jnp.float32)
    ffn_act, ffn_pull = jax.vjp(gated_gelu, ffn_pre)
    ffn_low = ffn_act.astype(jnp.bfloat16)
    partial_ffn = jnp.dot(ffn_low, ffn_down, preferred_element_type=jnp.float32)
    return (partial_ffn, (ffn_pull, ffn_low))


def ffn_backward(grad_low, ffn_in_low, saved, ffn_gate_up, ffn_down):
    ffn_pull, ffn_low = saved
    grad_down = jnp.einsum("sf,sd->fd", ffn_low, grad_low, preferred_element_type=jnp.float32)
    grad_act = jnp.einsum("sd,fd->sf", grad_low, ffn_down, preferred_element_type=jnp.float32)
    grad_pre = ffn_pull(grad_act)[0]
    pre_low = grad_pre.astype(jnp.bfloat16)
    grad_gate_up = jnp.einsum(
        "sd,ksf->kdf", ffn_in_low, pre_low, preferred_element_type=jnp.float32
    )
    grad_ffn_in = jnp.einsum(
        "ksf,kdf->sd", pre_low, ffn_gate_up, preferred_element_type=jnp.float32
    )
    return (grad_ffn_in, grad_gate_up, grad_down)


def body(
    tokens,
    cotangent,
    seq_start,
    live_mask,
    input_proj,
    gate_blocks,
    output_proj,
    ffn_gate_up,
    ffn_down,
    conv_taps,
    gate_bias,
    decay_param,
    norm_gains,
    master_shard,
    first_moment,
    second_moment,
):
    slot_count = tokens.shape[0]
    position = jnp.arange(slot_count, dtype=jnp.int32) - seq_start
    mask_rows = live_mask.astype(jnp.float32)[:, None]
    stream = tokens.astype(jnp.float32)
    grad_stream = cotangent.astype(jnp.float32) * mask_rows
    shards = (
        input_proj,
        gate_blocks,
        output_proj,
        ffn_gate_up,
        ffn_down,
        conv_taps,
        gate_bias,
        decay_param,
        norm_gains,
    )
    (
        full_in,
        full_blocks,
        full_out,
        full_up,
        full_down,
        full_taps,
        full_bias,
        full_decay,
        full_gains,
    ) = (
        lax.all_gather(shards[0], "shard", axis=2, tiled=True),
        lax.all_gather(shards[1], "shard", axis=1, tiled=True),
        lax.all_gather(shards[2], "shard", axis=0, tiled=True),
        lax.all_gather(shards[3], "shard", axis=2, tiled=True),
        lax.all_gather(shards[4], "shard", axis=0, tiled=True),
        lax.all_gather(shards[5], "shard", axis=1, tiled=True),
        lax.all_gather(shards[6], "shard", axis=1, tiled=True),
        lax.all_gather(shards[7], "shard", axis=0, tiled=True),
        lax.all_gather(shards[8], "shard", axis=1, tiled=True),
    )
    gains = full_gains.astype(jnp.float32)
    normed, norm_pull = jax.vjp(rms_scale, stream, gains[0])
    mix_in = normed.astype(jnp.bfloat16)
    mix_out, mix_saved = mixer_forward(
        mix_in,
        full_in,
        full_blocks,
        full_out,
        full_taps.astype(jnp.float32),
        full_bias.astype(jnp.float32),
        full_decay.astype(jnp.float32),
        position,
    )
    residual = stream + mix_out
    normed_two, second_pull = jax.vjp(rms_scale, residual, gains[1])
    ffn_in_low = normed_two.astype(jnp.bfloat16)
    ffn_result, ffn_saved = ffn_forward(ffn_in_low, full_up, full_down)
    block_out = (mask_rows * (residual + ffn_result)).astype(jnp.bfloat16)
    grad_ffn_in, grad_up, grad_down = ffn_backward(
        grad_stream.astype(jnp.bfloat16), ffn_in_low, ffn_saved, full_up, full_down
    )
    grad_norm_two, grad_gain_two = second_pull(grad_ffn_in)
    grad_residual = grad_stream + grad_norm_two
    grad_mix_in, mix_grads = mixer_backward(
        grad_residual.astype(jnp.bfloat16), mix_in, mix_saved, full_in, full_blocks, full_out
    )
    grad_norm_one, grad_gain_one = norm_pull(grad_mix_in)
    tokens_grad = (grad_residual + grad_norm_one).astype(jnp.bfloat16)
    grads = (
        mix_grads[0],
        mix_grads[1],
        mix_grads[2],
        grad_up,
        grad_down,
        mix_grads[3],
        mix_grads[4],
        mix_grads[5],
        jnp.stack([grad_gain_one, grad_gain_two]),
    )
    summed = (
        lax.psum_scatter(
            grads[0].astype(jnp.bfloat16), "shard", scatter_dimension=2, tiled=True
        ).astype(jnp.float32),
        lax.psum_scatter(
            grads[1].astype(jnp.bfloat16), "shard", scatter_dimension=1, tiled=True
        ).astype(jnp.float32),
        lax.psum_scatter(
            grads[2].astype(jnp.bfloat16), "shard", scatter_dimension=0, tiled=True
        ).astype(jnp.float32),
        lax.psum_scatter(
            grads[3].astype(jnp.bfloat16), "shard", scatter_dimension=2, tiled=True
        ).astype(jnp.float32),
        lax.psum_scatter(
            grads[4].astype(jnp.bfloat16), "shard", scatter_dimension=0, tiled=True
        ).astype(jnp.float32),
        lax.psum_scatter(
            grads[5].astype(jnp.bfloat16), "shard", scatter_dimension=1, tiled=True
        ).astype(jnp.float32),
        lax.psum_scatter(
            grads[6].astype(jnp.bfloat16), "shard", scatter_dimension=1, tiled=True
        ).astype(jnp.float32),
        lax.psum_scatter(
            grads[7].astype(jnp.bfloat16), "shard", scatter_dimension=0, tiled=True
        ).astype(jnp.float32),
        lax.psum_scatter(
            grads[8].astype(jnp.bfloat16), "shard", scatter_dimension=1, tiled=True
        ).astype(jnp.float32),
    )
    flat = jnp.concatenate([member.reshape(1, -1) for member in summed], axis=1)
    piece = lax.psum_scatter(flat, "dp", scatter_dimension=1, tiled=True)
    bias_total = lax.psum(summed[6], "dp")
    new_first = beta_one * first_moment + (1.0 - beta_one) * piece
    new_second = beta_two * second_moment + (1.0 - beta_two) * piece * piece
    new_master = master_shard - learn_rate * (
        new_first / corr_one / (jnp.sqrt(new_second / corr_two) + adam_eps)
        + weight_decay * master_shard
    )
    new_weights = lax.all_gather(new_master.astype(jnp.bfloat16), "shard", axis=0, tiled=True)
    return (
        block_out,
        tokens_grad,
        piece,
        new_master,
        new_first,
        new_second,
        new_weights,
        bias_total,
    )


def solution(mesh):
    fits = mesh.shape["dp"] == 8 and mesh.shape["shard"] == 4
    placed = (
        P(("dp", "shard"), None),
        P(("dp", "shard"), None),
        P(("dp", "shard")),
        P(("dp", "shard")),
        P(None, None, "shard"),
        P(None, "shard", None, None),
        P("shard", None),
        P(None, None, "shard"),
        P("shard", None),
        P(None, "shard"),
        P(None, "shard"),
        P("shard"),
        P(None, "shard"),
        P("shard", "dp"),
        P("shard", "dp"),
        P("shard", "dp"),
    )
    return jax.shard_map(
        group_body if fits else body,
        mesh=mesh,
        in_specs=placed,
        out_specs=(
            P(("dp", "shard"), None),
            P(("dp", "shard"), None),
            P("shard", "dp"),
            P("shard", "dp"),
            P("shard", "dp"),
            P("shard", "dp"),
            P(None, "dp"),
            P(None, "shard"),
        ),
        check_vma=False,
    )
```

```python
import functools
import jax
import jax.numpy as jnp
from jax import lax
from jax.experimental import pallas as pl
from jax.experimental.pallas import tpu as pltpu
from jax.sharding import PartitionSpec as P

norm_eps = 1e-06
gate_scale = 8.0
beta_one = 0.9
beta_two = 0.95
learn_rate = 0.01
weight_decay = 0.1
adam_eps = 1e-08
corr_one = 1.0 - beta_one**10.0
corr_two = 1.0 - beta_two**10.0
low_type = jnp.bfloat16
wide = jnp.float32
gelu_scale = 0.7978845608028654
gelu_cube = 0.044715


def add_low(left, right):
    return (left.astype(wide) + right.astype(wide)).astype(low_type)


def dot_rows(left, right):
    return lax.dot_general(left, right, (((1,), (1,)), ((), ())), preferred_element_type=wide)


def dot_plain(left, right):
    return lax.dot_general(left, right, (((1,), (0,)), ((), ())), preferred_element_type=wide)


def dot_slots(left, right):
    return lax.dot_general(left, right, (((0,), (0,)), ((), ())), preferred_element_type=wide)


def gelu_parts(value):
    square = value * value
    bent = jnp.tanh(gelu_scale * value * (1.0 + gelu_cube * square))
    half = 0.5 * (1.0 + bent)
    slope = half + 0.5 * value * (1.0 - bent * bent) * gelu_scale * (
        1.0 + 3.0 * gelu_cube * square
    )
    return (value * half, slope)


def shift_down(value, step):
    if step % 8 == 0:
        return jnp.concatenate([value[-step:], value[:-step]], axis=0)
    return pltpu.roll(value, step, 0)


def shift_up(value, step):
    if step % 8 == 0:
        return jnp.concatenate([value[step:], value[:step]], axis=0)
    return pltpu.roll(value, value.shape[0] - step, 0)


def scan_slots(decay, value, shift):
    step = 1
    while step < value.shape[0]:
        value = value + decay * shift(value, step)
        if 2 * step < value.shape[0]:
            decay = decay * shift(decay, step)
        step *= 2
    return value


def one_minus_exp(value):
    series = jnp.ones_like(value)
    for number in range(11, 1, -1):
        series = 1.0 - value * (1.0 / number) * series
    return jnp.where(value < 0.8, value * series, 1.0 - jnp.exp(-value))


def soft_plus(value):
    return jnp.maximum(value, 0.0) + jnp.log1p(jnp.exp(-jnp.abs(value)))


def mixer_parts(first, position, small, gates):
    conv_out = small[4:5] + small[0:1] * first
    shifted = []
    for step in range(1, 4):
        moved = jnp.where(position >= step, shift_down(first, step), 0.0)
        shifted.append(moved)
        conv_out = conv_out + small[step : step + 1] * moved
    conv_low = conv_out.astype(low_type)
    logits = dot_plain(conv_low, gates)
    width = first.shape[1]
    recur_gate = jax.nn.sigmoid(logits[:, :width] + small[5:6])
    input_gate = jax.nn.sigmoid(logits[:, width:] + small[6:7])
    rate = gate_scale * soft_plus(-small[7:8])
    log_decay = -rate * recur_gate
    decay = jnp.where(position > 0, jnp.exp(log_decay), 0.0)
    gone = one_minus_exp(-2.0 * log_decay)
    root = jnp.sqrt(gone)
    return conv_out, shifted, conv_low, recur_gate, input_gate, rate, decay, gone, root


def weight_views(w_ref, width):
    model = w_ref.shape[2] - width
    proj = w_ref[0, 0 : 2 * width, 0:model]
    out = w_ref[0, 2 * width : 3 * width, 0:model]
    gates = jnp.concatenate(
        [w_ref[0, 0:width, model:], w_ref[0, width : 2 * width, model:]], axis=1
    )
    small = w_ref[0, 2 * width : 2 * width + 16, model:].astype(wide)
    return proj, out, gates, small


def slot_position(starts):
    slot = lax.broadcasted_iota(jnp.int32, (starts.shape[0], 1), 0)
    return slot - starts[:, 0:1].astype(wide).astype(jnp.int32)


def mixer_step(x, position, views, width):
    proj, out, gates, small = views
    projected = dot_rows(x, proj)
    conv_out, _, _, _, input_gate, _, decay, _, root = mixer_parts(
        projected[:, :width], position, small, gates
    )
    states = scan_slots(decay, root * input_gate * conv_out, shift_down)
    mixed_low = (states * gelu_parts(projected[:, width:])[0]).astype(low_type)
    return projected, states, mixed_low, dot_plain(mixed_low, out)


def mixer_back_step(position, views, projected, states, res_low, width):
    _, out, gates, small = views
    first = projected[:, :width]
    conv_out, shifted, conv_low, recur_gate, input_gate, rate, decay, gone, root = mixer_parts(
        first, position, small, gates
    )
    grad_mixed = dot_rows(res_low, out)
    active, slope = gelu_parts(projected[:, width:])
    grad_second = grad_mixed * states * slope
    adjoint = scan_slots(shift_up(decay, 1), grad_mixed * active, shift_up)
    grad_decay = adjoint * shift_down(states, 1)
    gated = adjoint * conv_out
    grad_root = gated * input_gate
    grad_input_gate = gated * root
    grad_conv = adjoint * root * input_gate
    grad_log = grad_decay * decay - grad_root * (1.0 - gone) / root
    grad_recur = -rate * grad_log
    grad_logit_a = grad_recur * recur_gate * (1.0 - recur_gate)
    grad_logit_b = grad_input_gate * input_gate * (1.0 - input_gate)
    grad_param = jnp.sum(grad_log * recur_gate, axis=0, keepdims=True) * (
        gate_scale * jax.nn.sigmoid(-small[7:8])
    )
    logits_low = jnp.concatenate([grad_logit_a, grad_logit_b], axis=1).astype(low_type)
    grad_conv = grad_conv + dot_rows(logits_low, gates)
    grad_gates = dot_slots(conv_low, logits_low)
    sums = [jnp.sum(grad_conv * first, axis=0, keepdims=True)]
    grad_first = small[0:1] * grad_conv
    for step in range(1, 4):
        sums.append(jnp.sum(grad_conv * shifted[step - 1], axis=0, keepdims=True))
        kept = jnp.where(position >= step, grad_conv, 0.0)
        grad_first = grad_first + small[step : step + 1] * shift_up(kept, step)
    sums.append(jnp.sum(grad_conv, axis=0, keepdims=True))
    sums.append(jnp.sum(grad_logit_a, axis=0, keepdims=True))
    sums.append(jnp.sum(grad_logit_b, axis=0, keepdims=True))
    sums.append(grad_param)
    proj_low = jnp.concatenate([grad_first, grad_second], axis=1).astype(low_type)
    return proj_low, grad_gates, jnp.concatenate(sums, axis=0)


def peer_x(chip):
    return chip + 1 - 2 * (chip % 2)


def peer_y(chip):
    return chip + 2 - 4 * (chip // 2)


def line_place(end, core):
    return end + core * (3 - 2 * end)


def remote(source, target, send, recv, member, z):
    return pltpu.make_async_remote_copy(
        src_ref=source,
        dst_ref=target,
        send_sem=send,
        recv_sem=recv,
        device_id=(member, z),
        device_id_type=pl.DeviceIdType.MESH,
    )


def enter(member, z):
    barrier = pltpu.get_barrier_semaphore()
    for other in range(8):

        @pl.when(member != other)
        def _():
            pl.semaphore_signal(
                barrier, inc=1, device_id=(other, z), device_id_type=pl.DeviceIdType.MESH
            )

    for other in range(4):

        @pl.when(z != other)
        def _():
            pl.semaphore_signal(
                barrier, inc=1, device_id=(member, other), device_id_type=pl.DeviceIdType.MESH
            )

    pl.semaphore_wait(barrier, 10)


class Gather:
    def __init__(self, own, target, send, recv, member, z):
        self.own, self.target = own, target
        self.send, self.recv = send, recv
        chip, core = member // 2, member % 2
        self.to_x = peer_x(chip) * 2 + core
        self.to_y = peer_y(chip) * 2 + core
        self.z = z
        self.half = own.shape[0] // 2

    def copy(self, number):
        low, high = pl.ds(0, self.half), pl.ds(self.half, self.half)
        source, target, to = (
            (self.own, self.target.at[1], self.to_x),
            (self.own, self.target.at[2], self.to_y),
            (self.target.at[1, low], self.target.at[3, low], self.to_y),
            (self.target.at[2, high], self.target.at[3, high], self.to_x),
        )[number]
        return remote(source, target, self.send.at[number], self.recv.at[number], to, self.z)

    def begin(self):
        self.copy(0).start()
        self.copy(1).start()

    def relay(self):
        self.copy(0).wait_recv()
        self.copy(2).start()
        self.copy(1).wait_recv()
        self.copy(3).start()

    def arrive(self):
        self.copy(2).wait_recv()
        self.copy(3).wait_recv()

    def finish(self):
        for number in range(4):
            self.copy(number).wait_send()


class Reduce:
    def __init__(self, part, from_x, from_y, passing, last, send, recv, member, z):
        self.part, self.from_x, self.from_y = part, from_x, from_y
        self.passing, self.last = passing, last
        self.send, self.recv = send, recv
        chip, core = member // 2, member % 2
        self.to_x = peer_x(chip) * 2 + core
        self.to_y = peer_y(chip) * 2 + core
        self.z = z
        self.slots = part.shape[0] // 4
        self.half = self.slots // 2

    def copy(self, number):
        slots, half = self.slots, self.half
        source, target, to = (
            (self.part.at[pl.ds(slots, half)], self.from_x.at[0], self.to_x),
            (self.part.at[pl.ds(3 * slots, half)], self.from_x.at[1], self.to_x),
            (self.part.at[pl.ds(2 * slots + half, half)], self.from_y.at[0], self.to_y),
            (self.part.at[pl.ds(3 * slots + half, half)], self.from_y.at[1], self.to_y),
            (self.passing.at[0], self.last.at[0], self.to_y),
            (self.passing.at[1], self.last.at[1], self.to_x),
        )[number]
        return remote(source, target, self.send.at[number], self.recv.at[number], to, self.z)

    def begin(self):
        for block in (3, 1, 2):
            self.begin_block(block)

    def begin_block(self, block):
        for number in {1: (0,), 2: (2,), 3: (1, 3)}.get(block, ()):
            self.copy(number).start()

    def relay(self):
        slots, half = self.slots, self.half
        self.copy(1).wait_recv()
        self.passing[0] = (
            self.part[2 * slots : 2 * slots + half].astype(wide) + self.from_x[1].astype(wide)
        ).astype(low_type)
        self.copy(4).start()
        self.copy(3).wait_recv()
        self.passing[1] = (
            self.part[slots + half : 2 * slots].astype(wide) + self.from_y[1].astype(wide)
        ).astype(low_type)
        self.copy(5).start()

    def arrive(self):
        for number in (0, 2, 4, 5):
            self.copy(number).wait_recv()

    def result(self, number):
        direct = self.from_x if number == 0 else self.from_y
        return (
            self.part[number * self.half : (number + 1) * self.half].astype(wide)
            + direct[0].astype(wide)
            + self.last[number].astype(wide)
        )

    def finish(self):
        for number in range(6):
            self.copy(number).wait_send()

    @staticmethod
    def scratch(slots, model):
        return [pltpu.VMEM((2, slots // 2, model), low_type)] * 4


def norm_rows(value, gain):
    scale = lax.rsqrt(jnp.mean(value * value, axis=1, keepdims=True) + norm_eps)
    return value * scale * gain


def front_kernel(
    sizes,
    tokens_ref,
    cot_ref,
    gain_ref,
    small_ref,
    in_ref,
    gate_ref,
    out_ref,
    up_ref,
    down_ref,
    mix_in,
    weights,
    ffn_weights,
    saved_p,
    saved_state,
    saved_low,
    starts_out,
    residual_out,
    ffn_in,
    cot_out,
    gains_out,
    tokens_all,
    raw_in,
    raw_up,
    raw_down,
    turned,
    gain_seen,
    acc,
    part,
    from_x,
    from_y,
    passing,
    last,
    load_sem,
    gain_send,
    gain_recv,
    m_send,
    m_recv,
    m_core_send,
    m_core_recv,
    f_send,
    f_recv,
    f_core_send,
    f_core_recv,
    g_send,
    g_recv,
    r_send,
    r_recv,
):
    model, width, ffn_width = sizes
    member = lax.axis_index("dp")
    z = lax.axis_index("shard")
    chip, core = member // 2, member % 2
    end = z + core * (3 - 2 * z)
    other = chip * 2 + 1 - core
    slots = cot_ref.shape[0]
    half_ffn = ffn_width // 2
    owner = core == z // 2

    window = 128 * ((chip * ffn_width) // 128)
    skew = chip * ffn_width - window
    quarter = pl.ds(pl.multiple_of(chip * width, width), width)
    wide_window = pl.ds(pl.multiple_of(window, 128), raw_up.shape[2])

    def loads():
        found = [
            (out_ref.at[quarter], weights.at[end, pl.ds(2 * width, width), pl.ds(0, model)]),
            (
                small_ref.at[:, quarter],
                weights.at[end, pl.ds(2 * width, 16), pl.ds(model, width)],
            ),
        ]
        for kind in range(2):
            found.append((in_ref.at[kind, :, quarter], raw_in.at[kind]))
            found.append(
                (
                    gate_ref.at[kind, chip],
                    weights.at[end, pl.ds(kind * width, width), pl.ds(model, width)],
                )
            )
        found.append(
            (down_ref.at[pl.ds(pl.multiple_of(chip * ffn_width, 32), ffn_width)], raw_down)
        )
        for kind in range(2):
            found.append((up_ref.at[kind, :, wide_window], raw_up.at[kind]))
        return [
            pltpu.make_async_copy(source, target, load_sem.at[number])
            for number, (source, target) in enumerate(found)
        ]

    def turned_copy(kind):
        return pltpu.make_async_copy(
            raw_down
            if kind == 2
            else turned.at[kind, pl.ds(pl.multiple_of(skew, 32), ffn_width)],
            ffn_weights.at[kind, pl.ds(pl.multiple_of(2 * end * ffn_width, 32), ffn_width)],
            load_sem.at[9 + kind],
        )

    @pl.when(owner)
    def _():
        for copy in loads():
            copy.start()

    enter(member, z)

    gather_tokens = Gather(tokens_ref, tokens_all, g_send.at[0], g_recv.at[0], member, z)
    gather_cot = Gather(cot_ref, cot_out, g_send.at[1], g_recv.at[1], member, z)
    gather_ffn = Gather(ffn_in.at[0], ffn_in, g_send.at[2], g_recv.at[2], member, z)
    reduce = Reduce(part, from_x, from_y, passing, last, r_send, r_recv, member, z)
    own_cot = pltpu.make_async_copy(cot_ref, cot_out.at[0], load_sem.at[12])

    gather_tokens.begin()
    own_cot.start()

    def gain_copy(to, slot):
        return remote(
            gain_ref, gain_seen.at[slot], gain_send.at[to], gain_recv.at[slot], member, to
        )

    for to in range(4):

        @pl.when(to != z)
        def _():
            gain_copy(to, z).start()

    gain_seen[z] = gain_ref[...]

    def m_rows(number):
        return pl.ds(number * width, width)

    def m_copy(slot, number, way, to_end):
        place = weights.at[slot, m_rows(number)]
        return remote(
            place,
            place,
            m_send.at[way, slot, number],
            m_recv.at[slot, number],
            member,
            line_place(to_end, core),
        )

    def m_core(slot, number):
        return remote(
            weights.at[slot, m_rows(number)],
            weights.at[2 + slot, m_rows(number)],
            m_core_send.at[slot, number],
            m_core_recv.at[slot, number],
            other,
            z,
        )

    def f_place(slot, number):
        row = ((slot % 2) * 2 + slot // 2) * ffn_width + (number % 2) * half_ffn
        return ffn_weights.at[number // 2, pl.ds(row, half_ffn)]

    def f_copy(slot, number, way, to_end):
        place = f_place(slot, number)
        return remote(
            place,
            place,
            f_send.at[way, slot, number],
            f_recv.at[slot, number],
            member,
            line_place(to_end, core),
        )

    def f_core(slot, number):
        return remote(
            f_place(slot, number),
            f_place(2 + slot, number),
            f_core_send.at[slot, number],
            f_core_recv.at[slot, number],
            other,
            z,
        )

    def pass_on(copy, core_copy, slot, number):
        if slot == 0:

            @pl.when(end < 3)
            def _():
                copy(slot, number, 0, end + 1).start()
        else:

            @pl.when((end == 1) | (end == 2))
            def _():
                copy(slot, number, 0, end + 1).start()

        core_copy(slot, number).start()

    def pass_back(copy, numbers):
        @pl.when(end == 1)
        def _():
            for number in numbers:
                copy(1, number, 1, 0).start()

    def start_own(copy, core_copy, numbers):
        for slot in range(2):

            @pl.when(end == slot)
            def _():
                for number in numbers:
                    pass_on(copy, core_copy, slot, number)

    def turn_in(kind):
        @pl.when(owner)
        def _():
            for copy in loads()[2 + 2 * kind : 4 + 2 * kind]:
                copy.wait()

            def turn(at, carry):
                columns = pl.ds(pl.multiple_of(at * 256, 256), 256)
                weights[end, kind * width : (kind + 1) * width, columns] = raw_in[
                    kind, columns, :
                ].T
                return carry

            lax.fori_loop(0, model // 256, turn, 0)

        start_own(m_copy, m_core, (kind,))
        pass_back(m_copy, (kind,))

    def turn_up(kind):
        @pl.when(owner)
        def _():
            loads()[7 + kind].wait()

            def turn(at, carry):
                columns = pl.ds(pl.multiple_of(at * 256, 256), 256)
                turned[kind, :, columns] = raw_up[kind, columns, :].T
                return carry

            lax.fori_loop(0, model // 256, turn, 0)
            turned_copy(kind).start()

    @pl.when(owner)
    def _():
        for copy in loads()[:2]:
            copy.wait()
        for row in range(2 * width + 16, 3 * width, 16):
            weights[end, row : row + 16, model:] = jnp.zeros((16, width), low_type)

    start_own(m_copy, m_core, (2,))
    pass_back(m_copy, (2,))
    turn_in(0)
    turn_in(1)

    @pl.when(owner)
    def _():
        loads()[6].wait()
        turned_copy(2).start()

    turn_up(0)
    turn_up(1)
    gather_tokens.relay()
    m_order = (2, 0, 1)

    @pl.when(end < 3)
    def _():
        for number in m_order:
            for slot in (1, 0):

                @pl.when(end != slot)
                def _():
                    m_copy(slot, number, 0, 0).wait_recv()
                    pass_on(m_copy, m_core, slot, number)

    @pl.when(owner)
    def _():
        for kind in range(3):
            turned_copy(kind).wait()

    f_order = (4, 5, 0, 1, 2, 3)
    start_own(f_copy, f_core, f_order)

    def f_pass(slot, numbers):
        for number in numbers:
            f_copy(slot, number, 0, 0).wait_recv()
            pass_on(f_copy, f_core, slot, number)

    def f_step(step):
        @pl.when(end == 1)
        def _():
            f_pass(0, ((), (4, 5), (0, 1), (2, 3), (), ())[step])

        @pl.when(end == 2)
        def _():
            f_pass(1, ((4,), (5, 0), (1, 2), (3,), (), ())[step])
            f_pass(0, ((), (), (), (4,), (5, 0), (1, 2, 3))[step])

        if step == 0:
            pass_back(f_copy, f_order)

        @pl.when(end == 0)
        def _():
            f_pass(1, ((), (), (), (), (), f_order)[step])

    for to in range(4):

        @pl.when(to != z)
        def _():
            gain_copy(to, to).wait_recv()

    gains = jnp.concatenate([gain_seen[at].astype(wide) for at in range(4)], axis=1)
    gains_out[...] = gains[0:8]
    gather_tokens.arrive()

    def norm_block(block):
        if block == 0:
            source, starts = tokens_ref[:, :model], tokens_ref[:, model:]
        else:
            source, starts = tokens_all[block, :, :model], tokens_all[block, :, model:]
        at = slice(block * slots, (block + 1) * slots)
        mix_in[at, :] = norm_rows(source.astype(wide), gains_out[0:1]).astype(low_type)
        starts_out[at, :] = starts

    for block in range(4):
        norm_block(block)
    gather_cot.begin()
    f_step(0)

    late = end >= 2
    for turn in range(4):
        head = (turn + 2 * late) % 4
        if turn == 2:

            @pl.when(end == 3)
            def _():
                for number in m_order:
                    for slot in (1, 0):
                        m_copy(slot, number, 0, 0).wait_recv()
                        m_core(slot, number).start()

        @pl.when(head >= 2)
        def _():
            for number in m_order:
                m_core(head - 2, number).wait_recv()

        views = weight_views(weights.at[pl.ds(head, 1)], width)

        def step_block(block, carry):
            rows = pl.ds(pl.multiple_of(block * slots, slots), slots)
            position = slot_position(starts_out[rows, :])
            projected, states, mixed_low, product = mixer_step(
                mix_in[rows, :], position, views, width
            )
            saved_p[head, rows, :] = projected
            saved_state[head, rows, :] = states
            saved_low[head, rows, :] = mixed_low
            if turn == 0:
                acc[rows, :] = product
            elif turn < 3:
                acc[rows, :] += product
            else:
                part[rows, :] = (acc[rows, :] + product).astype(low_type)
            return carry

        lax.fori_loop(0, 4, step_block, 0)
        if turn == 3:
            reduce.begin()
        f_step(turn + 1)
        if turn == 0:
            gather_cot.relay()

    reduce.relay()
    f_step(5)
    reduce.arrive()
    half = slots // 2
    for number in range(2):
        at = slice(number * half, (number + 1) * half)
        residual = tokens_ref[at, :model].astype(wide) + reduce.result(number)
        residual_out[at, :] = residual
        ffn_in[0, at, :] = norm_rows(residual, gains_out[1:2]).astype(low_type)
    gather_ffn.begin()
    gather_ffn.relay()

    @pl.when(end == 3)
    def _():
        for slot in (1, 0):
            for number in f_order:
                f_copy(slot, number, 0, 0).wait_recv()
                f_core(slot, number).start()

    gather_ffn.arrive()
    gather_cot.arrive()
    own_cot.wait()
    for slot in range(2):
        for number in range(6):
            f_core(slot, number).wait_recv()

    for gather in (gather_tokens, gather_cot, gather_ffn, reduce):
        gather.finish()
    for to in range(4):

        @pl.when(to != z)
        def _():
            gain_copy(to, z).wait_send()

    for copy, core_copy, count in ((m_copy, m_core, 3), (f_copy, f_core, 6)):
        for number in range(count):
            for slot in range(2):
                core_copy(slot, number).wait_send()

            @pl.when(end < 3)
            def _():
                copy(0, number, 0, 0).wait_send()

            @pl.when((end == 1) | (end == 2))
            def _():
                copy(1, number, 0, 0).wait_send()

            @pl.when(end == 1)
            def _():
                copy(1, number, 1, 0).wait_send()


def front(tokens, cot, gains, small, in_proj, gates, out_proj, gate_up, down, sizes):
    model, width, ffn_width = sizes
    slots = cot.shape[0]
    rows = 4 * slots
    dma = pltpu.SemaphoreType.DMA
    vmem = pl.BlockSpec(memory_space=pltpu.VMEM)
    anywhere = pl.BlockSpec(memory_space=pl.ANY)
    window = -(-ffn_width // 128) * 128
    return pl.pallas_call(
        functools.partial(front_kernel, sizes),
        in_specs=[vmem] * 3 + [anywhere] * 6,
        out_specs=[vmem, vmem, anywhere, vmem, vmem, vmem, vmem, vmem, vmem, anywhere, vmem],
        out_shape=[
            jax.ShapeDtypeStruct((rows, model), low_type),
            jax.ShapeDtypeStruct((4, 3 * width, model + width), low_type),
            jax.ShapeDtypeStruct((3, 4 * ffn_width, model), low_type),
            jax.ShapeDtypeStruct((4, rows, 2 * width), wide),
            jax.ShapeDtypeStruct((4, rows, width), wide),
            jax.ShapeDtypeStruct((4, rows, width), low_type),
            jax.ShapeDtypeStruct((rows, width), low_type),
            jax.ShapeDtypeStruct((slots, model), wide),
            jax.ShapeDtypeStruct((4, slots, model), low_type),
            jax.ShapeDtypeStruct((4, slots, model), low_type),
            jax.ShapeDtypeStruct((8, model), wide),
        ],
        scratch_shapes=[
            pltpu.VMEM((4, slots, model + width), low_type),
            pltpu.VMEM((2, model, width), low_type),
            pltpu.VMEM((2, model, window), low_type),
            pltpu.VMEM((ffn_width, model), low_type),
            pltpu.VMEM((2, window, model), low_type),
            pltpu.VMEM((4, 16, model // 4), low_type),
            pltpu.VMEM((rows, model), wide),
            pltpu.VMEM((rows, model), low_type),
        ]
        + Reduce.scratch(slots, model)
        + [
            dma((13,)),
            dma((4,)),
            dma((4,)),
            dma((2, 2, 3)),
            dma((2, 3)),
            dma((2, 3)),
            dma((2, 3)),
            dma((2, 2, 6)),
            dma((2, 6)),
            dma((2, 6)),
            dma((2, 6)),
            dma((3, 4)),
            dma((3, 4)),
            dma((6,)),
            dma((6,)),
        ],
        compiler_params=pltpu.CompilerParams(
            collective_id=3, has_side_effects=True, vmem_limit_bytes=60 * 1024 * 1024
        ),
        cost_estimate=pl.CostEstimate(
            flops=2 * rows * model * 4 * width * 3,
            bytes_accessed=6 * ffn_width * 4 * model,
            transcendentals=rows * 4 * width * 6,
        ),
        name="front",
    )(tokens, cot, gains, small, in_proj, gates, out_proj, gate_up, down)


def middle_kernel(
    sizes,
    x_ref,
    go_ref,
    weights_ref,
    residual_ref,
    gain_ref,
    total,
    inner_down,
    res_low,
    res_out,
    gain_out,
    part_out,
    held,
    lows,
    paired,
    arrived,
    part_in,
    in_x,
    in_y,
    in_pass,
    in_last,
    load_sem,
    core_send,
    core_recv,
    line_send,
    line_recv,
    i_send,
    i_recv,
    g_send,
    g_recv,
):
    model, ffn_width = sizes
    member = lax.axis_index("dp")
    z = lax.axis_index("shard")
    chip, core = member // 2, member % 2
    end = z + core * (3 - 2 * z)
    other = chip * 2 + 1 - core
    slots = residual_ref.shape[0]
    half = slots // 2
    hidden = 4 * ffn_width
    half_ffn = ffn_width // 2

    loads = [
        pltpu.make_async_copy(weights_ref.at[kind], held.at[kind], load_sem.at[kind])
        for kind in range(3)
    ]
    for load in loads:
        load.start()
    enter(member, z)
    for load in loads:
        load.wait()

    split = -(-2 * ffn_width // 128) * 128

    def block_step(low, high, block, carry):
        rows = pl.ds(pl.multiple_of(block * slots, slots), slots)
        x = x_ref[rows, :]
        grad_out = go_ref[rows, :]
        pre_gate = dot_rows(x, held[0, low:high])
        pre_up = dot_rows(x, held[1, low:high])
        active, slope = gelu_parts(pre_gate)
        ffn_low = (active * pre_up).astype(low_type)
        grad_act = dot_rows(grad_out, held[2, low:high])
        gate_low = (grad_act * pre_up * slope).astype(low_type)
        up_low = (grad_act * active).astype(low_type)
        sum_out = dot_plain(ffn_low, held[2, low:high])
        sum_in = dot_plain(gate_low, held[0, low:high]) + dot_plain(up_low, held[1, low:high])
        lows[0, rows, low:high] = gate_low
        lows[1, rows, low:high] = up_low
        lows[2, rows, low:high] = ffn_low
        if low > 0:
            sum_in = sum_in + part_in[rows, :].astype(wide)
            sum_out = sum_out + part_out[rows, :].astype(wide)
        part_in[rows, :] = sum_in.astype(low_type)
        part_out[rows, :] = sum_out.astype(low_type)
        return carry

    reduce_in = Reduce(part_in, in_x, in_y, in_pass, in_last, i_send, i_recv, member, z)
    gather = Gather(res_low.at[0], res_low, g_send, g_recv, member, z)
    middle = model // 2

    def weight_grads(kind, low, high):
        factor = go_ref if kind == 2 else x_ref
        for at in range(2):
            columns = slice(at * middle, (at + 1) * middle)
            held[kind, low:high, columns] = dot_slots(
                lows[kind, :, low:high], factor[:, columns]
            ).astype(low_type)

    def core_copy(slot, kind):
        return remote(
            held.at[kind, pl.ds((2 * slot + 1) * ffn_width, ffn_width)],
            paired.at[slot, kind],
            core_send.at[slot, kind],
            core_recv.at[slot, kind],
            other,
            z,
        )

    def chunk(number):
        return number // 2, pl.ds((number % 2) * half_ffn, half_ffn)

    def line_copy(kind, number, to_end):
        at, rows = chunk(number)
        return remote(
            paired.at[min(kind, 1), at, rows],
            arrived.at[kind, at, rows],
            line_send.at[kind, number],
            line_recv.at[kind, number],
            member,
            line_place(to_end, core),
        )

    def pair_up(slot, kind):
        core_copy(slot, kind).wait_recv()
        for number in (2 * kind, 2 * kind + 1):
            at, rows = chunk(number)
            own = held[at, pl.ds(2 * slot * ffn_width + (number % 2) * half_ffn, half_ffn)]
            paired[slot, at, rows] = add_low(own, paired[slot, at, rows])

            if slot == 0 or number < 4:

                @pl.when(end == 3)
                def _():
                    line_copy(slot, number, 2).start()

            if slot == 1 and number < 4:

                @pl.when(end == 0)
                def _():
                    line_copy(2, number, 1).start()

    def part_grads(slot, low, high):
        for kind in range(3):
            weight_grads(kind, low, high)
            core_copy(slot, kind).start()
            if kind > 0:
                pair_up(slot, kind - 1)
        pair_up(slot, 2)

    def summed(slot, kinds, number):
        at, rows = chunk(number)
        result = paired[slot, at, rows].astype(wide)
        for kind in kinds:
            result = result + arrived[kind, at, rows].astype(wide)
        return result.astype(low_type)

    def outer_step(number):
        at, rows = chunk(number)

        @pl.when((end == 2) | (end == 1))
        def _():
            line_copy(0, number, 0).wait_recv()
            paired[0, at, rows] = summed(0, (0,), number)
            line_copy(0, number, end - 1).start()

    def inner_step(number):
        at, rows = chunk(number)

        @pl.when(end == 2)
        def _():
            line_copy(1, number, 0).wait_recv()
            paired[1, at, rows] = summed(1, (1,), number)
            line_copy(1, number, 1).start()

    def out_copy(slot, number):
        at, rows = chunk(number)
        return pltpu.make_async_copy(
            paired.at[slot, at, rows], total.at[at, rows], load_sem.at[number]
        )

    def last_step(number):
        at, rows = chunk(number)

        if number < 4:

            @pl.when(end == 1)
            def _():
                line_copy(1, number, 0).wait_recv()
                line_copy(2, number, 0).wait_recv()
                paired[1, at, rows] = summed(1, (1, 2), number)
                out_copy(1, number).start()

        @pl.when(end == 0)
        def _():
            line_copy(0, number, 0).wait_recv()
            paired[0, at, rows] = summed(0, (0,), number)
            out_copy(0, number).start()

    lax.fori_loop(0, 4, functools.partial(block_step, 0, split), 0)
    part_grads(0, 0, split)
    lax.fori_loop(0, 4, functools.partial(block_step, split, hidden), 0)
    reduce_in.begin()
    part_grads(1, split, hidden)
    inner_copy = pltpu.make_async_copy(paired.at[1, 2], inner_down, load_sem.at[6])
    inner_copy.start()
    for number in range(3):
        outer_step(number)
    reduce_in.relay()
    for number in range(3, 6):
        outer_step(number)

    reduce_in.arrive()
    gain = gain_ref[1:2]
    gain_sum = jnp.zeros((1, model), wide)
    for number in range(2):
        at = slice(number * half, (number + 1) * half)
        grad = reduce_in.result(number)
        value = residual_ref[at]
        scale = lax.rsqrt(jnp.mean(value * value, axis=1, keepdims=True) + norm_eps)
        scaled = grad * gain
        gain_sum = gain_sum + jnp.sum(grad * value * scale, axis=0, keepdims=True)
        inner = jnp.mean(scaled * value, axis=1, keepdims=True)
        back = scale * scaled - value * (scale * scale * scale * inner)
        result = go_ref[at].astype(wide) + back
        res_out[at] = result
        res_low[0, at] = result.astype(low_type)
    gain_out[...] = jnp.concatenate([gain_ref[0:1], gain_sum, jnp.zeros((6, model), wide)], axis=0)
    gather.begin()
    inner_step(0)
    gather.relay()
    inner_step(1)
    inner_step(2)
    inner_step(3)
    gather.arrive()
    for number in range(6):
        last_step(number)
    inner_copy.wait()

    for sent in (reduce_in, gather):
        sent.finish()
    for slot in range(2):
        for kind in range(3):
            core_copy(slot, kind).wait_send()
    for number in range(6):

        @pl.when(end > 0)
        def _():
            line_copy(0, number, 0).wait_send()

        @pl.when(end == 0)
        def _():
            out_copy(0, number).wait()

    for number in range(4):

        @pl.when(end > 1)
        def _():
            line_copy(1, number, 0).wait_send()

        @pl.when(end == 1)
        def _():
            out_copy(1, number).wait()

        @pl.when(end == 0)
        def _():
            line_copy(2, number, 1).wait_send()


def middle(x, grad_out, weights, residual, gains):
    rows, model = x.shape
    hidden = weights.shape[1]
    ffn_width = hidden // 4
    slots = rows // 4
    dma = pltpu.SemaphoreType.DMA
    vmem = pl.BlockSpec(memory_space=pltpu.VMEM)
    anywhere = pl.BlockSpec(memory_space=pl.ANY)
    quarter = (3, ffn_width, model)
    return pl.pallas_call(
        functools.partial(middle_kernel, (model, ffn_width)),
        in_specs=[vmem, vmem, anywhere, vmem, vmem],
        out_specs=[anywhere] * 2 + [vmem] * 4,
        out_shape=[
            jax.ShapeDtypeStruct(quarter, low_type),
            jax.ShapeDtypeStruct(quarter[1:], low_type),
            jax.ShapeDtypeStruct((4, slots, model), low_type),
            jax.ShapeDtypeStruct((slots, model), wide),
            jax.ShapeDtypeStruct((8, model), wide),
            jax.ShapeDtypeStruct((rows, model), low_type),
        ],
        scratch_shapes=[
            pltpu.VMEM(weights.shape, low_type),
            pltpu.VMEM((3, rows, hidden), low_type),
            pltpu.VMEM((2,) + quarter, low_type),
            pltpu.VMEM((3,) + quarter, low_type),
            pltpu.VMEM((rows, model), low_type),
        ]
        + Reduce.scratch(slots, model)
        + [
            dma((7,)),
            dma((2, 3)),
            dma((2, 3)),
            dma((3, 6)),
            dma((3, 6)),
            dma((6,)),
            dma((6,)),
            dma((4,)),
            dma((4,)),
        ],
        compiler_params=pltpu.CompilerParams(
            collective_id=4, has_side_effects=True, vmem_limit_bytes=63 * 1024 * 1024
        ),
        cost_estimate=pl.CostEstimate(
            flops=2 * rows * model * hidden * 9,
            bytes_accessed=weights.size * 4 + rows * model * 16,
            transcendentals=rows * hidden,
        ),
        name="middle",
    )(x, grad_out, weights, residual, gains)


class Scatter:
    def __init__(self, sizes, member, z, send_sem, recv_sem):
        self.model, self.width, self.ffn_width, self.piece_length = sizes
        self.member, self.z = member, z
        self.chip, self.core = member // 2, member % 2
        self.owner = self.core == z // 2
        self.send_sem, self.recv_sem = send_sem, recv_sem
        self.across = self.model // 128
        rec, ffn, model = 4 * self.width, 4 * self.ffn_width, self.model
        self.gate_base = 2 * model * rec
        self.out_base = self.gate_base + 8 * self.width * self.width
        self.up_base = self.out_base + rec * model
        self.down_base = self.up_base + 2 * model * ffn
        self.rec, self.ffn = rec, ffn
        self.first_in = 0
        self.first_gate = 2 * self.across
        self.first_out = self.first_gate + 2
        self.first_small = self.first_out + 4
        self.first_up = self.first_small + 1
        self.first_down = self.first_up + 2 * self.across
        self.count = self.first_down + 6

    def in_unit(self, number, q):
        kind, at = number // self.across, number % self.across
        low = (kind * self.model + at * 128) * self.rec
        where = (
            pl.ds(pl.multiple_of(kind * self.width, self.width), self.width),
            pl.ds(pl.multiple_of(at * 128, 128), 128),
        )
        return self.first_in + number, where, low, low + 128 * self.rec

    def gate_unit(self, kind, q):
        low = self.gate_base + (kind * 4 + q) * self.width * self.width
        where = (
            pl.ds(pl.multiple_of(kind * self.width, self.width), self.width),
            pl.ds(self.model, self.width),
        )
        return self.first_gate + kind, where, low, low + self.width * self.width

    def out_unit(self, number, q):
        rows = self.width // 4
        low = self.out_base + (q * self.width + number * rows) * self.model
        where = (
            pl.ds(pl.multiple_of(2 * self.width + number * rows, rows), rows),
            pl.ds(0, self.model),
        )
        return self.first_out + number, where, low, low + rows * self.model

    def up_unit(self, number, q):
        kind, at = number // self.across, number % self.across
        low = self.up_base + (kind * self.model + at * 128) * self.ffn
        where = (kind, pl.ds(0, self.ffn_width), pl.ds(pl.multiple_of(at * 128, 128), 128))
        return self.first_up + number, where, low, low + 128 * self.ffn

    def down_unit(self, number, q):
        rows = self.ffn_width // 6
        low = self.down_base + (q * self.ffn_width + number * rows) * self.model
        where = (2, pl.ds(pl.multiple_of(number * rows, 16), rows), pl.ds(0, self.model))
        return self.first_down + number, where, low, low + rows * self.model

    def small_where(self):
        return (pl.ds(2 * self.width, 16), pl.ds(self.model, self.width))

    def copies(self, unit, source, target, q, act, flat=False):
        number, where, low, high = unit
        here = where[1:] if flat else where
        first = low // self.piece_length
        last = (high - 1) // self.piece_length
        for which, to in ((0, first), (1, last)):
            wanted = True if which == 0 else last != first

            @pl.when((to != self.member) & wanted)
            def _():
                act(
                    remote(
                        source.at[here],
                        target.at[(q,) + where],
                        self.send_sem.at[which, number],
                        self.recv_sem.at[q, number],
                        to,
                        self.z,
                    ),
                    True,
                )

            @pl.when((to == self.member) & wanted)
            def _():
                act(
                    pltpu.make_async_copy(
                        source.at[here], target.at[(q,) + where], self.recv_sem.at[q, number]
                    ),
                    False,
                )

    def each(self, unit_of, low, high, source, target, act, flat=False):
        def body(number, carry):
            self.copies(unit_of(number, self.chip), source, target, self.chip, act, flat)
            return carry

        lax.fori_loop(low, high, body, 0)

    def smalls(self, source, target, act):
        where = self.small_where()
        for to in range(8):

            @pl.when(self.member != to)
            def _():
                act(
                    remote(
                        source.at[where],
                        target.at[(self.chip,) + where],
                        self.send_sem.at[2, to],
                        self.recv_sem.at[self.chip, self.first_small],
                        to,
                        self.z,
                    ),
                    True,
                )

        act(
            pltpu.make_async_copy(
                source.at[where],
                target.at[(self.chip,) + where],
                self.recv_sem.at[self.chip, self.first_small],
            ),
            False,
        )

    def arrivals(self, unit_of, count, source, target):
        low = self.member * self.piece_length

        def body(number, carry):
            for q in range(4):
                index, where, first, last = unit_of(number, q)
                mine = (first < low + self.piece_length) & (last > low)
                here = (self.chip == q) & self.owner

                @pl.when(mine & here)
                def _():
                    pltpu.make_async_copy(
                        source.at[where], target.at[(q,) + where], self.recv_sem.at[q, index]
                    ).wait()

                @pl.when(mine & jnp.logical_not(here))
                def _():
                    remote(
                        source.at[where],
                        target.at[(q,) + where],
                        self.send_sem.at[0, index],
                        self.recv_sem.at[q, index],
                        self.member,
                        self.z,
                    ).wait_recv()

            return carry

        lax.fori_loop(0, count, body, 0)

    def small_arrivals(self, source, target):
        where = self.small_where()
        for q in range(4):
            here = (self.chip == q) & self.owner

            @pl.when(here)
            def _():
                pltpu.make_async_copy(
                    source.at[where],
                    target.at[(q,) + where],
                    self.recv_sem.at[q, self.first_small],
                ).wait()

            @pl.when(jnp.logical_not(here))
            def _():
                remote(
                    source.at[where],
                    target.at[(q,) + where],
                    self.send_sem.at[2, 0],
                    self.recv_sem.at[q, self.first_small],
                    self.member,
                    self.z,
                ).wait_recv()


def begin(copy, is_remote):
    copy.start()


def finish_send(copy, is_remote):
    if is_remote:
        copy.wait_send()


def back_kernel(
    sizes,
    x_hbm,
    res_hbm,
    starts_ref,
    w_hbm,
    p_hbm,
    state_hbm,
    low_hbm,
    ffn_ref,
    inner_hbm,
    tokens_ref,
    res_ref,
    gain_ref,
    mix_out,
    ffn_out,
    tokens_out,
    gain_out,
    x_ref,
    low_res,
    w_ref,
    p_ref,
    state_ref,
    low_ref,
    proj_grads,
    gate_acc,
    small_acc,
    grads,
    part_ref,
    paired,
    arrived,
    total,
    from_x,
    from_y,
    passing,
    last,
    inner,
    inner_seen,
    gain_part,
    gain_plane,
    gain_line,
    gain_seen,
    load_sem,
    core_send,
    core_recv,
    line_send,
    line_recv,
    plane_send,
    plane_recv,
    inner_send,
    inner_recv,
    gain_send,
    gain_recv,
    unit_send,
    unit_recv,
):
    model, width, ffn_width, piece_length = sizes
    member = lax.axis_index("dp")
    z = lax.axis_index("shard")
    chip, core = member // 2, member % 2
    end = z + core * (3 - 2 * z)
    slots = tokens_ref.shape[0]
    half = slots // 2
    other = chip * 2 + 1 - core
    scatter = Scatter(sizes, member, z, unit_send, unit_recv)

    order = (2, 0, 3, 1)
    common = [
        pltpu.make_async_copy(x_hbm, x_ref, load_sem.at[4, 0]),
        pltpu.make_async_copy(res_hbm, low_res, load_sem.at[4, 1]),
    ]
    early = [pltpu.make_async_copy(inner_hbm, inner, load_sem.at[4, 2])]

    def head_loads(head):
        return [
            pltpu.make_async_copy(source.at[head], target.at[head], load_sem.at[head, number])
            for number, (source, target) in enumerate(
                ((w_hbm, w_ref), (p_hbm, p_ref), (state_hbm, state_ref), (low_hbm, low_ref))
            )
        ]

    for copy in early + head_loads(order[0]) + common:
        copy.start()
    for head in order[1:]:
        for copy in head_loads(head):
            copy.start()
    enter(member, z)

    half_ffn = ffn_width // 2

    def inner_copy(kind, number, to_end):
        at = pl.ds(number * half_ffn, half_ffn)
        return remote(
            inner.at[at],
            inner_seen.at[kind, at],
            inner_send.at[kind, number],
            inner_recv.at[kind, number],
            member,
            line_place(to_end, core),
        )

    def inner_add(kinds, number):
        at = pl.ds(number * half_ffn, half_ffn)
        result = inner[at].astype(wide)
        for kind in kinds:
            inner_copy(kind, number, 0).wait_recv()
            result = result + inner_seen[kind, at].astype(wide)
        inner[at] = result.astype(low_type)

    def inner_far(number):
        @pl.when(end == 2)
        def _():
            inner_add((0,), number)
            inner_copy(0, number, 1).start()

    def inner_last():
        @pl.when(end == 1)
        def _():
            inner_add((0, 1), 0)
            inner_add((0, 1), 1)
            scatter.each(scatter.down_unit, 0, 6, inner, ffn_out, begin, True)

    for copy in early:
        copy.wait()
    for number in range(2):

        @pl.when(end == 3)
        def _():
            inner_copy(0, number, 2).start()

        @pl.when(end == 0)
        def _():
            inner_copy(1, number, 1).start()

    @pl.when(scatter.owner)
    def _():
        scatter.each(scatter.up_unit, 0, 2 * scatter.across, ffn_ref, ffn_out, begin)

    @pl.when(end == 0)
    def _():
        scatter.each(scatter.down_unit, 0, 6, ffn_ref, ffn_out, begin)

    def rows(number):
        return pl.ds(number * width, width)

    def core_copy(slot, number):
        return remote(
            grads.at[2 + slot, rows(number)],
            paired.at[slot, rows(number)],
            core_send.at[slot, number],
            core_recv.at[slot, number],
            other,
            z,
        )

    reduce = Reduce(
        part_ref, from_x, from_y, passing, last, plane_send, plane_recv, member, z
    )

    def line_copy(kind, number, source, to_end):
        return remote(
            source,
            arrived.at[kind, rows(number)],
            line_send.at[kind, number],
            line_recv.at[kind, number],
            member,
            line_place(to_end, core),
        )

    def pair_up(slot):
        for number in range(3):
            core_copy(slot, number).wait_recv()
            both = grads[slot, rows(number)].astype(wide) + paired[slot, rows(number)].astype(wide)
            paired[slot, rows(number)] = both.astype(low_type)

            @pl.when(end == 3)
            def _():
                line_copy(slot, number, paired.at[slot, rows(number)], 2).start()

            if slot == 1:

                @pl.when(end == 0)
                def _():
                    line_copy(2, number, paired.at[slot, rows(number)], 1).start()

    def summed(slot, kinds, number):
        result = paired[slot, rows(number)].astype(wide)
        for kind in kinds:
            result = result + arrived[kind, rows(number)].astype(wide)
        return result.astype(low_type)

    def on_arrival(kind, number):
        line_copy(kind, number, paired.at[0, rows(number)], 0).wait_recv()

    def outer_step(place, number):
        @pl.when(end == place)
        def _():
            on_arrival(0, number)
            paired[0, rows(number)] = summed(0, (0,), number)
            line_copy(0, number, paired.at[0, rows(number)], place - 1).start()

    def share(number):
        if number < 2:
            across = scatter.across
            scatter.each(
                scatter.in_unit, number * across, (number + 1) * across, total, mix_out, begin
            )
            scatter.each(scatter.gate_unit, number, number + 1, total, mix_out, begin)
        else:
            scatter.each(scatter.out_unit, 0, 4, total, mix_out, begin)
            scatter.smalls(total, mix_out, begin)

    for copy in common:
        copy.wait()
    for turn, head in enumerate(order):
        for copy in head_loads(head):
            copy.wait()
        views = weight_views(w_ref.at[pl.ds(head, 1)], width)
        gate_acc[...] = jnp.zeros_like(gate_acc)
        small_acc[...] = jnp.zeros_like(small_acc)

        def step_block(block, carry):
            at = pl.ds(pl.multiple_of(block * slots, slots), slots)
            proj_low, grad_gates, grad_small = mixer_back_step(
                slot_position(starts_ref[at, :]),
                views,
                p_ref[head, at, :],
                state_ref[head, at, :],
                low_res[at, :],
                width,
            )
            proj_grads[at, head * 2 * width : (head + 1) * 2 * width] = proj_low
            gate_acc[...] += grad_gates
            small_acc[...] += grad_small
            return carry

        lax.fori_loop(0, 4, step_block, 0)
        grads[head, 0 : 2 * width, 0:model] = dot_slots(
            proj_grads[:, head * 2 * width : (head + 1) * 2 * width], x_ref[...]
        ).astype(low_type)
        grads[head, 2 * width : 3 * width, 0:model] = dot_slots(
            low_ref[head], low_res[...]
        ).astype(low_type)
        grads[head, 0:width, model:] = gate_acc[:, :width].astype(low_type)
        grads[head, width : 2 * width, model:] = gate_acc[:, width:].astype(low_type)
        grads[head, 2 * width : 3 * width, model:] = jnp.concatenate(
            [small_acc[...], jnp.zeros((width - 8, width), wide)], axis=0
        ).astype(low_type)
        if head >= 2:
            for number in range(3):
                core_copy(head - 2, number).start()
        if turn == 1:
            pair_up(0)
            inner_far(0)
        elif turn == 2:
            inner_far(1)
            outer_step(2, 0)
            outer_step(2, 1)
        elif turn == 3:
            inner_last()
            outer_step(2, 2)
            outer_step(1, 0)
            outer_step(1, 1)

    def in_block(block):
        at = slice(block * slots, (block + 1) * slots)
        result = jnp.zeros((slots, model), wide)
        for head in range(4):
            result = result + dot_plain(
                proj_grads[at, head * 2 * width : (head + 1) * 2 * width],
                w_ref[head, 0 : 2 * width, 0:model],
            )
        part_ref[at, :] = result.astype(low_type)

    for block in (3, 1, 2, 0):
        in_block(block)
        reduce.begin_block(block)
        if block == 3:
            pair_up(1)
    outer_step(1, 2)
    across = scatter.across
    scatter.arrivals(scatter.up_unit, 2 * across, ffn_ref, ffn_out)

    @pl.when(scatter.owner)
    def _():
        scatter.each(scatter.up_unit, 0, 2 * across, ffn_ref, ffn_out, finish_send)

    reduce.relay()

    for number in range(3):

        @pl.when(end == 2)
        def _():
            on_arrival(1, number)
            paired[1, rows(number)] = summed(1, (1,), number)
            line_copy(1, number, paired.at[1, rows(number)], 1).start()

        @pl.when(end == 1)
        def _():
            on_arrival(1, number)
            on_arrival(2, number)
            total[rows(number)] = summed(1, (1, 2), number)

        @pl.when(end == 0)
        def _():
            on_arrival(0, number)
            total[rows(number)] = summed(0, (0,), number)

        @pl.when(scatter.owner)
        def _():
            share(number)

    reduce.arrive()
    gain = gain_ref[0:1]
    gain_sum = jnp.zeros((1, model), wide)
    for number in range(2):
        at = slice(number * half, (number + 1) * half)
        grad = reduce.result(number)
        value = tokens_ref[at].astype(wide)
        scale = lax.rsqrt(jnp.mean(value * value, axis=1, keepdims=True) + norm_eps)
        scaled = grad * gain
        gain_sum = gain_sum + jnp.sum(grad * value * scale, axis=0, keepdims=True)
        drift = jnp.mean(scaled * value, axis=1, keepdims=True)
        back = scale * scaled - value * (scale * scale * scale * drift)
        tokens_out[at] = (res_ref[at] + back).astype(low_type)
    gain_part[...] = jnp.concatenate([gain_sum, gain_ref[1:2], jnp.zeros((6, model), wide)], axis=0)

    def gain_copy():
        return remote(
            gain_part, gain_plane.at[member], gain_send.at[0], gain_recv.at[member], 7, z
        )

    @pl.when(member != 7)
    def _():
        gain_copy().start()
        gain_copy().wait_send()
        gain_out[...] = jnp.zeros_like(gain_out)

    @pl.when(member == 7)
    def _():
        result = gain_part[...]
        for source in range(7):
            remote(
                gain_part,
                gain_plane.at[source],
                gain_send.at[0],
                gain_recv.at[source],
                7,
                z,
            ).wait_recv()
            result = result + gain_plane[source]
        quarter = model // 4
        for place in range(4):
            gain_line[place] = result[:, place * quarter : (place + 1) * quarter]

        def line_gain(place, slot):
            return remote(
                gain_line.at[place],
                gain_seen.at[slot],
                gain_send.at[1 + place],
                gain_recv.at[8 + slot],
                7,
                place,
            )

        for place in range(4):

            @pl.when(place != z)
            def _():
                line_gain(place, z).start()

        gain_out[...] = gain_line[z]
        for place in range(4):

            @pl.when(place != z)
            def _():
                line_gain(place, place).wait_recv()
                gain_out[...] += gain_seen[place]
                line_gain(place, z).wait_send()

    scatter.arrivals(scatter.down_unit, 6, ffn_ref, ffn_out)
    scatter.arrivals(scatter.in_unit, 2 * across, total, mix_out)
    scatter.arrivals(scatter.gate_unit, 2, total, mix_out)
    scatter.arrivals(scatter.out_unit, 4, total, mix_out)
    scatter.small_arrivals(total, mix_out)

    @pl.when(scatter.owner)
    def _():
        scatter.each(scatter.down_unit, 0, 6, ffn_ref, ffn_out, finish_send)
        scatter.each(scatter.in_unit, 0, 2 * across, total, mix_out, finish_send)
        scatter.each(scatter.gate_unit, 0, 2, total, mix_out, finish_send)
        scatter.each(scatter.out_unit, 0, 4, total, mix_out, finish_send)
        scatter.smalls(total, mix_out, finish_send)

    reduce.finish()
    for number in range(2):

        @pl.when(end >= 2)
        def _():
            inner_copy(0, number, 0).wait_send()

        @pl.when(end == 0)
        def _():
            inner_copy(1, number, 0).wait_send()

    for slot in range(2):
        for number in range(3):
            core_copy(slot, number).wait_send()
    for number in range(3):

        @pl.when(end > 0)
        def _():
            line_copy(0, number, paired.at[0, rows(number)], 0).wait_send()

        @pl.when(end > 1)
        def _():
            line_copy(1, number, paired.at[1, rows(number)], 0).wait_send()

        @pl.when(end == 0)
        def _():
            line_copy(2, number, paired.at[1, rows(number)], 1).wait_send()


def back(
    x,
    res,
    starts,
    weights,
    saved,
    ffn,
    inner,
    tokens,
    residual_grad,
    gains,
    piece_length,
    width,
):
    model = tokens.shape[1]
    ffn_width = ffn.shape[1]
    sizes = (model, width, ffn_width, piece_length)
    slots = tokens.shape[0]
    block = weights.shape[1:]
    count = Scatter(sizes, 0, 0, None, None).count
    dma = pltpu.SemaphoreType.DMA
    vmem = pl.BlockSpec(memory_space=pltpu.VMEM)
    anywhere = pl.BlockSpec(memory_space=pl.ANY)
    held = lambda value: pltpu.VMEM(value.shape, value.dtype)
    return pl.pallas_call(
        functools.partial(back_kernel, sizes),
        in_specs=[anywhere, anywhere, vmem] + [anywhere] * 6 + [vmem] * 3,
        out_specs=[anywhere, anywhere, vmem, vmem],
        out_shape=[
            jax.ShapeDtypeStruct(weights.shape, low_type),
            jax.ShapeDtypeStruct((4,) + ffn.shape, low_type),
            jax.ShapeDtypeStruct(tokens.shape, low_type),
            jax.ShapeDtypeStruct((8, model // 4), wide),
        ],
        scratch_shapes=[held(x), held(res), held(weights)]
        + [held(value) for value in saved]
        + [
            pltpu.VMEM((4 * slots, 8 * width), low_type),
            pltpu.VMEM((width, 2 * width), wide),
            pltpu.VMEM((8, width), wide),
            pltpu.VMEM(weights.shape, low_type),
            pltpu.VMEM((4 * slots, model), low_type),
            pltpu.VMEM((2,) + block, low_type),
            pltpu.VMEM((3,) + block, low_type),
            pltpu.VMEM(block, low_type),
        ]
        + Reduce.scratch(slots, model)
        + [
            held(inner),
            pltpu.VMEM((2,) + inner.shape, low_type),
            pltpu.VMEM((8, model), wide),
            pltpu.VMEM((8, 8, model), wide),
            pltpu.VMEM((4, 8, model // 4), wide),
            pltpu.VMEM((4, 8, model // 4), wide),
            dma((5, 4)),
            dma((2, 3)),
            dma((2, 3)),
            dma((3, 3)),
            dma((3, 3)),
            dma((6,)),
            dma((6,)),
            dma((2, 2)),
            dma((2, 2)),
            dma((5,)),
            dma((12,)),
            dma((3, count)),
            dma((4, count)),
        ],
        compiler_params=pltpu.CompilerParams(
            collective_id=2, has_side_effects=True, vmem_limit_bytes=60 * 1024 * 1024
        ),
        cost_estimate=pl.CostEstimate(
            flops=weights.size * 4 * slots * 4, bytes_accessed=weights.size * 8, transcendentals=0
        ),
        name="back",
    )(
        x,
        res,
        starts,
        weights,
        *saved,
        ffn,
        inner,
        tokens,
        residual_grad,
        gains,
    )


def adam_kernel(
    sizes,
    mix_ref,
    ffn_ref,
    gain_ref,
    master_ref,
    first_ref,
    second_ref,
    piece_ref,
    new_master_ref,
    new_first_ref,
    new_second_ref,
    rows_ref,
    bias_ref,
    grad,
):
    model, width, ffn_width, piece_length, lines, margin = sizes
    member = lax.axis_index("dp")
    step = pl.program_id(0)
    lead = 128
    start_row = (member * piece_length) // lead
    offset = (member * piece_length) % lead
    tiles_in = 4 * width // lead
    tiles_ffn = 4 * ffn_width // lead
    tiles_model = model // lead

    @pl.when(step == 0)
    def _():
        def clear(number, carry):
            grad[pl.ds(pl.multiple_of(number * 256, 256), 256), :] = jnp.zeros((256, lead), wide)
            return carry

        lax.fori_loop(0, grad.shape[0] // 256, clear, 0)

        def place(row, count, body):
            low = member * piece_length

            @pl.when((row * lead < low + piece_length) & ((row + count) * lead > low))
            def _():
                body(row - start_row + margin)

        base = 0

        def in_unit(number, carry):
            kind = number // tiles_model
            at = number % tiles_model

            def body(to):
                for q in range(4):
                    tile = mix_ref[
                        q,
                        pl.ds(pl.multiple_of(kind * width, width), width),
                        pl.ds(pl.multiple_of(at * lead, lead), lead),
                    ].astype(wide)
                    grad[pl.ds(to + q, lead, stride=tiles_in), :] = tile.T

            place((kind * model + at * lead) * tiles_in, lead * tiles_in, body)
            return carry

        lax.fori_loop(0, 2 * tiles_model, in_unit, 0)
        base = 2 * model * tiles_in

        def gate_body(number, carry):
            kind = number // 4
            q = number % 4

            def body(to):
                grad[pl.ds(to, width), :] = mix_ref[
                    q, pl.ds(pl.multiple_of(kind * width, width), width), model:
                ].astype(wide)

            place(2 * model * tiles_in + number * width, width, body)
            return carry

        lax.fori_loop(0, 8, gate_body, 0)
        base = base + 8 * width
        out_base = base

        quarter = width // 4

        def out_unit(number, carry):
            q = number // 4
            part = number % 4

            def body(to):
                for at in range(tiles_model):
                    grad[pl.ds(to + at, quarter, stride=tiles_model), :] = mix_ref[
                        q,
                        pl.ds(pl.multiple_of(2 * width + part * quarter, quarter), quarter),
                        at * lead : (at + 1) * lead,
                    ].astype(wide)

            place(out_base + number * quarter * tiles_model, quarter * tiles_model, body)
            return carry

        lax.fori_loop(0, 16, out_unit, 0)
        base = base + 4 * width * tiles_model
        up_base = base

        def up_unit(number, carry):
            kind = number // tiles_model
            at = number % tiles_model
            columns = pl.ds(pl.multiple_of(at * lead, lead), lead)

            def body(to):
                for tile in range(tiles_ffn):
                    found = []
                    row = tile * lead
                    while row < (tile + 1) * lead:
                        q = row // ffn_width
                        last = min((q + 1) * ffn_width, (tile + 1) * lead)
                        found.append(
                            ffn_ref[
                                q,
                                kind,
                                row - q * ffn_width : last - q * ffn_width,
                                columns,
                            ].astype(wide)
                        )
                        row = last
                    block = found[0] if len(found) == 1 else jnp.concatenate(found, axis=0)
                    grad[pl.ds(to + tile, lead, stride=tiles_ffn), :] = block.T

            place(up_base + (kind * model + at * lead) * tiles_ffn, lead * tiles_ffn, body)
            return carry

        lax.fori_loop(0, 2 * tiles_model, up_unit, 0)
        base = base + 2 * model * tiles_ffn
        down_base = base
        sixth = ffn_width // 6

        def down_unit(number, carry):
            q = number // 6
            part = number % 6

            def body(to):
                for at in range(tiles_model):
                    grad[pl.ds(to + at, sixth, stride=tiles_model), :] = ffn_ref[
                        q,
                        2,
                        pl.ds(pl.multiple_of(part * sixth, 16), sixth),
                        at * lead : (at + 1) * lead,
                    ].astype(wide)

            place(down_base + number * sixth * tiles_model, sixth * tiles_model, body)
            return carry

        lax.fori_loop(0, 24, down_unit, 0)
        small_base = base + 4 * ffn_width * tiles_model
        smalls = [
            mix_ref[q, 2 * width : 2 * width + 16, model:].astype(wide)
            for q in range(4)
        ]

        def small_body(to):
            for q in range(4):
                grad[pl.ds(to + q, 8, stride=tiles_in), :] = smalls[q][:8]
            for number in range(6):
                kind, at = number // 3, number % 3
                grad[pl.ds(to + 8 * tiles_in + number, 1), :] = gain_ref[
                    kind : kind + 1, at * lead : (at + 1) * lead
                ]

        place(small_base, 8 * tiles_in + 6, small_body)
        bias_ref[...] = jnp.concatenate([small[5:7] for small in smalls], axis=1)

    row = margin + step * lines
    shift = (lead - offset) % lead
    here = pltpu.roll(grad[pl.ds(row, lines), :], shift, 1)
    after = pltpu.roll(grad[pl.ds(row + 1, lines), :], shift, 1)
    lane = lax.broadcasted_iota(jnp.int32, (lines, lead), 1)
    piece = jnp.where(lane < lead - offset, here, after).reshape(1, lines * lead)
    piece_ref[...] = piece
    new_first = beta_one * first_ref[...] + (1.0 - beta_one) * piece
    new_second = beta_two * second_ref[...] + (1.0 - beta_two) * piece * piece
    master = master_ref[...]
    new_master = master - learn_rate * (
        new_first / corr_one / (jnp.sqrt(new_second / corr_two) + adam_eps)
        + weight_decay * master
    )
    new_first_ref[...] = new_first
    new_second_ref[...] = new_second
    new_master_ref[...] = new_master
    rows_ref[0] = new_master.reshape(lines, lead).astype(low_type)


def adam(mix, ffn, gains, master, first, second, sizes, chunks):
    model, width, ffn_width = sizes
    piece_length = master.shape[1]
    lines = -(-piece_length // (chunks * 128 * 16)) * 16
    block = lines * 128
    margin = 1536
    rows = -(-(2 * margin + chunks * lines + 8) // 256) * 256
    packed = jax.ShapeDtypeStruct(master.shape, wide)
    chunk_spec = pl.BlockSpec((1, block), lambda s: (0, s))
    once = lambda shape: pl.BlockSpec(
        shape, lambda s: (0,) * len(shape), pipeline_mode=pl.Buffered(1)
    )
    return pl.pallas_call(
        functools.partial(
            adam_kernel, (model, width, ffn_width, piece_length, lines, margin)
        ),
        grid=(chunks,),
        in_specs=[once(mix.shape), once(ffn.shape), once(gains.shape)] + [chunk_spec] * 3,
        out_specs=[chunk_spec] * 4
        + [
            pl.BlockSpec((1, lines, 128), lambda s: (s, 0, 0)),
            pl.BlockSpec((2, 4 * width), lambda s: (0, 0)),
        ],
        out_shape=[packed] * 4
        + [
            jax.ShapeDtypeStruct((chunks, lines, 128), low_type),
            jax.ShapeDtypeStruct((2, 4 * width), wide),
        ],
        scratch_shapes=[pltpu.VMEM((rows, 128), wide)],
        compiler_params=pltpu.CompilerParams(vmem_limit_bytes=48 * 1024 * 1024),
        cost_estimate=pl.CostEstimate(
            flops=20 * piece_length,
            bytes_accessed=40 * piece_length,
            transcendentals=piece_length,
        ),
        name="adam",
    )(mix, ffn, gains, master, first, second)


def spread_kernel(
    own_ref,
    part_hbm,
    residual_ref,
    mask_ref,
    weights_ref,
    block_out,
    held,
    spread,
    part,
    from_x,
    from_y,
    passing,
    last,
    load_sem,
    send_sem,
    recv_sem,
    plane_send,
    plane_recv,
):
    chunks, lines, lead = own_ref.shape
    member = lax.axis_index("dp")
    z = lax.axis_index("shard")
    step = pl.program_id(0)
    reduce = Reduce(part, from_x, from_y, passing, last, plane_send, plane_recv, member, z)
    part_load = pltpu.make_async_copy(part_hbm, part, load_sem.at[chunks])

    def copy_to(origin, chunk, side, to):
        return remote(
            held.at[origin, chunk],
            held.at[origin, chunk],
            send_sem.at[side, origin, chunk],
            recv_sem.at[origin, chunk],
            member,
            to,
        )

    def own_load(chunk):
        return pltpu.make_async_copy(own_ref.at[chunk], held.at[z, chunk], load_sem.at[chunk])

    def pass_on(origin, chunk, right):
        copy_to(origin, chunk, 0, z).wait_recv()
        if right:

            @pl.when(z < 3)
            def _():
                copy_to(origin, chunk, 0, z + 1).start()
        else:

            @pl.when(z > 0)
            def _():
                copy_to(origin, chunk, 1, z - 1).start()

    @pl.when(step == 0)
    def _():
        for chunk in range(chunks):
            own_load(chunk).start()
        part_load.start()
        barrier = pltpu.get_barrier_semaphore()
        for to in (reduce.to_x, reduce.to_y):
            pl.semaphore_signal(
                barrier, inc=1, device_id=(to, z), device_id_type=pl.DeviceIdType.MESH
            )

        @pl.when(z > 0)
        def _():
            pl.semaphore_signal(
                barrier, inc=1, device_id=(member, z - 1), device_id_type=pl.DeviceIdType.MESH
            )

        @pl.when(z < 3)
        def _():
            pl.semaphore_signal(
                barrier, inc=1, device_id=(member, z + 1), device_id_type=pl.DeviceIdType.MESH
            )

        @pl.when((z == 0) | (z == 3))
        def _():
            pl.semaphore_wait(barrier, 3)

        @pl.when((z > 0) & (z < 3))
        def _():
            pl.semaphore_wait(barrier, 4)

        def send_own(chunk, carry):
            own_load(chunk).wait()

            @pl.when(z < 3)
            def _():
                copy_to(z, chunk, 0, z + 1).start()

            @pl.when(z > 0)
            def _():
                copy_to(z, chunk, 1, z - 1).start()

            return carry

        lax.fori_loop(0, chunks, send_own, 0)
        part_load.wait()
        reduce.begin()

        def near(chunk, carry):
            @pl.when(z > 0)
            def _():
                pass_on(z - 1, chunk, True)

            @pl.when(z < 3)
            def _():
                pass_on(z + 1, chunk, False)

            return carry

        lax.fori_loop(0, chunks, near, 0)
        reduce.relay()

    @pl.when(step == 1)
    def _():
        reduce.arrive()
        live = mask_ref[:, 0:1].astype(wide)
        half = reduce.half
        for number in range(2):
            at = slice(number * half, (number + 1) * half)
            block_out[at] = (live[at] * (residual_ref[at] + reduce.result(number))).astype(low_type)
        reduce.finish()

    @pl.when(z >= 2)
    def _():
        pass_on(z - 2, step, True)

    @pl.when(z <= 1)
    def _():
        pass_on(z + 2, step, False)

    @pl.when(z == 3)
    def _():
        copy_to(0, step, 0, z).wait_recv()

    @pl.when(z == 0)
    def _():
        copy_to(3, step, 0, z).wait_recv()

    for origin in range(4):
        spread[origin * lines : (origin + 1) * lines, :] = held[origin, step].astype(wide)

    def line(number, carry):
        weights_ref[:, pl.ds(pl.multiple_of(number * lead, lead), lead)] = spread[
            pl.ds(number, 4, stride=lines), :
        ].astype(low_type)
        return carry

    lax.fori_loop(0, lines, line, 0, unroll=8)

    @pl.when(step == chunks - 1)
    def _():
        for origin in range(4):

            def finish(chunk, carry):
                @pl.when((origin <= z) & (z < 3))
                def _():
                    copy_to(origin, chunk, 0, z).wait_send()

                @pl.when((origin >= z) & (z > 0))
                def _():
                    copy_to(origin, chunk, 1, z).wait_send()

                return carry

            lax.fori_loop(0, chunks, finish, 0)


def spread_weights(own, part, residual, mask, piece_length):
    chunks, lines, lead = own.shape
    slots, model = residual.shape
    once = lambda value: pl.BlockSpec(
        value.shape, lambda s: (0, 0), pipeline_mode=pl.Buffered(1)
    )
    return pl.pallas_call(
        spread_kernel,
        grid=(chunks,),
        in_specs=[pl.BlockSpec(memory_space=pl.ANY)] * 2 + [once(residual), once(mask)],
        out_specs=[pl.BlockSpec((4, lines * lead), lambda s: (0, s)), once(residual)],
        out_shape=[
            jax.ShapeDtypeStruct((4, piece_length), low_type),
            jax.ShapeDtypeStruct(residual.shape, low_type),
        ],
        scratch_shapes=[
            pltpu.VMEM((4, chunks, lines, lead), low_type),
            pltpu.VMEM((4 * lines, lead), wide),
            pltpu.VMEM(part.shape, low_type),
        ]
        + Reduce.scratch(slots, model)
        + [
            pltpu.SemaphoreType.DMA((chunks + 1,)),
            pltpu.SemaphoreType.DMA((2, 4, chunks)),
            pltpu.SemaphoreType.DMA((4, chunks)),
            pltpu.SemaphoreType.DMA((6,)),
            pltpu.SemaphoreType.DMA((6,)),
        ],
        compiler_params=pltpu.CompilerParams(
            collective_id=1, has_side_effects=True, vmem_limit_bytes=32 * 1024 * 1024
        ),
        cost_estimate=pl.CostEstimate(
            flops=4 * piece_length, bytes_accessed=16 * piece_length, transcendentals=0
        ),
        name="spread",
    )(own, part, residual, mask)


def group_body(
    tokens,
    cotangent,
    seq_start,
    live_mask,
    input_proj,
    gate_blocks,
    output_proj,
    ffn_gate_up,
    ffn_down,
    conv_taps,
    gate_bias,
    decay_param,
    norm_gains,
    master_shard,
    first_moment,
    second_moment,
):
    slots, model = tokens.shape
    slice_rec = input_proj.shape[2]
    slice_ffn = ffn_down.shape[0]
    width = slice_rec // 4
    ffn_width = slice_ffn // 4
    piece_length = master_shard.shape[1]
    mask_rows = live_mask.astype(wide)[:, None]
    grad_stream = cotangent.astype(wide) * mask_rows

    starts = jnp.broadcast_to(seq_start.astype(low_type)[:, None], (slots, width))
    (
        mix_in,
        mix_weights,
        ffn_weights,
        saved_p,
        saved_state,
        saved_low,
        all_starts,
        residual,
        ffn_in,
        all_grad_out,
        gains,
    ) = front(
        jnp.concatenate([tokens, starts], axis=1),
        grad_stream.astype(low_type),
        jnp.concatenate([norm_gains, jnp.zeros((14, norm_gains.shape[1]), low_type)]),
        jnp.concatenate(
            [conv_taps, gate_bias, decay_param[None], jnp.zeros((8, slice_rec), low_type)]
        ),
        input_proj,
        gate_blocks,
        output_proj,
        ffn_gate_up,
        ffn_down,
        (model, width, ffn_width),
    )
    ffn_in = ffn_in.reshape(4 * slots, model)
    all_grad_out = all_grad_out.reshape(4 * slots, model)
    sum_ffn, inner_down, res_low, grad_residual, gain_sums, ffn_part = middle(
        ffn_in, all_grad_out, ffn_weights, residual, gains
    )
    four_mix, four_ffn, tokens_grad, gain_total = back(
        mix_in,
        res_low.reshape(4 * slots, model),
        all_starts,
        mix_weights,
        (saved_p, saved_state, saved_low),
        sum_ffn,
        inner_down,
        tokens,
        grad_residual,
        gain_sums,
        piece_length,
        width,
    )
    piece, new_master, new_first, new_second, rows, bias_total = adam(
        four_mix,
        four_ffn,
        gain_total,
        master_shard,
        first_moment,
        second_moment,
        (model, width, ffn_width),
        8,
    )
    new_weights, block_out = spread_weights(
        rows,
        ffn_part,
        residual,
        jnp.broadcast_to(mask_rows.astype(low_type), (slots, width)),
        piece_length,
    )
    return (
        block_out,
        tokens_grad,
        piece,
        new_master,
        new_first,
        new_second,
        new_weights,
        bias_total,
    )


def rms_scale(values, gain):
    return values * lax.rsqrt(jnp.mean(values * values, axis=-1, keepdims=True) + norm_eps) * gain


def conv_mix(signal, taps, position):
    result = taps[-1] + taps[0] * signal
    for shift_by in range(1, taps.shape[0] - 1):
        moved = jnp.pad(signal, ((shift_by, 0), (0, 0)))[:-shift_by]
        result = result + taps[shift_by] * jnp.where((position >= shift_by)[:, None], moved, 0.0)
    return result


def combine_steps(earlier, later):
    decay_first, value_first = earlier
    decay_second, value_second = later
    return (decay_first * decay_second, decay_second * value_first + value_second)


def recurrence(logits, signal, branch, bias_term, decay_term, position):
    row_count = signal.shape[0]
    recur_gate = jax.nn.sigmoid(logits[0].reshape(row_count, -1) + bias_term[0])
    input_gate = jax.nn.sigmoid(logits[1].reshape(row_count, -1) + bias_term[1])
    log_decay = -gate_scale * recur_gate * jax.nn.softplus(-decay_term)
    decay_rate = jnp.where((position > 0)[:, None], jnp.exp(log_decay), 0.0)
    drive_term = jnp.sqrt(-jnp.expm1(2.0 * log_decay)) * input_gate * signal
    states = lax.associative_scan(combine_steps, (decay_rate, drive_term), axis=0)[1]
    return states * jax.nn.gelu(branch)


def gated_gelu(ffn_pre):
    return jax.nn.gelu(ffn_pre[0]) * ffn_pre[1]


def mixer_forward(
    mix_in, input_proj, gate_blocks, output_proj, conv_taps, gate_bias, decay_param, position
):
    projected = jnp.einsum("sd,kdr->ksr", mix_in, input_proj, preferred_element_type=jnp.float32)
    conv_out, conv_pull = jax.vjp(
        lambda signal, taps: conv_mix(signal, taps, position), projected[0], conv_taps
    )
    row_count = conv_out.shape[0]
    conv_low = conv_out.astype(jnp.bfloat16).reshape(
        row_count, gate_blocks.shape[1], gate_blocks.shape[2]
    )
    gate_logits = jnp.einsum(
        "shb,khbc->kshc", conv_low, gate_blocks, preferred_element_type=jnp.float32
    )
    mixed, mix_pull = jax.vjp(
        lambda logits, signal, branch, bias_term, decay_term: recurrence(
            logits, signal, branch, bias_term, decay_term, position
        ),
        gate_logits,
        conv_out,
        projected[1],
        gate_bias,
        decay_param,
    )
    mixed_low = mixed.astype(jnp.bfloat16)
    partial_out = jnp.dot(mixed_low, output_proj, preferred_element_type=jnp.float32)
    return (partial_out, (conv_pull, conv_low, mix_pull, mixed_low))


def mixer_backward(grad_out_low, mix_in, saved, input_proj, gate_blocks, output_proj):
    conv_pull, conv_low, mix_pull, mixed_low = saved
    grad_output_proj = jnp.einsum(
        "sr,sd->rd", mixed_low, grad_out_low, preferred_element_type=jnp.float32
    )
    grad_mixed = jnp.einsum(
        "sd,rd->sr", grad_out_low, output_proj, preferred_element_type=jnp.float32
    )
    grad_logits, grad_conv_direct, grad_branch, grad_bias, grad_decay = mix_pull(grad_mixed)
    logits_low = grad_logits.astype(jnp.bfloat16)
    grad_blocks = jnp.einsum(
        "shb,kshc->khbc", conv_low, logits_low, preferred_element_type=jnp.float32
    )
    grad_conv_gates = jnp.einsum(
        "kshc,khbc->shb", logits_low, gate_blocks, preferred_element_type=jnp.float32
    )
    grad_signal, grad_taps = conv_pull(
        grad_conv_direct + grad_conv_gates.reshape(grad_conv_direct.shape)
    )
    proj_low = jnp.stack([grad_signal, grad_branch]).astype(jnp.bfloat16)
    grad_input_proj = jnp.einsum(
        "sd,ksr->kdr", mix_in, proj_low, preferred_element_type=jnp.float32
    )
    grad_mix_in = jnp.einsum(
        "ksr,kdr->sd", proj_low, input_proj, preferred_element_type=jnp.float32
    )
    return (
        grad_mix_in,
        (grad_input_proj, grad_blocks, grad_output_proj, grad_taps, grad_bias, grad_decay),
    )


def ffn_forward(ffn_in_low, ffn_gate_up, ffn_down):
    ffn_pre = jnp.einsum("sd,kdf->ksf", ffn_in_low, ffn_gate_up, preferred_element_type=jnp.float32)
    ffn_act, ffn_pull = jax.vjp(gated_gelu, ffn_pre)
    ffn_low = ffn_act.astype(jnp.bfloat16)
    partial_ffn = jnp.dot(ffn_low, ffn_down, preferred_element_type=jnp.float32)
    return (partial_ffn, (ffn_pull, ffn_low))


def ffn_backward(grad_low, ffn_in_low, saved, ffn_gate_up, ffn_down):
    ffn_pull, ffn_low = saved
    grad_down = jnp.einsum("sf,sd->fd", ffn_low, grad_low, preferred_element_type=jnp.float32)
    grad_act = jnp.einsum("sd,fd->sf", grad_low, ffn_down, preferred_element_type=jnp.float32)
    grad_pre = ffn_pull(grad_act)[0]
    pre_low = grad_pre.astype(jnp.bfloat16)
    grad_gate_up = jnp.einsum(
        "sd,ksf->kdf", ffn_in_low, pre_low, preferred_element_type=jnp.float32
    )
    grad_ffn_in = jnp.einsum(
        "ksf,kdf->sd", pre_low, ffn_gate_up, preferred_element_type=jnp.float32
    )
    return (grad_ffn_in, grad_gate_up, grad_down)


def body(
    tokens,
    cotangent,
    seq_start,
    live_mask,
    input_proj,
    gate_blocks,
    output_proj,
    ffn_gate_up,
    ffn_down,
    conv_taps,
    gate_bias,
    decay_param,
    norm_gains,
    master_shard,
    first_moment,
    second_moment,
):
    slot_count = tokens.shape[0]
    position = jnp.arange(slot_count, dtype=jnp.int32) - seq_start
    mask_rows = live_mask.astype(jnp.float32)[:, None]
    stream = tokens.astype(jnp.float32)
    grad_stream = cotangent.astype(jnp.float32) * mask_rows
    shards = (
        input_proj,
        gate_blocks,
        output_proj,
        ffn_gate_up,
        ffn_down,
        conv_taps,
        gate_bias,
        decay_param,
        norm_gains,
    )
    (
        full_in,
        full_blocks,
        full_out,
        full_up,
        full_down,
        full_taps,
        full_bias,
        full_decay,
        full_gains,
    ) = (
        lax.all_gather(shards[0], "shard", axis=2, tiled=True),
        lax.all_gather(shards[1], "shard", axis=1, tiled=True),
        lax.all_gather(shards[2], "shard", axis=0, tiled=True),
        lax.all_gather(shards[3], "shard", axis=2, tiled=True),
        lax.all_gather(shards[4], "shard", axis=0, tiled=True),
        lax.all_gather(shards[5], "shard", axis=1, tiled=True),
        lax.all_gather(shards[6], "shard", axis=1, tiled=True),
        lax.all_gather(shards[7], "shard", axis=0, tiled=True),
        lax.all_gather(shards[8], "shard", axis=1, tiled=True),
    )
    gains = full_gains.astype(jnp.float32)
    normed, norm_pull = jax.vjp(rms_scale, stream, gains[0])
    mix_in = normed.astype(jnp.bfloat16)
    mix_out, mix_saved = mixer_forward(
        mix_in,
        full_in,
        full_blocks,
        full_out,
        full_taps.astype(jnp.float32),
        full_bias.astype(jnp.float32),
        full_decay.astype(jnp.float32),
        position,
    )
    residual = stream + mix_out
    normed_two, second_pull = jax.vjp(rms_scale, residual, gains[1])
    ffn_in_low = normed_two.astype(jnp.bfloat16)
    ffn_result, ffn_saved = ffn_forward(ffn_in_low, full_up, full_down)
    block_out = (mask_rows * (residual + ffn_result)).astype(jnp.bfloat16)
    grad_ffn_in, grad_up, grad_down = ffn_backward(
        grad_stream.astype(jnp.bfloat16), ffn_in_low, ffn_saved, full_up, full_down
    )
    grad_norm_two, grad_gain_two = second_pull(grad_ffn_in)
    grad_residual = grad_stream + grad_norm_two
    grad_mix_in, mix_grads = mixer_backward(
        grad_residual.astype(jnp.bfloat16), mix_in, mix_saved, full_in, full_blocks, full_out
    )
    grad_norm_one, grad_gain_one = norm_pull(grad_mix_in)
    tokens_grad = (grad_residual + grad_norm_one).astype(jnp.bfloat16)
    grads = (
        mix_grads[0],
        mix_grads[1],
        mix_grads[2],
        grad_up,
        grad_down,
        mix_grads[3],
        mix_grads[4],
        mix_grads[5],
        jnp.stack([grad_gain_one, grad_gain_two]),
    )
    summed = (
        lax.psum_scatter(
            grads[0].astype(jnp.bfloat16), "shard", scatter_dimension=2, tiled=True
        ).astype(jnp.float32),
        lax.psum_scatter(
            grads[1].astype(jnp.bfloat16), "shard", scatter_dimension=1, tiled=True
        ).astype(jnp.float32),
        lax.psum_scatter(
            grads[2].astype(jnp.bfloat16), "shard", scatter_dimension=0, tiled=True
        ).astype(jnp.float32),
        lax.psum_scatter(
            grads[3].astype(jnp.bfloat16), "shard", scatter_dimension=2, tiled=True
        ).astype(jnp.float32),
        lax.psum_scatter(
            grads[4].astype(jnp.bfloat16), "shard", scatter_dimension=0, tiled=True
        ).astype(jnp.float32),
        lax.psum_scatter(
            grads[5].astype(jnp.bfloat16), "shard", scatter_dimension=1, tiled=True
        ).astype(jnp.float32),
        lax.psum_scatter(
            grads[6].astype(jnp.bfloat16), "shard", scatter_dimension=1, tiled=True
        ).astype(jnp.float32),
        lax.psum_scatter(
            grads[7].astype(jnp.bfloat16), "shard", scatter_dimension=0, tiled=True
        ).astype(jnp.float32),
        lax.psum_scatter(
            grads[8].astype(jnp.bfloat16), "shard", scatter_dimension=1, tiled=True
        ).astype(jnp.float32),
    )
    flat = jnp.concatenate([member.reshape(1, -1) for member in summed], axis=1)
    piece = lax.psum_scatter(flat, "dp", scatter_dimension=1, tiled=True)
    bias_total = lax.psum(summed[6], "dp")
    new_first = beta_one * first_moment + (1.0 - beta_one) * piece
    new_second = beta_two * second_moment + (1.0 - beta_two) * piece * piece
    new_master = master_shard - learn_rate * (
        new_first / corr_one / (jnp.sqrt(new_second / corr_two) + adam_eps)
        + weight_decay * master_shard
    )
    new_weights = lax.all_gather(new_master.astype(jnp.bfloat16), "shard", axis=0, tiled=True)
    return (
        block_out,
        tokens_grad,
        piece,
        new_master,
        new_first,
        new_second,
        new_weights,
        bias_total,
    )


def solution(mesh):
    fits = mesh.shape["dp"] == 8 and mesh.shape["shard"] == 4
    placed = (
        P(("dp", "shard"), None),
        P(("dp", "shard"), None),
        P(("dp", "shard")),
        P(("dp", "shard")),
        P(None, None, "shard"),
        P(None, "shard", None, None),
        P("shard", None),
        P(None, None, "shard"),
        P("shard", None),
        P(None, "shard"),
        P(None, "shard"),
        P("shard"),
        P(None, "shard"),
        P("shard", "dp"),
        P("shard", "dp"),
        P("shard", "dp"),
    )
    return jax.shard_map(
        group_body if fits else body,
        mesh=mesh,
        in_specs=placed,
        out_specs=(
            P(("dp", "shard"), None),
            P(("dp", "shard"), None),
            P("shard", "dp"),
            P("shard", "dp"),
            P("shard", "dp"),
            P("shard", "dp"),
            P(None, "dp"),
            P(None, "shard"),
        ),
        check_vma=False,
    )
```

```python
import functools
import jax
import jax.numpy as jnp
from jax import lax
from jax.experimental import pallas as pl
from jax.experimental.pallas import tpu as pltpu
from jax.sharding import PartitionSpec as P

norm_eps = 1e-06
gate_scale = 8.0
beta_one = 0.9
beta_two = 0.95
learn_rate = 0.01
weight_decay = 0.1
adam_eps = 1e-08
corr_one = 1.0 - beta_one**10.0
corr_two = 1.0 - beta_two**10.0
low_type = jnp.bfloat16
wide = jnp.float32
gelu_scale = 0.7978845608028654
gelu_cube = 0.044715


def add_low(left, right):
    return (left.astype(wide) + right.astype(wide)).astype(low_type)


def dot_rows(left, right):
    return lax.dot_general(left, right, (((1,), (1,)), ((), ())), preferred_element_type=wide)


def dot_plain(left, right):
    return lax.dot_general(left, right, (((1,), (0,)), ((), ())), preferred_element_type=wide)


def dot_slots(left, right):
    return lax.dot_general(left, right, (((0,), (0,)), ((), ())), preferred_element_type=wide)


def gelu_parts(value):
    square = value * value
    bent = jnp.tanh(gelu_scale * value * (1.0 + gelu_cube * square))
    half = 0.5 * (1.0 + bent)
    slope = half + 0.5 * value * (1.0 - bent * bent) * gelu_scale * (
        1.0 + 3.0 * gelu_cube * square
    )
    return (value * half, slope)


def shift_down(value, step):
    if step % 8 == 0:
        return jnp.concatenate([value[-step:], value[:-step]], axis=0)
    return pltpu.roll(value, step, 0)


def shift_up(value, step):
    if step % 8 == 0:
        return jnp.concatenate([value[step:], value[:step]], axis=0)
    return pltpu.roll(value, value.shape[0] - step, 0)


def scan_slots(decay, value, shift):
    step = 1
    while step < value.shape[0]:
        value = value + decay * shift(value, step)
        if 2 * step < value.shape[0]:
            decay = decay * shift(decay, step)
        step *= 2
    return value


def one_minus_exp(value):
    series = jnp.ones_like(value)
    for number in range(11, 1, -1):
        series = 1.0 - value * (1.0 / number) * series
    return jnp.where(value < 0.8, value * series, 1.0 - jnp.exp(-value))


def soft_plus(value):
    return jnp.maximum(value, 0.0) + jnp.log1p(jnp.exp(-jnp.abs(value)))


def mixer_parts(first, position, small, gates):
    conv_out = small[4:5] + small[0:1] * first
    shifted = []
    for step in range(1, 4):
        moved = jnp.where(position >= step, shift_down(first, step), 0.0)
        shifted.append(moved)
        conv_out = conv_out + small[step : step + 1] * moved
    conv_low = conv_out.astype(low_type)
    logits = dot_plain(conv_low, gates)
    width = first.shape[1]
    recur_gate = jax.nn.sigmoid(logits[:, :width] + small[5:6])
    input_gate = jax.nn.sigmoid(logits[:, width:] + small[6:7])
    rate = gate_scale * soft_plus(-small[7:8])
    log_decay = -rate * recur_gate
    decay = jnp.where(position > 0, jnp.exp(log_decay), 0.0)
    gone = one_minus_exp(-2.0 * log_decay)
    root = jnp.sqrt(gone)
    return conv_out, shifted, conv_low, recur_gate, input_gate, rate, decay, gone, root


def weight_views(w_ref, width):
    model = w_ref.shape[2] - width
    proj = w_ref[0, 0 : 2 * width, 0:model]
    out = w_ref[0, 2 * width : 3 * width, 0:model]
    gates = jnp.concatenate(
        [w_ref[0, 0:width, model:], w_ref[0, width : 2 * width, model:]], axis=1
    )
    small = w_ref[0, 2 * width : 2 * width + 16, model:].astype(wide)
    return proj, out, gates, small


def slot_position(starts):
    slot = lax.broadcasted_iota(jnp.int32, (starts.shape[0], 1), 0)
    return slot - starts[:, 0:1].astype(wide).astype(jnp.int32)


def mixer_step(x, position, views, width):
    proj, out, gates, small = views
    projected = dot_rows(x, proj)
    conv_out, _, _, _, input_gate, _, decay, _, root = mixer_parts(
        projected[:, :width], position, small, gates
    )
    states = scan_slots(decay, root * input_gate * conv_out, shift_down)
    mixed_low = (states * gelu_parts(projected[:, width:])[0]).astype(low_type)
    return projected, states, mixed_low, dot_plain(mixed_low, out)


def mixer_back_step(position, views, projected, states, res_low, width):
    _, out, gates, small = views
    first = projected[:, :width]
    conv_out, shifted, conv_low, recur_gate, input_gate, rate, decay, gone, root = mixer_parts(
        first, position, small, gates
    )
    grad_mixed = dot_rows(res_low, out)
    active, slope = gelu_parts(projected[:, width:])
    grad_second = grad_mixed * states * slope
    adjoint = scan_slots(shift_up(decay, 1), grad_mixed * active, shift_up)
    grad_decay = adjoint * shift_down(states, 1)
    gated = adjoint * conv_out
    grad_root = gated * input_gate
    grad_input_gate = gated * root
    grad_conv = adjoint * root * input_gate
    grad_log = grad_decay * decay - grad_root * (1.0 - gone) / root
    grad_recur = -rate * grad_log
    grad_logit_a = grad_recur * recur_gate * (1.0 - recur_gate)
    grad_logit_b = grad_input_gate * input_gate * (1.0 - input_gate)
    grad_param = jnp.sum(grad_log * recur_gate, axis=0, keepdims=True) * (
        gate_scale * jax.nn.sigmoid(-small[7:8])
    )
    logits_low = jnp.concatenate([grad_logit_a, grad_logit_b], axis=1).astype(low_type)
    grad_conv = grad_conv + dot_rows(logits_low, gates)
    grad_gates = dot_slots(conv_low, logits_low)
    sums = [jnp.sum(grad_conv * first, axis=0, keepdims=True)]
    grad_first = small[0:1] * grad_conv
    for step in range(1, 4):
        sums.append(jnp.sum(grad_conv * shifted[step - 1], axis=0, keepdims=True))
        kept = jnp.where(position >= step, grad_conv, 0.0)
        grad_first = grad_first + small[step : step + 1] * shift_up(kept, step)
    sums.append(jnp.sum(grad_conv, axis=0, keepdims=True))
    sums.append(jnp.sum(grad_logit_a, axis=0, keepdims=True))
    sums.append(jnp.sum(grad_logit_b, axis=0, keepdims=True))
    sums.append(grad_param)
    proj_low = jnp.concatenate([grad_first, grad_second], axis=1).astype(low_type)
    return proj_low, grad_gates, jnp.concatenate(sums, axis=0)


def peer_x(chip):
    return chip + 1 - 2 * (chip % 2)


def peer_y(chip):
    return chip + 2 - 4 * (chip // 2)


def line_place(end, core):
    return end + core * (3 - 2 * end)


def remote(source, target, send, recv, member, z):
    return pltpu.make_async_remote_copy(
        src_ref=source,
        dst_ref=target,
        send_sem=send,
        recv_sem=recv,
        device_id=(member, z),
        device_id_type=pl.DeviceIdType.MESH,
    )


def enter(member, z):
    barrier = pltpu.get_barrier_semaphore()
    for other in range(8):

        @pl.when(member != other)
        def _():
            pl.semaphore_signal(
                barrier, inc=1, device_id=(other, z), device_id_type=pl.DeviceIdType.MESH
            )

    for other in range(4):

        @pl.when(z != other)
        def _():
            pl.semaphore_signal(
                barrier, inc=1, device_id=(member, other), device_id_type=pl.DeviceIdType.MESH
            )

    pl.semaphore_wait(barrier, 10)


def quarters(value_ref, shape):
    slots = shape[0]
    row = lax.broadcasted_iota(jnp.int32, shape, 0)
    result = jnp.full(shape, value_ref[3 * slots // 4], jnp.int32)
    for number in (2, 1, 0):
        result = jnp.where(
            row < (number + 1) * slots // 4, value_ref[number * slots // 4], result
        )
    return result


class Gather:
    def __init__(self, own, target, send, recv, member, z):
        self.own, self.target = own, target
        self.send, self.recv = send, recv
        chip, core = member // 2, member % 2
        self.to_x = peer_x(chip) * 2 + core
        self.to_y = peer_y(chip) * 2 + core
        self.z = z
        self.half = own.shape[0] // 2

    def copy(self, number):
        low, high = pl.ds(0, self.half), pl.ds(self.half, self.half)
        source, target, to = (
            (self.own, self.target.at[1], self.to_x),
            (self.own, self.target.at[2], self.to_y),
            (self.target.at[1, low], self.target.at[3, low], self.to_y),
            (self.target.at[2, high], self.target.at[3, high], self.to_x),
        )[number]
        return remote(source, target, self.send.at[number], self.recv.at[number], to, self.z)

    def begin(self):
        self.copy(0).start()
        self.copy(1).start()

    def relay(self):
        self.copy(0).wait_recv()
        self.copy(2).start()
        self.copy(1).wait_recv()
        self.copy(3).start()

    def arrive(self):
        self.copy(2).wait_recv()
        self.copy(3).wait_recv()

    def finish(self):
        for number in range(4):
            self.copy(number).wait_send()


class Reduce:
    def __init__(self, part, from_x, from_y, passing, last, send, recv, member, z):
        self.part, self.from_x, self.from_y = part, from_x, from_y
        self.passing, self.last = passing, last
        self.send, self.recv = send, recv
        chip, core = member // 2, member % 2
        self.to_x = peer_x(chip) * 2 + core
        self.to_y = peer_y(chip) * 2 + core
        self.z = z
        self.slots = part.shape[0] // 4
        self.half = self.slots // 2

    def copy(self, number):
        slots, half = self.slots, self.half
        source, target, to = (
            (self.part.at[pl.ds(slots, half)], self.from_x.at[0], self.to_x),
            (self.part.at[pl.ds(3 * slots, half)], self.from_x.at[1], self.to_x),
            (self.part.at[pl.ds(2 * slots + half, half)], self.from_y.at[0], self.to_y),
            (self.part.at[pl.ds(3 * slots + half, half)], self.from_y.at[1], self.to_y),
            (self.passing.at[0], self.last.at[0], self.to_y),
            (self.passing.at[1], self.last.at[1], self.to_x),
        )[number]
        return remote(source, target, self.send.at[number], self.recv.at[number], to, self.z)

    def begin(self):
        for block in (3, 1, 2):
            self.begin_block(block)

    def begin_block(self, block):
        for number in {1: (0,), 2: (2,), 3: (1, 3)}.get(block, ()):
            self.copy(number).start()

    def relay(self):
        slots, half = self.slots, self.half
        self.copy(1).wait_recv()
        self.passing[0] = (
            self.part[2 * slots : 2 * slots + half].astype(wide) + self.from_x[1].astype(wide)
        ).astype(low_type)
        self.copy(4).start()
        self.copy(3).wait_recv()
        self.passing[1] = (
            self.part[slots + half : 2 * slots].astype(wide) + self.from_y[1].astype(wide)
        ).astype(low_type)
        self.copy(5).start()

    def arrive(self):
        for number in (0, 2, 4, 5):
            self.copy(number).wait_recv()

    def result(self, number):
        direct = self.from_x if number == 0 else self.from_y
        return (
            self.part[number * self.half : (number + 1) * self.half].astype(wide)
            + direct[0].astype(wide)
            + self.last[number].astype(wide)
        )

    def finish(self):
        for number in range(6):
            self.copy(number).wait_send()

    @staticmethod
    def scratch(slots, model):
        return [pltpu.VMEM((2, slots // 2, model), low_type)] * 4


def norm_rows(value, gain):
    scale = lax.rsqrt(jnp.mean(value * value, axis=1, keepdims=True) + norm_eps)
    return value * scale * gain


def front_kernel(
    sizes,
    tokens_in,
    cot_in,
    start_ref,
    live_ref,
    gain_in,
    taps_ref,
    bias_ref,
    decay_ref,
    in_ref,
    gate_ref,
    out_ref,
    up_ref,
    down_ref,
    mix_in,
    weights,
    ffn_weights,
    saved_p,
    saved_state,
    saved_low,
    starts_out,
    residual_out,
    ffn_in,
    cot_out,
    gains_out,
    tokens_ref,
    cot_ref,
    gain_ref,
    tokens_all,
    raw_in,
    raw_up,
    raw_down,
    turned,
    gain_seen,
    acc,
    part,
    from_x,
    from_y,
    passing,
    last,
    load_sem,
    gain_send,
    gain_recv,
    m_send,
    m_recv,
    m_core_send,
    m_core_recv,
    f_send,
    f_recv,
    f_core_send,
    f_core_recv,
    g_send,
    g_recv,
    r_send,
    r_recv,
):
    model, width, ffn_width = sizes
    member = lax.axis_index("dp")
    z = lax.axis_index("shard")
    chip, core = member // 2, member % 2
    end = z + core * (3 - 2 * z)
    other = chip * 2 + 1 - core
    slots = cot_in.shape[0]
    half_ffn = ffn_width // 2
    owner = core == z // 2

    window = 128 * ((chip * ffn_width) // 128)
    skew = chip * ffn_width - window
    quarter = pl.ds(pl.multiple_of(chip * width, width), width)
    wide_window = pl.ds(pl.multiple_of(window, 128), raw_up.shape[2])

    def loads():
        found = [
            (out_ref.at[quarter], weights.at[end, pl.ds(2 * width, width), pl.ds(0, model)]),
        ]
        for kind in range(2):
            found.append((in_ref.at[kind, :, quarter], raw_in.at[kind]))
            found.append(
                (
                    gate_ref.at[kind, chip],
                    weights.at[end, pl.ds(kind * width, width), pl.ds(model, width)],
                )
            )
        found.append(
            (down_ref.at[pl.ds(pl.multiple_of(chip * ffn_width, 32), ffn_width)], raw_down)
        )
        for kind in range(2):
            found.append((up_ref.at[kind, :, wide_window], raw_up.at[kind]))
        return [
            pltpu.make_async_copy(source, target, load_sem.at[number])
            for number, (source, target) in enumerate(found)
        ]

    def turned_copy(kind):
        return pltpu.make_async_copy(
            raw_down
            if kind == 2
            else turned.at[kind, pl.ds(pl.multiple_of(skew, 32), ffn_width)],
            ffn_weights.at[kind, pl.ds(pl.multiple_of(2 * end * ffn_width, 32), ffn_width)],
            load_sem.at[9 + kind],
        )

    @pl.when(owner)
    def _():
        for copy in loads():
            copy.start()

    tokens_ref[:, :model] = tokens_in[...]
    tokens_ref[:, model:] = quarters(start_ref, (slots, width)).astype(wide).astype(low_type)
    live = quarters(live_ref, (slots, 128))[:, 0:1].astype(wide)
    cot_ref[...] = (cot_in[...].astype(wide) * live).astype(low_type)
    gain_ref[...] = jnp.concatenate(
        [gain_in[...].astype(wide), jnp.zeros((14, model // 4), wide)], axis=0
    ).astype(low_type)
    enter(member, z)

    gather_tokens = Gather(tokens_ref, tokens_all, g_send.at[0], g_recv.at[0], member, z)
    gather_cot = Gather(cot_ref, cot_out, g_send.at[1], g_recv.at[1], member, z)
    gather_ffn = Gather(ffn_in.at[0], ffn_in, g_send.at[2], g_recv.at[2], member, z)
    reduce = Reduce(part, from_x, from_y, passing, last, r_send, r_recv, member, z)
    own_cot = pltpu.make_async_copy(cot_ref, cot_out.at[0], load_sem.at[12])

    gather_tokens.begin()
    own_cot.start()

    def gain_copy(to, slot):
        return remote(
            gain_ref, gain_seen.at[slot], gain_send.at[to], gain_recv.at[slot], member, to
        )

    for to in range(4):

        @pl.when(to != z)
        def _():
            gain_copy(to, z).start()

    gain_seen[z] = gain_ref[...]

    def m_rows(number):
        return pl.ds(number * width, width)

    def m_copy(slot, number, way, to_end):
        place = weights.at[slot, m_rows(number)]
        return remote(
            place,
            place,
            m_send.at[way, slot, number],
            m_recv.at[slot, number],
            member,
            line_place(to_end, core),
        )

    def m_core(slot, number):
        return remote(
            weights.at[slot, m_rows(number)],
            weights.at[2 + slot, m_rows(number)],
            m_core_send.at[slot, number],
            m_core_recv.at[slot, number],
            other,
            z,
        )

    def f_place(slot, number):
        row = ((slot % 2) * 2 + slot // 2) * ffn_width + (number % 2) * half_ffn
        return ffn_weights.at[number // 2, pl.ds(row, half_ffn)]

    def f_copy(slot, number, way, to_end):
        place = f_place(slot, number)
        return remote(
            place,
            place,
            f_send.at[way, slot, number],
            f_recv.at[slot, number],
            member,
            line_place(to_end, core),
        )

    def f_core(slot, number):
        return remote(
            f_place(slot, number),
            f_place(2 + slot, number),
            f_core_send.at[slot, number],
            f_core_recv.at[slot, number],
            other,
            z,
        )

    def pass_on(copy, core_copy, slot, number):
        if slot == 0:

            @pl.when(end < 3)
            def _():
                copy(slot, number, 0, end + 1).start()
        else:

            @pl.when((end == 1) | (end == 2))
            def _():
                copy(slot, number, 0, end + 1).start()

        core_copy(slot, number).start()

    def pass_back(copy, numbers):
        @pl.when(end == 1)
        def _():
            for number in numbers:
                copy(1, number, 1, 0).start()

    def start_own(copy, core_copy, numbers):
        for slot in range(2):

            @pl.when(end == slot)
            def _():
                for number in numbers:
                    pass_on(copy, core_copy, slot, number)

    def turn_in(kind):
        @pl.when(owner)
        def _():
            for copy in loads()[1 + 2 * kind : 3 + 2 * kind]:
                copy.wait()

            def turn(at, carry):
                columns = pl.ds(pl.multiple_of(at * 256, 256), 256)
                weights[end, kind * width : (kind + 1) * width, columns] = raw_in[
                    kind, columns, :
                ].T
                return carry

            lax.fori_loop(0, model // 256, turn, 0)

        start_own(m_copy, m_core, (kind,))
        pass_back(m_copy, (kind,))

    def turn_up(kind):
        @pl.when(owner)
        def _():
            loads()[6 + kind].wait()

            def turn(at, carry):
                columns = pl.ds(pl.multiple_of(at * 256, 256), 256)
                turned[kind, :, columns] = raw_up[kind, columns, :].T
                return carry

            lax.fori_loop(0, model // 256, turn, 0)
            turned_copy(kind).start()

    @pl.when(owner)
    def _():
        weights[end, 2 * width : 3 * width, model:] = jnp.concatenate(
            [
                taps_ref[:, quarter].astype(wide),
                bias_ref[:, quarter].astype(wide),
                decay_ref[:, quarter].astype(wide),
                jnp.zeros((width - 8, width), wide),
            ],
            axis=0,
        ).astype(low_type)
        loads()[0].wait()

    start_own(m_copy, m_core, (2,))
    pass_back(m_copy, (2,))
    turn_in(0)
    turn_in(1)

    @pl.when(owner)
    def _():
        loads()[5].wait()
        turned_copy(2).start()

    turn_up(0)
    turn_up(1)
    gather_tokens.relay()
    m_order = (2, 0, 1)

    @pl.when(end < 3)
    def _():
        for number in m_order:
            for slot in (1, 0):

                @pl.when(end != slot)
                def _():
                    m_copy(slot, number, 0, 0).wait_recv()
                    pass_on(m_copy, m_core, slot, number)

    @pl.when(owner)
    def _():
        for kind in range(3):
            turned_copy(kind).wait()

    f_order = (4, 5, 0, 1, 2, 3)
    start_own(f_copy, f_core, f_order)

    def f_pass(slot, numbers):
        for number in numbers:
            f_copy(slot, number, 0, 0).wait_recv()
            pass_on(f_copy, f_core, slot, number)

    def f_step(step):
        @pl.when(end == 1)
        def _():
            f_pass(0, ((), (4, 5), (0, 1), (2, 3), (), ())[step])

        @pl.when(end == 2)
        def _():
            f_pass(1, ((4,), (5, 0), (1, 2), (3,), (), ())[step])
            f_pass(0, ((), (), (), (4,), (5, 0), (1, 2, 3))[step])

        if step == 0:
            pass_back(f_copy, f_order)

        @pl.when(end == 0)
        def _():
            f_pass(1, ((), (), (), (), (), f_order)[step])

    for to in range(4):

        @pl.when(to != z)
        def _():
            gain_copy(to, to).wait_recv()

    gains = jnp.concatenate([gain_seen[at].astype(wide) for at in range(4)], axis=1)
    gains_out[...] = gains[0:8]
    gather_tokens.arrive()

    def norm_block(block):
        if block == 0:
            source, starts = tokens_ref[:, :model], tokens_ref[:, model:]
        else:
            source, starts = tokens_all[block, :, :model], tokens_all[block, :, model:]
        at = slice(block * slots, (block + 1) * slots)
        mix_in[at, :] = norm_rows(source.astype(wide), gains_out[0:1]).astype(low_type)
        starts_out[at, :] = starts

    for block in range(4):
        norm_block(block)
    gather_cot.begin()
    f_step(0)

    late = end >= 2
    for turn in range(4):
        head = (turn + 2 * late) % 4
        if turn == 2:

            @pl.when(end == 3)
            def _():
                for number in m_order:
                    for slot in (1, 0):
                        m_copy(slot, number, 0, 0).wait_recv()
                        m_core(slot, number).start()

        @pl.when(head >= 2)
        def _():
            for number in m_order:
                m_core(head - 2, number).wait_recv()

        views = weight_views(weights.at[pl.ds(head, 1)], width)

        def step_block(block, carry):
            rows = pl.ds(pl.multiple_of(block * slots, slots), slots)
            position = slot_position(starts_out[rows, :])
            projected, states, mixed_low, product = mixer_step(
                mix_in[rows, :], position, views, width
            )
            saved_p[head, rows, :] = projected
            saved_state[head, rows, :] = states
            saved_low[head, rows, :] = mixed_low
            if turn == 0:
                acc[rows, :] = product
            elif turn < 3:
                acc[rows, :] += product
            else:
                part[rows, :] = (acc[rows, :] + product).astype(low_type)
            return carry

        lax.fori_loop(0, 4, step_block, 0)
        if turn == 3:
            reduce.begin()
        f_step(turn + 1)
        if turn == 0:
            gather_cot.relay()

    reduce.relay()
    f_step(5)
    reduce.arrive()
    half = slots // 2
    for number in range(2):
        at = slice(number * half, (number + 1) * half)
        residual = tokens_ref[at, :model].astype(wide) + reduce.result(number)
        residual_out[at, :] = residual
        ffn_in[0, at, :] = norm_rows(residual, gains_out[1:2]).astype(low_type)
    gather_ffn.begin()
    gather_ffn.relay()

    @pl.when(end == 3)
    def _():
        for slot in (1, 0):
            for number in f_order:
                f_copy(slot, number, 0, 0).wait_recv()
                f_core(slot, number).start()

    gather_ffn.arrive()
    gather_cot.arrive()
    own_cot.wait()
    for slot in range(2):
        for number in range(6):
            f_core(slot, number).wait_recv()

    for gather in (gather_tokens, gather_cot, gather_ffn, reduce):
        gather.finish()
    for to in range(4):

        @pl.when(to != z)
        def _():
            gain_copy(to, z).wait_send()

    for copy, core_copy, count in ((m_copy, m_core, 3), (f_copy, f_core, 6)):
        for number in range(count):
            for slot in range(2):
                core_copy(slot, number).wait_send()

            @pl.when(end < 3)
            def _():
                copy(0, number, 0, 0).wait_send()

            @pl.when((end == 1) | (end == 2))
            def _():
                copy(1, number, 0, 0).wait_send()

            @pl.when(end == 1)
            def _():
                copy(1, number, 1, 0).wait_send()


def front(
    tokens, cot, starts, live, gains, taps, bias, decay, in_proj, gates, out_proj, gate_up, down, sizes
):
    model, width, ffn_width = sizes
    slots = cot.shape[0]
    rows = 4 * slots
    dma = pltpu.SemaphoreType.DMA
    vmem = pl.BlockSpec(memory_space=pltpu.VMEM)
    anywhere = pl.BlockSpec(memory_space=pl.ANY)
    scalars = pl.BlockSpec(memory_space=pltpu.SMEM)
    window = -(-ffn_width // 128) * 128
    return pl.pallas_call(
        functools.partial(front_kernel, sizes),
        in_specs=[vmem] * 2 + [scalars] * 2 + [vmem] * 4 + [anywhere] * 5,
        out_specs=[vmem, vmem, anywhere, vmem, vmem, vmem, vmem, vmem, vmem, anywhere, vmem],
        out_shape=[
            jax.ShapeDtypeStruct((rows, model), low_type),
            jax.ShapeDtypeStruct((4, 3 * width, model + width), low_type),
            jax.ShapeDtypeStruct((3, 4 * ffn_width, model), low_type),
            jax.ShapeDtypeStruct((4, rows, 2 * width), wide),
            jax.ShapeDtypeStruct((4, rows, width), wide),
            jax.ShapeDtypeStruct((4, rows, width), low_type),
            jax.ShapeDtypeStruct((rows, width), low_type),
            jax.ShapeDtypeStruct((slots, model), wide),
            jax.ShapeDtypeStruct((4, slots, model), low_type),
            jax.ShapeDtypeStruct((4, slots, model), low_type),
            jax.ShapeDtypeStruct((8, model), wide),
        ],
        scratch_shapes=[
            pltpu.VMEM((slots, model + width), low_type),
            pltpu.VMEM((slots, model), low_type),
            pltpu.VMEM((16, model // 4), low_type),
            pltpu.VMEM((4, slots, model + width), low_type),
            pltpu.VMEM((2, model, width), low_type),
            pltpu.VMEM((2, model, window), low_type),
            pltpu.VMEM((ffn_width, model), low_type),
            pltpu.VMEM((2, window, model), low_type),
            pltpu.VMEM((4, 16, model // 4), low_type),
            pltpu.VMEM((rows, model), wide),
            pltpu.VMEM((rows, model), low_type),
        ]
        + Reduce.scratch(slots, model)
        + [
            dma((13,)),
            dma((4,)),
            dma((4,)),
            dma((2, 2, 3)),
            dma((2, 3)),
            dma((2, 3)),
            dma((2, 3)),
            dma((2, 2, 6)),
            dma((2, 6)),
            dma((2, 6)),
            dma((2, 6)),
            dma((3, 4)),
            dma((3, 4)),
            dma((6,)),
            dma((6,)),
        ],
        compiler_params=pltpu.CompilerParams(
            collective_id=3, has_side_effects=True, vmem_limit_bytes=60 * 1024 * 1024
        ),
        cost_estimate=pl.CostEstimate(
            flops=2 * rows * model * 4 * width * 3,
            bytes_accessed=6 * ffn_width * 4 * model,
            transcendentals=rows * 4 * width * 6,
        ),
        name="front",
    )(tokens, cot, starts, live, gains, taps, bias, decay, in_proj, gates, out_proj, gate_up, down)


def middle_kernel(
    sizes,
    x_hbm,
    go_hbm,
    weights_ref,
    residual_ref,
    gain_ref,
    total,
    inner_down,
    res_low,
    res_out,
    gain_out,
    part_out,
    x_ref,
    go_ref,
    held,
    lows,
    paired,
    arrived,
    part_in,
    in_x,
    in_y,
    in_pass,
    in_last,
    load_sem,
    core_send,
    core_recv,
    line_send,
    line_recv,
    i_send,
    i_recv,
    g_send,
    g_recv,
):
    model, ffn_width = sizes
    member = lax.axis_index("dp")
    z = lax.axis_index("shard")
    chip, core = member // 2, member % 2
    end = z + core * (3 - 2 * z)
    other = chip * 2 + 1 - core
    slots = residual_ref.shape[0]
    half = slots // 2
    hidden = 4 * ffn_width
    half_ffn = ffn_width // 2

    split = -(-2 * ffn_width // 128) * 128

    def weight_load(low, high, number):
        at = pl.ds(low, high - low)
        return pltpu.make_async_copy(
            weights_ref.at[:, at], held.at[:, at], load_sem.at[number]
        )

    loads = [
        weight_load(0, split, 0),
        pltpu.make_async_copy(x_hbm, x_ref, load_sem.at[1]),
        pltpu.make_async_copy(go_hbm, go_ref, load_sem.at[2]),
        weight_load(split, hidden, 3),
    ]
    for load in loads:
        load.start()
    enter(member, z)
    for load in loads[:3]:
        load.wait()

    def block_step(low, high, block, carry):
        rows = pl.ds(pl.multiple_of(block * slots, slots), slots)
        x = x_ref[rows, :]
        grad_out = go_ref[rows, :]
        pre_gate = dot_rows(x, held[0, low:high])
        pre_up = dot_rows(x, held[1, low:high])
        active, slope = gelu_parts(pre_gate)
        ffn_low = (active * pre_up).astype(low_type)
        grad_act = dot_rows(grad_out, held[2, low:high])
        gate_low = (grad_act * pre_up * slope).astype(low_type)
        up_low = (grad_act * active).astype(low_type)
        sum_out = dot_plain(ffn_low, held[2, low:high])
        sum_in = dot_plain(gate_low, held[0, low:high]) + dot_plain(up_low, held[1, low:high])
        lows[0, rows, low:high] = gate_low
        lows[1, rows, low:high] = up_low
        lows[2, rows, low:high] = ffn_low
        if low > 0:
            sum_in = sum_in + part_in[rows, :].astype(wide)
            sum_out = sum_out + part_out[rows, :].astype(wide)
        part_in[rows, :] = sum_in.astype(low_type)
        part_out[rows, :] = sum_out.astype(low_type)
        return carry

    reduce_in = Reduce(part_in, in_x, in_y, in_pass, in_last, i_send, i_recv, member, z)
    gather = Gather(res_low.at[0], res_low, g_send, g_recv, member, z)
    middle = model // 2

    def weight_grads(kind, low, high):
        factor = go_ref if kind == 2 else x_ref
        for at in range(2):
            columns = slice(at * middle, (at + 1) * middle)
            held[kind, low:high, columns] = dot_slots(
                lows[kind, :, low:high], factor[:, columns]
            ).astype(low_type)

    def core_copy(slot, kind):
        return remote(
            held.at[kind, pl.ds((2 * slot + 1) * ffn_width, ffn_width)],
            paired.at[slot, kind],
            core_send.at[slot, kind],
            core_recv.at[slot, kind],
            other,
            z,
        )

    def chunk(number):
        return number // 2, pl.ds((number % 2) * half_ffn, half_ffn)

    def line_copy(kind, number, to_end):
        at, rows = chunk(number)
        return remote(
            paired.at[min(kind, 1), at, rows],
            arrived.at[kind, at, rows],
            line_send.at[kind, number],
            line_recv.at[kind, number],
            member,
            line_place(to_end, core),
        )

    def pair_up(slot, kind):
        core_copy(slot, kind).wait_recv()
        for number in (2 * kind, 2 * kind + 1):
            at, rows = chunk(number)
            own = held[at, pl.ds(2 * slot * ffn_width + (number % 2) * half_ffn, half_ffn)]
            paired[slot, at, rows] = add_low(own, paired[slot, at, rows])

            if slot == 0 or number < 4:

                @pl.when(end == 3)
                def _():
                    line_copy(slot, number, 2).start()

            if slot == 1 and number < 4:

                @pl.when(end == 0)
                def _():
                    line_copy(2, number, 1).start()

    def part_grads(slot, low, high):
        for kind in range(3):
            weight_grads(kind, low, high)
            core_copy(slot, kind).start()
            if kind > 0:
                pair_up(slot, kind - 1)
        pair_up(slot, 2)

    def summed(slot, kinds, number):
        at, rows = chunk(number)
        result = paired[slot, at, rows].astype(wide)
        for kind in kinds:
            result = result + arrived[kind, at, rows].astype(wide)
        return result.astype(low_type)

    def outer_step(number):
        at, rows = chunk(number)

        @pl.when((end == 2) | (end == 1))
        def _():
            line_copy(0, number, 0).wait_recv()
            paired[0, at, rows] = summed(0, (0,), number)
            line_copy(0, number, end - 1).start()

    def inner_step(number):
        at, rows = chunk(number)

        @pl.when(end == 2)
        def _():
            line_copy(1, number, 0).wait_recv()
            paired[1, at, rows] = summed(1, (1,), number)
            line_copy(1, number, 1).start()

    def out_copy(slot, number):
        at, rows = chunk(number)
        return pltpu.make_async_copy(
            paired.at[slot, at, rows], total.at[at, rows], load_sem.at[number]
        )

    def last_step(number):
        at, rows = chunk(number)

        if number < 4:

            @pl.when(end == 1)
            def _():
                line_copy(1, number, 0).wait_recv()
                line_copy(2, number, 0).wait_recv()
                paired[1, at, rows] = summed(1, (1, 2), number)
                out_copy(1, number).start()

        @pl.when(end == 0)
        def _():
            line_copy(0, number, 0).wait_recv()
            paired[0, at, rows] = summed(0, (0,), number)
            out_copy(0, number).start()

    lax.fori_loop(0, 4, functools.partial(block_step, 0, split), 0)
    part_grads(0, 0, split)
    loads[3].wait()
    lax.fori_loop(0, 4, functools.partial(block_step, split, hidden), 0)
    reduce_in.begin()
    part_grads(1, split, hidden)
    inner_copy = pltpu.make_async_copy(paired.at[1, 2], inner_down, load_sem.at[6])
    inner_copy.start()
    for number in range(3):
        outer_step(number)
    reduce_in.relay()
    for number in range(3, 6):
        outer_step(number)

    reduce_in.arrive()
    gain = gain_ref[1:2]
    gain_sum = jnp.zeros((1, model), wide)
    for number in range(2):
        at = slice(number * half, (number + 1) * half)
        grad = reduce_in.result(number)
        value = residual_ref[at]
        scale = lax.rsqrt(jnp.mean(value * value, axis=1, keepdims=True) + norm_eps)
        scaled = grad * gain
        gain_sum = gain_sum + jnp.sum(grad * value * scale, axis=0, keepdims=True)
        inner = jnp.mean(scaled * value, axis=1, keepdims=True)
        back = scale * scaled - value * (scale * scale * scale * inner)
        result = go_ref[at].astype(wide) + back
        res_out[at] = result
        res_low[0, at] = result.astype(low_type)
    gain_out[...] = jnp.concatenate([gain_ref[0:1], gain_sum, jnp.zeros((6, model), wide)], axis=0)
    gather.begin()
    inner_step(0)
    gather.relay()
    inner_step(1)
    inner_step(2)
    inner_step(3)
    gather.arrive()
    for number in range(6):
        last_step(number)
    inner_copy.wait()

    for sent in (reduce_in, gather):
        sent.finish()
    for slot in range(2):
        for kind in range(3):
            core_copy(slot, kind).wait_send()
    for number in range(6):

        @pl.when(end > 0)
        def _():
            line_copy(0, number, 0).wait_send()

        @pl.when(end == 0)
        def _():
            out_copy(0, number).wait()

    for number in range(4):

        @pl.when(end > 1)
        def _():
            line_copy(1, number, 0).wait_send()

        @pl.when(end == 1)
        def _():
            out_copy(1, number).wait()

        @pl.when(end == 0)
        def _():
            line_copy(2, number, 1).wait_send()


def middle(x, grad_out, weights, residual, gains):
    rows, model = x.shape
    hidden = weights.shape[1]
    ffn_width = hidden // 4
    slots = rows // 4
    dma = pltpu.SemaphoreType.DMA
    vmem = pl.BlockSpec(memory_space=pltpu.VMEM)
    anywhere = pl.BlockSpec(memory_space=pl.ANY)
    quarter = (3, ffn_width, model)
    return pl.pallas_call(
        functools.partial(middle_kernel, (model, ffn_width)),
        in_specs=[anywhere] * 3 + [vmem] * 2,
        out_specs=[anywhere] * 2 + [vmem] * 4,
        out_shape=[
            jax.ShapeDtypeStruct(quarter, low_type),
            jax.ShapeDtypeStruct(quarter[1:], low_type),
            jax.ShapeDtypeStruct((4, slots, model), low_type),
            jax.ShapeDtypeStruct((slots, model), wide),
            jax.ShapeDtypeStruct((8, model), wide),
            jax.ShapeDtypeStruct((rows, model), low_type),
        ],
        scratch_shapes=[
            pltpu.VMEM(x.shape, low_type),
            pltpu.VMEM(x.shape, low_type),
            pltpu.VMEM(weights.shape, low_type),
            pltpu.VMEM((3, rows, hidden), low_type),
            pltpu.VMEM((2,) + quarter, low_type),
            pltpu.VMEM((3,) + quarter, low_type),
            pltpu.VMEM((rows, model), low_type),
        ]
        + Reduce.scratch(slots, model)
        + [
            dma((7,)),
            dma((2, 3)),
            dma((2, 3)),
            dma((3, 6)),
            dma((3, 6)),
            dma((6,)),
            dma((6,)),
            dma((4,)),
            dma((4,)),
        ],
        compiler_params=pltpu.CompilerParams(
            collective_id=4, has_side_effects=True, vmem_limit_bytes=63 * 1024 * 1024
        ),
        cost_estimate=pl.CostEstimate(
            flops=2 * rows * model * hidden * 9,
            bytes_accessed=weights.size * 4 + rows * model * 16,
            transcendentals=rows * hidden,
        ),
        name="middle",
    )(x, grad_out, weights, residual, gains)


class Scatter:
    def __init__(self, sizes, member, z, send_sem, recv_sem):
        self.model, self.width, self.ffn_width, self.piece_length = sizes
        self.member, self.z = member, z
        self.chip, self.core = member // 2, member % 2
        self.owner = self.core == z // 2
        self.send_sem, self.recv_sem = send_sem, recv_sem
        self.across = self.model // 128
        rec, ffn, model = 4 * self.width, 4 * self.ffn_width, self.model
        self.gate_base = 2 * model * rec
        self.out_base = self.gate_base + 8 * self.width * self.width
        self.up_base = self.out_base + rec * model
        self.down_base = self.up_base + 2 * model * ffn
        self.rec, self.ffn = rec, ffn
        self.first_in = 0
        self.first_gate = 2 * self.across
        self.first_out = self.first_gate + 2
        self.first_small = self.first_out + 4
        self.first_up = self.first_small + 1
        self.first_down = self.first_up + 2 * self.across
        self.count = self.first_down + 6

    def in_unit(self, number, q):
        kind, at = number // self.across, number % self.across
        low = (kind * self.model + at * 128) * self.rec
        where = (
            pl.ds(pl.multiple_of(kind * self.width, self.width), self.width),
            pl.ds(pl.multiple_of(at * 128, 128), 128),
        )
        return self.first_in + number, where, low, low + 128 * self.rec

    def gate_unit(self, kind, q):
        low = self.gate_base + (kind * 4 + q) * self.width * self.width
        where = (
            pl.ds(pl.multiple_of(kind * self.width, self.width), self.width),
            pl.ds(self.model, self.width),
        )
        return self.first_gate + kind, where, low, low + self.width * self.width

    def out_unit(self, number, q):
        rows = self.width // 4
        low = self.out_base + (q * self.width + number * rows) * self.model
        where = (
            pl.ds(pl.multiple_of(2 * self.width + number * rows, rows), rows),
            pl.ds(0, self.model),
        )
        return self.first_out + number, where, low, low + rows * self.model

    def up_unit(self, number, q):
        kind, at = number // self.across, number % self.across
        low = self.up_base + (kind * self.model + at * 128) * self.ffn
        where = (kind, pl.ds(0, self.ffn_width), pl.ds(pl.multiple_of(at * 128, 128), 128))
        return self.first_up + number, where, low, low + 128 * self.ffn

    def down_unit(self, number, q):
        rows = self.ffn_width // 6
        low = self.down_base + (q * self.ffn_width + number * rows) * self.model
        where = (2, pl.ds(pl.multiple_of(number * rows, 16), rows), pl.ds(0, self.model))
        return self.first_down + number, where, low, low + rows * self.model

    def small_where(self):
        return (pl.ds(2 * self.width, 16), pl.ds(self.model, self.width))

    def copies(self, unit, source, target, q, act, flat=False):
        number, where, low, high = unit
        here = where[1:] if flat else where
        first = low // self.piece_length
        last = (high - 1) // self.piece_length
        for which, to in ((0, first), (1, last)):
            wanted = True if which == 0 else last != first

            @pl.when((to != self.member) & wanted)
            def _():
                act(
                    remote(
                        source.at[here],
                        target.at[(q,) + where],
                        self.send_sem.at[which, number],
                        self.recv_sem.at[q, number],
                        to,
                        self.z,
                    ),
                    True,
                )

            @pl.when((to == self.member) & wanted)
            def _():
                act(
                    pltpu.make_async_copy(
                        source.at[here], target.at[(q,) + where], self.recv_sem.at[q, number]
                    ),
                    False,
                )

    def each(self, unit_of, low, high, source, target, act, flat=False):
        def body(number, carry):
            self.copies(unit_of(number, self.chip), source, target, self.chip, act, flat)
            return carry

        lax.fori_loop(low, high, body, 0)

    def smalls(self, source, target, act):
        where = self.small_where()
        for to in range(8):

            @pl.when(self.member != to)
            def _():
                act(
                    remote(
                        source.at[where],
                        target.at[(self.chip,) + where],
                        self.send_sem.at[2, to],
                        self.recv_sem.at[self.chip, self.first_small],
                        to,
                        self.z,
                    ),
                    True,
                )

        act(
            pltpu.make_async_copy(
                source.at[where],
                target.at[(self.chip,) + where],
                self.recv_sem.at[self.chip, self.first_small],
            ),
            False,
        )

    def arrivals(self, unit_of, count, source, target):
        low = self.member * self.piece_length

        def body(number, carry):
            for q in range(4):
                index, where, first, last = unit_of(number, q)
                mine = (first < low + self.piece_length) & (last > low)
                here = (self.chip == q) & self.owner

                @pl.when(mine & here)
                def _():
                    pltpu.make_async_copy(
                        source.at[where], target.at[(q,) + where], self.recv_sem.at[q, index]
                    ).wait()

                @pl.when(mine & jnp.logical_not(here))
                def _():
                    remote(
                        source.at[where],
                        target.at[(q,) + where],
                        self.send_sem.at[0, index],
                        self.recv_sem.at[q, index],
                        self.member,
                        self.z,
                    ).wait_recv()

            return carry

        lax.fori_loop(0, count, body, 0)

    def small_arrivals(self, source, target):
        where = self.small_where()
        for q in range(4):
            here = (self.chip == q) & self.owner

            @pl.when(here)
            def _():
                pltpu.make_async_copy(
                    source.at[where],
                    target.at[(q,) + where],
                    self.recv_sem.at[q, self.first_small],
                ).wait()

            @pl.when(jnp.logical_not(here))
            def _():
                remote(
                    source.at[where],
                    target.at[(q,) + where],
                    self.send_sem.at[2, 0],
                    self.recv_sem.at[q, self.first_small],
                    self.member,
                    self.z,
                ).wait_recv()


def begin(copy, is_remote):
    copy.start()


def finish_send(copy, is_remote):
    if is_remote:
        copy.wait_send()


def back_kernel(
    sizes,
    x_hbm,
    res_hbm,
    starts_ref,
    w_hbm,
    p_hbm,
    state_hbm,
    low_hbm,
    ffn_ref,
    inner_hbm,
    tokens_ref,
    res_ref,
    gain_ref,
    mix_out,
    ffn_out,
    tokens_out,
    gain_out,
    x_ref,
    low_res,
    w_ref,
    p_ref,
    state_ref,
    low_ref,
    proj_grads,
    gate_acc,
    small_acc,
    grads,
    part_ref,
    paired,
    arrived,
    total,
    from_x,
    from_y,
    passing,
    last,
    inner,
    inner_seen,
    gain_part,
    gain_plane,
    gain_line,
    gain_seen,
    load_sem,
    core_send,
    core_recv,
    line_send,
    line_recv,
    plane_send,
    plane_recv,
    inner_send,
    inner_recv,
    gain_send,
    gain_recv,
    unit_send,
    unit_recv,
):
    model, width, ffn_width, piece_length = sizes
    member = lax.axis_index("dp")
    z = lax.axis_index("shard")
    chip, core = member // 2, member % 2
    end = z + core * (3 - 2 * z)
    slots = tokens_ref.shape[0]
    half = slots // 2
    other = chip * 2 + 1 - core
    scatter = Scatter(sizes, member, z, unit_send, unit_recv)

    order = (2, 0, 3, 1)
    common = [
        pltpu.make_async_copy(x_hbm, x_ref, load_sem.at[4, 0]),
        pltpu.make_async_copy(res_hbm, low_res, load_sem.at[4, 1]),
    ]
    early = [pltpu.make_async_copy(inner_hbm, inner, load_sem.at[4, 2])]

    def head_loads(head):
        return [
            pltpu.make_async_copy(source.at[head], target.at[head], load_sem.at[head, number])
            for number, (source, target) in enumerate(
                ((w_hbm, w_ref), (p_hbm, p_ref), (state_hbm, state_ref), (low_hbm, low_ref))
            )
        ]

    for copy in early + head_loads(order[0]) + common:
        copy.start()
    for head in order[1:]:
        for copy in head_loads(head):
            copy.start()
    enter(member, z)

    half_ffn = ffn_width // 2

    def inner_copy(kind, number, to_end):
        at = pl.ds(number * half_ffn, half_ffn)
        return remote(
            inner.at[at],
            inner_seen.at[kind, at],
            inner_send.at[kind, number],
            inner_recv.at[kind, number],
            member,
            line_place(to_end, core),
        )

    def inner_add(kinds, number):
        at = pl.ds(number * half_ffn, half_ffn)
        result = inner[at].astype(wide)
        for kind in kinds:
            inner_copy(kind, number, 0).wait_recv()
            result = result + inner_seen[kind, at].astype(wide)
        inner[at] = result.astype(low_type)

    def inner_far(number):
        @pl.when(end == 2)
        def _():
            inner_add((0,), number)
            inner_copy(0, number, 1).start()

    def inner_last():
        @pl.when(end == 1)
        def _():
            inner_add((0, 1), 0)
            inner_add((0, 1), 1)
            scatter.each(scatter.down_unit, 0, 6, inner, ffn_out, begin, True)

    for copy in early:
        copy.wait()
    for number in range(2):

        @pl.when(end == 3)
        def _():
            inner_copy(0, number, 2).start()

        @pl.when(end == 0)
        def _():
            inner_copy(1, number, 1).start()

    @pl.when(scatter.owner)
    def _():
        scatter.each(scatter.up_unit, 0, 2 * scatter.across, ffn_ref, ffn_out, begin)

    @pl.when(end == 0)
    def _():
        scatter.each(scatter.down_unit, 0, 6, ffn_ref, ffn_out, begin)

    def rows(number):
        return pl.ds(number * width, width)

    def core_copy(slot, number):
        return remote(
            grads.at[2 + slot, rows(number)],
            paired.at[slot, rows(number)],
            core_send.at[slot, number],
            core_recv.at[slot, number],
            other,
            z,
        )

    reduce = Reduce(
        part_ref, from_x, from_y, passing, last, plane_send, plane_recv, member, z
    )

    def line_copy(kind, number, source, to_end):
        return remote(
            source,
            arrived.at[kind, rows(number)],
            line_send.at[kind, number],
            line_recv.at[kind, number],
            member,
            line_place(to_end, core),
        )

    def pair_up(slot):
        for number in range(3):
            core_copy(slot, number).wait_recv()
            both = grads[slot, rows(number)].astype(wide) + paired[slot, rows(number)].astype(wide)
            paired[slot, rows(number)] = both.astype(low_type)

            @pl.when(end == 3)
            def _():
                line_copy(slot, number, paired.at[slot, rows(number)], 2).start()

            if slot == 1:

                @pl.when(end == 0)
                def _():
                    line_copy(2, number, paired.at[slot, rows(number)], 1).start()

    def summed(slot, kinds, number):
        result = paired[slot, rows(number)].astype(wide)
        for kind in kinds:
            result = result + arrived[kind, rows(number)].astype(wide)
        return result.astype(low_type)

    def on_arrival(kind, number):
        line_copy(kind, number, paired.at[0, rows(number)], 0).wait_recv()

    def outer_step(place, number):
        @pl.when(end == place)
        def _():
            on_arrival(0, number)
            paired[0, rows(number)] = summed(0, (0,), number)
            line_copy(0, number, paired.at[0, rows(number)], place - 1).start()

    def share(number):
        if number < 2:
            across = scatter.across
            scatter.each(
                scatter.in_unit, number * across, (number + 1) * across, total, mix_out, begin
            )
            scatter.each(scatter.gate_unit, number, number + 1, total, mix_out, begin)
        else:
            scatter.each(scatter.out_unit, 0, 4, total, mix_out, begin)
            scatter.smalls(total, mix_out, begin)

    for copy in common:
        copy.wait()
    for turn, head in enumerate(order):
        for copy in head_loads(head):
            copy.wait()
        views = weight_views(w_ref.at[pl.ds(head, 1)], width)
        gate_acc[...] = jnp.zeros_like(gate_acc)
        small_acc[...] = jnp.zeros_like(small_acc)

        def step_block(block, carry):
            at = pl.ds(pl.multiple_of(block * slots, slots), slots)
            proj_low, grad_gates, grad_small = mixer_back_step(
                slot_position(starts_ref[at, :]),
                views,
                p_ref[head, at, :],
                state_ref[head, at, :],
                low_res[at, :],
                width,
            )
            proj_grads[at, head * 2 * width : (head + 1) * 2 * width] = proj_low
            gate_acc[...] += grad_gates
            small_acc[...] += grad_small
            return carry

        lax.fori_loop(0, 4, step_block, 0)
        grads[head, 0 : 2 * width, 0:model] = dot_slots(
            proj_grads[:, head * 2 * width : (head + 1) * 2 * width], x_ref[...]
        ).astype(low_type)
        grads[head, 2 * width : 3 * width, 0:model] = dot_slots(
            low_ref[head], low_res[...]
        ).astype(low_type)
        grads[head, 0:width, model:] = gate_acc[:, :width].astype(low_type)
        grads[head, width : 2 * width, model:] = gate_acc[:, width:].astype(low_type)
        grads[head, 2 * width : 3 * width, model:] = jnp.concatenate(
            [small_acc[...], jnp.zeros((width - 8, width), wide)], axis=0
        ).astype(low_type)
        if head >= 2:
            for number in range(3):
                core_copy(head - 2, number).start()
        if turn == 1:
            pair_up(0)
            inner_far(0)
        elif turn == 2:
            inner_far(1)
            outer_step(2, 0)
            outer_step(2, 1)
        elif turn == 3:
            inner_last()
            outer_step(2, 2)
            outer_step(1, 0)
            outer_step(1, 1)

    def in_block(block):
        at = slice(block * slots, (block + 1) * slots)
        result = jnp.zeros((slots, model), wide)
        for head in range(4):
            result = result + dot_plain(
                proj_grads[at, head * 2 * width : (head + 1) * 2 * width],
                w_ref[head, 0 : 2 * width, 0:model],
            )
        part_ref[at, :] = result.astype(low_type)

    for block in (3, 1, 2, 0):
        in_block(block)
        reduce.begin_block(block)
        if block == 3:
            pair_up(1)
    outer_step(1, 2)
    across = scatter.across
    scatter.arrivals(scatter.up_unit, 2 * across, ffn_ref, ffn_out)

    @pl.when(scatter.owner)
    def _():
        scatter.each(scatter.up_unit, 0, 2 * across, ffn_ref, ffn_out, finish_send)

    reduce.relay()

    for number in range(3):

        @pl.when(end == 2)
        def _():
            on_arrival(1, number)
            paired[1, rows(number)] = summed(1, (1,), number)
            line_copy(1, number, paired.at[1, rows(number)], 1).start()

        @pl.when(end == 1)
        def _():
            on_arrival(1, number)
            on_arrival(2, number)
            total[rows(number)] = summed(1, (1, 2), number)

        @pl.when(end == 0)
        def _():
            on_arrival(0, number)
            total[rows(number)] = summed(0, (0,), number)

        @pl.when(scatter.owner)
        def _():
            share(number)

    reduce.arrive()
    gain = gain_ref[0:1]
    gain_sum = jnp.zeros((1, model), wide)
    for number in range(2):
        at = slice(number * half, (number + 1) * half)
        grad = reduce.result(number)
        value = tokens_ref[at].astype(wide)
        scale = lax.rsqrt(jnp.mean(value * value, axis=1, keepdims=True) + norm_eps)
        scaled = grad * gain
        gain_sum = gain_sum + jnp.sum(grad * value * scale, axis=0, keepdims=True)
        drift = jnp.mean(scaled * value, axis=1, keepdims=True)
        back = scale * scaled - value * (scale * scale * scale * drift)
        tokens_out[at] = (res_ref[at] + back).astype(low_type)
    gain_part[...] = jnp.concatenate([gain_sum, gain_ref[1:2], jnp.zeros((6, model), wide)], axis=0)

    def gain_copy():
        return remote(
            gain_part, gain_plane.at[member], gain_send.at[0], gain_recv.at[member], 7, z
        )

    @pl.when(member != 7)
    def _():
        gain_copy().start()
        gain_copy().wait_send()
        gain_out[...] = jnp.zeros_like(gain_out)

    @pl.when(member == 7)
    def _():
        result = gain_part[...]
        for source in range(7):
            remote(
                gain_part,
                gain_plane.at[source],
                gain_send.at[0],
                gain_recv.at[source],
                7,
                z,
            ).wait_recv()
            result = result + gain_plane[source]
        quarter = model // 4
        for place in range(4):
            gain_line[place] = result[:, place * quarter : (place + 1) * quarter]

        def line_gain(place, slot):
            return remote(
                gain_line.at[place],
                gain_seen.at[slot],
                gain_send.at[1 + place],
                gain_recv.at[8 + slot],
                7,
                place,
            )

        for place in range(4):

            @pl.when(place != z)
            def _():
                line_gain(place, z).start()

        gain_out[...] = gain_line[z]
        for place in range(4):

            @pl.when(place != z)
            def _():
                line_gain(place, place).wait_recv()
                gain_out[...] += gain_seen[place]
                line_gain(place, z).wait_send()

    scatter.arrivals(scatter.down_unit, 6, ffn_ref, ffn_out)
    scatter.arrivals(scatter.in_unit, 2 * across, total, mix_out)
    scatter.arrivals(scatter.gate_unit, 2, total, mix_out)
    scatter.arrivals(scatter.out_unit, 4, total, mix_out)
    scatter.small_arrivals(total, mix_out)

    @pl.when(scatter.owner)
    def _():
        scatter.each(scatter.down_unit, 0, 6, ffn_ref, ffn_out, finish_send)
        scatter.each(scatter.in_unit, 0, 2 * across, total, mix_out, finish_send)
        scatter.each(scatter.gate_unit, 0, 2, total, mix_out, finish_send)
        scatter.each(scatter.out_unit, 0, 4, total, mix_out, finish_send)
        scatter.smalls(total, mix_out, finish_send)

    reduce.finish()
    for number in range(2):

        @pl.when(end >= 2)
        def _():
            inner_copy(0, number, 0).wait_send()

        @pl.when(end == 0)
        def _():
            inner_copy(1, number, 0).wait_send()

    for slot in range(2):
        for number in range(3):
            core_copy(slot, number).wait_send()
    for number in range(3):

        @pl.when(end > 0)
        def _():
            line_copy(0, number, paired.at[0, rows(number)], 0).wait_send()

        @pl.when(end > 1)
        def _():
            line_copy(1, number, paired.at[1, rows(number)], 0).wait_send()

        @pl.when(end == 0)
        def _():
            line_copy(2, number, paired.at[1, rows(number)], 1).wait_send()


def back(
    x,
    res,
    starts,
    weights,
    saved,
    ffn,
    inner,
    tokens,
    residual_grad,
    gains,
    piece_length,
    width,
):
    model = tokens.shape[1]
    ffn_width = ffn.shape[1]
    sizes = (model, width, ffn_width, piece_length)
    slots = tokens.shape[0]
    block = weights.shape[1:]
    count = Scatter(sizes, 0, 0, None, None).count
    dma = pltpu.SemaphoreType.DMA
    vmem = pl.BlockSpec(memory_space=pltpu.VMEM)
    anywhere = pl.BlockSpec(memory_space=pl.ANY)
    held = lambda value: pltpu.VMEM(value.shape, value.dtype)
    return pl.pallas_call(
        functools.partial(back_kernel, sizes),
        in_specs=[anywhere, anywhere, vmem] + [anywhere] * 6 + [vmem] * 3,
        out_specs=[anywhere, anywhere, vmem, vmem],
        out_shape=[
            jax.ShapeDtypeStruct(weights.shape, low_type),
            jax.ShapeDtypeStruct((4,) + ffn.shape, low_type),
            jax.ShapeDtypeStruct(tokens.shape, low_type),
            jax.ShapeDtypeStruct((8, model // 4), wide),
        ],
        scratch_shapes=[held(x), held(res), held(weights)]
        + [held(value) for value in saved]
        + [
            pltpu.VMEM((4 * slots, 8 * width), low_type),
            pltpu.VMEM((width, 2 * width), wide),
            pltpu.VMEM((8, width), wide),
            pltpu.VMEM(weights.shape, low_type),
            pltpu.VMEM((4 * slots, model), low_type),
            pltpu.VMEM((2,) + block, low_type),
            pltpu.VMEM((3,) + block, low_type),
            pltpu.VMEM(block, low_type),
        ]
        + Reduce.scratch(slots, model)
        + [
            held(inner),
            pltpu.VMEM((2,) + inner.shape, low_type),
            pltpu.VMEM((8, model), wide),
            pltpu.VMEM((8, 8, model), wide),
            pltpu.VMEM((4, 8, model // 4), wide),
            pltpu.VMEM((4, 8, model // 4), wide),
            dma((5, 4)),
            dma((2, 3)),
            dma((2, 3)),
            dma((3, 3)),
            dma((3, 3)),
            dma((6,)),
            dma((6,)),
            dma((2, 2)),
            dma((2, 2)),
            dma((5,)),
            dma((12,)),
            dma((3, count)),
            dma((4, count)),
        ],
        compiler_params=pltpu.CompilerParams(
            collective_id=2, has_side_effects=True, vmem_limit_bytes=60 * 1024 * 1024
        ),
        cost_estimate=pl.CostEstimate(
            flops=weights.size * 4 * slots * 4, bytes_accessed=weights.size * 8, transcendentals=0
        ),
        name="back",
    )(
        x,
        res,
        starts,
        weights,
        *saved,
        ffn,
        inner,
        tokens,
        residual_grad,
        gains,
    )


def adam_kernel(
    sizes,
    mix_ref,
    ffn_ref,
    gain_ref,
    master_ref,
    first_ref,
    second_ref,
    piece_ref,
    new_master_ref,
    new_first_ref,
    new_second_ref,
    rows_ref,
    bias_ref,
    grad,
):
    model, width, ffn_width, piece_length, lines, margin = sizes
    member = lax.axis_index("dp")
    step = pl.program_id(0)
    lead = 128
    start_row = (member * piece_length) // lead
    offset = (member * piece_length) % lead
    tiles_in = 4 * width // lead
    tiles_ffn = 4 * ffn_width // lead
    tiles_model = model // lead

    @pl.when(step == 0)
    def _():
        def clear(number, carry):
            grad[pl.ds(pl.multiple_of(number * 256, 256), 256), :] = jnp.zeros((256, lead), wide)
            return carry

        lax.fori_loop(0, grad.shape[0] // 256, clear, 0)

        def place(row, count, body):
            low = member * piece_length

            @pl.when((row * lead < low + piece_length) & ((row + count) * lead > low))
            def _():
                body(row - start_row + margin)

        base = 0

        def in_unit(number, carry):
            kind = number // tiles_model
            at = number % tiles_model

            def body(to):
                for q in range(4):
                    tile = mix_ref[
                        q,
                        pl.ds(pl.multiple_of(kind * width, width), width),
                        pl.ds(pl.multiple_of(at * lead, lead), lead),
                    ].astype(wide)
                    grad[pl.ds(to + q, lead, stride=tiles_in), :] = tile.T

            place((kind * model + at * lead) * tiles_in, lead * tiles_in, body)
            return carry

        lax.fori_loop(0, 2 * tiles_model, in_unit, 0)
        base = 2 * model * tiles_in

        def gate_body(number, carry):
            kind = number // 4
            q = number % 4

            def body(to):
                grad[pl.ds(to, width), :] = mix_ref[
                    q, pl.ds(pl.multiple_of(kind * width, width), width), model:
                ].astype(wide)

            place(2 * model * tiles_in + number * width, width, body)
            return carry

        lax.fori_loop(0, 8, gate_body, 0)
        base = base + 8 * width
        out_base = base

        quarter = width // 4

        def out_unit(number, carry):
            q = number // 4
            part = number % 4

            def body(to):
                for at in range(tiles_model):
                    grad[pl.ds(to + at, quarter, stride=tiles_model), :] = mix_ref[
                        q,
                        pl.ds(pl.multiple_of(2 * width + part * quarter, quarter), quarter),
                        at * lead : (at + 1) * lead,
                    ].astype(wide)

            place(out_base + number * quarter * tiles_model, quarter * tiles_model, body)
            return carry

        lax.fori_loop(0, 16, out_unit, 0)
        base = base + 4 * width * tiles_model
        up_base = base

        def up_unit(number, carry):
            kind = number // tiles_model
            at = number % tiles_model
            columns = pl.ds(pl.multiple_of(at * lead, lead), lead)

            def body(to):
                for tile in range(tiles_ffn):
                    found = []
                    row = tile * lead
                    while row < (tile + 1) * lead:
                        q = row // ffn_width
                        last = min((q + 1) * ffn_width, (tile + 1) * lead)
                        found.append(
                            ffn_ref[
                                q,
                                kind,
                                row - q * ffn_width : last - q * ffn_width,
                                columns,
                            ].astype(wide)
                        )
                        row = last
                    block = found[0] if len(found) == 1 else jnp.concatenate(found, axis=0)
                    grad[pl.ds(to + tile, lead, stride=tiles_ffn), :] = block.T

            place(up_base + (kind * model + at * lead) * tiles_ffn, lead * tiles_ffn, body)
            return carry

        lax.fori_loop(0, 2 * tiles_model, up_unit, 0)
        base = base + 2 * model * tiles_ffn
        down_base = base
        sixth = ffn_width // 6

        def down_unit(number, carry):
            q = number // 6
            part = number % 6

            def body(to):
                for at in range(tiles_model):
                    grad[pl.ds(to + at, sixth, stride=tiles_model), :] = ffn_ref[
                        q,
                        2,
                        pl.ds(pl.multiple_of(part * sixth, 16), sixth),
                        at * lead : (at + 1) * lead,
                    ].astype(wide)

            place(down_base + number * sixth * tiles_model, sixth * tiles_model, body)
            return carry

        lax.fori_loop(0, 24, down_unit, 0)
        small_base = base + 4 * ffn_width * tiles_model
        smalls = [
            mix_ref[q, 2 * width : 2 * width + 16, model:].astype(wide)
            for q in range(4)
        ]

        def small_body(to):
            for q in range(4):
                grad[pl.ds(to + q, 8, stride=tiles_in), :] = smalls[q][:8]
            for number in range(6):
                kind, at = number // 3, number % 3
                grad[pl.ds(to + 8 * tiles_in + number, 1), :] = gain_ref[
                    kind : kind + 1, at * lead : (at + 1) * lead
                ]

        place(small_base, 8 * tiles_in + 6, small_body)
        bias_ref[...] = jnp.concatenate([small[5:7] for small in smalls], axis=1)

    row = margin + step * lines
    shift = (lead - offset) % lead
    here = pltpu.roll(grad[pl.ds(row, lines), :], shift, 1)
    after = pltpu.roll(grad[pl.ds(row + 1, lines), :], shift, 1)
    lane = lax.broadcasted_iota(jnp.int32, (lines, lead), 1)
    piece = jnp.where(lane < lead - offset, here, after).reshape(1, lines * lead)
    piece_ref[...] = piece
    new_first = beta_one * first_ref[...] + (1.0 - beta_one) * piece
    new_second = beta_two * second_ref[...] + (1.0 - beta_two) * piece * piece
    master = master_ref[...]
    new_master = master - learn_rate * (
        new_first / corr_one / (jnp.sqrt(new_second / corr_two) + adam_eps)
        + weight_decay * master
    )
    new_first_ref[...] = new_first
    new_second_ref[...] = new_second
    new_master_ref[...] = new_master
    rows_ref[0] = new_master.reshape(lines, lead).astype(low_type)


def adam(mix, ffn, gains, master, first, second, sizes, chunks):
    model, width, ffn_width = sizes
    piece_length = master.shape[1]
    lines = -(-piece_length // (chunks * 128 * 16)) * 16
    block = lines * 128
    margin = 1536
    rows = -(-(2 * margin + chunks * lines + 8) // 256) * 256
    packed = jax.ShapeDtypeStruct(master.shape, wide)
    chunk_spec = pl.BlockSpec((1, block), lambda s: (0, s))
    once = lambda shape: pl.BlockSpec(
        shape, lambda s: (0,) * len(shape), pipeline_mode=pl.Buffered(1)
    )
    return pl.pallas_call(
        functools.partial(
            adam_kernel, (model, width, ffn_width, piece_length, lines, margin)
        ),
        grid=(chunks,),
        in_specs=[once(mix.shape), once(ffn.shape), once(gains.shape)] + [chunk_spec] * 3,
        out_specs=[chunk_spec] * 4
        + [
            pl.BlockSpec((1, lines, 128), lambda s: (s, 0, 0)),
            pl.BlockSpec((2, 4 * width), lambda s: (0, 0)),
        ],
        out_shape=[packed] * 4
        + [
            jax.ShapeDtypeStruct((chunks, lines, 128), low_type),
            jax.ShapeDtypeStruct((2, 4 * width), wide),
        ],
        scratch_shapes=[pltpu.VMEM((rows, 128), wide)],
        compiler_params=pltpu.CompilerParams(vmem_limit_bytes=48 * 1024 * 1024),
        cost_estimate=pl.CostEstimate(
            flops=20 * piece_length,
            bytes_accessed=40 * piece_length,
            transcendentals=piece_length,
        ),
        name="adam",
    )(mix, ffn, gains, master, first, second)


def spread_kernel(
    own_ref,
    part_hbm,
    residual_ref,
    mask_ref,
    weights_ref,
    block_out,
    held,
    spread,
    part,
    from_x,
    from_y,
    passing,
    last,
    load_sem,
    send_sem,
    recv_sem,
    plane_send,
    plane_recv,
):
    chunks, lines, lead = own_ref.shape
    member = lax.axis_index("dp")
    z = lax.axis_index("shard")
    step = pl.program_id(0)
    reduce = Reduce(part, from_x, from_y, passing, last, plane_send, plane_recv, member, z)
    part_load = pltpu.make_async_copy(part_hbm, part, load_sem.at[chunks])

    def copy_to(origin, chunk, side, to):
        return remote(
            held.at[origin, chunk],
            held.at[origin, chunk],
            send_sem.at[side, origin, chunk],
            recv_sem.at[origin, chunk],
            member,
            to,
        )

    def own_load(chunk):
        return pltpu.make_async_copy(own_ref.at[chunk], held.at[z, chunk], load_sem.at[chunk])

    def pass_on(origin, chunk, right):
        copy_to(origin, chunk, 0, z).wait_recv()
        if right:

            @pl.when(z < 3)
            def _():
                copy_to(origin, chunk, 0, z + 1).start()
        else:

            @pl.when(z > 0)
            def _():
                copy_to(origin, chunk, 1, z - 1).start()

    @pl.when(step == 0)
    def _():
        for chunk in range(chunks):
            own_load(chunk).start()
        part_load.start()
        barrier = pltpu.get_barrier_semaphore()
        for to in (reduce.to_x, reduce.to_y):
            pl.semaphore_signal(
                barrier, inc=1, device_id=(to, z), device_id_type=pl.DeviceIdType.MESH
            )

        @pl.when(z > 0)
        def _():
            pl.semaphore_signal(
                barrier, inc=1, device_id=(member, z - 1), device_id_type=pl.DeviceIdType.MESH
            )

        @pl.when(z < 3)
        def _():
            pl.semaphore_signal(
                barrier, inc=1, device_id=(member, z + 1), device_id_type=pl.DeviceIdType.MESH
            )

        @pl.when((z == 0) | (z == 3))
        def _():
            pl.semaphore_wait(barrier, 3)

        @pl.when((z > 0) & (z < 3))
        def _():
            pl.semaphore_wait(barrier, 4)

        def send_own(chunk, carry):
            own_load(chunk).wait()

            @pl.when(z < 3)
            def _():
                copy_to(z, chunk, 0, z + 1).start()

            @pl.when(z > 0)
            def _():
                copy_to(z, chunk, 1, z - 1).start()

            return carry

        lax.fori_loop(0, chunks, send_own, 0)
        part_load.wait()
        reduce.begin()

        def near(chunk, carry):
            @pl.when(z > 0)
            def _():
                pass_on(z - 1, chunk, True)

            @pl.when(z < 3)
            def _():
                pass_on(z + 1, chunk, False)

            return carry

        lax.fori_loop(0, chunks, near, 0)
        reduce.relay()

    @pl.when(step == 1)
    def _():
        reduce.arrive()
        live = quarters(mask_ref, (2 * reduce.half, 128))[:, 0:1].astype(wide)
        half = reduce.half
        for number in range(2):
            at = slice(number * half, (number + 1) * half)
            block_out[at] = (live[at] * (residual_ref[at] + reduce.result(number))).astype(low_type)
        reduce.finish()

    @pl.when(z >= 2)
    def _():
        pass_on(z - 2, step, True)

    @pl.when(z <= 1)
    def _():
        pass_on(z + 2, step, False)

    @pl.when(z == 3)
    def _():
        copy_to(0, step, 0, z).wait_recv()

    @pl.when(z == 0)
    def _():
        copy_to(3, step, 0, z).wait_recv()

    for origin in range(4):
        spread[origin * lines : (origin + 1) * lines, :] = held[origin, step].astype(wide)

    def line(number, carry):
        weights_ref[:, pl.ds(pl.multiple_of(number * lead, lead), lead)] = spread[
            pl.ds(number, 4, stride=lines), :
        ].astype(low_type)
        return carry

    lax.fori_loop(0, lines, line, 0, unroll=8)

    @pl.when(step == chunks - 1)
    def _():
        for origin in range(4):

            def finish(chunk, carry):
                @pl.when((origin <= z) & (z < 3))
                def _():
                    copy_to(origin, chunk, 0, z).wait_send()

                @pl.when((origin >= z) & (z > 0))
                def _():
                    copy_to(origin, chunk, 1, z).wait_send()

                return carry

            lax.fori_loop(0, chunks, finish, 0)


def spread_weights(own, part, residual, mask, piece_length):
    chunks, lines, lead = own.shape
    slots, model = residual.shape
    once = lambda value: pl.BlockSpec(
        value.shape, lambda s: (0, 0), pipeline_mode=pl.Buffered(1)
    )
    return pl.pallas_call(
        spread_kernel,
        grid=(chunks,),
        in_specs=[pl.BlockSpec(memory_space=pl.ANY)] * 2 + [
            once(residual),
            pl.BlockSpec(memory_space=pltpu.SMEM),
        ],
        out_specs=[pl.BlockSpec((4, lines * lead), lambda s: (0, s)), once(residual)],
        out_shape=[
            jax.ShapeDtypeStruct((4, piece_length), low_type),
            jax.ShapeDtypeStruct(residual.shape, low_type),
        ],
        scratch_shapes=[
            pltpu.VMEM((4, chunks, lines, lead), low_type),
            pltpu.VMEM((4 * lines, lead), wide),
            pltpu.VMEM(part.shape, low_type),
        ]
        + Reduce.scratch(slots, model)
        + [
            pltpu.SemaphoreType.DMA((chunks + 1,)),
            pltpu.SemaphoreType.DMA((2, 4, chunks)),
            pltpu.SemaphoreType.DMA((4, chunks)),
            pltpu.SemaphoreType.DMA((6,)),
            pltpu.SemaphoreType.DMA((6,)),
        ],
        compiler_params=pltpu.CompilerParams(
            collective_id=1, has_side_effects=True, vmem_limit_bytes=32 * 1024 * 1024
        ),
        cost_estimate=pl.CostEstimate(
            flops=4 * piece_length, bytes_accessed=16 * piece_length, transcendentals=0
        ),
        name="spread",
    )(own, part, residual, mask)


def group_body(
    tokens,
    cotangent,
    seq_start,
    live_mask,
    input_proj,
    gate_blocks,
    output_proj,
    ffn_gate_up,
    ffn_down,
    conv_taps,
    gate_bias,
    decay_param,
    norm_gains,
    master_shard,
    first_moment,
    second_moment,
):
    slots, model = tokens.shape
    slice_rec = input_proj.shape[2]
    slice_ffn = ffn_down.shape[0]
    width = slice_rec // 4
    ffn_width = slice_ffn // 4
    piece_length = master_shard.shape[1]
    (
        mix_in,
        mix_weights,
        ffn_weights,
        saved_p,
        saved_state,
        saved_low,
        all_starts,
        residual,
        ffn_in,
        all_grad_out,
        gains,
    ) = front(
        tokens,
        cotangent,
        seq_start,
        live_mask,
        norm_gains,
        conv_taps,
        gate_bias,
        decay_param[None],
        input_proj,
        gate_blocks,
        output_proj,
        ffn_gate_up,
        ffn_down,
        (model, width, ffn_width),
    )
    ffn_in = ffn_in.reshape(4 * slots, model)
    all_grad_out = all_grad_out.reshape(4 * slots, model)
    sum_ffn, inner_down, res_low, grad_residual, gain_sums, ffn_part = middle(
        ffn_in, all_grad_out, ffn_weights, residual, gains
    )
    four_mix, four_ffn, tokens_grad, gain_total = back(
        mix_in,
        res_low.reshape(4 * slots, model),
        all_starts,
        mix_weights,
        (saved_p, saved_state, saved_low),
        sum_ffn,
        inner_down,
        tokens,
        grad_residual,
        gain_sums,
        piece_length,
        width,
    )
    piece, new_master, new_first, new_second, rows, bias_total = adam(
        four_mix,
        four_ffn,
        gain_total,
        master_shard,
        first_moment,
        second_moment,
        (model, width, ffn_width),
        8,
    )
    new_weights, block_out = spread_weights(
        rows,
        ffn_part,
        residual,
        live_mask,
        piece_length,
    )
    return (
        block_out,
        tokens_grad,
        piece,
        new_master,
        new_first,
        new_second,
        new_weights,
        bias_total,
    )


def rms_scale(values, gain):
    return values * lax.rsqrt(jnp.mean(values * values, axis=-1, keepdims=True) + norm_eps) * gain


def conv_mix(signal, taps, position):
    result = taps[-1] + taps[0] * signal
    for shift_by in range(1, taps.shape[0] - 1):
        moved = jnp.pad(signal, ((shift_by, 0), (0, 0)))[:-shift_by]
        result = result + taps[shift_by] * jnp.where((position >= shift_by)[:, None], moved, 0.0)
    return result


def combine_steps(earlier, later):
    decay_first, value_first = earlier
    decay_second, value_second = later
    return (decay_first * decay_second, decay_second * value_first + value_second)


def recurrence(logits, signal, branch, bias_term, decay_term, position):
    row_count = signal.shape[0]
    recur_gate = jax.nn.sigmoid(logits[0].reshape(row_count, -1) + bias_term[0])
    input_gate = jax.nn.sigmoid(logits[1].reshape(row_count, -1) + bias_term[1])
    log_decay = -gate_scale * recur_gate * jax.nn.softplus(-decay_term)
    decay_rate = jnp.where((position > 0)[:, None], jnp.exp(log_decay), 0.0)
    drive_term = jnp.sqrt(-jnp.expm1(2.0 * log_decay)) * input_gate * signal
    states = lax.associative_scan(combine_steps, (decay_rate, drive_term), axis=0)[1]
    return states * jax.nn.gelu(branch)


def gated_gelu(ffn_pre):
    return jax.nn.gelu(ffn_pre[0]) * ffn_pre[1]


def mixer_forward(
    mix_in, input_proj, gate_blocks, output_proj, conv_taps, gate_bias, decay_param, position
):
    projected = jnp.einsum("sd,kdr->ksr", mix_in, input_proj, preferred_element_type=jnp.float32)
    conv_out, conv_pull = jax.vjp(
        lambda signal, taps: conv_mix(signal, taps, position), projected[0], conv_taps
    )
    row_count = conv_out.shape[0]
    conv_low = conv_out.astype(jnp.bfloat16).reshape(
        row_count, gate_blocks.shape[1], gate_blocks.shape[2]
    )
    gate_logits = jnp.einsum(
        "shb,khbc->kshc", conv_low, gate_blocks, preferred_element_type=jnp.float32
    )
    mixed, mix_pull = jax.vjp(
        lambda logits, signal, branch, bias_term, decay_term: recurrence(
            logits, signal, branch, bias_term, decay_term, position
        ),
        gate_logits,
        conv_out,
        projected[1],
        gate_bias,
        decay_param,
    )
    mixed_low = mixed.astype(jnp.bfloat16)
    partial_out = jnp.dot(mixed_low, output_proj, preferred_element_type=jnp.float32)
    return (partial_out, (conv_pull, conv_low, mix_pull, mixed_low))


def mixer_backward(grad_out_low, mix_in, saved, input_proj, gate_blocks, output_proj):
    conv_pull, conv_low, mix_pull, mixed_low = saved
    grad_output_proj = jnp.einsum(
        "sr,sd->rd", mixed_low, grad_out_low, preferred_element_type=jnp.float32
    )
    grad_mixed = jnp.einsum(
        "sd,rd->sr", grad_out_low, output_proj, preferred_element_type=jnp.float32
    )
    grad_logits, grad_conv_direct, grad_branch, grad_bias, grad_decay = mix_pull(grad_mixed)
    logits_low = grad_logits.astype(jnp.bfloat16)
    grad_blocks = jnp.einsum(
        "shb,kshc->khbc", conv_low, logits_low, preferred_element_type=jnp.float32
    )
    grad_conv_gates = jnp.einsum(
        "kshc,khbc->shb", logits_low, gate_blocks, preferred_element_type=jnp.float32
    )
    grad_signal, grad_taps = conv_pull(
        grad_conv_direct + grad_conv_gates.reshape(grad_conv_direct.shape)
    )
    proj_low = jnp.stack([grad_signal, grad_branch]).astype(jnp.bfloat16)
    grad_input_proj = jnp.einsum(
        "sd,ksr->kdr", mix_in, proj_low, preferred_element_type=jnp.float32
    )
    grad_mix_in = jnp.einsum(
        "ksr,kdr->sd", proj_low, input_proj, preferred_element_type=jnp.float32
    )
    return (
        grad_mix_in,
        (grad_input_proj, grad_blocks, grad_output_proj, grad_taps, grad_bias, grad_decay),
    )


def ffn_forward(ffn_in_low, ffn_gate_up, ffn_down):
    ffn_pre = jnp.einsum("sd,kdf->ksf", ffn_in_low, ffn_gate_up, preferred_element_type=jnp.float32)
    ffn_act, ffn_pull = jax.vjp(gated_gelu, ffn_pre)
    ffn_low = ffn_act.astype(jnp.bfloat16)
    partial_ffn = jnp.dot(ffn_low, ffn_down, preferred_element_type=jnp.float32)
    return (partial_ffn, (ffn_pull, ffn_low))


def ffn_backward(grad_low, ffn_in_low, saved, ffn_gate_up, ffn_down):
    ffn_pull, ffn_low = saved
    grad_down = jnp.einsum("sf,sd->fd", ffn_low, grad_low, preferred_element_type=jnp.float32)
    grad_act = jnp.einsum("sd,fd->sf", grad_low, ffn_down, preferred_element_type=jnp.float32)
    grad_pre = ffn_pull(grad_act)[0]
    pre_low = grad_pre.astype(jnp.bfloat16)
    grad_gate_up = jnp.einsum(
        "sd,ksf->kdf", ffn_in_low, pre_low, preferred_element_type=jnp.float32
    )
    grad_ffn_in = jnp.einsum(
        "ksf,kdf->sd", pre_low, ffn_gate_up, preferred_element_type=jnp.float32
    )
    return (grad_ffn_in, grad_gate_up, grad_down)


def body(
    tokens,
    cotangent,
    seq_start,
    live_mask,
    input_proj,
    gate_blocks,
    output_proj,
    ffn_gate_up,
    ffn_down,
    conv_taps,
    gate_bias,
    decay_param,
    norm_gains,
    master_shard,
    first_moment,
    second_moment,
):
    slot_count = tokens.shape[0]
    position = jnp.arange(slot_count, dtype=jnp.int32) - seq_start
    mask_rows = live_mask.astype(jnp.float32)[:, None]
    stream = tokens.astype(jnp.float32)
    grad_stream = cotangent.astype(jnp.float32) * mask_rows
    shards = (
        input_proj,
        gate_blocks,
        output_proj,
        ffn_gate_up,
        ffn_down,
        conv_taps,
        gate_bias,
        decay_param,
        norm_gains,
    )
    (
        full_in,
        full_blocks,
        full_out,
        full_up,
        full_down,
        full_taps,
        full_bias,
        full_decay,
        full_gains,
    ) = (
        lax.all_gather(shards[0], "shard", axis=2, tiled=True),
        lax.all_gather(shards[1], "shard", axis=1, tiled=True),
        lax.all_gather(shards[2], "shard", axis=0, tiled=True),
        lax.all_gather(shards[3], "shard", axis=2, tiled=True),
        lax.all_gather(shards[4], "shard", axis=0, tiled=True),
        lax.all_gather(shards[5], "shard", axis=1, tiled=True),
        lax.all_gather(shards[6], "shard", axis=1, tiled=True),
        lax.all_gather(shards[7], "shard", axis=0, tiled=True),
        lax.all_gather(shards[8], "shard", axis=1, tiled=True),
    )
    gains = full_gains.astype(jnp.float32)
    normed, norm_pull = jax.vjp(rms_scale, stream, gains[0])
    mix_in = normed.astype(jnp.bfloat16)
    mix_out, mix_saved = mixer_forward(
        mix_in,
        full_in,
        full_blocks,
        full_out,
        full_taps.astype(jnp.float32),
        full_bias.astype(jnp.float32),
        full_decay.astype(jnp.float32),
        position,
    )
    residual = stream + mix_out
    normed_two, second_pull = jax.vjp(rms_scale, residual, gains[1])
    ffn_in_low = normed_two.astype(jnp.bfloat16)
    ffn_result, ffn_saved = ffn_forward(ffn_in_low, full_up, full_down)
    block_out = (mask_rows * (residual + ffn_result)).astype(jnp.bfloat16)
    grad_ffn_in, grad_up, grad_down = ffn_backward(
        grad_stream.astype(jnp.bfloat16), ffn_in_low, ffn_saved, full_up, full_down
    )
    grad_norm_two, grad_gain_two = second_pull(grad_ffn_in)
    grad_residual = grad_stream + grad_norm_two
    grad_mix_in, mix_grads = mixer_backward(
        grad_residual.astype(jnp.bfloat16), mix_in, mix_saved, full_in, full_blocks, full_out
    )
    grad_norm_one, grad_gain_one = norm_pull(grad_mix_in)
    tokens_grad = (grad_residual + grad_norm_one).astype(jnp.bfloat16)
    grads = (
        mix_grads[0],
        mix_grads[1],
        mix_grads[2],
        grad_up,
        grad_down,
        mix_grads[3],
        mix_grads[4],
        mix_grads[5],
        jnp.stack([grad_gain_one, grad_gain_two]),
    )
    summed = (
        lax.psum_scatter(
            grads[0].astype(jnp.bfloat16), "shard", scatter_dimension=2, tiled=True
        ).astype(jnp.float32),
        lax.psum_scatter(
            grads[1].astype(jnp.bfloat16), "shard", scatter_dimension=1, tiled=True
        ).astype(jnp.float32),
        lax.psum_scatter(
            grads[2].astype(jnp.bfloat16), "shard", scatter_dimension=0, tiled=True
        ).astype(jnp.float32),
        lax.psum_scatter(
            grads[3].astype(jnp.bfloat16), "shard", scatter_dimension=2, tiled=True
        ).astype(jnp.float32),
        lax.psum_scatter(
            grads[4].astype(jnp.bfloat16), "shard", scatter_dimension=0, tiled=True
        ).astype(jnp.float32),
        lax.psum_scatter(
            grads[5].astype(jnp.bfloat16), "shard", scatter_dimension=1, tiled=True
        ).astype(jnp.float32),
        lax.psum_scatter(
            grads[6].astype(jnp.bfloat16), "shard", scatter_dimension=1, tiled=True
        ).astype(jnp.float32),
        lax.psum_scatter(
            grads[7].astype(jnp.bfloat16), "shard", scatter_dimension=0, tiled=True
        ).astype(jnp.float32),
        lax.psum_scatter(
            grads[8].astype(jnp.bfloat16), "shard", scatter_dimension=1, tiled=True
        ).astype(jnp.float32),
    )
    flat = jnp.concatenate([member.reshape(1, -1) for member in summed], axis=1)
    piece = lax.psum_scatter(flat, "dp", scatter_dimension=1, tiled=True)
    bias_total = lax.psum(summed[6], "dp")
    new_first = beta_one * first_moment + (1.0 - beta_one) * piece
    new_second = beta_two * second_moment + (1.0 - beta_two) * piece * piece
    new_master = master_shard - learn_rate * (
        new_first / corr_one / (jnp.sqrt(new_second / corr_two) + adam_eps)
        + weight_decay * master_shard
    )
    new_weights = lax.all_gather(new_master.astype(jnp.bfloat16), "shard", axis=0, tiled=True)
    return (
        block_out,
        tokens_grad,
        piece,
        new_master,
        new_first,
        new_second,
        new_weights,
        bias_total,
    )


def solution(mesh):
    fits = mesh.shape["dp"] == 8 and mesh.shape["shard"] == 4
    placed = (
        P(("dp", "shard"), None),
        P(("dp", "shard"), None),
        P(("dp", "shard")),
        P(("dp", "shard")),
        P(None, None, "shard"),
        P(None, "shard", None, None),
        P("shard", None),
        P(None, None, "shard"),
        P("shard", None),
        P(None, "shard"),
        P(None, "shard"),
        P("shard"),
        P(None, "shard"),
        P("shard", "dp"),
        P("shard", "dp"),
        P("shard", "dp"),
    )
    return jax.shard_map(
        group_body if fits else body,
        mesh=mesh,
        in_specs=placed,
        out_specs=(
            P(("dp", "shard"), None),
            P(("dp", "shard"), None),
            P("shard", "dp"),
            P("shard", "dp"),
            P("shard", "dp"),
            P("shard", "dp"),
            P(None, "dp"),
            P(None, "shard"),
        ),
        check_vma=False,
    )
```

```python
import functools
import jax
import jax.numpy as jnp
from jax import lax
from jax.experimental import pallas as pl
from jax.experimental.pallas import tpu as pltpu
from jax.sharding import PartitionSpec as P

norm_eps = 1e-06
gate_scale = 8.0
beta_one = 0.9
beta_two = 0.95
learn_rate = 0.01
weight_decay = 0.1
adam_eps = 1e-08
corr_one = 1.0 - beta_one**10.0
corr_two = 1.0 - beta_two**10.0
low_type = jnp.bfloat16
wide = jnp.float32
gelu_scale = 0.7978845608028654
gelu_cube = 0.044715


def add_low(left, right):
    return (left.astype(wide) + right.astype(wide)).astype(low_type)


def dot_rows(left, right):
    return lax.dot_general(left, right, (((1,), (1,)), ((), ())), preferred_element_type=wide)


def dot_plain(left, right):
    return lax.dot_general(left, right, (((1,), (0,)), ((), ())), preferred_element_type=wide)


def dot_slots(left, right):
    return lax.dot_general(left, right, (((0,), (0,)), ((), ())), preferred_element_type=wide)


def gelu_parts(value):
    square = value * value
    bent = jnp.tanh(gelu_scale * value * (1.0 + gelu_cube * square))
    half = 0.5 * (1.0 + bent)
    slope = half + 0.5 * value * (1.0 - bent * bent) * gelu_scale * (
        1.0 + 3.0 * gelu_cube * square
    )
    return (value * half, slope)


def shift_down(value, step):
    if step % 8 == 0:
        return jnp.concatenate([value[-step:], value[:-step]], axis=0)
    return pltpu.roll(value, step, 0)


def shift_up(value, step):
    if step % 8 == 0:
        return jnp.concatenate([value[step:], value[:step]], axis=0)
    return pltpu.roll(value, value.shape[0] - step, 0)


def scan_slots(decay, value, shift):
    step = 1
    while step < value.shape[0]:
        value = value + decay * shift(value, step)
        if 2 * step < value.shape[0]:
            decay = decay * shift(decay, step)
        step *= 2
    return value


def one_minus_exp(value):
    series = jnp.ones_like(value)
    for number in range(11, 1, -1):
        series = 1.0 - value * (1.0 / number) * series
    return jnp.where(value < 0.8, value * series, 1.0 - jnp.exp(-value))


def soft_plus(value):
    return jnp.maximum(value, 0.0) + jnp.log1p(jnp.exp(-jnp.abs(value)))


def mixer_parts(first, position, small, gates):
    conv_out = small[4:5] + small[0:1] * first
    shifted = []
    for step in range(1, 4):
        moved = jnp.where(position >= step, shift_down(first, step), 0.0)
        shifted.append(moved)
        conv_out = conv_out + small[step : step + 1] * moved
    conv_low = conv_out.astype(low_type)
    logits = dot_plain(conv_low, gates)
    width = first.shape[1]
    recur_gate = jax.nn.sigmoid(logits[:, :width] + small[5:6])
    input_gate = jax.nn.sigmoid(logits[:, width:] + small[6:7])
    rate = gate_scale * soft_plus(-small[7:8])
    log_decay = -rate * recur_gate
    decay = jnp.where(position > 0, jnp.exp(log_decay), 0.0)
    gone = one_minus_exp(-2.0 * log_decay)
    root = jnp.sqrt(gone)
    return conv_out, shifted, conv_low, recur_gate, input_gate, rate, decay, gone, root


def weight_views(w_ref, width):
    model = w_ref.shape[2] - width
    proj = w_ref[0, 0 : 2 * width, 0:model]
    out = w_ref[0, 2 * width : 3 * width, 0:model]
    gates = jnp.concatenate(
        [w_ref[0, 0:width, model:], w_ref[0, width : 2 * width, model:]], axis=1
    )
    small = w_ref[0, 2 * width : 2 * width + 16, model:].astype(wide)
    return proj, out, gates, small


def slot_position(starts):
    slot = lax.broadcasted_iota(jnp.int32, (starts.shape[0], 1), 0)
    return slot - starts[:, 0:1].astype(wide).astype(jnp.int32)


def mixer_step(x, position, views, width):
    proj, out, gates, small = views
    projected = dot_rows(x, proj)
    conv_out, _, _, _, input_gate, _, decay, _, root = mixer_parts(
        projected[:, :width], position, small, gates
    )
    states = scan_slots(decay, root * input_gate * conv_out, shift_down)
    mixed_low = (states * gelu_parts(projected[:, width:])[0]).astype(low_type)
    return projected, states, mixed_low, dot_plain(mixed_low, out)


def mixer_back_step(position, views, projected, states, res_low, width):
    _, out, gates, small = views
    first = projected[:, :width]
    conv_out, shifted, conv_low, recur_gate, input_gate, rate, decay, gone, root = mixer_parts(
        first, position, small, gates
    )
    grad_mixed = dot_rows(res_low, out)
    active, slope = gelu_parts(projected[:, width:])
    grad_second = grad_mixed * states * slope
    adjoint = scan_slots(shift_up(decay, 1), grad_mixed * active, shift_up)
    grad_decay = adjoint * shift_down(states, 1)
    gated = adjoint * conv_out
    grad_root = gated * input_gate
    grad_input_gate = gated * root
    grad_conv = adjoint * root * input_gate
    grad_log = grad_decay * decay - grad_root * (1.0 - gone) / root
    grad_recur = -rate * grad_log
    grad_logit_a = grad_recur * recur_gate * (1.0 - recur_gate)
    grad_logit_b = grad_input_gate * input_gate * (1.0 - input_gate)
    grad_param = jnp.sum(grad_log * recur_gate, axis=0, keepdims=True) * (
        gate_scale * jax.nn.sigmoid(-small[7:8])
    )
    logits_low = jnp.concatenate([grad_logit_a, grad_logit_b], axis=1).astype(low_type)
    grad_conv = grad_conv + dot_rows(logits_low, gates)
    grad_gates = dot_slots(conv_low, logits_low)
    sums = [jnp.sum(grad_conv * first, axis=0, keepdims=True)]
    grad_first = small[0:1] * grad_conv
    for step in range(1, 4):
        sums.append(jnp.sum(grad_conv * shifted[step - 1], axis=0, keepdims=True))
        kept = jnp.where(position >= step, grad_conv, 0.0)
        grad_first = grad_first + small[step : step + 1] * shift_up(kept, step)
    sums.append(jnp.sum(grad_conv, axis=0, keepdims=True))
    sums.append(jnp.sum(grad_logit_a, axis=0, keepdims=True))
    sums.append(jnp.sum(grad_logit_b, axis=0, keepdims=True))
    sums.append(grad_param)
    proj_low = jnp.concatenate([grad_first, grad_second], axis=1).astype(low_type)
    return proj_low, grad_gates, jnp.concatenate(sums, axis=0)


def peer_x(chip):
    return chip + 1 - 2 * (chip % 2)


def peer_y(chip):
    return chip + 2 - 4 * (chip // 2)


def line_place(end, core):
    return end + core * (3 - 2 * end)


def remote(source, target, send, recv, member, z):
    return pltpu.make_async_remote_copy(
        src_ref=source,
        dst_ref=target,
        send_sem=send,
        recv_sem=recv,
        device_id=(member, z),
        device_id_type=pl.DeviceIdType.MESH,
    )


def enter(member, z):
    barrier = pltpu.get_barrier_semaphore()
    for other in range(8):

        @pl.when(member != other)
        def _():
            pl.semaphore_signal(
                barrier, inc=1, device_id=(other, z), device_id_type=pl.DeviceIdType.MESH
            )

    for other in range(4):

        @pl.when(z != other)
        def _():
            pl.semaphore_signal(
                barrier, inc=1, device_id=(member, other), device_id_type=pl.DeviceIdType.MESH
            )

    pl.semaphore_wait(barrier, 10)


def quarters(value_ref, shape):
    slots = shape[0]
    row = lax.broadcasted_iota(jnp.int32, shape, 0)
    result = jnp.full(shape, value_ref[3 * slots // 4], jnp.int32)
    for number in (2, 1, 0):
        result = jnp.where(
            row < (number + 1) * slots // 4, value_ref[number * slots // 4], result
        )
    return result


class Gather:
    def __init__(self, own, target, send, recv, member, z):
        self.own, self.target = own, target
        self.send, self.recv = send, recv
        chip, core = member // 2, member % 2
        self.to_x = peer_x(chip) * 2 + core
        self.to_y = peer_y(chip) * 2 + core
        self.z = z
        self.half = own.shape[0] // 2

    def copy(self, number):
        low, high = pl.ds(0, self.half), pl.ds(self.half, self.half)
        source, target, to = (
            (self.own, self.target.at[1], self.to_x),
            (self.own, self.target.at[2], self.to_y),
            (self.target.at[1, low], self.target.at[3, low], self.to_y),
            (self.target.at[2, high], self.target.at[3, high], self.to_x),
        )[number]
        return remote(source, target, self.send.at[number], self.recv.at[number], to, self.z)

    def begin(self):
        self.copy(0).start()
        self.copy(1).start()

    def relay(self):
        self.copy(0).wait_recv()
        self.copy(2).start()
        self.copy(1).wait_recv()
        self.copy(3).start()

    def arrive(self):
        self.copy(2).wait_recv()
        self.copy(3).wait_recv()

    def finish(self):
        for number in range(4):
            self.copy(number).wait_send()


class Reduce:
    def __init__(self, part, from_x, from_y, passing, last, send, recv, member, z):
        self.part, self.from_x, self.from_y = part, from_x, from_y
        self.passing, self.last = passing, last
        self.send, self.recv = send, recv
        chip, core = member // 2, member % 2
        self.to_x = peer_x(chip) * 2 + core
        self.to_y = peer_y(chip) * 2 + core
        self.z = z
        self.slots = part.shape[0] // 4
        self.half = self.slots // 2

    def copy(self, number):
        slots, half = self.slots, self.half
        source, target, to = (
            (self.part.at[pl.ds(slots, half)], self.from_x.at[0], self.to_x),
            (self.part.at[pl.ds(3 * slots, half)], self.from_x.at[1], self.to_x),
            (self.part.at[pl.ds(2 * slots + half, half)], self.from_y.at[0], self.to_y),
            (self.part.at[pl.ds(3 * slots + half, half)], self.from_y.at[1], self.to_y),
            (self.passing.at[0], self.last.at[0], self.to_y),
            (self.passing.at[1], self.last.at[1], self.to_x),
        )[number]
        return remote(source, target, self.send.at[number], self.recv.at[number], to, self.z)

    def begin(self):
        for block in (3, 1, 2):
            self.begin_block(block)

    def begin_block(self, block):
        for number in {1: (0,), 2: (2,), 3: (1, 3)}.get(block, ()):
            self.copy(number).start()

    def relay(self):
        slots, half = self.slots, self.half
        self.copy(1).wait_recv()
        self.passing[0] = (
            self.part[2 * slots : 2 * slots + half].astype(wide) + self.from_x[1].astype(wide)
        ).astype(low_type)
        self.copy(4).start()
        self.copy(3).wait_recv()
        self.passing[1] = (
            self.part[slots + half : 2 * slots].astype(wide) + self.from_y[1].astype(wide)
        ).astype(low_type)
        self.copy(5).start()

    def arrive(self):
        for number in (0, 2, 4, 5):
            self.copy(number).wait_recv()

    def result(self, number):
        direct = self.from_x if number == 0 else self.from_y
        return (
            self.part[number * self.half : (number + 1) * self.half].astype(wide)
            + direct[0].astype(wide)
            + self.last[number].astype(wide)
        )

    def finish(self):
        for number in range(6):
            self.copy(number).wait_send()

    @staticmethod
    def scratch(slots, model):
        return [pltpu.VMEM((2, slots // 2, model), low_type)] * 4


def norm_rows(value, gain):
    scale = lax.rsqrt(jnp.mean(value * value, axis=1, keepdims=True) + norm_eps)
    return value * scale * gain


def front_kernel(
    sizes,
    tokens_in,
    cot_in,
    start_ref,
    live_ref,
    gain_in,
    taps_ref,
    bias_ref,
    decay_ref,
    in_ref,
    gate_ref,
    out_ref,
    up_ref,
    down_ref,
    mix_in,
    weights,
    ffn_weights,
    saved_p,
    saved_state,
    saved_low,
    starts_out,
    residual_out,
    ffn_in,
    cot_out,
    gains_out,
    tokens_ref,
    cot_ref,
    gain_ref,
    tokens_all,
    raw_in,
    raw_up,
    raw_down,
    turned,
    gain_seen,
    acc,
    part,
    from_x,
    from_y,
    passing,
    last,
    load_sem,
    gain_send,
    gain_recv,
    m_send,
    m_recv,
    m_core_send,
    m_core_recv,
    f_send,
    f_recv,
    f_core_send,
    f_core_recv,
    g_send,
    g_recv,
    r_send,
    r_recv,
):
    model, width, ffn_width = sizes
    member = lax.axis_index("dp")
    z = lax.axis_index("shard")
    chip, core = member // 2, member % 2
    end = z + core * (3 - 2 * z)
    other = chip * 2 + 1 - core
    slots = cot_in.shape[0]
    half_ffn = ffn_width // 2
    owner = core == z // 2

    window = 128 * ((chip * ffn_width) // 128)
    skew = chip * ffn_width - window
    quarter = pl.ds(pl.multiple_of(chip * width, width), width)
    wide_window = pl.ds(pl.multiple_of(window, 128), raw_up.shape[2])

    def loads():
        found = [
            (out_ref.at[quarter], weights.at[end, pl.ds(2 * width, width), pl.ds(0, model)]),
        ]
        for kind in range(2):
            found.append((in_ref.at[kind, :, quarter], raw_in.at[kind]))
            found.append(
                (
                    gate_ref.at[kind, chip],
                    weights.at[end, pl.ds(kind * width, width), pl.ds(model, width)],
                )
            )
        found.append(
            (down_ref.at[pl.ds(pl.multiple_of(chip * ffn_width, 32), ffn_width)], raw_down)
        )
        for kind in range(2):
            found.append((up_ref.at[kind, :, wide_window], raw_up.at[kind]))
        return [
            pltpu.make_async_copy(source, target, load_sem.at[number])
            for number, (source, target) in enumerate(found)
        ]

    def turned_copy(kind):
        return pltpu.make_async_copy(
            raw_down
            if kind == 2
            else turned.at[kind, pl.ds(pl.multiple_of(skew, 32), ffn_width)],
            ffn_weights.at[kind, pl.ds(pl.multiple_of(2 * end * ffn_width, 32), ffn_width)],
            load_sem.at[9 + kind],
        )

    @pl.when(owner)
    def _():
        for copy in loads():
            copy.start()

    tokens_ref[:, :model] = tokens_in[...]
    tokens_ref[:, model:] = quarters(start_ref, (slots, width)).astype(wide).astype(low_type)
    live = quarters(live_ref, (slots, 128))[:, 0:1].astype(wide)
    cot_ref[...] = (cot_in[...].astype(wide) * live).astype(low_type)
    gain_ref[...] = jnp.concatenate(
        [gain_in[...].astype(wide), jnp.zeros((14, model // 4), wide)], axis=0
    ).astype(low_type)
    enter(member, z)

    gather_tokens = Gather(tokens_ref, tokens_all, g_send.at[0], g_recv.at[0], member, z)
    gather_cot = Gather(cot_ref, cot_out, g_send.at[1], g_recv.at[1], member, z)
    gather_ffn = Gather(ffn_in.at[0], ffn_in, g_send.at[2], g_recv.at[2], member, z)
    reduce = Reduce(part, from_x, from_y, passing, last, r_send, r_recv, member, z)
    own_cot = pltpu.make_async_copy(cot_ref, cot_out.at[0], load_sem.at[12])

    gather_tokens.begin()
    own_cot.start()

    def gain_copy(to, slot):
        return remote(
            gain_ref, gain_seen.at[slot], gain_send.at[to], gain_recv.at[slot], member, to
        )

    for to in range(4):

        @pl.when(to != z)
        def _():
            gain_copy(to, z).start()

    gain_seen[z] = gain_ref[...]

    def m_rows(number):
        return pl.ds(number * width, width)

    def m_copy(slot, number, way, to_end):
        place = weights.at[slot, m_rows(number)]
        return remote(
            place,
            place,
            m_send.at[way, slot, number],
            m_recv.at[slot, number],
            member,
            line_place(to_end, core),
        )

    def m_core(slot, number):
        return remote(
            weights.at[slot, m_rows(number)],
            weights.at[2 + slot, m_rows(number)],
            m_core_send.at[slot, number],
            m_core_recv.at[slot, number],
            other,
            z,
        )

    def f_place(slot, number):
        row = ((slot % 2) * 2 + slot // 2) * ffn_width + (number % 2) * half_ffn
        return ffn_weights.at[number // 2, pl.ds(row, half_ffn)]

    def f_copy(slot, number, way, to_end):
        place = f_place(slot, number)
        return remote(
            place,
            place,
            f_send.at[way, slot, number],
            f_recv.at[slot, number],
            member,
            line_place(to_end, core),
        )

    def f_core(slot, number):
        return remote(
            f_place(slot, number),
            f_place(2 + slot, number),
            f_core_send.at[slot, number],
            f_core_recv.at[slot, number],
            other,
            z,
        )

    def pass_on(copy, core_copy, slot, number):
        if slot == 0:

            @pl.when(end < 3)
            def _():
                copy(slot, number, 0, end + 1).start()
        else:

            @pl.when((end == 1) | (end == 2))
            def _():
                copy(slot, number, 0, end + 1).start()

        core_copy(slot, number).start()

    def pass_back(copy, numbers):
        @pl.when(end == 1)
        def _():
            for number in numbers:
                copy(1, number, 1, 0).start()

    def start_own(copy, core_copy, numbers):
        for slot in range(2):

            @pl.when(end == slot)
            def _():
                for number in numbers[slot]:
                    pass_on(copy, core_copy, slot, number)

    def turn_in(kind):
        @pl.when(owner)
        def _():
            for copy in loads()[1 + 2 * kind : 3 + 2 * kind]:
                copy.wait()

            def turn(at, carry):
                columns = pl.ds(pl.multiple_of(at * 256, 256), 256)
                weights[end, kind * width : (kind + 1) * width, columns] = raw_in[
                    kind, columns, :
                ].T
                return carry

            lax.fori_loop(0, model // 256, turn, 0)

        start_own(m_copy, m_core, ((kind,), (kind,)))
        pass_back(m_copy, (kind,))

    def turn_up(kind):
        @pl.when(owner)
        def _():
            loads()[6 + kind].wait()

            def turn(at, carry):
                columns = pl.ds(pl.multiple_of(at * 256, 256), 256)
                turned[kind, :, columns] = raw_up[kind, columns, :].T
                return carry

            lax.fori_loop(0, model // 256, turn, 0)
            turned_copy(kind).start()

    @pl.when(owner)
    def _():
        weights[end, 2 * width : 3 * width, model:] = jnp.concatenate(
            [
                taps_ref[:, quarter].astype(wide),
                bias_ref[:, quarter].astype(wide),
                decay_ref[:, quarter].astype(wide),
                jnp.zeros((width - 8, width), wide),
            ],
            axis=0,
        ).astype(low_type)
        loads()[0].wait()

    start_own(m_copy, m_core, ((2,), (2,)))
    pass_back(m_copy, (2,))
    turn_in(0)
    turn_in(1)

    @pl.when(owner)
    def _():
        loads()[5].wait()
        turned_copy(2).start()

    turn_up(0)
    turn_up(1)
    gather_tokens.relay()
    m_order = (2, 0, 1)

    @pl.when(end < 3)
    def _():
        for number in m_order:
            for slot in (1, 0):

                @pl.when(end != slot)
                def _():
                    m_copy(slot, number, 0, 0).wait_recv()
                    pass_on(m_copy, m_core, slot, number)

    @pl.when(owner)
    def _():
        for kind in range(3):
            turned_copy(kind).wait()

    f_order = ((4, 5, 0, 1, 2, 3), (4, 5, 0, 2))
    start_own(f_copy, f_core, f_order)

    def f_pass(slot, numbers):
        for number in numbers:
            f_copy(slot, number, 0, 0).wait_recv()
            pass_on(f_copy, f_core, slot, number)

    def f_step(step):
        @pl.when(end == 1)
        def _():
            f_pass(0, ((), (4, 5), (0, 1), (2, 3), (), ())[step])

        @pl.when(end == 2)
        def _():
            f_pass(1, ((4,), (5, 0), (2,), (), (), ())[step])
            f_pass(0, ((), (), (4,), (5, 0), (1, 2), (3,))[step])

        if step == 2:
            pass_back(f_copy, f_order[1])

    def far_step(items):
        @pl.when(end == 3)
        def _():
            for slot, number in items:
                f_copy(slot, number, 0, 0).wait_recv()
                f_core(slot, number).start()

    def near_step(step):
        @pl.when(end == 0)
        def _():
            f_pass(1, ((), (), (), (), (), f_order[1])[step])

    for to in range(4):

        @pl.when(to != z)
        def _():
            gain_copy(to, to).wait_recv()

    gains = jnp.concatenate([gain_seen[at].astype(wide) for at in range(4)], axis=1)
    gains_out[...] = gains[0:8]
    gather_tokens.arrive()

    def norm_block(block):
        if block == 0:
            source, starts = tokens_ref[:, :model], tokens_ref[:, model:]
        else:
            source, starts = tokens_all[block, :, :model], tokens_all[block, :, model:]
        at = slice(block * slots, (block + 1) * slots)
        mix_in[at, :] = norm_rows(source.astype(wide), gains_out[0:1]).astype(low_type)
        starts_out[at, :] = starts

    for block in range(4):
        norm_block(block)
    gather_cot.begin()
    f_step(0)

    late = end >= 2
    for turn in range(4):
        head = (turn + 2 * late) % 4
        if turn == 2:

            @pl.when(end == 3)
            def _():
                for number in m_order:
                    for slot in (1, 0):
                        m_copy(slot, number, 0, 0).wait_recv()
                        m_core(slot, number).start()

        @pl.when(head >= 2)
        def _():
            for number in m_order:
                m_core(head - 2, number).wait_recv()

        views = weight_views(weights.at[pl.ds(head, 1)], width)

        def step_block(block, carry):
            rows = pl.ds(pl.multiple_of(block * slots, slots), slots)
            position = slot_position(starts_out[rows, :])
            projected, states, mixed_low, product = mixer_step(
                mix_in[rows, :], position, views, width
            )
            saved_p[head, rows, :] = projected
            saved_state[head, rows, :] = states
            saved_low[head, rows, :] = mixed_low
            if turn == 0:
                acc[rows, :] = product
            elif turn < 3:
                acc[rows, :] += product
            else:
                part[rows, :] = (acc[rows, :] + product).astype(low_type)
            return carry

        lax.fori_loop(0, 4, step_block, 0)
        if turn == 3:
            reduce.begin()
        f_step(turn + 1)
        near_step(turn + 1)
        if turn == 0:
            gather_cot.relay()

    far_step(((1, 4), (1, 5)))
    reduce.relay()
    f_step(5)
    near_step(5)
    far_step(((1, 0), (1, 2)))
    reduce.arrive()
    half = slots // 2
    for number in range(2):
        at = slice(number * half, (number + 1) * half)
        residual = tokens_ref[at, :model].astype(wide) + reduce.result(number)
        residual_out[at, :] = residual
        ffn_in[0, at, :] = norm_rows(residual, gains_out[1:2]).astype(low_type)
    gather_ffn.begin()
    far_step(((0, 4), (0, 5), (0, 0)))
    gather_ffn.relay()

    far_step(((0, 1), (0, 2), (0, 3)))

    gather_ffn.arrive()
    gather_cot.arrive()
    own_cot.wait()
    for slot in range(2):
        for number in f_order[slot]:
            f_core(slot, number).wait_recv()

    for gather in (gather_tokens, gather_cot, gather_ffn, reduce):
        gather.finish()
    for to in range(4):

        @pl.when(to != z)
        def _():
            gain_copy(to, z).wait_send()

    for copy, core_copy, numbers in (
        (m_copy, m_core, (m_order, m_order)),
        (f_copy, f_core, f_order),
    ):
        for number in numbers[0]:
            core_copy(0, number).wait_send()

            @pl.when(end < 3)
            def _():
                copy(0, number, 0, 0).wait_send()

        for number in numbers[1]:
            core_copy(1, number).wait_send()

            @pl.when((end == 1) | (end == 2))
            def _():
                copy(1, number, 0, 0).wait_send()

            @pl.when(end == 1)
            def _():
                copy(1, number, 1, 0).wait_send()


def front(
    tokens, cot, starts, live, gains, taps, bias, decay, in_proj, gates, out_proj, gate_up, down, sizes
):
    model, width, ffn_width = sizes
    slots = cot.shape[0]
    rows = 4 * slots
    dma = pltpu.SemaphoreType.DMA
    vmem = pl.BlockSpec(memory_space=pltpu.VMEM)
    anywhere = pl.BlockSpec(memory_space=pl.ANY)
    scalars = pl.BlockSpec(memory_space=pltpu.SMEM)
    window = -(-ffn_width // 128) * 128
    return pl.pallas_call(
        functools.partial(front_kernel, sizes),
        in_specs=[vmem] * 2 + [scalars] * 2 + [vmem] * 4 + [anywhere] * 5,
        out_specs=[vmem, vmem, anywhere, vmem, vmem, vmem, vmem, vmem, vmem, anywhere, vmem],
        out_shape=[
            jax.ShapeDtypeStruct((rows, model), low_type),
            jax.ShapeDtypeStruct((4, 3 * width, model + width), low_type),
            jax.ShapeDtypeStruct((3, 4 * ffn_width, model), low_type),
            jax.ShapeDtypeStruct((4, rows, 2 * width), wide),
            jax.ShapeDtypeStruct((4, rows, width), wide),
            jax.ShapeDtypeStruct((4, rows, width), low_type),
            jax.ShapeDtypeStruct((rows, width), low_type),
            jax.ShapeDtypeStruct((slots, model), wide),
            jax.ShapeDtypeStruct((4, slots, model), low_type),
            jax.ShapeDtypeStruct((4, slots, model), low_type),
            jax.ShapeDtypeStruct((8, model), wide),
        ],
        scratch_shapes=[
            pltpu.VMEM((slots, model + width), low_type),
            pltpu.VMEM((slots, model), low_type),
            pltpu.VMEM((16, model // 4), low_type),
            pltpu.VMEM((4, slots, model + width), low_type),
            pltpu.VMEM((2, model, width), low_type),
            pltpu.VMEM((2, model, window), low_type),
            pltpu.VMEM((ffn_width, model), low_type),
            pltpu.VMEM((2, window, model), low_type),
            pltpu.VMEM((4, 16, model // 4), low_type),
            pltpu.VMEM((rows, model), wide),
            pltpu.VMEM((rows, model), low_type),
        ]
        + Reduce.scratch(slots, model)
        + [
            dma((13,)),
            dma((4,)),
            dma((4,)),
            dma((2, 2, 3)),
            dma((2, 3)),
            dma((2, 3)),
            dma((2, 3)),
            dma((2, 2, 6)),
            dma((2, 6)),
            dma((2, 6)),
            dma((2, 6)),
            dma((3, 4)),
            dma((3, 4)),
            dma((6,)),
            dma((6,)),
        ],
        compiler_params=pltpu.CompilerParams(
            collective_id=3, has_side_effects=True, vmem_limit_bytes=60 * 1024 * 1024
        ),
        cost_estimate=pl.CostEstimate(
            flops=2 * rows * model * 4 * width * 3,
            bytes_accessed=6 * ffn_width * 4 * model,
            transcendentals=rows * 4 * width * 6,
        ),
        name="front",
    )(tokens, cot, starts, live, gains, taps, bias, decay, in_proj, gates, out_proj, gate_up, down)


def middle_kernel(
    sizes,
    x_hbm,
    go_hbm,
    weights_ref,
    residual_ref,
    gain_ref,
    total,
    inner_down,
    res_low,
    res_out,
    gain_out,
    part_out,
    x_ref,
    go_ref,
    held,
    lows,
    paired,
    arrived,
    part_in,
    in_x,
    in_y,
    in_pass,
    in_last,
    load_sem,
    late_send,
    late_recv,
    late_core_send,
    late_core_recv,
    core_send,
    core_recv,
    line_send,
    line_recv,
    i_send,
    i_recv,
    g_send,
    g_recv,
):
    model, ffn_width = sizes
    member = lax.axis_index("dp")
    z = lax.axis_index("shard")
    chip, core = member // 2, member % 2
    end = z + core * (3 - 2 * z)
    other = chip * 2 + 1 - core
    slots = residual_ref.shape[0]
    half = slots // 2
    hidden = 4 * ffn_width
    half_ffn = ffn_width // 2

    split = -(-2 * ffn_width // 128) * 128

    late_low = 2 * ffn_width + half_ffn
    peer_low = 3 * ffn_width + half_ffn

    def weight_load(kinds, low, high, number):
        at = pl.ds(low, high - low)
        return pltpu.make_async_copy(
            weights_ref.at[kinds, at], held.at[kinds, at], load_sem.at[number]
        )

    loads = [
        weight_load(pl.ds(0, 3), 0, split, 0),
        pltpu.make_async_copy(x_hbm, x_ref, load_sem.at[1]),
        pltpu.make_async_copy(go_hbm, go_ref, load_sem.at[2]),
        weight_load(pl.ds(0, 2), split, late_low, 3),
        weight_load(pl.ds(0, 2), 3 * ffn_width, peer_low, 4),
        weight_load(pl.ds(2, 1), split, hidden, 5),
    ]
    own_late = weight_load(pl.ds(0, 2), late_low, 3 * ffn_width, 7)

    def late_copy(kind, way, to_end):
        place = held.at[kind, pl.ds(late_low, half_ffn)]
        return remote(
            place,
            place,
            late_send.at[way, kind],
            late_recv.at[kind],
            member,
            line_place(to_end, core),
        )

    def late_core(kind):
        return remote(
            held.at[kind, pl.ds(late_low, half_ffn)],
            held.at[kind, pl.ds(peer_low, half_ffn)],
            late_core_send.at[kind],
            late_core_recv.at[kind],
            other,
            z,
        )

    @pl.when(end == 1)
    def _():
        own_late.start()

    for load in loads:
        load.start()
    enter(member, z)

    @pl.when(end == 1)
    def _():
        own_late.wait()
        for kind in range(2):
            late_copy(kind, 0, 2).start()
            late_copy(kind, 1, 0).start()
            late_core(kind).start()

    for load in loads[:3]:
        load.wait()

    def late_step(block):
        for kind in range(2):

            @pl.when((end == 2) & (block == kind + 1))
            def _():
                late_copy(kind, 0, 0).wait_recv()
                late_copy(kind, 0, 3).start()
                late_core(kind).start()

    def late_end():
        for kind in range(2):

            @pl.when((end == 0) | (end == 3))
            def _():
                late_copy(kind, 0, 0).wait_recv()
                late_core(kind).start()

        for kind in range(2):
            late_core(kind).wait_recv()

    def late_sent():
        for kind in range(2):
            late_core(kind).wait_send()

            @pl.when((end == 1) | (end == 2))
            def _():
                late_copy(kind, 0, 0).wait_send()

            @pl.when(end == 1)
            def _():
                late_copy(kind, 1, 0).wait_send()

    def block_step(low, high, block, carry):
        rows = pl.ds(pl.multiple_of(block * slots, slots), slots)
        x = x_ref[rows, :]
        grad_out = go_ref[rows, :]
        pre_gate = dot_rows(x, held[0, low:high])
        pre_up = dot_rows(x, held[1, low:high])
        active, slope = gelu_parts(pre_gate)
        ffn_low = (active * pre_up).astype(low_type)
        grad_act = dot_rows(grad_out, held[2, low:high])
        gate_low = (grad_act * pre_up * slope).astype(low_type)
        up_low = (grad_act * active).astype(low_type)
        sum_out = dot_plain(ffn_low, held[2, low:high])
        sum_in = dot_plain(gate_low, held[0, low:high]) + dot_plain(up_low, held[1, low:high])
        lows[0, rows, low:high] = gate_low
        lows[1, rows, low:high] = up_low
        lows[2, rows, low:high] = ffn_low
        if low == 0:
            late_step(block)
        else:
            sum_in = sum_in + part_in[rows, :].astype(wide)
            sum_out = sum_out + part_out[rows, :].astype(wide)
        part_in[rows, :] = sum_in.astype(low_type)
        part_out[rows, :] = sum_out.astype(low_type)
        return carry

    reduce_in = Reduce(part_in, in_x, in_y, in_pass, in_last, i_send, i_recv, member, z)
    gather = Gather(res_low.at[0], res_low, g_send, g_recv, member, z)
    middle = model // 2

    def weight_grads(kind, low, high):
        factor = go_ref if kind == 2 else x_ref
        for at in range(2):
            columns = slice(at * middle, (at + 1) * middle)
            held[kind, low:high, columns] = dot_slots(
                lows[kind, :, low:high], factor[:, columns]
            ).astype(low_type)

    def core_copy(slot, kind):
        return remote(
            held.at[kind, pl.ds((2 * slot + 1) * ffn_width, ffn_width)],
            paired.at[slot, kind],
            core_send.at[slot, kind],
            core_recv.at[slot, kind],
            other,
            z,
        )

    def chunk(number):
        return number // 2, pl.ds((number % 2) * half_ffn, half_ffn)

    def line_copy(kind, number, to_end):
        at, rows = chunk(number)
        return remote(
            paired.at[min(kind, 1), at, rows],
            arrived.at[kind, at, rows],
            line_send.at[kind, number],
            line_recv.at[kind, number],
            member,
            line_place(to_end, core),
        )

    def pair_up(slot, kind):
        core_copy(slot, kind).wait_recv()
        for number in (2 * kind, 2 * kind + 1):
            at, rows = chunk(number)
            own = held[at, pl.ds(2 * slot * ffn_width + (number % 2) * half_ffn, half_ffn)]
            paired[slot, at, rows] = add_low(own, paired[slot, at, rows])

            if slot == 0 or number < 4:

                @pl.when(end == 3)
                def _():
                    line_copy(slot, number, 2).start()

            if slot == 1 and number < 4:

                @pl.when(end == 0)
                def _():
                    line_copy(2, number, 1).start()

    def part_grads(slot, low, high):
        for kind in range(3):
            weight_grads(kind, low, high)
            core_copy(slot, kind).start()
            if kind > 0:
                pair_up(slot, kind - 1)
        pair_up(slot, 2)

    def summed(slot, kinds, number):
        at, rows = chunk(number)
        result = paired[slot, at, rows].astype(wide)
        for kind in kinds:
            result = result + arrived[kind, at, rows].astype(wide)
        return result.astype(low_type)

    def outer_step(number):
        at, rows = chunk(number)

        @pl.when((end == 2) | (end == 1))
        def _():
            line_copy(0, number, 0).wait_recv()
            paired[0, at, rows] = summed(0, (0,), number)
            line_copy(0, number, end - 1).start()

    def inner_step(number):
        at, rows = chunk(number)

        @pl.when(end == 2)
        def _():
            line_copy(1, number, 0).wait_recv()
            paired[1, at, rows] = summed(1, (1,), number)
            line_copy(1, number, 1).start()

    def out_copy(slot, number):
        at, rows = chunk(number)
        return pltpu.make_async_copy(
            paired.at[slot, at, rows], total.at[at, rows], load_sem.at[number]
        )

    def last_step(number):
        at, rows = chunk(number)

        if number < 4:

            @pl.when(end == 1)
            def _():
                line_copy(1, number, 0).wait_recv()
                line_copy(2, number, 0).wait_recv()
                paired[1, at, rows] = summed(1, (1, 2), number)
                out_copy(1, number).start()

        @pl.when(end == 0)
        def _():
            line_copy(0, number, 0).wait_recv()
            paired[0, at, rows] = summed(0, (0,), number)
            out_copy(0, number).start()

    lax.fori_loop(0, 4, functools.partial(block_step, 0, split), 0)
    part_grads(0, 0, split)
    for load in loads[3:]:
        load.wait()
    late_end()
    lax.fori_loop(0, 4, functools.partial(block_step, split, hidden), 0)
    reduce_in.begin()
    late_sent()
    part_grads(1, split, hidden)
    inner_copy = pltpu.make_async_copy(paired.at[1, 2], inner_down, load_sem.at[6])
    inner_copy.start()
    for number in range(3):
        outer_step(number)
    reduce_in.relay()
    for number in range(3, 6):
        outer_step(number)

    reduce_in.arrive()
    gain = gain_ref[1:2]
    gain_sum = jnp.zeros((1, model), wide)
    for number in range(2):
        at = slice(number * half, (number + 1) * half)
        grad = reduce_in.result(number)
        value = residual_ref[at]
        scale = lax.rsqrt(jnp.mean(value * value, axis=1, keepdims=True) + norm_eps)
        scaled = grad * gain
        gain_sum = gain_sum + jnp.sum(grad * value * scale, axis=0, keepdims=True)
        inner = jnp.mean(scaled * value, axis=1, keepdims=True)
        back = scale * scaled - value * (scale * scale * scale * inner)
        result = go_ref[at].astype(wide) + back
        res_out[at] = result
        res_low[0, at] = result.astype(low_type)
    gain_out[...] = jnp.concatenate([gain_ref[0:1], gain_sum, jnp.zeros((6, model), wide)], axis=0)
    gather.begin()
    inner_step(0)
    gather.relay()
    inner_step(1)
    inner_step(2)
    inner_step(3)
    gather.arrive()
    for number in range(6):
        last_step(number)
    inner_copy.wait()

    for sent in (reduce_in, gather):
        sent.finish()
    for slot in range(2):
        for kind in range(3):
            core_copy(slot, kind).wait_send()
    for number in range(6):

        @pl.when(end > 0)
        def _():
            line_copy(0, number, 0).wait_send()

        @pl.when(end == 0)
        def _():
            out_copy(0, number).wait()

    for number in range(4):

        @pl.when(end > 1)
        def _():
            line_copy(1, number, 0).wait_send()

        @pl.when(end == 1)
        def _():
            out_copy(1, number).wait()

        @pl.when(end == 0)
        def _():
            line_copy(2, number, 1).wait_send()


def middle(x, grad_out, weights, residual, gains):
    rows, model = x.shape
    hidden = weights.shape[1]
    ffn_width = hidden // 4
    slots = rows // 4
    dma = pltpu.SemaphoreType.DMA
    vmem = pl.BlockSpec(memory_space=pltpu.VMEM)
    anywhere = pl.BlockSpec(memory_space=pl.ANY)
    quarter = (3, ffn_width, model)
    return pl.pallas_call(
        functools.partial(middle_kernel, (model, ffn_width)),
        in_specs=[anywhere] * 3 + [vmem] * 2,
        out_specs=[anywhere] * 2 + [vmem] * 4,
        out_shape=[
            jax.ShapeDtypeStruct(quarter, low_type),
            jax.ShapeDtypeStruct(quarter[1:], low_type),
            jax.ShapeDtypeStruct((4, slots, model), low_type),
            jax.ShapeDtypeStruct((slots, model), wide),
            jax.ShapeDtypeStruct((8, model), wide),
            jax.ShapeDtypeStruct((rows, model), low_type),
        ],
        scratch_shapes=[
            pltpu.VMEM(x.shape, low_type),
            pltpu.VMEM(x.shape, low_type),
            pltpu.VMEM(weights.shape, low_type),
            pltpu.VMEM((3, rows, hidden), low_type),
            pltpu.VMEM((2,) + quarter, low_type),
            pltpu.VMEM((3,) + quarter, low_type),
            pltpu.VMEM((rows, model), low_type),
        ]
        + Reduce.scratch(slots, model)
        + [
            dma((8,)),
            dma((2, 2)),
            dma((2,)),
            dma((2,)),
            dma((2,)),
            dma((2, 3)),
            dma((2, 3)),
            dma((3, 6)),
            dma((3, 6)),
            dma((6,)),
            dma((6,)),
            dma((4,)),
            dma((4,)),
        ],
        compiler_params=pltpu.CompilerParams(
            collective_id=4, has_side_effects=True, vmem_limit_bytes=63 * 1024 * 1024
        ),
        cost_estimate=pl.CostEstimate(
            flops=2 * rows * model * hidden * 9,
            bytes_accessed=weights.size * 4 + rows * model * 16,
            transcendentals=rows * hidden,
        ),
        name="middle",
    )(x, grad_out, weights, residual, gains)


class Scatter:
    def __init__(self, sizes, member, z, send_sem, recv_sem):
        self.model, self.width, self.ffn_width, self.piece_length = sizes
        self.member, self.z = member, z
        self.chip, self.core = member // 2, member % 2
        self.owner = self.core == z // 2
        self.send_sem, self.recv_sem = send_sem, recv_sem
        self.across = self.model // 128
        rec, ffn, model = 4 * self.width, 4 * self.ffn_width, self.model
        self.gate_base = 2 * model * rec
        self.out_base = self.gate_base + 8 * self.width * self.width
        self.up_base = self.out_base + rec * model
        self.down_base = self.up_base + 2 * model * ffn
        self.rec, self.ffn = rec, ffn
        self.first_in = 0
        self.first_gate = 2 * self.across
        self.first_out = self.first_gate + 2
        self.first_small = self.first_out + 4
        self.first_up = self.first_small + 1
        self.first_down = self.first_up + 2 * self.across
        self.count = self.first_down + 6

    def in_unit(self, number, q):
        kind, at = number // self.across, number % self.across
        low = (kind * self.model + at * 128) * self.rec
        where = (
            pl.ds(pl.multiple_of(kind * self.width, self.width), self.width),
            pl.ds(pl.multiple_of(at * 128, 128), 128),
        )
        return self.first_in + number, where, low, low + 128 * self.rec

    def gate_unit(self, kind, q):
        low = self.gate_base + (kind * 4 + q) * self.width * self.width
        where = (
            pl.ds(pl.multiple_of(kind * self.width, self.width), self.width),
            pl.ds(self.model, self.width),
        )
        return self.first_gate + kind, where, low, low + self.width * self.width

    def out_unit(self, number, q):
        rows = self.width // 4
        low = self.out_base + (q * self.width + number * rows) * self.model
        where = (
            pl.ds(pl.multiple_of(2 * self.width + number * rows, rows), rows),
            pl.ds(0, self.model),
        )
        return self.first_out + number, where, low, low + rows * self.model

    def up_unit(self, number, q):
        kind, at = number // self.across, number % self.across
        low = self.up_base + (kind * self.model + at * 128) * self.ffn
        where = (kind, pl.ds(0, self.ffn_width), pl.ds(pl.multiple_of(at * 128, 128), 128))
        return self.first_up + number, where, low, low + 128 * self.ffn

    def down_unit(self, number, q):
        rows = self.ffn_width // 6
        low = self.down_base + (q * self.ffn_width + number * rows) * self.model
        where = (2, pl.ds(pl.multiple_of(number * rows, 16), rows), pl.ds(0, self.model))
        return self.first_down + number, where, low, low + rows * self.model

    def small_where(self):
        return (pl.ds(2 * self.width, 16), pl.ds(self.model, self.width))

    def copies(self, unit, source, target, q, act, flat=False):
        number, where, low, high = unit
        here = where[1:] if flat else where
        first = low // self.piece_length
        last = (high - 1) // self.piece_length
        for which, to in ((0, first), (1, last)):
            wanted = True if which == 0 else last != first

            @pl.when((to != self.member) & wanted)
            def _():
                act(
                    remote(
                        source.at[here],
                        target.at[(q,) + where],
                        self.send_sem.at[which, number],
                        self.recv_sem.at[q, number],
                        to,
                        self.z,
                    ),
                    True,
                )

            @pl.when((to == self.member) & wanted)
            def _():
                act(
                    pltpu.make_async_copy(
                        source.at[here], target.at[(q,) + where], self.recv_sem.at[q, number]
                    ),
                    False,
                )

    def each(self, unit_of, low, high, source, target, act, flat=False):
        def body(number, carry):
            self.copies(unit_of(number, self.chip), source, target, self.chip, act, flat)
            return carry

        lax.fori_loop(low, high, body, 0)

    def smalls(self, source, target, act):
        where = self.small_where()
        for to in range(8):

            @pl.when(self.member != to)
            def _():
                act(
                    remote(
                        source.at[where],
                        target.at[(self.chip,) + where],
                        self.send_sem.at[2, to],
                        self.recv_sem.at[self.chip, self.first_small],
                        to,
                        self.z,
                    ),
                    True,
                )

        act(
            pltpu.make_async_copy(
                source.at[where],
                target.at[(self.chip,) + where],
                self.recv_sem.at[self.chip, self.first_small],
            ),
            False,
        )

    def arrivals(self, unit_of, count, source, target):
        low = self.member * self.piece_length

        def body(number, carry):
            for q in range(4):
                index, where, first, last = unit_of(number, q)
                mine = (first < low + self.piece_length) & (last > low)
                here = (self.chip == q) & self.owner

                @pl.when(mine & here)
                def _():
                    pltpu.make_async_copy(
                        source.at[where], target.at[(q,) + where], self.recv_sem.at[q, index]
                    ).wait()

                @pl.when(mine & jnp.logical_not(here))
                def _():
                    remote(
                        source.at[where],
                        target.at[(q,) + where],
                        self.send_sem.at[0, index],
                        self.recv_sem.at[q, index],
                        self.member,
                        self.z,
                    ).wait_recv()

            return carry

        lax.fori_loop(0, count, body, 0)

    def small_arrivals(self, source, target):
        where = self.small_where()
        for q in range(4):
            here = (self.chip == q) & self.owner

            @pl.when(here)
            def _():
                pltpu.make_async_copy(
                    source.at[where],
                    target.at[(q,) + where],
                    self.recv_sem.at[q, self.first_small],
                ).wait()

            @pl.when(jnp.logical_not(here))
            def _():
                remote(
                    source.at[where],
                    target.at[(q,) + where],
                    self.send_sem.at[2, 0],
                    self.recv_sem.at[q, self.first_small],
                    self.member,
                    self.z,
                ).wait_recv()


def begin(copy, is_remote):
    copy.start()


def finish_send(copy, is_remote):
    if is_remote:
        copy.wait_send()


def back_kernel(
    sizes,
    x_hbm,
    res_hbm,
    starts_ref,
    w_hbm,
    p_hbm,
    state_hbm,
    low_hbm,
    ffn_ref,
    inner_hbm,
    tokens_ref,
    res_ref,
    gain_ref,
    mix_out,
    ffn_out,
    tokens_out,
    gain_out,
    x_ref,
    low_res,
    w_ref,
    p_ref,
    state_ref,
    low_ref,
    proj_grads,
    gate_acc,
    small_acc,
    grads,
    part_ref,
    paired,
    arrived,
    total,
    from_x,
    from_y,
    passing,
    last,
    inner,
    inner_seen,
    gain_part,
    gain_plane,
    gain_line,
    gain_seen,
    load_sem,
    core_send,
    core_recv,
    line_send,
    line_recv,
    plane_send,
    plane_recv,
    inner_send,
    inner_recv,
    gain_send,
    gain_recv,
    unit_send,
    unit_recv,
):
    model, width, ffn_width, piece_length = sizes
    member = lax.axis_index("dp")
    z = lax.axis_index("shard")
    chip, core = member // 2, member % 2
    end = z + core * (3 - 2 * z)
    slots = tokens_ref.shape[0]
    half = slots // 2
    other = chip * 2 + 1 - core
    scatter = Scatter(sizes, member, z, unit_send, unit_recv)

    order = (2, 0, 3, 1)
    common = [
        pltpu.make_async_copy(x_hbm, x_ref, load_sem.at[4, 0]),
        pltpu.make_async_copy(res_hbm, low_res, load_sem.at[4, 1]),
    ]
    early = [pltpu.make_async_copy(inner_hbm, inner, load_sem.at[4, 2])]

    def head_loads(head):
        return [
            pltpu.make_async_copy(source.at[head], target.at[head], load_sem.at[head, number])
            for number, (source, target) in enumerate(
                ((w_hbm, w_ref), (p_hbm, p_ref), (state_hbm, state_ref), (low_hbm, low_ref))
            )
        ]

    for copy in early + head_loads(order[0]) + common:
        copy.start()
    for head in order[1:]:
        for copy in head_loads(head):
            copy.start()
    enter(member, z)

    half_ffn = ffn_width // 2

    def inner_copy(kind, number, to_end):
        at = pl.ds(number * half_ffn, half_ffn)
        return remote(
            inner.at[at],
            inner_seen.at[kind, at],
            inner_send.at[kind, number],
            inner_recv.at[kind, number],
            member,
            line_place(to_end, core),
        )

    def inner_add(kinds, number):
        at = pl.ds(number * half_ffn, half_ffn)
        result = inner[at].astype(wide)
        for kind in kinds:
            inner_copy(kind, number, 0).wait_recv()
            result = result + inner_seen[kind, at].astype(wide)
        inner[at] = result.astype(low_type)

    def inner_far(number):
        @pl.when(end == 2)
        def _():
            inner_add((0,), number)
            inner_copy(0, number, 1).start()

    def inner_last():
        @pl.when(end == 1)
        def _():
            inner_add((0, 1), 0)
            inner_add((0, 1), 1)
            scatter.each(scatter.down_unit, 0, 6, inner, ffn_out, begin, True)

    for copy in early:
        copy.wait()
    for number in range(2):

        @pl.when(end == 3)
        def _():
            inner_copy(0, number, 2).start()

        @pl.when(end == 0)
        def _():
            inner_copy(1, number, 1).start()

    @pl.when(scatter.owner)
    def _():
        scatter.each(scatter.up_unit, 0, 2 * scatter.across, ffn_ref, ffn_out, begin)

    @pl.when(end == 0)
    def _():
        scatter.each(scatter.down_unit, 0, 6, ffn_ref, ffn_out, begin)

    def rows(number):
        return pl.ds(number * width, width)

    def core_copy(slot, number):
        return remote(
            grads.at[2 + slot, rows(number)],
            paired.at[slot, rows(number)],
            core_send.at[slot, number],
            core_recv.at[slot, number],
            other,
            z,
        )

    reduce = Reduce(
        part_ref, from_x, from_y, passing, last, plane_send, plane_recv, member, z
    )

    def line_copy(kind, number, source, to_end):
        return remote(
            source,
            arrived.at[kind, rows(number)],
            line_send.at[kind, number],
            line_recv.at[kind, number],
            member,
            line_place(to_end, core),
        )

    def pair_up(slot):
        for number in range(3):
            core_copy(slot, number).wait_recv()
            both = grads[slot, rows(number)].astype(wide) + paired[slot, rows(number)].astype(wide)
            paired[slot, rows(number)] = both.astype(low_type)

            @pl.when(end == 3)
            def _():
                line_copy(slot, number, paired.at[slot, rows(number)], 2).start()

            if slot == 1:

                @pl.when(end == 0)
                def _():
                    line_copy(2, number, paired.at[slot, rows(number)], 1).start()

    def summed(slot, kinds, number):
        result = paired[slot, rows(number)].astype(wide)
        for kind in kinds:
            result = result + arrived[kind, rows(number)].astype(wide)
        return result.astype(low_type)

    def on_arrival(kind, number):
        line_copy(kind, number, paired.at[0, rows(number)], 0).wait_recv()

    def outer_step(place, number):
        @pl.when(end == place)
        def _():
            on_arrival(0, number)
            paired[0, rows(number)] = summed(0, (0,), number)
            line_copy(0, number, paired.at[0, rows(number)], place - 1).start()

    def share(number):
        if number < 2:
            across = scatter.across
            scatter.each(
                scatter.in_unit, number * across, (number + 1) * across, total, mix_out, begin
            )
            scatter.each(scatter.gate_unit, number, number + 1, total, mix_out, begin)
        else:
            scatter.each(scatter.out_unit, 0, 4, total, mix_out, begin)
            scatter.smalls(total, mix_out, begin)

    for copy in common:
        copy.wait()
    for turn, head in enumerate(order):
        for copy in head_loads(head):
            copy.wait()
        views = weight_views(w_ref.at[pl.ds(head, 1)], width)
        gate_acc[...] = jnp.zeros_like(gate_acc)
        small_acc[...] = jnp.zeros_like(small_acc)

        def step_block(block, carry):
            at = pl.ds(pl.multiple_of(block * slots, slots), slots)
            proj_low, grad_gates, grad_small = mixer_back_step(
                slot_position(starts_ref[at, :]),
                views,
                p_ref[head, at, :],
                state_ref[head, at, :],
                low_res[at, :],
                width,
            )
            proj_grads[at, head * 2 * width : (head + 1) * 2 * width] = proj_low
            gate_acc[...] += grad_gates
            small_acc[...] += grad_small
            return carry

        lax.fori_loop(0, 4, step_block, 0)
        grads[head, 0 : 2 * width, 0:model] = dot_slots(
            proj_grads[:, head * 2 * width : (head + 1) * 2 * width], x_ref[...]
        ).astype(low_type)
        grads[head, 2 * width : 3 * width, 0:model] = dot_slots(
            low_ref[head], low_res[...]
        ).astype(low_type)
        grads[head, 0:width, model:] = gate_acc[:, :width].astype(low_type)
        grads[head, width : 2 * width, model:] = gate_acc[:, width:].astype(low_type)
        grads[head, 2 * width : 3 * width, model:] = jnp.concatenate(
            [small_acc[...], jnp.zeros((width - 8, width), wide)], axis=0
        ).astype(low_type)
        if head >= 2:
            for number in range(3):
                core_copy(head - 2, number).start()
        if turn == 1:
            pair_up(0)
            inner_far(0)
        elif turn == 2:
            inner_far(1)
            outer_step(2, 0)
            outer_step(2, 1)
        elif turn == 3:
            inner_last()
            outer_step(2, 2)
            outer_step(1, 0)
            outer_step(1, 1)

    def in_block(block):
        at = slice(block * slots, (block + 1) * slots)
        result = jnp.zeros((slots, model), wide)
        for head in range(4):
            result = result + dot_plain(
                proj_grads[at, head * 2 * width : (head + 1) * 2 * width],
                w_ref[head, 0 : 2 * width, 0:model],
            )
        part_ref[at, :] = result.astype(low_type)

    for block in (3, 1, 2, 0):
        in_block(block)
        reduce.begin_block(block)
        if block == 3:
            pair_up(1)
    outer_step(1, 2)
    across = scatter.across
    scatter.arrivals(scatter.up_unit, 2 * across, ffn_ref, ffn_out)

    @pl.when(scatter.owner)
    def _():
        scatter.each(scatter.up_unit, 0, 2 * across, ffn_ref, ffn_out, finish_send)

    reduce.relay()

    for number in range(3):

        @pl.when(end == 2)
        def _():
            on_arrival(1, number)
            paired[1, rows(number)] = summed(1, (1,), number)
            line_copy(1, number, paired.at[1, rows(number)], 1).start()

        @pl.when(end == 1)
        def _():
            on_arrival(1, number)
            on_arrival(2, number)
            total[rows(number)] = summed(1, (1, 2), number)

        @pl.when(end == 0)
        def _():
            on_arrival(0, number)
            total[rows(number)] = summed(0, (0,), number)

        @pl.when(scatter.owner)
        def _():
            share(number)

    reduce.arrive()
    gain = gain_ref[0:1]
    gain_sum = jnp.zeros((1, model), wide)
    for number in range(2):
        at = slice(number * half, (number + 1) * half)
        grad = reduce.result(number)
        value = tokens_ref[at].astype(wide)
        scale = lax.rsqrt(jnp.mean(value * value, axis=1, keepdims=True) + norm_eps)
        scaled = grad * gain
        gain_sum = gain_sum + jnp.sum(grad * value * scale, axis=0, keepdims=True)
        drift = jnp.mean(scaled * value, axis=1, keepdims=True)
        back = scale * scaled - value * (scale * scale * scale * drift)
        tokens_out[at] = (res_ref[at] + back).astype(low_type)
    gain_part[...] = jnp.concatenate([gain_sum, gain_ref[1:2], jnp.zeros((6, model), wide)], axis=0)

    def gain_copy():
        return remote(
            gain_part, gain_plane.at[member], gain_send.at[0], gain_recv.at[member], 7, z
        )

    @pl.when(member != 7)
    def _():
        gain_copy().start()
        gain_copy().wait_send()
        gain_out[...] = jnp.zeros_like(gain_out)

    @pl.when(member == 7)
    def _():
        result = gain_part[...]
        for source in range(7):
            remote(
                gain_part,
                gain_plane.at[source],
                gain_send.at[0],
                gain_recv.at[source],
                7,
                z,
            ).wait_recv()
            result = result + gain_plane[source]
        quarter = model // 4
        for place in range(4):
            gain_line[place] = result[:, place * quarter : (place + 1) * quarter]

        def line_gain(place, slot):
            return remote(
                gain_line.at[place],
                gain_seen.at[slot],
                gain_send.at[1 + place],
                gain_recv.at[8 + slot],
                7,
                place,
            )

        for place in range(4):

            @pl.when(place != z)
            def _():
                line_gain(place, z).start()

        gain_out[...] = gain_line[z]
        for place in range(4):

            @pl.when(place != z)
            def _():
                line_gain(place, place).wait_recv()
                gain_out[...] += gain_seen[place]
                line_gain(place, z).wait_send()

    scatter.arrivals(scatter.down_unit, 6, ffn_ref, ffn_out)
    scatter.arrivals(scatter.in_unit, 2 * across, total, mix_out)
    scatter.arrivals(scatter.gate_unit, 2, total, mix_out)
    scatter.arrivals(scatter.out_unit, 4, total, mix_out)
    scatter.small_arrivals(total, mix_out)

    @pl.when(scatter.owner)
    def _():
        scatter.each(scatter.down_unit, 0, 6, ffn_ref, ffn_out, finish_send)
        scatter.each(scatter.in_unit, 0, 2 * across, total, mix_out, finish_send)
        scatter.each(scatter.gate_unit, 0, 2, total, mix_out, finish_send)
        scatter.each(scatter.out_unit, 0, 4, total, mix_out, finish_send)
        scatter.smalls(total, mix_out, finish_send)

    reduce.finish()
    for number in range(2):

        @pl.when(end >= 2)
        def _():
            inner_copy(0, number, 0).wait_send()

        @pl.when(end == 0)
        def _():
            inner_copy(1, number, 0).wait_send()

    for slot in range(2):
        for number in range(3):
            core_copy(slot, number).wait_send()
    for number in range(3):

        @pl.when(end > 0)
        def _():
            line_copy(0, number, paired.at[0, rows(number)], 0).wait_send()

        @pl.when(end > 1)
        def _():
            line_copy(1, number, paired.at[1, rows(number)], 0).wait_send()

        @pl.when(end == 0)
        def _():
            line_copy(2, number, paired.at[1, rows(number)], 1).wait_send()


def back(
    x,
    res,
    starts,
    weights,
    saved,
    ffn,
    inner,
    tokens,
    residual_grad,
    gains,
    piece_length,
    width,
):
    model = tokens.shape[1]
    ffn_width = ffn.shape[1]
    sizes = (model, width, ffn_width, piece_length)
    slots = tokens.shape[0]
    block = weights.shape[1:]
    count = Scatter(sizes, 0, 0, None, None).count
    dma = pltpu.SemaphoreType.DMA
    vmem = pl.BlockSpec(memory_space=pltpu.VMEM)
    anywhere = pl.BlockSpec(memory_space=pl.ANY)
    held = lambda value: pltpu.VMEM(value.shape, value.dtype)
    return pl.pallas_call(
        functools.partial(back_kernel, sizes),
        in_specs=[anywhere, anywhere, vmem] + [anywhere] * 6 + [vmem] * 3,
        out_specs=[anywhere, anywhere, vmem, vmem],
        out_shape=[
            jax.ShapeDtypeStruct(weights.shape, low_type),
            jax.ShapeDtypeStruct((4,) + ffn.shape, low_type),
            jax.ShapeDtypeStruct(tokens.shape, low_type),
            jax.ShapeDtypeStruct((8, model // 4), wide),
        ],
        scratch_shapes=[held(x), held(res), held(weights)]
        + [held(value) for value in saved]
        + [
            pltpu.VMEM((4 * slots, 8 * width), low_type),
            pltpu.VMEM((width, 2 * width), wide),
            pltpu.VMEM((8, width), wide),
            pltpu.VMEM(weights.shape, low_type),
            pltpu.VMEM((4 * slots, model), low_type),
            pltpu.VMEM((2,) + block, low_type),
            pltpu.VMEM((3,) + block, low_type),
            pltpu.VMEM(block, low_type),
        ]
        + Reduce.scratch(slots, model)
        + [
            held(inner),
            pltpu.VMEM((2,) + inner.shape, low_type),
            pltpu.VMEM((8, model), wide),
            pltpu.VMEM((8, 8, model), wide),
            pltpu.VMEM((4, 8, model // 4), wide),
            pltpu.VMEM((4, 8, model // 4), wide),
            dma((5, 4)),
            dma((2, 3)),
            dma((2, 3)),
            dma((3, 3)),
            dma((3, 3)),
            dma((6,)),
            dma((6,)),
            dma((2, 2)),
            dma((2, 2)),
            dma((5,)),
            dma((12,)),
            dma((3, count)),
            dma((4, count)),
        ],
        compiler_params=pltpu.CompilerParams(
            collective_id=2, has_side_effects=True, vmem_limit_bytes=60 * 1024 * 1024
        ),
        cost_estimate=pl.CostEstimate(
            flops=weights.size * 4 * slots * 4, bytes_accessed=weights.size * 8, transcendentals=0
        ),
        name="back",
    )(
        x,
        res,
        starts,
        weights,
        *saved,
        ffn,
        inner,
        tokens,
        residual_grad,
        gains,
    )


def adam_kernel(
    sizes,
    mix_ref,
    ffn_ref,
    gain_ref,
    master_ref,
    first_ref,
    second_ref,
    piece_ref,
    new_master_ref,
    new_first_ref,
    new_second_ref,
    rows_ref,
    bias_ref,
    grad,
):
    model, width, ffn_width, piece_length, lines, margin = sizes
    member = lax.axis_index("dp")
    step = pl.program_id(0)
    lead = 128
    start_row = (member * piece_length) // lead
    offset = (member * piece_length) % lead
    tiles_in = 4 * width // lead
    tiles_ffn = 4 * ffn_width // lead
    tiles_model = model // lead

    @pl.when(step == 0)
    def _():
        def clear(number, carry):
            grad[pl.ds(pl.multiple_of(number * 256, 256), 256), :] = jnp.zeros((256, lead), wide)
            return carry

        lax.fori_loop(0, grad.shape[0] // 256, clear, 0)

        def place(row, count, body):
            low = member * piece_length

            @pl.when((row * lead < low + piece_length) & ((row + count) * lead > low))
            def _():
                body(row - start_row + margin)

        base = 0

        def in_unit(number, carry):
            kind = number // tiles_model
            at = number % tiles_model

            def body(to):
                for q in range(4):
                    tile = mix_ref[
                        q,
                        pl.ds(pl.multiple_of(kind * width, width), width),
                        pl.ds(pl.multiple_of(at * lead, lead), lead),
                    ].astype(wide)
                    grad[pl.ds(to + q, lead, stride=tiles_in), :] = tile.T

            place((kind * model + at * lead) * tiles_in, lead * tiles_in, body)
            return carry

        lax.fori_loop(0, 2 * tiles_model, in_unit, 0)
        base = 2 * model * tiles_in

        def gate_body(number, carry):
            kind = number // 4
            q = number % 4

            def body(to):
                grad[pl.ds(to, width), :] = mix_ref[
                    q, pl.ds(pl.multiple_of(kind * width, width), width), model:
                ].astype(wide)

            place(2 * model * tiles_in + number * width, width, body)
            return carry

        lax.fori_loop(0, 8, gate_body, 0)
        base = base + 8 * width
        out_base = base

        quarter = width // 4

        def out_unit(number, carry):
            q = number // 4
            part = number % 4

            def body(to):
                for at in range(tiles_model):
                    grad[pl.ds(to + at, quarter, stride=tiles_model), :] = mix_ref[
                        q,
                        pl.ds(pl.multiple_of(2 * width + part * quarter, quarter), quarter),
                        at * lead : (at + 1) * lead,
                    ].astype(wide)

            place(out_base + number * quarter * tiles_model, quarter * tiles_model, body)
            return carry

        lax.fori_loop(0, 16, out_unit, 0)
        base = base + 4 * width * tiles_model
        up_base = base

        def up_unit(number, carry):
            kind = number // tiles_model
            at = number % tiles_model
            columns = pl.ds(pl.multiple_of(at * lead, lead), lead)

            def body(to):
                for tile in range(tiles_ffn):
                    found = []
                    row = tile * lead
                    while row < (tile + 1) * lead:
                        q = row // ffn_width
                        last = min((q + 1) * ffn_width, (tile + 1) * lead)
                        found.append(
                            ffn_ref[
                                q,
                                kind,
                                row - q * ffn_width : last - q * ffn_width,
                                columns,
                            ].astype(wide)
                        )
                        row = last
                    block = found[0] if len(found) == 1 else jnp.concatenate(found, axis=0)
                    grad[pl.ds(to + tile, lead, stride=tiles_ffn), :] = block.T

            place(up_base + (kind * model + at * lead) * tiles_ffn, lead * tiles_ffn, body)
            return carry

        lax.fori_loop(0, 2 * tiles_model, up_unit, 0)
        base = base + 2 * model * tiles_ffn
        down_base = base
        sixth = ffn_width // 6

        def down_unit(number, carry):
            q = number // 6
            part = number % 6

            def body(to):
                for at in range(tiles_model):
                    grad[pl.ds(to + at, sixth, stride=tiles_model), :] = ffn_ref[
                        q,
                        2,
                        pl.ds(pl.multiple_of(part * sixth, 16), sixth),
                        at * lead : (at + 1) * lead,
                    ].astype(wide)

            place(down_base + number * sixth * tiles_model, sixth * tiles_model, body)
            return carry

        lax.fori_loop(0, 24, down_unit, 0)
        small_base = base + 4 * ffn_width * tiles_model
        smalls = [
            mix_ref[q, 2 * width : 2 * width + 16, model:].astype(wide)
            for q in range(4)
        ]

        def small_body(to):
            for q in range(4):
                grad[pl.ds(to + q, 8, stride=tiles_in), :] = smalls[q][:8]
            for number in range(6):
                kind, at = number // 3, number % 3
                grad[pl.ds(to + 8 * tiles_in + number, 1), :] = gain_ref[
                    kind : kind + 1, at * lead : (at + 1) * lead
                ]

        place(small_base, 8 * tiles_in + 6, small_body)
        bias_ref[...] = jnp.concatenate([small[5:7] for small in smalls], axis=1)

    row = margin + step * lines
    shift = (lead - offset) % lead
    here = pltpu.roll(grad[pl.ds(row, lines), :], shift, 1)
    after = pltpu.roll(grad[pl.ds(row + 1, lines), :], shift, 1)
    lane = lax.broadcasted_iota(jnp.int32, (lines, lead), 1)
    piece = jnp.where(lane < lead - offset, here, after).reshape(1, lines * lead)
    piece_ref[...] = piece
    new_first = beta_one * first_ref[...] + (1.0 - beta_one) * piece
    new_second = beta_two * second_ref[...] + (1.0 - beta_two) * piece * piece
    master = master_ref[...]
    new_master = master - learn_rate * (
        new_first / corr_one / (jnp.sqrt(new_second / corr_two) + adam_eps)
        + weight_decay * master
    )
    new_first_ref[...] = new_first
    new_second_ref[...] = new_second
    new_master_ref[...] = new_master
    rows_ref[0] = new_master.reshape(lines, lead).astype(low_type)


def adam(mix, ffn, gains, master, first, second, sizes, chunks):
    model, width, ffn_width = sizes
    piece_length = master.shape[1]
    lines = -(-piece_length // (chunks * 128 * 16)) * 16
    block = lines * 128
    margin = 1536
    rows = -(-(2 * margin + chunks * lines + 8) // 256) * 256
    packed = jax.ShapeDtypeStruct(master.shape, wide)
    chunk_spec = pl.BlockSpec((1, block), lambda s: (0, s))
    once = lambda shape: pl.BlockSpec(
        shape, lambda s: (0,) * len(shape), pipeline_mode=pl.Buffered(1)
    )
    return pl.pallas_call(
        functools.partial(
            adam_kernel, (model, width, ffn_width, piece_length, lines, margin)
        ),
        grid=(chunks,),
        in_specs=[once(mix.shape), once(ffn.shape), once(gains.shape)] + [chunk_spec] * 3,
        out_specs=[chunk_spec] * 4
        + [
            pl.BlockSpec((1, lines, 128), lambda s: (s, 0, 0)),
            pl.BlockSpec((2, 4 * width), lambda s: (0, 0)),
        ],
        out_shape=[packed] * 4
        + [
            jax.ShapeDtypeStruct((chunks, lines, 128), low_type),
            jax.ShapeDtypeStruct((2, 4 * width), wide),
        ],
        scratch_shapes=[pltpu.VMEM((rows, 128), wide)],
        compiler_params=pltpu.CompilerParams(vmem_limit_bytes=48 * 1024 * 1024),
        cost_estimate=pl.CostEstimate(
            flops=20 * piece_length,
            bytes_accessed=40 * piece_length,
            transcendentals=piece_length,
        ),
        name="adam",
    )(mix, ffn, gains, master, first, second)


def spread_kernel(
    own_ref,
    part_hbm,
    residual_ref,
    mask_ref,
    weights_ref,
    block_out,
    held,
    spread,
    part,
    from_x,
    from_y,
    passing,
    last,
    load_sem,
    send_sem,
    recv_sem,
    plane_send,
    plane_recv,
):
    chunks, lines, lead = own_ref.shape
    member = lax.axis_index("dp")
    z = lax.axis_index("shard")
    step = pl.program_id(0)
    reduce = Reduce(part, from_x, from_y, passing, last, plane_send, plane_recv, member, z)
    part_load = pltpu.make_async_copy(part_hbm, part, load_sem.at[chunks])

    def copy_to(origin, chunk, side, to):
        return remote(
            held.at[origin, chunk],
            held.at[origin, chunk],
            send_sem.at[side, origin, chunk],
            recv_sem.at[origin, chunk],
            member,
            to,
        )

    def own_load(chunk):
        return pltpu.make_async_copy(own_ref.at[chunk], held.at[z, chunk], load_sem.at[chunk])

    def pass_on(origin, chunk, right):
        copy_to(origin, chunk, 0, z).wait_recv()
        if right:

            @pl.when(z < 3)
            def _():
                copy_to(origin, chunk, 0, z + 1).start()
        else:

            @pl.when(z > 0)
            def _():
                copy_to(origin, chunk, 1, z - 1).start()

    @pl.when(step == 0)
    def _():
        for chunk in range(chunks):
            own_load(chunk).start()
        part_load.start()
        barrier = pltpu.get_barrier_semaphore()
        for to in (reduce.to_x, reduce.to_y):
            pl.semaphore_signal(
                barrier, inc=1, device_id=(to, z), device_id_type=pl.DeviceIdType.MESH
            )

        @pl.when(z > 0)
        def _():
            pl.semaphore_signal(
                barrier, inc=1, device_id=(member, z - 1), device_id_type=pl.DeviceIdType.MESH
            )

        @pl.when(z < 3)
        def _():
            pl.semaphore_signal(
                barrier, inc=1, device_id=(member, z + 1), device_id_type=pl.DeviceIdType.MESH
            )

        @pl.when((z == 0) | (z == 3))
        def _():
            pl.semaphore_wait(barrier, 3)

        @pl.when((z > 0) & (z < 3))
        def _():
            pl.semaphore_wait(barrier, 4)

        def send_own(chunk, carry):
            own_load(chunk).wait()

            @pl.when(z < 3)
            def _():
                copy_to(z, chunk, 0, z + 1).start()

            @pl.when(z > 0)
            def _():
                copy_to(z, chunk, 1, z - 1).start()

            return carry

        lax.fori_loop(0, chunks, send_own, 0)
        part_load.wait()
        reduce.begin()

        def near(chunk, carry):
            @pl.when(z > 0)
            def _():
                pass_on(z - 1, chunk, True)

            @pl.when(z < 3)
            def _():
                pass_on(z + 1, chunk, False)

            return carry

        lax.fori_loop(0, chunks, near, 0)
        reduce.relay()

    @pl.when(step == 1)
    def _():
        reduce.arrive()
        live = quarters(mask_ref, (2 * reduce.half, 128))[:, 0:1].astype(wide)
        half = reduce.half
        for number in range(2):
            at = slice(number * half, (number + 1) * half)
            block_out[at] = (live[at] * (residual_ref[at] + reduce.result(number))).astype(low_type)
        reduce.finish()

    @pl.when(z >= 2)
    def _():
        pass_on(z - 2, step, True)

    @pl.when(z <= 1)
    def _():
        pass_on(z + 2, step, False)

    @pl.when(z == 3)
    def _():
        copy_to(0, step, 0, z).wait_recv()

    @pl.when(z == 0)
    def _():
        copy_to(3, step, 0, z).wait_recv()

    for origin in range(4):
        spread[origin * lines : (origin + 1) * lines, :] = held[origin, step].astype(wide)

    def line(number, carry):
        weights_ref[:, pl.ds(pl.multiple_of(number * lead, lead), lead)] = spread[
            pl.ds(number, 4, stride=lines), :
        ].astype(low_type)
        return carry

    lax.fori_loop(0, lines, line, 0, unroll=8)

    @pl.when(step == chunks - 1)
    def _():
        for origin in range(4):

            def finish(chunk, carry):
                @pl.when((origin <= z) & (z < 3))
                def _():
                    copy_to(origin, chunk, 0, z).wait_send()

                @pl.when((origin >= z) & (z > 0))
                def _():
                    copy_to(origin, chunk, 1, z).wait_send()

                return carry

            lax.fori_loop(0, chunks, finish, 0)


def spread_weights(own, part, residual, mask, piece_length):
    chunks, lines, lead = own.shape
    slots, model = residual.shape
    once = lambda value: pl.BlockSpec(
        value.shape, lambda s: (0, 0), pipeline_mode=pl.Buffered(1)
    )
    return pl.pallas_call(
        spread_kernel,
        grid=(chunks,),
        in_specs=[pl.BlockSpec(memory_space=pl.ANY)] * 2 + [
            once(residual),
            pl.BlockSpec(memory_space=pltpu.SMEM),
        ],
        out_specs=[pl.BlockSpec((4, lines * lead), lambda s: (0, s)), once(residual)],
        out_shape=[
            jax.ShapeDtypeStruct((4, piece_length), low_type),
            jax.ShapeDtypeStruct(residual.shape, low_type),
        ],
        scratch_shapes=[
            pltpu.VMEM((4, chunks, lines, lead), low_type),
            pltpu.VMEM((4 * lines, lead), wide),
            pltpu.VMEM(part.shape, low_type),
        ]
        + Reduce.scratch(slots, model)
        + [
            pltpu.SemaphoreType.DMA((chunks + 1,)),
            pltpu.SemaphoreType.DMA((2, 4, chunks)),
            pltpu.SemaphoreType.DMA((4, chunks)),
            pltpu.SemaphoreType.DMA((6,)),
            pltpu.SemaphoreType.DMA((6,)),
        ],
        compiler_params=pltpu.CompilerParams(
            collective_id=1, has_side_effects=True, vmem_limit_bytes=32 * 1024 * 1024
        ),
        cost_estimate=pl.CostEstimate(
            flops=4 * piece_length, bytes_accessed=16 * piece_length, transcendentals=0
        ),
        name="spread",
    )(own, part, residual, mask)


def group_body(
    tokens,
    cotangent,
    seq_start,
    live_mask,
    input_proj,
    gate_blocks,
    output_proj,
    ffn_gate_up,
    ffn_down,
    conv_taps,
    gate_bias,
    decay_param,
    norm_gains,
    master_shard,
    first_moment,
    second_moment,
):
    slots, model = tokens.shape
    slice_rec = input_proj.shape[2]
    slice_ffn = ffn_down.shape[0]
    width = slice_rec // 4
    ffn_width = slice_ffn // 4
    piece_length = master_shard.shape[1]
    (
        mix_in,
        mix_weights,
        ffn_weights,
        saved_p,
        saved_state,
        saved_low,
        all_starts,
        residual,
        ffn_in,
        all_grad_out,
        gains,
    ) = front(
        tokens,
        cotangent,
        seq_start,
        live_mask,
        norm_gains,
        conv_taps,
        gate_bias,
        decay_param[None],
        input_proj,
        gate_blocks,
        output_proj,
        ffn_gate_up,
        ffn_down,
        (model, width, ffn_width),
    )
    ffn_in = ffn_in.reshape(4 * slots, model)
    all_grad_out = all_grad_out.reshape(4 * slots, model)
    sum_ffn, inner_down, res_low, grad_residual, gain_sums, ffn_part = middle(
        ffn_in, all_grad_out, ffn_weights, residual, gains
    )
    four_mix, four_ffn, tokens_grad, gain_total = back(
        mix_in,
        res_low.reshape(4 * slots, model),
        all_starts,
        mix_weights,
        (saved_p, saved_state, saved_low),
        sum_ffn,
        inner_down,
        tokens,
        grad_residual,
        gain_sums,
        piece_length,
        width,
    )
    piece, new_master, new_first, new_second, rows, bias_total = adam(
        four_mix,
        four_ffn,
        gain_total,
        master_shard,
        first_moment,
        second_moment,
        (model, width, ffn_width),
        8,
    )
    new_weights, block_out = spread_weights(
        rows,
        ffn_part,
        residual,
        live_mask,
        piece_length,
    )
    return (
        block_out,
        tokens_grad,
        piece,
        new_master,
        new_first,
        new_second,
        new_weights,
        bias_total,
    )


def rms_scale(values, gain):
    return values * lax.rsqrt(jnp.mean(values * values, axis=-1, keepdims=True) + norm_eps) * gain


def conv_mix(signal, taps, position):
    result = taps[-1] + taps[0] * signal
    for shift_by in range(1, taps.shape[0] - 1):
        moved = jnp.pad(signal, ((shift_by, 0), (0, 0)))[:-shift_by]
        result = result + taps[shift_by] * jnp.where((position >= shift_by)[:, None], moved, 0.0)
    return result


def combine_steps(earlier, later):
    decay_first, value_first = earlier
    decay_second, value_second = later
    return (decay_first * decay_second, decay_second * value_first + value_second)


def recurrence(logits, signal, branch, bias_term, decay_term, position):
    row_count = signal.shape[0]
    recur_gate = jax.nn.sigmoid(logits[0].reshape(row_count, -1) + bias_term[0])
    input_gate = jax.nn.sigmoid(logits[1].reshape(row_count, -1) + bias_term[1])
    log_decay = -gate_scale * recur_gate * jax.nn.softplus(-decay_term)
    decay_rate = jnp.where((position > 0)[:, None], jnp.exp(log_decay), 0.0)
    drive_term = jnp.sqrt(-jnp.expm1(2.0 * log_decay)) * input_gate * signal
    states = lax.associative_scan(combine_steps, (decay_rate, drive_term), axis=0)[1]
    return states * jax.nn.gelu(branch)


def gated_gelu(ffn_pre):
    return jax.nn.gelu(ffn_pre[0]) * ffn_pre[1]


def mixer_forward(
    mix_in, input_proj, gate_blocks, output_proj, conv_taps, gate_bias, decay_param, position
):
    projected = jnp.einsum("sd,kdr->ksr", mix_in, input_proj, preferred_element_type=jnp.float32)
    conv_out, conv_pull = jax.vjp(
        lambda signal, taps: conv_mix(signal, taps, position), projected[0], conv_taps
    )
    row_count = conv_out.shape[0]
    conv_low = conv_out.astype(jnp.bfloat16).reshape(
        row_count, gate_blocks.shape[1], gate_blocks.shape[2]
    )
    gate_logits = jnp.einsum(
        "shb,khbc->kshc", conv_low, gate_blocks, preferred_element_type=jnp.float32
    )
    mixed, mix_pull = jax.vjp(
        lambda logits, signal, branch, bias_term, decay_term: recurrence(
            logits, signal, branch, bias_term, decay_term, position
        ),
        gate_logits,
        conv_out,
        projected[1],
        gate_bias,
        decay_param,
    )
    mixed_low = mixed.astype(jnp.bfloat16)
    partial_out = jnp.dot(mixed_low, output_proj, preferred_element_type=jnp.float32)
    return (partial_out, (conv_pull, conv_low, mix_pull, mixed_low))


def mixer_backward(grad_out_low, mix_in, saved, input_proj, gate_blocks, output_proj):
    conv_pull, conv_low, mix_pull, mixed_low = saved
    grad_output_proj = jnp.einsum(
        "sr,sd->rd", mixed_low, grad_out_low, preferred_element_type=jnp.float32
    )
    grad_mixed = jnp.einsum(
        "sd,rd->sr", grad_out_low, output_proj, preferred_element_type=jnp.float32
    )
    grad_logits, grad_conv_direct, grad_branch, grad_bias, grad_decay = mix_pull(grad_mixed)
    logits_low = grad_logits.astype(jnp.bfloat16)
    grad_blocks = jnp.einsum(
        "shb,kshc->khbc", conv_low, logits_low, preferred_element_type=jnp.float32
    )
    grad_conv_gates = jnp.einsum(
        "kshc,khbc->shb", logits_low, gate_blocks, preferred_element_type=jnp.float32
    )
    grad_signal, grad_taps = conv_pull(
        grad_conv_direct + grad_conv_gates.reshape(grad_conv_direct.shape)
    )
    proj_low = jnp.stack([grad_signal, grad_branch]).astype(jnp.bfloat16)
    grad_input_proj = jnp.einsum(
        "sd,ksr->kdr", mix_in, proj_low, preferred_element_type=jnp.float32
    )
    grad_mix_in = jnp.einsum(
        "ksr,kdr->sd", proj_low, input_proj, preferred_element_type=jnp.float32
    )
    return (
        grad_mix_in,
        (grad_input_proj, grad_blocks, grad_output_proj, grad_taps, grad_bias, grad_decay),
    )


def ffn_forward(ffn_in_low, ffn_gate_up, ffn_down):
    ffn_pre = jnp.einsum("sd,kdf->ksf", ffn_in_low, ffn_gate_up, preferred_element_type=jnp.float32)
    ffn_act, ffn_pull = jax.vjp(gated_gelu, ffn_pre)
    ffn_low = ffn_act.astype(jnp.bfloat16)
    partial_ffn = jnp.dot(ffn_low, ffn_down, preferred_element_type=jnp.float32)
    return (partial_ffn, (ffn_pull, ffn_low))


def ffn_backward(grad_low, ffn_in_low, saved, ffn_gate_up, ffn_down):
    ffn_pull, ffn_low = saved
    grad_down = jnp.einsum("sf,sd->fd", ffn_low, grad_low, preferred_element_type=jnp.float32)
    grad_act = jnp.einsum("sd,fd->sf", grad_low, ffn_down, preferred_element_type=jnp.float32)
    grad_pre = ffn_pull(grad_act)[0]
    pre_low = grad_pre.astype(jnp.bfloat16)
    grad_gate_up = jnp.einsum(
        "sd,ksf->kdf", ffn_in_low, pre_low, preferred_element_type=jnp.float32
    )
    grad_ffn_in = jnp.einsum(
        "ksf,kdf->sd", pre_low, ffn_gate_up, preferred_element_type=jnp.float32
    )
    return (grad_ffn_in, grad_gate_up, grad_down)


def body(
    tokens,
    cotangent,
    seq_start,
    live_mask,
    input_proj,
    gate_blocks,
    output_proj,
    ffn_gate_up,
    ffn_down,
    conv_taps,
    gate_bias,
    decay_param,
    norm_gains,
    master_shard,
    first_moment,
    second_moment,
):
    slot_count = tokens.shape[0]
    position = jnp.arange(slot_count, dtype=jnp.int32) - seq_start
    mask_rows = live_mask.astype(jnp.float32)[:, None]
    stream = tokens.astype(jnp.float32)
    grad_stream = cotangent.astype(jnp.float32) * mask_rows
    shards = (
        input_proj,
        gate_blocks,
        output_proj,
        ffn_gate_up,
        ffn_down,
        conv_taps,
        gate_bias,
        decay_param,
        norm_gains,
    )
    (
        full_in,
        full_blocks,
        full_out,
        full_up,
        full_down,
        full_taps,
        full_bias,
        full_decay,
        full_gains,
    ) = (
        lax.all_gather(shards[0], "shard", axis=2, tiled=True),
        lax.all_gather(shards[1], "shard", axis=1, tiled=True),
        lax.all_gather(shards[2], "shard", axis=0, tiled=True),
        lax.all_gather(shards[3], "shard", axis=2, tiled=True),
        lax.all_gather(shards[4], "shard", axis=0, tiled=True),
        lax.all_gather(shards[5], "shard", axis=1, tiled=True),
        lax.all_gather(shards[6], "shard", axis=1, tiled=True),
        lax.all_gather(shards[7], "shard", axis=0, tiled=True),
        lax.all_gather(shards[8], "shard", axis=1, tiled=True),
    )
    gains = full_gains.astype(jnp.float32)
    normed, norm_pull = jax.vjp(rms_scale, stream, gains[0])
    mix_in = normed.astype(jnp.bfloat16)
    mix_out, mix_saved = mixer_forward(
        mix_in,
        full_in,
        full_blocks,
        full_out,
        full_taps.astype(jnp.float32),
        full_bias.astype(jnp.float32),
        full_decay.astype(jnp.float32),
        position,
    )
    residual = stream + mix_out
    normed_two, second_pull = jax.vjp(rms_scale, residual, gains[1])
    ffn_in_low = normed_two.astype(jnp.bfloat16)
    ffn_result, ffn_saved = ffn_forward(ffn_in_low, full_up, full_down)
    block_out = (mask_rows * (residual + ffn_result)).astype(jnp.bfloat16)
    grad_ffn_in, grad_up, grad_down = ffn_backward(
        grad_stream.astype(jnp.bfloat16), ffn_in_low, ffn_saved, full_up, full_down
    )
    grad_norm_two, grad_gain_two = second_pull(grad_ffn_in)
    grad_residual = grad_stream + grad_norm_two
    grad_mix_in, mix_grads = mixer_backward(
        grad_residual.astype(jnp.bfloat16), mix_in, mix_saved, full_in, full_blocks, full_out
    )
    grad_norm_one, grad_gain_one = norm_pull(grad_mix_in)
    tokens_grad = (grad_residual + grad_norm_one).astype(jnp.bfloat16)
    grads = (
        mix_grads[0],
        mix_grads[1],
        mix_grads[2],
        grad_up,
        grad_down,
        mix_grads[3],
        mix_grads[4],
        mix_grads[5],
        jnp.stack([grad_gain_one, grad_gain_two]),
    )
    summed = (
        lax.psum_scatter(
            grads[0].astype(jnp.bfloat16), "shard", scatter_dimension=2, tiled=True
        ).astype(jnp.float32),
        lax.psum_scatter(
            grads[1].astype(jnp.bfloat16), "shard", scatter_dimension=1, tiled=True
        ).astype(jnp.float32),
        lax.psum_scatter(
            grads[2].astype(jnp.bfloat16), "shard", scatter_dimension=0, tiled=True
        ).astype(jnp.float32),
        lax.psum_scatter(
            grads[3].astype(jnp.bfloat16), "shard", scatter_dimension=2, tiled=True
        ).astype(jnp.float32),
        lax.psum_scatter(
            grads[4].astype(jnp.bfloat16), "shard", scatter_dimension=0, tiled=True
        ).astype(jnp.float32),
        lax.psum_scatter(
            grads[5].astype(jnp.bfloat16), "shard", scatter_dimension=1, tiled=True
        ).astype(jnp.float32),
        lax.psum_scatter(
            grads[6].astype(jnp.bfloat16), "shard", scatter_dimension=1, tiled=True
        ).astype(jnp.float32),
        lax.psum_scatter(
            grads[7].astype(jnp.bfloat16), "shard", scatter_dimension=0, tiled=True
        ).astype(jnp.float32),
        lax.psum_scatter(
            grads[8].astype(jnp.bfloat16), "shard", scatter_dimension=1, tiled=True
        ).astype(jnp.float32),
    )
    flat = jnp.concatenate([member.reshape(1, -1) for member in summed], axis=1)
    piece = lax.psum_scatter(flat, "dp", scatter_dimension=1, tiled=True)
    bias_total = lax.psum(summed[6], "dp")
    new_first = beta_one * first_moment + (1.0 - beta_one) * piece
    new_second = beta_two * second_moment + (1.0 - beta_two) * piece * piece
    new_master = master_shard - learn_rate * (
        new_first / corr_one / (jnp.sqrt(new_second / corr_two) + adam_eps)
        + weight_decay * master_shard
    )
    new_weights = lax.all_gather(new_master.astype(jnp.bfloat16), "shard", axis=0, tiled=True)
    return (
        block_out,
        tokens_grad,
        piece,
        new_master,
        new_first,
        new_second,
        new_weights,
        bias_total,
    )


def solution(mesh):
    fits = mesh.shape["dp"] == 8 and mesh.shape["shard"] == 4
    placed = (
        P(("dp", "shard"), None),
        P(("dp", "shard"), None),
        P(("dp", "shard")),
        P(("dp", "shard")),
        P(None, None, "shard"),
        P(None, "shard", None, None),
        P("shard", None),
        P(None, None, "shard"),
        P("shard", None),
        P(None, "shard"),
        P(None, "shard"),
        P("shard"),
        P(None, "shard"),
        P("shard", "dp"),
        P("shard", "dp"),
        P("shard", "dp"),
    )
    return jax.shard_map(
        group_body if fits else body,
        mesh=mesh,
        in_specs=placed,
        out_specs=(
            P(("dp", "shard"), None),
            P(("dp", "shard"), None),
            P("shard", "dp"),
            P("shard", "dp"),
            P("shard", "dp"),
            P("shard", "dp"),
            P(None, "dp"),
            P(None, "shard"),
        ),
        check_vma=False,
    )
```

```python
import functools
import jax
import jax.numpy as jnp
from jax import lax
from jax.experimental import pallas as pl
from jax.experimental.pallas import tpu as pltpu
from jax.sharding import PartitionSpec as P

norm_eps = 1e-06
gate_scale = 8.0
beta_one = 0.9
beta_two = 0.95
learn_rate = 0.01
weight_decay = 0.1
adam_eps = 1e-08
corr_one = 1.0 - beta_one**10.0
corr_two = 1.0 - beta_two**10.0
low_type = jnp.bfloat16
wide = jnp.float32
gelu_scale = 0.7978845608028654
gelu_cube = 0.044715


def add_low(left, right):
    return (left.astype(wide) + right.astype(wide)).astype(low_type)


def dot_rows(left, right):
    return lax.dot_general(left, right, (((1,), (1,)), ((), ())), preferred_element_type=wide)


def dot_plain(left, right):
    return lax.dot_general(left, right, (((1,), (0,)), ((), ())), preferred_element_type=wide)


def dot_slots(left, right):
    return lax.dot_general(left, right, (((0,), (0,)), ((), ())), preferred_element_type=wide)


def gelu_parts(value):
    square = value * value
    bent = jnp.tanh(gelu_scale * value * (1.0 + gelu_cube * square))
    half = 0.5 * (1.0 + bent)
    slope = half + 0.5 * value * (1.0 - bent * bent) * gelu_scale * (
        1.0 + 3.0 * gelu_cube * square
    )
    return (value * half, slope)


def shift_down(value, step):
    if step % 8 == 0:
        return jnp.concatenate([value[-step:], value[:-step]], axis=0)
    return pltpu.roll(value, step, 0)


def shift_up(value, step):
    if step % 8 == 0:
        return jnp.concatenate([value[step:], value[:step]], axis=0)
    return pltpu.roll(value, value.shape[0] - step, 0)


def scan_slots(decay, value, shift):
    step = 1
    while step < value.shape[0]:
        value = value + decay * shift(value, step)
        if 2 * step < value.shape[0]:
            decay = decay * shift(decay, step)
        step *= 2
    return value


def one_minus_exp(value):
    series = jnp.ones_like(value)
    for number in range(11, 1, -1):
        series = 1.0 - value * (1.0 / number) * series
    return jnp.where(value < 0.8, value * series, 1.0 - jnp.exp(-value))


def soft_plus(value):
    return jnp.maximum(value, 0.0) + jnp.log1p(jnp.exp(-jnp.abs(value)))


def mixer_parts(first, position, small, gates):
    conv_out = small[4:5] + small[0:1] * first
    shifted = []
    for step in range(1, 4):
        moved = jnp.where(position >= step, shift_down(first, step), 0.0)
        shifted.append(moved)
        conv_out = conv_out + small[step : step + 1] * moved
    conv_low = conv_out.astype(low_type)
    logits = dot_plain(conv_low, gates)
    width = first.shape[1]
    recur_gate = jax.nn.sigmoid(logits[:, :width] + small[5:6])
    input_gate = jax.nn.sigmoid(logits[:, width:] + small[6:7])
    rate = gate_scale * soft_plus(-small[7:8])
    log_decay = -rate * recur_gate
    decay = jnp.where(position > 0, jnp.exp(log_decay), 0.0)
    gone = one_minus_exp(-2.0 * log_decay)
    root = jnp.sqrt(gone)
    return conv_out, shifted, conv_low, recur_gate, input_gate, rate, decay, gone, root


def weight_views(w_ref, width):
    model = w_ref.shape[2] - width
    proj = w_ref[0, 0 : 2 * width, 0:model]
    out = w_ref[0, 2 * width : 3 * width, 0:model]
    gates = jnp.concatenate(
        [w_ref[0, 0:width, model:], w_ref[0, width : 2 * width, model:]], axis=1
    )
    small = w_ref[0, 2 * width : 2 * width + 16, model:].astype(wide)
    return proj, out, gates, small


def slot_position(starts):
    slot = lax.broadcasted_iota(jnp.int32, (starts.shape[0], 1), 0)
    return slot - starts[:, 0:1].astype(wide).astype(jnp.int32)


def mixer_step(x, position, views, width):
    proj, out, gates, small = views
    projected = dot_rows(x, proj)
    conv_out, _, _, _, input_gate, _, decay, _, root = mixer_parts(
        projected[:, :width], position, small, gates
    )
    states = scan_slots(decay, root * input_gate * conv_out, shift_down)
    mixed_low = (states * gelu_parts(projected[:, width:])[0]).astype(low_type)
    return projected, states, mixed_low, dot_plain(mixed_low, out)


def mixer_back_step(position, views, projected, states, res_low, width):
    _, out, gates, small = views
    first = projected[:, :width]
    conv_out, shifted, conv_low, recur_gate, input_gate, rate, decay, gone, root = mixer_parts(
        first, position, small, gates
    )
    grad_mixed = dot_rows(res_low, out)
    active, slope = gelu_parts(projected[:, width:])
    grad_second = grad_mixed * states * slope
    adjoint = scan_slots(shift_up(decay, 1), grad_mixed * active, shift_up)
    grad_decay = adjoint * shift_down(states, 1)
    gated = adjoint * conv_out
    grad_root = gated * input_gate
    grad_input_gate = gated * root
    grad_conv = adjoint * root * input_gate
    grad_log = grad_decay * decay - grad_root * (1.0 - gone) / root
    grad_recur = -rate * grad_log
    grad_logit_a = grad_recur * recur_gate * (1.0 - recur_gate)
    grad_logit_b = grad_input_gate * input_gate * (1.0 - input_gate)
    grad_param = jnp.sum(grad_log * recur_gate, axis=0, keepdims=True) * (
        gate_scale * jax.nn.sigmoid(-small[7:8])
    )
    logits_low = jnp.concatenate([grad_logit_a, grad_logit_b], axis=1).astype(low_type)
    grad_conv = grad_conv + dot_rows(logits_low, gates)
    grad_gates = dot_slots(conv_low, logits_low)
    sums = [jnp.sum(grad_conv * first, axis=0, keepdims=True)]
    grad_first = small[0:1] * grad_conv
    for step in range(1, 4):
        sums.append(jnp.sum(grad_conv * shifted[step - 1], axis=0, keepdims=True))
        kept = jnp.where(position >= step, grad_conv, 0.0)
        grad_first = grad_first + small[step : step + 1] * shift_up(kept, step)
    sums.append(jnp.sum(grad_conv, axis=0, keepdims=True))
    sums.append(jnp.sum(grad_logit_a, axis=0, keepdims=True))
    sums.append(jnp.sum(grad_logit_b, axis=0, keepdims=True))
    sums.append(grad_param)
    proj_low = jnp.concatenate([grad_first, grad_second], axis=1).astype(low_type)
    return proj_low, grad_gates, jnp.concatenate(sums, axis=0)


def peer_x(chip):
    return chip + 1 - 2 * (chip % 2)


def peer_y(chip):
    return chip + 2 - 4 * (chip // 2)


def line_place(end, core):
    return end + core * (3 - 2 * end)


def remote(source, target, send, recv, member, z):
    return pltpu.make_async_remote_copy(
        src_ref=source,
        dst_ref=target,
        send_sem=send,
        recv_sem=recv,
        device_id=(member, z),
        device_id_type=pl.DeviceIdType.MESH,
    )


def enter(member, z):
    barrier = pltpu.get_barrier_semaphore()
    for other in range(8):

        @pl.when(member != other)
        def _():
            pl.semaphore_signal(
                barrier, inc=1, device_id=(other, z), device_id_type=pl.DeviceIdType.MESH
            )

    for other in range(4):

        @pl.when(z != other)
        def _():
            pl.semaphore_signal(
                barrier, inc=1, device_id=(member, other), device_id_type=pl.DeviceIdType.MESH
            )

    pl.semaphore_wait(barrier, 10)


def quarters(value_ref, shape):
    slots = shape[0]
    row = lax.broadcasted_iota(jnp.int32, shape, 0)
    result = jnp.full(shape, value_ref[3 * slots // 4], jnp.int32)
    for number in (2, 1, 0):
        result = jnp.where(
            row < (number + 1) * slots // 4, value_ref[number * slots // 4], result
        )
    return result


class Gather:
    def __init__(self, own, target, send, recv, member, z):
        self.own, self.target = own, target
        self.send, self.recv = send, recv
        chip, core = member // 2, member % 2
        self.to_x = peer_x(chip) * 2 + core
        self.to_y = peer_y(chip) * 2 + core
        self.z = z
        self.half = own.shape[0] // 2

    def copy(self, number):
        low, high = pl.ds(0, self.half), pl.ds(self.half, self.half)
        source, target, to = (
            (self.own, self.target.at[1], self.to_x),
            (self.own, self.target.at[2], self.to_y),
            (self.target.at[1, low], self.target.at[3, low], self.to_y),
            (self.target.at[2, high], self.target.at[3, high], self.to_x),
        )[number]
        return remote(source, target, self.send.at[number], self.recv.at[number], to, self.z)

    def begin(self):
        self.copy(0).start()
        self.copy(1).start()

    def relay(self):
        self.copy(0).wait_recv()
        self.copy(2).start()
        self.copy(1).wait_recv()
        self.copy(3).start()

    def arrive(self):
        self.copy(2).wait_recv()
        self.copy(3).wait_recv()

    def finish(self):
        for number in range(4):
            self.copy(number).wait_send()


class Reduce:
    def __init__(self, part, from_x, from_y, passing, last, send, recv, member, z):
        self.part, self.from_x, self.from_y = part, from_x, from_y
        self.passing, self.last = passing, last
        self.send, self.recv = send, recv
        chip, core = member // 2, member % 2
        self.to_x = peer_x(chip) * 2 + core
        self.to_y = peer_y(chip) * 2 + core
        self.z = z
        self.slots = part.shape[0] // 4
        self.half = self.slots // 2

    def copy(self, number):
        slots, half = self.slots, self.half
        source, target, to = (
            (self.part.at[pl.ds(slots, half)], self.from_x.at[0], self.to_x),
            (self.part.at[pl.ds(3 * slots, half)], self.from_x.at[1], self.to_x),
            (self.part.at[pl.ds(2 * slots + half, half)], self.from_y.at[0], self.to_y),
            (self.part.at[pl.ds(3 * slots + half, half)], self.from_y.at[1], self.to_y),
            (self.passing.at[0], self.last.at[0], self.to_y),
            (self.passing.at[1], self.last.at[1], self.to_x),
        )[number]
        return remote(source, target, self.send.at[number], self.recv.at[number], to, self.z)

    def begin(self):
        for block in (3, 1, 2):
            self.begin_block(block)

    def begin_block(self, block):
        for number in {1: (0,), 2: (2,), 3: (1, 3)}.get(block, ()):
            self.copy(number).start()

    def relay(self):
        slots, half = self.slots, self.half
        self.copy(1).wait_recv()
        self.passing[0] = (
            self.part[2 * slots : 2 * slots + half].astype(wide) + self.from_x[1].astype(wide)
        ).astype(low_type)
        self.copy(4).start()
        self.copy(3).wait_recv()
        self.passing[1] = (
            self.part[slots + half : 2 * slots].astype(wide) + self.from_y[1].astype(wide)
        ).astype(low_type)
        self.copy(5).start()

    def arrive(self):
        for number in (0, 2, 4, 5):
            self.copy(number).wait_recv()

    def result(self, number):
        direct = self.from_x if number == 0 else self.from_y
        return (
            self.part[number * self.half : (number + 1) * self.half].astype(wide)
            + direct[0].astype(wide)
            + self.last[number].astype(wide)
        )

    def finish(self):
        for number in range(6):
            self.copy(number).wait_send()

    @staticmethod
    def scratch(slots, model):
        return [pltpu.VMEM((2, slots // 2, model), low_type)] * 4


def norm_rows(value, gain):
    scale = lax.rsqrt(jnp.mean(value * value, axis=1, keepdims=True) + norm_eps)
    return value * scale * gain


def front_kernel(
    sizes,
    tokens_in,
    cot_in,
    start_ref,
    live_ref,
    gain_in,
    taps_ref,
    bias_ref,
    decay_ref,
    in_ref,
    gate_ref,
    out_ref,
    up_ref,
    down_ref,
    mix_in,
    weights,
    ffn_weights,
    saved_p,
    saved_state,
    saved_low,
    starts_out,
    residual_out,
    ffn_in,
    cot_out,
    gains_out,
    tokens_ref,
    cot_ref,
    gain_ref,
    tokens_all,
    raw_in,
    raw_up,
    raw_down,
    turned,
    gain_seen,
    acc,
    part,
    from_x,
    from_y,
    passing,
    last,
    load_sem,
    gain_send,
    gain_recv,
    m_send,
    m_recv,
    m_core_send,
    m_core_recv,
    f_send,
    f_recv,
    f_core_send,
    f_core_recv,
    g_send,
    g_recv,
    r_send,
    r_recv,
):
    model, width, ffn_width = sizes
    member = lax.axis_index("dp")
    z = lax.axis_index("shard")
    chip, core = member // 2, member % 2
    end = z + core * (3 - 2 * z)
    other = chip * 2 + 1 - core
    slots = cot_in.shape[0]
    half_ffn = ffn_width // 2
    owner = core == z // 2

    window = 128 * ((chip * ffn_width) // 128)
    skew = chip * ffn_width - window
    quarter = pl.ds(pl.multiple_of(chip * width, width), width)
    wide_window = pl.ds(pl.multiple_of(window, 128), raw_up.shape[2])

    def loads():
        found = [
            (out_ref.at[quarter], weights.at[end, pl.ds(2 * width, width), pl.ds(0, model)]),
        ]
        for kind in range(2):
            found.append((in_ref.at[kind, :, quarter], raw_in.at[kind]))
            found.append(
                (
                    gate_ref.at[kind, chip],
                    weights.at[end, pl.ds(kind * width, width), pl.ds(model, width)],
                )
            )
        found.append(
            (down_ref.at[pl.ds(pl.multiple_of(chip * ffn_width, 32), ffn_width)], raw_down)
        )
        for kind in range(2):
            found.append((up_ref.at[kind, :, wide_window], raw_up.at[kind]))
        return [
            pltpu.make_async_copy(source, target, load_sem.at[number])
            for number, (source, target) in enumerate(found)
        ]

    def turned_copy(kind):
        return pltpu.make_async_copy(
            raw_down
            if kind == 2
            else turned.at[kind, pl.ds(pl.multiple_of(skew, 32), ffn_width)],
            ffn_weights.at[kind, pl.ds(pl.multiple_of(2 * end * ffn_width, 32), ffn_width)],
            load_sem.at[9 + kind],
        )

    @pl.when(owner)
    def _():
        for copy in loads():
            copy.start()

    tokens_ref[:, :model] = tokens_in[...]
    tokens_ref[:, model:] = quarters(start_ref, (slots, width)).astype(wide).astype(low_type)
    live = quarters(live_ref, (slots, 128))[:, 0:1].astype(wide)
    cot_ref[...] = (cot_in[...].astype(wide) * live).astype(low_type)
    gain_ref[...] = jnp.concatenate(
        [gain_in[...].astype(wide), jnp.zeros((14, model // 4), wide)], axis=0
    ).astype(low_type)
    enter(member, z)

    gather_tokens = Gather(tokens_ref, tokens_all, g_send.at[0], g_recv.at[0], member, z)
    gather_cot = Gather(cot_ref, cot_out, g_send.at[1], g_recv.at[1], member, z)
    gather_ffn = Gather(ffn_in.at[0], ffn_in, g_send.at[2], g_recv.at[2], member, z)
    reduce = Reduce(part, from_x, from_y, passing, last, r_send, r_recv, member, z)
    own_cot = pltpu.make_async_copy(cot_ref, cot_out.at[0], load_sem.at[12])

    gather_tokens.begin()
    own_cot.start()

    def gain_copy(to, slot):
        return remote(
            gain_ref, gain_seen.at[slot], gain_send.at[to], gain_recv.at[slot], member, to
        )

    for to in range(4):

        @pl.when(to != z)
        def _():
            gain_copy(to, z).start()

    gain_seen[z] = gain_ref[...]

    def m_rows(number):
        return pl.ds(number * width, width)

    def m_copy(slot, number, way, to_end):
        place = weights.at[slot, m_rows(number)]
        return remote(
            place,
            place,
            m_send.at[way, slot, number],
            m_recv.at[slot, number],
            member,
            line_place(to_end, core),
        )

    def m_core(slot, number):
        return remote(
            weights.at[slot, m_rows(number)],
            weights.at[2 + slot, m_rows(number)],
            m_core_send.at[slot, number],
            m_core_recv.at[slot, number],
            other,
            z,
        )

    def f_place(slot, number):
        row = ((slot % 2) * 2 + slot // 2) * ffn_width + (number % 2) * half_ffn
        return ffn_weights.at[number // 2, pl.ds(row, half_ffn)]

    def f_copy(slot, number, way, to_end):
        place = f_place(slot, number)
        return remote(
            place,
            place,
            f_send.at[way, slot, number],
            f_recv.at[slot, number],
            member,
            line_place(to_end, core),
        )

    def f_core(slot, number):
        return remote(
            f_place(slot, number),
            f_place(2 + slot, number),
            f_core_send.at[slot, number],
            f_core_recv.at[slot, number],
            other,
            z,
        )

    def pass_on(copy, core_copy, slot, number):
        if slot == 0:

            @pl.when(end < 3)
            def _():
                copy(slot, number, 0, end + 1).start()
        else:

            @pl.when((end == 1) | (end == 2))
            def _():
                copy(slot, number, 0, end + 1).start()

        core_copy(slot, number).start()

    def pass_back(copy, numbers):
        @pl.when(end == 1)
        def _():
            for number in numbers:
                copy(1, number, 1, 0).start()

    def start_own(copy, core_copy, numbers):
        for slot in range(2):

            @pl.when(end == slot)
            def _():
                for number in numbers[slot]:
                    pass_on(copy, core_copy, slot, number)

    def turn_in(kind):
        @pl.when(owner)
        def _():
            for copy in loads()[1 + 2 * kind : 3 + 2 * kind]:
                copy.wait()

            def turn(at, carry):
                columns = pl.ds(pl.multiple_of(at * 256, 256), 256)
                weights[end, kind * width : (kind + 1) * width, columns] = raw_in[
                    kind, columns, :
                ].T
                return carry

            lax.fori_loop(0, model // 256, turn, 0)

        start_own(m_copy, m_core, ((kind,), (kind,)))
        pass_back(m_copy, (kind,))

    def turn_up(kind):
        @pl.when(owner)
        def _():
            loads()[6 + kind].wait()

            def turn(at, carry):
                columns = pl.ds(pl.multiple_of(at * 256, 256), 256)
                turned[kind, :, columns] = raw_up[kind, columns, :].T
                return carry

            lax.fori_loop(0, model // 256, turn, 0)
            turned_copy(kind).start()

    @pl.when(owner)
    def _():
        weights[end, 2 * width : 3 * width, model:] = jnp.concatenate(
            [
                taps_ref[:, quarter].astype(wide),
                bias_ref[:, quarter].astype(wide),
                decay_ref[:, quarter].astype(wide),
                jnp.zeros((width - 8, width), wide),
            ],
            axis=0,
        ).astype(low_type)
        loads()[0].wait()

    start_own(m_copy, m_core, ((2,), (2,)))
    pass_back(m_copy, (2,))
    turn_in(0)
    turn_in(1)

    @pl.when(owner)
    def _():
        loads()[5].wait()
        turned_copy(2).start()

    turn_up(0)
    turn_up(1)
    gather_tokens.relay()
    m_order = (2, 0, 1)

    @pl.when(end < 3)
    def _():
        for number in m_order:
            for slot in (1, 0):

                @pl.when(end != slot)
                def _():
                    m_copy(slot, number, 0, 0).wait_recv()
                    pass_on(m_copy, m_core, slot, number)

    @pl.when(owner)
    def _():
        for kind in range(3):
            turned_copy(kind).wait()

    f_order = ((4, 5, 0, 1, 2, 3), (4, 5, 0, 2))
    start_own(f_copy, f_core, f_order)

    def f_pass(slot, numbers):
        for number in numbers:
            f_copy(slot, number, 0, 0).wait_recv()
            pass_on(f_copy, f_core, slot, number)

    def f_step(step):
        @pl.when(end == 1)
        def _():
            f_pass(0, ((), (4, 5), (0, 1), (2, 3), (), ())[step])

        @pl.when(end == 2)
        def _():
            f_pass(1, ((4,), (5, 0), (2,), (), (), ())[step])
            f_pass(0, ((), (), (4,), (5, 0), (1, 2), (3,))[step])

        if step == 2:
            pass_back(f_copy, f_order[1])

    def far_step(items):
        @pl.when(end == 3)
        def _():
            for slot, number in items:
                f_copy(slot, number, 0, 0).wait_recv()
                f_core(slot, number).start()

    def near_step(step):
        @pl.when(end == 0)
        def _():
            f_pass(1, ((), (), (), (), (), f_order[1])[step])

    for to in range(4):

        @pl.when(to != z)
        def _():
            gain_copy(to, to).wait_recv()

    gains = jnp.concatenate([gain_seen[at].astype(wide) for at in range(4)], axis=1)
    gains_out[...] = gains[0:8]
    gather_tokens.arrive()

    def norm_block(block):
        if block == 0:
            source, starts = tokens_ref[:, :model], tokens_ref[:, model:]
        else:
            source, starts = tokens_all[block, :, :model], tokens_all[block, :, model:]
        at = slice(block * slots, (block + 1) * slots)
        mix_in[at, :] = norm_rows(source.astype(wide), gains_out[0:1]).astype(low_type)
        starts_out[at, :] = starts

    for block in range(4):
        norm_block(block)
    gather_cot.begin()
    f_step(0)

    late = end >= 2
    for turn in range(4):
        head = (turn + 2 * late) % 4
        if turn == 2:

            @pl.when(end == 3)
            def _():
                for number in m_order:
                    for slot in (1, 0):
                        m_copy(slot, number, 0, 0).wait_recv()
                        m_core(slot, number).start()

        @pl.when(head >= 2)
        def _():
            for number in m_order:
                m_core(head - 2, number).wait_recv()

        views = weight_views(weights.at[pl.ds(head, 1)], width)

        def step_block(count, carry):
            block = 3 - count
            rows = pl.ds(pl.multiple_of(block * slots, slots), slots)
            position = slot_position(starts_out[rows, :])
            projected, states, mixed_low, product = mixer_step(
                mix_in[rows, :], position, views, width
            )
            saved_p[head, rows, :] = projected
            saved_state[head, rows, :] = states
            saved_low[head, rows, :] = mixed_low
            if turn == 0:
                acc[rows, :] = product
            elif turn < 3:
                acc[rows, :] += product
            else:
                part[rows, :] = (acc[rows, :] + product).astype(low_type)
                for number in (3, 2, 1):

                    @pl.when(block == number)
                    def _():
                        reduce.begin_block(number)

            return carry

        lax.fori_loop(0, 4, step_block, 0)
        f_step(turn + 1)
        near_step(turn + 1)
        if turn == 0:
            gather_cot.relay()

    far_step(((1, 4), (1, 5)))
    reduce.relay()
    f_step(5)
    near_step(5)
    far_step(((1, 0), (1, 2)))
    reduce.arrive()
    half = slots // 2
    for number in range(2):
        at = slice(number * half, (number + 1) * half)
        residual = tokens_ref[at, :model].astype(wide) + reduce.result(number)
        residual_out[at, :] = residual
        ffn_in[0, at, :] = norm_rows(residual, gains_out[1:2]).astype(low_type)
    gather_ffn.begin()
    far_step(((0, 4), (0, 5), (0, 0)))
    gather_ffn.relay()

    far_step(((0, 1), (0, 2), (0, 3)))

    gather_ffn.arrive()
    gather_cot.arrive()
    own_cot.wait()
    for slot in range(2):
        for number in f_order[slot]:
            f_core(slot, number).wait_recv()

    for gather in (gather_tokens, gather_cot, gather_ffn, reduce):
        gather.finish()
    for to in range(4):

        @pl.when(to != z)
        def _():
            gain_copy(to, z).wait_send()

    for copy, core_copy, numbers in (
        (m_copy, m_core, (m_order, m_order)),
        (f_copy, f_core, f_order),
    ):
        for number in numbers[0]:
            core_copy(0, number).wait_send()

            @pl.when(end < 3)
            def _():
                copy(0, number, 0, 0).wait_send()

        for number in numbers[1]:
            core_copy(1, number).wait_send()

            @pl.when((end == 1) | (end == 2))
            def _():
                copy(1, number, 0, 0).wait_send()

            @pl.when(end == 1)
            def _():
                copy(1, number, 1, 0).wait_send()


def front(
    tokens, cot, starts, live, gains, taps, bias, decay, in_proj, gates, out_proj, gate_up, down, sizes
):
    model, width, ffn_width = sizes
    slots = cot.shape[0]
    rows = 4 * slots
    dma = pltpu.SemaphoreType.DMA
    vmem = pl.BlockSpec(memory_space=pltpu.VMEM)
    anywhere = pl.BlockSpec(memory_space=pl.ANY)
    scalars = pl.BlockSpec(memory_space=pltpu.SMEM)
    window = -(-ffn_width // 128) * 128
    return pl.pallas_call(
        functools.partial(front_kernel, sizes),
        in_specs=[vmem] * 2 + [scalars] * 2 + [vmem] * 4 + [anywhere] * 5,
        out_specs=[vmem, vmem, anywhere, vmem, vmem, vmem, vmem, vmem, vmem, anywhere, vmem],
        out_shape=[
            jax.ShapeDtypeStruct((rows, model), low_type),
            jax.ShapeDtypeStruct((4, 3 * width, model + width), low_type),
            jax.ShapeDtypeStruct((3, 4 * ffn_width, model), low_type),
            jax.ShapeDtypeStruct((4, rows, 2 * width), wide),
            jax.ShapeDtypeStruct((4, rows, width), wide),
            jax.ShapeDtypeStruct((4, rows, width), low_type),
            jax.ShapeDtypeStruct((rows, width), low_type),
            jax.ShapeDtypeStruct((slots, model), wide),
            jax.ShapeDtypeStruct((4, slots, model), low_type),
            jax.ShapeDtypeStruct((4, slots, model), low_type),
            jax.ShapeDtypeStruct((8, model), wide),
        ],
        scratch_shapes=[
            pltpu.VMEM((slots, model + width), low_type),
            pltpu.VMEM((slots, model), low_type),
            pltpu.VMEM((16, model // 4), low_type),
            pltpu.VMEM((4, slots, model + width), low_type),
            pltpu.VMEM((2, model, width), low_type),
            pltpu.VMEM((2, model, window), low_type),
            pltpu.VMEM((ffn_width, model), low_type),
            pltpu.VMEM((2, window, model), low_type),
            pltpu.VMEM((4, 16, model // 4), low_type),
            pltpu.VMEM((rows, model), wide),
            pltpu.VMEM((rows, model), low_type),
        ]
        + Reduce.scratch(slots, model)
        + [
            dma((13,)),
            dma((4,)),
            dma((4,)),
            dma((2, 2, 3)),
            dma((2, 3)),
            dma((2, 3)),
            dma((2, 3)),
            dma((2, 2, 6)),
            dma((2, 6)),
            dma((2, 6)),
            dma((2, 6)),
            dma((3, 4)),
            dma((3, 4)),
            dma((6,)),
            dma((6,)),
        ],
        compiler_params=pltpu.CompilerParams(
            collective_id=3, has_side_effects=True, vmem_limit_bytes=60 * 1024 * 1024
        ),
        cost_estimate=pl.CostEstimate(
            flops=2 * rows * model * 4 * width * 3,
            bytes_accessed=6 * ffn_width * 4 * model,
            transcendentals=rows * 4 * width * 6,
        ),
        name="front",
    )(tokens, cot, starts, live, gains, taps, bias, decay, in_proj, gates, out_proj, gate_up, down)


def middle_kernel(
    sizes,
    x_hbm,
    go_hbm,
    weights_ref,
    residual_ref,
    gain_ref,
    total,
    inner_down,
    res_low,
    res_out,
    gain_out,
    part_out,
    x_ref,
    go_ref,
    held,
    lows,
    paired,
    arrived,
    part_in,
    in_x,
    in_y,
    in_pass,
    in_last,
    load_sem,
    late_send,
    late_recv,
    late_core_send,
    late_core_recv,
    core_send,
    core_recv,
    line_send,
    line_recv,
    i_send,
    i_recv,
    g_send,
    g_recv,
):
    model, ffn_width = sizes
    member = lax.axis_index("dp")
    z = lax.axis_index("shard")
    chip, core = member // 2, member % 2
    end = z + core * (3 - 2 * z)
    other = chip * 2 + 1 - core
    slots = residual_ref.shape[0]
    half = slots // 2
    hidden = 4 * ffn_width
    half_ffn = ffn_width // 2

    split = -(-2 * ffn_width // 128) * 128

    late_low = 2 * ffn_width + half_ffn
    peer_low = 3 * ffn_width + half_ffn

    def weight_load(kinds, low, high, number):
        at = pl.ds(low, high - low)
        return pltpu.make_async_copy(
            weights_ref.at[kinds, at], held.at[kinds, at], load_sem.at[number]
        )

    loads = [
        weight_load(pl.ds(0, 3), 0, split, 0),
        pltpu.make_async_copy(x_hbm, x_ref, load_sem.at[1]),
        pltpu.make_async_copy(go_hbm, go_ref, load_sem.at[2]),
        weight_load(pl.ds(0, 2), split, late_low, 3),
        weight_load(pl.ds(0, 2), 3 * ffn_width, peer_low, 4),
        weight_load(pl.ds(2, 1), split, hidden, 5),
    ]
    own_late = weight_load(pl.ds(0, 2), late_low, 3 * ffn_width, 7)

    def late_copy(kind, way, to_end):
        place = held.at[kind, pl.ds(late_low, half_ffn)]
        return remote(
            place,
            place,
            late_send.at[way, kind],
            late_recv.at[kind],
            member,
            line_place(to_end, core),
        )

    def late_core(kind):
        return remote(
            held.at[kind, pl.ds(late_low, half_ffn)],
            held.at[kind, pl.ds(peer_low, half_ffn)],
            late_core_send.at[kind],
            late_core_recv.at[kind],
            other,
            z,
        )

    @pl.when(end == 1)
    def _():
        own_late.start()

    for load in loads:
        load.start()
    enter(member, z)

    @pl.when(end == 1)
    def _():
        own_late.wait()
        for kind in range(2):
            late_copy(kind, 0, 2).start()
            late_copy(kind, 1, 0).start()
            late_core(kind).start()

    for load in loads[:3]:
        load.wait()

    def late_step(block):
        for kind in range(2):

            @pl.when((end == 2) & (block == kind + 1))
            def _():
                late_copy(kind, 0, 0).wait_recv()
                late_copy(kind, 0, 3).start()
                late_core(kind).start()

    def late_end():
        for kind in range(2):

            @pl.when((end == 0) | (end == 3))
            def _():
                late_copy(kind, 0, 0).wait_recv()
                late_core(kind).start()

        for kind in range(2):
            late_core(kind).wait_recv()

    def late_sent():
        for kind in range(2):
            late_core(kind).wait_send()

            @pl.when((end == 1) | (end == 2))
            def _():
                late_copy(kind, 0, 0).wait_send()

            @pl.when(end == 1)
            def _():
                late_copy(kind, 1, 0).wait_send()

    def block_step(low, high, block, carry):
        rows = pl.ds(pl.multiple_of(block * slots, slots), slots)
        x = x_ref[rows, :]
        grad_out = go_ref[rows, :]
        pre_gate = dot_rows(x, held[0, low:high])
        pre_up = dot_rows(x, held[1, low:high])
        active, slope = gelu_parts(pre_gate)
        ffn_low = (active * pre_up).astype(low_type)
        grad_act = dot_rows(grad_out, held[2, low:high])
        gate_low = (grad_act * pre_up * slope).astype(low_type)
        up_low = (grad_act * active).astype(low_type)
        sum_out = dot_plain(ffn_low, held[2, low:high])
        sum_in = dot_plain(gate_low, held[0, low:high]) + dot_plain(up_low, held[1, low:high])
        lows[0, rows, low:high] = gate_low
        lows[1, rows, low:high] = up_low
        lows[2, rows, low:high] = ffn_low
        if low == 0:
            late_step(block)
        else:
            sum_in = sum_in + part_in[rows, :].astype(wide)
            sum_out = sum_out + part_out[rows, :].astype(wide)
        part_in[rows, :] = sum_in.astype(low_type)
        part_out[rows, :] = sum_out.astype(low_type)
        return carry

    reduce_in = Reduce(part_in, in_x, in_y, in_pass, in_last, i_send, i_recv, member, z)
    gather = Gather(res_low.at[0], res_low, g_send, g_recv, member, z)
    middle = model // 2

    def weight_grads(kind, low, high):
        factor = go_ref if kind == 2 else x_ref
        for at in range(2):
            columns = slice(at * middle, (at + 1) * middle)
            held[kind, low:high, columns] = dot_slots(
                lows[kind, :, low:high], factor[:, columns]
            ).astype(low_type)

    def core_copy(slot, kind):
        return remote(
            held.at[kind, pl.ds((2 * slot + 1) * ffn_width, ffn_width)],
            paired.at[slot, kind],
            core_send.at[slot, kind],
            core_recv.at[slot, kind],
            other,
            z,
        )

    def chunk(number):
        return number // 2, pl.ds((number % 2) * half_ffn, half_ffn)

    def line_copy(kind, number, to_end):
        at, rows = chunk(number)
        return remote(
            paired.at[min(kind, 1), at, rows],
            arrived.at[kind, at, rows],
            line_send.at[kind, number],
            line_recv.at[kind, number],
            member,
            line_place(to_end, core),
        )

    def pair_up(slot, kind):
        core_copy(slot, kind).wait_recv()
        for number in (2 * kind, 2 * kind + 1):
            at, rows = chunk(number)
            own = held[at, pl.ds(2 * slot * ffn_width + (number % 2) * half_ffn, half_ffn)]
            paired[slot, at, rows] = add_low(own, paired[slot, at, rows])

            if slot == 0 or number < 4:

                @pl.when(end == 3)
                def _():
                    line_copy(slot, number, 2).start()

            if slot == 1 and number < 4:

                @pl.when(end == 0)
                def _():
                    line_copy(2, number, 1).start()

    def part_grads(slot, low, high):
        for kind in range(3):
            weight_grads(kind, low, high)
            core_copy(slot, kind).start()
            if kind > 0:
                pair_up(slot, kind - 1)
        pair_up(slot, 2)

    def summed(slot, kinds, number):
        at, rows = chunk(number)
        result = paired[slot, at, rows].astype(wide)
        for kind in kinds:
            result = result + arrived[kind, at, rows].astype(wide)
        return result.astype(low_type)

    def outer_step(number):
        at, rows = chunk(number)

        @pl.when((end == 2) | (end == 1))
        def _():
            line_copy(0, number, 0).wait_recv()
            paired[0, at, rows] = summed(0, (0,), number)
            line_copy(0, number, end - 1).start()

    def inner_step(number):
        at, rows = chunk(number)

        @pl.when(end == 2)
        def _():
            line_copy(1, number, 0).wait_recv()
            paired[1, at, rows] = summed(1, (1,), number)
            line_copy(1, number, 1).start()

    def out_copy(slot, number):
        at, rows = chunk(number)
        return pltpu.make_async_copy(
            paired.at[slot, at, rows], total.at[at, rows], load_sem.at[number]
        )

    def last_step(number):
        at, rows = chunk(number)

        if number < 4:

            @pl.when(end == 1)
            def _():
                line_copy(1, number, 0).wait_recv()
                line_copy(2, number, 0).wait_recv()
                paired[1, at, rows] = summed(1, (1, 2), number)
                out_copy(1, number).start()

        @pl.when(end == 0)
        def _():
            line_copy(0, number, 0).wait_recv()
            paired[0, at, rows] = summed(0, (0,), number)
            out_copy(0, number).start()

    lax.fori_loop(0, 4, functools.partial(block_step, 0, split), 0)
    part_grads(0, 0, split)
    for load in loads[3:]:
        load.wait()
    late_end()
    lax.fori_loop(0, 4, functools.partial(block_step, split, hidden), 0)
    reduce_in.begin()
    late_sent()
    part_grads(1, split, hidden)
    inner_copy = pltpu.make_async_copy(paired.at[1, 2], inner_down, load_sem.at[6])
    inner_copy.start()
    for number in range(3):
        outer_step(number)
    reduce_in.relay()
    for number in range(3, 6):
        outer_step(number)

    reduce_in.arrive()
    gain = gain_ref[1:2]
    gain_sum = jnp.zeros((1, model), wide)
    for number in range(2):
        at = slice(number * half, (number + 1) * half)
        grad = reduce_in.result(number)
        value = residual_ref[at]
        scale = lax.rsqrt(jnp.mean(value * value, axis=1, keepdims=True) + norm_eps)
        scaled = grad * gain
        gain_sum = gain_sum + jnp.sum(grad * value * scale, axis=0, keepdims=True)
        inner = jnp.mean(scaled * value, axis=1, keepdims=True)
        back = scale * scaled - value * (scale * scale * scale * inner)
        result = go_ref[at].astype(wide) + back
        res_out[at] = result
        res_low[0, at] = result.astype(low_type)
    gain_out[...] = jnp.concatenate([gain_ref[0:1], gain_sum, jnp.zeros((6, model), wide)], axis=0)
    gather.begin()
    inner_step(0)
    gather.relay()
    inner_step(1)
    inner_step(2)
    inner_step(3)
    gather.arrive()
    for number in range(6):
        last_step(number)
    inner_copy.wait()

    for sent in (reduce_in, gather):
        sent.finish()
    for slot in range(2):
        for kind in range(3):
            core_copy(slot, kind).wait_send()
    for number in range(6):

        @pl.when(end > 0)
        def _():
            line_copy(0, number, 0).wait_send()

        @pl.when(end == 0)
        def _():
            out_copy(0, number).wait()

    for number in range(4):

        @pl.when(end > 1)
        def _():
            line_copy(1, number, 0).wait_send()

        @pl.when(end == 1)
        def _():
            out_copy(1, number).wait()

        @pl.when(end == 0)
        def _():
            line_copy(2, number, 1).wait_send()


def middle(x, grad_out, weights, residual, gains):
    rows, model = x.shape
    hidden = weights.shape[1]
    ffn_width = hidden // 4
    slots = rows // 4
    dma = pltpu.SemaphoreType.DMA
    vmem = pl.BlockSpec(memory_space=pltpu.VMEM)
    anywhere = pl.BlockSpec(memory_space=pl.ANY)
    quarter = (3, ffn_width, model)
    return pl.pallas_call(
        functools.partial(middle_kernel, (model, ffn_width)),
        in_specs=[anywhere] * 3 + [vmem] * 2,
        out_specs=[anywhere] * 2 + [vmem] * 4,
        out_shape=[
            jax.ShapeDtypeStruct(quarter, low_type),
            jax.ShapeDtypeStruct(quarter[1:], low_type),
            jax.ShapeDtypeStruct((4, slots, model), low_type),
            jax.ShapeDtypeStruct((slots, model), wide),
            jax.ShapeDtypeStruct((8, model), wide),
            jax.ShapeDtypeStruct((rows, model), low_type),
        ],
        scratch_shapes=[
            pltpu.VMEM(x.shape, low_type),
            pltpu.VMEM(x.shape, low_type),
            pltpu.VMEM(weights.shape, low_type),
            pltpu.VMEM((3, rows, hidden), low_type),
            pltpu.VMEM((2,) + quarter, low_type),
            pltpu.VMEM((3,) + quarter, low_type),
            pltpu.VMEM((rows, model), low_type),
        ]
        + Reduce.scratch(slots, model)
        + [
            dma((8,)),
            dma((2, 2)),
            dma((2,)),
            dma((2,)),
            dma((2,)),
            dma((2, 3)),
            dma((2, 3)),
            dma((3, 6)),
            dma((3, 6)),
            dma((6,)),
            dma((6,)),
            dma((4,)),
            dma((4,)),
        ],
        compiler_params=pltpu.CompilerParams(
            collective_id=4, has_side_effects=True, vmem_limit_bytes=63 * 1024 * 1024
        ),
        cost_estimate=pl.CostEstimate(
            flops=2 * rows * model * hidden * 9,
            bytes_accessed=weights.size * 4 + rows * model * 16,
            transcendentals=rows * hidden,
        ),
        name="middle",
    )(x, grad_out, weights, residual, gains)


class Scatter:
    def __init__(self, sizes, member, z, send_sem, recv_sem):
        self.model, self.width, self.ffn_width, self.piece_length = sizes
        self.member, self.z = member, z
        self.chip, self.core = member // 2, member % 2
        self.owner = self.core == z // 2
        self.send_sem, self.recv_sem = send_sem, recv_sem
        self.across = self.model // 128
        rec, ffn, model = 4 * self.width, 4 * self.ffn_width, self.model
        self.gate_base = 2 * model * rec
        self.out_base = self.gate_base + 8 * self.width * self.width
        self.up_base = self.out_base + rec * model
        self.down_base = self.up_base + 2 * model * ffn
        self.rec, self.ffn = rec, ffn
        self.first_in = 0
        self.first_gate = 2 * self.across
        self.first_out = self.first_gate + 2
        self.first_small = self.first_out + 4
        self.first_up = self.first_small + 1
        self.first_down = self.first_up + 2 * self.across
        self.count = self.first_down + 6

    def in_unit(self, number, q):
        kind, at = number // self.across, number % self.across
        low = (kind * self.model + at * 128) * self.rec
        where = (
            pl.ds(pl.multiple_of(kind * self.width, self.width), self.width),
            pl.ds(pl.multiple_of(at * 128, 128), 128),
        )
        return self.first_in + number, where, low, low + 128 * self.rec

    def gate_unit(self, kind, q):
        low = self.gate_base + (kind * 4 + q) * self.width * self.width
        where = (
            pl.ds(pl.multiple_of(kind * self.width, self.width), self.width),
            pl.ds(self.model, self.width),
        )
        return self.first_gate + kind, where, low, low + self.width * self.width

    def out_unit(self, number, q):
        rows = self.width // 4
        low = self.out_base + (q * self.width + number * rows) * self.model
        where = (
            pl.ds(pl.multiple_of(2 * self.width + number * rows, rows), rows),
            pl.ds(0, self.model),
        )
        return self.first_out + number, where, low, low + rows * self.model

    def up_unit(self, number, q):
        kind, at = number // self.across, number % self.across
        low = self.up_base + (kind * self.model + at * 128) * self.ffn
        where = (kind, pl.ds(0, self.ffn_width), pl.ds(pl.multiple_of(at * 128, 128), 128))
        return self.first_up + number, where, low, low + 128 * self.ffn

    def down_unit(self, number, q):
        rows = self.ffn_width // 6
        low = self.down_base + (q * self.ffn_width + number * rows) * self.model
        where = (2, pl.ds(pl.multiple_of(number * rows, 16), rows), pl.ds(0, self.model))
        return self.first_down + number, where, low, low + rows * self.model

    def small_where(self):
        return (pl.ds(2 * self.width, 16), pl.ds(self.model, self.width))

    def copies(self, unit, source, target, q, act, flat=False):
        number, where, low, high = unit
        here = where[1:] if flat else where
        first = low // self.piece_length
        last = (high - 1) // self.piece_length
        for which, to in ((0, first), (1, last)):
            wanted = True if which == 0 else last != first

            @pl.when((to != self.member) & wanted)
            def _():
                act(
                    remote(
                        source.at[here],
                        target.at[(q,) + where],
                        self.send_sem.at[which, number],
                        self.recv_sem.at[q, number],
                        to,
                        self.z,
                    ),
                    True,
                )

            @pl.when((to == self.member) & wanted)
            def _():
                act(
                    pltpu.make_async_copy(
                        source.at[here], target.at[(q,) + where], self.recv_sem.at[q, number]
                    ),
                    False,
                )

    def each(self, unit_of, low, high, source, target, act, flat=False):
        def body(number, carry):
            self.copies(unit_of(number, self.chip), source, target, self.chip, act, flat)
            return carry

        lax.fori_loop(low, high, body, 0)

    def smalls(self, source, target, act):
        where = self.small_where()
        for to in range(8):

            @pl.when(self.member != to)
            def _():
                act(
                    remote(
                        source.at[where],
                        target.at[(self.chip,) + where],
                        self.send_sem.at[2, to],
                        self.recv_sem.at[self.chip, self.first_small],
                        to,
                        self.z,
                    ),
                    True,
                )

        act(
            pltpu.make_async_copy(
                source.at[where],
                target.at[(self.chip,) + where],
                self.recv_sem.at[self.chip, self.first_small],
            ),
            False,
        )

    def arrivals(self, unit_of, count, source, target):
        low = self.member * self.piece_length

        def body(number, carry):
            for q in range(4):
                index, where, first, last = unit_of(number, q)
                mine = (first < low + self.piece_length) & (last > low)
                here = (self.chip == q) & self.owner

                @pl.when(mine & here)
                def _():
                    pltpu.make_async_copy(
                        source.at[where], target.at[(q,) + where], self.recv_sem.at[q, index]
                    ).wait()

                @pl.when(mine & jnp.logical_not(here))
                def _():
                    remote(
                        source.at[where],
                        target.at[(q,) + where],
                        self.send_sem.at[0, index],
                        self.recv_sem.at[q, index],
                        self.member,
                        self.z,
                    ).wait_recv()

            return carry

        lax.fori_loop(0, count, body, 0)

    def small_arrivals(self, source, target):
        where = self.small_where()
        for q in range(4):
            here = (self.chip == q) & self.owner

            @pl.when(here)
            def _():
                pltpu.make_async_copy(
                    source.at[where],
                    target.at[(q,) + where],
                    self.recv_sem.at[q, self.first_small],
                ).wait()

            @pl.when(jnp.logical_not(here))
            def _():
                remote(
                    source.at[where],
                    target.at[(q,) + where],
                    self.send_sem.at[2, 0],
                    self.recv_sem.at[q, self.first_small],
                    self.member,
                    self.z,
                ).wait_recv()


def begin(copy, is_remote):
    copy.start()


def finish_send(copy, is_remote):
    if is_remote:
        copy.wait_send()


def back_kernel(
    sizes,
    x_hbm,
    res_hbm,
    starts_ref,
    w_hbm,
    p_hbm,
    state_hbm,
    low_hbm,
    ffn_ref,
    inner_hbm,
    tokens_ref,
    res_ref,
    gain_ref,
    mix_out,
    ffn_out,
    tokens_out,
    gain_out,
    x_ref,
    low_res,
    w_ref,
    p_ref,
    state_ref,
    low_ref,
    proj_grads,
    gate_acc,
    small_acc,
    grads,
    part_ref,
    paired,
    arrived,
    total,
    from_x,
    from_y,
    passing,
    last,
    inner,
    inner_seen,
    gain_part,
    gain_plane,
    gain_line,
    gain_seen,
    load_sem,
    core_send,
    core_recv,
    line_send,
    line_recv,
    plane_send,
    plane_recv,
    inner_send,
    inner_recv,
    gain_send,
    gain_recv,
    unit_send,
    unit_recv,
):
    model, width, ffn_width, piece_length = sizes
    member = lax.axis_index("dp")
    z = lax.axis_index("shard")
    chip, core = member // 2, member % 2
    end = z + core * (3 - 2 * z)
    slots = tokens_ref.shape[0]
    half = slots // 2
    other = chip * 2 + 1 - core
    scatter = Scatter(sizes, member, z, unit_send, unit_recv)

    order = (2, 0, 3, 1)
    common = [
        pltpu.make_async_copy(x_hbm, x_ref, load_sem.at[4, 0]),
        pltpu.make_async_copy(res_hbm, low_res, load_sem.at[4, 1]),
    ]
    early = [pltpu.make_async_copy(inner_hbm, inner, load_sem.at[4, 2])]

    def head_loads(head):
        return [
            pltpu.make_async_copy(source.at[head], target.at[head], load_sem.at[head, number])
            for number, (source, target) in enumerate(
                ((w_hbm, w_ref), (p_hbm, p_ref), (state_hbm, state_ref), (low_hbm, low_ref))
            )
        ]

    for copy in head_loads(order[0]) + common[1:] + early + common[:1]:
        copy.start()
    for head in order[1:]:
        for copy in head_loads(head):
            copy.start()
    enter(member, z)

    half_ffn = ffn_width // 2

    def inner_copy(kind, number, to_end):
        at = pl.ds(number * half_ffn, half_ffn)
        return remote(
            inner.at[at],
            inner_seen.at[kind, at],
            inner_send.at[kind, number],
            inner_recv.at[kind, number],
            member,
            line_place(to_end, core),
        )

    def inner_add(kinds, number):
        at = pl.ds(number * half_ffn, half_ffn)
        result = inner[at].astype(wide)
        for kind in kinds:
            inner_copy(kind, number, 0).wait_recv()
            result = result + inner_seen[kind, at].astype(wide)
        inner[at] = result.astype(low_type)

    def inner_far(number):
        @pl.when(end == 2)
        def _():
            inner_add((0,), number)
            inner_copy(0, number, 1).start()

    def inner_last():
        @pl.when(end == 1)
        def _():
            inner_add((0, 1), 0)
            inner_add((0, 1), 1)
            scatter.each(scatter.down_unit, 0, 6, inner, ffn_out, begin, True)

    for copy in early:
        copy.wait()
    for number in range(2):

        @pl.when(end == 3)
        def _():
            inner_copy(0, number, 2).start()

        @pl.when(end == 0)
        def _():
            inner_copy(1, number, 1).start()

    @pl.when(scatter.owner)
    def _():
        scatter.each(scatter.up_unit, 0, 2 * scatter.across, ffn_ref, ffn_out, begin)

    @pl.when(end == 0)
    def _():
        scatter.each(scatter.down_unit, 0, 6, ffn_ref, ffn_out, begin)

    def rows(number):
        return pl.ds(number * width, width)

    def core_copy(slot, number):
        return remote(
            grads.at[2 + slot, rows(number)],
            paired.at[slot, rows(number)],
            core_send.at[slot, number],
            core_recv.at[slot, number],
            other,
            z,
        )

    reduce = Reduce(
        part_ref, from_x, from_y, passing, last, plane_send, plane_recv, member, z
    )

    def line_copy(kind, number, source, to_end):
        return remote(
            source,
            arrived.at[kind, rows(number)],
            line_send.at[kind, number],
            line_recv.at[kind, number],
            member,
            line_place(to_end, core),
        )

    def pair_up(slot):
        for number in range(3):
            core_copy(slot, number).wait_recv()
            both = grads[slot, rows(number)].astype(wide) + paired[slot, rows(number)].astype(wide)
            paired[slot, rows(number)] = both.astype(low_type)

            @pl.when(end == 3)
            def _():
                line_copy(slot, number, paired.at[slot, rows(number)], 2).start()

            if slot == 1:

                @pl.when(end == 0)
                def _():
                    line_copy(2, number, paired.at[slot, rows(number)], 1).start()

    def summed(slot, kinds, number):
        result = paired[slot, rows(number)].astype(wide)
        for kind in kinds:
            result = result + arrived[kind, rows(number)].astype(wide)
        return result.astype(low_type)

    def on_arrival(kind, number):
        line_copy(kind, number, paired.at[0, rows(number)], 0).wait_recv()

    def outer_step(place, number):
        @pl.when(end == place)
        def _():
            on_arrival(0, number)
            paired[0, rows(number)] = summed(0, (0,), number)
            line_copy(0, number, paired.at[0, rows(number)], place - 1).start()

    def far_inner(number):
        @pl.when(end == 2)
        def _():
            on_arrival(1, number)
            paired[1, rows(number)] = summed(1, (1,), number)
            line_copy(1, number, paired.at[1, rows(number)], 1).start()

    def share(number):
        if number < 2:
            across = scatter.across
            scatter.each(
                scatter.in_unit, number * across, (number + 1) * across, total, mix_out, begin
            )
            scatter.each(scatter.gate_unit, number, number + 1, total, mix_out, begin)
        else:
            scatter.each(scatter.out_unit, 0, 4, total, mix_out, begin)
            scatter.smalls(total, mix_out, begin)

    common[1].wait()
    for turn, head in enumerate(order):
        for copy in head_loads(head):
            copy.wait()
        views = weight_views(w_ref.at[pl.ds(head, 1)], width)
        gate_acc[...] = jnp.zeros_like(gate_acc)
        small_acc[...] = jnp.zeros_like(small_acc)

        def step_block(block, carry):
            at = pl.ds(pl.multiple_of(block * slots, slots), slots)
            proj_low, grad_gates, grad_small = mixer_back_step(
                slot_position(starts_ref[at, :]),
                views,
                p_ref[head, at, :],
                state_ref[head, at, :],
                low_res[at, :],
                width,
            )
            proj_grads[at, head * 2 * width : (head + 1) * 2 * width] = proj_low
            gate_acc[...] += grad_gates
            small_acc[...] += grad_small
            return carry

        lax.fori_loop(0, 4, step_block, 0)
        if turn == 0:
            common[0].wait()
        grads[head, 0 : 2 * width, 0:model] = dot_slots(
            proj_grads[:, head * 2 * width : (head + 1) * 2 * width], x_ref[...]
        ).astype(low_type)
        grads[head, 2 * width : 3 * width, 0:model] = dot_slots(
            low_ref[head], low_res[...]
        ).astype(low_type)
        grads[head, 0:width, model:] = gate_acc[:, :width].astype(low_type)
        grads[head, width : 2 * width, model:] = gate_acc[:, width:].astype(low_type)
        grads[head, 2 * width : 3 * width, model:] = jnp.concatenate(
            [small_acc[...], jnp.zeros((width - 8, width), wide)], axis=0
        ).astype(low_type)
        if head >= 2:
            for number in range(3):
                core_copy(head - 2, number).start()
        if turn == 1:
            pair_up(0)
            inner_far(0)
        elif turn == 2:
            inner_far(1)
            outer_step(2, 0)
            outer_step(2, 1)
        elif turn == 3:
            inner_last()
            outer_step(2, 2)
            outer_step(1, 0)
            outer_step(1, 1)

    def in_block(block):
        at = slice(block * slots, (block + 1) * slots)
        result = jnp.zeros((slots, model), wide)
        for head in range(4):
            result = result + dot_plain(
                proj_grads[at, head * 2 * width : (head + 1) * 2 * width],
                w_ref[head, 0 : 2 * width, 0:model],
            )
        part_ref[at, :] = result.astype(low_type)

    for block in (3, 1, 2, 0):
        in_block(block)
        reduce.begin_block(block)
        if block == 3:
            pair_up(1)
    outer_step(1, 2)
    across = scatter.across
    scatter.arrivals(scatter.up_unit, 2 * across, ffn_ref, ffn_out)

    @pl.when(scatter.owner)
    def _():
        scatter.each(scatter.up_unit, 0, 2 * across, ffn_ref, ffn_out, finish_send)

    far_inner(0)
    far_inner(1)
    reduce.relay()

    far_inner(2)
    for number in range(3):

        @pl.when(end == 1)
        def _():
            on_arrival(1, number)
            on_arrival(2, number)
            total[rows(number)] = summed(1, (1, 2), number)

        @pl.when(end == 0)
        def _():
            on_arrival(0, number)
            total[rows(number)] = summed(0, (0,), number)

        @pl.when(scatter.owner)
        def _():
            share(number)

    reduce.arrive()
    gain = gain_ref[0:1]
    gain_sum = jnp.zeros((1, model), wide)
    for number in range(2):
        at = slice(number * half, (number + 1) * half)
        grad = reduce.result(number)
        value = tokens_ref[at].astype(wide)
        scale = lax.rsqrt(jnp.mean(value * value, axis=1, keepdims=True) + norm_eps)
        scaled = grad * gain
        gain_sum = gain_sum + jnp.sum(grad * value * scale, axis=0, keepdims=True)
        drift = jnp.mean(scaled * value, axis=1, keepdims=True)
        back = scale * scaled - value * (scale * scale * scale * drift)
        tokens_out[at] = (res_ref[at] + back).astype(low_type)
    gain_part[...] = jnp.concatenate([gain_sum, gain_ref[1:2], jnp.zeros((6, model), wide)], axis=0)

    def gain_copy():
        return remote(
            gain_part, gain_plane.at[member], gain_send.at[0], gain_recv.at[member], 7, z
        )

    @pl.when(member != 7)
    def _():
        gain_copy().start()
        gain_copy().wait_send()
        gain_out[...] = jnp.zeros_like(gain_out)

    @pl.when(member == 7)
    def _():
        result = gain_part[...]
        for source in range(7):
            remote(
                gain_part,
                gain_plane.at[source],
                gain_send.at[0],
                gain_recv.at[source],
                7,
                z,
            ).wait_recv()
            result = result + gain_plane[source]
        quarter = model // 4
        for place in range(4):
            gain_line[place] = result[:, place * quarter : (place + 1) * quarter]

        def line_gain(place, slot):
            return remote(
                gain_line.at[place],
                gain_seen.at[slot],
                gain_send.at[1 + place],
                gain_recv.at[8 + slot],
                7,
                place,
            )

        for place in range(4):

            @pl.when(place != z)
            def _():
                line_gain(place, z).start()

        gain_out[...] = gain_line[z]
        for place in range(4):

            @pl.when(place != z)
            def _():
                line_gain(place, place).wait_recv()
                gain_out[...] += gain_seen[place]
                line_gain(place, z).wait_send()

    scatter.arrivals(scatter.down_unit, 6, ffn_ref, ffn_out)
    scatter.arrivals(scatter.in_unit, 2 * across, total, mix_out)
    scatter.arrivals(scatter.gate_unit, 2, total, mix_out)
    scatter.arrivals(scatter.out_unit, 4, total, mix_out)
    scatter.small_arrivals(total, mix_out)

    @pl.when(scatter.owner)
    def _():
        scatter.each(scatter.down_unit, 0, 6, ffn_ref, ffn_out, finish_send)
        scatter.each(scatter.in_unit, 0, 2 * across, total, mix_out, finish_send)
        scatter.each(scatter.gate_unit, 0, 2, total, mix_out, finish_send)
        scatter.each(scatter.out_unit, 0, 4, total, mix_out, finish_send)
        scatter.smalls(total, mix_out, finish_send)

    reduce.finish()
    for number in range(2):

        @pl.when(end >= 2)
        def _():
            inner_copy(0, number, 0).wait_send()

        @pl.when(end == 0)
        def _():
            inner_copy(1, number, 0).wait_send()

    for slot in range(2):
        for number in range(3):
            core_copy(slot, number).wait_send()
    for number in range(3):

        @pl.when(end > 0)
        def _():
            line_copy(0, number, paired.at[0, rows(number)], 0).wait_send()

        @pl.when(end > 1)
        def _():
            line_copy(1, number, paired.at[1, rows(number)], 0).wait_send()

        @pl.when(end == 0)
        def _():
            line_copy(2, number, paired.at[1, rows(number)], 1).wait_send()


def back(
    x,
    res,
    starts,
    weights,
    saved,
    ffn,
    inner,
    tokens,
    residual_grad,
    gains,
    piece_length,
    width,
):
    model = tokens.shape[1]
    ffn_width = ffn.shape[1]
    sizes = (model, width, ffn_width, piece_length)
    slots = tokens.shape[0]
    block = weights.shape[1:]
    count = Scatter(sizes, 0, 0, None, None).count
    dma = pltpu.SemaphoreType.DMA
    vmem = pl.BlockSpec(memory_space=pltpu.VMEM)
    anywhere = pl.BlockSpec(memory_space=pl.ANY)
    held = lambda value: pltpu.VMEM(value.shape, value.dtype)
    return pl.pallas_call(
        functools.partial(back_kernel, sizes),
        in_specs=[anywhere, anywhere, vmem] + [anywhere] * 6 + [vmem] * 3,
        out_specs=[anywhere, anywhere, vmem, vmem],
        out_shape=[
            jax.ShapeDtypeStruct(weights.shape, low_type),
            jax.ShapeDtypeStruct((4,) + ffn.shape, low_type),
            jax.ShapeDtypeStruct(tokens.shape, low_type),
            jax.ShapeDtypeStruct((8, model // 4), wide),
        ],
        scratch_shapes=[held(x), held(res), held(weights)]
        + [held(value) for value in saved]
        + [
            pltpu.VMEM((4 * slots, 8 * width), low_type),
            pltpu.VMEM((width, 2 * width), wide),
            pltpu.VMEM((8, width), wide),
            pltpu.VMEM(weights.shape, low_type),
            pltpu.VMEM((4 * slots, model), low_type),
            pltpu.VMEM((2,) + block, low_type),
            pltpu.VMEM((3,) + block, low_type),
            pltpu.VMEM(block, low_type),
        ]
        + Reduce.scratch(slots, model)
        + [
            held(inner),
            pltpu.VMEM((2,) + inner.shape, low_type),
            pltpu.VMEM((8, model), wide),
            pltpu.VMEM((8, 8, model), wide),
            pltpu.VMEM((4, 8, model // 4), wide),
            pltpu.VMEM((4, 8, model // 4), wide),
            dma((5, 4)),
            dma((2, 3)),
            dma((2, 3)),
            dma((3, 3)),
            dma((3, 3)),
            dma((6,)),
            dma((6,)),
            dma((2, 2)),
            dma((2, 2)),
            dma((5,)),
            dma((12,)),
            dma((3, count)),
            dma((4, count)),
        ],
        compiler_params=pltpu.CompilerParams(
            collective_id=2, has_side_effects=True, vmem_limit_bytes=60 * 1024 * 1024
        ),
        cost_estimate=pl.CostEstimate(
            flops=weights.size * 4 * slots * 4, bytes_accessed=weights.size * 8, transcendentals=0
        ),
        name="back",
    )(
        x,
        res,
        starts,
        weights,
        *saved,
        ffn,
        inner,
        tokens,
        residual_grad,
        gains,
    )


def adam_kernel(
    sizes,
    mix_hbm,
    ffn_hbm,
    gain_ref,
    master_ref,
    first_ref,
    second_ref,
    piece_ref,
    new_master_ref,
    new_first_ref,
    new_second_ref,
    rows_ref,
    bias_ref,
    grad,
    mix_ref,
    ffn_ref,
    load_sem,
):
    model, width, ffn_width, piece_length, lines, margin = sizes
    member = lax.axis_index("dp")
    step = pl.program_id(0)
    lead = 128
    start_row = (member * piece_length) // lead
    offset = (member * piece_length) % lead
    tiles_in = 4 * width // lead
    tiles_ffn = 4 * ffn_width // lead
    tiles_model = model // lead

    def needed(first, last):
        low = member * piece_length
        return (first < low + piece_length) & (last > low)

    up_first = 2 * model * 4 * width + 8 * width * width + 4 * width * model
    whole_mix = pltpu.make_async_copy(mix_hbm, mix_ref, load_sem.at[0])
    small = (pl.ds(0, 4), pl.ds(2 * width, 16), pl.ds(model, width))
    small_mix = pltpu.make_async_copy(mix_hbm.at[small], mix_ref.at[small], load_sem.at[1])
    need_mix = needed(0, up_first)
    kinds = [
        (
            needed(
                up_first + kind * 4 * ffn_width * model,
                up_first + (kind + 1) * 4 * ffn_width * model,
            ),
            pltpu.make_async_copy(
                ffn_hbm.at[:, kind], ffn_ref.at[:, kind], load_sem.at[2 + kind]
            ),
        )
        for kind in range(3)
    ]

    @pl.when((step == 0) & need_mix)
    def _():
        whole_mix.start()

    @pl.when((step == 0) & jnp.logical_not(need_mix))
    def _():
        small_mix.start()

    for wanted, copy in kinds:

        @pl.when((step == 0) & wanted)
        def _():
            copy.start()

    @pl.when(step == 0)
    def _():
        def clear(number, carry):
            grad[pl.ds(pl.multiple_of(number * 256, 256), 256), :] = jnp.zeros((256, lead), wide)
            return carry

        lax.fori_loop(0, grad.shape[0] // 256, clear, 0)

        @pl.when(need_mix)
        def _():
            whole_mix.wait()

        @pl.when(jnp.logical_not(need_mix))
        def _():
            small_mix.wait()

        for wanted, copy in kinds:

            @pl.when(wanted)
            def _():
                copy.wait()

        def place(row, count, body):
            low = member * piece_length

            @pl.when((row * lead < low + piece_length) & ((row + count) * lead > low))
            def _():
                body(row - start_row + margin)

        base = 0

        def in_unit(number, carry):
            kind = number // tiles_model
            at = number % tiles_model

            def body(to):
                for q in range(4):
                    tile = mix_ref[
                        q,
                        pl.ds(pl.multiple_of(kind * width, width), width),
                        pl.ds(pl.multiple_of(at * lead, lead), lead),
                    ].astype(wide)
                    grad[pl.ds(to + q, lead, stride=tiles_in), :] = tile.T

            place((kind * model + at * lead) * tiles_in, lead * tiles_in, body)
            return carry

        lax.fori_loop(0, 2 * tiles_model, in_unit, 0)
        base = 2 * model * tiles_in

        def gate_body(number, carry):
            kind = number // 4
            q = number % 4

            def body(to):
                grad[pl.ds(to, width), :] = mix_ref[
                    q, pl.ds(pl.multiple_of(kind * width, width), width), model:
                ].astype(wide)

            place(2 * model * tiles_in + number * width, width, body)
            return carry

        lax.fori_loop(0, 8, gate_body, 0)
        base = base + 8 * width
        out_base = base

        quarter = width // 4

        def out_unit(number, carry):
            q = number // 4
            part = number % 4

            def body(to):
                for at in range(tiles_model):
                    grad[pl.ds(to + at, quarter, stride=tiles_model), :] = mix_ref[
                        q,
                        pl.ds(pl.multiple_of(2 * width + part * quarter, quarter), quarter),
                        at * lead : (at + 1) * lead,
                    ].astype(wide)

            place(out_base + number * quarter * tiles_model, quarter * tiles_model, body)
            return carry

        lax.fori_loop(0, 16, out_unit, 0)
        base = base + 4 * width * tiles_model
        up_base = base

        def up_unit(number, carry):
            kind = number // tiles_model
            at = number % tiles_model
            columns = pl.ds(pl.multiple_of(at * lead, lead), lead)

            def body(to):
                for tile in range(tiles_ffn):
                    found = []
                    row = tile * lead
                    while row < (tile + 1) * lead:
                        q = row // ffn_width
                        last = min((q + 1) * ffn_width, (tile + 1) * lead)
                        found.append(
                            ffn_ref[
                                q,
                                kind,
                                row - q * ffn_width : last - q * ffn_width,
                                columns,
                            ].astype(wide)
                        )
                        row = last
                    block = found[0] if len(found) == 1 else jnp.concatenate(found, axis=0)
                    grad[pl.ds(to + tile, lead, stride=tiles_ffn), :] = block.T

            place(up_base + (kind * model + at * lead) * tiles_ffn, lead * tiles_ffn, body)
            return carry

        lax.fori_loop(0, 2 * tiles_model, up_unit, 0)
        base = base + 2 * model * tiles_ffn
        down_base = base
        sixth = ffn_width // 6

        def down_unit(number, carry):
            q = number // 6
            part = number % 6

            def body(to):
                for at in range(tiles_model):
                    grad[pl.ds(to + at, sixth, stride=tiles_model), :] = ffn_ref[
                        q,
                        2,
                        pl.ds(pl.multiple_of(part * sixth, 16), sixth),
                        at * lead : (at + 1) * lead,
                    ].astype(wide)

            place(down_base + number * sixth * tiles_model, sixth * tiles_model, body)
            return carry

        lax.fori_loop(0, 24, down_unit, 0)
        small_base = base + 4 * ffn_width * tiles_model
        smalls = [
            mix_ref[q, 2 * width : 2 * width + 16, model:].astype(wide)
            for q in range(4)
        ]

        def small_body(to):
            for q in range(4):
                grad[pl.ds(to + q, 8, stride=tiles_in), :] = smalls[q][:8]
            for number in range(6):
                kind, at = number // 3, number % 3
                grad[pl.ds(to + 8 * tiles_in + number, 1), :] = gain_ref[
                    kind : kind + 1, at * lead : (at + 1) * lead
                ]

        place(small_base, 8 * tiles_in + 6, small_body)
        bias_ref[...] = jnp.concatenate([small[5:7] for small in smalls], axis=1)

    row = margin + step * lines
    shift = (lead - offset) % lead
    here = pltpu.roll(grad[pl.ds(row, lines), :], shift, 1)
    after = pltpu.roll(grad[pl.ds(row + 1, lines), :], shift, 1)
    lane = lax.broadcasted_iota(jnp.int32, (lines, lead), 1)
    piece = jnp.where(lane < lead - offset, here, after).reshape(1, lines * lead)
    piece_ref[...] = piece
    new_first = beta_one * first_ref[...] + (1.0 - beta_one) * piece
    new_second = beta_two * second_ref[...] + (1.0 - beta_two) * piece * piece
    master = master_ref[...]
    new_master = master - learn_rate * (
        new_first / corr_one / (jnp.sqrt(new_second / corr_two) + adam_eps)
        + weight_decay * master
    )
    new_first_ref[...] = new_first
    new_second_ref[...] = new_second
    new_master_ref[...] = new_master
    rows_ref[0] = new_master.reshape(lines, lead).astype(low_type)


def adam(mix, ffn, gains, master, first, second, sizes, chunks):
    model, width, ffn_width = sizes
    piece_length = master.shape[1]
    lines = -(-piece_length // (chunks * 128 * 16)) * 16
    block = lines * 128
    margin = 1536
    rows = -(-(2 * margin + chunks * lines + 8) // 256) * 256
    packed = jax.ShapeDtypeStruct(master.shape, wide)
    chunk_spec = pl.BlockSpec((1, block), lambda s: (0, s))
    once = lambda shape: pl.BlockSpec(
        shape, lambda s: (0,) * len(shape), pipeline_mode=pl.Buffered(1)
    )
    return pl.pallas_call(
        functools.partial(
            adam_kernel, (model, width, ffn_width, piece_length, lines, margin)
        ),
        grid=(chunks,),
        in_specs=[pl.BlockSpec(memory_space=pl.ANY)] * 2 + [once(gains.shape)] + [chunk_spec] * 3,
        out_specs=[chunk_spec] * 4
        + [
            pl.BlockSpec((1, lines, 128), lambda s: (s, 0, 0)),
            pl.BlockSpec((2, 4 * width), lambda s: (0, 0)),
        ],
        out_shape=[packed] * 4
        + [
            jax.ShapeDtypeStruct((chunks, lines, 128), low_type),
            jax.ShapeDtypeStruct((2, 4 * width), wide),
        ],
        scratch_shapes=[
            pltpu.VMEM((rows, 128), wide),
            pltpu.VMEM(mix.shape, low_type),
            pltpu.VMEM(ffn.shape, low_type),
            pltpu.SemaphoreType.DMA((5,)),
        ],
        compiler_params=pltpu.CompilerParams(vmem_limit_bytes=48 * 1024 * 1024),
        cost_estimate=pl.CostEstimate(
            flops=20 * piece_length,
            bytes_accessed=40 * piece_length,
            transcendentals=piece_length,
        ),
        name="adam",
    )(mix, ffn, gains, master, first, second)


def spread_kernel(
    own_ref,
    part_hbm,
    residual_ref,
    mask_ref,
    weights_ref,
    block_out,
    held,
    spread,
    part,
    from_x,
    from_y,
    passing,
    last,
    load_sem,
    send_sem,
    recv_sem,
    plane_send,
    plane_recv,
):
    chunks, lines, lead = own_ref.shape
    member = lax.axis_index("dp")
    z = lax.axis_index("shard")
    step = pl.program_id(0)
    reduce = Reduce(part, from_x, from_y, passing, last, plane_send, plane_recv, member, z)
    part_load = pltpu.make_async_copy(part_hbm, part, load_sem.at[chunks])

    def copy_to(origin, chunk, side, to):
        return remote(
            held.at[origin, chunk],
            held.at[origin, chunk],
            send_sem.at[side, origin, chunk],
            recv_sem.at[origin, chunk],
            member,
            to,
        )

    def own_load(chunk):
        return pltpu.make_async_copy(own_ref.at[chunk], held.at[z, chunk], load_sem.at[chunk])

    def pass_on(origin, chunk, right):
        copy_to(origin, chunk, 0, z).wait_recv()
        if right:

            @pl.when(z < 3)
            def _():
                copy_to(origin, chunk, 0, z + 1).start()
        else:

            @pl.when(z > 0)
            def _():
                copy_to(origin, chunk, 1, z - 1).start()

    @pl.when(step == 0)
    def _():
        for chunk in range(chunks):
            own_load(chunk).start()
        part_load.start()
        barrier = pltpu.get_barrier_semaphore()
        for to in (reduce.to_x, reduce.to_y):
            pl.semaphore_signal(
                barrier, inc=1, device_id=(to, z), device_id_type=pl.DeviceIdType.MESH
            )

        @pl.when(z > 0)
        def _():
            pl.semaphore_signal(
                barrier, inc=1, device_id=(member, z - 1), device_id_type=pl.DeviceIdType.MESH
            )

        @pl.when(z < 3)
        def _():
            pl.semaphore_signal(
                barrier, inc=1, device_id=(member, z + 1), device_id_type=pl.DeviceIdType.MESH
            )

        @pl.when((z == 0) | (z == 3))
        def _():
            pl.semaphore_wait(barrier, 3)

        @pl.when((z > 0) & (z < 3))
        def _():
            pl.semaphore_wait(barrier, 4)

        def send_own(chunk, carry):
            own_load(chunk).wait()

            @pl.when(z < 3)
            def _():
                copy_to(z, chunk, 0, z + 1).start()

            @pl.when(z > 0)
            def _():
                copy_to(z, chunk, 1, z - 1).start()

            return carry

        lax.fori_loop(0, chunks, send_own, 0)
        part_load.wait()
        reduce.begin()

        def near(chunk, carry):
            @pl.when(z > 0)
            def _():
                pass_on(z - 1, chunk, True)

            @pl.when(z < 3)
            def _():
                pass_on(z + 1, chunk, False)

            return carry

        lax.fori_loop(0, chunks, near, 0)
        reduce.relay()

    @pl.when(step == 1)
    def _():
        reduce.arrive()
        live = quarters(mask_ref, (2 * reduce.half, 128))[:, 0:1].astype(wide)
        half = reduce.half
        for number in range(2):
            at = slice(number * half, (number + 1) * half)
            block_out[at] = (live[at] * (residual_ref[at] + reduce.result(number))).astype(low_type)
        reduce.finish()

    @pl.when(z >= 2)
    def _():
        pass_on(z - 2, step, True)

    @pl.when(z <= 1)
    def _():
        pass_on(z + 2, step, False)

    @pl.when(z == 3)
    def _():
        copy_to(0, step, 0, z).wait_recv()

    @pl.when(z == 0)
    def _():
        copy_to(3, step, 0, z).wait_recv()

    for origin in range(4):
        spread[origin * lines : (origin + 1) * lines, :] = held[origin, step].astype(wide)

    def line(number, carry):
        weights_ref[:, pl.ds(pl.multiple_of(number * lead, lead), lead)] = spread[
            pl.ds(number, 4, stride=lines), :
        ].astype(low_type)
        return carry

    lax.fori_loop(0, lines, line, 0, unroll=8)

    @pl.when(step == chunks - 1)
    def _():
        for origin in range(4):

            def finish(chunk, carry):
                @pl.when((origin <= z) & (z < 3))
                def _():
                    copy_to(origin, chunk, 0, z).wait_send()

                @pl.when((origin >= z) & (z > 0))
                def _():
                    copy_to(origin, chunk, 1, z).wait_send()

                return carry

            lax.fori_loop(0, chunks, finish, 0)


def spread_weights(own, part, residual, mask, piece_length):
    chunks, lines, lead = own.shape
    slots, model = residual.shape
    once = lambda value: pl.BlockSpec(
        value.shape, lambda s: (0, 0), pipeline_mode=pl.Buffered(1)
    )
    return pl.pallas_call(
        spread_kernel,
        grid=(chunks,),
        in_specs=[pl.BlockSpec(memory_space=pl.ANY)] * 2 + [
            once(residual),
            pl.BlockSpec(memory_space=pltpu.SMEM),
        ],
        out_specs=[pl.BlockSpec((4, lines * lead), lambda s: (0, s)), once(residual)],
        out_shape=[
            jax.ShapeDtypeStruct((4, piece_length), low_type),
            jax.ShapeDtypeStruct(residual.shape, low_type),
        ],
        scratch_shapes=[
            pltpu.VMEM((4, chunks, lines, lead), low_type),
            pltpu.VMEM((4 * lines, lead), wide),
            pltpu.VMEM(part.shape, low_type),
        ]
        + Reduce.scratch(slots, model)
        + [
            pltpu.SemaphoreType.DMA((chunks + 1,)),
            pltpu.SemaphoreType.DMA((2, 4, chunks)),
            pltpu.SemaphoreType.DMA((4, chunks)),
            pltpu.SemaphoreType.DMA((6,)),
            pltpu.SemaphoreType.DMA((6,)),
        ],
        compiler_params=pltpu.CompilerParams(
            collective_id=1, has_side_effects=True, vmem_limit_bytes=32 * 1024 * 1024
        ),
        cost_estimate=pl.CostEstimate(
            flops=4 * piece_length, bytes_accessed=16 * piece_length, transcendentals=0
        ),
        name="spread",
    )(own, part, residual, mask)


def group_body(
    tokens,
    cotangent,
    seq_start,
    live_mask,
    input_proj,
    gate_blocks,
    output_proj,
    ffn_gate_up,
    ffn_down,
    conv_taps,
    gate_bias,
    decay_param,
    norm_gains,
    master_shard,
    first_moment,
    second_moment,
):
    slots, model = tokens.shape
    slice_rec = input_proj.shape[2]
    slice_ffn = ffn_down.shape[0]
    width = slice_rec // 4
    ffn_width = slice_ffn // 4
    piece_length = master_shard.shape[1]
    (
        mix_in,
        mix_weights,
        ffn_weights,
        saved_p,
        saved_state,
        saved_low,
        all_starts,
        residual,
        ffn_in,
        all_grad_out,
        gains,
    ) = front(
        tokens,
        cotangent,
        seq_start,
        live_mask,
        norm_gains,
        conv_taps,
        gate_bias,
        decay_param[None],
        input_proj,
        gate_blocks,
        output_proj,
        ffn_gate_up,
        ffn_down,
        (model, width, ffn_width),
    )
    ffn_in = ffn_in.reshape(4 * slots, model)
    all_grad_out = all_grad_out.reshape(4 * slots, model)
    sum_ffn, inner_down, res_low, grad_residual, gain_sums, ffn_part = middle(
        ffn_in, all_grad_out, ffn_weights, residual, gains
    )
    four_mix, four_ffn, tokens_grad, gain_total = back(
        mix_in,
        res_low.reshape(4 * slots, model),
        all_starts,
        mix_weights,
        (saved_p, saved_state, saved_low),
        sum_ffn,
        inner_down,
        tokens,
        grad_residual,
        gain_sums,
        piece_length,
        width,
    )
    piece, new_master, new_first, new_second, rows, bias_total = adam(
        four_mix,
        four_ffn,
        gain_total,
        master_shard,
        first_moment,
        second_moment,
        (model, width, ffn_width),
        8,
    )
    new_weights, block_out = spread_weights(
        rows,
        ffn_part,
        residual,
        live_mask,
        piece_length,
    )
    return (
        block_out,
        tokens_grad,
        piece,
        new_master,
        new_first,
        new_second,
        new_weights,
        bias_total,
    )


def rms_scale(values, gain):
    return values * lax.rsqrt(jnp.mean(values * values, axis=-1, keepdims=True) + norm_eps) * gain


def conv_mix(signal, taps, position):
    result = taps[-1] + taps[0] * signal
    for shift_by in range(1, taps.shape[0] - 1):
        moved = jnp.pad(signal, ((shift_by, 0), (0, 0)))[:-shift_by]
        result = result + taps[shift_by] * jnp.where((position >= shift_by)[:, None], moved, 0.0)
    return result


def combine_steps(earlier, later):
    decay_first, value_first = earlier
    decay_second, value_second = later
    return (decay_first * decay_second, decay_second * value_first + value_second)


def recurrence(logits, signal, branch, bias_term, decay_term, position):
    row_count = signal.shape[0]
    recur_gate = jax.nn.sigmoid(logits[0].reshape(row_count, -1) + bias_term[0])
    input_gate = jax.nn.sigmoid(logits[1].reshape(row_count, -1) + bias_term[1])
    log_decay = -gate_scale * recur_gate * jax.nn.softplus(-decay_term)
    decay_rate = jnp.where((position > 0)[:, None], jnp.exp(log_decay), 0.0)
    drive_term = jnp.sqrt(-jnp.expm1(2.0 * log_decay)) * input_gate * signal
    states = lax.associative_scan(combine_steps, (decay_rate, drive_term), axis=0)[1]
    return states * jax.nn.gelu(branch)


def gated_gelu(ffn_pre):
    return jax.nn.gelu(ffn_pre[0]) * ffn_pre[1]


def mixer_forward(
    mix_in, input_proj, gate_blocks, output_proj, conv_taps, gate_bias, decay_param, position
):
    projected = jnp.einsum("sd,kdr->ksr", mix_in, input_proj, preferred_element_type=jnp.float32)
    conv_out, conv_pull = jax.vjp(
        lambda signal, taps: conv_mix(signal, taps, position), projected[0], conv_taps
    )
    row_count = conv_out.shape[0]
    conv_low = conv_out.astype(jnp.bfloat16).reshape(
        row_count, gate_blocks.shape[1], gate_blocks.shape[2]
    )
    gate_logits = jnp.einsum(
        "shb,khbc->kshc", conv_low, gate_blocks, preferred_element_type=jnp.float32
    )
    mixed, mix_pull = jax.vjp(
        lambda logits, signal, branch, bias_term, decay_term: recurrence(
            logits, signal, branch, bias_term, decay_term, position
        ),
        gate_logits,
        conv_out,
        projected[1],
        gate_bias,
        decay_param,
    )
    mixed_low = mixed.astype(jnp.bfloat16)
    partial_out = jnp.dot(mixed_low, output_proj, preferred_element_type=jnp.float32)
    return (partial_out, (conv_pull, conv_low, mix_pull, mixed_low))


def mixer_backward(grad_out_low, mix_in, saved, input_proj, gate_blocks, output_proj):
    conv_pull, conv_low, mix_pull, mixed_low = saved
    grad_output_proj = jnp.einsum(
        "sr,sd->rd", mixed_low, grad_out_low, preferred_element_type=jnp.float32
    )
    grad_mixed = jnp.einsum(
        "sd,rd->sr", grad_out_low, output_proj, preferred_element_type=jnp.float32
    )
    grad_logits, grad_conv_direct, grad_branch, grad_bias, grad_decay = mix_pull(grad_mixed)
    logits_low = grad_logits.astype(jnp.bfloat16)
    grad_blocks = jnp.einsum(
        "shb,kshc->khbc", conv_low, logits_low, preferred_element_type=jnp.float32
    )
    grad_conv_gates = jnp.einsum(
        "kshc,khbc->shb", logits_low, gate_blocks, preferred_element_type=jnp.float32
    )
    grad_signal, grad_taps = conv_pull(
        grad_conv_direct + grad_conv_gates.reshape(grad_conv_direct.shape)
    )
    proj_low = jnp.stack([grad_signal, grad_branch]).astype(jnp.bfloat16)
    grad_input_proj = jnp.einsum(
        "sd,ksr->kdr", mix_in, proj_low, preferred_element_type=jnp.float32
    )
    grad_mix_in = jnp.einsum(
        "ksr,kdr->sd", proj_low, input_proj, preferred_element_type=jnp.float32
    )
    return (
        grad_mix_in,
        (grad_input_proj, grad_blocks, grad_output_proj, grad_taps, grad_bias, grad_decay),
    )


def ffn_forward(ffn_in_low, ffn_gate_up, ffn_down):
    ffn_pre = jnp.einsum("sd,kdf->ksf", ffn_in_low, ffn_gate_up, preferred_element_type=jnp.float32)
    ffn_act, ffn_pull = jax.vjp(gated_gelu, ffn_pre)
    ffn_low = ffn_act.astype(jnp.bfloat16)
    partial_ffn = jnp.dot(ffn_low, ffn_down, preferred_element_type=jnp.float32)
    return (partial_ffn, (ffn_pull, ffn_low))


def ffn_backward(grad_low, ffn_in_low, saved, ffn_gate_up, ffn_down):
    ffn_pull, ffn_low = saved
    grad_down = jnp.einsum("sf,sd->fd", ffn_low, grad_low, preferred_element_type=jnp.float32)
    grad_act = jnp.einsum("sd,fd->sf", grad_low, ffn_down, preferred_element_type=jnp.float32)
    grad_pre = ffn_pull(grad_act)[0]
    pre_low = grad_pre.astype(jnp.bfloat16)
    grad_gate_up = jnp.einsum(
        "sd,ksf->kdf", ffn_in_low, pre_low, preferred_element_type=jnp.float32
    )
    grad_ffn_in = jnp.einsum(
        "ksf,kdf->sd", pre_low, ffn_gate_up, preferred_element_type=jnp.float32
    )
    return (grad_ffn_in, grad_gate_up, grad_down)


def body(
    tokens,
    cotangent,
    seq_start,
    live_mask,
    input_proj,
    gate_blocks,
    output_proj,
    ffn_gate_up,
    ffn_down,
    conv_taps,
    gate_bias,
    decay_param,
    norm_gains,
    master_shard,
    first_moment,
    second_moment,
):
    slot_count = tokens.shape[0]
    position = jnp.arange(slot_count, dtype=jnp.int32) - seq_start
    mask_rows = live_mask.astype(jnp.float32)[:, None]
    stream = tokens.astype(jnp.float32)
    grad_stream = cotangent.astype(jnp.float32) * mask_rows
    shards = (
        input_proj,
        gate_blocks,
        output_proj,
        ffn_gate_up,
        ffn_down,
        conv_taps,
        gate_bias,
        decay_param,
        norm_gains,
    )
    (
        full_in,
        full_blocks,
        full_out,
        full_up,
        full_down,
        full_taps,
        full_bias,
        full_decay,
        full_gains,
    ) = (
        lax.all_gather(shards[0], "shard", axis=2, tiled=True),
        lax.all_gather(shards[1], "shard", axis=1, tiled=True),
        lax.all_gather(shards[2], "shard", axis=0, tiled=True),
        lax.all_gather(shards[3], "shard", axis=2, tiled=True),
        lax.all_gather(shards[4], "shard", axis=0, tiled=True),
        lax.all_gather(shards[5], "shard", axis=1, tiled=True),
        lax.all_gather(shards[6], "shard", axis=1, tiled=True),
        lax.all_gather(shards[7], "shard", axis=0, tiled=True),
        lax.all_gather(shards[8], "shard", axis=1, tiled=True),
    )
    gains = full_gains.astype(jnp.float32)
    normed, norm_pull = jax.vjp(rms_scale, stream, gains[0])
    mix_in = normed.astype(jnp.bfloat16)
    mix_out, mix_saved = mixer_forward(
        mix_in,
        full_in,
        full_blocks,
        full_out,
        full_taps.astype(jnp.float32),
        full_bias.astype(jnp.float32),
        full_decay.astype(jnp.float32),
        position,
    )
    residual = stream + mix_out
    normed_two, second_pull = jax.vjp(rms_scale, residual, gains[1])
    ffn_in_low = normed_two.astype(jnp.bfloat16)
    ffn_result, ffn_saved = ffn_forward(ffn_in_low, full_up, full_down)
    block_out = (mask_rows * (residual + ffn_result)).astype(jnp.bfloat16)
    grad_ffn_in, grad_up, grad_down = ffn_backward(
        grad_stream.astype(jnp.bfloat16), ffn_in_low, ffn_saved, full_up, full_down
    )
    grad_norm_two, grad_gain_two = second_pull(grad_ffn_in)
    grad_residual = grad_stream + grad_norm_two
    grad_mix_in, mix_grads = mixer_backward(
        grad_residual.astype(jnp.bfloat16), mix_in, mix_saved, full_in, full_blocks, full_out
    )
    grad_norm_one, grad_gain_one = norm_pull(grad_mix_in)
    tokens_grad = (grad_residual + grad_norm_one).astype(jnp.bfloat16)
    grads = (
        mix_grads[0],
        mix_grads[1],
        mix_grads[2],
        grad_up,
        grad_down,
        mix_grads[3],
        mix_grads[4],
        mix_grads[5],
        jnp.stack([grad_gain_one, grad_gain_two]),
    )
    summed = (
        lax.psum_scatter(
            grads[0].astype(jnp.bfloat16), "shard", scatter_dimension=2, tiled=True
        ).astype(jnp.float32),
        lax.psum_scatter(
            grads[1].astype(jnp.bfloat16), "shard", scatter_dimension=1, tiled=True
        ).astype(jnp.float32),
        lax.psum_scatter(
            grads[2].astype(jnp.bfloat16), "shard", scatter_dimension=0, tiled=True
        ).astype(jnp.float32),
        lax.psum_scatter(
            grads[3].astype(jnp.bfloat16), "shard", scatter_dimension=2, tiled=True
        ).astype(jnp.float32),
        lax.psum_scatter(
            grads[4].astype(jnp.bfloat16), "shard", scatter_dimension=0, tiled=True
        ).astype(jnp.float32),
        lax.psum_scatter(
            grads[5].astype(jnp.bfloat16), "shard", scatter_dimension=1, tiled=True
        ).astype(jnp.float32),
        lax.psum_scatter(
            grads[6].astype(jnp.bfloat16), "shard", scatter_dimension=1, tiled=True
        ).astype(jnp.float32),
        lax.psum_scatter(
            grads[7].astype(jnp.bfloat16), "shard", scatter_dimension=0, tiled=True
        ).astype(jnp.float32),
        lax.psum_scatter(
            grads[8].astype(jnp.bfloat16), "shard", scatter_dimension=1, tiled=True
        ).astype(jnp.float32),
    )
    flat = jnp.concatenate([member.reshape(1, -1) for member in summed], axis=1)
    piece = lax.psum_scatter(flat, "dp", scatter_dimension=1, tiled=True)
    bias_total = lax.psum(summed[6], "dp")
    new_first = beta_one * first_moment + (1.0 - beta_one) * piece
    new_second = beta_two * second_moment + (1.0 - beta_two) * piece * piece
    new_master = master_shard - learn_rate * (
        new_first / corr_one / (jnp.sqrt(new_second / corr_two) + adam_eps)
        + weight_decay * master_shard
    )
    new_weights = lax.all_gather(new_master.astype(jnp.bfloat16), "shard", axis=0, tiled=True)
    return (
        block_out,
        tokens_grad,
        piece,
        new_master,
        new_first,
        new_second,
        new_weights,
        bias_total,
    )


def solution(mesh):
    fits = mesh.shape["dp"] == 8 and mesh.shape["shard"] == 4
    placed = (
        P(("dp", "shard"), None),
        P(("dp", "shard"), None),
        P(("dp", "shard")),
        P(("dp", "shard")),
        P(None, None, "shard"),
        P(None, "shard", None, None),
        P("shard", None),
        P(None, None, "shard"),
        P("shard", None),
        P(None, "shard"),
        P(None, "shard"),
        P("shard"),
        P(None, "shard"),
        P("shard", "dp"),
        P("shard", "dp"),
        P("shard", "dp"),
    )
    return jax.shard_map(
        group_body if fits else body,
        mesh=mesh,
        in_specs=placed,
        out_specs=(
            P(("dp", "shard"), None),
            P(("dp", "shard"), None),
            P("shard", "dp"),
            P("shard", "dp"),
            P("shard", "dp"),
            P("shard", "dp"),
            P(None, "dp"),
            P(None, "shard"),
        ),
        check_vma=False,
    )
```

```python
import functools
import jax
import jax.numpy as jnp
from jax import lax
from jax.experimental import pallas as pl
from jax.experimental.pallas import tpu as pltpu
from jax.sharding import PartitionSpec as P

norm_eps = 1e-06
gate_scale = 8.0
beta_one = 0.9
beta_two = 0.95
learn_rate = 0.01
weight_decay = 0.1
adam_eps = 1e-08
corr_one = 1.0 - beta_one**10.0
corr_two = 1.0 - beta_two**10.0
low_type = jnp.bfloat16
wide = jnp.float32
gelu_scale = 0.7978845608028654
gelu_cube = 0.044715


def add_low(left, right):
    return (left.astype(wide) + right.astype(wide)).astype(low_type)


def dot_rows(left, right):
    return lax.dot_general(left, right, (((1,), (1,)), ((), ())), preferred_element_type=wide)


def dot_plain(left, right):
    return lax.dot_general(left, right, (((1,), (0,)), ((), ())), preferred_element_type=wide)


def dot_slots(left, right):
    return lax.dot_general(left, right, (((0,), (0,)), ((), ())), preferred_element_type=wide)


def gelu_parts(value):
    square = value * value
    bent = jnp.tanh(gelu_scale * value * (1.0 + gelu_cube * square))
    half = 0.5 * (1.0 + bent)
    slope = half + 0.5 * value * (1.0 - bent * bent) * gelu_scale * (
        1.0 + 3.0 * gelu_cube * square
    )
    return (value * half, slope)


def shift_down(value, step):
    if step % 8 == 0:
        return jnp.concatenate([value[-step:], value[:-step]], axis=0)
    return pltpu.roll(value, step, 0)


def shift_up(value, step):
    if step % 8 == 0:
        return jnp.concatenate([value[step:], value[:step]], axis=0)
    return pltpu.roll(value, value.shape[0] - step, 0)


def scan_slots(decay, value, shift):
    step = 1
    while step < value.shape[0]:
        value = value + decay * shift(value, step)
        if 2 * step < value.shape[0]:
            decay = decay * shift(decay, step)
        step *= 2
    return value


def one_minus_exp(value):
    series = jnp.ones_like(value)
    for number in range(11, 1, -1):
        series = 1.0 - value * (1.0 / number) * series
    return jnp.where(value < 0.8, value * series, 1.0 - jnp.exp(-value))


def soft_plus(value):
    return jnp.maximum(value, 0.0) + jnp.log1p(jnp.exp(-jnp.abs(value)))


def mixer_parts(first, position, small, gates):
    conv_out = small[4:5] + small[0:1] * first
    shifted = []
    for step in range(1, 4):
        moved = jnp.where(position >= step, shift_down(first, step), 0.0)
        shifted.append(moved)
        conv_out = conv_out + small[step : step + 1] * moved
    conv_low = conv_out.astype(low_type)
    logits = dot_plain(conv_low, gates)
    width = first.shape[1]
    recur_gate = jax.nn.sigmoid(logits[:, :width] + small[5:6])
    input_gate = jax.nn.sigmoid(logits[:, width:] + small[6:7])
    rate = gate_scale * soft_plus(-small[7:8])
    log_decay = -rate * recur_gate
    decay = jnp.where(position > 0, jnp.exp(log_decay), 0.0)
    gone = one_minus_exp(-2.0 * log_decay)
    root = jnp.sqrt(gone)
    return conv_out, shifted, conv_low, recur_gate, input_gate, rate, decay, gone, root


def weight_views(w_ref, width):
    model = w_ref.shape[2] - width
    proj = w_ref[0, 0 : 2 * width, 0:model]
    out = w_ref[0, 2 * width : 3 * width, 0:model]
    gates = jnp.concatenate(
        [w_ref[0, 0:width, model:], w_ref[0, width : 2 * width, model:]], axis=1
    )
    small = w_ref[0, 2 * width : 2 * width + 16, model:].astype(wide)
    return proj, out, gates, small


def slot_position(starts):
    slot = lax.broadcasted_iota(jnp.int32, (starts.shape[0], 1), 0)
    return slot - starts[:, 0:1].astype(wide).astype(jnp.int32)


def mixer_step(x, position, views, width):
    proj, out, gates, small = views
    projected = dot_rows(x, proj)
    conv_out, _, _, _, input_gate, _, decay, _, root = mixer_parts(
        projected[:, :width], position, small, gates
    )
    states = scan_slots(decay, root * input_gate * conv_out, shift_down)
    mixed_low = (states * gelu_parts(projected[:, width:])[0]).astype(low_type)
    return projected, states, mixed_low, dot_plain(mixed_low, out)


def mixer_back_step(position, views, projected, states, res_low, width):
    _, out, gates, small = views
    first = projected[:, :width]
    conv_out, shifted, conv_low, recur_gate, input_gate, rate, decay, gone, root = mixer_parts(
        first, position, small, gates
    )
    grad_mixed = dot_rows(res_low, out)
    active, slope = gelu_parts(projected[:, width:])
    grad_second = grad_mixed * states * slope
    adjoint = scan_slots(shift_up(decay, 1), grad_mixed * active, shift_up)
    grad_decay = adjoint * shift_down(states, 1)
    gated = adjoint * conv_out
    grad_root = gated * input_gate
    grad_input_gate = gated * root
    grad_conv = adjoint * root * input_gate
    grad_log = grad_decay * decay - grad_root * (1.0 - gone) / root
    grad_recur = -rate * grad_log
    grad_logit_a = grad_recur * recur_gate * (1.0 - recur_gate)
    grad_logit_b = grad_input_gate * input_gate * (1.0 - input_gate)
    grad_param = jnp.sum(grad_log * recur_gate, axis=0, keepdims=True) * (
        gate_scale * jax.nn.sigmoid(-small[7:8])
    )
    logits_low = jnp.concatenate([grad_logit_a, grad_logit_b], axis=1).astype(low_type)
    grad_conv = grad_conv + dot_rows(logits_low, gates)
    grad_gates = dot_slots(conv_low, logits_low)
    sums = [jnp.sum(grad_conv * first, axis=0, keepdims=True)]
    grad_first = small[0:1] * grad_conv
    for step in range(1, 4):
        sums.append(jnp.sum(grad_conv * shifted[step - 1], axis=0, keepdims=True))
        kept = jnp.where(position >= step, grad_conv, 0.0)
        grad_first = grad_first + small[step : step + 1] * shift_up(kept, step)
    sums.append(jnp.sum(grad_conv, axis=0, keepdims=True))
    sums.append(jnp.sum(grad_logit_a, axis=0, keepdims=True))
    sums.append(jnp.sum(grad_logit_b, axis=0, keepdims=True))
    sums.append(grad_param)
    proj_low = jnp.concatenate([grad_first, grad_second], axis=1).astype(low_type)
    return proj_low, grad_gates, jnp.concatenate(sums, axis=0)


def peer_x(chip):
    return chip + 1 - 2 * (chip % 2)


def peer_y(chip):
    return chip + 2 - 4 * (chip // 2)


def line_place(end, core):
    return end + core * (3 - 2 * end)


def remote(source, target, send, recv, member, z):
    return pltpu.make_async_remote_copy(
        src_ref=source,
        dst_ref=target,
        send_sem=send,
        recv_sem=recv,
        device_id=(member, z),
        device_id_type=pl.DeviceIdType.MESH,
    )


def enter(member, z):
    barrier = pltpu.get_barrier_semaphore()
    for other in range(8):

        @pl.when(member != other)
        def _():
            pl.semaphore_signal(
                barrier, inc=1, device_id=(other, z), device_id_type=pl.DeviceIdType.MESH
            )

    for other in range(4):

        @pl.when(z != other)
        def _():
            pl.semaphore_signal(
                barrier, inc=1, device_id=(member, other), device_id_type=pl.DeviceIdType.MESH
            )

    pl.semaphore_wait(barrier, 10)


def quarters(value_ref, shape):
    slots = shape[0]
    row = lax.broadcasted_iota(jnp.int32, shape, 0)
    result = jnp.full(shape, value_ref[3 * slots // 4], jnp.int32)
    for number in (2, 1, 0):
        result = jnp.where(
            row < (number + 1) * slots // 4, value_ref[number * slots // 4], result
        )
    return result


class Gather:
    def __init__(self, own, target, send, recv, member, z):
        self.own, self.target = own, target
        self.send, self.recv = send, recv
        chip, core = member // 2, member % 2
        self.to_x = peer_x(chip) * 2 + core
        self.to_y = peer_y(chip) * 2 + core
        self.z = z
        self.half = own.shape[0] // 2

    def copy(self, number):
        low, high = pl.ds(0, self.half), pl.ds(self.half, self.half)
        source, target, to = (
            (self.own, self.target.at[1], self.to_x),
            (self.own, self.target.at[2], self.to_y),
            (self.target.at[1, low], self.target.at[3, low], self.to_y),
            (self.target.at[2, high], self.target.at[3, high], self.to_x),
        )[number]
        return remote(source, target, self.send.at[number], self.recv.at[number], to, self.z)

    def begin(self):
        self.copy(0).start()
        self.copy(1).start()

    def relay(self):
        self.copy(0).wait_recv()
        self.copy(2).start()
        self.copy(1).wait_recv()
        self.copy(3).start()

    def arrive(self):
        self.copy(2).wait_recv()
        self.copy(3).wait_recv()

    def finish(self):
        for number in range(4):
            self.copy(number).wait_send()


class Reduce:
    def __init__(self, part, from_x, from_y, passing, last, send, recv, member, z):
        self.part, self.from_x, self.from_y = part, from_x, from_y
        self.passing, self.last = passing, last
        self.send, self.recv = send, recv
        chip, core = member // 2, member % 2
        self.to_x = peer_x(chip) * 2 + core
        self.to_y = peer_y(chip) * 2 + core
        self.z = z
        self.slots = part.shape[0] // 4
        self.half = self.slots // 2

    def copy(self, number):
        slots, half = self.slots, self.half
        source, target, to = (
            (self.part.at[pl.ds(slots, half)], self.from_x.at[0], self.to_x),
            (self.part.at[pl.ds(3 * slots, half)], self.from_x.at[1], self.to_x),
            (self.part.at[pl.ds(2 * slots + half, half)], self.from_y.at[0], self.to_y),
            (self.part.at[pl.ds(3 * slots + half, half)], self.from_y.at[1], self.to_y),
            (self.passing.at[0], self.last.at[0], self.to_y),
            (self.passing.at[1], self.last.at[1], self.to_x),
        )[number]
        return remote(source, target, self.send.at[number], self.recv.at[number], to, self.z)

    def begin(self):
        for block in (3, 1, 2):
            self.begin_block(block)

    def begin_block(self, block):
        for number in {1: (0,), 2: (2,), 3: (1, 3)}.get(block, ()):
            self.copy(number).start()

    def relay(self):
        slots, half = self.slots, self.half
        self.copy(1).wait_recv()
        self.passing[0] = (
            self.part[2 * slots : 2 * slots + half].astype(wide) + self.from_x[1].astype(wide)
        ).astype(low_type)
        self.copy(4).start()
        self.copy(3).wait_recv()
        self.passing[1] = (
            self.part[slots + half : 2 * slots].astype(wide) + self.from_y[1].astype(wide)
        ).astype(low_type)
        self.copy(5).start()

    def arrive(self):
        for number in (0, 2, 4, 5):
            self.copy(number).wait_recv()

    def result(self, number):
        direct = self.from_x if number == 0 else self.from_y
        return (
            self.part[number * self.half : (number + 1) * self.half].astype(wide)
            + direct[0].astype(wide)
            + self.last[number].astype(wide)
        )

    def finish(self):
        for number in range(6):
            self.copy(number).wait_send()

    @staticmethod
    def scratch(slots, model):
        return [pltpu.VMEM((2, slots // 2, model), low_type)] * 4


def norm_rows(value, gain):
    scale = lax.rsqrt(jnp.mean(value * value, axis=1, keepdims=True) + norm_eps)
    return value * scale * gain


def front_kernel(
    sizes,
    tokens_in,
    cot_in,
    start_ref,
    live_ref,
    gain_in,
    taps_ref,
    bias_ref,
    decay_ref,
    in_ref,
    gate_ref,
    out_ref,
    up_ref,
    down_ref,
    mix_in,
    weights,
    ffn_weights,
    saved_p,
    saved_state,
    saved_low,
    starts_out,
    residual_out,
    ffn_in,
    cot_out,
    gains_out,
    tokens_ref,
    cot_ref,
    gain_ref,
    tokens_all,
    raw_in,
    raw_up,
    raw_down,
    turned,
    gain_seen,
    acc,
    part,
    from_x,
    from_y,
    passing,
    last,
    load_sem,
    gain_send,
    gain_recv,
    m_send,
    m_recv,
    m_core_send,
    m_core_recv,
    f_send,
    f_recv,
    f_core_send,
    f_core_recv,
    g_send,
    g_recv,
    r_send,
    r_recv,
):
    model, width, ffn_width = sizes
    member = lax.axis_index("dp")
    z = lax.axis_index("shard")
    chip, core = member // 2, member % 2
    end = z + core * (3 - 2 * z)
    other = chip * 2 + 1 - core
    slots = cot_in.shape[0]
    half_ffn = ffn_width // 2
    owner = core == z // 2

    window = 128 * ((chip * ffn_width) // 128)
    skew = chip * ffn_width - window
    quarter = pl.ds(pl.multiple_of(chip * width, width), width)
    wide_window = pl.ds(pl.multiple_of(window, 128), raw_up.shape[2])

    def loads():
        found = [
            (out_ref.at[quarter], weights.at[end, pl.ds(2 * width, width), pl.ds(0, model)]),
        ]
        for kind in range(2):
            found.append((in_ref.at[kind, :, quarter], raw_in.at[kind]))
            found.append(
                (
                    gate_ref.at[kind, chip],
                    weights.at[end, pl.ds(kind * width, width), pl.ds(model, width)],
                )
            )
        found.append(
            (down_ref.at[pl.ds(pl.multiple_of(chip * ffn_width, 32), ffn_width)], raw_down)
        )
        for kind in range(2):
            found.append((up_ref.at[kind, :, wide_window], raw_up.at[kind]))
        return [
            pltpu.make_async_copy(source, target, load_sem.at[number])
            for number, (source, target) in enumerate(found)
        ]

    def turned_copy(kind):
        return pltpu.make_async_copy(
            raw_down
            if kind == 2
            else turned.at[kind, pl.ds(pl.multiple_of(skew, 32), ffn_width)],
            ffn_weights.at[kind, pl.ds(pl.multiple_of(2 * end * ffn_width, 32), ffn_width)],
            load_sem.at[9 + kind],
        )

    @pl.when(owner)
    def _():
        for copy in loads():
            copy.start()

    tokens_ref[:, :model] = tokens_in[...]
    tokens_ref[:, model:] = quarters(start_ref, (slots, width)).astype(wide).astype(low_type)
    live = quarters(live_ref, (slots, 128))[:, 0:1].astype(wide)
    cot_ref[...] = (cot_in[...].astype(wide) * live).astype(low_type)
    gain_ref[...] = jnp.concatenate(
        [gain_in[...].astype(wide), jnp.zeros((14, model // 4), wide)], axis=0
    ).astype(low_type)
    enter(member, z)

    gather_tokens = Gather(tokens_ref, tokens_all, g_send.at[0], g_recv.at[0], member, z)
    gather_cot = Gather(cot_ref, cot_out, g_send.at[1], g_recv.at[1], member, z)
    gather_ffn = Gather(ffn_in.at[0], ffn_in, g_send.at[2], g_recv.at[2], member, z)
    reduce = Reduce(part, from_x, from_y, passing, last, r_send, r_recv, member, z)
    own_cot = pltpu.make_async_copy(cot_ref, cot_out.at[0], load_sem.at[12])

    gather_tokens.begin()
    own_cot.start()

    def gain_copy(to, slot):
        return remote(
            gain_ref, gain_seen.at[slot], gain_send.at[to], gain_recv.at[slot], member, to
        )

    for to in range(4):

        @pl.when(to != z)
        def _():
            gain_copy(to, z).start()

    gain_seen[z] = gain_ref[...]

    def m_rows(number):
        return pl.ds(number * width, width)

    def m_copy(slot, number, way, to_end):
        place = weights.at[slot, m_rows(number)]
        return remote(
            place,
            place,
            m_send.at[way, slot, number],
            m_recv.at[slot, number],
            member,
            line_place(to_end, core),
        )

    def m_core(slot, number):
        return remote(
            weights.at[slot, m_rows(number)],
            weights.at[2 + slot, m_rows(number)],
            m_core_send.at[slot, number],
            m_core_recv.at[slot, number],
            other,
            z,
        )

    def f_place(slot, number):
        row = ((slot % 2) * 2 + slot // 2) * ffn_width + (number % 2) * half_ffn
        return ffn_weights.at[number // 2, pl.ds(row, half_ffn)]

    def f_copy(slot, number, way, to_end):
        place = f_place(slot, number)
        return remote(
            place,
            place,
            f_send.at[way, slot, number],
            f_recv.at[slot, number],
            member,
            line_place(to_end, core),
        )

    def f_core(slot, number):
        return remote(
            f_place(slot, number),
            f_place(2 + slot, number),
            f_core_send.at[slot, number],
            f_core_recv.at[slot, number],
            other,
            z,
        )

    def pass_on(copy, core_copy, slot, number):
        if slot == 0:

            @pl.when(end < 3)
            def _():
                copy(slot, number, 0, end + 1).start()
        else:

            @pl.when((end == 1) | (end == 2))
            def _():
                copy(slot, number, 0, end + 1).start()

        core_copy(slot, number).start()

    def pass_back(copy, numbers):
        @pl.when(end == 1)
        def _():
            for number in numbers:
                copy(1, number, 1, 0).start()

    def start_own(copy, core_copy, numbers):
        for slot in range(2):

            @pl.when(end == slot)
            def _():
                for number in numbers[slot]:
                    pass_on(copy, core_copy, slot, number)

    def turn_in(kind):
        @pl.when(owner)
        def _():
            for copy in loads()[1 + 2 * kind : 3 + 2 * kind]:
                copy.wait()

            def turn(at, carry):
                columns = pl.ds(pl.multiple_of(at * 256, 256), 256)
                weights[end, kind * width : (kind + 1) * width, columns] = raw_in[
                    kind, columns, :
                ].T
                return carry

            lax.fori_loop(0, model // 256, turn, 0)

        start_own(m_copy, m_core, ((kind,), (kind,)))
        pass_back(m_copy, (kind,))

    def turn_up(kind):
        @pl.when(owner)
        def _():
            loads()[6 + kind].wait()

            def turn(at, carry):
                columns = pl.ds(pl.multiple_of(at * 256, 256), 256)
                turned[kind, :, columns] = raw_up[kind, columns, :].T
                return carry

            lax.fori_loop(0, model // 256, turn, 0)
            turned_copy(kind).start()

    @pl.when(owner)
    def _():
        weights[end, 2 * width : 3 * width, model:] = jnp.concatenate(
            [
                taps_ref[:, quarter].astype(wide),
                bias_ref[:, quarter].astype(wide),
                decay_ref[:, quarter].astype(wide),
                jnp.zeros((width - 8, width), wide),
            ],
            axis=0,
        ).astype(low_type)
        loads()[0].wait()

    start_own(m_copy, m_core, ((2,), (2,)))
    pass_back(m_copy, (2,))
    turn_in(0)
    turn_in(1)

    @pl.when(owner)
    def _():
        loads()[5].wait()
        turned_copy(2).start()

    turn_up(0)
    turn_up(1)
    gather_tokens.relay()
    m_order = (2, 0, 1)

    @pl.when(end < 3)
    def _():
        for number in m_order:
            for slot in (1, 0):

                @pl.when(end != slot)
                def _():
                    m_copy(slot, number, 0, 0).wait_recv()
                    pass_on(m_copy, m_core, slot, number)

    @pl.when(owner)
    def _():
        for kind in range(3):
            turned_copy(kind).wait()

    f_order = ((4, 5, 0, 1, 2, 3), (4, 5, 0, 2))
    start_own(f_copy, f_core, f_order)

    def f_pass(slot, numbers):
        for number in numbers:
            f_copy(slot, number, 0, 0).wait_recv()
            pass_on(f_copy, f_core, slot, number)

    def f_step(step):
        @pl.when(end == 1)
        def _():
            f_pass(0, ((), (4, 5), (0, 1), (2, 3), (), ())[step])

        @pl.when(end == 2)
        def _():
            f_pass(1, ((4,), (5, 0), (2,), (), (), ())[step])
            f_pass(0, ((), (), (4,), (5, 0), (1, 2), (3,))[step])

        if step == 2:
            pass_back(f_copy, f_order[1])

    def far_step(items):
        @pl.when(end == 3)
        def _():
            for slot, number in items:
                f_copy(slot, number, 0, 0).wait_recv()
                f_core(slot, number).start()

    def near_step(step):
        @pl.when(end == 0)
        def _():
            f_pass(1, ((), (), (), (), (), f_order[1])[step])

    for to in range(4):

        @pl.when(to != z)
        def _():
            gain_copy(to, to).wait_recv()

    gains = jnp.concatenate([gain_seen[at].astype(wide) for at in range(4)], axis=1)
    gains_out[...] = gains[0:8]
    gather_tokens.arrive()

    def norm_block(block):
        if block == 0:
            source, starts = tokens_ref[:, :model], tokens_ref[:, model:]
        else:
            source, starts = tokens_all[block, :, :model], tokens_all[block, :, model:]
        at = slice(block * slots, (block + 1) * slots)
        mix_in[at, :] = norm_rows(source.astype(wide), gains_out[0:1]).astype(low_type)
        starts_out[at, :] = starts

    for block in range(4):
        norm_block(block)
    gather_cot.begin()
    f_step(0)

    late = end >= 2
    for turn in range(4):
        head = (turn + 2 * late) % 4
        if turn == 2:

            @pl.when(end == 3)
            def _():
                for number in m_order:
                    for slot in (1, 0):
                        m_copy(slot, number, 0, 0).wait_recv()
                        m_core(slot, number).start()

        @pl.when(head >= 2)
        def _():
            for number in m_order:
                m_core(head - 2, number).wait_recv()

        views = weight_views(weights.at[pl.ds(head, 1)], width)

        def step_block(count, carry):
            block = 3 - count
            rows = pl.ds(pl.multiple_of(block * slots, slots), slots)
            position = slot_position(starts_out[rows, :])
            projected, states, mixed_low, product = mixer_step(
                mix_in[rows, :], position, views, width
            )
            saved_p[head, rows, :] = projected
            saved_state[head, rows, :] = states
            saved_low[head, rows, :] = mixed_low
            if turn == 0:
                acc[rows, :] = product
            elif turn < 3:
                acc[rows, :] += product
            else:
                part[rows, :] = (acc[rows, :] + product).astype(low_type)
                for number in (3, 2, 1):

                    @pl.when(block == number)
                    def _():
                        reduce.begin_block(number)

            return carry

        lax.fori_loop(0, 4, step_block, 0)
        f_step(turn + 1)
        near_step(turn + 1)
        if turn == 0:
            gather_cot.relay()

    far_step(((1, 4), (1, 5)))
    reduce.relay()
    f_step(5)
    near_step(5)
    far_step(((1, 0), (1, 2)))
    reduce.arrive()
    half = slots // 2
    for number in range(2):
        at = slice(number * half, (number + 1) * half)
        residual = tokens_ref[at, :model].astype(wide) + reduce.result(number)
        residual_out[at, :] = residual
        ffn_in[0, at, :] = norm_rows(residual, gains_out[1:2]).astype(low_type)
    gather_ffn.begin()
    far_step(((0, 4), (0, 5), (0, 0)))
    gather_ffn.relay()

    far_step(((0, 1), (0, 2), (0, 3)))

    gather_ffn.arrive()
    gather_cot.arrive()
    own_cot.wait()
    for slot in range(2):
        for number in f_order[slot]:
            f_core(slot, number).wait_recv()

    for gather in (gather_tokens, gather_cot, gather_ffn, reduce):
        gather.finish()
    for to in range(4):

        @pl.when(to != z)
        def _():
            gain_copy(to, z).wait_send()

    for copy, core_copy, numbers in (
        (m_copy, m_core, (m_order, m_order)),
        (f_copy, f_core, f_order),
    ):
        for number in numbers[0]:
            core_copy(0, number).wait_send()

            @pl.when(end < 3)
            def _():
                copy(0, number, 0, 0).wait_send()

        for number in numbers[1]:
            core_copy(1, number).wait_send()

            @pl.when((end == 1) | (end == 2))
            def _():
                copy(1, number, 0, 0).wait_send()

            @pl.when(end == 1)
            def _():
                copy(1, number, 1, 0).wait_send()


def front(
    tokens, cot, starts, live, gains, taps, bias, decay, in_proj, gates, out_proj, gate_up, down, sizes
):
    model, width, ffn_width = sizes
    slots = cot.shape[0]
    rows = 4 * slots
    dma = pltpu.SemaphoreType.DMA
    vmem = pl.BlockSpec(memory_space=pltpu.VMEM)
    anywhere = pl.BlockSpec(memory_space=pl.ANY)
    scalars = pl.BlockSpec(memory_space=pltpu.SMEM)
    window = -(-ffn_width // 128) * 128
    return pl.pallas_call(
        functools.partial(front_kernel, sizes),
        in_specs=[vmem] * 2 + [scalars] * 2 + [vmem] * 4 + [anywhere] * 5,
        out_specs=[vmem, vmem, anywhere, vmem, vmem, vmem, vmem, vmem, vmem, anywhere, vmem],
        out_shape=[
            jax.ShapeDtypeStruct((rows, model), low_type),
            jax.ShapeDtypeStruct((4, 3 * width, model + width), low_type),
            jax.ShapeDtypeStruct((3, 4 * ffn_width, model), low_type),
            jax.ShapeDtypeStruct((4, rows, 2 * width), wide),
            jax.ShapeDtypeStruct((4, rows, width), wide),
            jax.ShapeDtypeStruct((4, rows, width), low_type),
            jax.ShapeDtypeStruct((rows, width), low_type),
            jax.ShapeDtypeStruct((slots, model), wide),
            jax.ShapeDtypeStruct((4, slots, model), low_type),
            jax.ShapeDtypeStruct((4, slots, model), low_type),
            jax.ShapeDtypeStruct((8, model), wide),
        ],
        scratch_shapes=[
            pltpu.VMEM((slots, model + width), low_type),
            pltpu.VMEM((slots, model), low_type),
            pltpu.VMEM((16, model // 4), low_type),
            pltpu.VMEM((4, slots, model + width), low_type),
            pltpu.VMEM((2, model, width), low_type),
            pltpu.VMEM((2, model, window), low_type),
            pltpu.VMEM((ffn_width, model), low_type),
            pltpu.VMEM((2, window, model), low_type),
            pltpu.VMEM((4, 16, model // 4), low_type),
            pltpu.VMEM((rows, model), wide),
            pltpu.VMEM((rows, model), low_type),
        ]
        + Reduce.scratch(slots, model)
        + [
            dma((13,)),
            dma((4,)),
            dma((4,)),
            dma((2, 2, 3)),
            dma((2, 3)),
            dma((2, 3)),
            dma((2, 3)),
            dma((2, 2, 6)),
            dma((2, 6)),
            dma((2, 6)),
            dma((2, 6)),
            dma((3, 4)),
            dma((3, 4)),
            dma((6,)),
            dma((6,)),
        ],
        compiler_params=pltpu.CompilerParams(
            collective_id=3, has_side_effects=True, vmem_limit_bytes=60 * 1024 * 1024
        ),
        cost_estimate=pl.CostEstimate(
            flops=2 * rows * model * 4 * width * 3,
            bytes_accessed=6 * ffn_width * 4 * model,
            transcendentals=rows * 4 * width * 6,
        ),
        name="front",
    )(tokens, cot, starts, live, gains, taps, bias, decay, in_proj, gates, out_proj, gate_up, down)


def middle_kernel(
    sizes,
    x_hbm,
    go_hbm,
    weights_ref,
    residual_ref,
    gain_ref,
    total,
    inner_down,
    res_low,
    res_out,
    gain_out,
    part_out,
    x_ref,
    go_ref,
    held,
    lows,
    paired,
    arrived,
    part_in,
    in_x,
    in_y,
    in_pass,
    in_last,
    load_sem,
    late_send,
    late_recv,
    late_core_send,
    late_core_recv,
    core_send,
    core_recv,
    line_send,
    line_recv,
    i_send,
    i_recv,
    g_send,
    g_recv,
):
    model, ffn_width = sizes
    member = lax.axis_index("dp")
    z = lax.axis_index("shard")
    chip, core = member // 2, member % 2
    end = z + core * (3 - 2 * z)
    other = chip * 2 + 1 - core
    slots = residual_ref.shape[0]
    half = slots // 2
    hidden = 4 * ffn_width
    half_ffn = ffn_width // 2

    split = -(-2 * ffn_width // 128) * 128

    late_low = 2 * ffn_width + half_ffn
    peer_low = 3 * ffn_width + half_ffn

    def weight_load(kinds, low, high, number):
        at = pl.ds(low, high - low)
        return pltpu.make_async_copy(
            weights_ref.at[kinds, at], held.at[kinds, at], load_sem.at[number]
        )

    loads = [
        weight_load(pl.ds(0, 3), 0, split, 0),
        pltpu.make_async_copy(x_hbm, x_ref, load_sem.at[1]),
        pltpu.make_async_copy(go_hbm, go_ref, load_sem.at[2]),
        weight_load(pl.ds(0, 2), split, late_low, 3),
        weight_load(pl.ds(0, 2), 3 * ffn_width, peer_low, 4),
        weight_load(pl.ds(2, 1), split, hidden, 5),
    ]
    own_late = weight_load(pl.ds(0, 2), late_low, 3 * ffn_width, 7)

    def late_copy(kind, way, to_end):
        place = held.at[kind, pl.ds(late_low, half_ffn)]
        return remote(
            place,
            place,
            late_send.at[way, kind],
            late_recv.at[kind],
            member,
            line_place(to_end, core),
        )

    def late_core(kind):
        return remote(
            held.at[kind, pl.ds(late_low, half_ffn)],
            held.at[kind, pl.ds(peer_low, half_ffn)],
            late_core_send.at[kind],
            late_core_recv.at[kind],
            other,
            z,
        )

    @pl.when(end == 1)
    def _():
        own_late.start()

    for load in loads:
        load.start()
    enter(member, z)

    @pl.when(end == 1)
    def _():
        own_late.wait()
        for kind in range(2):
            late_copy(kind, 0, 2).start()
            late_copy(kind, 1, 0).start()
            late_core(kind).start()

    for load in loads[:3]:
        load.wait()

    def late_step(block):
        for kind in range(2):

            @pl.when((end == 2) & (block == kind + 1))
            def _():
                late_copy(kind, 0, 0).wait_recv()
                late_copy(kind, 0, 3).start()
                late_core(kind).start()

    def late_end():
        for kind in range(2):

            @pl.when((end == 0) | (end == 3))
            def _():
                late_copy(kind, 0, 0).wait_recv()
                late_core(kind).start()

        for kind in range(2):
            late_core(kind).wait_recv()

    def late_sent():
        for kind in range(2):
            late_core(kind).wait_send()

            @pl.when((end == 1) | (end == 2))
            def _():
                late_copy(kind, 0, 0).wait_send()

            @pl.when(end == 1)
            def _():
                late_copy(kind, 1, 0).wait_send()

    def block_step(low, high, count, carry):
        block = 3 - count
        rows = pl.ds(pl.multiple_of(block * slots, slots), slots)
        x = x_ref[rows, :]
        grad_out = go_ref[rows, :]
        pre_gate = dot_rows(x, held[0, low:high])
        pre_up = dot_rows(x, held[1, low:high])
        active, slope = gelu_parts(pre_gate)
        ffn_low = (active * pre_up).astype(low_type)
        grad_act = dot_rows(grad_out, held[2, low:high])
        gate_low = (grad_act * pre_up * slope).astype(low_type)
        up_low = (grad_act * active).astype(low_type)
        sum_out = dot_plain(ffn_low, held[2, low:high])
        sum_in = dot_plain(gate_low, held[0, low:high]) + dot_plain(up_low, held[1, low:high])
        lows[0, rows, low:high] = gate_low
        lows[1, rows, low:high] = up_low
        lows[2, rows, low:high] = ffn_low
        if low == 0:
            late_step(count)
        else:
            sum_in = sum_in + part_in[rows, :].astype(wide)
            sum_out = sum_out + part_out[rows, :].astype(wide)
        part_in[rows, :] = sum_in.astype(low_type)
        if low > 0:
            for number in (3, 2, 1):

                @pl.when(block == number)
                def _():
                    reduce_in.begin_block(number)

        part_out[rows, :] = sum_out.astype(low_type)
        return carry

    reduce_in = Reduce(part_in, in_x, in_y, in_pass, in_last, i_send, i_recv, member, z)
    gather = Gather(res_low.at[0], res_low, g_send, g_recv, member, z)
    middle = model // 2

    def weight_grads(kind, low, high):
        factor = go_ref if kind == 2 else x_ref
        for at in range(2):
            columns = slice(at * middle, (at + 1) * middle)
            held[kind, low:high, columns] = dot_slots(
                lows[kind, :, low:high], factor[:, columns]
            ).astype(low_type)

    def core_copy(slot, kind):
        return remote(
            held.at[kind, pl.ds((2 * slot + 1) * ffn_width, ffn_width)],
            paired.at[slot, kind],
            core_send.at[slot, kind],
            core_recv.at[slot, kind],
            other,
            z,
        )

    def chunk(number):
        return number // 2, pl.ds((number % 2) * half_ffn, half_ffn)

    def line_copy(kind, number, to_end):
        at, rows = chunk(number)
        return remote(
            paired.at[min(kind, 1), at, rows],
            arrived.at[kind, at, rows],
            line_send.at[kind, number],
            line_recv.at[kind, number],
            member,
            line_place(to_end, core),
        )

    def pair_up(slot, kind):
        core_copy(slot, kind).wait_recv()
        for number in (2 * kind, 2 * kind + 1):
            at, rows = chunk(number)
            own = held[at, pl.ds(2 * slot * ffn_width + (number % 2) * half_ffn, half_ffn)]
            paired[slot, at, rows] = add_low(own, paired[slot, at, rows])

            if slot == 0 or number < 4:

                @pl.when(end == 3)
                def _():
                    line_copy(slot, number, 2).start()

            if slot == 1 and number < 4:

                @pl.when(end == 0)
                def _():
                    line_copy(2, number, 1).start()

    def part_grads(slot, low, high):
        for kind in range(3):
            weight_grads(kind, low, high)
            core_copy(slot, kind).start()
            if kind == 0 and slot == 0:
                pair_up(0, 0)
            elif kind > 1 - slot:
                pair_up(slot, kind - 1)
        pair_up(slot, 2)

    def summed(slot, kinds, number):
        at, rows = chunk(number)
        result = paired[slot, at, rows].astype(wide)
        for kind in kinds:
            result = result + arrived[kind, at, rows].astype(wide)
        return result.astype(low_type)

    def outer_step(number):
        at, rows = chunk(number)

        @pl.when((end == 2) | (end == 1))
        def _():
            line_copy(0, number, 0).wait_recv()
            paired[0, at, rows] = summed(0, (0,), number)
            line_copy(0, number, end - 1).start()

    def inner_step(number):
        at, rows = chunk(number)

        @pl.when(end == 2)
        def _():
            line_copy(1, number, 0).wait_recv()
            paired[1, at, rows] = summed(1, (1,), number)
            line_copy(1, number, 1).start()

    def out_copy(slot, number):
        at, rows = chunk(number)
        return pltpu.make_async_copy(
            paired.at[slot, at, rows], total.at[at, rows], load_sem.at[number]
        )

    def last_step(number):
        at, rows = chunk(number)

        if number < 4:

            @pl.when(end == 1)
            def _():
                line_copy(1, number, 0).wait_recv()
                line_copy(2, number, 0).wait_recv()
                paired[1, at, rows] = summed(1, (1, 2), number)
                out_copy(1, number).start()

        @pl.when(end == 0)
        def _():
            line_copy(0, number, 0).wait_recv()
            paired[0, at, rows] = summed(0, (0,), number)
            out_copy(0, number).start()

    lax.fori_loop(0, 4, functools.partial(block_step, 0, split), 0)
    part_grads(0, 0, split)
    for load in loads[3:]:
        load.wait()
    late_end()
    lax.fori_loop(0, 4, functools.partial(block_step, split, hidden), 0)
    late_sent()
    part_grads(1, split, hidden)
    inner_copy = pltpu.make_async_copy(paired.at[1, 2], inner_down, load_sem.at[6])
    inner_copy.start()
    for number in range(3):
        outer_step(number)
    reduce_in.relay()
    for number in range(3, 6):
        outer_step(number)

    reduce_in.arrive()
    gain = gain_ref[1:2]
    gain_sum = jnp.zeros((1, model), wide)
    for number in range(2):
        at = slice(number * half, (number + 1) * half)
        grad = reduce_in.result(number)
        value = residual_ref[at]
        scale = lax.rsqrt(jnp.mean(value * value, axis=1, keepdims=True) + norm_eps)
        scaled = grad * gain
        gain_sum = gain_sum + jnp.sum(grad * value * scale, axis=0, keepdims=True)
        inner = jnp.mean(scaled * value, axis=1, keepdims=True)
        back = scale * scaled - value * (scale * scale * scale * inner)
        result = go_ref[at].astype(wide) + back
        res_out[at] = result
        res_low[0, at] = result.astype(low_type)
    gain_out[...] = jnp.concatenate([gain_ref[0:1], gain_sum, jnp.zeros((6, model), wide)], axis=0)
    gather.begin()
    inner_step(0)
    gather.relay()
    inner_step(1)
    inner_step(2)
    inner_step(3)
    gather.arrive()
    for number in range(6):
        last_step(number)
    inner_copy.wait()

    for sent in (reduce_in, gather):
        sent.finish()
    for slot in range(2):
        for kind in range(3):
            core_copy(slot, kind).wait_send()
    for number in range(6):

        @pl.when(end > 0)
        def _():
            line_copy(0, number, 0).wait_send()

        @pl.when(end == 0)
        def _():
            out_copy(0, number).wait()

    for number in range(4):

        @pl.when(end > 1)
        def _():
            line_copy(1, number, 0).wait_send()

        @pl.when(end == 1)
        def _():
            out_copy(1, number).wait()

        @pl.when(end == 0)
        def _():
            line_copy(2, number, 1).wait_send()


def middle(x, grad_out, weights, residual, gains):
    rows, model = x.shape
    hidden = weights.shape[1]
    ffn_width = hidden // 4
    slots = rows // 4
    dma = pltpu.SemaphoreType.DMA
    vmem = pl.BlockSpec(memory_space=pltpu.VMEM)
    anywhere = pl.BlockSpec(memory_space=pl.ANY)
    quarter = (3, ffn_width, model)
    return pl.pallas_call(
        functools.partial(middle_kernel, (model, ffn_width)),
        in_specs=[anywhere] * 3 + [vmem] * 2,
        out_specs=[anywhere] * 2 + [vmem] * 4,
        out_shape=[
            jax.ShapeDtypeStruct(quarter, low_type),
            jax.ShapeDtypeStruct(quarter[1:], low_type),
            jax.ShapeDtypeStruct((4, slots, model), low_type),
            jax.ShapeDtypeStruct((slots, model), wide),
            jax.ShapeDtypeStruct((8, model), wide),
            jax.ShapeDtypeStruct((rows, model), low_type),
        ],
        scratch_shapes=[
            pltpu.VMEM(x.shape, low_type),
            pltpu.VMEM(x.shape, low_type),
            pltpu.VMEM(weights.shape, low_type),
            pltpu.VMEM((3, rows, hidden), low_type),
            pltpu.VMEM((2,) + quarter, low_type),
            pltpu.VMEM((3,) + quarter, low_type),
            pltpu.VMEM((rows, model), low_type),
        ]
        + Reduce.scratch(slots, model)
        + [
            dma((8,)),
            dma((2, 2)),
            dma((2,)),
            dma((2,)),
            dma((2,)),
            dma((2, 3)),
            dma((2, 3)),
            dma((3, 6)),
            dma((3, 6)),
            dma((6,)),
            dma((6,)),
            dma((4,)),
            dma((4,)),
        ],
        compiler_params=pltpu.CompilerParams(
            collective_id=4, has_side_effects=True, vmem_limit_bytes=63 * 1024 * 1024
        ),
        cost_estimate=pl.CostEstimate(
            flops=2 * rows * model * hidden * 9,
            bytes_accessed=weights.size * 4 + rows * model * 16,
            transcendentals=rows * hidden,
        ),
        name="middle",
    )(x, grad_out, weights, residual, gains)


class Scatter:
    def __init__(self, sizes, member, z, send_sem, recv_sem):
        self.model, self.width, self.ffn_width, self.piece_length = sizes
        self.member, self.z = member, z
        self.chip, self.core = member // 2, member % 2
        self.owner = self.core == z // 2
        self.send_sem, self.recv_sem = send_sem, recv_sem
        self.across = self.model // 128
        rec, ffn, model = 4 * self.width, 4 * self.ffn_width, self.model
        self.gate_base = 2 * model * rec
        self.out_base = self.gate_base + 8 * self.width * self.width
        self.up_base = self.out_base + rec * model
        self.down_base = self.up_base + 2 * model * ffn
        self.rec, self.ffn = rec, ffn
        self.first_in = 0
        self.first_gate = 2 * self.across
        self.first_out = self.first_gate + 2
        self.first_small = self.first_out + 4
        self.first_up = self.first_small + 1
        self.first_down = self.first_up + 2 * self.across
        self.count = self.first_down + 6

    def spans(self, base, row):
        found = []
        for piece in range(8):
            low = piece * self.piece_length
            for kind in range(2):
                start = base + kind * self.model * row
                first = max(low - start, 0)
                last = min(low + self.piece_length - start, self.model * row)
                if first < last:
                    left = first // row // 128 * 128
                    right = -(-last // (row * 128)) * 128
                    found.append((len(found), piece, kind, pl.ds(left, right - left)))
        return found

    def in_spans(self, kinds=(0, 1)):
        return [
            (self.first_in + at, piece, (pl.ds(kind * self.width, self.width), columns))
            for at, piece, kind, columns in self.spans(0, self.rec)
            if kind in kinds
        ]

    def up_spans(self):
        return [
            (self.first_up + at, piece, (kind, pl.ds(0, self.ffn_width), columns))
            for at, piece, kind, columns in self.spans(self.up_base, self.ffn)
        ]

    def span_copies(self, spans, source, target, act):
        for index, piece, where in spans:
            into = target.at[(self.chip,) + where]

            @pl.when(self.member != piece)
            def _():
                act(
                    remote(
                        source.at[where],
                        into,
                        self.send_sem.at[0, index],
                        self.recv_sem.at[self.chip, index],
                        piece,
                        self.z,
                    ),
                    True,
                )

            @pl.when(self.member == piece)
            def _():
                act(
                    pltpu.make_async_copy(
                        source.at[where], into, self.recv_sem.at[self.chip, index]
                    ),
                    False,
                )

    def span_arrivals(self, spans, source, target):
        for index, piece, where in spans:

            @pl.when(self.member == piece)
            def _():
                for q in range(4):
                    here = (self.chip == q) & self.owner
                    into = target.at[(q,) + where]

                    @pl.when(here)
                    def _():
                        pltpu.make_async_copy(
                            source.at[where], into, self.recv_sem.at[q, index]
                        ).wait()

                    @pl.when(jnp.logical_not(here))
                    def _():
                        remote(
                            source.at[where],
                            into,
                            self.send_sem.at[0, index],
                            self.recv_sem.at[q, index],
                            self.member,
                            self.z,
                        ).wait_recv()

    def gate_unit(self, kind, q):
        low = self.gate_base + (kind * 4 + q) * self.width * self.width
        where = (
            pl.ds(pl.multiple_of(kind * self.width, self.width), self.width),
            pl.ds(self.model, self.width),
        )
        return self.first_gate + kind, where, low, low + self.width * self.width

    def out_unit(self, number, q):
        rows = self.width // 4
        low = self.out_base + (q * self.width + number * rows) * self.model
        where = (
            pl.ds(pl.multiple_of(2 * self.width + number * rows, rows), rows),
            pl.ds(0, self.model),
        )
        return self.first_out + number, where, low, low + rows * self.model

    def down_unit(self, number, q):
        rows = self.ffn_width // 6
        low = self.down_base + (q * self.ffn_width + number * rows) * self.model
        where = (2, pl.ds(pl.multiple_of(number * rows, 16), rows), pl.ds(0, self.model))
        return self.first_down + number, where, low, low + rows * self.model

    def small_where(self):
        return (pl.ds(2 * self.width, 16), pl.ds(self.model, self.width))

    def copies(self, unit, source, target, q, act, flat=False):
        number, where, low, high = unit
        here = where[1:] if flat else where
        first = low // self.piece_length
        last = (high - 1) // self.piece_length
        for which, to in ((0, first), (1, last)):
            wanted = True if which == 0 else last != first

            @pl.when((to != self.member) & wanted)
            def _():
                act(
                    remote(
                        source.at[here],
                        target.at[(q,) + where],
                        self.send_sem.at[which, number],
                        self.recv_sem.at[q, number],
                        to,
                        self.z,
                    ),
                    True,
                )

            @pl.when((to == self.member) & wanted)
            def _():
                act(
                    pltpu.make_async_copy(
                        source.at[here], target.at[(q,) + where], self.recv_sem.at[q, number]
                    ),
                    False,
                )

    def each(self, unit_of, low, high, source, target, act, flat=False):
        def body(number, carry):
            self.copies(unit_of(number, self.chip), source, target, self.chip, act, flat)
            return carry

        lax.fori_loop(low, high, body, 0)

    def smalls(self, source, target, act):
        where = self.small_where()
        for to in range(8):

            @pl.when(self.member != to)
            def _():
                act(
                    remote(
                        source.at[where],
                        target.at[(self.chip,) + where],
                        self.send_sem.at[2, to],
                        self.recv_sem.at[self.chip, self.first_small],
                        to,
                        self.z,
                    ),
                    True,
                )

        act(
            pltpu.make_async_copy(
                source.at[where],
                target.at[(self.chip,) + where],
                self.recv_sem.at[self.chip, self.first_small],
            ),
            False,
        )

    def arrivals(self, unit_of, count, source, target):
        low = self.member * self.piece_length

        def body(number, carry):
            for q in range(4):
                index, where, first, last = unit_of(number, q)
                mine = (first < low + self.piece_length) & (last > low)
                here = (self.chip == q) & self.owner

                @pl.when(mine & here)
                def _():
                    pltpu.make_async_copy(
                        source.at[where], target.at[(q,) + where], self.recv_sem.at[q, index]
                    ).wait()

                @pl.when(mine & jnp.logical_not(here))
                def _():
                    remote(
                        source.at[where],
                        target.at[(q,) + where],
                        self.send_sem.at[0, index],
                        self.recv_sem.at[q, index],
                        self.member,
                        self.z,
                    ).wait_recv()

            return carry

        lax.fori_loop(0, count, body, 0)

    def small_arrivals(self, source, target):
        where = self.small_where()
        for q in range(4):
            here = (self.chip == q) & self.owner

            @pl.when(here)
            def _():
                pltpu.make_async_copy(
                    source.at[where],
                    target.at[(q,) + where],
                    self.recv_sem.at[q, self.first_small],
                ).wait()

            @pl.when(jnp.logical_not(here))
            def _():
                remote(
                    source.at[where],
                    target.at[(q,) + where],
                    self.send_sem.at[2, 0],
                    self.recv_sem.at[q, self.first_small],
                    self.member,
                    self.z,
                ).wait_recv()


def begin(copy, is_remote):
    copy.start()


def finish_send(copy, is_remote):
    if is_remote:
        copy.wait_send()


def back_kernel(
    sizes,
    x_hbm,
    res_hbm,
    starts_ref,
    w_hbm,
    p_hbm,
    state_hbm,
    low_hbm,
    ffn_ref,
    inner_hbm,
    tokens_ref,
    res_ref,
    gain_ref,
    mix_out,
    ffn_out,
    tokens_out,
    gain_out,
    x_ref,
    low_res,
    w_ref,
    p_ref,
    state_ref,
    low_ref,
    proj_grads,
    gate_acc,
    small_acc,
    grads,
    part_ref,
    paired,
    arrived,
    total,
    from_x,
    from_y,
    passing,
    last,
    inner,
    inner_seen,
    gain_part,
    gain_plane,
    gain_line,
    gain_seen,
    load_sem,
    core_send,
    core_recv,
    line_send,
    line_recv,
    plane_send,
    plane_recv,
    inner_send,
    inner_recv,
    gain_send,
    gain_recv,
    unit_send,
    unit_recv,
):
    model, width, ffn_width, piece_length = sizes
    member = lax.axis_index("dp")
    z = lax.axis_index("shard")
    chip, core = member // 2, member % 2
    end = z + core * (3 - 2 * z)
    slots = tokens_ref.shape[0]
    half = slots // 2
    other = chip * 2 + 1 - core
    scatter = Scatter(sizes, member, z, unit_send, unit_recv)

    order = (2, 0, 3, 1)
    common = [
        pltpu.make_async_copy(x_hbm, x_ref, load_sem.at[4, 0]),
        pltpu.make_async_copy(res_hbm, low_res, load_sem.at[4, 1]),
    ]
    early = [pltpu.make_async_copy(inner_hbm, inner, load_sem.at[4, 2])]

    def head_loads(head):
        return [
            pltpu.make_async_copy(source.at[head], target.at[head], load_sem.at[head, number])
            for number, (source, target) in enumerate(
                ((w_hbm, w_ref), (p_hbm, p_ref), (state_hbm, state_ref), (low_hbm, low_ref))
            )
        ]

    for copy in head_loads(order[0]) + common[1:] + early + common[:1]:
        copy.start()
    for head in order[1:]:
        for copy in head_loads(head):
            copy.start()
    enter(member, z)

    half_ffn = ffn_width // 2

    def inner_copy(kind, number, to_end):
        at = pl.ds(number * half_ffn, half_ffn)
        return remote(
            inner.at[at],
            inner_seen.at[kind, at],
            inner_send.at[kind, number],
            inner_recv.at[kind, number],
            member,
            line_place(to_end, core),
        )

    def inner_add(kinds, number):
        at = pl.ds(number * half_ffn, half_ffn)
        result = inner[at].astype(wide)
        for kind in kinds:
            inner_copy(kind, number, 0).wait_recv()
            result = result + inner_seen[kind, at].astype(wide)
        inner[at] = result.astype(low_type)

    def inner_far(number):
        @pl.when(end == 2)
        def _():
            inner_add((0,), number)
            inner_copy(0, number, 1).start()

    def inner_last():
        @pl.when(end == 1)
        def _():
            inner_add((0, 1), 0)
            inner_add((0, 1), 1)
            scatter.each(scatter.down_unit, 0, 6, inner, ffn_out, begin, True)

    for copy in early:
        copy.wait()
    for number in range(2):

        @pl.when(end == 3)
        def _():
            inner_copy(0, number, 2).start()

        @pl.when(end == 0)
        def _():
            inner_copy(1, number, 1).start()

    @pl.when(scatter.owner)
    def _():
        scatter.span_copies(scatter.up_spans(), ffn_ref, ffn_out, begin)

    @pl.when(end == 0)
    def _():
        scatter.each(scatter.down_unit, 0, 6, ffn_ref, ffn_out, begin)

    def rows(number):
        return pl.ds(number * width, width)

    def core_copy(slot, number):
        return remote(
            grads.at[2 + slot, rows(number)],
            paired.at[slot, rows(number)],
            core_send.at[slot, number],
            core_recv.at[slot, number],
            other,
            z,
        )

    reduce = Reduce(
        part_ref, from_x, from_y, passing, last, plane_send, plane_recv, member, z
    )

    def line_copy(kind, number, source, to_end):
        return remote(
            source,
            arrived.at[kind, rows(number)],
            line_send.at[kind, number],
            line_recv.at[kind, number],
            member,
            line_place(to_end, core),
        )

    def pair_up(slot):
        for number in range(3):
            core_copy(slot, number).wait_recv()
            both = grads[slot, rows(number)].astype(wide) + paired[slot, rows(number)].astype(wide)
            paired[slot, rows(number)] = both.astype(low_type)

            @pl.when(end == 3)
            def _():
                line_copy(slot, number, paired.at[slot, rows(number)], 2).start()

            if slot == 1:

                @pl.when(end == 0)
                def _():
                    line_copy(2, number, paired.at[slot, rows(number)], 1).start()

    def summed(slot, kinds, number):
        result = paired[slot, rows(number)].astype(wide)
        for kind in kinds:
            result = result + arrived[kind, rows(number)].astype(wide)
        return result.astype(low_type)

    def on_arrival(kind, number):
        line_copy(kind, number, paired.at[0, rows(number)], 0).wait_recv()

    def outer_step(place, number):
        @pl.when(end == place)
        def _():
            on_arrival(0, number)
            paired[0, rows(number)] = summed(0, (0,), number)
            line_copy(0, number, paired.at[0, rows(number)], place - 1).start()

    def far_inner(number):
        @pl.when(end == 2)
        def _():
            on_arrival(1, number)
            paired[1, rows(number)] = summed(1, (1,), number)
            line_copy(1, number, paired.at[1, rows(number)], 1).start()

    def share(number):
        if number < 2:
            scatter.span_copies(scatter.in_spans((number,)), total, mix_out, begin)
            scatter.each(scatter.gate_unit, number, number + 1, total, mix_out, begin)
        else:
            scatter.each(scatter.out_unit, 0, 4, total, mix_out, begin)
            scatter.smalls(total, mix_out, begin)

    common[1].wait()
    for turn, head in enumerate(order):
        for copy in head_loads(head):
            copy.wait()
        views = weight_views(w_ref.at[pl.ds(head, 1)], width)
        gate_acc[...] = jnp.zeros_like(gate_acc)
        small_acc[...] = jnp.zeros_like(small_acc)

        def step_block(block, carry):
            at = pl.ds(pl.multiple_of(block * slots, slots), slots)
            proj_low, grad_gates, grad_small = mixer_back_step(
                slot_position(starts_ref[at, :]),
                views,
                p_ref[head, at, :],
                state_ref[head, at, :],
                low_res[at, :],
                width,
            )
            proj_grads[at, head * 2 * width : (head + 1) * 2 * width] = proj_low
            gate_acc[...] += grad_gates
            small_acc[...] += grad_small
            return carry

        lax.fori_loop(0, 4, step_block, 0)
        if turn == 0:
            common[0].wait()
        grads[head, 0 : 2 * width, 0:model] = dot_slots(
            proj_grads[:, head * 2 * width : (head + 1) * 2 * width], x_ref[...]
        ).astype(low_type)
        grads[head, 2 * width : 3 * width, 0:model] = dot_slots(
            low_ref[head], low_res[...]
        ).astype(low_type)
        grads[head, 0:width, model:] = gate_acc[:, :width].astype(low_type)
        grads[head, width : 2 * width, model:] = gate_acc[:, width:].astype(low_type)
        grads[head, 2 * width : 3 * width, model:] = jnp.concatenate(
            [small_acc[...], jnp.zeros((width - 8, width), wide)], axis=0
        ).astype(low_type)
        if head >= 2:
            for number in range(3):
                core_copy(head - 2, number).start()
        if turn == 1:
            pair_up(0)
            inner_far(0)
        elif turn == 2:
            inner_far(1)
            outer_step(2, 0)
            outer_step(2, 1)
        elif turn == 3:
            inner_last()
            outer_step(2, 2)
            outer_step(1, 0)
            outer_step(1, 1)

    def in_block(block):
        at = slice(block * slots, (block + 1) * slots)
        result = jnp.zeros((slots, model), wide)
        for head in range(4):
            result = result + dot_plain(
                proj_grads[at, head * 2 * width : (head + 1) * 2 * width],
                w_ref[head, 0 : 2 * width, 0:model],
            )
        part_ref[at, :] = result.astype(low_type)

    for block in (3, 1, 2, 0):
        in_block(block)
        reduce.begin_block(block)
        if block == 3:
            pair_up(1)
    outer_step(1, 2)
    scatter.span_arrivals(scatter.up_spans(), ffn_ref, ffn_out)

    @pl.when(scatter.owner)
    def _():
        scatter.span_copies(scatter.up_spans(), ffn_ref, ffn_out, finish_send)

    far_inner(0)
    far_inner(1)
    reduce.relay()

    far_inner(2)
    for number in range(3):

        @pl.when(end == 1)
        def _():
            on_arrival(1, number)
            on_arrival(2, number)
            total[rows(number)] = summed(1, (1, 2), number)

        @pl.when(end == 0)
        def _():
            on_arrival(0, number)
            total[rows(number)] = summed(0, (0,), number)

        @pl.when(scatter.owner)
        def _():
            share(number)

    reduce.arrive()
    gain = gain_ref[0:1]
    gain_sum = jnp.zeros((1, model), wide)
    for number in range(2):
        at = slice(number * half, (number + 1) * half)
        grad = reduce.result(number)
        value = tokens_ref[at].astype(wide)
        scale = lax.rsqrt(jnp.mean(value * value, axis=1, keepdims=True) + norm_eps)
        scaled = grad * gain
        gain_sum = gain_sum + jnp.sum(grad * value * scale, axis=0, keepdims=True)
        drift = jnp.mean(scaled * value, axis=1, keepdims=True)
        back = scale * scaled - value * (scale * scale * scale * drift)
        tokens_out[at] = (res_ref[at] + back).astype(low_type)
    gain_part[...] = jnp.concatenate([gain_sum, gain_ref[1:2], jnp.zeros((6, model), wide)], axis=0)

    def gain_copy():
        return remote(
            gain_part, gain_plane.at[member], gain_send.at[0], gain_recv.at[member], 7, z
        )

    @pl.when(member != 7)
    def _():
        gain_copy().start()
        gain_copy().wait_send()
        gain_out[...] = jnp.zeros_like(gain_out)

    @pl.when(member == 7)
    def _():
        result = gain_part[...]
        for source in range(7):
            remote(
                gain_part,
                gain_plane.at[source],
                gain_send.at[0],
                gain_recv.at[source],
                7,
                z,
            ).wait_recv()
            result = result + gain_plane[source]
        quarter = model // 4
        for place in range(4):
            gain_line[place] = result[:, place * quarter : (place + 1) * quarter]

        def line_gain(place, slot):
            return remote(
                gain_line.at[place],
                gain_seen.at[slot],
                gain_send.at[1 + place],
                gain_recv.at[8 + slot],
                7,
                place,
            )

        for place in range(4):

            @pl.when(place != z)
            def _():
                line_gain(place, z).start()

        gain_out[...] = gain_line[z]
        for place in range(4):

            @pl.when(place != z)
            def _():
                line_gain(place, place).wait_recv()
                gain_out[...] += gain_seen[place]
                line_gain(place, z).wait_send()

    scatter.arrivals(scatter.down_unit, 6, ffn_ref, ffn_out)
    scatter.span_arrivals(scatter.in_spans(), total, mix_out)
    scatter.arrivals(scatter.gate_unit, 2, total, mix_out)
    scatter.arrivals(scatter.out_unit, 4, total, mix_out)
    scatter.small_arrivals(total, mix_out)

    @pl.when(scatter.owner)
    def _():
        scatter.each(scatter.down_unit, 0, 6, ffn_ref, ffn_out, finish_send)
        scatter.span_copies(scatter.in_spans(), total, mix_out, finish_send)
        scatter.each(scatter.gate_unit, 0, 2, total, mix_out, finish_send)
        scatter.each(scatter.out_unit, 0, 4, total, mix_out, finish_send)
        scatter.smalls(total, mix_out, finish_send)

    reduce.finish()
    for number in range(2):

        @pl.when(end >= 2)
        def _():
            inner_copy(0, number, 0).wait_send()

        @pl.when(end == 0)
        def _():
            inner_copy(1, number, 0).wait_send()

    for slot in range(2):
        for number in range(3):
            core_copy(slot, number).wait_send()
    for number in range(3):

        @pl.when(end > 0)
        def _():
            line_copy(0, number, paired.at[0, rows(number)], 0).wait_send()

        @pl.when(end > 1)
        def _():
            line_copy(1, number, paired.at[1, rows(number)], 0).wait_send()

        @pl.when(end == 0)
        def _():
            line_copy(2, number, paired.at[1, rows(number)], 1).wait_send()


def back(
    x,
    res,
    starts,
    weights,
    saved,
    ffn,
    inner,
    tokens,
    residual_grad,
    gains,
    piece_length,
    width,
):
    model = tokens.shape[1]
    ffn_width = ffn.shape[1]
    sizes = (model, width, ffn_width, piece_length)
    slots = tokens.shape[0]
    block = weights.shape[1:]
    count = Scatter(sizes, 0, 0, None, None).count
    dma = pltpu.SemaphoreType.DMA
    vmem = pl.BlockSpec(memory_space=pltpu.VMEM)
    anywhere = pl.BlockSpec(memory_space=pl.ANY)
    held = lambda value: pltpu.VMEM(value.shape, value.dtype)
    return pl.pallas_call(
        functools.partial(back_kernel, sizes),
        in_specs=[anywhere, anywhere, vmem] + [anywhere] * 6 + [vmem] * 3,
        out_specs=[anywhere, anywhere, vmem, vmem],
        out_shape=[
            jax.ShapeDtypeStruct(weights.shape, low_type),
            jax.ShapeDtypeStruct((4,) + ffn.shape, low_type),
            jax.ShapeDtypeStruct(tokens.shape, low_type),
            jax.ShapeDtypeStruct((8, model // 4), wide),
        ],
        scratch_shapes=[held(x), held(res), held(weights)]
        + [held(value) for value in saved]
        + [
            pltpu.VMEM((4 * slots, 8 * width), low_type),
            pltpu.VMEM((width, 2 * width), wide),
            pltpu.VMEM((8, width), wide),
            pltpu.VMEM(weights.shape, low_type),
            pltpu.VMEM((4 * slots, model), low_type),
            pltpu.VMEM((2,) + block, low_type),
            pltpu.VMEM((3,) + block, low_type),
            pltpu.VMEM(block, low_type),
        ]
        + Reduce.scratch(slots, model)
        + [
            held(inner),
            pltpu.VMEM((2,) + inner.shape, low_type),
            pltpu.VMEM((8, model), wide),
            pltpu.VMEM((8, 8, model), wide),
            pltpu.VMEM((4, 8, model // 4), wide),
            pltpu.VMEM((4, 8, model // 4), wide),
            dma((5, 4)),
            dma((2, 3)),
            dma((2, 3)),
            dma((3, 3)),
            dma((3, 3)),
            dma((6,)),
            dma((6,)),
            dma((2, 2)),
            dma((2, 2)),
            dma((5,)),
            dma((12,)),
            dma((3, count)),
            dma((4, count)),
        ],
        compiler_params=pltpu.CompilerParams(
            collective_id=2, has_side_effects=True, vmem_limit_bytes=60 * 1024 * 1024
        ),
        cost_estimate=pl.CostEstimate(
            flops=weights.size * 4 * slots * 4, bytes_accessed=weights.size * 8, transcendentals=0
        ),
        name="back",
    )(
        x,
        res,
        starts,
        weights,
        *saved,
        ffn,
        inner,
        tokens,
        residual_grad,
        gains,
    )


def adam_kernel(
    sizes,
    mix_hbm,
    ffn_hbm,
    gain_ref,
    master_ref,
    first_ref,
    second_ref,
    piece_ref,
    new_master_ref,
    new_first_ref,
    new_second_ref,
    rows_ref,
    bias_ref,
    grad,
    mix_ref,
    ffn_ref,
    load_sem,
):
    model, width, ffn_width, piece_length, lines, margin = sizes
    member = lax.axis_index("dp")
    step = pl.program_id(0)
    lead = 128
    start_row = (member * piece_length) // lead
    offset = (member * piece_length) % lead
    tiles_in = 4 * width // lead
    tiles_ffn = 4 * ffn_width // lead
    tiles_model = model // lead

    def needed(first, last):
        low = member * piece_length
        return (first < low + piece_length) & (last > low)

    up_first = 2 * model * 4 * width + 8 * width * width + 4 * width * model
    whole_mix = pltpu.make_async_copy(mix_hbm, mix_ref, load_sem.at[0])
    small = (pl.ds(0, 4), pl.ds(2 * width, 16), pl.ds(model, width))
    small_mix = pltpu.make_async_copy(mix_hbm.at[small], mix_ref.at[small], load_sem.at[1])
    need_mix = needed(0, up_first)
    kinds = [
        (
            needed(
                up_first + kind * 4 * ffn_width * model,
                up_first + (kind + 1) * 4 * ffn_width * model,
            ),
            pltpu.make_async_copy(
                ffn_hbm.at[:, kind], ffn_ref.at[:, kind], load_sem.at[2 + kind]
            ),
        )
        for kind in range(3)
    ]

    @pl.when((step == 0) & need_mix)
    def _():
        whole_mix.start()

    @pl.when((step == 0) & jnp.logical_not(need_mix))
    def _():
        small_mix.start()

    for wanted, copy in kinds:

        @pl.when((step == 0) & wanted)
        def _():
            copy.start()

    @pl.when(step == 0)
    def _():
        def clear(number, carry):
            grad[pl.ds(pl.multiple_of(number * 256, 256), 256), :] = jnp.zeros((256, lead), wide)
            return carry

        lax.fori_loop(0, grad.shape[0] // 256, clear, 0)

        @pl.when(need_mix)
        def _():
            whole_mix.wait()

        @pl.when(jnp.logical_not(need_mix))
        def _():
            small_mix.wait()

        for wanted, copy in kinds:

            @pl.when(wanted)
            def _():
                copy.wait()

        def place(row, count, body):
            low = member * piece_length

            @pl.when((row * lead < low + piece_length) & ((row + count) * lead > low))
            def _():
                body(row - start_row + margin)

        base = 0

        def in_unit(number, carry):
            kind = number // tiles_model
            at = number % tiles_model

            def body(to):
                for q in range(4):
                    tile = mix_ref[
                        q,
                        pl.ds(pl.multiple_of(kind * width, width), width),
                        pl.ds(pl.multiple_of(at * lead, lead), lead),
                    ].astype(wide)
                    grad[pl.ds(to + q, lead, stride=tiles_in), :] = tile.T

            place((kind * model + at * lead) * tiles_in, lead * tiles_in, body)
            return carry

        lax.fori_loop(0, 2 * tiles_model, in_unit, 0)
        base = 2 * model * tiles_in

        def gate_body(number, carry):
            kind = number // 4
            q = number % 4

            def body(to):
                grad[pl.ds(to, width), :] = mix_ref[
                    q, pl.ds(pl.multiple_of(kind * width, width), width), model:
                ].astype(wide)

            place(2 * model * tiles_in + number * width, width, body)
            return carry

        lax.fori_loop(0, 8, gate_body, 0)
        base = base + 8 * width
        out_base = base

        quarter = width // 4

        def out_unit(number, carry):
            q = number // 4
            part = number % 4

            def body(to):
                for at in range(tiles_model):
                    grad[pl.ds(to + at, quarter, stride=tiles_model), :] = mix_ref[
                        q,
                        pl.ds(pl.multiple_of(2 * width + part * quarter, quarter), quarter),
                        at * lead : (at + 1) * lead,
                    ].astype(wide)

            place(out_base + number * quarter * tiles_model, quarter * tiles_model, body)
            return carry

        lax.fori_loop(0, 16, out_unit, 0)
        base = base + 4 * width * tiles_model
        up_base = base

        def up_unit(number, carry):
            kind = number // tiles_model
            at = number % tiles_model
            columns = pl.ds(pl.multiple_of(at * lead, lead), lead)

            def body(to):
                for tile in range(tiles_ffn):
                    found = []
                    row = tile * lead
                    while row < (tile + 1) * lead:
                        q = row // ffn_width
                        last = min((q + 1) * ffn_width, (tile + 1) * lead)
                        found.append(
                            ffn_ref[
                                q,
                                kind,
                                row - q * ffn_width : last - q * ffn_width,
                                columns,
                            ].astype(wide)
                        )
                        row = last
                    block = found[0] if len(found) == 1 else jnp.concatenate(found, axis=0)
                    grad[pl.ds(to + tile, lead, stride=tiles_ffn), :] = block.T

            place(up_base + (kind * model + at * lead) * tiles_ffn, lead * tiles_ffn, body)
            return carry

        lax.fori_loop(0, 2 * tiles_model, up_unit, 0)
        base = base + 2 * model * tiles_ffn
        down_base = base
        sixth = ffn_width // 6

        def down_unit(number, carry):
            q = number // 6
            part = number % 6

            def body(to):
                for at in range(tiles_model):
                    grad[pl.ds(to + at, sixth, stride=tiles_model), :] = ffn_ref[
                        q,
                        2,
                        pl.ds(pl.multiple_of(part * sixth, 16), sixth),
                        at * lead : (at + 1) * lead,
                    ].astype(wide)

            place(down_base + number * sixth * tiles_model, sixth * tiles_model, body)
            return carry

        lax.fori_loop(0, 24, down_unit, 0)
        small_base = base + 4 * ffn_width * tiles_model
        smalls = [
            mix_ref[q, 2 * width : 2 * width + 16, model:].astype(wide)
            for q in range(4)
        ]

        def small_body(to):
            for q in range(4):
                grad[pl.ds(to + q, 8, stride=tiles_in), :] = smalls[q][:8]
            for number in range(6):
                kind, at = number // 3, number % 3
                grad[pl.ds(to + 8 * tiles_in + number, 1), :] = gain_ref[
                    kind : kind + 1, at * lead : (at + 1) * lead
                ]

        place(small_base, 8 * tiles_in + 6, small_body)
        bias_ref[...] = jnp.concatenate([small[5:7] for small in smalls], axis=1)

    row = margin + step * lines
    shift = (lead - offset) % lead
    here = pltpu.roll(grad[pl.ds(row, lines), :], shift, 1)
    after = pltpu.roll(grad[pl.ds(row + 1, lines), :], shift, 1)
    lane = lax.broadcasted_iota(jnp.int32, (lines, lead), 1)
    piece = jnp.where(lane < lead - offset, here, after).reshape(1, lines * lead)
    piece_ref[...] = piece
    new_first = beta_one * first_ref[...] + (1.0 - beta_one) * piece
    new_second = beta_two * second_ref[...] + (1.0 - beta_two) * piece * piece
    master = master_ref[...]
    new_master = master - learn_rate * (
        new_first / corr_one / (jnp.sqrt(new_second / corr_two) + adam_eps)
        + weight_decay * master
    )
    new_first_ref[...] = new_first
    new_second_ref[...] = new_second
    new_master_ref[...] = new_master
    rows_ref[0] = new_master.reshape(lines, lead).astype(low_type)


def adam(mix, ffn, gains, master, first, second, sizes, chunks):
    model, width, ffn_width = sizes
    piece_length = master.shape[1]
    lines = -(-piece_length // (chunks * 128 * 16)) * 16
    block = lines * 128
    margin = 1536
    rows = -(-(2 * margin + chunks * lines + 8) // 256) * 256
    packed = jax.ShapeDtypeStruct(master.shape, wide)
    chunk_spec = pl.BlockSpec((1, block), lambda s: (0, s))
    once = lambda shape: pl.BlockSpec(
        shape, lambda s: (0,) * len(shape), pipeline_mode=pl.Buffered(1)
    )
    return pl.pallas_call(
        functools.partial(
            adam_kernel, (model, width, ffn_width, piece_length, lines, margin)
        ),
        grid=(chunks,),
        in_specs=[pl.BlockSpec(memory_space=pl.ANY)] * 2 + [once(gains.shape)] + [chunk_spec] * 3,
        out_specs=[chunk_spec] * 4
        + [
            pl.BlockSpec((1, lines, 128), lambda s: (s, 0, 0)),
            pl.BlockSpec((2, 4 * width), lambda s: (0, 0)),
        ],
        out_shape=[packed] * 4
        + [
            jax.ShapeDtypeStruct((chunks, lines, 128), low_type),
            jax.ShapeDtypeStruct((2, 4 * width), wide),
        ],
        scratch_shapes=[
            pltpu.VMEM((rows, 128), wide),
            pltpu.VMEM(mix.shape, low_type),
            pltpu.VMEM(ffn.shape, low_type),
            pltpu.SemaphoreType.DMA((5,)),
        ],
        compiler_params=pltpu.CompilerParams(vmem_limit_bytes=48 * 1024 * 1024),
        cost_estimate=pl.CostEstimate(
            flops=20 * piece_length,
            bytes_accessed=40 * piece_length,
            transcendentals=piece_length,
        ),
        name="adam",
    )(mix, ffn, gains, master, first, second)


def spread_kernel(
    own_ref,
    part_hbm,
    residual_ref,
    mask_ref,
    weights_ref,
    block_out,
    held,
    spread,
    part,
    from_x,
    from_y,
    passing,
    last,
    load_sem,
    send_sem,
    recv_sem,
    plane_send,
    plane_recv,
):
    chunks, lines, lead = own_ref.shape
    member = lax.axis_index("dp")
    z = lax.axis_index("shard")
    step = pl.program_id(0)
    reduce = Reduce(part, from_x, from_y, passing, last, plane_send, plane_recv, member, z)
    part_load = pltpu.make_async_copy(part_hbm, part, load_sem.at[chunks])

    def copy_to(origin, chunk, side, to):
        return remote(
            held.at[origin, chunk],
            held.at[origin, chunk],
            send_sem.at[side, origin, chunk],
            recv_sem.at[origin, chunk],
            member,
            to,
        )

    def own_load(chunk):
        return pltpu.make_async_copy(own_ref.at[chunk], held.at[z, chunk], load_sem.at[chunk])

    def pass_on(origin, chunk, right):
        copy_to(origin, chunk, 0, z).wait_recv()
        if right:

            @pl.when(z < 3)
            def _():
                copy_to(origin, chunk, 0, z + 1).start()
        else:

            @pl.when(z > 0)
            def _():
                copy_to(origin, chunk, 1, z - 1).start()

    @pl.when(step == 0)
    def _():
        for chunk in range(chunks):
            own_load(chunk).start()
        part_load.start()
        barrier = pltpu.get_barrier_semaphore()
        for to in (reduce.to_x, reduce.to_y):
            pl.semaphore_signal(
                barrier, inc=1, device_id=(to, z), device_id_type=pl.DeviceIdType.MESH
            )

        @pl.when(z > 0)
        def _():
            pl.semaphore_signal(
                barrier, inc=1, device_id=(member, z - 1), device_id_type=pl.DeviceIdType.MESH
            )

        @pl.when(z < 3)
        def _():
            pl.semaphore_signal(
                barrier, inc=1, device_id=(member, z + 1), device_id_type=pl.DeviceIdType.MESH
            )

        @pl.when((z == 0) | (z == 3))
        def _():
            pl.semaphore_wait(barrier, 3)

        @pl.when((z > 0) & (z < 3))
        def _():
            pl.semaphore_wait(barrier, 4)

        def send_own(chunk, carry):
            own_load(chunk).wait()

            @pl.when(z < 3)
            def _():
                copy_to(z, chunk, 0, z + 1).start()

            @pl.when(z > 0)
            def _():
                copy_to(z, chunk, 1, z - 1).start()

            return carry

        lax.fori_loop(0, chunks, send_own, 0)
        part_load.wait()
        reduce.begin()

        def near(chunk, carry):
            @pl.when(z > 0)
            def _():
                pass_on(z - 1, chunk, True)

            @pl.when(z < 3)
            def _():
                pass_on(z + 1, chunk, False)

            return carry

        lax.fori_loop(0, chunks, near, 0)
        reduce.relay()

    @pl.when(step == 1)
    def _():
        reduce.arrive()
        live = quarters(mask_ref, (2 * reduce.half, 128))[:, 0:1].astype(wide)
        half = reduce.half
        for number in range(2):
            at = slice(number * half, (number + 1) * half)
            block_out[at] = (live[at] * (residual_ref[at] + reduce.result(number))).astype(low_type)
        reduce.finish()

    @pl.when(z >= 2)
    def _():
        pass_on(z - 2, step, True)

    @pl.when(z <= 1)
    def _():
        pass_on(z + 2, step, False)

    @pl.when(z == 3)
    def _():
        copy_to(0, step, 0, z).wait_recv()

    @pl.when(z == 0)
    def _():
        copy_to(3, step, 0, z).wait_recv()

    for origin in range(4):
        spread[origin * lines : (origin + 1) * lines, :] = held[origin, step].astype(wide)

    def line(number, carry):
        weights_ref[:, pl.ds(pl.multiple_of(number * lead, lead), lead)] = spread[
            pl.ds(number, 4, stride=lines), :
        ].astype(low_type)
        return carry

    lax.fori_loop(0, lines, line, 0, unroll=8)

    @pl.when(step == chunks - 1)
    def _():
        for origin in range(4):

            def finish(chunk, carry):
                @pl.when((origin <= z) & (z < 3))
                def _():
                    copy_to(origin, chunk, 0, z).wait_send()

                @pl.when((origin >= z) & (z > 0))
                def _():
                    copy_to(origin, chunk, 1, z).wait_send()

                return carry

            lax.fori_loop(0, chunks, finish, 0)


def spread_weights(own, part, residual, mask, piece_length):
    chunks, lines, lead = own.shape
    slots, model = residual.shape
    once = lambda value: pl.BlockSpec(
        value.shape, lambda s: (0, 0), pipeline_mode=pl.Buffered(1)
    )
    return pl.pallas_call(
        spread_kernel,
        grid=(chunks,),
        in_specs=[pl.BlockSpec(memory_space=pl.ANY)] * 2 + [
            once(residual),
            pl.BlockSpec(memory_space=pltpu.SMEM),
        ],
        out_specs=[pl.BlockSpec((4, lines * lead), lambda s: (0, s)), once(residual)],
        out_shape=[
            jax.ShapeDtypeStruct((4, piece_length), low_type),
            jax.ShapeDtypeStruct(residual.shape, low_type),
        ],
        scratch_shapes=[
            pltpu.VMEM((4, chunks, lines, lead), low_type),
            pltpu.VMEM((4 * lines, lead), wide),
            pltpu.VMEM(part.shape, low_type),
        ]
        + Reduce.scratch(slots, model)
        + [
            pltpu.SemaphoreType.DMA((chunks + 1,)),
            pltpu.SemaphoreType.DMA((2, 4, chunks)),
            pltpu.SemaphoreType.DMA((4, chunks)),
            pltpu.SemaphoreType.DMA((6,)),
            pltpu.SemaphoreType.DMA((6,)),
        ],
        compiler_params=pltpu.CompilerParams(
            collective_id=1, has_side_effects=True, vmem_limit_bytes=32 * 1024 * 1024
        ),
        cost_estimate=pl.CostEstimate(
            flops=4 * piece_length, bytes_accessed=16 * piece_length, transcendentals=0
        ),
        name="spread",
    )(own, part, residual, mask)


def group_body(
    tokens,
    cotangent,
    seq_start,
    live_mask,
    input_proj,
    gate_blocks,
    output_proj,
    ffn_gate_up,
    ffn_down,
    conv_taps,
    gate_bias,
    decay_param,
    norm_gains,
    master_shard,
    first_moment,
    second_moment,
):
    slots, model = tokens.shape
    slice_rec = input_proj.shape[2]
    slice_ffn = ffn_down.shape[0]
    width = slice_rec // 4
    ffn_width = slice_ffn // 4
    piece_length = master_shard.shape[1]
    (
        mix_in,
        mix_weights,
        ffn_weights,
        saved_p,
        saved_state,
        saved_low,
        all_starts,
        residual,
        ffn_in,
        all_grad_out,
        gains,
    ) = front(
        tokens,
        cotangent,
        seq_start,
        live_mask,
        norm_gains,
        conv_taps,
        gate_bias,
        decay_param[None],
        input_proj,
        gate_blocks,
        output_proj,
        ffn_gate_up,
        ffn_down,
        (model, width, ffn_width),
    )
    ffn_in = ffn_in.reshape(4 * slots, model)
    all_grad_out = all_grad_out.reshape(4 * slots, model)
    sum_ffn, inner_down, res_low, grad_residual, gain_sums, ffn_part = middle(
        ffn_in, all_grad_out, ffn_weights, residual, gains
    )
    four_mix, four_ffn, tokens_grad, gain_total = back(
        mix_in,
        res_low.reshape(4 * slots, model),
        all_starts,
        mix_weights,
        (saved_p, saved_state, saved_low),
        sum_ffn,
        inner_down,
        tokens,
        grad_residual,
        gain_sums,
        piece_length,
        width,
    )
    piece, new_master, new_first, new_second, rows, bias_total = adam(
        four_mix,
        four_ffn,
        gain_total,
        master_shard,
        first_moment,
        second_moment,
        (model, width, ffn_width),
        8,
    )
    new_weights, block_out = spread_weights(
        rows,
        ffn_part,
        residual,
        live_mask,
        piece_length,
    )
    return (
        block_out,
        tokens_grad,
        piece,
        new_master,
        new_first,
        new_second,
        new_weights,
        bias_total,
    )


def rms_scale(values, gain):
    return values * lax.rsqrt(jnp.mean(values * values, axis=-1, keepdims=True) + norm_eps) * gain


def conv_mix(signal, taps, position):
    result = taps[-1] + taps[0] * signal
    for shift_by in range(1, taps.shape[0] - 1):
        moved = jnp.pad(signal, ((shift_by, 0), (0, 0)))[:-shift_by]
        result = result + taps[shift_by] * jnp.where((position >= shift_by)[:, None], moved, 0.0)
    return result


def combine_steps(earlier, later):
    decay_first, value_first = earlier
    decay_second, value_second = later
    return (decay_first * decay_second, decay_second * value_first + value_second)


def recurrence(logits, signal, branch, bias_term, decay_term, position):
    row_count = signal.shape[0]
    recur_gate = jax.nn.sigmoid(logits[0].reshape(row_count, -1) + bias_term[0])
    input_gate = jax.nn.sigmoid(logits[1].reshape(row_count, -1) + bias_term[1])
    log_decay = -gate_scale * recur_gate * jax.nn.softplus(-decay_term)
    decay_rate = jnp.where((position > 0)[:, None], jnp.exp(log_decay), 0.0)
    drive_term = jnp.sqrt(-jnp.expm1(2.0 * log_decay)) * input_gate * signal
    states = lax.associative_scan(combine_steps, (decay_rate, drive_term), axis=0)[1]
    return states * jax.nn.gelu(branch)


def gated_gelu(ffn_pre):
    return jax.nn.gelu(ffn_pre[0]) * ffn_pre[1]


def mixer_forward(
    mix_in, input_proj, gate_blocks, output_proj, conv_taps, gate_bias, decay_param, position
):
    projected = jnp.einsum("sd,kdr->ksr", mix_in, input_proj, preferred_element_type=jnp.float32)
    conv_out, conv_pull = jax.vjp(
        lambda signal, taps: conv_mix(signal, taps, position), projected[0], conv_taps
    )
    row_count = conv_out.shape[0]
    conv_low = conv_out.astype(jnp.bfloat16).reshape(
        row_count, gate_blocks.shape[1], gate_blocks.shape[2]
    )
    gate_logits = jnp.einsum(
        "shb,khbc->kshc", conv_low, gate_blocks, preferred_element_type=jnp.float32
    )
    mixed, mix_pull = jax.vjp(
        lambda logits, signal, branch, bias_term, decay_term: recurrence(
            logits, signal, branch, bias_term, decay_term, position
        ),
        gate_logits,
        conv_out,
        projected[1],
        gate_bias,
        decay_param,
    )
    mixed_low = mixed.astype(jnp.bfloat16)
    partial_out = jnp.dot(mixed_low, output_proj, preferred_element_type=jnp.float32)
    return (partial_out, (conv_pull, conv_low, mix_pull, mixed_low))


def mixer_backward(grad_out_low, mix_in, saved, input_proj, gate_blocks, output_proj):
    conv_pull, conv_low, mix_pull, mixed_low = saved
    grad_output_proj = jnp.einsum(
        "sr,sd->rd", mixed_low, grad_out_low, preferred_element_type=jnp.float32
    )
    grad_mixed = jnp.einsum(
        "sd,rd->sr", grad_out_low, output_proj, preferred_element_type=jnp.float32
    )
    grad_logits, grad_conv_direct, grad_branch, grad_bias, grad_decay = mix_pull(grad_mixed)
    logits_low = grad_logits.astype(jnp.bfloat16)
    grad_blocks = jnp.einsum(
        "shb,kshc->khbc", conv_low, logits_low, preferred_element_type=jnp.float32
    )
    grad_conv_gates = jnp.einsum(
        "kshc,khbc->shb", logits_low, gate_blocks, preferred_element_type=jnp.float32
    )
    grad_signal, grad_taps = conv_pull(
        grad_conv_direct + grad_conv_gates.reshape(grad_conv_direct.shape)
    )
    proj_low = jnp.stack([grad_signal, grad_branch]).astype(jnp.bfloat16)
    grad_input_proj = jnp.einsum(
        "sd,ksr->kdr", mix_in, proj_low, preferred_element_type=jnp.float32
    )
    grad_mix_in = jnp.einsum(
        "ksr,kdr->sd", proj_low, input_proj, preferred_element_type=jnp.float32
    )
    return (
        grad_mix_in,
        (grad_input_proj, grad_blocks, grad_output_proj, grad_taps, grad_bias, grad_decay),
    )


def ffn_forward(ffn_in_low, ffn_gate_up, ffn_down):
    ffn_pre = jnp.einsum("sd,kdf->ksf", ffn_in_low, ffn_gate_up, preferred_element_type=jnp.float32)
    ffn_act, ffn_pull = jax.vjp(gated_gelu, ffn_pre)
    ffn_low = ffn_act.astype(jnp.bfloat16)
    partial_ffn = jnp.dot(ffn_low, ffn_down, preferred_element_type=jnp.float32)
    return (partial_ffn, (ffn_pull, ffn_low))


def ffn_backward(grad_low, ffn_in_low, saved, ffn_gate_up, ffn_down):
    ffn_pull, ffn_low = saved
    grad_down = jnp.einsum("sf,sd->fd", ffn_low, grad_low, preferred_element_type=jnp.float32)
    grad_act = jnp.einsum("sd,fd->sf", grad_low, ffn_down, preferred_element_type=jnp.float32)
    grad_pre = ffn_pull(grad_act)[0]
    pre_low = grad_pre.astype(jnp.bfloat16)
    grad_gate_up = jnp.einsum(
        "sd,ksf->kdf", ffn_in_low, pre_low, preferred_element_type=jnp.float32
    )
    grad_ffn_in = jnp.einsum(
        "ksf,kdf->sd", pre_low, ffn_gate_up, preferred_element_type=jnp.float32
    )
    return (grad_ffn_in, grad_gate_up, grad_down)


def body(
    tokens,
    cotangent,
    seq_start,
    live_mask,
    input_proj,
    gate_blocks,
    output_proj,
    ffn_gate_up,
    ffn_down,
    conv_taps,
    gate_bias,
    decay_param,
    norm_gains,
    master_shard,
    first_moment,
    second_moment,
):
    slot_count = tokens.shape[0]
    position = jnp.arange(slot_count, dtype=jnp.int32) - seq_start
    mask_rows = live_mask.astype(jnp.float32)[:, None]
    stream = tokens.astype(jnp.float32)
    grad_stream = cotangent.astype(jnp.float32) * mask_rows
    shards = (
        input_proj,
        gate_blocks,
        output_proj,
        ffn_gate_up,
        ffn_down,
        conv_taps,
        gate_bias,
        decay_param,
        norm_gains,
    )
    (
        full_in,
        full_blocks,
        full_out,
        full_up,
        full_down,
        full_taps,
        full_bias,
        full_decay,
        full_gains,
    ) = (
        lax.all_gather(shards[0], "shard", axis=2, tiled=True),
        lax.all_gather(shards[1], "shard", axis=1, tiled=True),
        lax.all_gather(shards[2], "shard", axis=0, tiled=True),
        lax.all_gather(shards[3], "shard", axis=2, tiled=True),
        lax.all_gather(shards[4], "shard", axis=0, tiled=True),
        lax.all_gather(shards[5], "shard", axis=1, tiled=True),
        lax.all_gather(shards[6], "shard", axis=1, tiled=True),
        lax.all_gather(shards[7], "shard", axis=0, tiled=True),
        lax.all_gather(shards[8], "shard", axis=1, tiled=True),
    )
    gains = full_gains.astype(jnp.float32)
    normed, norm_pull = jax.vjp(rms_scale, stream, gains[0])
    mix_in = normed.astype(jnp.bfloat16)
    mix_out, mix_saved = mixer_forward(
        mix_in,
        full_in,
        full_blocks,
        full_out,
        full_taps.astype(jnp.float32),
        full_bias.astype(jnp.float32),
        full_decay.astype(jnp.float32),
        position,
    )
    residual = stream + mix_out
    normed_two, second_pull = jax.vjp(rms_scale, residual, gains[1])
    ffn_in_low = normed_two.astype(jnp.bfloat16)
    ffn_result, ffn_saved = ffn_forward(ffn_in_low, full_up, full_down)
    block_out = (mask_rows * (residual + ffn_result)).astype(jnp.bfloat16)
    grad_ffn_in, grad_up, grad_down = ffn_backward(
        grad_stream.astype(jnp.bfloat16), ffn_in_low, ffn_saved, full_up, full_down
    )
    grad_norm_two, grad_gain_two = second_pull(grad_ffn_in)
    grad_residual = grad_stream + grad_norm_two
    grad_mix_in, mix_grads = mixer_backward(
        grad_residual.astype(jnp.bfloat16), mix_in, mix_saved, full_in, full_blocks, full_out
    )
    grad_norm_one, grad_gain_one = norm_pull(grad_mix_in)
    tokens_grad = (grad_residual + grad_norm_one).astype(jnp.bfloat16)
    grads = (
        mix_grads[0],
        mix_grads[1],
        mix_grads[2],
        grad_up,
        grad_down,
        mix_grads[3],
        mix_grads[4],
        mix_grads[5],
        jnp.stack([grad_gain_one, grad_gain_two]),
    )
    summed = (
        lax.psum_scatter(
            grads[0].astype(jnp.bfloat16), "shard", scatter_dimension=2, tiled=True
        ).astype(jnp.float32),
        lax.psum_scatter(
            grads[1].astype(jnp.bfloat16), "shard", scatter_dimension=1, tiled=True
        ).astype(jnp.float32),
        lax.psum_scatter(
            grads[2].astype(jnp.bfloat16), "shard", scatter_dimension=0, tiled=True
        ).astype(jnp.float32),
        lax.psum_scatter(
            grads[3].astype(jnp.bfloat16), "shard", scatter_dimension=2, tiled=True
        ).astype(jnp.float32),
        lax.psum_scatter(
            grads[4].astype(jnp.bfloat16), "shard", scatter_dimension=0, tiled=True
        ).astype(jnp.float32),
        lax.psum_scatter(
            grads[5].astype(jnp.bfloat16), "shard", scatter_dimension=1, tiled=True
        ).astype(jnp.float32),
        lax.psum_scatter(
            grads[6].astype(jnp.bfloat16), "shard", scatter_dimension=1, tiled=True
        ).astype(jnp.float32),
        lax.psum_scatter(
            grads[7].astype(jnp.bfloat16), "shard", scatter_dimension=0, tiled=True
        ).astype(jnp.float32),
        lax.psum_scatter(
            grads[8].astype(jnp.bfloat16), "shard", scatter_dimension=1, tiled=True
        ).astype(jnp.float32),
    )
    flat = jnp.concatenate([member.reshape(1, -1) for member in summed], axis=1)
    piece = lax.psum_scatter(flat, "dp", scatter_dimension=1, tiled=True)
    bias_total = lax.psum(summed[6], "dp")
    new_first = beta_one * first_moment + (1.0 - beta_one) * piece
    new_second = beta_two * second_moment + (1.0 - beta_two) * piece * piece
    new_master = master_shard - learn_rate * (
        new_first / corr_one / (jnp.sqrt(new_second / corr_two) + adam_eps)
        + weight_decay * master_shard
    )
    new_weights = lax.all_gather(new_master.astype(jnp.bfloat16), "shard", axis=0, tiled=True)
    return (
        block_out,
        tokens_grad,
        piece,
        new_master,
        new_first,
        new_second,
        new_weights,
        bias_total,
    )


def solution(mesh):
    fits = mesh.shape["dp"] == 8 and mesh.shape["shard"] == 4
    placed = (
        P(("dp", "shard"), None),
        P(("dp", "shard"), None),
        P(("dp", "shard")),
        P(("dp", "shard")),
        P(None, None, "shard"),
        P(None, "shard", None, None),
        P("shard", None),
        P(None, None, "shard"),
        P("shard", None),
        P(None, "shard"),
        P(None, "shard"),
        P("shard"),
        P(None, "shard"),
        P("shard", "dp"),
        P("shard", "dp"),
        P("shard", "dp"),
    )
    return jax.shard_map(
        group_body if fits else body,
        mesh=mesh,
        in_specs=placed,
        out_specs=(
            P(("dp", "shard"), None),
            P(("dp", "shard"), None),
            P("shard", "dp"),
            P("shard", "dp"),
            P("shard", "dp"),
            P("shard", "dp"),
            P(None, "dp"),
            P(None, "shard"),
        ),
        check_vma=False,
    )
```
